32 devices in a mesh: tm: 2 (over y), clip: 4 (over x, core), mp: 4 (over z).
Axes of the slice: x: 2, y: 2, z: 4, core: 2. Of those that a mesh axis runs over, the one named last changes fastest.
Arguments:
- tokens: bfloat16 [8, 16, 128, 1024], P('clip', 'tm', None, 'mp'), may hold values from -6 to 6
- cotangent: bfloat16 [8, 16, 128, 1024], P('clip', 'tm', None, 'mp'), may hold values from -6 to 6
- ratio: int32 [8], P('clip'), may hold values from 50 to 100
- priority: int32 [8, 16, 128], P('clip', 'tm'), may hold values from 0 to 99
- frame_order: int32 [8, 16], P('clip'), may hold values from 0 to 15, each once within a row
- mask_embed: bfloat16 [1024], P('mp'), may hold values from -6 to 6
- gains: bfloat16 [3, 1024], P(None, 'mp'), may hold values from 0.099609375 to 1.8984375
- qkv_space: bfloat16 [1024, 3, 1024], P(None, None, 'mp'), may hold values from -0.1875 to 0.1875
- out_space: bfloat16 [1024, 1024], P('mp'), may hold values from -0.75 to 0.75
- qkv_time: bfloat16 [1024, 3, 1024], P(None, None, 'mp'), may hold values from -0.1875 to 0.1875
- out_time: bfloat16 [1024, 1024], P('mp'), may hold values from -0.375 to 0.375
- w_in: bfloat16 [1024, 4096], P(None, 'mp'), may hold values from -0.1875 to 0.1875
- w_out: bfloat16 [4096, 1024], P('mp'), may hold values from -0.09375 to 0.09375
Outputs:
- block_out: bfloat16 [8, 16, 128, 1024], P('clip', 'tm', None, 'mp')
- grad_tokens: float32 [8, 16, 128, 1024], P('clip', 'tm', None, 'mp')
- grad_mask_embed: float32 [1024], P('mp')
- grad_gains: float32 [3, 1024], P(None, 'mp')
- grad_qkv_space: float32 [1024, 3, 1024], P(('tm', 'clip'), None, 'mp')
- grad_out_space: float32 [1024, 1024], P('mp', ('tm', 'clip'))
- grad_qkv_time: float32 [1024, 3, 1024], P(('tm', 'clip'), None, 'mp')
- grad_out_time: float32 [1024, 1024], P('mp', ('tm', 'clip'))
- grad_w_in: float32 [1024, 4096], P(('tm', 'clip'), 'mp')
- grad_w_out: float32 [4096, 1024], P('mp', ('tm', 'clip'))
The draws below stay inside these ranges and needn't reach their ends.
Inputs may be any that keep to these rules, and one draw needn't show every extreme that they name: Each row of frame_order holds each of 0 to 15 once.
All inputs are finite; a program needn't handle non-finite values.
Results may differ from the reference program's by a relative error of at most 0.02.
Values may be sent and summed in bfloat16 or wider, within the bound.
A program may use at most 192 MiB of HBM per device.

```python
import math
import jax
import jax.numpy as jnp
from jax import lax

D = 1024
HEADS = 16
HEAD_DIM = 64
FF = 4096
PATCHES = 128
FRAMES = 16
CLIPS = 8


def with_ends(result, own_key, low, top_value):
    extent = result.shape
    place = [jax.random.randint(jax.random.fold_in(own_key, axis), (), 0, extent[axis]) for axis in range(len(extent))]
    result = result.at[tuple(place)].set(low)
    longest = extent.index(max(extent))
    place[longest] = (place[longest] + 1) % extent[longest]
    return result.at[tuple(place)].set(top_value)


def block_scale(rng, dims, shards, low, top_value):
    factor_of = 1.0
    for position, shards_of in shards:
        steps = jax.random.uniform(jax.random.fold_in(jax.random.fold_in(rng, 6), position), (shards_of,), jnp.float32, low / len(shards), top_value / len(shards))
        factor_of = factor_of * jnp.repeat(jnp.exp(steps), dims[position] // shards_of).reshape((-1,) + (1,) * (len(dims) - 1 - position))
    return factor_of


def gaussian(key, extent, scale, most, shards=(), held_as=jnp.bfloat16):
    entries = scale * jax.random.normal(key, extent, jnp.float32)
    if shards:
        entries = entries * block_scale(key, extent, shards, -0.22, 0.18)
    return jnp.clip(entries, -most, most).astype(held_as)


def setup_inputs(seed: int = 0) -> dict:
    keys = jax.random.split(jax.random.key(seed), 14)
    tokens = gaussian(keys[0], (CLIPS, FRAMES, PATCHES, D), 1.0, 6.0, ((0, 4), (1, 2), (3, 4)))
    cotangent = gaussian(keys[1], (CLIPS, FRAMES, PATCHES, D), 1.0, 6.0, ((0, 4), (1, 2), (3, 4)))
    ratio = with_ends(jax.random.randint(keys[2], (CLIPS,), 50, 101), jax.random.fold_in(keys[2], 1), 50, 100).astype(jnp.int32)
    priority = with_ends(jax.random.randint(keys[3], (CLIPS, FRAMES, PATCHES), 0, 100), jax.random.fold_in(keys[3], 1), 0, 99).astype(jnp.int32)
    frame_order = jax.vmap(lambda own: jax.random.permutation(own, FRAMES))(jax.random.split(keys[4], CLIPS)).reshape((CLIPS, FRAMES)).astype(jnp.int32)
    mask_embed = gaussian(keys[5], (D,), 1.0, 6.0, ((0, 4),))
    gains = jnp.clip(1.0 + 0.18 * jax.random.normal(keys[6], (3, D), jnp.float32), 0.099609375, 1.8984375).astype(jnp.bfloat16)
    qkv_space = gaussian(keys[7], (D, 3, HEADS * HEAD_DIM), D ** -0.5, 0.1875, ((2, 4),))
    out_space = gaussian(keys[8], (HEADS * HEAD_DIM, D), (HEADS * HEAD_DIM // 16) ** -0.5, 0.75, ((0, 4),))
    qkv_time = gaussian(keys[9], (D, 3, HEADS * HEAD_DIM), D ** -0.5, 0.1875, ((2, 4),))
    out_time = gaussian(keys[10], (HEADS * HEAD_DIM, D), (HEADS * HEAD_DIM // 4) ** -0.5, 0.375, ((0, 4),))
    w_in = gaussian(keys[11], (D, FF), D ** -0.5, 0.1875, ((1, 4),))
    w_out = gaussian(keys[12], (FF, D), FF ** -0.5, 0.09375, ((0, 4),))
    return dict(tokens=tokens, cotangent=cotangent, ratio=ratio, priority=priority, frame_order=frame_order, mask_embed=mask_embed, gains=gains, qkv_space=qkv_space, out_space=out_space, qkv_time=qkv_time, out_time=out_time, w_in=w_in, w_out=w_out)


exact_mode = lax.Precision.HIGHEST
eps_norm = 1e-05

@jax.custom_vjp
def low(v):
    return lax.optimization_barrier(v.astype(jnp.bfloat16)).astype(jnp.float32)

@jax.custom_vjp
def low_back(v):
    return v

def low_keep(v):
    return (low(v), None)

def low_pass(kept, grad):
    return (grad,)

def back_keep(v):
    return (v, None)

def back_low(kept, grad):
    return (low(grad),)
low.defvjp(low_keep, low_pass)
low_back.defvjp(back_keep, back_low)

def normalize(residual_stream, gain_coefficients):
    centered_rows = lax.optimization_barrier(jnp.mean(residual_stream, axis=-1, keepdims=True))
    spread = lax.optimization_barrier(jnp.mean((residual_stream - centered_rows) ** 2, axis=-1, keepdims=True))
    return low((residual_stream - centered_rows) * lax.rsqrt(spread + eps_norm) * gain_coefficients)

def project_qkv(normalized_rows, weight):
    joined = jnp.einsum('fsd,dtk->tfsk', normalized_rows, weight, precision=exact_mode)
    joined = low(low_back(joined))
    return joined.reshape(3, joined.shape[1], joined.shape[2], HEADS, HEAD_DIM)

def branch(hidden, weight):
    return low_back(jnp.einsum('fsk,kd->fsd', hidden, weight, precision=exact_mode))

def forward_clip(source, masked, clip_order, mask_embed, gains, qkv_space, out_space, qkv_time, out_time, w_in, w_out):
    scale = 1.0 / math.sqrt(HEAD_DIM)
    joined_width = HEADS * HEAD_DIM
    residual_stream = jnp.where(masked[..., None], mask_embed, source)
    joined = project_qkv(normalize(residual_stream, gains[0]), qkv_space)
    scores = low_back(jnp.einsum('fshd,fthd->fhst', joined[0], joined[1], precision=exact_mode) * scale)
    attention = low(jax.nn.softmax(scores, axis=-1))
    mixed = low(low_back(jnp.einsum('fhst,fthd->fshd', attention, joined[2], precision=exact_mode)))
    residual_stream = residual_stream + branch(mixed.reshape(FRAMES, PATCHES, joined_width), out_space)
    joined = project_qkv(normalize(residual_stream, gains[1]), qkv_time)
    scores = low_back(jnp.einsum('fshd,gshd->hfgs', joined[0], joined[1], precision=exact_mode) * scale)
    visible = clip_order[None, :] <= clip_order[:, None]
    scores = jnp.where(visible[None, :, :, None], scores, -1e+30)
    attention = low(jax.nn.softmax(scores, axis=2))
    mixed = low(low_back(jnp.einsum('hfgs,gshd->fshd', attention, joined[2], precision=exact_mode)))
    residual_stream = residual_stream + branch(mixed.reshape(FRAMES, PATCHES, joined_width), out_time)
    normalized_rows = normalize(residual_stream, gains[2])
    projected = low_back(jnp.einsum('fsd,dk->fsk', normalized_rows, w_in, precision=exact_mode))
    hidden = low(jax.nn.gelu(projected, approximate=True))
    return residual_stream + branch(hidden, w_out)

def reference(tokens, cotangent, ratio, priority, frame_order, mask_embed, gains, qkv_space, out_space, qkv_time, out_time, w_in, w_out):
    params = (mask_embed.astype(jnp.float32), gains.astype(jnp.float32), qkv_space.astype(jnp.float32), out_space.astype(jnp.float32), qkv_time.astype(jnp.float32), out_time.astype(jnp.float32), w_in.astype(jnp.float32), w_out.astype(jnp.float32))

    def one_clip(carry, inputs):
        source, upstream, clip_ratio, clip_priority, clip_order = inputs
        masked = clip_priority < clip_ratio

        def layer(source_rows, *weights):
            return forward_clip(source_rows, masked, clip_order, *weights)
        output, pullback = jax.vjp(layer, source.astype(jnp.float32), *params)
        grads = pullback(jnp.where(masked[..., None], upstream.astype(jnp.float32), jnp.float32(0.0)))
        carry = tuple((total + grad for total, grad in zip(carry, grads[1:])))
        return (carry, (output.astype(jnp.bfloat16), grads[0]))
    zeros = tuple((jnp.zeros_like(param) for param in params))
    reduced_totals, (outputs, input_grads) = lax.scan(one_clip, zeros, (tokens, cotangent, ratio, priority, frame_order))
    return (outputs, input_grads, reduced_totals[0], reduced_totals[1], reduced_totals[2], reduced_totals[3], reduced_totals[4], reduced_totals[5], reduced_totals[6], reduced_totals[7])
```

```python
import math

import jax
import jax.numpy as jnp
from jax import lax
from jax.experimental import pallas as pl
from jax.experimental.pallas import tpu as pltpu
from jax.sharding import PartitionSpec as P

HEAD_DIM = 64
MICRO = 2


eps_norm = 1e-05


def gelu_tanh(values):
    return jax.nn.gelu(values, approximate=True)


def norm_forward_pass(residual_stream, gain_coefficients, complete_width):
    reduced_totals = lax.psum(
        (jnp.sum(residual_stream, axis=-1), jnp.sum(residual_stream * residual_stream, axis=-1)),
        "mp",
    )
    centered_rows = reduced_totals[0] / complete_width
    spread = reduced_totals[1] / complete_width - centered_rows * centered_rows
    inverse_scale = lax.rsqrt(spread + eps_norm)
    standardized_rows = (residual_stream - centered_rows[:, None]) * inverse_scale[:, None]
    shard_rows = (standardized_rows * gain_coefficients).astype(jnp.bfloat16)
    normalized_rows = lax.all_gather(shard_rows, "mp", axis=1, tiled=True)
    return (normalized_rows, standardized_rows, inverse_scale)


def norm_reverse_pass(
    normalized_gradient, standardized_rows, inverse_scale, gain_coefficients, complete_width
):
    gain_gradient = jnp.sum(normalized_gradient * standardized_rows, axis=0)
    standardized_gradient = normalized_gradient * gain_coefficients
    reduced_totals = lax.psum(
        (
            jnp.sum(standardized_gradient, axis=-1),
            jnp.sum(standardized_gradient * standardized_rows, axis=-1),
        ),
        "mp",
    )
    grad_resid = (
        standardized_gradient
        - reduced_totals[0][:, None] / complete_width
        - standardized_rows * (reduced_totals[1][:, None] / complete_width)
    ) * inverse_scale[:, None]
    return (grad_resid, gain_gradient)


def sum_features(grad_full):
    return lax.psum_scatter(
        grad_full.astype(jnp.bfloat16), "mp", scatter_dimension=1, tiled=True
    ).astype(jnp.float32)


def branch_out(hidden, weight):
    partial_rows = jnp.dot(hidden, weight, preferred_element_type=jnp.float32)
    return lax.psum_scatter(partial_rows, "mp", scatter_dimension=1, tiled=True)


def branch_back(grad_resid, hidden, weight):
    grad_rows = lax.all_gather(grad_resid.astype(jnp.bfloat16), "mp", axis=1, tiled=True)
    weight_grad = jnp.einsum("rk,rd->kd", hidden, grad_rows, preferred_element_type=jnp.float32)
    grad_hidden = jnp.einsum("rd,kd->rk", grad_rows, weight, preferred_element_type=jnp.float32)
    return (grad_hidden, weight_grad)


def qkv_back(normalized_rows, grad_joined, weight):
    weight_grad = jnp.einsum(
        "rd,trk->dtk", normalized_rows, grad_joined, preferred_element_type=jnp.float32
    )
    grad_full = jnp.einsum("trk,dtk->rd", grad_joined, weight, preferred_element_type=jnp.float32)
    return (weight_grad, sum_features(grad_full))


def reduce_grads(local_grads, small_grads):
    reduced = (
        lax.psum_scatter(local_grads[0], ("tm", "clip"), scatter_dimension=0, tiled=True),
        lax.psum_scatter(local_grads[1], ("tm", "clip"), scatter_dimension=1, tiled=True),
        lax.psum_scatter(local_grads[2], ("tm", "clip"), scatter_dimension=0, tiled=True),
        lax.psum_scatter(local_grads[3], ("tm", "clip"), scatter_dimension=1, tiled=True),
        lax.psum_scatter(local_grads[4], ("tm", "clip"), scatter_dimension=0, tiled=True),
        lax.psum_scatter(local_grads[5], ("tm", "clip"), scatter_dimension=1, tiled=True),
    )
    reduced_small = lax.psum((small_grads[0], small_grads[1]), ("tm", "clip"))
    return (reduced, reduced_small)


def space_forward(normalized_rows, weight, frame_count, patches, heads_local, scale):
    joined = jnp.einsum(
        "rd,dtk->trk", normalized_rows, weight, preferred_element_type=jnp.float32
    ).astype(jnp.bfloat16)
    shape_heads = (frame_count, patches, heads_local, HEAD_DIM)
    scores = (
        jnp.einsum(
            "bshd,bthd->bhst",
            joined[0].reshape(shape_heads),
            joined[1].reshape(shape_heads),
            preferred_element_type=jnp.float32,
        )
        * scale
    )
    highest = jnp.max(scores, axis=-1, keepdims=True)
    exponent = jnp.exp(scores - highest)
    reduced_totals = jnp.sum(exponent, axis=-1, keepdims=True)
    log_total = highest + jnp.log(reduced_totals)
    attention = (exponent / reduced_totals).astype(jnp.bfloat16)
    mixed = jnp.einsum(
        "bhst,bthd->bshd",
        attention,
        joined[2].reshape(shape_heads),
        preferred_element_type=jnp.float32,
    )
    return (
        joined,
        log_total,
        mixed.astype(jnp.bfloat16).reshape(frame_count * patches, heads_local * HEAD_DIM),
    )


def space_backward(grad_mixed, joined, log_total, frame_count, patches, heads_local, scale):
    shape_heads = (frame_count, patches, heads_local, HEAD_DIM)
    queries = joined[0].reshape(shape_heads)
    key_rows = joined[1].reshape(shape_heads)
    values = joined[2].reshape(shape_heads)
    grad_out = grad_mixed.reshape(shape_heads)
    scores = (
        jnp.einsum("bshd,bthd->bhst", queries, key_rows, preferred_element_type=jnp.float32) * scale
    )
    attention = jnp.exp(scores - log_total)
    grad_values = jnp.einsum(
        "bhst,bshd->bthd",
        attention.astype(jnp.bfloat16),
        grad_out,
        preferred_element_type=jnp.float32,
    )
    grad_att = jnp.einsum("bshd,bthd->bhst", grad_out, values, preferred_element_type=jnp.float32)
    grad_scores = (
        attention * (grad_att - jnp.sum(attention * grad_att, axis=-1, keepdims=True))
    ).astype(jnp.bfloat16)
    grad_queries = (
        jnp.einsum("bhst,bthd->bshd", grad_scores, key_rows, preferred_element_type=jnp.float32)
        * scale
    )
    grad_keys = (
        jnp.einsum("bhst,bshd->bthd", grad_scores, queries, preferred_element_type=jnp.float32)
        * scale
    )
    row_count = frame_count * patches
    stacked = jnp.stack(
        [
            grad_queries.reshape(row_count, -1),
            grad_keys.reshape(row_count, -1),
            grad_values.reshape(row_count, -1),
        ]
    )
    return stacked.astype(jnp.bfloat16)


def time_scores(queries, keys_all, visible, scale):
    scores = (
        jnp.einsum("cfshd,cgshd->chfgs", queries, keys_all, preferred_element_type=jnp.float32)
        * scale
    )
    return jnp.where(visible, scores, -1e30)


def time_forward(queries, keys_all, values_all, visible, scale):
    scores = time_scores(queries, keys_all, visible, scale)
    highest = jnp.max(scores, axis=3, keepdims=True)
    exponent = jnp.exp(scores - highest)
    reduced_totals = jnp.sum(exponent, axis=3, keepdims=True)
    log_total = highest + jnp.log(reduced_totals)
    attention = (exponent / reduced_totals).astype(jnp.bfloat16)
    mixed = jnp.einsum(
        "chfgs,cgshd->cfshd", attention, values_all, preferred_element_type=jnp.float32
    )
    return (log_total, mixed.astype(jnp.bfloat16))


def time_backward(grad_mixed, queries, keys_all, values_all, visible, log_total, scale):
    grad_out = grad_mixed.reshape(queries.shape)
    scores = time_scores(queries, keys_all, visible, scale)
    attention = jnp.exp(scores - log_total)
    grad_values = jnp.einsum(
        "chfgs,cfshd->cgshd",
        attention.astype(jnp.bfloat16),
        grad_out,
        preferred_element_type=jnp.float32,
    )
    grad_att = jnp.einsum(
        "cfshd,cgshd->chfgs", grad_out, values_all, preferred_element_type=jnp.float32
    )
    grad_scores = (
        attention * (grad_att - jnp.sum(attention * grad_att, axis=3, keepdims=True))
    ).astype(jnp.bfloat16)
    grad_queries = (
        jnp.einsum("chfgs,cgshd->cfshd", grad_scores, keys_all, preferred_element_type=jnp.float32)
        * scale
    )
    grad_keys = (
        jnp.einsum("chfgs,cfshd->cgshd", grad_scores, queries, preferred_element_type=jnp.float32)
        * scale
    )
    return (grad_queries, grad_keys, grad_values)


def shards(
    tokens,
    cotangent,
    ratio,
    priority,
    frame_order,
    mask_embed,
    gains,
    qkv_space,
    out_space,
    qkv_time,
    out_time,
    w_in,
    w_out,
):
    scale = 1.0 / math.sqrt(HEAD_DIM)
    clips_local = tokens.shape[0] // MICRO
    frames_local = tokens.shape[1]
    patches = tokens.shape[2]
    cols_local = tokens.shape[3]
    frames_all = frame_order.shape[1]
    hidden_width = qkv_space.shape[0]
    joined_local = qkv_space.shape[2]
    heads_local = joined_local // HEAD_DIM
    row_count = clips_local * frames_local * patches
    gain_broadcast = gains.astype(jnp.float32)
    embed_row = mask_embed.astype(jnp.float32)
    first_frame = lax.axis_index("tm") * frames_local
    shape_local = (clips_local, frames_local, patches, joined_local)
    shape_heads = (clips_local, frames_local, patches, heads_local, HEAD_DIM)
    shape_all = (clips_local, frames_all, patches, heads_local, HEAD_DIM)
    outputs = []
    input_grads = []
    weight_total = None
    small_total = None
    for batch_index in range(MICRO):
        lower = batch_index * clips_local
        upper = lower + clips_local
        source = tokens[lower:upper].reshape(row_count, cols_local).astype(jnp.float32)
        upstream = cotangent[lower:upper].reshape(row_count, cols_local).astype(jnp.float32)
        masked = (priority[lower:upper] < ratio[lower:upper][:, None, None]).reshape(row_count)
        order_rows = frame_order[lower:upper]
        residual_stream0 = jnp.where(masked[:, None], embed_row[None, :], source)
        normalized_rows0, standardized_rows0, inverse_deviation0 = norm_forward_pass(
            residual_stream0, gain_broadcast[0], hidden_width
        )
        joined0, total0, mixed0 = space_forward(
            normalized_rows0, qkv_space, clips_local * frames_local, patches, heads_local, scale
        )
        residual_stream1 = residual_stream0 + branch_out(mixed0, out_space)
        normalized_rows1, standardized_rows1, inverse_deviation1 = norm_forward_pass(
            residual_stream1, gain_broadcast[1], hidden_width
        )
        joined1 = jnp.einsum(
            "rd,dtk->trk", normalized_rows1, qkv_time, preferred_element_type=jnp.float32
        ).astype(jnp.bfloat16)
        queries_local = joined1[0].reshape(shape_local)
        keys_local = joined1[1].reshape(shape_local)
        values_local = joined1[2].reshape(shape_local)
        keys_all, values_all = (
            lax.all_gather(keys_local, "tm", axis=1, tiled=True),
            lax.all_gather(values_local, "tm", axis=1, tiled=True),
        )
        query_order = lax.dynamic_slice_in_dim(order_rows, first_frame, frames_local, axis=1)
        time_visible = (order_rows[:, None, :] <= query_order[:, :, None])[:, None, :, :, None]
        time_q = queries_local.reshape(shape_heads)
        time_k = keys_all.reshape(shape_all)
        time_v = values_all.reshape(shape_all)
        total1, mixed_frames = time_forward(time_q, time_k, time_v, time_visible, scale)
        mixed1 = mixed_frames.reshape(row_count, joined_local)
        residual_stream2 = residual_stream1 + branch_out(mixed1, out_time)
        normalized_rows2, standardized_rows2, inverse_deviation2 = norm_forward_pass(
            residual_stream2, gain_broadcast[2], hidden_width
        )
        projected = jnp.dot(normalized_rows2, w_in, preferred_element_type=jnp.float32)
        activated, gelu_pull = jax.vjp(gelu_tanh, projected)
        hidden = activated.astype(jnp.bfloat16)
        resid3 = residual_stream2 + branch_out(hidden, w_out)
        outputs.append(
            resid3.astype(jnp.bfloat16).reshape(clips_local, frames_local, patches, cols_local)
        )
        grad3 = jnp.where(masked[:, None], upstream, 0.0)
        grad_hidden, grad_w_out = branch_back(grad3, hidden, w_out)
        grad_inner = gelu_pull(grad_hidden)[0].astype(jnp.bfloat16)
        grad_w_in = jnp.einsum(
            "rd,rk->dk", normalized_rows2, grad_inner, preferred_element_type=jnp.float32
        )
        normalized_gradient2 = sum_features(
            jnp.einsum("rk,dk->rd", grad_inner, w_in, preferred_element_type=jnp.float32)
        )
        backward_third, gain_gradient2 = norm_reverse_pass(
            normalized_gradient2,
            standardized_rows2,
            inverse_deviation2,
            gain_broadcast[2],
            hidden_width,
        )
        grad2 = grad3 + backward_third
        grad_mixed1, grad_out_time = branch_back(grad2, mixed1, out_time)
        grad_mixed_low = grad_mixed1.astype(jnp.bfloat16).reshape(shape_local)
        grad_queries, grad_keys, grad_values = time_backward(
            grad_mixed_low, time_q, time_k, time_v, time_visible, total1, scale
        )
        key_part, value_part = (
            lax.psum_scatter(
                grad_keys.reshape(clips_local, frames_all, patches, joined_local).astype(
                    jnp.bfloat16
                ),
                "tm",
                scatter_dimension=1,
                tiled=True,
            ).astype(jnp.float32),
            lax.psum_scatter(
                grad_values.reshape(clips_local, frames_all, patches, joined_local).astype(
                    jnp.bfloat16
                ),
                "tm",
                scatter_dimension=1,
                tiled=True,
            ).astype(jnp.float32),
        )
        grad_joined1 = jnp.stack(
            [
                grad_queries.reshape(row_count, joined_local),
                key_part.reshape(row_count, joined_local),
                value_part.reshape(row_count, joined_local),
            ]
        ).astype(jnp.bfloat16)
        grad_qkv_time, normalized_gradient1 = qkv_back(normalized_rows1, grad_joined1, qkv_time)
        backward_second, gain_gradient1 = norm_reverse_pass(
            normalized_gradient1,
            standardized_rows1,
            inverse_deviation1,
            gain_broadcast[1],
            hidden_width,
        )
        grad1 = grad2 + backward_second
        grad_mixed0, grad_out_space = branch_back(grad1, mixed0, out_space)
        grad_joined0 = space_backward(
            grad_mixed0.astype(jnp.bfloat16),
            joined0,
            total0,
            clips_local * frames_local,
            patches,
            heads_local,
            scale,
        )
        grad_qkv_space, normalized_gradient0 = qkv_back(normalized_rows0, grad_joined0, qkv_space)
        backward_first, gain_gradient0 = norm_reverse_pass(
            normalized_gradient0,
            standardized_rows0,
            inverse_deviation0,
            gain_broadcast[0],
            hidden_width,
        )
        grad0 = grad1 + backward_first
        input_grads.append(
            jnp.where(masked[:, None], 0.0, grad0).reshape(
                clips_local, frames_local, patches, cols_local
            )
        )
        grad_embed = jnp.sum(jnp.where(masked[:, None], grad0, 0.0), axis=0)
        gain_grads = jnp.stack([gain_gradient0, gain_gradient1, gain_gradient2])
        local_grads = (
            grad_qkv_space,
            grad_out_space,
            grad_qkv_time,
            grad_out_time,
            grad_w_in,
            grad_w_out,
        )
        small_grads = (gain_grads, grad_embed)
        reduced, reduced_small = reduce_grads(local_grads, small_grads)
        if weight_total is None:
            weight_total = reduced
            small_total = reduced_small
        else:
            weight_total = tuple((total + grad for total, grad in zip(weight_total, reduced)))
            small_total = tuple((total + grad for total, grad in zip(small_total, reduced_small)))
    return (
        jnp.concatenate(outputs, axis=0),
        jnp.concatenate(input_grads, axis=0),
        small_total[1],
        small_total[0],
        weight_total[0],
        weight_total[1],
        weight_total[2],
        weight_total[3],
        weight_total[4],
        weight_total[5],
    )


AXES = ("tm", "clip", "mp")
F32 = jnp.float32
BF16 = jnp.bfloat16
BLK = 256


def device_pairs(move):
    pairs = []
    for y in range(2):
        for x in range(2):
            for c in range(2):
                for z in range(4):
                    there = move(y, x, c, z)
                    pairs.append(tuple((q[0] * 4 + q[1] * 2 + q[2]) * 4 + q[3] for q in ((y, x, c, z), there)))
    return pairs


def hop_y(v):
    return lax.ppermute(v, AXES, device_pairs(lambda y, x, c, z: (1 - y, x, c, z)))


def hop_x(v):
    return lax.ppermute(v, AXES, device_pairs(lambda y, x, c, z: (y, 1 - x, c, z)))


def hop_c(v):
    return lax.ppermute(v, AXES, device_pairs(lambda y, x, c, z: (y, x, 1 - c, z)))


def hop_z(v, shift):
    return lax.ppermute(v, AXES, device_pairs(lambda y, x, c, z: (y, x, c, (z + shift) % 4)))


def spread_pairs(r):
    def move(y, x, c, z):
        k = z ^ r
        return (y, x, k & 1, 2 * c + (k >> 1))

    return device_pairs(move)


def dot_nn(a, b):
    return lax.dot_general(a, b, (((1,), (0,)), ((), ())), preferred_element_type=F32)


def dot_nt(a, b):
    return lax.dot_general(a, b, (((1,), (1,)), ((), ())), preferred_element_type=F32)


def dot_tn(a, b):
    return lax.dot_general(a, b, (((0,), (0,)), ((), ())), preferred_element_type=F32)


def attention_probs(q, k, bias, scale):
    scores = dot_nt(q, k) * scale
    if bias is not None:
        scores = scores + bias
    exponent = jnp.exp(scores - jnp.max(scores, axis=-1, keepdims=True))
    return exponent / jnp.sum(exponent, axis=-1, keepdims=True)


def attend_kernel(heads, scale, qkv_ref, bias_ref, out_ref):
    width = heads * HEAD_DIM
    bias = None if bias_ref is None else bias_ref[...]
    rows = qkv_ref.size // (3 * width)

    def load(part, h):
        lo = part * width + h * HEAD_DIM
        if len(qkv_ref.shape) == 2:
            return qkv_ref[:, lo : lo + HEAD_DIM]
        return qkv_ref[:, :, lo : lo + HEAD_DIM].astype(F32).reshape(rows, HEAD_DIM).astype(BF16)

    done = []
    for h in range(heads):
        p = attention_probs(load(0, h), load(1, h), bias, scale)
        done.append(dot_nn(p.astype(BF16), load(2, h)))
    out = jnp.concatenate(done, axis=1)
    if len(out_ref.shape) == 2:
        out_ref[...] = out.astype(BF16)
    else:
        out_ref[...] = out.reshape(out_ref.shape).astype(BF16)


def attend_back_kernel(heads, scale, qkv_ref, grad_ref, bias_ref, out_ref):
    width = heads * HEAD_DIM
    bias = None if bias_ref is None else bias_ref[...]
    rows = qkv_ref.size // (3 * width)

    def load(ref, lo):
        if len(ref.shape) == 2:
            return ref[:, lo : lo + HEAD_DIM]
        return ref[:, :, lo : lo + HEAD_DIM].astype(F32).reshape(rows, HEAD_DIM).astype(BF16)

    parts = ([], [], [])
    for h in range(heads):
        q = load(qkv_ref, h * HEAD_DIM)
        k = load(qkv_ref, width + h * HEAD_DIM)
        v = load(qkv_ref, 2 * width + h * HEAD_DIM)
        g = load(grad_ref, h * HEAD_DIM)
        p = attention_probs(q, k, bias, scale)
        dp = dot_nt(g, v)
        ds = (p * (dp - jnp.sum(p * dp, axis=-1, keepdims=True))).astype(BF16)
        parts[0].append(dot_nn(ds, k) * scale)
        parts[1].append(dot_tn(ds, q) * scale)
        parts[2].append(dot_tn(p.astype(BF16), g))
    out = jnp.concatenate(parts[0] + parts[1] + parts[2], axis=1)
    if len(out_ref.shape) == 2:
        out_ref[...] = out.astype(BF16)
    else:
        out_ref[...] = out.reshape(out_ref.shape).astype(BF16)


def attention_cost(groups, rows, heads, products):
    return pl.CostEstimate(
        flops=2 * products * groups * heads * rows * rows * HEAD_DIM,
        transcendentals=groups * heads * rows * rows,
        bytes_accessed=2 * groups * rows * heads * HEAD_DIM * 2 * products,
    )


def space_attend(qkv, frames, patches, heads, scale):
    width = heads * HEAD_DIM
    return pl.pallas_call(
        lambda q, o: attend_kernel(heads, scale, q, None, o),
        grid=(frames,),
        in_specs=[pl.BlockSpec((patches, 3 * width), lambda i: (i, 0))],
        out_specs=pl.BlockSpec((patches, width), lambda i: (i, 0)),
        out_shape=jax.ShapeDtypeStruct((frames * patches, width), BF16),
        cost_estimate=attention_cost(frames, patches, heads, 2),
        name="space_attend",
    )(qkv)


def space_attend_back(qkv, grad, frames, patches, heads, scale):
    width = heads * HEAD_DIM
    return pl.pallas_call(
        lambda q, g, o: attend_back_kernel(heads, scale, q, g, None, o),
        grid=(frames,),
        in_specs=[
            pl.BlockSpec((patches, 3 * width), lambda i: (i, 0)),
            pl.BlockSpec((patches, width), lambda i: (i, 0)),
        ],
        out_specs=pl.BlockSpec((patches, 3 * width), lambda i: (i, 0)),
        out_shape=jax.ShapeDtypeStruct((frames * patches, 3 * width), BF16),
        cost_estimate=attention_cost(frames, patches, heads, 5),
        name="space_attend_back",
    )(qkv, grad)


GROUP = 8


def time_attend(qkv, bias, frames, patches, heads, scale):
    width = heads * HEAD_DIM
    rows = frames * GROUP
    return pl.pallas_call(
        lambda q, b, o: attend_kernel(heads, scale, q, b, o),
        grid=(patches // GROUP,),
        in_specs=[
            pl.BlockSpec((frames, GROUP, 3 * width), lambda i: (0, i, 0)),
            pl.BlockSpec((rows, rows), lambda i: (0, 0)),
        ],
        out_specs=pl.BlockSpec((frames, GROUP, width), lambda i: (0, i, 0)),
        out_shape=jax.ShapeDtypeStruct((frames, patches, width), BF16),
        cost_estimate=attention_cost(patches // GROUP, rows, heads, 2),
        name="time_attend",
    )(qkv.reshape(frames, patches, 3 * width), bias).reshape(frames * patches, width)


def time_attend_back(qkv, grad, bias, frames, patches, heads, scale):
    width = heads * HEAD_DIM
    rows = frames * GROUP
    return pl.pallas_call(
        lambda q, g, b, o: attend_back_kernel(heads, scale, q, g, b, o),
        grid=(patches // GROUP,),
        in_specs=[
            pl.BlockSpec((frames, GROUP, 3 * width), lambda i: (0, i, 0)),
            pl.BlockSpec((frames, GROUP, width), lambda i: (0, i, 0)),
            pl.BlockSpec((rows, rows), lambda i: (0, 0)),
        ],
        out_specs=pl.BlockSpec((frames, GROUP, 3 * width), lambda i: (0, i, 0)),
        out_shape=jax.ShapeDtypeStruct((frames, patches, 3 * width), BF16),
        cost_estimate=attention_cost(patches // GROUP, rows, heads, 5),
        name="time_attend_back",
    )(
        qkv.reshape(frames, patches, 3 * width), grad.reshape(frames, patches, width), bias
    ).reshape(frames * patches, 3 * width)


def norm_rows(resid):
    mean = jnp.mean(resid, axis=-1, keepdims=True)
    centered = resid - mean
    inverse = lax.rsqrt(jnp.mean(centered * centered, axis=-1, keepdims=True) + eps_norm)
    return (centered * inverse, inverse)


def norm_rows_back(grad, standardized, inverse, gain):
    gain_grad = jnp.sum(grad * standardized, axis=0)
    inner = grad * gain
    mean = jnp.mean(inner, axis=-1, keepdims=True)
    along = jnp.mean(inner * standardized, axis=-1, keepdims=True)
    return ((inner - mean - standardized * along) * inverse, gain_grad)


def swap_y(v):
    return jnp.concatenate(
        [v[:, BLK : 2 * BLK], v[:, :BLK], v[:, 3 * BLK :], v[:, 2 * BLK : 3 * BLK]], axis=1
    )


def cols(parts):
    return jnp.concatenate(parts, axis=1)


def rows_of(parts):
    return jnp.concatenate(parts, axis=0)


def token_parallel(
    tokens,
    cotangent,
    ratio,
    priority,
    frame_order,
    mask_embed,
    gains,
    qkv_space,
    out_space,
    qkv_time,
    out_time,
    w_in,
    w_out,
):
    scale = 1.0 / math.sqrt(HEAD_DIM)
    y = lax.axis_index("tm")
    x = lax.axis_index("clip") // 2
    c = lax.axis_index("clip") % 2
    z = lax.axis_index("mp")
    patches = tokens.shape[2]
    width = qkv_space.shape[0]
    frames_own = tokens.shape[0] * tokens.shape[1] // 4
    frames_all = frame_order.shape[1]
    own = frames_own * patches
    hidden_own = w_in.shape[1] // 2
    block_at = [2 * (y ^ (i & 1)) + (x ^ (i >> 1)) for i in range(4)]

    def rel_rows(w):
        return rows_of([lax.dynamic_slice_in_dim(w, b * BLK, BLK, 0) for b in block_at])

    def to_absolute(v):
        v = jnp.swapaxes(v.reshape(-1, 2, 2, BLK), 1, 2)
        v = jnp.where(y == 1, v[:, ::-1], v)
        return jnp.where(x == 1, v[:, :, ::-1], v).reshape(-1, width)

    k_own = 2 * (z % 2) + c

    def gather_rows(v, extra):
        pieces = v.reshape(4, own, BLK)
        landed = []
        for r in range(4):
            piece = lax.dynamic_index_in_dim(pieces, z ^ r, 0, keepdims=False)
            if extra is not None:
                piece = rows_of([piece, extra])
            landed.append(lax.ppermute(piece, AXES, spread_pairs(r)))
        landed = jnp.stack(landed)
        return cols(
            [lax.dynamic_index_in_dim(landed, k_own ^ b, 0, keepdims=False) for b in block_at]
        )

    def return_rows(v):
        pieces = jnp.stack([v[:, i * BLK : (i + 1) * BLK] for i in range(4)])
        landed = []
        for r in range(4):
            block = k_own ^ r
            place = 2 * ((block % 2) ^ x) + ((block // 2) ^ y)
            piece = lax.dynamic_index_in_dim(pieces, place, 0, keepdims=False)
            landed.append(lax.ppermute(piece, AXES, [(b, a) for a, b in spread_pairs(r)]))
        landed = jnp.stack(landed)
        return jnp.stack(
            [lax.dynamic_index_in_dim(landed, k ^ z, 0, keepdims=False) for k in range(4)]
        ).reshape(tokens.shape)

    vectors = rows_of([mask_embed[None], gains, jnp.zeros((4, BLK), BF16)])
    arrived = gather_rows(tokens, vectors)
    source = arrived[:own].astype(F32)
    embed_row = arrived[own : own + 1].astype(F32)
    gain = [arrived[own + 1 + i : own + 2 + i].astype(F32) for i in range(3)]
    upstream = gather_rows(cotangent, None)

    masked_here = (priority < ratio[:, None, None]).astype(jnp.int32).reshape(2, -1)
    info = cols([masked_here, frame_order])
    info = jnp.where(z // 2 == c, info, hop_c(info))
    info = lax.dynamic_index_in_dim(info, z % 2, 0, keepdims=False)
    masked = lax.dynamic_slice_in_dim(info, c * own, own, 0)[:, None] != 0
    order = info[2 * own :].reshape(2, 2, frames_own)
    order = jnp.where(y == 1, order[::-1], order)
    order = jnp.where(c == 1, order[:, ::-1], order).swapaxes(0, 1).reshape(frames_all)
    order = jnp.repeat(order, GROUP)
    patch = jnp.arange(frames_all * GROUP) % GROUP
    visible = (order[None, :] <= order[:, None]) & (patch[None, :] == patch[:, None])
    bias = jnp.where(visible, 0.0, -1e30).astype(F32)

    def fetch(mine):
        landed = cols([hop_z(mine, -r) for r in (1, 2, 3)])
        return landed

    half = qkv_space.shape[2] // 2
    sp_qkv = rel_rows(lax.dynamic_slice_in_dim(qkv_space, c * half, half, 2))
    sp_out = rel_rows(lax.dynamic_slice_in_dim(out_space, c * half, half, 0).T)
    sp_own = cols([sp_qkv.reshape(width, -1), sp_out])
    sp_far = fetch(sp_own[:BLK])
    sp_far = rows_of([sp_far, hop_y(sp_far)])
    sp_far = rows_of([sp_far, hop_x(sp_far)])
    sp_all = [sp_own] + [sp_far[:, r * 4 * half : (r + 1) * 4 * half] for r in range(3)]
    ws_qkv = cols([w[:, j * half : (j + 1) * half] for j in range(3) for w in sp_all])
    ws_out = cols([w[:, 3 * half :] for w in sp_all])

    head = (2 * y + c) * HEAD_DIM
    ti_qkv = rel_rows(lax.dynamic_slice_in_dim(qkv_time, head, HEAD_DIM, 2))
    ti_out = rel_rows(lax.dynamic_slice_in_dim(out_time, head, HEAD_DIM, 0).T)
    ti_own = cols([ti_qkv.reshape(width, -1), ti_out])
    ti_far = fetch(ti_own[: 2 * BLK])
    ti_far = rows_of([ti_far, hop_x(ti_far)])
    ti_all = [ti_own] + [ti_far[:, r * 4 * HEAD_DIM : (r + 1) * 4 * HEAD_DIM] for r in range(3)]
    wt_qkv = cols([w[:, j * HEAD_DIM : (j + 1) * HEAD_DIM] for j in range(3) for w in ti_all])
    wt_out = cols([w[:, 3 * HEAD_DIM :] for w in ti_all])

    ff_in = rel_rows(lax.dynamic_slice_in_dim(w_in, c * hidden_own, hidden_own, 1))
    ff_out = rel_rows(lax.dynamic_slice_in_dim(w_out, c * hidden_own, hidden_own, 0).T)
    far = []
    for w in (ff_in, ff_out):
        w_far = fetch(w[:BLK])
        w_far = rows_of([w_far, hop_y(w_far)])
        w_far = rows_of([w_far, hop_x(w_far)])
        far.append(cols([w, w_far]))
    wf_in, wf_out = far

    def pair_gather(v):
        return rows_of([v, hop_c(v)])

    def pair_scatter(v):
        return v[:own] + hop_c(v[own:].astype(BF16)).astype(F32)

    def quad_gather(v):
        both = rows_of([v, hop_y(swap_y(v))])
        return rows_of([both, hop_c(both)])

    def quad_scatter(v):
        both = v[: 2 * own] + hop_c(v[2 * own :].astype(BF16)).astype(F32)
        return both[:own] + hop_y(swap_y(both[own:].astype(BF16))).astype(F32)

    heads_s = 4 * half // HEAD_DIM
    heads_t = 4
    frames_pair = 2 * frames_own
    resid0 = jnp.where(masked, embed_row, source)
    std0, inv0 = norm_rows(resid0)
    normed0 = pair_gather((std0 * gain[0]).astype(BF16))
    joined0 = dot_nn(normed0, ws_qkv).astype(BF16)
    mixed0 = space_attend(joined0, frames_pair, patches, heads_s, scale)
    resid1 = resid0 + pair_scatter(dot_nt(mixed0, ws_out))
    std1, inv1 = norm_rows(resid1)
    normed1 = quad_gather((std1 * gain[1]).astype(BF16))
    joined1 = dot_nn(normed1, wt_qkv).astype(BF16)
    mixed1 = time_attend(joined1, bias, frames_all, patches, heads_t, scale)
    resid2 = resid1 + quad_scatter(dot_nt(mixed1, wt_out))
    std2, inv2 = norm_rows(resid2)
    normed2 = pair_gather((std2 * gain[2]).astype(BF16))
    inner = dot_nn(normed2, wf_in)
    activated, gelu_pull = jax.vjp(gelu_tanh, inner)
    hidden = activated.astype(BF16)
    block_out = return_rows((resid2 + pair_scatter(dot_nt(hidden, wf_out))).astype(BF16))

    def reduce_plane(lhs, rhs):
        sent = hop_x(dot_tn(lhs[:, 2 * BLK :], rhs).astype(BF16))
        kept = dot_tn(lhs[:, : 2 * BLK], rhs) + sent.astype(F32)
        return kept

    def reduce_y(kept):
        return kept[:BLK] + hop_y(kept[BLK:].astype(BF16)).astype(F32)

    def reduce_z(pieces):
        total = pieces[0]
        for r in (1, 2, 3):
            total = total + hop_z(pieces[r].astype(BF16), r).astype(F32)
        return total

    def swap_c(total):
        rows = BLK // 2
        kept = lax.dynamic_slice_in_dim(total, c * rows, rows, 0)
        sent = hop_c(lax.dynamic_slice_in_dim(total, (1 - c) * rows, rows, 0).astype(BF16))
        return (kept, sent.astype(F32))

    def by_core(kept, landed):
        return jnp.where(c == 0, jnp.concatenate([kept, landed], -1), jnp.concatenate([landed, kept], -1))

    grad3 = jnp.where(masked, upstream, jnp.zeros((), BF16))
    gb3 = pair_gather(grad3)
    grad_inner = gelu_pull(dot_nn(gb3, wf_out))[0].astype(BF16)
    g_w_out = reduce_y(reduce_plane(gb3, hidden))
    g_w_out = reduce_z([g_w_out[:, r * hidden_own : (r + 1) * hidden_own] for r in range(4)])
    g_w_in = reduce_y(reduce_plane(normed2, grad_inner))
    g_w_in = reduce_z([g_w_in[:, r * hidden_own : (r + 1) * hidden_own] for r in range(4)])
    back2, gain_grad2 = norm_rows_back(pair_scatter(dot_nt(grad_inner, wf_in)), std2, inv2, gain[2])
    grad2 = grad3.astype(F32) + back2

    gb2 = quad_gather(grad2.astype(BF16))
    dmixed1 = dot_nn(gb2, wt_out).astype(BF16)
    djoined1 = time_attend_back(joined1, dmixed1, bias, frames_all, patches, heads_t, scale)
    g_t_out = reduce_plane(gb2, mixed1)
    g_t_qkv = reduce_plane(normed1, djoined1)
    span = heads_t * HEAD_DIM
    g_time = reduce_z(
        [
            cols(
                [g_t_qkv[:, j * span + r * HEAD_DIM : j * span + (r + 1) * HEAD_DIM] for j in range(3)]
                + [g_t_out[:, r * HEAD_DIM : (r + 1) * HEAD_DIM]]
            )
            for r in range(4)
        ]
    )
    back1, gain_grad1 = norm_rows_back(quad_scatter(dot_nt(djoined1, wt_qkv)), std1, inv1, gain[1])
    grad1 = grad2 + back1

    gb1 = pair_gather(grad1.astype(BF16))
    dmixed0 = dot_nn(gb1, ws_out).astype(BF16)
    djoined0 = space_attend_back(joined0, dmixed0, frames_pair, patches, heads_s, scale)
    g_s_out = reduce_y(reduce_plane(gb1, mixed0))
    g_s_qkv = reduce_y(reduce_plane(normed0, djoined0))
    span = 4 * half
    g_space = reduce_z(
        [
            cols(
                [g_s_qkv[:, j * span + r * half : j * span + (r + 1) * half] for j in range(3)]
                + [g_s_out[:, r * half : (r + 1) * half]]
            )
            for r in range(4)
        ]
    )
    back0, gain_grad0 = norm_rows_back(pair_scatter(dot_nt(djoined0, ws_qkv)), std0, inv0, gain[0])
    grad0 = grad1 + back0
    grad_tokens = return_rows(jnp.where(masked, 0.0, grad0).astype(BF16)).astype(F32)
    grad_embed = jnp.sum(jnp.where(masked, grad0, 0.0), axis=0)
    small = lax.psum(to_absolute(jnp.stack([gain_grad0, gain_grad1, gain_grad2, grad_embed])), AXES)
    small = lax.dynamic_slice_in_dim(small, z * BLK, BLK, 1)

    rows = BLK // 2
    kept, landed = swap_c(g_space)
    grad_qkv_space = by_core(
        kept[:, : 3 * half].reshape(rows, 3, half), landed[:, : 3 * half].reshape(rows, 3, half)
    )
    grad_out_space = by_core(kept[:, 3 * half :], landed[:, 3 * half :]).T
    kept, landed = swap_c(cols([g_w_in, g_w_out]))
    grad_w_in = by_core(kept[:, :hidden_own], landed[:, :hidden_own])
    grad_w_out = by_core(kept[:, hidden_own:], landed[:, hidden_own:]).T
    both = cols([g_time[:BLK], hop_y(g_time[BLK:].astype(BF16)).astype(F32)])
    kept, landed = swap_c(both)
    quad = jnp.stack([kept, landed], 1).reshape(rows, 2, 2, 4, HEAD_DIM)
    quad = jnp.where(c == 1, quad[:, ::-1], quad)
    quad = jnp.where(y == 1, quad[:, :, ::-1], quad)
    quad = jnp.transpose(quad, (0, 3, 2, 1, 4)).reshape(rows, 4, 4 * HEAD_DIM)
    grad_qkv_time = quad[:, :3]
    grad_out_time = quad[:, 3].T
    return (
        block_out,
        grad_tokens,
        small[3],
        small[:3],
        grad_qkv_space,
        grad_out_space,
        grad_qkv_time,
        grad_out_time,
        grad_w_in,
        grad_w_out,
    )


def solution(mesh):
    sizes = (mesh.shape["tm"], mesh.shape["clip"], mesh.shape["mp"])
    return jax.shard_map(
        token_parallel if sizes == (2, 4, 4) else shards,
        mesh=mesh,
        in_specs=(
            P("clip", "tm", None, "mp"),
            P("clip", "tm", None, "mp"),
            P("clip"),
            P("clip", "tm", None),
            P("clip", None),
            P("mp"),
            P(None, "mp"),
            P(None, None, "mp"),
            P("mp", None),
            P(None, None, "mp"),
            P("mp", None),
            P(None, "mp"),
            P("mp", None),
        ),
        out_specs=(
            P("clip", "tm", None, "mp"),
            P("clip", "tm", None, "mp"),
            P("mp"),
            P(None, "mp"),
            P(("tm", "clip"), None, "mp"),
            P("mp", ("tm", "clip")),
            P(("tm", "clip"), None, "mp"),
            P("mp", ("tm", "clip")),
            P(("tm", "clip"), "mp"),
            P("mp", ("tm", "clip")),
        ),
        check_vma=False,
    )
```

```python
import math

import jax
import jax.numpy as jnp
from jax import lax
from jax.experimental import pallas as pl
from jax.experimental.pallas import tpu as pltpu
from jax.sharding import PartitionSpec as P

HEAD_DIM = 64
MICRO = 2


eps_norm = 1e-05


def gelu_tanh(values):
    return jax.nn.gelu(values, approximate=True)


def norm_forward_pass(residual_stream, gain_coefficients, complete_width):
    reduced_totals = lax.psum(
        (jnp.sum(residual_stream, axis=-1), jnp.sum(residual_stream * residual_stream, axis=-1)),
        "mp",
    )
    centered_rows = reduced_totals[0] / complete_width
    spread = reduced_totals[1] / complete_width - centered_rows * centered_rows
    inverse_scale = lax.rsqrt(spread + eps_norm)
    standardized_rows = (residual_stream - centered_rows[:, None]) * inverse_scale[:, None]
    shard_rows = (standardized_rows * gain_coefficients).astype(jnp.bfloat16)
    normalized_rows = lax.all_gather(shard_rows, "mp", axis=1, tiled=True)
    return (normalized_rows, standardized_rows, inverse_scale)


def norm_reverse_pass(
    normalized_gradient, standardized_rows, inverse_scale, gain_coefficients, complete_width
):
    gain_gradient = jnp.sum(normalized_gradient * standardized_rows, axis=0)
    standardized_gradient = normalized_gradient * gain_coefficients
    reduced_totals = lax.psum(
        (
            jnp.sum(standardized_gradient, axis=-1),
            jnp.sum(standardized_gradient * standardized_rows, axis=-1),
        ),
        "mp",
    )
    grad_resid = (
        standardized_gradient
        - reduced_totals[0][:, None] / complete_width
        - standardized_rows * (reduced_totals[1][:, None] / complete_width)
    ) * inverse_scale[:, None]
    return (grad_resid, gain_gradient)


def sum_features(grad_full):
    return lax.psum_scatter(
        grad_full.astype(jnp.bfloat16), "mp", scatter_dimension=1, tiled=True
    ).astype(jnp.float32)


def branch_out(hidden, weight):
    partial_rows = jnp.dot(hidden, weight, preferred_element_type=jnp.float32)
    return lax.psum_scatter(partial_rows, "mp", scatter_dimension=1, tiled=True)


def branch_back(grad_resid, hidden, weight):
    grad_rows = lax.all_gather(grad_resid.astype(jnp.bfloat16), "mp", axis=1, tiled=True)
    weight_grad = jnp.einsum("rk,rd->kd", hidden, grad_rows, preferred_element_type=jnp.float32)
    grad_hidden = jnp.einsum("rd,kd->rk", grad_rows, weight, preferred_element_type=jnp.float32)
    return (grad_hidden, weight_grad)


def qkv_back(normalized_rows, grad_joined, weight):
    weight_grad = jnp.einsum(
        "rd,trk->dtk", normalized_rows, grad_joined, preferred_element_type=jnp.float32
    )
    grad_full = jnp.einsum("trk,dtk->rd", grad_joined, weight, preferred_element_type=jnp.float32)
    return (weight_grad, sum_features(grad_full))


def reduce_grads(local_grads, small_grads):
    reduced = (
        lax.psum_scatter(local_grads[0], ("tm", "clip"), scatter_dimension=0, tiled=True),
        lax.psum_scatter(local_grads[1], ("tm", "clip"), scatter_dimension=1, tiled=True),
        lax.psum_scatter(local_grads[2], ("tm", "clip"), scatter_dimension=0, tiled=True),
        lax.psum_scatter(local_grads[3], ("tm", "clip"), scatter_dimension=1, tiled=True),
        lax.psum_scatter(local_grads[4], ("tm", "clip"), scatter_dimension=0, tiled=True),
        lax.psum_scatter(local_grads[5], ("tm", "clip"), scatter_dimension=1, tiled=True),
    )
    reduced_small = lax.psum((small_grads[0], small_grads[1]), ("tm", "clip"))
    return (reduced, reduced_small)


def space_forward(normalized_rows, weight, frame_count, patches, heads_local, scale):
    joined = jnp.einsum(
        "rd,dtk->trk", normalized_rows, weight, preferred_element_type=jnp.float32
    ).astype(jnp.bfloat16)
    shape_heads = (frame_count, patches, heads_local, HEAD_DIM)
    scores = (
        jnp.einsum(
            "bshd,bthd->bhst",
            joined[0].reshape(shape_heads),
            joined[1].reshape(shape_heads),
            preferred_element_type=jnp.float32,
        )
        * scale
    )
    highest = jnp.max(scores, axis=-1, keepdims=True)
    exponent = jnp.exp(scores - highest)
    reduced_totals = jnp.sum(exponent, axis=-1, keepdims=True)
    log_total = highest + jnp.log(reduced_totals)
    attention = (exponent / reduced_totals).astype(jnp.bfloat16)
    mixed = jnp.einsum(
        "bhst,bthd->bshd",
        attention,
        joined[2].reshape(shape_heads),
        preferred_element_type=jnp.float32,
    )
    return (
        joined,
        log_total,
        mixed.astype(jnp.bfloat16).reshape(frame_count * patches, heads_local * HEAD_DIM),
    )


def space_backward(grad_mixed, joined, log_total, frame_count, patches, heads_local, scale):
    shape_heads = (frame_count, patches, heads_local, HEAD_DIM)
    queries = joined[0].reshape(shape_heads)
    key_rows = joined[1].reshape(shape_heads)
    values = joined[2].reshape(shape_heads)
    grad_out = grad_mixed.reshape(shape_heads)
    scores = (
        jnp.einsum("bshd,bthd->bhst", queries, key_rows, preferred_element_type=jnp.float32) * scale
    )
    attention = jnp.exp(scores - log_total)
    grad_values = jnp.einsum(
        "bhst,bshd->bthd",
        attention.astype(jnp.bfloat16),
        grad_out,
        preferred_element_type=jnp.float32,
    )
    grad_att = jnp.einsum("bshd,bthd->bhst", grad_out, values, preferred_element_type=jnp.float32)
    grad_scores = (
        attention * (grad_att - jnp.sum(attention * grad_att, axis=-1, keepdims=True))
    ).astype(jnp.bfloat16)
    grad_queries = (
        jnp.einsum("bhst,bthd->bshd", grad_scores, key_rows, preferred_element_type=jnp.float32)
        * scale
    )
    grad_keys = (
        jnp.einsum("bhst,bshd->bthd", grad_scores, queries, preferred_element_type=jnp.float32)
        * scale
    )
    row_count = frame_count * patches
    stacked = jnp.stack(
        [
            grad_queries.reshape(row_count, -1),
            grad_keys.reshape(row_count, -1),
            grad_values.reshape(row_count, -1),
        ]
    )
    return stacked.astype(jnp.bfloat16)


def time_scores(queries, keys_all, visible, scale):
    scores = (
        jnp.einsum("cfshd,cgshd->chfgs", queries, keys_all, preferred_element_type=jnp.float32)
        * scale
    )
    return jnp.where(visible, scores, -1e30)


def time_forward(queries, keys_all, values_all, visible, scale):
    scores = time_scores(queries, keys_all, visible, scale)
    highest = jnp.max(scores, axis=3, keepdims=True)
    exponent = jnp.exp(scores - highest)
    reduced_totals = jnp.sum(exponent, axis=3, keepdims=True)
    log_total = highest + jnp.log(reduced_totals)
    attention = (exponent / reduced_totals).astype(jnp.bfloat16)
    mixed = jnp.einsum(
        "chfgs,cgshd->cfshd", attention, values_all, preferred_element_type=jnp.float32
    )
    return (log_total, mixed.astype(jnp.bfloat16))


def time_backward(grad_mixed, queries, keys_all, values_all, visible, log_total, scale):
    grad_out = grad_mixed.reshape(queries.shape)
    scores = time_scores(queries, keys_all, visible, scale)
    attention = jnp.exp(scores - log_total)
    grad_values = jnp.einsum(
        "chfgs,cfshd->cgshd",
        attention.astype(jnp.bfloat16),
        grad_out,
        preferred_element_type=jnp.float32,
    )
    grad_att = jnp.einsum(
        "cfshd,cgshd->chfgs", grad_out, values_all, preferred_element_type=jnp.float32
    )
    grad_scores = (
        attention * (grad_att - jnp.sum(attention * grad_att, axis=3, keepdims=True))
    ).astype(jnp.bfloat16)
    grad_queries = (
        jnp.einsum("chfgs,cgshd->cfshd", grad_scores, keys_all, preferred_element_type=jnp.float32)
        * scale
    )
    grad_keys = (
        jnp.einsum("chfgs,cfshd->cgshd", grad_scores, queries, preferred_element_type=jnp.float32)
        * scale
    )
    return (grad_queries, grad_keys, grad_values)


def shards(
    tokens,
    cotangent,
    ratio,
    priority,
    frame_order,
    mask_embed,
    gains,
    qkv_space,
    out_space,
    qkv_time,
    out_time,
    w_in,
    w_out,
):
    scale = 1.0 / math.sqrt(HEAD_DIM)
    clips_local = tokens.shape[0] // MICRO
    frames_local = tokens.shape[1]
    patches = tokens.shape[2]
    cols_local = tokens.shape[3]
    frames_all = frame_order.shape[1]
    hidden_width = qkv_space.shape[0]
    joined_local = qkv_space.shape[2]
    heads_local = joined_local // HEAD_DIM
    row_count = clips_local * frames_local * patches
    gain_broadcast = gains.astype(jnp.float32)
    embed_row = mask_embed.astype(jnp.float32)
    first_frame = lax.axis_index("tm") * frames_local
    shape_local = (clips_local, frames_local, patches, joined_local)
    shape_heads = (clips_local, frames_local, patches, heads_local, HEAD_DIM)
    shape_all = (clips_local, frames_all, patches, heads_local, HEAD_DIM)
    outputs = []
    input_grads = []
    weight_total = None
    small_total = None
    for batch_index in range(MICRO):
        lower = batch_index * clips_local
        upper = lower + clips_local
        source = tokens[lower:upper].reshape(row_count, cols_local).astype(jnp.float32)
        upstream = cotangent[lower:upper].reshape(row_count, cols_local).astype(jnp.float32)
        masked = (priority[lower:upper] < ratio[lower:upper][:, None, None]).reshape(row_count)
        order_rows = frame_order[lower:upper]
        residual_stream0 = jnp.where(masked[:, None], embed_row[None, :], source)
        normalized_rows0, standardized_rows0, inverse_deviation0 = norm_forward_pass(
            residual_stream0, gain_broadcast[0], hidden_width
        )
        joined0, total0, mixed0 = space_forward(
            normalized_rows0, qkv_space, clips_local * frames_local, patches, heads_local, scale
        )
        residual_stream1 = residual_stream0 + branch_out(mixed0, out_space)
        normalized_rows1, standardized_rows1, inverse_deviation1 = norm_forward_pass(
            residual_stream1, gain_broadcast[1], hidden_width
        )
        joined1 = jnp.einsum(
            "rd,dtk->trk", normalized_rows1, qkv_time, preferred_element_type=jnp.float32
        ).astype(jnp.bfloat16)
        queries_local = joined1[0].reshape(shape_local)
        keys_local = joined1[1].reshape(shape_local)
        values_local = joined1[2].reshape(shape_local)
        keys_all, values_all = (
            lax.all_gather(keys_local, "tm", axis=1, tiled=True),
            lax.all_gather(values_local, "tm", axis=1, tiled=True),
        )
        query_order = lax.dynamic_slice_in_dim(order_rows, first_frame, frames_local, axis=1)
        time_visible = (order_rows[:, None, :] <= query_order[:, :, None])[:, None, :, :, None]
        time_q = queries_local.reshape(shape_heads)
        time_k = keys_all.reshape(shape_all)
        time_v = values_all.reshape(shape_all)
        total1, mixed_frames = time_forward(time_q, time_k, time_v, time_visible, scale)
        mixed1 = mixed_frames.reshape(row_count, joined_local)
        residual_stream2 = residual_stream1 + branch_out(mixed1, out_time)
        normalized_rows2, standardized_rows2, inverse_deviation2 = norm_forward_pass(
            residual_stream2, gain_broadcast[2], hidden_width
        )
        projected = jnp.dot(normalized_rows2, w_in, preferred_element_type=jnp.float32)
        activated, gelu_pull = jax.vjp(gelu_tanh, projected)
        hidden = activated.astype(jnp.bfloat16)
        resid3 = residual_stream2 + branch_out(hidden, w_out)
        outputs.append(
            resid3.astype(jnp.bfloat16).reshape(clips_local, frames_local, patches, cols_local)
        )
        grad3 = jnp.where(masked[:, None], upstream, 0.0)
        grad_hidden, grad_w_out = branch_back(grad3, hidden, w_out)
        grad_inner = gelu_pull(grad_hidden)[0].astype(jnp.bfloat16)
        grad_w_in = jnp.einsum(
            "rd,rk->dk", normalized_rows2, grad_inner, preferred_element_type=jnp.float32
        )
        normalized_gradient2 = sum_features(
            jnp.einsum("rk,dk->rd", grad_inner, w_in, preferred_element_type=jnp.float32)
        )
        backward_third, gain_gradient2 = norm_reverse_pass(
            normalized_gradient2,
            standardized_rows2,
            inverse_deviation2,
            gain_broadcast[2],
            hidden_width,
        )
        grad2 = grad3 + backward_third
        grad_mixed1, grad_out_time = branch_back(grad2, mixed1, out_time)
        grad_mixed_low = grad_mixed1.astype(jnp.bfloat16).reshape(shape_local)
        grad_queries, grad_keys, grad_values = time_backward(
            grad_mixed_low, time_q, time_k, time_v, time_visible, total1, scale
        )
        key_part, value_part = (
            lax.psum_scatter(
                grad_keys.reshape(clips_local, frames_all, patches, joined_local).astype(
                    jnp.bfloat16
                ),
                "tm",
                scatter_dimension=1,
                tiled=True,
            ).astype(jnp.float32),
            lax.psum_scatter(
                grad_values.reshape(clips_local, frames_all, patches, joined_local).astype(
                    jnp.bfloat16
                ),
                "tm",
                scatter_dimension=1,
                tiled=True,
            ).astype(jnp.float32),
        )
        grad_joined1 = jnp.stack(
            [
                grad_queries.reshape(row_count, joined_local),
                key_part.reshape(row_count, joined_local),
                value_part.reshape(row_count, joined_local),
            ]
        ).astype(jnp.bfloat16)
        grad_qkv_time, normalized_gradient1 = qkv_back(normalized_rows1, grad_joined1, qkv_time)
        backward_second, gain_gradient1 = norm_reverse_pass(
            normalized_gradient1,
            standardized_rows1,
            inverse_deviation1,
            gain_broadcast[1],
            hidden_width,
        )
        grad1 = grad2 + backward_second
        grad_mixed0, grad_out_space = branch_back(grad1, mixed0, out_space)
        grad_joined0 = space_backward(
            grad_mixed0.astype(jnp.bfloat16),
            joined0,
            total0,
            clips_local * frames_local,
            patches,
            heads_local,
            scale,
        )
        grad_qkv_space, normalized_gradient0 = qkv_back(normalized_rows0, grad_joined0, qkv_space)
        backward_first, gain_gradient0 = norm_reverse_pass(
            normalized_gradient0,
            standardized_rows0,
            inverse_deviation0,
            gain_broadcast[0],
            hidden_width,
        )
        grad0 = grad1 + backward_first
        input_grads.append(
            jnp.where(masked[:, None], 0.0, grad0).reshape(
                clips_local, frames_local, patches, cols_local
            )
        )
        grad_embed = jnp.sum(jnp.where(masked[:, None], grad0, 0.0), axis=0)
        gain_grads = jnp.stack([gain_gradient0, gain_gradient1, gain_gradient2])
        local_grads = (
            grad_qkv_space,
            grad_out_space,
            grad_qkv_time,
            grad_out_time,
            grad_w_in,
            grad_w_out,
        )
        small_grads = (gain_grads, grad_embed)
        reduced, reduced_small = reduce_grads(local_grads, small_grads)
        if weight_total is None:
            weight_total = reduced
            small_total = reduced_small
        else:
            weight_total = tuple((total + grad for total, grad in zip(weight_total, reduced)))
            small_total = tuple((total + grad for total, grad in zip(small_total, reduced_small)))
    return (
        jnp.concatenate(outputs, axis=0),
        jnp.concatenate(input_grads, axis=0),
        small_total[1],
        small_total[0],
        weight_total[0],
        weight_total[1],
        weight_total[2],
        weight_total[3],
        weight_total[4],
        weight_total[5],
    )


AXES = ("tm", "x", "c", "mp")
F32 = jnp.float32
BF16 = jnp.bfloat16
BLK = 256
MESH = pl.DeviceIdType.MESH


def device_pairs(move):
    pairs = []
    for y in range(2):
        for x in range(2):
            for c in range(2):
                for z in range(4):
                    there = move(y, x, c, z)
                    pairs.append(tuple(((q[0] * 2 + q[1]) * 2 + q[2]) * 4 + q[3] for q in ((y, x, c, z), there)))
    return pairs


def hop_y(v):
    return lax.ppermute(v, AXES, device_pairs(lambda y, x, c, z: (1 - y, x, c, z)))


def hop_x(v):
    return lax.ppermute(v, AXES, device_pairs(lambda y, x, c, z: (y, 1 - x, c, z)))


def hop_c(v):
    return lax.ppermute(v, AXES, device_pairs(lambda y, x, c, z: (y, x, 1 - c, z)))


def hop_z(v, shift):
    return lax.ppermute(v, AXES, device_pairs(lambda y, x, c, z: (y, x, c, (z + shift) % 4)))


def spread_pairs(r):
    def move(y, x, c, z):
        k = z ^ r
        return (y, x, k & 1, 2 * c + (k >> 1))

    return device_pairs(move)


def arrive_kernel(
    tok, vec, mine, rows_out, vec_out, wq, wo,
    z_send, z_recv, y_send, y_recv, x_send, x_recv, p_send, p_recv, q_send, q_recv,
    t_send, t_recv, v_send, v_recv, local,
):
    y, x, c, z = (lax.axis_index(name) for name in AXES)
    half = wo.shape[1] // 4
    wide = 3 * half

    barrier = pltpu.get_barrier_semaphore()
    for dc in range(2):
        for dz in range(4):
            if dc or dz:
                peer = (y, x, (c + dc) % 2, (z + dz) % 4)
                pl.semaphore_signal(barrier, inc=1, device_id=peer, device_id_type=MESH)
    near_y, near_x = (1 - y, x, c, z), (y, 1 - x, c, z)
    for peer in (near_y, near_x):
        pl.semaphore_signal(barrier, inc=1, device_id=peer, device_id_type=MESH)
    pl.semaphore_wait(barrier, 9)

    def rows(dy, dx):
        return pl.ds(pl.multiple_of(BLK * (2 * ((y + dy) % 2) + (x + dx) % 2), BLK), BLK)

    def piece(dy, dx, r, split=False):
        s = (z + r) % 4
        at = pl.multiple_of(s * wide, half)
        out = wo.at[rows(dy, dx), pl.ds(pl.multiple_of(s * half, half), half)]
        if split:
            late = pl.multiple_of(s * wide + 2 * half, half)
            return (wq.at[rows(dy, dx), pl.ds(at, 2 * half)], wq.at[rows(dy, dx), pl.ds(late, half)], out)
        return (wq.at[rows(dy, dx), pl.ds(at, wide)], out)

    def copies(sources, targets, send, recv, peer):
        return [
            pltpu.make_async_remote_copy(
                src_ref=src, dst_ref=dst, send_sem=send.at[i], recv_sem=recv.at[i], device_id=peer, device_id_type=MESH
            )
            for i, (src, dst) in enumerate(zip(sources, targets))
        ]

    own_rows = rows(0, 0)
    own_slice = (mine.at[own_rows, pl.ds(0, wide)], mine.at[own_rows, pl.ds(wide, half)])

    def z_copies(right, step):
        if right:
            r = 0 if step == 0 else 4 - step
            peer, lands = (y, x, c, (z + 1) % 4), 3 - step
        else:
            r = step
            peer, lands = (y, x, c, (z + 3) % 4), step + 1
        target = piece(0, 0, r)
        source = own_slice if step == 0 else target
        return copies(source, target, z_send.at[int(right), step], z_recv.at[lands], peer)

    def y_copies(r):
        return copies(piece(0, 0, r), piece(0, 0, r), y_send.at[r], y_recv.at[r], near_y)

    def x_copies(r):
        return copies(piece(0, 0, r), piece(0, 0, r), x_send.at[r], x_recv.at[r], near_x)

    def corner_x(r):
        part = piece(1, 0, r, split=True)[:1]
        return copies(part, part, p_send.at[r], p_recv.at[r], near_x)

    def corner_y(r):
        part = piece(0, 1, r, split=True)[1:]
        return copies(part, part, q_send.at[r], q_recv.at[r], near_y)

    def start(all_copies):
        for copy in all_copies:
            copy.start()

    def landed(all_copies):
        for copy in all_copies:
            copy.wait_recv()

    def sent(all_copies):
        for copy in all_copies:
            copy.wait_send()

    def token_copies(k):
        peer = (y, x, k % 2, 2 * c + k // 2)
        at = pl.ds(pl.multiple_of(z * BLK, BLK), BLK)
        return [
            pltpu.make_async_remote_copy(
                src_ref=src, dst_ref=dst, send_sem=send.at[k], recv_sem=recv.at[z], device_id=peer, device_id_type=MESH
            )
            for src, dst, send, recv in (
                (tok.at[k], rows_out.at[:, at], t_send, t_recv),
                (vec, vec_out.at[:, at], v_send, v_recv),
            )
        ]

    def token_local(k):
        at = pl.ds(pl.multiple_of(z * BLK, BLK), BLK)
        return [
            pltpu.make_async_copy(tok.at[k], rows_out.at[:, at], local.at[2]),
            pltpu.make_async_copy(vec, vec_out.at[:, at], local.at[3]),
        ]

    def stays(k):
        return jnp.logical_and(2 * c + k // 2 == z, c == k % 2)

    def from_right(j):
        return z <= 2 - j

    def from_left(j):
        return z >= j + 1

    pl.when(z < 3)(lambda: start(z_copies(True, 0)))
    pl.when(z > 0)(lambda: start(z_copies(False, 0)))
    keep = [
        pltpu.make_async_copy(mine.at[:, pl.ds(0, wide)], wq.at[:, pl.ds(pl.multiple_of(z * wide, half), wide)], local.at[0]),
        pltpu.make_async_copy(mine.at[:, pl.ds(wide, half)], wo.at[:, pl.ds(pl.multiple_of(z * half, half), half)], local.at[1]),
    ]
    start(keep)

    def forward(j, left):
        r = 3 - j if left else j + 1
        landed(copies(piece(0, 0, r), piece(0, 0, r), z_send.at[0, 0], z_recv.at[r], near_y))
        if j < 2:
            pl.when(z < 3 if left else z > 0)(lambda: start(z_copies(left, j + 1)))
        start(y_copies(r))
        start(x_copies(r))

    def corners(j, left):
        r = 3 - j if left else j + 1
        landed(copies(piece(1, 0, r), piece(1, 0, r), y_send.at[r], y_recv.at[r], near_y))
        start(corner_x(r))
        landed(copies(piece(0, 1, r), piece(0, 1, r), x_send.at[r], x_recv.at[r], near_x))
        start(corner_y(r))

    for j in range(3):
        for left in (True, False):
            pl.when(from_left(j) if left else from_right(j))(lambda j=j, left=left: forward(j, left))
        if j == 0:
            for k in range(4):
                pl.when(stays(k))(lambda k=k: start(token_local(k)))
                pl.when(jnp.logical_not(stays(k)))(lambda k=k: start(token_copies(k)))
        else:
            for left in (True, False):
                pl.when(from_left(j - 1) if left else from_right(j - 1))(lambda j=j, left=left: corners(j - 1, left))
    for left in (True, False):
        pl.when(from_left(2) if left else from_right(2))(lambda left=left: corners(2, left))

    for copy in keep:
        copy.wait()
    for r in (1, 2, 3):
        part = piece(1, 1, r, split=True)
        landed(copies(part[:1], part[:1], p_send.at[r], p_recv.at[r], near_x))
        landed(copies(part[1:], part[1:], q_send.at[r], q_recv.at[r], near_y))
        for group in (y_copies(r), x_copies(r), corner_x(r), corner_y(r)):
            sent(group)
    for step in range(3):
        pl.when(jnp.logical_and(z >= step, z < 3))(lambda step=step: sent(z_copies(True, step)))
        pl.when(jnp.logical_and(z + step <= 3, z > 0))(lambda step=step: sent(z_copies(False, step)))
    for k in range(4):
        def finish_local(k=k):
            for copy in token_local(k):
                copy.wait()

        pl.when(stays(k))(finish_local)
        pl.when(jnp.logical_not(stays(k)))(lambda k=k: sent(token_copies(k)))
    for s in range(4):
        at = pl.ds(s * BLK, BLK)
        away = jnp.logical_not(jnp.logical_and(z == s, z // 2 == c))

        def arrived(s=s, at=at):
            for src, dst, send, recv in (
                (tok.at[0], rows_out.at[:, at], t_send, t_recv),
                (vec, vec_out.at[:, at], v_send, v_recv),
            ):
                pltpu.make_async_remote_copy(
                    src_ref=src, dst_ref=dst, send_sem=send.at[0], recv_sem=recv.at[s], device_id=near_y, device_id_type=MESH
                ).wait_recv()

        pl.when(away)(arrived)


def arrive(tok, vec, mine):
    own, width, half = tok.shape[1], 4 * tok.shape[2], mine.shape[1] // 4
    dma = pltpu.SemaphoreType.DMA
    anywhere = pl.BlockSpec(memory_space=pl.ANY)
    return pl.pallas_call(
        arrive_kernel,
        in_specs=[anywhere] * 3,
        out_specs=[anywhere] * 4,
        out_shape=[
            jax.ShapeDtypeStruct((own, width), BF16),
            jax.ShapeDtypeStruct((vec.shape[0], width), BF16),
            jax.ShapeDtypeStruct((width, 12 * half), BF16),
            jax.ShapeDtypeStruct((width, 4 * half), BF16),
        ],
        scratch_shapes=[
            dma((2, 3, 2)), dma((4, 2)), dma((4, 2)), dma((4, 2)), dma((4, 2)), dma((4, 2)),
            dma((4, 1)), dma((4, 1)), dma((4, 2)), dma((4, 2)),
            dma((4,)), dma((4,)), dma((4,)), dma((4,)), dma((4,)),
        ],
        compiler_params=pltpu.CompilerParams(collective_id=0, has_side_effects=True),
        name="arrive",
    )(tok, vec, mine)


def dot_nn(a, b):
    return lax.dot_general(a, b, (((1,), (0,)), ((), ())), preferred_element_type=F32)


def dot_nt(a, b):
    return lax.dot_general(a, b, (((1,), (1,)), ((), ())), preferred_element_type=F32)


def dot_tn(a, b):
    return lax.dot_general(a, b, (((0,), (0,)), ((), ())), preferred_element_type=F32)


def row_reader(ref):
    if len(ref.shape) == 2:
        return lambda lo, width: ref[:, lo : lo + width]
    rows = ref.shape[0] * ref.shape[1]
    return lambda lo, width: ref[:, :, lo : lo + width].astype(F32).reshape(rows, width).astype(BF16)


def row_writer(ref):
    def write(lo, v):
        if len(ref.shape) == 2:
            ref[:, lo : lo + v.shape[1]] = v.astype(BF16)
        else:
            ref[:, :, lo : lo + v.shape[1]] = v.reshape(ref.shape[:2] + v.shape[1:]).astype(BF16)

    return write


def by_pair(lo):
    return (3 * lo, 3 * lo + 2 * HEAD_DIM, 3 * lo + 4 * HEAD_DIM)


def by_part(width):
    return lambda lo: (lo, width + lo, 2 * width + lo)


def attend_kernel(heads, scale, places, qkv_ref, bias_ref, out_ref, total_ref):
    width = heads * HEAD_DIM
    read, write = row_reader(qkv_ref), row_writer(out_ref)
    for lo in range(0, width, 2 * HEAD_DIM):
        q, k, v = (read(at, 2 * HEAD_DIM) for at in places(lo))
        mixed = []
        for i in range(2):
            mine = slice(i * HEAD_DIM, (i + 1) * HEAD_DIM)
            h = lo // HEAD_DIM + i
            scores = dot_nt(k[:, mine], q[:, mine]) * scale
            if bias_ref is not None:
                scores = scores + bias_ref[...]
            highest = jnp.max(scores, axis=0, keepdims=True)
            exponent = jnp.exp(scores - highest)
            total = jnp.sum(exponent, axis=0, keepdims=True)
            total_ref[0, h : h + 1, :] = highest + jnp.log(total)
            mixed.append(dot_tn(v[:, mine], exponent.astype(BF16)) * (1.0 / total))
        write(lo, jnp.concatenate(mixed, axis=0).T)


def attend_back_kernel(heads, scale, places, qkv_ref, grad_ref, total_ref, bias_ref, out_ref):
    width = heads * HEAD_DIM
    read, read_grad, write = row_reader(qkv_ref), row_reader(grad_ref), row_writer(out_ref)
    for lo in range(0, width, 2 * HEAD_DIM):
        q, k, v = (read(at, 2 * HEAD_DIM) for at in places(lo))
        g = read_grad(lo, 2 * HEAD_DIM)
        grads = ([], [], [])
        for i in range(2):
            mine = slice(i * HEAD_DIM, (i + 1) * HEAD_DIM)
            h = lo // HEAD_DIM + i
            scores = dot_nt(k[:, mine], q[:, mine]) * scale
            if bias_ref is not None:
                scores = scores + bias_ref[...]
            p = jnp.exp(scores - total_ref[0, h : h + 1, :])
            dp = dot_nt(v[:, mine], g[:, mine])
            ds = (p * (dp - jnp.sum(p * dp, axis=0, keepdims=True))).astype(BF16)
            grads[0].append(dot_tn(k[:, mine], ds) * scale)
            grads[1].append(dot_nn(ds, q[:, mine]) * scale)
            grads[2].append(dot_nn(p.astype(BF16), g[:, mine]))
        at_q, at_k, at_v = places(lo)
        write(at_q, jnp.concatenate(grads[0], axis=0).T)
        write(at_k, jnp.concatenate(grads[1], axis=1))
        write(at_v, jnp.concatenate(grads[2], axis=1))


def attention_cost(groups, rows, heads, products):
    return pl.CostEstimate(
        flops=8 * products * groups * heads * rows * rows * HEAD_DIM,
        transcendentals=groups * heads * rows * rows,
        bytes_accessed=2 * groups * rows * heads * HEAD_DIM * 2 * products,
    )


def space_attend(qkv, frames, patches, heads, scale):
    width = heads * HEAD_DIM
    return pl.pallas_call(
        lambda q, o, t: attend_kernel(heads, scale, by_pair, q, None, o, t),
        grid=(frames,),
        in_specs=[pl.BlockSpec((patches, 3 * width), lambda i: (i, 0))],
        out_specs=[
            pl.BlockSpec((patches, width), lambda i: (i, 0)),
            pl.BlockSpec((1, heads, patches), lambda i: (i, 0, 0)),
        ],
        out_shape=[
            jax.ShapeDtypeStruct((frames * patches, width), BF16),
            jax.ShapeDtypeStruct((frames, heads, patches), F32),
        ],
        cost_estimate=attention_cost(frames, patches, heads, 2),
        name="space_attend",
    )(qkv)


def space_attend_back(qkv, grad, total, frames, patches, heads, scale):
    width = heads * HEAD_DIM
    return pl.pallas_call(
        lambda q, g, t, o: attend_back_kernel(heads, scale, by_pair, q, g, t, None, o),
        grid=(frames,),
        in_specs=[
            pl.BlockSpec((patches, 3 * width), lambda i: (i, 0)),
            pl.BlockSpec((patches, width), lambda i: (i, 0)),
            pl.BlockSpec((1, heads, patches), lambda i: (i, 0, 0)),
        ],
        out_specs=pl.BlockSpec((patches, 3 * width), lambda i: (i, 0)),
        out_shape=jax.ShapeDtypeStruct((frames * patches, 3 * width), BF16),
        cost_estimate=attention_cost(frames, patches, heads, 5),
        name="space_attend_back",
    )(qkv, grad, total)


GROUP = 8


def time_attend(qkv, bias, frames, patches, heads, scale):
    width = heads * HEAD_DIM
    rows = frames * GROUP
    groups = patches // GROUP
    mixed, total = pl.pallas_call(
        lambda q, b, o, t: attend_kernel(heads, scale, by_part(width), q, b, o, t),
        grid=(groups,),
        in_specs=[
            pl.BlockSpec((frames, GROUP, 3 * width), lambda i: (0, i, 0)),
            pl.BlockSpec((rows, rows), lambda i: (0, 0)),
        ],
        out_specs=[
            pl.BlockSpec((frames, GROUP, width), lambda i: (0, i, 0)),
            pl.BlockSpec((1, heads, rows), lambda i: (i, 0, 0)),
        ],
        out_shape=[
            jax.ShapeDtypeStruct((frames, patches, width), BF16),
            jax.ShapeDtypeStruct((groups, heads, rows), F32),
        ],
        cost_estimate=attention_cost(groups, rows, heads, 2),
        name="time_attend",
    )(qkv.reshape(frames, patches, 3 * width), bias)
    return (mixed.reshape(frames * patches, width), total)


def time_attend_back(qkv, grad, total, bias, frames, patches, heads, scale):
    width = heads * HEAD_DIM
    rows = frames * GROUP
    groups = patches // GROUP
    return pl.pallas_call(
        lambda q, g, t, b, o: attend_back_kernel(heads, scale, by_part(width), q, g, t, b, o),
        grid=(groups,),
        in_specs=[
            pl.BlockSpec((frames, GROUP, 3 * width), lambda i: (0, i, 0)),
            pl.BlockSpec((frames, GROUP, width), lambda i: (0, i, 0)),
            pl.BlockSpec((1, heads, rows), lambda i: (i, 0, 0)),
            pl.BlockSpec((rows, rows), lambda i: (0, 0)),
        ],
        out_specs=pl.BlockSpec((frames, GROUP, 3 * width), lambda i: (0, i, 0)),
        out_shape=jax.ShapeDtypeStruct((frames, patches, 3 * width), BF16),
        cost_estimate=attention_cost(groups, rows, heads, 5),
        name="time_attend_back",
    )(
        qkv.reshape(frames, patches, 3 * width),
        grad.reshape(frames, patches, width),
        total,
        bias,
    ).reshape(frames * patches, 3 * width)


def tie(*values):
    return lax.optimization_barrier(values)


def norm_rows(resid):
    mean = jnp.mean(resid, axis=-1, keepdims=True)
    centered = resid - mean
    inverse = lax.rsqrt(jnp.mean(centered * centered, axis=-1, keepdims=True) + eps_norm)
    return (centered * inverse, inverse)


def norm_rows_back(grad, standardized, inverse, gain):
    gain_grad = jnp.sum(grad * standardized, axis=0)
    inner = grad * gain
    mean = jnp.mean(inner, axis=-1, keepdims=True)
    along = jnp.mean(inner * standardized, axis=-1, keepdims=True)
    return ((inner - mean - standardized * along) * inverse, gain_grad)


def cols(parts):
    return jnp.concatenate(parts, axis=1)


def rows_of(parts):
    return jnp.concatenate(parts, axis=0)


def token_parallel(
    tokens,
    cotangent,
    ratio,
    priority,
    frame_order,
    mask_embed,
    gains,
    qkv_space,
    out_space,
    qkv_time,
    out_time,
    w_in,
    w_out,
):
    scale = 1.0 / math.sqrt(HEAD_DIM)
    y, x, c, z = (lax.axis_index(name) for name in AXES)
    patches = tokens.shape[2]
    width = qkv_space.shape[0]
    frames_own = tokens.shape[0] * tokens.shape[1] // 4
    frames_all = frame_order.shape[1]
    own = frames_own * patches
    hidden_own = w_in.shape[1] // 2
    plane = 2 * y + x
    k_own = 2 * (z % 2) + c

    def gather_rows(v):
        pieces = v.reshape(4, own, BLK)
        landed = jnp.stack(
            [
                lax.ppermute(
                    lax.dynamic_index_in_dim(pieces, z ^ r, 0, keepdims=False), AXES, spread_pairs(r)
                )
                for r in range(4)
            ]
        )
        return cols([lax.dynamic_index_in_dim(landed, k_own ^ b, 0, keepdims=False) for b in range(4)])

    def return_rows(v):
        landed = jnp.stack(
            [
                lax.ppermute(
                    lax.dynamic_slice_in_dim(v, (k_own ^ r) * BLK, BLK, 1),
                    AXES,
                    [(b, a) for a, b in spread_pairs(r)],
                )
                for r in range(4)
            ]
        )
        return jnp.stack(
            [lax.dynamic_index_in_dim(landed, k ^ z, 0, keepdims=False) for k in range(4)]
        ).reshape(tokens.shape)

    masked_here = (priority < ratio[:, None, None]).astype(jnp.int32).reshape(2, -1)
    info = cols([masked_here, frame_order])
    info = jnp.where(z // 2 == c, info, hop_c(info))
    info = lax.dynamic_index_in_dim(info, z % 2, 0, keepdims=False)
    masked = lax.dynamic_slice_in_dim(info, c * own, own, 0)[:, None] != 0
    order = info[2 * own :].reshape(2, 2, frames_own)
    order = jnp.where(y == 1, order[::-1], order)
    order = jnp.where(c == 1, order[:, ::-1], order).swapaxes(0, 1).reshape(frames_all)
    order = jnp.repeat(order, GROUP)
    patch = jnp.arange(frames_all * GROUP) % GROUP
    visible = (order[:, None] <= order[None, :]) & (patch[:, None] == patch[None, :])
    bias = jnp.where(visible, 0.0, -1e30).astype(F32)

    half = qkv_space.shape[2] // 2
    sp_own = cols(
        [
            lax.dynamic_slice_in_dim(qkv_space, c * half, half, 2).reshape(width, -1),
            lax.dynamic_slice_in_dim(out_space, c * half, half, 0).T,
        ]
    )
    vectors = rows_of([mask_embed[None], gains, jnp.zeros((4, BLK), BF16)])
    arrived, vectors, ws_qkv, ws_out = arrive(tokens.reshape(4, own, BLK), vectors, sp_own)
    source = arrived.astype(F32)
    embed_row = vectors[:1].astype(F32)
    gain = [vectors[1 + i : 2 + i].astype(F32) for i in range(3)]

    head = (2 * y + c) * HEAD_DIM
    ff_in = lax.dynamic_slice(w_in, (plane * BLK, c * hidden_own), (BLK, hidden_own))
    ff_out = lax.dynamic_slice(w_out, (c * hidden_own, plane * BLK), (hidden_own, BLK)).T
    ti_own = cols(
        [
            lax.dynamic_slice_in_dim(qkv_time, head, HEAD_DIM, 2).reshape(width, -1),
            lax.dynamic_slice_in_dim(out_time, head, HEAD_DIM, 0).T,
        ]
    )
    arrived, ff_in, ff_out, ti_own = tie(arrived, ff_in, ff_out, ti_own)

    def gather_ff(w):
        w = lax.all_gather(w, ("tm", "x", "mp")).reshape(4, 4, BLK, hidden_own)
        return jnp.swapaxes(w, 1, 2).reshape(width, 4 * hidden_own)

    def pair_gather(v):
        return rows_of([v, hop_c(v)])

    def pair_scatter(v):
        return v[:own] + hop_c(v[own:].astype(BF16)).astype(F32)

    def quad_gather(v):
        both = rows_of([v, hop_y(v)])
        return rows_of([both, hop_c(both)])

    def quad_scatter(v):
        both = v[: 2 * own] + hop_c(v[2 * own :].astype(BF16)).astype(F32)
        return both[:own] + hop_y(both[own:].astype(BF16)).astype(F32)

    heads_s = 4 * half // HEAD_DIM
    heads_t = 4
    frames_pair = 2 * frames_own
    resid0 = jnp.where(masked, embed_row, source)
    std0, inv0 = norm_rows(resid0)
    normed0 = pair_gather((std0 * gain[0]).astype(BF16))
    ti_half = lax.dynamic_slice_in_dim(ti_own, x * 2 * BLK, 2 * BLK, 0)
    ti_z = [hop_z(ti_half, -r) for r in (1, 2, 3)]
    wf_in, wf_out = gather_ff(ff_in), gather_ff(ff_out)
    joined0 = dot_nn(normed0, ws_qkv).astype(BF16)
    mixed0, total0 = space_attend(joined0, frames_pair, patches, heads_s, scale)
    mixed0, ti_z = tie(mixed0, ti_z)
    ti_z = cols(ti_z)
    ti_x = hop_x(ti_z)
    ti_far = jnp.where(x == 0, rows_of([ti_z, ti_x]), rows_of([ti_x, ti_z]))
    resid1 = resid0 + pair_scatter(dot_nt(mixed0, ws_out))
    std1, inv1 = norm_rows(resid1)
    normed1 = quad_gather((std1 * gain[1]).astype(BF16))
    normed1, ti_far, cotangent = tie(normed1, ti_far, cotangent)
    ti_all = [ti_own] + [ti_far[:, r * 4 * HEAD_DIM : (r + 1) * 4 * HEAD_DIM] for r in range(3)]
    wt_qkv = cols([w[:, j * HEAD_DIM : (j + 1) * HEAD_DIM] for j in range(3) for w in ti_all])
    wt_out = cols([w[:, 3 * HEAD_DIM :] for w in ti_all])
    upstream = gather_rows(cotangent)
    joined1 = dot_nn(normed1, wt_qkv).astype(BF16)
    mixed1, total1 = time_attend(joined1, bias, frames_all, patches, heads_t, scale)
    mixed1, upstream = tie(mixed1, upstream)
    grad3 = jnp.where(masked, upstream, jnp.zeros((), BF16))
    gb3 = pair_gather(grad3)
    resid2 = resid1 + quad_scatter(dot_nt(mixed1, wt_out))
    std2, inv2 = norm_rows(resid2)
    normed2 = pair_gather((std2 * gain[2]).astype(BF16))
    inner = dot_nn(normed2, wf_in)
    activated, gelu_pull = jax.vjp(gelu_tanh, inner)
    hidden = activated.astype(BF16)

    def plane_scatter(lhs, rhs):
        return lax.psum_scatter(dot_tn(lhs, rhs).astype(BF16), ("tm", "x"), scatter_dimension=0, tiled=True)

    def line_scatter(v):
        v = jnp.swapaxes(v.reshape(BLK, 4, -1), 0, 1)
        return lax.psum_scatter(v, "mp", scatter_dimension=0).astype(F32)

    def send_x(lhs, rhs):
        there = jnp.where(x == 0, cols([lhs[:, BLK : 2 * BLK], lhs[:, 3 * BLK :]]), cols([lhs[:, :BLK], lhs[:, 2 * BLK : 3 * BLK]]))
        return hop_x(dot_tn(there, rhs).astype(BF16))

    def keep_x(lhs, rhs, landed):
        here = jnp.where(x == 1, cols([lhs[:, BLK : 2 * BLK], lhs[:, 3 * BLK :]]), cols([lhs[:, :BLK], lhs[:, 2 * BLK : 3 * BLK]]))
        return dot_tn(here, rhs) + landed.astype(F32)

    def mine_y(v):
        return jnp.where(y == 0, v[:BLK], v[BLK:])

    def other_y(v):
        return jnp.where(y == 1, v[:BLK], v[BLK:])

    def reduce_z(pieces):
        total = pieces[0]
        for r in (1, 2, 3):
            total = total + hop_z(pieces[r].astype(BF16), r).astype(F32)
        return total

    def swap_c(total):
        rows = BLK // 2
        kept = lax.dynamic_slice_in_dim(total, c * rows, rows, 0)
        sent = hop_c(lax.dynamic_slice_in_dim(total, (1 - c) * rows, rows, 0).astype(BF16))
        return (kept, sent.astype(F32))

    def by_core(kept, landed):
        return jnp.where(c == 0, jnp.concatenate([kept, landed], -1), jnp.concatenate([landed, kept], -1))

    w_out_part = plane_scatter(gb3, hidden)
    grad_inner = gelu_pull(dot_nn(gb3, wf_out))[0].astype(BF16)
    part2 = pair_scatter(dot_nt(grad_inner, wf_in))
    w_in_part = plane_scatter(normed2, grad_inner)
    back2, gain_grad2 = norm_rows_back(part2, std2, inv2, gain[2])
    grad2 = grad3.astype(F32) + back2
    gb2 = quad_gather(grad2.astype(BF16))
    block_part = dot_nt(hidden, wf_out)
    block_out = return_rows((resid2 + pair_scatter(block_part)).astype(BF16))

    dmixed1 = dot_nn(gb2, wt_out).astype(BF16)
    djoined1 = time_attend_back(joined1, dmixed1, total1, bias, frames_all, patches, heads_t, scale)
    djoined1, block_out = tie(djoined1, block_out)
    part1 = quad_scatter(dot_nt(djoined1, wt_qkv))
    back1, gain_grad1 = norm_rows_back(part1, std1, inv1, gain[1])
    grad1 = grad2 + back1
    gb1 = pair_gather(grad1.astype(BF16))
    t_out_x = send_x(gb2, mixed1)
    t_qkv_x = send_x(normed1, djoined1)
    dmixed0 = dot_nn(gb1, ws_out).astype(BF16)
    s_out_x = send_x(gb1, mixed0)
    djoined0 = space_attend_back(joined0, dmixed0, total0, frames_pair, patches, heads_s, scale)
    djoined0, t_out_x, t_qkv_x, w_out_part, s_out_x = tie(djoined0, t_out_x, t_qkv_x, w_out_part, s_out_x)
    g_w_out = line_scatter(w_out_part)
    s_qkv_x = send_x(normed0, djoined0)
    part0 = pair_scatter(dot_nt(djoined0, ws_qkv))
    s_out_kept = keep_x(gb1, mixed0, s_out_x)
    s_out_y = hop_y(other_y(s_out_kept).astype(BF16))
    g_w_in = line_scatter(w_in_part)
    g_t_out = keep_x(gb2, mixed1, t_out_x)
    g_t_qkv = keep_x(normed1, djoined1, t_qkv_x)
    z_at = [(z + r) % 4 for r in range(4)]
    span = heads_t * HEAD_DIM
    g_time = reduce_z(
        [
            cols(
                [lax.dynamic_slice_in_dim(g_t_qkv, j * span + r * HEAD_DIM, HEAD_DIM, 1) for j in range(3)]
                + [lax.dynamic_slice_in_dim(g_t_out, r * HEAD_DIM, HEAD_DIM, 1)]
            )
            for r in range(4)
        ]
    )
    s_qkv_kept = keep_x(normed0, djoined0, s_qkv_x)
    s_qkv = mine_y(s_qkv_kept) + hop_y(other_y(s_qkv_kept).astype(BF16)).astype(F32)
    s_out = mine_y(s_out_kept) + s_out_y.astype(F32)
    g_space = reduce_z(
        [
            cols(
                [
                    lax.dynamic_slice_in_dim(s_qkv, s * 3 * half, 3 * half, 1),
                    lax.dynamic_slice_in_dim(s_out, s * half, half, 1),
                ]
            )
            for s in z_at
        ]
    )
    back0, gain_grad0 = norm_rows_back(part0, std0, inv0, gain[0])
    grad0 = grad1 + back0
    grad_tokens = return_rows(jnp.where(masked, 0.0, grad0).astype(BF16)).astype(F32)
    grad_embed = jnp.sum(jnp.where(masked, grad0, 0.0), axis=0)
    small = jnp.stack([gain_grad0, gain_grad1, gain_grad2, grad_embed])
    for hop in (hop_c, hop_y, hop_x):
        small = small + hop(small)
    small_at = [lax.dynamic_slice_in_dim(small, s * BLK, BLK, 1) for s in z_at]
    small = small_at[0]
    for r in (1, 2, 3):
        small = small + hop_z(small_at[r], r)

    rows = BLK // 2
    kept, landed = swap_c(g_space)
    grad_qkv_space = by_core(
        kept[:, : 3 * half].reshape(rows, 3, half), landed[:, : 3 * half].reshape(rows, 3, half)
    )
    grad_out_space = by_core(kept[:, 3 * half :], landed[:, 3 * half :]).T
    kept, landed = swap_c(cols([g_w_in, g_w_out]))
    grad_w_in = by_core(kept[:, :hidden_own], landed[:, :hidden_own])
    grad_w_out = by_core(kept[:, hidden_own:], landed[:, hidden_own:]).T
    both = cols([mine_y(g_time), hop_y(other_y(g_time).astype(BF16)).astype(F32)])
    kept, landed = swap_c(both)
    quad = jnp.stack([kept, landed], 1).reshape(rows, 2, 2, 4, HEAD_DIM)
    quad = jnp.where(c == 1, quad[:, ::-1], quad)
    quad = jnp.where(y == 1, quad[:, :, ::-1], quad)
    quad = jnp.transpose(quad, (0, 3, 2, 1, 4)).reshape(rows, 4, 4 * HEAD_DIM)
    grad_qkv_time = quad[:, :3]
    grad_out_time = quad[:, 3].T
    return (
        block_out,
        grad_tokens,
        small[3],
        small[:3],
        grad_qkv_space,
        grad_out_space,
        grad_qkv_time,
        grad_out_time,
        grad_w_in,
        grad_w_out,
    )


def solution(mesh):
    sizes = (mesh.shape["tm"], mesh.shape["clip"], mesh.shape["mp"])
    if sizes == (2, 4, 4):
        mesh = jax.sharding.Mesh(mesh.devices.reshape(2, 2, 2, 4), AXES)
        step, clip = token_parallel, ("x", "c")
    else:
        step, clip = shards, ("clip",)
    return jax.shard_map(
        step,
        mesh=mesh,
        in_specs=(
            P(clip, "tm", None, "mp"),
            P(clip, "tm", None, "mp"),
            P(clip),
            P(clip, "tm", None),
            P(clip, None),
            P("mp"),
            P(None, "mp"),
            P(None, None, "mp"),
            P("mp", None),
            P(None, None, "mp"),
            P("mp", None),
            P(None, "mp"),
            P("mp", None),
        ),
        out_specs=(
            P(clip, "tm", None, "mp"),
            P(clip, "tm", None, "mp"),
            P("mp"),
            P(None, "mp"),
            P(("tm",) + clip, None, "mp"),
            P("mp", ("tm",) + clip),
            P(("tm",) + clip, None, "mp"),
            P("mp", ("tm",) + clip),
            P(("tm",) + clip, "mp"),
            P("mp", ("tm",) + clip),
        ),
        check_vma=False,
    )
```

```python
import functools
import math

import jax
import jax.numpy as jnp
from jax import lax
from jax.experimental import pallas as pl
from jax.experimental.pallas import tpu as pltpu
from jax.sharding import PartitionSpec as P

HEAD_DIM = 64
MICRO = 2


eps_norm = 1e-05


def gelu_tanh(values):
    return jax.nn.gelu(values, approximate=True)


def norm_forward_pass(residual_stream, gain_coefficients, complete_width):
    reduced_totals = lax.psum(
        (jnp.sum(residual_stream, axis=-1), jnp.sum(residual_stream * residual_stream, axis=-1)),
        "mp",
    )
    centered_rows = reduced_totals[0] / complete_width
    spread = reduced_totals[1] / complete_width - centered_rows * centered_rows
    inverse_scale = lax.rsqrt(spread + eps_norm)
    standardized_rows = (residual_stream - centered_rows[:, None]) * inverse_scale[:, None]
    shard_rows = (standardized_rows * gain_coefficients).astype(jnp.bfloat16)
    normalized_rows = lax.all_gather(shard_rows, "mp", axis=1, tiled=True)
    return (normalized_rows, standardized_rows, inverse_scale)


def norm_reverse_pass(
    normalized_gradient, standardized_rows, inverse_scale, gain_coefficients, complete_width
):
    gain_gradient = jnp.sum(normalized_gradient * standardized_rows, axis=0)
    standardized_gradient = normalized_gradient * gain_coefficients
    reduced_totals = lax.psum(
        (
            jnp.sum(standardized_gradient, axis=-1),
            jnp.sum(standardized_gradient * standardized_rows, axis=-1),
        ),
        "mp",
    )
    grad_resid = (
        standardized_gradient
        - reduced_totals[0][:, None] / complete_width
        - standardized_rows * (reduced_totals[1][:, None] / complete_width)
    ) * inverse_scale[:, None]
    return (grad_resid, gain_gradient)


def sum_features(grad_full):
    return lax.psum_scatter(
        grad_full.astype(jnp.bfloat16), "mp", scatter_dimension=1, tiled=True
    ).astype(jnp.float32)


def branch_out(hidden, weight):
    partial_rows = jnp.dot(hidden, weight, preferred_element_type=jnp.float32)
    return lax.psum_scatter(partial_rows, "mp", scatter_dimension=1, tiled=True)


def branch_back(grad_resid, hidden, weight):
    grad_rows = lax.all_gather(grad_resid.astype(jnp.bfloat16), "mp", axis=1, tiled=True)
    weight_grad = jnp.einsum("rk,rd->kd", hidden, grad_rows, preferred_element_type=jnp.float32)
    grad_hidden = jnp.einsum("rd,kd->rk", grad_rows, weight, preferred_element_type=jnp.float32)
    return (grad_hidden, weight_grad)


def qkv_back(normalized_rows, grad_joined, weight):
    weight_grad = jnp.einsum(
        "rd,trk->dtk", normalized_rows, grad_joined, preferred_element_type=jnp.float32
    )
    grad_full = jnp.einsum("trk,dtk->rd", grad_joined, weight, preferred_element_type=jnp.float32)
    return (weight_grad, sum_features(grad_full))


def reduce_grads(local_grads, small_grads):
    reduced = (
        lax.psum_scatter(local_grads[0], ("tm", "clip"), scatter_dimension=0, tiled=True),
        lax.psum_scatter(local_grads[1], ("tm", "clip"), scatter_dimension=1, tiled=True),
        lax.psum_scatter(local_grads[2], ("tm", "clip"), scatter_dimension=0, tiled=True),
        lax.psum_scatter(local_grads[3], ("tm", "clip"), scatter_dimension=1, tiled=True),
        lax.psum_scatter(local_grads[4], ("tm", "clip"), scatter_dimension=0, tiled=True),
        lax.psum_scatter(local_grads[5], ("tm", "clip"), scatter_dimension=1, tiled=True),
    )
    reduced_small = lax.psum((small_grads[0], small_grads[1]), ("tm", "clip"))
    return (reduced, reduced_small)


def space_forward(normalized_rows, weight, frame_count, patches, heads_local, scale):
    joined = jnp.einsum(
        "rd,dtk->trk", normalized_rows, weight, preferred_element_type=jnp.float32
    ).astype(jnp.bfloat16)
    shape_heads = (frame_count, patches, heads_local, HEAD_DIM)
    scores = (
        jnp.einsum(
            "bshd,bthd->bhst",
            joined[0].reshape(shape_heads),
            joined[1].reshape(shape_heads),
            preferred_element_type=jnp.float32,
        )
        * scale
    )
    highest = jnp.max(scores, axis=-1, keepdims=True)
    exponent = jnp.exp(scores - highest)
    reduced_totals = jnp.sum(exponent, axis=-1, keepdims=True)
    log_total = highest + jnp.log(reduced_totals)
    attention = (exponent / reduced_totals).astype(jnp.bfloat16)
    mixed = jnp.einsum(
        "bhst,bthd->bshd",
        attention,
        joined[2].reshape(shape_heads),
        preferred_element_type=jnp.float32,
    )
    return (
        joined,
        log_total,
        mixed.astype(jnp.bfloat16).reshape(frame_count * patches, heads_local * HEAD_DIM),
    )


def space_backward(grad_mixed, joined, log_total, frame_count, patches, heads_local, scale):
    shape_heads = (frame_count, patches, heads_local, HEAD_DIM)
    queries = joined[0].reshape(shape_heads)
    key_rows = joined[1].reshape(shape_heads)
    values = joined[2].reshape(shape_heads)
    grad_out = grad_mixed.reshape(shape_heads)
    scores = (
        jnp.einsum("bshd,bthd->bhst", queries, key_rows, preferred_element_type=jnp.float32) * scale
    )
    attention = jnp.exp(scores - log_total)
    grad_values = jnp.einsum(
        "bhst,bshd->bthd",
        attention.astype(jnp.bfloat16),
        grad_out,
        preferred_element_type=jnp.float32,
    )
    grad_att = jnp.einsum("bshd,bthd->bhst", grad_out, values, preferred_element_type=jnp.float32)
    grad_scores = (
        attention * (grad_att - jnp.sum(attention * grad_att, axis=-1, keepdims=True))
    ).astype(jnp.bfloat16)
    grad_queries = (
        jnp.einsum("bhst,bthd->bshd", grad_scores, key_rows, preferred_element_type=jnp.float32)
        * scale
    )
    grad_keys = (
        jnp.einsum("bhst,bshd->bthd", grad_scores, queries, preferred_element_type=jnp.float32)
        * scale
    )
    row_count = frame_count * patches
    stacked = jnp.stack(
        [
            grad_queries.reshape(row_count, -1),
            grad_keys.reshape(row_count, -1),
            grad_values.reshape(row_count, -1),
        ]
    )
    return stacked.astype(jnp.bfloat16)


def time_scores(queries, keys_all, visible, scale):
    scores = (
        jnp.einsum("cfshd,cgshd->chfgs", queries, keys_all, preferred_element_type=jnp.float32)
        * scale
    )
    return jnp.where(visible, scores, -1e30)


def time_forward(queries, keys_all, values_all, visible, scale):
    scores = time_scores(queries, keys_all, visible, scale)
    highest = jnp.max(scores, axis=3, keepdims=True)
    exponent = jnp.exp(scores - highest)
    reduced_totals = jnp.sum(exponent, axis=3, keepdims=True)
    log_total = highest + jnp.log(reduced_totals)
    attention = (exponent / reduced_totals).astype(jnp.bfloat16)
    mixed = jnp.einsum(
        "chfgs,cgshd->cfshd", attention, values_all, preferred_element_type=jnp.float32
    )
    return (log_total, mixed.astype(jnp.bfloat16))


def time_backward(grad_mixed, queries, keys_all, values_all, visible, log_total, scale):
    grad_out = grad_mixed.reshape(queries.shape)
    scores = time_scores(queries, keys_all, visible, scale)
    attention = jnp.exp(scores - log_total)
    grad_values = jnp.einsum(
        "chfgs,cfshd->cgshd",
        attention.astype(jnp.bfloat16),
        grad_out,
        preferred_element_type=jnp.float32,
    )
    grad_att = jnp.einsum(
        "cfshd,cgshd->chfgs", grad_out, values_all, preferred_element_type=jnp.float32
    )
    grad_scores = (
        attention * (grad_att - jnp.sum(attention * grad_att, axis=3, keepdims=True))
    ).astype(jnp.bfloat16)
    grad_queries = (
        jnp.einsum("chfgs,cgshd->cfshd", grad_scores, keys_all, preferred_element_type=jnp.float32)
        * scale
    )
    grad_keys = (
        jnp.einsum("chfgs,cfshd->cgshd", grad_scores, queries, preferred_element_type=jnp.float32)
        * scale
    )
    return (grad_queries, grad_keys, grad_values)


def shards(
    tokens,
    cotangent,
    ratio,
    priority,
    frame_order,
    mask_embed,
    gains,
    qkv_space,
    out_space,
    qkv_time,
    out_time,
    w_in,
    w_out,
):
    scale = 1.0 / math.sqrt(HEAD_DIM)
    clips_local = tokens.shape[0] // MICRO
    frames_local = tokens.shape[1]
    patches = tokens.shape[2]
    cols_local = tokens.shape[3]
    frames_all = frame_order.shape[1]
    hidden_width = qkv_space.shape[0]
    joined_local = qkv_space.shape[2]
    heads_local = joined_local // HEAD_DIM
    row_count = clips_local * frames_local * patches
    gain_broadcast = gains.astype(jnp.float32)
    embed_row = mask_embed.astype(jnp.float32)
    first_frame = lax.axis_index("tm") * frames_local
    shape_local = (clips_local, frames_local, patches, joined_local)
    shape_heads = (clips_local, frames_local, patches, heads_local, HEAD_DIM)
    shape_all = (clips_local, frames_all, patches, heads_local, HEAD_DIM)
    outputs = []
    input_grads = []
    weight_total = None
    small_total = None
    for batch_index in range(MICRO):
        lower = batch_index * clips_local
        upper = lower + clips_local
        source = tokens[lower:upper].reshape(row_count, cols_local).astype(jnp.float32)
        upstream = cotangent[lower:upper].reshape(row_count, cols_local).astype(jnp.float32)
        masked = (priority[lower:upper] < ratio[lower:upper][:, None, None]).reshape(row_count)
        order_rows = frame_order[lower:upper]
        residual_stream0 = jnp.where(masked[:, None], embed_row[None, :], source)
        normalized_rows0, standardized_rows0, inverse_deviation0 = norm_forward_pass(
            residual_stream0, gain_broadcast[0], hidden_width
        )
        joined0, total0, mixed0 = space_forward(
            normalized_rows0, qkv_space, clips_local * frames_local, patches, heads_local, scale
        )
        residual_stream1 = residual_stream0 + branch_out(mixed0, out_space)
        normalized_rows1, standardized_rows1, inverse_deviation1 = norm_forward_pass(
            residual_stream1, gain_broadcast[1], hidden_width
        )
        joined1 = jnp.einsum(
            "rd,dtk->trk", normalized_rows1, qkv_time, preferred_element_type=jnp.float32
        ).astype(jnp.bfloat16)
        queries_local = joined1[0].reshape(shape_local)
        keys_local = joined1[1].reshape(shape_local)
        values_local = joined1[2].reshape(shape_local)
        keys_all, values_all = (
            lax.all_gather(keys_local, "tm", axis=1, tiled=True),
            lax.all_gather(values_local, "tm", axis=1, tiled=True),
        )
        query_order = lax.dynamic_slice_in_dim(order_rows, first_frame, frames_local, axis=1)
        time_visible = (order_rows[:, None, :] <= query_order[:, :, None])[:, None, :, :, None]
        time_q = queries_local.reshape(shape_heads)
        time_k = keys_all.reshape(shape_all)
        time_v = values_all.reshape(shape_all)
        total1, mixed_frames = time_forward(time_q, time_k, time_v, time_visible, scale)
        mixed1 = mixed_frames.reshape(row_count, joined_local)
        residual_stream2 = residual_stream1 + branch_out(mixed1, out_time)
        normalized_rows2, standardized_rows2, inverse_deviation2 = norm_forward_pass(
            residual_stream2, gain_broadcast[2], hidden_width
        )
        projected = jnp.dot(normalized_rows2, w_in, preferred_element_type=jnp.float32)
        activated, gelu_pull = jax.vjp(gelu_tanh, projected)
        hidden = activated.astype(jnp.bfloat16)
        resid3 = residual_stream2 + branch_out(hidden, w_out)
        outputs.append(
            resid3.astype(jnp.bfloat16).reshape(clips_local, frames_local, patches, cols_local)
        )
        grad3 = jnp.where(masked[:, None], upstream, 0.0)
        grad_hidden, grad_w_out = branch_back(grad3, hidden, w_out)
        grad_inner = gelu_pull(grad_hidden)[0].astype(jnp.bfloat16)
        grad_w_in = jnp.einsum(
            "rd,rk->dk", normalized_rows2, grad_inner, preferred_element_type=jnp.float32
        )
        normalized_gradient2 = sum_features(
            jnp.einsum("rk,dk->rd", grad_inner, w_in, preferred_element_type=jnp.float32)
        )
        backward_third, gain_gradient2 = norm_reverse_pass(
            normalized_gradient2,
            standardized_rows2,
            inverse_deviation2,
            gain_broadcast[2],
            hidden_width,
        )
        grad2 = grad3 + backward_third
        grad_mixed1, grad_out_time = branch_back(grad2, mixed1, out_time)
        grad_mixed_low = grad_mixed1.astype(jnp.bfloat16).reshape(shape_local)
        grad_queries, grad_keys, grad_values = time_backward(
            grad_mixed_low, time_q, time_k, time_v, time_visible, total1, scale
        )
        key_part, value_part = (
            lax.psum_scatter(
                grad_keys.reshape(clips_local, frames_all, patches, joined_local).astype(
                    jnp.bfloat16
                ),
                "tm",
                scatter_dimension=1,
                tiled=True,
            ).astype(jnp.float32),
            lax.psum_scatter(
                grad_values.reshape(clips_local, frames_all, patches, joined_local).astype(
                    jnp.bfloat16
                ),
                "tm",
                scatter_dimension=1,
                tiled=True,
            ).astype(jnp.float32),
        )
        grad_joined1 = jnp.stack(
            [
                grad_queries.reshape(row_count, joined_local),
                key_part.reshape(row_count, joined_local),
                value_part.reshape(row_count, joined_local),
            ]
        ).astype(jnp.bfloat16)
        grad_qkv_time, normalized_gradient1 = qkv_back(normalized_rows1, grad_joined1, qkv_time)
        backward_second, gain_gradient1 = norm_reverse_pass(
            normalized_gradient1,
            standardized_rows1,
            inverse_deviation1,
            gain_broadcast[1],
            hidden_width,
        )
        grad1 = grad2 + backward_second
        grad_mixed0, grad_out_space = branch_back(grad1, mixed0, out_space)
        grad_joined0 = space_backward(
            grad_mixed0.astype(jnp.bfloat16),
            joined0,
            total0,
            clips_local * frames_local,
            patches,
            heads_local,
            scale,
        )
        grad_qkv_space, normalized_gradient0 = qkv_back(normalized_rows0, grad_joined0, qkv_space)
        backward_first, gain_gradient0 = norm_reverse_pass(
            normalized_gradient0,
            standardized_rows0,
            inverse_deviation0,
            gain_broadcast[0],
            hidden_width,
        )
        grad0 = grad1 + backward_first
        input_grads.append(
            jnp.where(masked[:, None], 0.0, grad0).reshape(
                clips_local, frames_local, patches, cols_local
            )
        )
        grad_embed = jnp.sum(jnp.where(masked[:, None], grad0, 0.0), axis=0)
        gain_grads = jnp.stack([gain_gradient0, gain_gradient1, gain_gradient2])
        local_grads = (
            grad_qkv_space,
            grad_out_space,
            grad_qkv_time,
            grad_out_time,
            grad_w_in,
            grad_w_out,
        )
        small_grads = (gain_grads, grad_embed)
        reduced, reduced_small = reduce_grads(local_grads, small_grads)
        if weight_total is None:
            weight_total = reduced
            small_total = reduced_small
        else:
            weight_total = tuple((total + grad for total, grad in zip(weight_total, reduced)))
            small_total = tuple((total + grad for total, grad in zip(small_total, reduced_small)))
    return (
        jnp.concatenate(outputs, axis=0),
        jnp.concatenate(input_grads, axis=0),
        small_total[1],
        small_total[0],
        weight_total[0],
        weight_total[1],
        weight_total[2],
        weight_total[3],
        weight_total[4],
        weight_total[5],
    )


AXES = ("tm", "x", "c", "mp")
F32 = jnp.float32
BF16 = jnp.bfloat16
BLK = 256
MESH = pl.DeviceIdType.MESH


def device_pairs(move):
    pairs = []
    for y in range(2):
        for x in range(2):
            for c in range(2):
                for z in range(4):
                    there = move(y, x, c, z)
                    pairs.append(tuple(((q[0] * 2 + q[1]) * 2 + q[2]) * 4 + q[3] for q in ((y, x, c, z), there)))
    return pairs


def hop_y(v):
    return lax.ppermute(v, AXES, device_pairs(lambda y, x, c, z: (1 - y, x, c, z)))


def hop_x(v):
    return lax.ppermute(v, AXES, device_pairs(lambda y, x, c, z: (y, 1 - x, c, z)))


def hop_c(v):
    return lax.ppermute(v, AXES, device_pairs(lambda y, x, c, z: (y, x, 1 - c, z)))


def hop_z(v, shift):
    return lax.ppermute(v, AXES, device_pairs(lambda y, x, c, z: (y, x, c, (z + shift) % 4)))


def spread_pairs(r):
    def move(y, x, c, z):
        k = z ^ r
        return (y, x, k & 1, 2 * c + (k >> 1))

    return device_pairs(move)


def arrive_kernel(
    tok, vec, mine, later, rows_out, vec_out, wq, wo, wt,
    z_send, z_recv, y_send, y_recv, x_send, x_recv, p_send, p_recv, q_send, q_recv,
    t_send, t_recv, v_send, v_recv, u_send, u_recv, w_send, w_recv, local,
):
    y, x, c, z = (lax.axis_index(name) for name in AXES)
    half = wo.shape[1] // 4
    wide = 3 * half

    barrier = pltpu.get_barrier_semaphore()
    for dc in range(2):
        for dz in range(4):
            if dc or dz:
                peer = (y, x, (c + dc) % 2, (z + dz) % 4)
                pl.semaphore_signal(barrier, inc=1, device_id=peer, device_id_type=MESH)
    near_y, near_x = (1 - y, x, c, z), (y, 1 - x, c, z)
    for peer in (near_y, near_x):
        pl.semaphore_signal(barrier, inc=1, device_id=peer, device_id_type=MESH)
    pl.semaphore_wait(barrier, 9)

    def rows(dy, dx):
        return pl.ds(pl.multiple_of(BLK * (2 * ((y + dy) % 2) + (x + dx) % 2), BLK), BLK)

    def piece(dy, dx, r, split=False):
        s = (z + r) % 4
        at = pl.multiple_of(s * wide, half)
        out = wo.at[rows(dy, dx), pl.ds(pl.multiple_of(s * half, half), half)]
        if split:
            late = pl.multiple_of(s * wide + 2 * half, half)
            return (wq.at[rows(dy, dx), pl.ds(at, 2 * half)], wq.at[rows(dy, dx), pl.ds(late, half)], out)
        return (wq.at[rows(dy, dx), pl.ds(at, wide)], out)

    def copies(sources, targets, send, recv, peer):
        return [
            pltpu.make_async_remote_copy(
                src_ref=src, dst_ref=dst, send_sem=send.at[i], recv_sem=recv.at[i], device_id=peer, device_id_type=MESH
            )
            for i, (src, dst) in enumerate(zip(sources, targets))
        ]

    own_rows = rows(0, 0)
    own_slice = (mine.at[own_rows, pl.ds(0, wide)], mine.at[own_rows, pl.ds(wide, half)])

    def z_copies(right, step):
        if right:
            r = 0 if step == 0 else 4 - step
            peer, lands = (y, x, c, (z + 1) % 4), 3 - step
        else:
            r = step
            peer, lands = (y, x, c, (z + 3) % 4), step + 1
        target = piece(0, 0, r)
        source = own_slice if step == 0 else target
        return copies(source, target, z_send.at[int(right), step], z_recv.at[lands], peer)

    def y_copies(r):
        return copies(piece(0, 0, r), piece(0, 0, r), y_send.at[r], y_recv.at[r], near_y)

    def x_copies(r):
        return copies(piece(0, 0, r), piece(0, 0, r), x_send.at[r], x_recv.at[r], near_x)

    def corner_x(r):
        part = piece(1, 0, r, split=True)[:1]
        return copies(part, part, p_send.at[r], p_recv.at[r], near_x)

    def corner_y(r):
        part = piece(0, 1, r, split=True)[1:]
        return copies(part, part, q_send.at[r], q_recv.at[r], near_y)

    span = wt.shape[1] // 4

    def time_piece(dx, r):
        at = pl.ds(pl.multiple_of(((z + r) % 4) * span, span), span)
        return wt.at[pl.ds(pl.multiple_of(2 * BLK * ((x + dx) % 2), BLK), 2 * BLK), at]

    def time_z(right, step):
        if right:
            r = 0 if step == 0 else 4 - step
            peer, lands = (y, x, c, (z + 1) % 4), 3 - step
        else:
            r = step
            peer, lands = (y, x, c, (z + 3) % 4), step + 1
        source = later.at[pl.ds(pl.multiple_of(2 * BLK * x, BLK), 2 * BLK)] if step == 0 else time_piece(0, r)
        return [
            pltpu.make_async_remote_copy(
                src_ref=source, dst_ref=time_piece(0, r), send_sem=u_send.at[int(right), step], recv_sem=u_recv.at[lands],
                device_id=peer, device_id_type=MESH,
            )
        ]

    def time_x(dx, r):
        return [
            pltpu.make_async_remote_copy(
                src_ref=time_piece(dx, r), dst_ref=time_piece(dx, r), send_sem=w_send.at[r], recv_sem=w_recv.at[r],
                device_id=near_x, device_id_type=MESH,
            )
        ]

    def time_forward(j, left):
        r = 3 - j if left else j + 1
        pltpu.make_async_remote_copy(
            src_ref=time_piece(0, r), dst_ref=time_piece(0, r), send_sem=u_send.at[0, 0], recv_sem=u_recv.at[r],
            device_id=near_x, device_id_type=MESH,
        ).wait_recv()
        if j < 2:
            pl.when(z < 3 if left else z > 0)(lambda: start(time_z(left, j + 1)))
        start(time_x(0, r))

    def start(all_copies):
        for copy in all_copies:
            copy.start()

    def landed(all_copies):
        for copy in all_copies:
            copy.wait_recv()

    def sent(all_copies):
        for copy in all_copies:
            copy.wait_send()

    def token_copies(k):
        peer = (y, x, k % 2, 2 * c + k // 2)
        at = pl.ds(pl.multiple_of(z * BLK, BLK), BLK)
        return [
            pltpu.make_async_remote_copy(
                src_ref=src, dst_ref=dst, send_sem=send.at[k], recv_sem=recv.at[z], device_id=peer, device_id_type=MESH
            )
            for src, dst, send, recv in (
                (tok.at[k], rows_out.at[:, at], t_send, t_recv),
                (vec, vec_out.at[:, at], v_send, v_recv),
            )
        ]

    def token_local(k):
        at = pl.ds(pl.multiple_of(z * BLK, BLK), BLK)
        return [
            pltpu.make_async_copy(tok.at[k], rows_out.at[:, at], local.at[2]),
            pltpu.make_async_copy(vec, vec_out.at[:, at], local.at[3]),
        ]

    def stays(k):
        return jnp.logical_and(2 * c + k // 2 == z, c == k % 2)

    def from_right(j):
        return z <= 2 - j

    def from_left(j):
        return z >= j + 1

    pl.when(z < 3)(lambda: start(z_copies(True, 0)))
    pl.when(z > 0)(lambda: start(z_copies(False, 0)))
    keep = [
        pltpu.make_async_copy(mine.at[:, pl.ds(0, wide)], wq.at[:, pl.ds(pl.multiple_of(z * wide, half), wide)], local.at[0]),
        pltpu.make_async_copy(mine.at[:, pl.ds(wide, half)], wo.at[:, pl.ds(pl.multiple_of(z * half, half), half)], local.at[1]),
        pltpu.make_async_copy(later, wt.at[:, pl.ds(pl.multiple_of(z * span, span), span)], local.at[4]),
    ]
    start(keep)

    def forward(j, left):
        r = 3 - j if left else j + 1
        landed(copies(piece(0, 0, r), piece(0, 0, r), z_send.at[0, 0], z_recv.at[r], near_y))
        if j < 2:
            pl.when(z < 3 if left else z > 0)(lambda: start(z_copies(left, j + 1)))
        start(y_copies(r))
        start(x_copies(r))

    def corners(j, left):
        r = 3 - j if left else j + 1
        landed(copies(piece(1, 0, r), piece(1, 0, r), y_send.at[r], y_recv.at[r], near_y))
        start(corner_x(r))
        landed(copies(piece(0, 1, r), piece(0, 1, r), x_send.at[r], x_recv.at[r], near_x))
        start(corner_y(r))

    for j in range(3):
        for left in (True, False):
            pl.when(from_left(j) if left else from_right(j))(lambda j=j, left=left: forward(j, left))
        if j == 0:
            for k in range(4):
                pl.when(stays(k))(lambda k=k: start(token_local(k)))
                pl.when(jnp.logical_not(stays(k)))(lambda k=k: start(token_copies(k)))
            pl.when(z < 3)(lambda: start(time_z(True, 0)))
            pl.when(z > 0)(lambda: start(time_z(False, 0)))
        else:
            for left in (True, False):
                pl.when(from_left(j - 1) if left else from_right(j - 1))(lambda j=j, left=left: corners(j - 1, left))
    for left in (True, False):
        pl.when(from_left(2) if left else from_right(2))(lambda left=left: corners(2, left))
    for j in range(3):
        for left in (True, False):
            pl.when(from_left(j) if left else from_right(j))(lambda j=j, left=left: time_forward(j, left))

    for copy in keep:
        copy.wait()
    for r in (1, 2, 3):
        part = piece(1, 1, r, split=True)
        landed(copies(part[:1], part[:1], p_send.at[r], p_recv.at[r], near_x))
        landed(copies(part[1:], part[1:], q_send.at[r], q_recv.at[r], near_y))
        for group in (y_copies(r), x_copies(r), corner_x(r), corner_y(r), time_x(0, r)):
            sent(group)
        landed(time_x(1, r))
    for step in range(3):
        pl.when(jnp.logical_and(z >= step, z < 3))(lambda step=step: sent(z_copies(True, step) + time_z(True, step)))
        pl.when(jnp.logical_and(z + step <= 3, z > 0))(lambda step=step: sent(z_copies(False, step) + time_z(False, step)))
    for k in range(4):
        def finish_local(k=k):
            for copy in token_local(k):
                copy.wait()

        pl.when(stays(k))(finish_local)
        pl.when(jnp.logical_not(stays(k)))(lambda k=k: sent(token_copies(k)))
    for s in range(4):
        at = pl.ds(s * BLK, BLK)
        away = jnp.logical_not(jnp.logical_and(z == s, z // 2 == c))

        def arrived(s=s, at=at):
            for src, dst, send, recv in (
                (tok.at[0], rows_out.at[:, at], t_send, t_recv),
                (vec, vec_out.at[:, at], v_send, v_recv),
            ):
                pltpu.make_async_remote_copy(
                    src_ref=src, dst_ref=dst, send_sem=send.at[0], recv_sem=recv.at[s], device_id=near_y, device_id_type=MESH
                ).wait_recv()

        pl.when(away)(arrived)


def arrive(tok, vec, mine, later):
    own, width, half = tok.shape[1], 4 * tok.shape[2], mine.shape[1] // 4
    dma = pltpu.SemaphoreType.DMA
    anywhere = pl.BlockSpec(memory_space=pl.ANY)
    return pl.pallas_call(
        arrive_kernel,
        in_specs=[anywhere] * 4,
        out_specs=[anywhere] * 5,
        out_shape=[
            jax.ShapeDtypeStruct((own, width), BF16),
            jax.ShapeDtypeStruct((vec.shape[0], width), BF16),
            jax.ShapeDtypeStruct((width, 12 * half), BF16),
            jax.ShapeDtypeStruct((width, 4 * half), BF16),
            jax.ShapeDtypeStruct((width, 4 * later.shape[1]), BF16),
        ],
        scratch_shapes=[
            dma((2, 3, 2)), dma((4, 2)), dma((4, 2)), dma((4, 2)), dma((4, 2)), dma((4, 2)),
            dma((4, 1)), dma((4, 1)), dma((4, 2)), dma((4, 2)),
            dma((4,)), dma((4,)), dma((4,)), dma((4,)),
            dma((2, 3)), dma((4,)), dma((4,)), dma((4,)), dma((5,)),
        ],
        compiler_params=pltpu.CompilerParams(collective_id=0, has_side_effects=True),
        name="arrive",
    )(tok, vec, mine, later)


def dot_nn(a, b):
    return lax.dot_general(a, b, (((1,), (0,)), ((), ())), preferred_element_type=F32)


def dot_nt(a, b):
    return lax.dot_general(a, b, (((1,), (1,)), ((), ())), preferred_element_type=F32)


def dot_tn(a, b):
    return lax.dot_general(a, b, (((0,), (0,)), ((), ())), preferred_element_type=F32)


def attend_pair(q, k, v, bias, scale):
    mixed, totals = [], []
    for i in range(2):
        mine = slice(i * HEAD_DIM, (i + 1) * HEAD_DIM)
        scores = dot_nt(k[:, mine], q[:, mine]) * scale
        if bias is not None:
            scores = scores + bias
        highest = jnp.max(scores, axis=0, keepdims=True)
        exponent = jnp.exp(scores - highest)
        total = jnp.sum(exponent, axis=0, keepdims=True)
        totals.append(highest + jnp.log(total))
        mixed.append(dot_tn(v[:, mine], exponent.astype(BF16)) * (1.0 / total))
    return (jnp.concatenate(mixed, axis=0).T, totals)


def attend_pair_back(q, k, v, g, totals, bias, scale):
    grads = ([], [], [])
    for i in range(2):
        mine = slice(i * HEAD_DIM, (i + 1) * HEAD_DIM)
        scores = dot_nt(k[:, mine], q[:, mine]) * scale
        if bias is not None:
            scores = scores + bias
        p = jnp.exp(scores - totals[i])
        dp = dot_nt(v[:, mine], g[:, mine])
        ds = (p * (dp - jnp.sum(p * dp, axis=0, keepdims=True))).astype(BF16)
        grads[0].append(dot_tn(k[:, mine], ds) * scale)
        grads[1].append(dot_nn(ds, q[:, mine]) * scale)
        grads[2].append(dot_nn(p.astype(BF16), g[:, mine]))
    return (
        jnp.concatenate(grads[0], axis=0).T,
        jnp.concatenate(grads[1], axis=1),
        jnp.concatenate(grads[2], axis=1),
    )


PAIR = 2 * HEAD_DIM


def space_attend_kernel(scale, qkv_ref, out_ref, total_ref):
    for i in range(out_ref.shape[1] // PAIR):
        q, k, v = (qkv_ref[:, (3 * i + part) * PAIR : (3 * i + part + 1) * PAIR] for part in range(3))
        mixed, totals = attend_pair(q, k, v, None, scale)
        out_ref[:, i * PAIR : (i + 1) * PAIR] = mixed.astype(BF16)
        for h in range(2):
            total_ref[0, 2 * i + h : 2 * i + h + 1, :] = totals[h]


def space_attend_back_kernel(scale, qkv_ref, grad_ref, total_ref, out_ref):
    for i in range(grad_ref.shape[1] // PAIR):
        q, k, v = (qkv_ref[:, (3 * i + part) * PAIR : (3 * i + part + 1) * PAIR] for part in range(3))
        totals = [total_ref[0, 2 * i + h : 2 * i + h + 1, :] for h in range(2)]
        grads = attend_pair_back(q, k, v, grad_ref[:, i * PAIR : (i + 1) * PAIR], totals, None, scale)
        for part in range(3):
            out_ref[:, (3 * i + part) * PAIR : (3 * i + part + 1) * PAIR] = grads[part].astype(BF16)


def attention_cost(groups, rows, heads, products):
    return pl.CostEstimate(
        flops=8 * products * groups * heads * rows * rows * HEAD_DIM,
        transcendentals=groups * heads * rows * rows,
        bytes_accessed=2 * groups * rows * heads * HEAD_DIM * 2 * products,
    )


def space_attend(qkv, frames, patches, heads, scale):
    width = heads * HEAD_DIM
    return pl.pallas_call(
        functools.partial(space_attend_kernel, scale),
        grid=(frames,),
        in_specs=[pl.BlockSpec((patches, 3 * width), lambda i: (i, 0))],
        out_specs=[
            pl.BlockSpec((patches, width), lambda i: (i, 0)),
            pl.BlockSpec((1, heads, patches), lambda i: (i, 0, 0)),
        ],
        out_shape=[
            jax.ShapeDtypeStruct((frames * patches, width), BF16),
            jax.ShapeDtypeStruct((frames, heads, patches), F32),
        ],
        cost_estimate=attention_cost(frames, patches, heads, 2),
        name="space_attend",
    )(qkv)


def space_attend_back(qkv, grad, total, frames, patches, heads, scale):
    width = heads * HEAD_DIM
    return pl.pallas_call(
        functools.partial(space_attend_back_kernel, scale),
        grid=(frames,),
        in_specs=[
            pl.BlockSpec((patches, 3 * width), lambda i: (i, 0)),
            pl.BlockSpec((patches, width), lambda i: (i, 0)),
            pl.BlockSpec((1, heads, patches), lambda i: (i, 0, 0)),
        ],
        out_specs=pl.BlockSpec((patches, 3 * width), lambda i: (i, 0)),
        out_shape=jax.ShapeDtypeStruct((frames * patches, 3 * width), BF16),
        cost_estimate=attention_cost(frames, patches, heads, 5),
        name="space_attend_back",
    )(qkv, grad, total)


GROUP = 8
CHUNK = 32


def time_kernel(back, scale, heads, *refs):
    if back:
        (own_ref, rider_ref, joined_ref, total_ref, wq_ref, wo_ref, bias_ref, all_ref, out_ref, delta_ref, rider_out) = refs[:11]
        refs = refs[11:]
    else:
        (own_ref, rider_ref, wq_ref, wo_ref, bias_ref, all_ref, out_ref, mixed_ref, total_ref, delta_ref, rider_out) = refs[:11]
        refs = refs[11:]
    (
        held, wide, narrow, kept, core_out, core_in, near_out, near_in,
        gy_send, gy_recv, gc_send, gc_recv, gd_send, gd_recv, sc_send, sc_recv, sy_send, sy_recv,
        r_send, r_recv, r_local, out_sem,
    ) = refs
    y, x, c, z = (lax.axis_index(name) for name in AXES)
    near, pair = (1 - y, x, c, z), (y, x, 1 - c, z)
    frames = held.shape[0] // 4
    chunks = held.shape[1] // CHUNK
    width = heads * HEAD_DIM
    groups = CHUNK // GROUP

    barrier = pltpu.get_barrier_semaphore()
    for dc in range(2):
        for dz in range(4):
            if dc or dz:
                pl.semaphore_signal(barrier, inc=1, device_id=(y, x, (c + dc) % 2, (z + dz) % 4), device_id_type=MESH)
    pl.semaphore_signal(barrier, inc=1, device_id=near, device_id_type=MESH)
    pl.semaphore_wait(barrier, 8)

    def remote(src, dst, send, recv, peer):
        return pltpu.make_async_remote_copy(
            src_ref=src, dst_ref=dst, send_sem=send, recv_sem=recv, device_id=peer, device_id_type=MESH
        )

    def patches(k):
        return pl.ds(pl.multiple_of(k * CHUNK, CHUNK), CHUNK)

    def block(b, k):
        return held.at[pl.ds(b * frames, frames), patches(k)]

    def gather_y(k):
        return remote(own_ref.at[:, patches(k)], block(1, k), gy_send.at[k], gy_recv.at[k], near)

    def gather_c(k):
        return remote(own_ref.at[:, patches(k)], block(2, k), gc_send.at[k], gc_recv.at[k], pair)

    def gather_d(k):
        return remote(block(1, k), block(3, k), gd_send.at[k], gd_recv.at[k], pair)

    def scatter_c(k):
        return remote(core_out.at[k], core_in.at[k], sc_send.at[k], sc_recv.at[k], pair)

    def scatter_y(k):
        return remote(near_out.at[k], near_in.at[k], sy_send.at[k], sy_recv.at[k], near)

    def save(k):
        return pltpu.make_async_copy(held.at[:, patches(k)], all_ref.at[:, patches(k)], out_sem.at[k])

    def columns(s):
        return pl.ds(pl.multiple_of(s * BLK, BLK), BLK)

    def stays(k):
        if back:
            return jnp.logical_and(z == k, z // 2 == c)
        return jnp.logical_and(2 * c + k // 2 == z, c == k % 2)

    def ride(k):
        if back:
            src, dst = rider_ref.at[:, columns(k)], rider_out.at[2 * (z % 2) + c]
            peer, slot = (y, x, z // 2, k), 2 * (z % 2) + c
        else:
            src, dst = rider_ref.at[k], rider_out.at[:, columns(z)]
            peer, slot = (y, x, k % 2, 2 * c + k // 2), z
        return src, dst, peer, slot

    def ride_remote(k):
        src, dst, peer, slot = ride(k)
        return remote(src, dst, r_send.at[k], r_recv.at[slot], peer)

    def ride_local(k):
        src, dst, _, _ = ride(k)
        return pltpu.make_async_copy(src, dst, r_local.at[0])

    def ride_landed(k):
        if back:
            src, dst = rider_ref.at[:, columns(k)], rider_out.at[k]
        else:
            src, dst = rider_ref.at[k], rider_out.at[:, columns(k)]
        return remote(src, dst, r_send.at[k], r_recv.at[k], near)

    def from_self(k):
        if back:
            return jnp.logical_and(2 * c + k // 2 == z, c == k % 2)
        return jnp.logical_and(z == k, z // 2 == c)

    for k in range(chunks):
        gather_y(k).start()
        gather_c(k).start()
    for k in range(4):
        pl.when(stays(k))(lambda k=k: ride_local(k).start())
        pl.when(jnp.logical_not(stays(k)))(lambda k=k: ride_remote(k).start())
    held[:frames] = own_ref[...]

    def finish(k):
        scatter_c(k).wait_recv()
        both = kept[:, patches(k)] + core_in[k].astype(F32)
        near_out[k] = both[frames:].astype(BF16)
        delta_ref[:, patches(k)] = both[:frames]
        scatter_y(k).start()

    def pass_on(k):
        gather_y(k).wait_recv()
        gather_d(k).start()

    def one_group(i, rows):
        at = pl.ds(pl.multiple_of(i * GROUP, GROUP), GROUP)
        count = 4 * frames * GROUP
        bias = bias_ref[...]
        for lo in range(0, width, PAIR):
            q, k, v = (
                wide[:, at, part * width + lo : part * width + lo + PAIR].reshape(count, PAIR).astype(BF16)
                for part in range(3)
            )
            h = lo // HEAD_DIM
            if back:
                g = narrow[:, at, lo : lo + PAIR].reshape(count, PAIR).astype(BF16)
                totals = [total_ref[rows * groups + i, h + j : h + j + 1, :] for j in range(2)]
                grads = attend_pair_back(q, k, v, g, totals, bias, scale)
                for part in range(3):
                    wide[:, at, part * width + lo : part * width + lo + PAIR] = grads[part].reshape(
                        4 * frames, GROUP, PAIR
                    )
            else:
                mixed, totals = attend_pair(q, k, v, bias, scale)
                narrow[:, at, lo : lo + PAIR] = mixed.reshape(4 * frames, GROUP, PAIR)
                for j in range(2):
                    total_ref[rows * groups + i, h + j : h + j + 1, :] = totals[j]

    def one_chunk(k, carry):
        pl.when(k + 1 < chunks)(lambda: pass_on(k + 1))
        gather_c(k).wait_recv()
        gather_d(k).wait_recv()
        count = 4 * frames * CHUNK
        lhs = held[:, patches(k)].reshape(count, held.shape[2])
        if back:
            wide[...] = joined_ref[:, patches(k)].astype(F32)
            narrow[...] = dot_nn(lhs, wo_ref[...]).astype(BF16).astype(F32).reshape(narrow.shape)
        else:
            joined = dot_nn(lhs, wq_ref[...]).astype(BF16)
            out_ref[:, patches(k)] = joined.reshape(wide.shape)
            wide[...] = joined.astype(F32).reshape(wide.shape)
        save(k).start()
        lax.fori_loop(0, groups, lambda i, carry: (one_group(i, k), carry)[1], 0)
        if back:
            grads = wide[...].astype(BF16)
            out_ref[:, patches(k)] = grads
            partial = dot_nt(grads.reshape(count, 3 * width), wq_ref[...])
        else:
            mixed = narrow[...].astype(BF16)
            mixed_ref[:, patches(k)] = mixed
            partial = dot_nt(mixed.reshape(count, width), wo_ref[...])
        partial = partial.reshape(4 * frames, CHUNK, held.shape[2])
        kept[:, patches(k)] = partial[: 2 * frames]
        core_out[k] = partial[2 * frames :].astype(BF16)
        scatter_c(k).start()
        pl.when(k > 0)(lambda: finish(k - 1))
        return carry

    pass_on(0)
    lax.fori_loop(0, chunks, one_chunk, 0)
    finish(chunks - 1)
    for k in range(chunks):
        scatter_y(k).wait_recv()
        delta_ref[:, patches(k)] = delta_ref[:, patches(k)] + near_in[k].astype(F32)
    for k in range(chunks):
        for copy in (gather_y(k), gather_c(k), gather_d(k), scatter_c(k), scatter_y(k)):
            copy.wait_send()
        save(k).wait()
    for k in range(4):
        pl.when(stays(k))(lambda k=k: ride_local(k).wait())
        pl.when(jnp.logical_not(stays(k)))(lambda k=k: ride_remote(k).wait_send())
        pl.when(jnp.logical_not(from_self(k)))(lambda k=k: ride_landed(k).wait_recv())


def time_call(back, own, rider, saved, wq, wo, bias, scale):
    frames, patches, features = own.shape
    width = wo.shape[1]
    heads = width // HEAD_DIM
    chunks = patches // CHUNK
    rows = 4 * frames * GROUP
    dma = pltpu.SemaphoreType.DMA
    anywhere = pl.BlockSpec(memory_space=pl.ANY)
    whole = pl.BlockSpec(memory_space=pltpu.VMEM)
    out_shape = [
        jax.ShapeDtypeStruct((4 * frames, patches, features), BF16),
        jax.ShapeDtypeStruct((4 * frames, patches, 3 * width), BF16),
    ]
    if not back:
        out_shape += [
            jax.ShapeDtypeStruct((4 * frames, patches, width), BF16),
            jax.ShapeDtypeStruct((patches // GROUP, heads, rows), F32),
        ]
    rider_shape = (4, frames * patches, BLK) if back else (frames * patches, features)
    out_shape += [
        jax.ShapeDtypeStruct((frames, patches, features), F32),
        jax.ShapeDtypeStruct(rider_shape, BF16),
    ]
    return pl.pallas_call(
        functools.partial(time_kernel, back, scale, heads),
        in_specs=[whole, anywhere] + [whole] * (len(saved) + 3),
        out_specs=[anywhere] + [whole] * (len(out_shape) - 2) + [anywhere],
        out_shape=out_shape,
        scratch_shapes=[
            pltpu.VMEM((4 * frames, patches, features), BF16),
            pltpu.VMEM((4 * frames, CHUNK, 3 * width), F32),
            pltpu.VMEM((4 * frames, CHUNK, width), F32),
            pltpu.VMEM((2 * frames, patches, features), F32),
            pltpu.VMEM((chunks, 2 * frames, CHUNK, features), BF16),
            pltpu.VMEM((chunks, 2 * frames, CHUNK, features), BF16),
            pltpu.VMEM((chunks, frames, CHUNK, features), BF16),
            pltpu.VMEM((chunks, frames, CHUNK, features), BF16),
        ]
        + [dma((chunks,))] * 10
        + [dma((4,)), dma((4,)), dma((1,)), dma((chunks,))],
        compiler_params=pltpu.CompilerParams(
            collective_id=2 if back else 1, has_side_effects=True, vmem_limit_bytes=48 * 1024 * 1024
        ),
        cost_estimate=pl.CostEstimate(flops=10**10, transcendentals=10**6, bytes_accessed=10**8),
        name="time_back" if back else "time_forward",
    )(own, rider, *saved, wq, wo, bias)


def tie(*values):
    return lax.optimization_barrier(values)


def norm_rows(resid):
    mean = jnp.mean(resid, axis=-1, keepdims=True)
    centered = resid - mean
    inverse = lax.rsqrt(jnp.mean(centered * centered, axis=-1, keepdims=True) + eps_norm)
    return (centered * inverse, inverse)


def norm_rows_back(grad, standardized, inverse, gain):
    gain_grad = jnp.sum(grad * standardized, axis=0)
    inner = grad * gain
    mean = jnp.mean(inner, axis=-1, keepdims=True)
    along = jnp.mean(inner * standardized, axis=-1, keepdims=True)
    return ((inner - mean - standardized * along) * inverse, gain_grad)


def cols(parts):
    return jnp.concatenate(parts, axis=1)


def rows_of(parts):
    return jnp.concatenate(parts, axis=0)


def token_parallel(
    tokens,
    cotangent,
    ratio,
    priority,
    frame_order,
    mask_embed,
    gains,
    qkv_space,
    out_space,
    qkv_time,
    out_time,
    w_in,
    w_out,
):
    scale = 1.0 / math.sqrt(HEAD_DIM)
    y, x, c, z = (lax.axis_index(name) for name in AXES)
    patches = tokens.shape[2]
    width = qkv_space.shape[0]
    frames_own = tokens.shape[0] * tokens.shape[1] // 4
    frames_all = frame_order.shape[1]
    own = frames_own * patches
    hidden_own = w_in.shape[1] // 2
    plane = 2 * y + x
    k_own = 2 * (z % 2) + c

    def return_rows(v):
        landed = jnp.stack(
            [
                lax.ppermute(
                    lax.dynamic_slice_in_dim(v, (k_own ^ r) * BLK, BLK, 1),
                    AXES,
                    [(b, a) for a, b in spread_pairs(r)],
                )
                for r in range(4)
            ]
        )
        return jnp.stack(
            [lax.dynamic_index_in_dim(landed, k ^ z, 0, keepdims=False) for k in range(4)]
        ).reshape(tokens.shape)

    masked_here = (priority < ratio[:, None, None]).astype(jnp.int32).reshape(2, -1)
    info = cols([masked_here, frame_order])
    info = jnp.where(z // 2 == c, info, hop_c(info))
    info = lax.dynamic_index_in_dim(info, z % 2, 0, keepdims=False)
    masked = lax.dynamic_slice_in_dim(info, c * own, own, 0)[:, None] != 0
    order = info[2 * own :].reshape(2, 2, frames_own)
    order = jnp.where(y == 1, order[::-1], order)
    order = jnp.where(c == 1, order[:, ::-1], order).swapaxes(0, 1).reshape(frames_all)
    order = jnp.repeat(order, GROUP)
    patch = jnp.arange(frames_all * GROUP) % GROUP
    visible = (order[:, None] <= order[None, :]) & (patch[:, None] == patch[None, :])
    bias = jnp.where(visible, 0.0, -1e30).astype(F32)

    half = qkv_space.shape[2] // 2
    sp_own = cols(
        [
            lax.dynamic_slice_in_dim(qkv_space, c * half, half, 2).reshape(width, -1),
            lax.dynamic_slice_in_dim(out_space, c * half, half, 0).T,
        ]
    )
    vectors = rows_of([mask_embed[None], gains, jnp.zeros((4, BLK), BF16)])
    head = (2 * y + c) * HEAD_DIM
    ti_own = cols(
        [
            lax.dynamic_slice_in_dim(qkv_time, head, HEAD_DIM, 2).reshape(width, -1),
            lax.dynamic_slice_in_dim(out_time, head, HEAD_DIM, 0).T,
        ]
    )
    arrived, vectors, ws_qkv, ws_out, wt_all = arrive(tokens.reshape(4, own, BLK), vectors, sp_own, ti_own)
    wt_all = wt_all.reshape(width, 4, 4, HEAD_DIM)
    wt_qkv = jnp.swapaxes(wt_all[:, :, :3], 1, 2).reshape(width, 12 * HEAD_DIM)
    wt_out = wt_all[:, :, 3].reshape(width, 4 * HEAD_DIM)
    source = arrived.astype(F32)
    embed_row = vectors[:1].astype(F32)
    gain = [vectors[1 + i : 2 + i].astype(F32) for i in range(3)]

    ff_in = lax.dynamic_slice(w_in, (plane * BLK, c * hidden_own), (BLK, hidden_own))
    ff_out = lax.dynamic_slice(w_out, (c * hidden_own, plane * BLK), (hidden_own, BLK)).T
    arrived, ff_in, ff_out = tie(arrived, ff_in, ff_out)

    def gather_ff(w):
        w = lax.all_gather(w, ("mp", "tm", "x")).reshape(4, width, hidden_own)
        return [w[s] for s in range(4)]

    def pair_gather(v):
        return rows_of([v, hop_c(v)])

    def pair_scatter(v):
        return v[:own] + hop_c(v[own:].astype(BF16)).astype(F32)

    heads_s = 4 * half // HEAD_DIM
    frames_pair = 2 * frames_own
    resid0 = jnp.where(masked, embed_row, source)
    std0, inv0 = norm_rows(resid0)
    normed0 = pair_gather((std0 * gain[0]).astype(BF16))
    wf_in, wf_out = gather_ff(ff_in), gather_ff(ff_out)
    joined0 = dot_nn(normed0, ws_qkv).astype(BF16)
    mixed0, total0 = space_attend(joined0, frames_pair, patches, heads_s, scale)
    resid1 = resid0 + pair_scatter(dot_nt(mixed0, ws_out))
    std1, inv1 = norm_rows(resid1)
    normed1, joined1, mixed1, total1, delta, upstream = time_call(
        False,
        (std1 * gain[1]).astype(BF16).reshape(frames_own, patches, width),
        cotangent.reshape(4, own, BLK),
        [],
        wt_qkv,
        wt_out,
        bias,
        scale,
    )
    normed1 = normed1.reshape(4 * own, width)
    mixed1 = mixed1.reshape(4 * own, -1)
    grad3 = jnp.where(masked, upstream, jnp.zeros((), BF16))
    gb3 = pair_gather(grad3)
    resid2 = resid1 + delta.reshape(own, width)
    std2, inv2 = norm_rows(resid2)
    normed2 = pair_gather((std2 * gain[2]).astype(BF16))
    hidden, pulls = [], []
    for w in wf_in:
        activated, pull = jax.vjp(gelu_tanh, dot_nn(normed2, w))
        hidden.append(activated.astype(BF16))
        pulls.append(pull)
    block_part = sum(dot_nt(h, w) for h, w in zip(hidden, wf_out))
    block_rows = (resid2 + pair_scatter(block_part)).astype(BF16)

    def plane_scatter(lhs, parts):
        parts = jnp.stack([dot_tn(lhs, rhs).astype(BF16) for rhs in parts])
        return lax.psum_scatter(parts, ("tm", "x"), scatter_dimension=1, tiled=True)

    def line_scatter(v):
        return lax.psum_scatter(v, "mp", scatter_dimension=0).astype(F32)

    def send_x(lhs, rhs):
        there = jnp.where(x == 0, cols([lhs[:, BLK : 2 * BLK], lhs[:, 3 * BLK :]]), cols([lhs[:, :BLK], lhs[:, 2 * BLK : 3 * BLK]]))
        return hop_x(dot_tn(there, rhs).astype(BF16))

    def keep_x(lhs, rhs, landed):
        here = jnp.where(x == 1, cols([lhs[:, BLK : 2 * BLK], lhs[:, 3 * BLK :]]), cols([lhs[:, :BLK], lhs[:, 2 * BLK : 3 * BLK]]))
        return dot_tn(here, rhs) + landed.astype(F32)

    def mine_y(v):
        return jnp.where(y == 0, v[:BLK], v[BLK:])

    def other_y(v):
        return jnp.where(y == 1, v[:BLK], v[BLK:])

    def reduce_z(pieces):
        total = pieces[0]
        for r in (1, 2, 3):
            total = total + hop_z(pieces[r].astype(BF16), r).astype(F32)
        return total

    def swap_c(total):
        rows = BLK // 2
        kept = lax.dynamic_slice_in_dim(total, c * rows, rows, 0)
        sent = hop_c(lax.dynamic_slice_in_dim(total, (1 - c) * rows, rows, 0).astype(BF16))
        return (kept, sent.astype(F32))

    def by_core(kept, landed):
        return jnp.where(c == 0, jnp.concatenate([kept, landed], -1), jnp.concatenate([landed, kept], -1))

    w_out_part = plane_scatter(gb3, hidden)
    grad_inner = [pull(dot_nn(gb3, w))[0].astype(BF16) for pull, w in zip(pulls, wf_out)]
    part2 = pair_scatter(sum(dot_nt(g, w) for g, w in zip(grad_inner, wf_in)))
    w_in_part = plane_scatter(normed2, grad_inner)
    back2, gain_grad2 = norm_rows_back(part2, std2, inv2, gain[2])
    grad2 = grad3.astype(F32) + back2
    gb2, djoined1, part1, block_out = time_call(
        True,
        grad2.astype(BF16).reshape(frames_own, patches, width),
        block_rows,
        [joined1, total1],
        wt_qkv,
        wt_out,
        bias,
        scale,
    )
    block_out = block_out.reshape(tokens.shape)
    gb2 = gb2.reshape(4 * own, width)
    djoined1 = djoined1.reshape(4 * own, -1)
    part1 = part1.reshape(own, width)
    back1, gain_grad1 = norm_rows_back(part1, std1, inv1, gain[1])
    grad1 = grad2 + back1
    gb1 = pair_gather(grad1.astype(BF16))
    t_out_x = send_x(gb2, mixed1)
    t_qkv_x = send_x(normed1, djoined1)
    dmixed0 = dot_nn(gb1, ws_out).astype(BF16)
    s_out_x = send_x(gb1, mixed0)
    djoined0 = space_attend_back(joined0, dmixed0, total0, frames_pair, patches, heads_s, scale)
    djoined0, t_out_x, t_qkv_x, w_out_part, s_out_x = tie(djoined0, t_out_x, t_qkv_x, w_out_part, s_out_x)
    g_w_out = line_scatter(w_out_part)
    s_qkv_x = send_x(normed0, djoined0)
    part0 = pair_scatter(dot_nt(djoined0, ws_qkv))
    s_out_kept = keep_x(gb1, mixed0, s_out_x)
    s_out_y = hop_y(other_y(s_out_kept).astype(BF16))
    g_w_in = line_scatter(w_in_part)
    g_t_out = keep_x(gb2, mixed1, t_out_x)
    g_t_qkv = keep_x(normed1, djoined1, t_qkv_x)
    z_at = [(z + r) % 4 for r in range(4)]
    span = 4 * HEAD_DIM
    g_time = reduce_z(
        [
            cols(
                [lax.dynamic_slice_in_dim(g_t_qkv, j * span + s * HEAD_DIM, HEAD_DIM, 1) for j in range(3)]
                + [lax.dynamic_slice_in_dim(g_t_out, s * HEAD_DIM, HEAD_DIM, 1)]
            )
            for s in z_at
        ]
    )
    s_qkv_kept = keep_x(normed0, djoined0, s_qkv_x)
    s_qkv = mine_y(s_qkv_kept) + hop_y(other_y(s_qkv_kept).astype(BF16)).astype(F32)
    s_out = mine_y(s_out_kept) + s_out_y.astype(F32)
    g_space = reduce_z(
        [
            cols(
                [
                    lax.dynamic_slice_in_dim(s_qkv, s * 3 * half, 3 * half, 1),
                    lax.dynamic_slice_in_dim(s_out, s * half, half, 1),
                ]
            )
            for s in z_at
        ]
    )
    back0, gain_grad0 = norm_rows_back(part0, std0, inv0, gain[0])
    grad0 = grad1 + back0
    grad_tokens = return_rows(jnp.where(masked, 0.0, grad0).astype(BF16)).astype(F32)
    grad_embed = jnp.sum(jnp.where(masked, grad0, 0.0), axis=0)
    small = jnp.stack([gain_grad0, gain_grad1, gain_grad2, grad_embed])
    for hop in (hop_c, hop_y, hop_x):
        small = small + hop(small)
    small_at = [lax.dynamic_slice_in_dim(small, s * BLK, BLK, 1) for s in z_at]
    small = small_at[0]
    for r in (1, 2, 3):
        small = small + hop_z(small_at[r], r)

    rows = BLK // 2
    kept, landed = swap_c(g_space)
    grad_qkv_space = by_core(
        kept[:, : 3 * half].reshape(rows, 3, half), landed[:, : 3 * half].reshape(rows, 3, half)
    )
    grad_out_space = by_core(kept[:, 3 * half :], landed[:, 3 * half :]).T
    kept, landed = swap_c(cols([g_w_in, g_w_out]))
    grad_w_in = by_core(kept[:, :hidden_own], landed[:, :hidden_own])
    grad_w_out = by_core(kept[:, hidden_own:], landed[:, hidden_own:]).T
    both = cols([mine_y(g_time), hop_y(other_y(g_time).astype(BF16)).astype(F32)])
    kept, landed = swap_c(both)
    quad = jnp.stack([kept, landed], 1).reshape(rows, 2, 2, 4, HEAD_DIM)
    quad = jnp.where(c == 1, quad[:, ::-1], quad)
    quad = jnp.where(y == 1, quad[:, :, ::-1], quad)
    quad = jnp.transpose(quad, (0, 3, 2, 1, 4)).reshape(rows, 4, 4 * HEAD_DIM)
    grad_qkv_time = quad[:, :3]
    grad_out_time = quad[:, 3].T
    return (
        block_out,
        grad_tokens,
        small[3],
        small[:3],
        grad_qkv_space,
        grad_out_space,
        grad_qkv_time,
        grad_out_time,
        grad_w_in,
        grad_w_out,
    )


def solution(mesh):
    sizes = (mesh.shape["tm"], mesh.shape["clip"], mesh.shape["mp"])
    if sizes == (2, 4, 4):
        mesh = jax.sharding.Mesh(mesh.devices.reshape(2, 2, 2, 4), AXES)
        step, clip = token_parallel, ("x", "c")
    else:
        step, clip = shards, ("clip",)
    return jax.shard_map(
        step,
        mesh=mesh,
        in_specs=(
            P(clip, "tm", None, "mp"),
            P(clip, "tm", None, "mp"),
            P(clip),
            P(clip, "tm", None),
            P(clip, None),
            P("mp"),
            P(None, "mp"),
            P(None, None, "mp"),
            P("mp", None),
            P(None, None, "mp"),
            P("mp", None),
            P(None, "mp"),
            P("mp", None),
        ),
        out_specs=(
            P(clip, "tm", None, "mp"),
            P(clip, "tm", None, "mp"),
            P("mp"),
            P(None, "mp"),
            P(("tm",) + clip, None, "mp"),
            P("mp", ("tm",) + clip),
            P(("tm",) + clip, None, "mp"),
            P("mp", ("tm",) + clip),
            P(("tm",) + clip, "mp"),
            P("mp", ("tm",) + clip),
        ),
        check_vma=False,
    )
```

```python
import functools
import math

import jax
import jax.numpy as jnp
from jax import lax
from jax.experimental import pallas as pl
from jax.experimental.pallas import tpu as pltpu
from jax.sharding import PartitionSpec as P

HEAD_DIM = 64
MICRO = 2


eps_norm = 1e-05


def gelu_tanh(values):
    return jax.nn.gelu(values, approximate=True)


def norm_forward_pass(residual_stream, gain_coefficients, complete_width):
    reduced_totals = lax.psum(
        (jnp.sum(residual_stream, axis=-1), jnp.sum(residual_stream * residual_stream, axis=-1)),
        "mp",
    )
    centered_rows = reduced_totals[0] / complete_width
    spread = reduced_totals[1] / complete_width - centered_rows * centered_rows
    inverse_scale = lax.rsqrt(spread + eps_norm)
    standardized_rows = (residual_stream - centered_rows[:, None]) * inverse_scale[:, None]
    shard_rows = (standardized_rows * gain_coefficients).astype(jnp.bfloat16)
    normalized_rows = lax.all_gather(shard_rows, "mp", axis=1, tiled=True)
    return (normalized_rows, standardized_rows, inverse_scale)


def norm_reverse_pass(
    normalized_gradient, standardized_rows, inverse_scale, gain_coefficients, complete_width
):
    gain_gradient = jnp.sum(normalized_gradient * standardized_rows, axis=0)
    standardized_gradient = normalized_gradient * gain_coefficients
    reduced_totals = lax.psum(
        (
            jnp.sum(standardized_gradient, axis=-1),
            jnp.sum(standardized_gradient * standardized_rows, axis=-1),
        ),
        "mp",
    )
    grad_resid = (
        standardized_gradient
        - reduced_totals[0][:, None] / complete_width
        - standardized_rows * (reduced_totals[1][:, None] / complete_width)
    ) * inverse_scale[:, None]
    return (grad_resid, gain_gradient)


def sum_features(grad_full):
    return lax.psum_scatter(
        grad_full.astype(jnp.bfloat16), "mp", scatter_dimension=1, tiled=True
    ).astype(jnp.float32)


def branch_out(hidden, weight):
    partial_rows = jnp.dot(hidden, weight, preferred_element_type=jnp.float32)
    return lax.psum_scatter(partial_rows, "mp", scatter_dimension=1, tiled=True)


def branch_back(grad_resid, hidden, weight):
    grad_rows = lax.all_gather(grad_resid.astype(jnp.bfloat16), "mp", axis=1, tiled=True)
    weight_grad = jnp.einsum("rk,rd->kd", hidden, grad_rows, preferred_element_type=jnp.float32)
    grad_hidden = jnp.einsum("rd,kd->rk", grad_rows, weight, preferred_element_type=jnp.float32)
    return (grad_hidden, weight_grad)


def qkv_back(normalized_rows, grad_joined, weight):
    weight_grad = jnp.einsum(
        "rd,trk->dtk", normalized_rows, grad_joined, preferred_element_type=jnp.float32
    )
    grad_full = jnp.einsum("trk,dtk->rd", grad_joined, weight, preferred_element_type=jnp.float32)
    return (weight_grad, sum_features(grad_full))


def reduce_grads(local_grads, small_grads):
    reduced = (
        lax.psum_scatter(local_grads[0], ("tm", "clip"), scatter_dimension=0, tiled=True),
        lax.psum_scatter(local_grads[1], ("tm", "clip"), scatter_dimension=1, tiled=True),
        lax.psum_scatter(local_grads[2], ("tm", "clip"), scatter_dimension=0, tiled=True),
        lax.psum_scatter(local_grads[3], ("tm", "clip"), scatter_dimension=1, tiled=True),
        lax.psum_scatter(local_grads[4], ("tm", "clip"), scatter_dimension=0, tiled=True),
        lax.psum_scatter(local_grads[5], ("tm", "clip"), scatter_dimension=1, tiled=True),
    )
    reduced_small = lax.psum((small_grads[0], small_grads[1]), ("tm", "clip"))
    return (reduced, reduced_small)


def space_forward(normalized_rows, weight, frame_count, patches, heads_local, scale):
    joined = jnp.einsum(
        "rd,dtk->trk", normalized_rows, weight, preferred_element_type=jnp.float32
    ).astype(jnp.bfloat16)
    shape_heads = (frame_count, patches, heads_local, HEAD_DIM)
    scores = (
        jnp.einsum(
            "bshd,bthd->bhst",
            joined[0].reshape(shape_heads),
            joined[1].reshape(shape_heads),
            preferred_element_type=jnp.float32,
        )
        * scale
    )
    highest = jnp.max(scores, axis=-1, keepdims=True)
    exponent = jnp.exp(scores - highest)
    reduced_totals = jnp.sum(exponent, axis=-1, keepdims=True)
    log_total = highest + jnp.log(reduced_totals)
    attention = (exponent / reduced_totals).astype(jnp.bfloat16)
    mixed = jnp.einsum(
        "bhst,bthd->bshd",
        attention,
        joined[2].reshape(shape_heads),
        preferred_element_type=jnp.float32,
    )
    return (
        joined,
        log_total,
        mixed.astype(jnp.bfloat16).reshape(frame_count * patches, heads_local * HEAD_DIM),
    )


def space_backward(grad_mixed, joined, log_total, frame_count, patches, heads_local, scale):
    shape_heads = (frame_count, patches, heads_local, HEAD_DIM)
    queries = joined[0].reshape(shape_heads)
    key_rows = joined[1].reshape(shape_heads)
    values = joined[2].reshape(shape_heads)
    grad_out = grad_mixed.reshape(shape_heads)
    scores = (
        jnp.einsum("bshd,bthd->bhst", queries, key_rows, preferred_element_type=jnp.float32) * scale
    )
    attention = jnp.exp(scores - log_total)
    grad_values = jnp.einsum(
        "bhst,bshd->bthd",
        attention.astype(jnp.bfloat16),
        grad_out,
        preferred_element_type=jnp.float32,
    )
    grad_att = jnp.einsum("bshd,bthd->bhst", grad_out, values, preferred_element_type=jnp.float32)
    grad_scores = (
        attention * (grad_att - jnp.sum(attention * grad_att, axis=-1, keepdims=True))
    ).astype(jnp.bfloat16)
    grad_queries = (
        jnp.einsum("bhst,bthd->bshd", grad_scores, key_rows, preferred_element_type=jnp.float32)
        * scale
    )
    grad_keys = (
        jnp.einsum("bhst,bshd->bthd", grad_scores, queries, preferred_element_type=jnp.float32)
        * scale
    )
    row_count = frame_count * patches
    stacked = jnp.stack(
        [
            grad_queries.reshape(row_count, -1),
            grad_keys.reshape(row_count, -1),
            grad_values.reshape(row_count, -1),
        ]
    )
    return stacked.astype(jnp.bfloat16)


def time_scores(queries, keys_all, visible, scale):
    scores = (
        jnp.einsum("cfshd,cgshd->chfgs", queries, keys_all, preferred_element_type=jnp.float32)
        * scale
    )
    return jnp.where(visible, scores, -1e30)


def time_forward(queries, keys_all, values_all, visible, scale):
    scores = time_scores(queries, keys_all, visible, scale)
    highest = jnp.max(scores, axis=3, keepdims=True)
    exponent = jnp.exp(scores - highest)
    reduced_totals = jnp.sum(exponent, axis=3, keepdims=True)
    log_total = highest + jnp.log(reduced_totals)
    attention = (exponent / reduced_totals).astype(jnp.bfloat16)
    mixed = jnp.einsum(
        "chfgs,cgshd->cfshd", attention, values_all, preferred_element_type=jnp.float32
    )
    return (log_total, mixed.astype(jnp.bfloat16))


def time_backward(grad_mixed, queries, keys_all, values_all, visible, log_total, scale):
    grad_out = grad_mixed.reshape(queries.shape)
    scores = time_scores(queries, keys_all, visible, scale)
    attention = jnp.exp(scores - log_total)
    grad_values = jnp.einsum(
        "chfgs,cfshd->cgshd",
        attention.astype(jnp.bfloat16),
        grad_out,
        preferred_element_type=jnp.float32,
    )
    grad_att = jnp.einsum(
        "cfshd,cgshd->chfgs", grad_out, values_all, preferred_element_type=jnp.float32
    )
    grad_scores = (
        attention * (grad_att - jnp.sum(attention * grad_att, axis=3, keepdims=True))
    ).astype(jnp.bfloat16)
    grad_queries = (
        jnp.einsum("chfgs,cgshd->cfshd", grad_scores, keys_all, preferred_element_type=jnp.float32)
        * scale
    )
    grad_keys = (
        jnp.einsum("chfgs,cfshd->cgshd", grad_scores, queries, preferred_element_type=jnp.float32)
        * scale
    )
    return (grad_queries, grad_keys, grad_values)


def shards(
    tokens,
    cotangent,
    ratio,
    priority,
    frame_order,
    mask_embed,
    gains,
    qkv_space,
    out_space,
    qkv_time,
    out_time,
    w_in,
    w_out,
):
    scale = 1.0 / math.sqrt(HEAD_DIM)
    clips_local = tokens.shape[0] // MICRO
    frames_local = tokens.shape[1]
    patches = tokens.shape[2]
    cols_local = tokens.shape[3]
    frames_all = frame_order.shape[1]
    hidden_width = qkv_space.shape[0]
    joined_local = qkv_space.shape[2]
    heads_local = joined_local // HEAD_DIM
    row_count = clips_local * frames_local * patches
    gain_broadcast = gains.astype(jnp.float32)
    embed_row = mask_embed.astype(jnp.float32)
    first_frame = lax.axis_index("tm") * frames_local
    shape_local = (clips_local, frames_local, patches, joined_local)
    shape_heads = (clips_local, frames_local, patches, heads_local, HEAD_DIM)
    shape_all = (clips_local, frames_all, patches, heads_local, HEAD_DIM)
    outputs = []
    input_grads = []
    weight_total = None
    small_total = None
    for batch_index in range(MICRO):
        lower = batch_index * clips_local
        upper = lower + clips_local
        source = tokens[lower:upper].reshape(row_count, cols_local).astype(jnp.float32)
        upstream = cotangent[lower:upper].reshape(row_count, cols_local).astype(jnp.float32)
        masked = (priority[lower:upper] < ratio[lower:upper][:, None, None]).reshape(row_count)
        order_rows = frame_order[lower:upper]
        residual_stream0 = jnp.where(masked[:, None], embed_row[None, :], source)
        normalized_rows0, standardized_rows0, inverse_deviation0 = norm_forward_pass(
            residual_stream0, gain_broadcast[0], hidden_width
        )
        joined0, total0, mixed0 = space_forward(
            normalized_rows0, qkv_space, clips_local * frames_local, patches, heads_local, scale
        )
        residual_stream1 = residual_stream0 + branch_out(mixed0, out_space)
        normalized_rows1, standardized_rows1, inverse_deviation1 = norm_forward_pass(
            residual_stream1, gain_broadcast[1], hidden_width
        )
        joined1 = jnp.einsum(
            "rd,dtk->trk", normalized_rows1, qkv_time, preferred_element_type=jnp.float32
        ).astype(jnp.bfloat16)
        queries_local = joined1[0].reshape(shape_local)
        keys_local = joined1[1].reshape(shape_local)
        values_local = joined1[2].reshape(shape_local)
        keys_all, values_all = (
            lax.all_gather(keys_local, "tm", axis=1, tiled=True),
            lax.all_gather(values_local, "tm", axis=1, tiled=True),
        )
        query_order = lax.dynamic_slice_in_dim(order_rows, first_frame, frames_local, axis=1)
        time_visible = (order_rows[:, None, :] <= query_order[:, :, None])[:, None, :, :, None]
        time_q = queries_local.reshape(shape_heads)
        time_k = keys_all.reshape(shape_all)
        time_v = values_all.reshape(shape_all)
        total1, mixed_frames = time_forward(time_q, time_k, time_v, time_visible, scale)
        mixed1 = mixed_frames.reshape(row_count, joined_local)
        residual_stream2 = residual_stream1 + branch_out(mixed1, out_time)
        normalized_rows2, standardized_rows2, inverse_deviation2 = norm_forward_pass(
            residual_stream2, gain_broadcast[2], hidden_width
        )
        projected = jnp.dot(normalized_rows2, w_in, preferred_element_type=jnp.float32)
        activated, gelu_pull = jax.vjp(gelu_tanh, projected)
        hidden = activated.astype(jnp.bfloat16)
        resid3 = residual_stream2 + branch_out(hidden, w_out)
        outputs.append(
            resid3.astype(jnp.bfloat16).reshape(clips_local, frames_local, patches, cols_local)
        )
        grad3 = jnp.where(masked[:, None], upstream, 0.0)
        grad_hidden, grad_w_out = branch_back(grad3, hidden, w_out)
        grad_inner = gelu_pull(grad_hidden)[0].astype(jnp.bfloat16)
        grad_w_in = jnp.einsum(
            "rd,rk->dk", normalized_rows2, grad_inner, preferred_element_type=jnp.float32
        )
        normalized_gradient2 = sum_features(
            jnp.einsum("rk,dk->rd", grad_inner, w_in, preferred_element_type=jnp.float32)
        )
        backward_third, gain_gradient2 = norm_reverse_pass(
            normalized_gradient2,
            standardized_rows2,
            inverse_deviation2,
            gain_broadcast[2],
            hidden_width,
        )
        grad2 = grad3 + backward_third
        grad_mixed1, grad_out_time = branch_back(grad2, mixed1, out_time)
        grad_mixed_low = grad_mixed1.astype(jnp.bfloat16).reshape(shape_local)
        grad_queries, grad_keys, grad_values = time_backward(
            grad_mixed_low, time_q, time_k, time_v, time_visible, total1, scale
        )
        key_part, value_part = (
            lax.psum_scatter(
                grad_keys.reshape(clips_local, frames_all, patches, joined_local).astype(
                    jnp.bfloat16
                ),
                "tm",
                scatter_dimension=1,
                tiled=True,
            ).astype(jnp.float32),
            lax.psum_scatter(
                grad_values.reshape(clips_local, frames_all, patches, joined_local).astype(
                    jnp.bfloat16
                ),
                "tm",
                scatter_dimension=1,
                tiled=True,
            ).astype(jnp.float32),
        )
        grad_joined1 = jnp.stack(
            [
                grad_queries.reshape(row_count, joined_local),
                key_part.reshape(row_count, joined_local),
                value_part.reshape(row_count, joined_local),
            ]
        ).astype(jnp.bfloat16)
        grad_qkv_time, normalized_gradient1 = qkv_back(normalized_rows1, grad_joined1, qkv_time)
        backward_second, gain_gradient1 = norm_reverse_pass(
            normalized_gradient1,
            standardized_rows1,
            inverse_deviation1,
            gain_broadcast[1],
            hidden_width,
        )
        grad1 = grad2 + backward_second
        grad_mixed0, grad_out_space = branch_back(grad1, mixed0, out_space)
        grad_joined0 = space_backward(
            grad_mixed0.astype(jnp.bfloat16),
            joined0,
            total0,
            clips_local * frames_local,
            patches,
            heads_local,
            scale,
        )
        grad_qkv_space, normalized_gradient0 = qkv_back(normalized_rows0, grad_joined0, qkv_space)
        backward_first, gain_gradient0 = norm_reverse_pass(
            normalized_gradient0,
            standardized_rows0,
            inverse_deviation0,
            gain_broadcast[0],
            hidden_width,
        )
        grad0 = grad1 + backward_first
        input_grads.append(
            jnp.where(masked[:, None], 0.0, grad0).reshape(
                clips_local, frames_local, patches, cols_local
            )
        )
        grad_embed = jnp.sum(jnp.where(masked[:, None], grad0, 0.0), axis=0)
        gain_grads = jnp.stack([gain_gradient0, gain_gradient1, gain_gradient2])
        local_grads = (
            grad_qkv_space,
            grad_out_space,
            grad_qkv_time,
            grad_out_time,
            grad_w_in,
            grad_w_out,
        )
        small_grads = (gain_grads, grad_embed)
        reduced, reduced_small = reduce_grads(local_grads, small_grads)
        if weight_total is None:
            weight_total = reduced
            small_total = reduced_small
        else:
            weight_total = tuple((total + grad for total, grad in zip(weight_total, reduced)))
            small_total = tuple((total + grad for total, grad in zip(small_total, reduced_small)))
    return (
        jnp.concatenate(outputs, axis=0),
        jnp.concatenate(input_grads, axis=0),
        small_total[1],
        small_total[0],
        weight_total[0],
        weight_total[1],
        weight_total[2],
        weight_total[3],
        weight_total[4],
        weight_total[5],
    )


AXES = ("tm", "x", "c", "mp")
F32 = jnp.float32
BF16 = jnp.bfloat16
BLK = 256
MESH = pl.DeviceIdType.MESH


def device_pairs(move):
    pairs = []
    for y in range(2):
        for x in range(2):
            for c in range(2):
                for z in range(4):
                    there = move(y, x, c, z)
                    pairs.append(tuple(((q[0] * 2 + q[1]) * 2 + q[2]) * 4 + q[3] for q in ((y, x, c, z), there)))
    return pairs


def hop_y(v):
    return lax.ppermute(v, AXES, device_pairs(lambda y, x, c, z: (1 - y, x, c, z)))


def hop_x(v):
    return lax.ppermute(v, AXES, device_pairs(lambda y, x, c, z: (y, 1 - x, c, z)))


def hop_c(v):
    return lax.ppermute(v, AXES, device_pairs(lambda y, x, c, z: (y, x, 1 - c, z)))


def hop_z(v, shift):
    return lax.ppermute(v, AXES, device_pairs(lambda y, x, c, z: (y, x, c, (z + shift) % 4)))


def spread_pairs(r):
    def move(y, x, c, z):
        k = z ^ r
        return (y, x, k & 1, 2 * c + (k >> 1))

    return device_pairs(move)


def arrive_kernel(
    tok, vec, mine, later, rows_out, vec_out, wq, wo, wt,
    z_send, z_recv, y_send, y_recv, x_send, x_recv, p_send, p_recv, q_send, q_recv,
    t_send, t_recv, v_send, v_recv, u_send, u_recv, w_send, w_recv, local,
):
    y, x, c, z = (lax.axis_index(name) for name in AXES)
    half = wo.shape[1] // 4
    wide = 3 * half

    barrier = pltpu.get_barrier_semaphore()
    for dc in range(2):
        for dz in range(4):
            if dc or dz:
                peer = (y, x, (c + dc) % 2, (z + dz) % 4)
                pl.semaphore_signal(barrier, inc=1, device_id=peer, device_id_type=MESH)
    near_y, near_x = (1 - y, x, c, z), (y, 1 - x, c, z)
    for peer in (near_y, near_x):
        pl.semaphore_signal(barrier, inc=1, device_id=peer, device_id_type=MESH)
    pl.semaphore_wait(barrier, 9)

    def rows(dy, dx):
        return pl.ds(pl.multiple_of(BLK * (2 * ((y + dy) % 2) + (x + dx) % 2), BLK), BLK)

    def piece(dy, dx, r, split=False):
        s = (z + r) % 4
        at = pl.multiple_of(s * wide, half)
        out = wo.at[rows(dy, dx), pl.ds(pl.multiple_of(s * half, half), half)]
        if split:
            late = pl.multiple_of(s * wide + 2 * half, half)
            return (wq.at[rows(dy, dx), pl.ds(at, 2 * half)], wq.at[rows(dy, dx), pl.ds(late, half)], out)
        return (wq.at[rows(dy, dx), pl.ds(at, wide)], out)

    def copies(sources, targets, send, recv, peer):
        return [
            pltpu.make_async_remote_copy(
                src_ref=src, dst_ref=dst, send_sem=send.at[i], recv_sem=recv.at[i], device_id=peer, device_id_type=MESH
            )
            for i, (src, dst) in enumerate(zip(sources, targets))
        ]

    own_rows = rows(0, 0)
    own_slice = (mine.at[own_rows, pl.ds(0, wide)], mine.at[own_rows, pl.ds(wide, half)])

    def z_copies(right, step):
        if right:
            r = 0 if step == 0 else 4 - step
            peer, lands = (y, x, c, (z + 1) % 4), 3 - step
        else:
            r = step
            peer, lands = (y, x, c, (z + 3) % 4), step + 1
        target = piece(0, 0, r)
        source = own_slice if step == 0 else target
        return copies(source, target, z_send.at[int(right), step], z_recv.at[lands], peer)

    def y_copies(r):
        return copies(piece(0, 0, r), piece(0, 0, r), y_send.at[r], y_recv.at[r], near_y)

    def x_copies(r):
        return copies(piece(0, 0, r), piece(0, 0, r), x_send.at[r], x_recv.at[r], near_x)

    def corner_x(r):
        part = piece(1, 0, r, split=True)[:1]
        return copies(part, part, p_send.at[r], p_recv.at[r], near_x)

    def corner_y(r):
        part = piece(0, 1, r, split=True)[1:]
        return copies(part, part, q_send.at[r], q_recv.at[r], near_y)

    span = wt.shape[1] // 4

    def time_piece(dx, r):
        at = pl.ds(pl.multiple_of(((z + r) % 4) * span, span), span)
        return wt.at[pl.ds(pl.multiple_of(2 * BLK * ((x + dx) % 2), BLK), 2 * BLK), at]

    def time_z(right, step):
        if right:
            r = 0 if step == 0 else 4 - step
            peer, lands = (y, x, c, (z + 1) % 4), 3 - step
        else:
            r = step
            peer, lands = (y, x, c, (z + 3) % 4), step + 1
        source = later.at[pl.ds(pl.multiple_of(2 * BLK * x, BLK), 2 * BLK)] if step == 0 else time_piece(0, r)
        return [
            pltpu.make_async_remote_copy(
                src_ref=source, dst_ref=time_piece(0, r), send_sem=u_send.at[int(right), step], recv_sem=u_recv.at[lands],
                device_id=peer, device_id_type=MESH,
            )
        ]

    def time_x(dx, r):
        return [
            pltpu.make_async_remote_copy(
                src_ref=time_piece(dx, r), dst_ref=time_piece(dx, r), send_sem=w_send.at[r], recv_sem=w_recv.at[r],
                device_id=near_x, device_id_type=MESH,
            )
        ]

    def time_forward(j, left):
        r = 3 - j if left else j + 1
        pltpu.make_async_remote_copy(
            src_ref=time_piece(0, r), dst_ref=time_piece(0, r), send_sem=u_send.at[0, 0], recv_sem=u_recv.at[r],
            device_id=near_x, device_id_type=MESH,
        ).wait_recv()
        if j < 2:
            pl.when(z < 3 if left else z > 0)(lambda: start(time_z(left, j + 1)))
        start(time_x(0, r))

    def start(all_copies):
        for copy in all_copies:
            copy.start()

    def landed(all_copies):
        for copy in all_copies:
            copy.wait_recv()

    def sent(all_copies):
        for copy in all_copies:
            copy.wait_send()

    def token_copies(k):
        peer = (y, x, k % 2, 2 * c + k // 2)
        at = pl.ds(pl.multiple_of(z * BLK, BLK), BLK)
        return [
            pltpu.make_async_remote_copy(
                src_ref=src, dst_ref=dst, send_sem=send.at[k], recv_sem=recv.at[z], device_id=peer, device_id_type=MESH
            )
            for src, dst, send, recv in (
                (tok.at[k], rows_out.at[:, at], t_send, t_recv),
                (vec, vec_out.at[:, at], v_send, v_recv),
            )
        ]

    def token_local(k):
        at = pl.ds(pl.multiple_of(z * BLK, BLK), BLK)
        return [
            pltpu.make_async_copy(tok.at[k], rows_out.at[:, at], local.at[2]),
            pltpu.make_async_copy(vec, vec_out.at[:, at], local.at[3]),
        ]

    def stays(k):
        return jnp.logical_and(2 * c + k // 2 == z, c == k % 2)

    def from_right(j):
        return z <= 2 - j

    def from_left(j):
        return z >= j + 1

    pl.when(z < 3)(lambda: start(z_copies(True, 0)))
    pl.when(z > 0)(lambda: start(z_copies(False, 0)))
    keep = [
        pltpu.make_async_copy(mine.at[:, pl.ds(0, wide)], wq.at[:, pl.ds(pl.multiple_of(z * wide, half), wide)], local.at[0]),
        pltpu.make_async_copy(mine.at[:, pl.ds(wide, half)], wo.at[:, pl.ds(pl.multiple_of(z * half, half), half)], local.at[1]),
        pltpu.make_async_copy(later, wt.at[:, pl.ds(pl.multiple_of(z * span, span), span)], local.at[4]),
    ]
    start(keep)

    def forward(j, left):
        r = 3 - j if left else j + 1
        landed(copies(piece(0, 0, r), piece(0, 0, r), z_send.at[0, 0], z_recv.at[r], near_y))
        if j < 2:
            pl.when(z < 3 if left else z > 0)(lambda: start(z_copies(left, j + 1)))
        start(y_copies(r))
        start(x_copies(r))

    def corners(j, left):
        r = 3 - j if left else j + 1
        landed(copies(piece(1, 0, r), piece(1, 0, r), y_send.at[r], y_recv.at[r], near_y))
        start(corner_x(r))
        landed(copies(piece(0, 1, r), piece(0, 1, r), x_send.at[r], x_recv.at[r], near_x))
        start(corner_y(r))

    for j in range(3):
        for left in (True, False):
            pl.when(from_left(j) if left else from_right(j))(lambda j=j, left=left: forward(j, left))
        if j == 0:
            for k in range(4):
                pl.when(stays(k))(lambda k=k: start(token_local(k)))
                pl.when(jnp.logical_not(stays(k)))(lambda k=k: start(token_copies(k)))
            pl.when(z < 3)(lambda: start(time_z(True, 0)))
            pl.when(z > 0)(lambda: start(time_z(False, 0)))
        else:
            for left in (True, False):
                pl.when(from_left(j - 1) if left else from_right(j - 1))(lambda j=j, left=left: corners(j - 1, left))
    for left in (True, False):
        pl.when(from_left(2) if left else from_right(2))(lambda left=left: corners(2, left))
    for j in range(3):
        for left in (True, False):
            pl.when(from_left(j) if left else from_right(j))(lambda j=j, left=left: time_forward(j, left))

    for copy in keep:
        copy.wait()
    for r in (1, 2, 3):
        part = piece(1, 1, r, split=True)
        landed(copies(part[:1], part[:1], p_send.at[r], p_recv.at[r], near_x))
        landed(copies(part[1:], part[1:], q_send.at[r], q_recv.at[r], near_y))
        for group in (y_copies(r), x_copies(r), corner_x(r), corner_y(r), time_x(0, r)):
            sent(group)
        landed(time_x(1, r))
    for step in range(3):
        pl.when(jnp.logical_and(z >= step, z < 3))(lambda step=step: sent(z_copies(True, step) + time_z(True, step)))
        pl.when(jnp.logical_and(z + step <= 3, z > 0))(lambda step=step: sent(z_copies(False, step) + time_z(False, step)))
    for k in range(4):
        def finish_local(k=k):
            for copy in token_local(k):
                copy.wait()

        pl.when(stays(k))(finish_local)
        pl.when(jnp.logical_not(stays(k)))(lambda k=k: sent(token_copies(k)))
    for s in range(4):
        at = pl.ds(s * BLK, BLK)
        away = jnp.logical_not(jnp.logical_and(z == s, z // 2 == c))

        def arrived(s=s, at=at):
            for src, dst, send, recv in (
                (tok.at[0], rows_out.at[:, at], t_send, t_recv),
                (vec, vec_out.at[:, at], v_send, v_recv),
            ):
                pltpu.make_async_remote_copy(
                    src_ref=src, dst_ref=dst, send_sem=send.at[0], recv_sem=recv.at[s], device_id=near_y, device_id_type=MESH
                ).wait_recv()

        pl.when(away)(arrived)


def arrive(tok, vec, mine, later):
    own, width, half = tok.shape[1], 4 * tok.shape[2], mine.shape[1] // 4
    dma = pltpu.SemaphoreType.DMA
    anywhere = pl.BlockSpec(memory_space=pl.ANY)
    return pl.pallas_call(
        arrive_kernel,
        in_specs=[anywhere] * 4,
        out_specs=[anywhere] * 5,
        out_shape=[
            jax.ShapeDtypeStruct((own, width), BF16),
            jax.ShapeDtypeStruct((vec.shape[0], width), BF16),
            jax.ShapeDtypeStruct((width, 12 * half), BF16),
            jax.ShapeDtypeStruct((width, 4 * half), BF16),
            jax.ShapeDtypeStruct((width, 4 * later.shape[1]), BF16),
        ],
        scratch_shapes=[
            dma((2, 3, 2)), dma((4, 2)), dma((4, 2)), dma((4, 2)), dma((4, 2)), dma((4, 2)),
            dma((4, 1)), dma((4, 1)), dma((4, 2)), dma((4, 2)),
            dma((4,)), dma((4,)), dma((4,)), dma((4,)),
            dma((2, 3)), dma((4,)), dma((4,)), dma((4,)), dma((5,)),
        ],
        compiler_params=pltpu.CompilerParams(collective_id=0, has_side_effects=True),
        name="arrive",
    )(tok, vec, mine, later)


def dot_nn(a, b):
    return lax.dot_general(a, b, (((1,), (0,)), ((), ())), preferred_element_type=F32)


def dot_nt(a, b):
    return lax.dot_general(a, b, (((1,), (1,)), ((), ())), preferred_element_type=F32)


def dot_tn(a, b):
    return lax.dot_general(a, b, (((0,), (0,)), ((), ())), preferred_element_type=F32)


def attend_pair(q, k, v, bias, scale):
    mixed, totals = [], []
    for i in range(2):
        mine = slice(i * HEAD_DIM, (i + 1) * HEAD_DIM)
        scores = dot_nt(k[:, mine], q[:, mine]) * scale
        if bias is not None:
            scores = scores + bias
        highest = jnp.max(scores, axis=0, keepdims=True)
        exponent = jnp.exp(scores - highest)
        total = jnp.sum(exponent, axis=0, keepdims=True)
        totals.append(highest + jnp.log(total))
        mixed.append(dot_tn(v[:, mine], exponent.astype(BF16)) * (1.0 / total))
    return (jnp.concatenate(mixed, axis=0).T, totals)


def attend_pair_back(q, k, v, g, totals, bias, scale):
    grads = ([], [], [])
    for i in range(2):
        mine = slice(i * HEAD_DIM, (i + 1) * HEAD_DIM)
        scores = dot_nt(k[:, mine], q[:, mine]) * scale
        if bias is not None:
            scores = scores + bias
        p = jnp.exp(scores - totals[i])
        dp = dot_nt(v[:, mine], g[:, mine])
        ds = (p * (dp - jnp.sum(p * dp, axis=0, keepdims=True))).astype(BF16)
        grads[0].append(dot_tn(k[:, mine], ds) * scale)
        grads[1].append(dot_nn(ds, q[:, mine]) * scale)
        grads[2].append(dot_nn(p.astype(BF16), g[:, mine]))
    return (
        jnp.concatenate(grads[0], axis=0).T,
        jnp.concatenate(grads[1], axis=1),
        jnp.concatenate(grads[2], axis=1),
    )


PAIR = 2 * HEAD_DIM


def space_attend_kernel(scale, qkv_ref, out_ref, total_ref):
    for i in range(out_ref.shape[1] // PAIR):
        q, k, v = (qkv_ref[:, (3 * i + part) * PAIR : (3 * i + part + 1) * PAIR] for part in range(3))
        mixed, totals = attend_pair(q, k, v, None, scale)
        out_ref[:, i * PAIR : (i + 1) * PAIR] = mixed.astype(BF16)
        for h in range(2):
            total_ref[0, 2 * i + h : 2 * i + h + 1, :] = totals[h]


def space_attend_back_kernel(scale, qkv_ref, grad_ref, total_ref, out_ref):
    for i in range(grad_ref.shape[1] // PAIR):
        q, k, v = (qkv_ref[:, (3 * i + part) * PAIR : (3 * i + part + 1) * PAIR] for part in range(3))
        totals = [total_ref[0, 2 * i + h : 2 * i + h + 1, :] for h in range(2)]
        grads = attend_pair_back(q, k, v, grad_ref[:, i * PAIR : (i + 1) * PAIR], totals, None, scale)
        for part in range(3):
            out_ref[:, (3 * i + part) * PAIR : (3 * i + part + 1) * PAIR] = grads[part].astype(BF16)


def attention_cost(groups, rows, heads, products):
    return pl.CostEstimate(
        flops=8 * products * groups * heads * rows * rows * HEAD_DIM,
        transcendentals=groups * heads * rows * rows,
        bytes_accessed=2 * groups * rows * heads * HEAD_DIM * 2 * products,
    )


def space_attend(qkv, frames, patches, heads, scale):
    width = heads * HEAD_DIM
    return pl.pallas_call(
        functools.partial(space_attend_kernel, scale),
        grid=(frames,),
        in_specs=[pl.BlockSpec((patches, 3 * width), lambda i: (i, 0))],
        out_specs=[
            pl.BlockSpec((patches, width), lambda i: (i, 0)),
            pl.BlockSpec((1, heads, patches), lambda i: (i, 0, 0)),
        ],
        out_shape=[
            jax.ShapeDtypeStruct((frames * patches, width), BF16),
            jax.ShapeDtypeStruct((frames, heads, patches), F32),
        ],
        cost_estimate=attention_cost(frames, patches, heads, 2),
        name="space_attend",
    )(qkv)


def space_attend_back(qkv, grad, total, frames, patches, heads, scale):
    width = heads * HEAD_DIM
    return pl.pallas_call(
        functools.partial(space_attend_back_kernel, scale),
        grid=(frames,),
        in_specs=[
            pl.BlockSpec((patches, 3 * width), lambda i: (i, 0)),
            pl.BlockSpec((patches, width), lambda i: (i, 0)),
            pl.BlockSpec((1, heads, patches), lambda i: (i, 0, 0)),
        ],
        out_specs=pl.BlockSpec((patches, 3 * width), lambda i: (i, 0)),
        out_shape=jax.ShapeDtypeStruct((frames * patches, 3 * width), BF16),
        cost_estimate=attention_cost(frames, patches, heads, 5),
        name="space_attend_back",
    )(qkv, grad, total)


GROUP = 8
CHUNK = 32


def time_kernel(back, scale, heads, *refs):
    if back:
        (own_ref, rider_ref, joined_ref, total_ref, wq_ref, wo_ref, bias_ref, all_ref, out_ref, delta_ref, rider_out) = refs[:11]
        refs = refs[11:]
    else:
        (own_ref, rider_ref, wq_ref, wo_ref, bias_ref, all_ref, out_ref, mixed_ref, total_ref, delta_ref, rider_out) = refs[:11]
        refs = refs[11:]
    (
        held, wide, narrow, kept, core_out, core_in, near_out, near_in,
        gy_send, gy_recv, gc_send, gc_recv, gd_send, gd_recv, sc_send, sc_recv, sy_send, sy_recv,
        r_send, r_recv, r_local, out_sem,
    ) = refs
    y, x, c, z = (lax.axis_index(name) for name in AXES)
    near, pair = (1 - y, x, c, z), (y, x, 1 - c, z)
    frames = held.shape[0] // 4
    chunks = held.shape[1] // CHUNK
    width = heads * HEAD_DIM
    groups = CHUNK // GROUP

    barrier = pltpu.get_barrier_semaphore()
    for dc in range(2):
        for dz in range(4):
            if dc or dz:
                pl.semaphore_signal(barrier, inc=1, device_id=(y, x, (c + dc) % 2, (z + dz) % 4), device_id_type=MESH)
    pl.semaphore_signal(barrier, inc=1, device_id=near, device_id_type=MESH)
    pl.semaphore_wait(barrier, 8)

    def remote(src, dst, send, recv, peer):
        return pltpu.make_async_remote_copy(
            src_ref=src, dst_ref=dst, send_sem=send, recv_sem=recv, device_id=peer, device_id_type=MESH
        )

    def patches(k):
        return pl.ds(pl.multiple_of(k * CHUNK, CHUNK), CHUNK)

    def block(b, k):
        return held.at[pl.ds(b * frames, frames), patches(k)]

    def gather_y(k):
        return remote(own_ref.at[:, patches(k)], block(1, k), gy_send.at[k], gy_recv.at[k], near)

    def gather_c(k):
        return remote(own_ref.at[:, patches(k)], block(2, k), gc_send.at[k], gc_recv.at[k], pair)

    def gather_d(k):
        return remote(block(1, k), block(3, k), gd_send.at[k], gd_recv.at[k], pair)

    def scatter_c(k):
        return remote(core_out.at[k], core_in.at[k], sc_send.at[k], sc_recv.at[k], pair)

    def scatter_y(k):
        return remote(near_out.at[k], near_in.at[k], sy_send.at[k], sy_recv.at[k], near)

    def save(k):
        return pltpu.make_async_copy(held.at[:, patches(k)], all_ref.at[:, patches(k)], out_sem.at[k])

    def columns(s):
        return pl.ds(pl.multiple_of(s * BLK, BLK), BLK)

    def stays(k):
        if back:
            return jnp.logical_and(z == k, z // 2 == c)
        return jnp.logical_and(2 * c + k // 2 == z, c == k % 2)

    def ride(k):
        if back:
            src, dst = rider_ref.at[:, columns(k)], rider_out.at[2 * (z % 2) + c]
            peer, slot = (y, x, z // 2, k), 2 * (z % 2) + c
        else:
            src, dst = rider_ref.at[k], rider_out.at[:, columns(z)]
            peer, slot = (y, x, k % 2, 2 * c + k // 2), z
        return src, dst, peer, slot

    def ride_remote(k):
        src, dst, peer, slot = ride(k)
        return remote(src, dst, r_send.at[k], r_recv.at[slot], peer)

    def ride_local(k):
        src, dst, _, _ = ride(k)
        return pltpu.make_async_copy(src, dst, r_local.at[0])

    def ride_landed(k):
        if back:
            src, dst = rider_ref.at[:, columns(k)], rider_out.at[k]
        else:
            src, dst = rider_ref.at[k], rider_out.at[:, columns(k)]
        return remote(src, dst, r_send.at[k], r_recv.at[k], near)

    def from_self(k):
        if back:
            return jnp.logical_and(2 * c + k // 2 == z, c == k % 2)
        return jnp.logical_and(z == k, z // 2 == c)

    for k in range(chunks):
        gather_y(k).start()
        gather_c(k).start()
    for k in range(4):
        pl.when(stays(k))(lambda k=k: ride_local(k).start())
        pl.when(jnp.logical_not(stays(k)))(lambda k=k: ride_remote(k).start())
    held[:frames] = own_ref[...]

    def finish(k):
        scatter_c(k).wait_recv()
        both = kept[:, patches(k)] + core_in[k].astype(F32)
        near_out[k] = both[frames:].astype(BF16)
        delta_ref[:, patches(k)] = both[:frames]
        scatter_y(k).start()

    def pass_on(k):
        gather_y(k).wait_recv()
        gather_d(k).start()

    def one_group(i, rows):
        at = pl.ds(pl.multiple_of(i * GROUP, GROUP), GROUP)
        count = 4 * frames * GROUP
        bias = bias_ref[...]
        for lo in range(0, width, PAIR):
            q, k, v = (
                wide[:, at, part * width + lo : part * width + lo + PAIR].reshape(count, PAIR).astype(BF16)
                for part in range(3)
            )
            h = lo // HEAD_DIM
            if back:
                g = narrow[:, at, lo : lo + PAIR].reshape(count, PAIR).astype(BF16)
                totals = [total_ref[rows * groups + i, h + j : h + j + 1, :] for j in range(2)]
                grads = attend_pair_back(q, k, v, g, totals, bias, scale)
                for part in range(3):
                    wide[:, at, part * width + lo : part * width + lo + PAIR] = grads[part].reshape(
                        4 * frames, GROUP, PAIR
                    )
            else:
                mixed, totals = attend_pair(q, k, v, bias, scale)
                narrow[:, at, lo : lo + PAIR] = mixed.reshape(4 * frames, GROUP, PAIR)
                for j in range(2):
                    total_ref[rows * groups + i, h + j : h + j + 1, :] = totals[j]

    def one_chunk(k, carry):
        pl.when(k + 1 < chunks)(lambda: pass_on(k + 1))
        gather_c(k).wait_recv()
        gather_d(k).wait_recv()
        count = 4 * frames * CHUNK
        lhs = held[:, patches(k)].reshape(count, held.shape[2])
        if back:
            wide[...] = joined_ref[:, patches(k)].astype(F32)
            narrow[...] = dot_nn(lhs, wo_ref[...]).astype(BF16).astype(F32).reshape(narrow.shape)
        else:
            joined = dot_nn(lhs, wq_ref[...]).astype(BF16)
            out_ref[:, patches(k)] = joined.reshape(wide.shape)
            wide[...] = joined.astype(F32).reshape(wide.shape)
        save(k).start()
        lax.fori_loop(0, groups, lambda i, carry: (one_group(i, k), carry)[1], 0)
        if back:
            grads = wide[...].astype(BF16)
            out_ref[:, patches(k)] = grads
            partial = dot_nt(grads.reshape(count, 3 * width), wq_ref[...])
        else:
            mixed = narrow[...].astype(BF16)
            mixed_ref[:, patches(k)] = mixed
            partial = dot_nt(mixed.reshape(count, width), wo_ref[...])
        partial = partial.reshape(4 * frames, CHUNK, held.shape[2])
        kept[:, patches(k)] = partial[: 2 * frames]
        core_out[k] = partial[2 * frames :].astype(BF16)
        scatter_c(k).start()
        pl.when(k > 0)(lambda: finish(k - 1))
        return carry

    pass_on(0)
    lax.fori_loop(0, chunks, one_chunk, 0)
    finish(chunks - 1)
    for k in range(chunks):
        scatter_y(k).wait_recv()
        delta_ref[:, patches(k)] = delta_ref[:, patches(k)] + near_in[k].astype(F32)
    for k in range(chunks):
        for copy in (gather_y(k), gather_c(k), gather_d(k), scatter_c(k), scatter_y(k)):
            copy.wait_send()
        save(k).wait()
    for k in range(4):
        pl.when(stays(k))(lambda k=k: ride_local(k).wait())
        pl.when(jnp.logical_not(stays(k)))(lambda k=k: ride_remote(k).wait_send())
        pl.when(jnp.logical_not(from_self(k)))(lambda k=k: ride_landed(k).wait_recv())


def time_call(back, own, rider, saved, wq, wo, bias, scale):
    frames, patches, features = own.shape
    width = wo.shape[1]
    heads = width // HEAD_DIM
    chunks = patches // CHUNK
    rows = 4 * frames * GROUP
    dma = pltpu.SemaphoreType.DMA
    anywhere = pl.BlockSpec(memory_space=pl.ANY)
    whole = pl.BlockSpec(memory_space=pltpu.VMEM)
    out_shape = [
        jax.ShapeDtypeStruct((4 * frames, patches, features), BF16),
        jax.ShapeDtypeStruct((4 * frames, patches, 3 * width), BF16),
    ]
    if not back:
        out_shape += [
            jax.ShapeDtypeStruct((4 * frames, patches, width), BF16),
            jax.ShapeDtypeStruct((patches // GROUP, heads, rows), F32),
        ]
    rider_shape = (4, frames * patches, BLK) if back else (frames * patches, features)
    out_shape += [
        jax.ShapeDtypeStruct((frames, patches, features), F32),
        jax.ShapeDtypeStruct(rider_shape, BF16),
    ]
    return pl.pallas_call(
        functools.partial(time_kernel, back, scale, heads),
        in_specs=[whole, anywhere] + [whole] * (len(saved) + 3),
        out_specs=[anywhere] + [whole] * (len(out_shape) - 2) + [anywhere],
        out_shape=out_shape,
        scratch_shapes=[
            pltpu.VMEM((4 * frames, patches, features), BF16),
            pltpu.VMEM((4 * frames, CHUNK, 3 * width), F32),
            pltpu.VMEM((4 * frames, CHUNK, width), F32),
            pltpu.VMEM((2 * frames, patches, features), F32),
            pltpu.VMEM((chunks, 2 * frames, CHUNK, features), BF16),
            pltpu.VMEM((chunks, 2 * frames, CHUNK, features), BF16),
            pltpu.VMEM((chunks, frames, CHUNK, features), BF16),
            pltpu.VMEM((chunks, frames, CHUNK, features), BF16),
        ]
        + [dma((chunks,))] * 10
        + [dma((4,)), dma((4,)), dma((1,)), dma((chunks,))],
        compiler_params=pltpu.CompilerParams(
            collective_id=2 if back else 1, has_side_effects=True, vmem_limit_bytes=48 * 1024 * 1024
        ),
        cost_estimate=pl.CostEstimate(flops=10**10, transcendentals=10**6, bytes_accessed=10**8),
        name="time_back" if back else "time_forward",
    )(own, rider, *saved, wq, wo, bias)


def settle_kernel(
    dj, go, lhs, weight_hbm, std_hbm, base_hbm, inverse, masked, gain, small_in,
    kept_out, landed_out, rows_out, small_out,
    weight, std, base, grads, a1_out, a1_in, b1_out, b1_in, a2_out, a2_in, b2_out, b2_in, z_out, z_in,
    half_out, half_in, ready, core_out, core_in, sums, sum_out, sum_in, share_in,
    a1_send, a1_recv, b1_send, b1_recv, a2_send, a2_recv, b2_send, b2_recv, z_send, z_recv,
    h_send, h_recv, r_send, r_recv, c_send, c_recv, s_send, s_recv, p_send, p_recv, local,
):
    y, x, c, z = (lax.axis_index(name) for name in AXES)
    near_y, near_x, pair = (1 - y, x, c, z), (y, 1 - x, c, z), (y, x, 1 - c, z)
    own = std.shape[0]
    third = go.shape[1] // 4
    wide = 3 * third
    two = 2 * third

    fetches = [
        pltpu.make_async_copy(weight_hbm, weight, local.at[0]),
        pltpu.make_async_copy(std_hbm, std, local.at[1]),
        pltpu.make_async_copy(base_hbm, base, local.at[2]),
    ]
    for copy in fetches:
        copy.start()

    barrier = pltpu.get_barrier_semaphore()
    for dc in range(2):
        for dz in range(4):
            if dc or dz:
                pl.semaphore_signal(barrier, inc=1, device_id=(y, x, (c + dc) % 2, (z + dz) % 4), device_id_type=MESH)
    for peer in (near_y, near_x):
        pl.semaphore_signal(barrier, inc=1, device_id=peer, device_id_type=MESH)
    pl.semaphore_wait(barrier, 9)

    def remote(src, dst, send, recv, peer):
        return pltpu.make_async_remote_copy(
            src_ref=src, dst_ref=dst, send_sem=send, recv_sem=recv, device_id=peer, device_id_type=MESH
        )

    def block(yb, xb):
        return pl.ds(pl.multiple_of(BLK * (2 * yb + xb), BLK), BLK)

    def a1(i):
        return remote(a1_out.at[i], a1_in.at[i], a1_send.at[i], a1_recv.at[i], near_x)

    def b1(i):
        return remote(b1_out.at[i], b1_in.at[i], b1_send.at[i], b1_recv.at[i], near_y)

    def a2(i):
        return remote(a2_out.at[i], a2_in.at[i], a2_send.at[i], a2_recv.at[i], near_y)

    def b2(i):
        return remote(b2_out.at[i], b2_in.at[i], b2_send.at[i], b2_recv.at[i], near_x)

    def to_z(r):
        return remote(z_out.at[r], z_in.at[r], z_send.at[r], z_recv.at[r], (y, x, c, (z + r) % 4))

    def piece(i, carry):
        s = (z + i + 1) % 4
        made = dot_nn(lhs[...], dj[:, pl.ds(pl.multiple_of(s * wide, third), wide)])
        grads[i, :, :wide] = made
        grads[i, :, wide:] = go[:, pl.ds(pl.multiple_of(s * third, third), third)].astype(F32)
        for b in range(2):
            a1_out[i, b] = grads[i, block(b, 1 - x), :two].astype(BF16)
            b1_out[i, b] = grads[i, block(1 - y, b), two:].astype(BF16)
        a1(i).start()
        b1(i).start()
        return carry

    lax.fori_loop(0, 4, piece, 0)

    def second(i):
        a1(i).wait_recv()
        a2_out[i] = (grads[i, block(1 - y, x), :two] + a1_in[i, 1 - y].astype(F32)).astype(BF16)
        a2(i).start()
        b1(i).wait_recv()
        b2_out[i] = (grads[i, block(y, 1 - x), two:] + b1_in[i, 1 - x].astype(F32)).astype(BF16)
        b2(i).start()
        grads[i, block(y, x), :two] = grads[i, block(y, x), :two] + a1_in[i, y].astype(F32)
        grads[i, block(y, x), two:] = grads[i, block(y, x), two:] + b1_in[i, x].astype(F32)

    def third_step(i):
        a2(i).wait_recv()
        b2(i).wait_recv()
        grads[i, block(y, x), :two] = grads[i, block(y, x), :two] + a2_in[i].astype(F32)
        grads[i, block(y, x), two:] = grads[i, block(y, x), two:] + b2_in[i].astype(F32)
        if i < 3:
            z_out[i + 1] = grads[i, block(y, x), :].astype(BF16)
            to_z(i + 1).start()

    step = own // 2
    fetches[0].wait()

    def away(i, carry):
        rows = pl.ds(pl.multiple_of(own + i * step, step), step)
        half_out[pl.ds(pl.multiple_of(i * step, step), step)] = dot_nt(dj[rows], weight[...]).astype(BF16)
        return carry

    lax.fori_loop(0, 2, away, 0)
    swap = remote(half_out, half_in, h_send.at[0], h_recv.at[0], pair)
    swap.start()
    second(0)
    for copy in fetches[1:]:
        copy.wait()
    sums[...] = small_in[...]
    swap.wait_recv()

    def home(i, totals):
        rows = pl.ds(pl.multiple_of(i * step, step), step)
        grad = dot_nt(dj[rows], weight[...]) + half_in[rows].astype(F32)
        standard = std[rows]
        inner = grad * gain[...]
        mean = jnp.mean(inner, axis=-1, keepdims=True)
        along = jnp.mean(inner * standard, axis=-1, keepdims=True)
        full = base[rows] + (inner - mean - standard * along) * inverse[rows]
        hide = masked[rows] > 0.0
        ready[rows] = jnp.where(hide, 0.0, full).astype(BF16)
        return (
            totals[0] + jnp.sum(grad * standard, axis=0, keepdims=True),
            totals[1] + jnp.sum(jnp.where(hide, full, 0.0), axis=0, keepdims=True),
        )

    zero = jnp.zeros((1, std.shape[1]), F32)
    gain_grad, embed_grad = lax.fori_loop(0, 2, home, (zero, zero))
    sums[0:1] = gain_grad
    sums[3:4] = embed_grad

    def columns(s):
        return pl.ds(pl.multiple_of(s * BLK, BLK), BLK)

    def stays(k):
        return jnp.logical_and(z == k, z // 2 == c)

    def ride(k):
        slot = 2 * (z % 2) + c
        return remote(ready.at[:, columns(k)], rows_out.at[slot], r_send.at[k], r_recv.at[slot], (y, x, z // 2, k))

    def ride_local(k):
        return pltpu.make_async_copy(ready.at[:, columns(k)], rows_out.at[2 * (z % 2) + c], local.at[3])

    for k in range(4):
        pl.when(stays(k))(lambda k=k: ride_local(k).start())
        pl.when(jnp.logical_not(stays(k)))(lambda k=k: ride(k).start())

    def share(h):
        peer = (pair, near_y, near_x)[h]
        return remote(sum_out.at[h], sum_in.at[h], s_send.at[h], s_recv.at[h], peer)

    def begin_share(h):
        sum_out[h] = sums[...]
        share(h).start()

    def end_share(h):
        share(h).wait_recv()
        sums[...] = sums[...] + sum_in[h]

    begin_share(0)
    second(1)
    third_step(0)
    end_share(0)
    begin_share(1)
    second(2)
    third_step(1)
    end_share(1)
    begin_share(2)
    second(3)
    third_step(2)
    end_share(2)
    sum_out[3] = sums[...]

    def deal(r):
        s = (z + r) % 4
        return remote(sum_out.at[3, :, columns(s)], share_in.at[r], p_send.at[r], p_recv.at[r], (y, x, c, s))

    for r in (1, 2, 3):
        deal(r).start()
    third_step(3)
    for r in (1, 2, 3):
        to_z(r).wait_recv()
    total = grads[3, block(y, x), :]
    for r in (1, 2, 3):
        total = total + z_in[r].astype(F32)
    grads[3, block(y, x), :] = total
    rows = BLK // 2

    def core_rows(core):
        return pl.ds(pl.multiple_of(BLK * (2 * y + x) + rows * core, rows), rows)

    core_out[...] = grads[3, core_rows(1 - c), :].astype(BF16)
    last = remote(core_out, core_in, c_send.at[0], c_recv.at[0], pair)
    last.start()
    kept_out[...] = grads[3, core_rows(c), :]
    result = sums[:, columns(z)]
    for r in (1, 2, 3):
        deal(r).wait_recv()
        result = result + share_in[r]
    small_out[...] = result
    last.wait_recv()
    landed_out[...] = core_in[...].astype(F32)

    last.wait_send()
    swap.wait_send()
    for i in range(4):
        for copy in (a1(i), b1(i), a2(i), b2(i)):
            copy.wait_send()
    for r in (1, 2, 3):
        to_z(r).wait_send()
        deal(r).wait_send()
    for h in range(3):
        share(h).wait_send()
    for k in range(4):
        pl.when(stays(k))(lambda k=k: ride_local(k).wait())
        pl.when(jnp.logical_not(stays(k)))(lambda k=k: ride(k).wait_send())
        from_self = jnp.logical_and(2 * c + k // 2 == z, c == k % 2)

        def landed(k=k):
            remote(ready.at[:, columns(k)], rows_out.at[k], r_send.at[k], r_recv.at[k], near_y).wait_recv()

        pl.when(jnp.logical_not(from_self))(landed)


def settle(dj, go, lhs, weight, std, base, inverse, masked, gain, small):
    own, features = std.shape
    cols4 = go.shape[1]
    quarter = cols4 // 4
    dma = pltpu.SemaphoreType.DMA
    anywhere = pl.BlockSpec(memory_space=pl.ANY)
    whole = pl.BlockSpec(memory_space=pltpu.VMEM)

    def low(*shape):
        return pltpu.VMEM(shape, BF16)

    def high(*shape):
        return pltpu.VMEM(shape, F32)

    return pl.pallas_call(
        settle_kernel,
        in_specs=[whole] * 3 + [anywhere] * 3 + [whole] * 4,
        out_specs=[whole, whole, anywhere, whole],
        out_shape=[
            jax.ShapeDtypeStruct((BLK // 2, cols4), F32),
            jax.ShapeDtypeStruct((BLK // 2, cols4), F32),
            jax.ShapeDtypeStruct((4, own, BLK), BF16),
            jax.ShapeDtypeStruct((8, BLK), F32),
        ],
        scratch_shapes=[
            low(*weight.shape), high(own, features), high(own, features), high(4, features, cols4),
            low(4, 2, BLK, 2 * quarter), low(4, 2, BLK, 2 * quarter), low(4, 2, BLK, 2 * quarter), low(4, 2, BLK, 2 * quarter),
            low(4, BLK, 2 * quarter), low(4, BLK, 2 * quarter), low(4, BLK, 2 * quarter), low(4, BLK, 2 * quarter),
            low(4, BLK, cols4), low(4, BLK, cols4),
            low(own, features), low(own, features), low(own, features),
            low(BLK // 2, cols4), low(BLK // 2, cols4),
            high(8, features), high(4, 8, features), high(3, 8, features), high(4, 8, BLK),
        ]
        + [dma((4,))] * 10
        + [dma((1,)), dma((1,)), dma((4,)), dma((4,)), dma((1,)), dma((1,)), dma((3,)), dma((3,)), dma((4,)), dma((4,)), dma((4,))],
        compiler_params=pltpu.CompilerParams(
            collective_id=3, has_side_effects=True, vmem_limit_bytes=56 * 1024 * 1024
        ),
        cost_estimate=pl.CostEstimate(flops=10**10, transcendentals=10**6, bytes_accessed=10**8),
        name="settle",
    )(dj, go, lhs, weight, std, base, inverse, masked, gain, small)


def tie(*values):
    return lax.optimization_barrier(values)


def norm_rows(resid):
    mean = jnp.mean(resid, axis=-1, keepdims=True)
    centered = resid - mean
    inverse = lax.rsqrt(jnp.mean(centered * centered, axis=-1, keepdims=True) + eps_norm)
    return (centered * inverse, inverse)


def norm_rows_back(grad, standardized, inverse, gain):
    gain_grad = jnp.sum(grad * standardized, axis=0)
    inner = grad * gain
    mean = jnp.mean(inner, axis=-1, keepdims=True)
    along = jnp.mean(inner * standardized, axis=-1, keepdims=True)
    return ((inner - mean - standardized * along) * inverse, gain_grad)


def cols(parts):
    return jnp.concatenate(parts, axis=1)


def rows_of(parts):
    return jnp.concatenate(parts, axis=0)


def token_parallel(
    tokens,
    cotangent,
    ratio,
    priority,
    frame_order,
    mask_embed,
    gains,
    qkv_space,
    out_space,
    qkv_time,
    out_time,
    w_in,
    w_out,
):
    scale = 1.0 / math.sqrt(HEAD_DIM)
    y, x, c, z = (lax.axis_index(name) for name in AXES)
    patches = tokens.shape[2]
    width = qkv_space.shape[0]
    frames_own = tokens.shape[0] * tokens.shape[1] // 4
    frames_all = frame_order.shape[1]
    own = frames_own * patches
    hidden_own = w_in.shape[1] // 2
    plane = 2 * y + x
    k_own = 2 * (z % 2) + c

    masked_here = (priority < ratio[:, None, None]).astype(jnp.int32).reshape(2, -1)
    info = cols([masked_here, frame_order])
    info = jnp.where(z // 2 == c, info, hop_c(info))
    info = lax.dynamic_index_in_dim(info, z % 2, 0, keepdims=False)
    masked = lax.dynamic_slice_in_dim(info, c * own, own, 0)[:, None] != 0
    order = info[2 * own :].reshape(2, 2, frames_own)
    order = jnp.where(y == 1, order[::-1], order)
    order = jnp.where(c == 1, order[:, ::-1], order).swapaxes(0, 1).reshape(frames_all)
    order = jnp.repeat(order, GROUP)
    patch = jnp.arange(frames_all * GROUP) % GROUP
    visible = (order[:, None] <= order[None, :]) & (patch[:, None] == patch[None, :])
    bias = jnp.where(visible, 0.0, -1e30).astype(F32)

    half = qkv_space.shape[2] // 2
    sp_own = cols(
        [
            lax.dynamic_slice_in_dim(qkv_space, c * half, half, 2).reshape(width, -1),
            lax.dynamic_slice_in_dim(out_space, c * half, half, 0).T,
        ]
    )
    vectors = rows_of([mask_embed[None], gains, jnp.zeros((4, BLK), BF16)])
    head = (2 * y + c) * HEAD_DIM
    ti_own = cols(
        [
            lax.dynamic_slice_in_dim(qkv_time, head, HEAD_DIM, 2).reshape(width, -1),
            lax.dynamic_slice_in_dim(out_time, head, HEAD_DIM, 0).T,
        ]
    )
    arrived, vectors, ws_qkv, ws_out, wt_all = arrive(tokens.reshape(4, own, BLK), vectors, sp_own, ti_own)
    wt_all = wt_all.reshape(width, 4, 4, HEAD_DIM)
    wt_qkv = jnp.swapaxes(wt_all[:, :, :3], 1, 2).reshape(width, 12 * HEAD_DIM)
    wt_out = wt_all[:, :, 3].reshape(width, 4 * HEAD_DIM)
    source = arrived.astype(F32)
    embed_row = vectors[:1].astype(F32)
    gain = [vectors[1 + i : 2 + i].astype(F32) for i in range(3)]

    ff_in = lax.dynamic_slice(w_in, (plane * BLK, c * hidden_own), (BLK, hidden_own))
    ff_out = lax.dynamic_slice(w_out, (c * hidden_own, plane * BLK), (hidden_own, BLK)).T
    arrived, ff_in, ff_out = tie(arrived, ff_in, ff_out)

    def gather_ff(w):
        w = lax.all_gather(w, ("mp", "tm", "x")).reshape(4, width, hidden_own)
        return [w[s] for s in range(4)]

    def pair_gather(v):
        return rows_of([v, hop_c(v)])

    def pair_scatter(v):
        return v[:own] + hop_c(v[own:].astype(BF16)).astype(F32)

    heads_s = 4 * half // HEAD_DIM
    frames_pair = 2 * frames_own
    resid0 = jnp.where(masked, embed_row, source)
    std0, inv0 = norm_rows(resid0)
    normed0 = pair_gather((std0 * gain[0]).astype(BF16))
    wf_in, wf_out = gather_ff(ff_in), gather_ff(ff_out)
    joined0 = dot_nn(normed0, ws_qkv).astype(BF16)
    mixed0, total0 = space_attend(joined0, frames_pair, patches, heads_s, scale)
    resid1 = resid0 + pair_scatter(dot_nt(mixed0, ws_out))
    std1, inv1 = norm_rows(resid1)
    normed1, joined1, mixed1, total1, delta, upstream = time_call(
        False,
        (std1 * gain[1]).astype(BF16).reshape(frames_own, patches, width),
        cotangent.reshape(4, own, BLK),
        [],
        wt_qkv,
        wt_out,
        bias,
        scale,
    )
    normed1 = normed1.reshape(4 * own, width)
    mixed1 = mixed1.reshape(4 * own, -1)
    grad3 = jnp.where(masked, upstream, jnp.zeros((), BF16))
    gb3 = pair_gather(grad3)
    resid2 = resid1 + delta.reshape(own, width)
    std2, inv2 = norm_rows(resid2)
    normed2 = pair_gather((std2 * gain[2]).astype(BF16))
    hidden, pulls = [], []
    for w in wf_in:
        activated, pull = jax.vjp(gelu_tanh, dot_nn(normed2, w))
        hidden.append(activated.astype(BF16))
        pulls.append(pull)
    block_part = sum(dot_nt(h, w) for h, w in zip(hidden, wf_out))
    block_rows = (resid2 + pair_scatter(block_part)).astype(BF16)

    def line_scatter(lhs, parts):
        parts = jnp.stack([dot_tn(lhs, rhs).astype(BF16) for rhs in parts])
        return lax.psum_scatter(parts, "mp", scatter_dimension=0)

    def plane_scatter(v):
        return lax.psum_scatter(v, ("tm", "x"), scatter_dimension=0, tiled=True).astype(F32)

    def send_x(lhs, rhs):
        there = jnp.where(x == 0, cols([lhs[:, BLK : 2 * BLK], lhs[:, 3 * BLK :]]), cols([lhs[:, :BLK], lhs[:, 2 * BLK : 3 * BLK]]))
        return hop_x(dot_tn(there, rhs).astype(BF16))

    def keep_x(lhs, rhs, landed):
        here = jnp.where(x == 1, cols([lhs[:, BLK : 2 * BLK], lhs[:, 3 * BLK :]]), cols([lhs[:, :BLK], lhs[:, 2 * BLK : 3 * BLK]]))
        return dot_tn(here, rhs) + landed.astype(F32)

    def mine_y(v):
        return jnp.where(y == 0, v[:BLK], v[BLK:])

    def other_y(v):
        return jnp.where(y == 1, v[:BLK], v[BLK:])

    def reduce_z(pieces):
        total = pieces[0]
        for r in (1, 2, 3):
            total = total + hop_z(pieces[r].astype(BF16), r).astype(F32)
        return total

    def swap_c(total):
        rows = BLK // 2
        kept = lax.dynamic_slice_in_dim(total, c * rows, rows, 0)
        sent = hop_c(lax.dynamic_slice_in_dim(total, (1 - c) * rows, rows, 0).astype(BF16))
        return (kept, sent.astype(F32))

    def by_core(kept, landed):
        return jnp.where(c == 0, jnp.concatenate([kept, landed], -1), jnp.concatenate([landed, kept], -1))

    w_out_part = line_scatter(gb3, hidden)
    grad_inner = [pull(dot_nn(gb3, w))[0].astype(BF16) for pull, w in zip(pulls, wf_out)]
    part2 = pair_scatter(sum(dot_nt(g, w) for g, w in zip(grad_inner, wf_in)))
    w_in_part = line_scatter(normed2, grad_inner)
    back2, gain_grad2 = norm_rows_back(part2, std2, inv2, gain[2])
    grad2 = grad3.astype(F32) + back2
    gb2, djoined1, part1, block_out = time_call(
        True,
        grad2.astype(BF16).reshape(frames_own, patches, width),
        block_rows,
        [joined1, total1],
        wt_qkv,
        wt_out,
        bias,
        scale,
    )
    block_out = block_out.reshape(tokens.shape)
    gb2 = gb2.reshape(4 * own, width)
    djoined1 = djoined1.reshape(4 * own, -1)
    part1 = part1.reshape(own, width)
    back1, gain_grad1 = norm_rows_back(part1, std1, inv1, gain[1])
    grad1 = grad2 + back1
    gb1 = pair_gather(grad1.astype(BF16))
    gb1, w_out_part = tie(gb1, w_out_part)
    g_w_out = plane_scatter(w_out_part)
    t_out_x = send_x(gb2, mixed1)
    t_qkv_x = send_x(normed1, djoined1)
    dmixed0 = dot_nn(gb1, ws_out).astype(BF16)
    go = dot_tn(gb1, mixed0).astype(BF16)
    djoined0 = space_attend_back(joined0, dmixed0, total0, frames_pair, patches, heads_s, scale)
    djoined0, t_out_x, t_qkv_x, w_in_part, go = tie(djoined0, t_out_x, t_qkv_x, w_in_part, go)
    g_w_in = plane_scatter(w_in_part)
    g_t_out = keep_x(gb2, mixed1, t_out_x)
    g_t_qkv = keep_x(normed1, djoined1, t_qkv_x)
    z_at = [(z + r) % 4 for r in range(4)]
    span = 4 * HEAD_DIM
    g_time = reduce_z(
        [
            cols(
                [lax.dynamic_slice_in_dim(g_t_qkv, j * span + s * HEAD_DIM, HEAD_DIM, 1) for j in range(3)]
                + [lax.dynamic_slice_in_dim(g_t_out, s * HEAD_DIM, HEAD_DIM, 1)]
            )
            for s in z_at
        ]
    )
    small = rows_of([jnp.zeros((1, width), F32), gain_grad1[None], gain_grad2[None], jnp.zeros((5, width), F32)])
    kept, landed, grad_tokens, small = settle(
        djoined0, go, normed0.T, ws_qkv, std0, grad1, inv0, masked.astype(F32), gain[0], small
    )
    grad_tokens = grad_tokens.reshape(tokens.shape).astype(F32)

    rows = BLK // 2
    grad_qkv_space = by_core(
        kept[:, : 3 * half].reshape(rows, 3, half), landed[:, : 3 * half].reshape(rows, 3, half)
    )
    grad_out_space = by_core(kept[:, 3 * half :], landed[:, 3 * half :]).T
    kept, landed = swap_c(cols([g_w_in, g_w_out]))
    grad_w_in = by_core(kept[:, :hidden_own], landed[:, :hidden_own])
    grad_w_out = by_core(kept[:, hidden_own:], landed[:, hidden_own:]).T
    both = cols([mine_y(g_time), hop_y(other_y(g_time).astype(BF16)).astype(F32)])
    kept, landed = swap_c(both)
    quad = jnp.stack([kept, landed], 1).reshape(rows, 2, 2, 4, HEAD_DIM)
    quad = jnp.where(c == 1, quad[:, ::-1], quad)
    quad = jnp.where(y == 1, quad[:, :, ::-1], quad)
    quad = jnp.transpose(quad, (0, 3, 2, 1, 4)).reshape(rows, 4, 4 * HEAD_DIM)
    grad_qkv_time = quad[:, :3]
    grad_out_time = quad[:, 3].T
    return (
        block_out,
        grad_tokens,
        small[3],
        small[:3],
        grad_qkv_space,
        grad_out_space,
        grad_qkv_time,
        grad_out_time,
        grad_w_in,
        grad_w_out,
    )


def solution(mesh):
    sizes = (mesh.shape["tm"], mesh.shape["clip"], mesh.shape["mp"])
    if sizes == (2, 4, 4):
        mesh = jax.sharding.Mesh(mesh.devices.reshape(2, 2, 2, 4), AXES)
        step, clip = token_parallel, ("x", "c")
    else:
        step, clip = shards, ("clip",)
    return jax.shard_map(
        step,
        mesh=mesh,
        in_specs=(
            P(clip, "tm", None, "mp"),
            P(clip, "tm", None, "mp"),
            P(clip),
            P(clip, "tm", None),
            P(clip, None),
            P("mp"),
            P(None, "mp"),
            P(None, None, "mp"),
            P("mp", None),
            P(None, None, "mp"),
            P("mp", None),
            P(None, "mp"),
            P("mp", None),
        ),
        out_specs=(
            P(clip, "tm", None, "mp"),
            P(clip, "tm", None, "mp"),
            P("mp"),
            P(None, "mp"),
            P(("tm",) + clip, None, "mp"),
            P("mp", ("tm",) + clip),
            P(("tm",) + clip, None, "mp"),
            P("mp", ("tm",) + clip),
            P(("tm",) + clip, "mp"),
            P("mp", ("tm",) + clip),
        ),
        check_vma=False,
    )
```

```python
import functools
import math

import jax
import jax.numpy as jnp
from jax import lax
from jax.experimental import pallas as pl
from jax.experimental.pallas import tpu as pltpu
from jax.sharding import PartitionSpec as P

HEAD_DIM = 64
MICRO = 2


eps_norm = 1e-05


def gelu_tanh(values):
    return jax.nn.gelu(values, approximate=True)


def norm_forward_pass(residual_stream, gain_coefficients, complete_width):
    reduced_totals = lax.psum(
        (jnp.sum(residual_stream, axis=-1), jnp.sum(residual_stream * residual_stream, axis=-1)),
        "mp",
    )
    centered_rows = reduced_totals[0] / complete_width
    spread = reduced_totals[1] / complete_width - centered_rows * centered_rows
    inverse_scale = lax.rsqrt(spread + eps_norm)
    standardized_rows = (residual_stream - centered_rows[:, None]) * inverse_scale[:, None]
    shard_rows = (standardized_rows * gain_coefficients).astype(jnp.bfloat16)
    normalized_rows = lax.all_gather(shard_rows, "mp", axis=1, tiled=True)
    return (normalized_rows, standardized_rows, inverse_scale)


def norm_reverse_pass(
    normalized_gradient, standardized_rows, inverse_scale, gain_coefficients, complete_width
):
    gain_gradient = jnp.sum(normalized_gradient * standardized_rows, axis=0)
    standardized_gradient = normalized_gradient * gain_coefficients
    reduced_totals = lax.psum(
        (
            jnp.sum(standardized_gradient, axis=-1),
            jnp.sum(standardized_gradient * standardized_rows, axis=-1),
        ),
        "mp",
    )
    grad_resid = (
        standardized_gradient
        - reduced_totals[0][:, None] / complete_width
        - standardized_rows * (reduced_totals[1][:, None] / complete_width)
    ) * inverse_scale[:, None]
    return (grad_resid, gain_gradient)


def sum_features(grad_full):
    return lax.psum_scatter(
        grad_full.astype(jnp.bfloat16), "mp", scatter_dimension=1, tiled=True
    ).astype(jnp.float32)


def branch_out(hidden, weight):
    partial_rows = jnp.dot(hidden, weight, preferred_element_type=jnp.float32)
    return lax.psum_scatter(partial_rows, "mp", scatter_dimension=1, tiled=True)


def branch_back(grad_resid, hidden, weight):
    grad_rows = lax.all_gather(grad_resid.astype(jnp.bfloat16), "mp", axis=1, tiled=True)
    weight_grad = jnp.einsum("rk,rd->kd", hidden, grad_rows, preferred_element_type=jnp.float32)
    grad_hidden = jnp.einsum("rd,kd->rk", grad_rows, weight, preferred_element_type=jnp.float32)
    return (grad_hidden, weight_grad)


def qkv_back(normalized_rows, grad_joined, weight):
    weight_grad = jnp.einsum(
        "rd,trk->dtk", normalized_rows, grad_joined, preferred_element_type=jnp.float32
    )
    grad_full = jnp.einsum("trk,dtk->rd", grad_joined, weight, preferred_element_type=jnp.float32)
    return (weight_grad, sum_features(grad_full))


def reduce_grads(local_grads, small_grads):
    reduced = (
        lax.psum_scatter(local_grads[0], ("tm", "clip"), scatter_dimension=0, tiled=True),
        lax.psum_scatter(local_grads[1], ("tm", "clip"), scatter_dimension=1, tiled=True),
        lax.psum_scatter(local_grads[2], ("tm", "clip"), scatter_dimension=0, tiled=True),
        lax.psum_scatter(local_grads[3], ("tm", "clip"), scatter_dimension=1, tiled=True),
        lax.psum_scatter(local_grads[4], ("tm", "clip"), scatter_dimension=0, tiled=True),
        lax.psum_scatter(local_grads[5], ("tm", "clip"), scatter_dimension=1, tiled=True),
    )
    reduced_small = lax.psum((small_grads[0], small_grads[1]), ("tm", "clip"))
    return (reduced, reduced_small)


def space_forward(normalized_rows, weight, frame_count, patches, heads_local, scale):
    joined = jnp.einsum(
        "rd,dtk->trk", normalized_rows, weight, preferred_element_type=jnp.float32
    ).astype(jnp.bfloat16)
    shape_heads = (frame_count, patches, heads_local, HEAD_DIM)
    scores = (
        jnp.einsum(
            "bshd,bthd->bhst",
            joined[0].reshape(shape_heads),
            joined[1].reshape(shape_heads),
            preferred_element_type=jnp.float32,
        )
        * scale
    )
    highest = jnp.max(scores, axis=-1, keepdims=True)
    exponent = jnp.exp(scores - highest)
    reduced_totals = jnp.sum(exponent, axis=-1, keepdims=True)
    log_total = highest + jnp.log(reduced_totals)
    attention = (exponent / reduced_totals).astype(jnp.bfloat16)
    mixed = jnp.einsum(
        "bhst,bthd->bshd",
        attention,
        joined[2].reshape(shape_heads),
        preferred_element_type=jnp.float32,
    )
    return (
        joined,
        log_total,
        mixed.astype(jnp.bfloat16).reshape(frame_count * patches, heads_local * HEAD_DIM),
    )


def space_backward(grad_mixed, joined, log_total, frame_count, patches, heads_local, scale):
    shape_heads = (frame_count, patches, heads_local, HEAD_DIM)
    queries = joined[0].reshape(shape_heads)
    key_rows = joined[1].reshape(shape_heads)
    values = joined[2].reshape(shape_heads)
    grad_out = grad_mixed.reshape(shape_heads)
    scores = (
        jnp.einsum("bshd,bthd->bhst", queries, key_rows, preferred_element_type=jnp.float32) * scale
    )
    attention = jnp.exp(scores - log_total)
    grad_values = jnp.einsum(
        "bhst,bshd->bthd",
        attention.astype(jnp.bfloat16),
        grad_out,
        preferred_element_type=jnp.float32,
    )
    grad_att = jnp.einsum("bshd,bthd->bhst", grad_out, values, preferred_element_type=jnp.float32)
    grad_scores = (
        attention * (grad_att - jnp.sum(attention * grad_att, axis=-1, keepdims=True))
    ).astype(jnp.bfloat16)
    grad_queries = (
        jnp.einsum("bhst,bthd->bshd", grad_scores, key_rows, preferred_element_type=jnp.float32)
        * scale
    )
    grad_keys = (
        jnp.einsum("bhst,bshd->bthd", grad_scores, queries, preferred_element_type=jnp.float32)
        * scale
    )
    row_count = frame_count * patches
    stacked = jnp.stack(
        [
            grad_queries.reshape(row_count, -1),
            grad_keys.reshape(row_count, -1),
            grad_values.reshape(row_count, -1),
        ]
    )
    return stacked.astype(jnp.bfloat16)


def time_scores(queries, keys_all, visible, scale):
    scores = (
        jnp.einsum("cfshd,cgshd->chfgs", queries, keys_all, preferred_element_type=jnp.float32)
        * scale
    )
    return jnp.where(visible, scores, -1e30)


def time_forward(queries, keys_all, values_all, visible, scale):
    scores = time_scores(queries, keys_all, visible, scale)
    highest = jnp.max(scores, axis=3, keepdims=True)
    exponent = jnp.exp(scores - highest)
    reduced_totals = jnp.sum(exponent, axis=3, keepdims=True)
    log_total = highest + jnp.log(reduced_totals)
    attention = (exponent / reduced_totals).astype(jnp.bfloat16)
    mixed = jnp.einsum(
        "chfgs,cgshd->cfshd", attention, values_all, preferred_element_type=jnp.float32
    )
    return (log_total, mixed.astype(jnp.bfloat16))


def time_backward(grad_mixed, queries, keys_all, values_all, visible, log_total, scale):
    grad_out = grad_mixed.reshape(queries.shape)
    scores = time_scores(queries, keys_all, visible, scale)
    attention = jnp.exp(scores - log_total)
    grad_values = jnp.einsum(
        "chfgs,cfshd->cgshd",
        attention.astype(jnp.bfloat16),
        grad_out,
        preferred_element_type=jnp.float32,
    )
    grad_att = jnp.einsum(
        "cfshd,cgshd->chfgs", grad_out, values_all, preferred_element_type=jnp.float32
    )
    grad_scores = (
        attention * (grad_att - jnp.sum(attention * grad_att, axis=3, keepdims=True))
    ).astype(jnp.bfloat16)
    grad_queries = (
        jnp.einsum("chfgs,cgshd->cfshd", grad_scores, keys_all, preferred_element_type=jnp.float32)
        * scale
    )
    grad_keys = (
        jnp.einsum("chfgs,cfshd->cgshd", grad_scores, queries, preferred_element_type=jnp.float32)
        * scale
    )
    return (grad_queries, grad_keys, grad_values)


def shards(
    tokens,
    cotangent,
    ratio,
    priority,
    frame_order,
    mask_embed,
    gains,
    qkv_space,
    out_space,
    qkv_time,
    out_time,
    w_in,
    w_out,
):
    scale = 1.0 / math.sqrt(HEAD_DIM)
    clips_local = tokens.shape[0] // MICRO
    frames_local = tokens.shape[1]
    patches = tokens.shape[2]
    cols_local = tokens.shape[3]
    frames_all = frame_order.shape[1]
    hidden_width = qkv_space.shape[0]
    joined_local = qkv_space.shape[2]
    heads_local = joined_local // HEAD_DIM
    row_count = clips_local * frames_local * patches
    gain_broadcast = gains.astype(jnp.float32)
    embed_row = mask_embed.astype(jnp.float32)
    first_frame = lax.axis_index("tm") * frames_local
    shape_local = (clips_local, frames_local, patches, joined_local)
    shape_heads = (clips_local, frames_local, patches, heads_local, HEAD_DIM)
    shape_all = (clips_local, frames_all, patches, heads_local, HEAD_DIM)
    outputs = []
    input_grads = []
    weight_total = None
    small_total = None
    for batch_index in range(MICRO):
        lower = batch_index * clips_local
        upper = lower + clips_local
        source = tokens[lower:upper].reshape(row_count, cols_local).astype(jnp.float32)
        upstream = cotangent[lower:upper].reshape(row_count, cols_local).astype(jnp.float32)
        masked = (priority[lower:upper] < ratio[lower:upper][:, None, None]).reshape(row_count)
        order_rows = frame_order[lower:upper]
        residual_stream0 = jnp.where(masked[:, None], embed_row[None, :], source)
        normalized_rows0, standardized_rows0, inverse_deviation0 = norm_forward_pass(
            residual_stream0, gain_broadcast[0], hidden_width
        )
        joined0, total0, mixed0 = space_forward(
            normalized_rows0, qkv_space, clips_local * frames_local, patches, heads_local, scale
        )
        residual_stream1 = residual_stream0 + branch_out(mixed0, out_space)
        normalized_rows1, standardized_rows1, inverse_deviation1 = norm_forward_pass(
            residual_stream1, gain_broadcast[1], hidden_width
        )
        joined1 = jnp.einsum(
            "rd,dtk->trk", normalized_rows1, qkv_time, preferred_element_type=jnp.float32
        ).astype(jnp.bfloat16)
        queries_local = joined1[0].reshape(shape_local)
        keys_local = joined1[1].reshape(shape_local)
        values_local = joined1[2].reshape(shape_local)
        keys_all, values_all = (
            lax.all_gather(keys_local, "tm", axis=1, tiled=True),
            lax.all_gather(values_local, "tm", axis=1, tiled=True),
        )
        query_order = lax.dynamic_slice_in_dim(order_rows, first_frame, frames_local, axis=1)
        time_visible = (order_rows[:, None, :] <= query_order[:, :, None])[:, None, :, :, None]
        time_q = queries_local.reshape(shape_heads)
        time_k = keys_all.reshape(shape_all)
        time_v = values_all.reshape(shape_all)
        total1, mixed_frames = time_forward(time_q, time_k, time_v, time_visible, scale)
        mixed1 = mixed_frames.reshape(row_count, joined_local)
        residual_stream2 = residual_stream1 + branch_out(mixed1, out_time)
        normalized_rows2, standardized_rows2, inverse_deviation2 = norm_forward_pass(
            residual_stream2, gain_broadcast[2], hidden_width
        )
        projected = jnp.dot(normalized_rows2, w_in, preferred_element_type=jnp.float32)
        activated, gelu_pull = jax.vjp(gelu_tanh, projected)
        hidden = activated.astype(jnp.bfloat16)
        resid3 = residual_stream2 + branch_out(hidden, w_out)
        outputs.append(
            resid3.astype(jnp.bfloat16).reshape(clips_local, frames_local, patches, cols_local)
        )
        grad3 = jnp.where(masked[:, None], upstream, 0.0)
        grad_hidden, grad_w_out = branch_back(grad3, hidden, w_out)
        grad_inner = gelu_pull(grad_hidden)[0].astype(jnp.bfloat16)
        grad_w_in = jnp.einsum(
            "rd,rk->dk", normalized_rows2, grad_inner, preferred_element_type=jnp.float32
        )
        normalized_gradient2 = sum_features(
            jnp.einsum("rk,dk->rd", grad_inner, w_in, preferred_element_type=jnp.float32)
        )
        backward_third, gain_gradient2 = norm_reverse_pass(
            normalized_gradient2,
            standardized_rows2,
            inverse_deviation2,
            gain_broadcast[2],
            hidden_width,
        )
        grad2 = grad3 + backward_third
        grad_mixed1, grad_out_time = branch_back(grad2, mixed1, out_time)
        grad_mixed_low = grad_mixed1.astype(jnp.bfloat16).reshape(shape_local)
        grad_queries, grad_keys, grad_values = time_backward(
            grad_mixed_low, time_q, time_k, time_v, time_visible, total1, scale
        )
        key_part, value_part = (
            lax.psum_scatter(
                grad_keys.reshape(clips_local, frames_all, patches, joined_local).astype(
                    jnp.bfloat16
                ),
                "tm",
                scatter_dimension=1,
                tiled=True,
            ).astype(jnp.float32),
            lax.psum_scatter(
                grad_values.reshape(clips_local, frames_all, patches, joined_local).astype(
                    jnp.bfloat16
                ),
                "tm",
                scatter_dimension=1,
                tiled=True,
            ).astype(jnp.float32),
        )
        grad_joined1 = jnp.stack(
            [
                grad_queries.reshape(row_count, joined_local),
                key_part.reshape(row_count, joined_local),
                value_part.reshape(row_count, joined_local),
            ]
        ).astype(jnp.bfloat16)
        grad_qkv_time, normalized_gradient1 = qkv_back(normalized_rows1, grad_joined1, qkv_time)
        backward_second, gain_gradient1 = norm_reverse_pass(
            normalized_gradient1,
            standardized_rows1,
            inverse_deviation1,
            gain_broadcast[1],
            hidden_width,
        )
        grad1 = grad2 + backward_second
        grad_mixed0, grad_out_space = branch_back(grad1, mixed0, out_space)
        grad_joined0 = space_backward(
            grad_mixed0.astype(jnp.bfloat16),
            joined0,
            total0,
            clips_local * frames_local,
            patches,
            heads_local,
            scale,
        )
        grad_qkv_space, normalized_gradient0 = qkv_back(normalized_rows0, grad_joined0, qkv_space)
        backward_first, gain_gradient0 = norm_reverse_pass(
            normalized_gradient0,
            standardized_rows0,
            inverse_deviation0,
            gain_broadcast[0],
            hidden_width,
        )
        grad0 = grad1 + backward_first
        input_grads.append(
            jnp.where(masked[:, None], 0.0, grad0).reshape(
                clips_local, frames_local, patches, cols_local
            )
        )
        grad_embed = jnp.sum(jnp.where(masked[:, None], grad0, 0.0), axis=0)
        gain_grads = jnp.stack([gain_gradient0, gain_gradient1, gain_gradient2])
        local_grads = (
            grad_qkv_space,
            grad_out_space,
            grad_qkv_time,
            grad_out_time,
            grad_w_in,
            grad_w_out,
        )
        small_grads = (gain_grads, grad_embed)
        reduced, reduced_small = reduce_grads(local_grads, small_grads)
        if weight_total is None:
            weight_total = reduced
            small_total = reduced_small
        else:
            weight_total = tuple((total + grad for total, grad in zip(weight_total, reduced)))
            small_total = tuple((total + grad for total, grad in zip(small_total, reduced_small)))
    return (
        jnp.concatenate(outputs, axis=0),
        jnp.concatenate(input_grads, axis=0),
        small_total[1],
        small_total[0],
        weight_total[0],
        weight_total[1],
        weight_total[2],
        weight_total[3],
        weight_total[4],
        weight_total[5],
    )


AXES = ("tm", "x", "c", "mp")
F32 = jnp.float32
BF16 = jnp.bfloat16
BLK = 256
MESH = pl.DeviceIdType.MESH


def device_pairs(move):
    pairs = []
    for y in range(2):
        for x in range(2):
            for c in range(2):
                for z in range(4):
                    there = move(y, x, c, z)
                    pairs.append(tuple(((q[0] * 2 + q[1]) * 2 + q[2]) * 4 + q[3] for q in ((y, x, c, z), there)))
    return pairs


def hop_y(v):
    return lax.ppermute(v, AXES, device_pairs(lambda y, x, c, z: (1 - y, x, c, z)))


def hop_x(v):
    return lax.ppermute(v, AXES, device_pairs(lambda y, x, c, z: (y, 1 - x, c, z)))


def hop_c(v):
    return lax.ppermute(v, AXES, device_pairs(lambda y, x, c, z: (y, x, 1 - c, z)))


def hop_z(v, shift):
    return lax.ppermute(v, AXES, device_pairs(lambda y, x, c, z: (y, x, c, (z + shift) % 4)))


def spread_pairs(r):
    def move(y, x, c, z):
        k = z ^ r
        return (y, x, k & 1, 2 * c + (k >> 1))

    return device_pairs(move)


def arrive_kernel(
    tok, vec, mine, later, rows_out, vec_out, wq, wo, wt,
    z_send, z_recv, y_send, y_recv, x_send, x_recv, p_send, p_recv, q_send, q_recv,
    t_send, t_recv, v_send, v_recv, u_send, u_recv, w_send, w_recv, local,
):
    y, x, c, z = (lax.axis_index(name) for name in AXES)
    half = wo.shape[1] // 4
    wide = 3 * half

    barrier = pltpu.get_barrier_semaphore()
    for dc in range(2):
        for dz in range(4):
            if dc or dz:
                peer = (y, x, (c + dc) % 2, (z + dz) % 4)
                pl.semaphore_signal(barrier, inc=1, device_id=peer, device_id_type=MESH)
    near_y, near_x = (1 - y, x, c, z), (y, 1 - x, c, z)
    for peer in (near_y, near_x):
        pl.semaphore_signal(barrier, inc=1, device_id=peer, device_id_type=MESH)
    pl.semaphore_wait(barrier, 9)

    def rows(dy, dx):
        return pl.ds(pl.multiple_of(BLK * (2 * ((y + dy) % 2) + (x + dx) % 2), BLK), BLK)

    def piece(dy, dx, r, split=False):
        s = (z + r) % 4
        at = pl.multiple_of(s * wide, half)
        out = wo.at[rows(dy, dx), pl.ds(pl.multiple_of(s * half, half), half)]
        if split:
            late = pl.multiple_of(s * wide + 2 * half, half)
            return (wq.at[rows(dy, dx), pl.ds(at, 2 * half)], wq.at[rows(dy, dx), pl.ds(late, half)], out)
        return (wq.at[rows(dy, dx), pl.ds(at, wide)], out)

    def copies(sources, targets, send, recv, peer):
        return [
            pltpu.make_async_remote_copy(
                src_ref=src, dst_ref=dst, send_sem=send.at[i], recv_sem=recv.at[i], device_id=peer, device_id_type=MESH
            )
            for i, (src, dst) in enumerate(zip(sources, targets))
        ]

    own_rows = rows(0, 0)
    own_slice = (mine.at[own_rows, pl.ds(0, wide)], mine.at[own_rows, pl.ds(wide, half)])

    def z_copies(right, step):
        if right:
            r = 0 if step == 0 else 4 - step
            peer, lands = (y, x, c, (z + 1) % 4), 3 - step
        else:
            r = step
            peer, lands = (y, x, c, (z + 3) % 4), step + 1
        target = piece(0, 0, r)
        source = own_slice if step == 0 else target
        return copies(source, target, z_send.at[int(right), step], z_recv.at[lands], peer)

    def y_copies(r):
        return copies(piece(0, 0, r), piece(0, 0, r), y_send.at[r], y_recv.at[r], near_y)

    def x_copies(r):
        return copies(piece(0, 0, r), piece(0, 0, r), x_send.at[r], x_recv.at[r], near_x)

    def corner_x(r):
        part = piece(1, 0, r, split=True)[:1]
        return copies(part, part, p_send.at[r], p_recv.at[r], near_x)

    def corner_y(r):
        part = piece(0, 1, r, split=True)[1:]
        return copies(part, part, q_send.at[r], q_recv.at[r], near_y)

    span = wt.shape[1] // 4

    def time_piece(dx, r):
        at = pl.ds(pl.multiple_of(((z + r) % 4) * span, span), span)
        return wt.at[pl.ds(pl.multiple_of(2 * BLK * ((x + dx) % 2), BLK), 2 * BLK), at]

    def time_z(right, step):
        if right:
            r = 0 if step == 0 else 4 - step
            peer, lands = (y, x, c, (z + 1) % 4), 3 - step
        else:
            r = step
            peer, lands = (y, x, c, (z + 3) % 4), step + 1
        source = later.at[pl.ds(pl.multiple_of(2 * BLK * x, BLK), 2 * BLK)] if step == 0 else time_piece(0, r)
        return [
            pltpu.make_async_remote_copy(
                src_ref=source, dst_ref=time_piece(0, r), send_sem=u_send.at[int(right), step], recv_sem=u_recv.at[lands],
                device_id=peer, device_id_type=MESH,
            )
        ]

    def time_x(dx, r):
        return [
            pltpu.make_async_remote_copy(
                src_ref=time_piece(dx, r), dst_ref=time_piece(dx, r), send_sem=w_send.at[r], recv_sem=w_recv.at[r],
                device_id=near_x, device_id_type=MESH,
            )
        ]

    def time_forward(j, left):
        r = 3 - j if left else j + 1
        pltpu.make_async_remote_copy(
            src_ref=time_piece(0, r), dst_ref=time_piece(0, r), send_sem=u_send.at[0, 0], recv_sem=u_recv.at[r],
            device_id=near_x, device_id_type=MESH,
        ).wait_recv()
        if j < 2:
            pl.when(z < 3 if left else z > 0)(lambda: start(time_z(left, j + 1)))
        start(time_x(0, r))

    def start(all_copies):
        for copy in all_copies:
            copy.start()

    def landed(all_copies):
        for copy in all_copies:
            copy.wait_recv()

    def sent(all_copies):
        for copy in all_copies:
            copy.wait_send()

    def token_copies(k):
        peer = (y, x, k % 2, 2 * c + k // 2)
        at = pl.ds(pl.multiple_of(z * BLK, BLK), BLK)
        return [
            pltpu.make_async_remote_copy(
                src_ref=src, dst_ref=dst, send_sem=send.at[k], recv_sem=recv.at[z], device_id=peer, device_id_type=MESH
            )
            for src, dst, send, recv in (
                (tok.at[k], rows_out.at[:, at], t_send, t_recv),
                (vec, vec_out.at[:, at], v_send, v_recv),
            )
        ]

    def token_local(k):
        at = pl.ds(pl.multiple_of(z * BLK, BLK), BLK)
        return [
            pltpu.make_async_copy(tok.at[k], rows_out.at[:, at], local.at[2]),
            pltpu.make_async_copy(vec, vec_out.at[:, at], local.at[3]),
        ]

    def stays(k):
        return jnp.logical_and(2 * c + k // 2 == z, c == k % 2)

    def from_right(j):
        return z <= 2 - j

    def from_left(j):
        return z >= j + 1

    pl.when(z < 3)(lambda: start(z_copies(True, 0)))
    pl.when(z > 0)(lambda: start(z_copies(False, 0)))
    keep = [
        pltpu.make_async_copy(mine.at[:, pl.ds(0, wide)], wq.at[:, pl.ds(pl.multiple_of(z * wide, half), wide)], local.at[0]),
        pltpu.make_async_copy(mine.at[:, pl.ds(wide, half)], wo.at[:, pl.ds(pl.multiple_of(z * half, half), half)], local.at[1]),
        pltpu.make_async_copy(later, wt.at[:, pl.ds(pl.multiple_of(z * span, span), span)], local.at[4]),
    ]
    start(keep)

    def forward(j, left):
        r = 3 - j if left else j + 1
        landed(copies(piece(0, 0, r), piece(0, 0, r), z_send.at[0, 0], z_recv.at[r], near_y))
        if j < 2:
            pl.when(z < 3 if left else z > 0)(lambda: start(z_copies(left, j + 1)))
        start(y_copies(r))
        start(x_copies(r))

    def corners(j, left):
        r = 3 - j if left else j + 1
        landed(copies(piece(1, 0, r), piece(1, 0, r), y_send.at[r], y_recv.at[r], near_y))
        start(corner_x(r))
        landed(copies(piece(0, 1, r), piece(0, 1, r), x_send.at[r], x_recv.at[r], near_x))
        start(corner_y(r))

    for j in range(3):
        for left in (True, False):
            pl.when(from_left(j) if left else from_right(j))(lambda j=j, left=left: forward(j, left))
        if j == 0:
            for k in range(4):
                pl.when(stays(k))(lambda k=k: start(token_local(k)))
                pl.when(jnp.logical_not(stays(k)))(lambda k=k: start(token_copies(k)))
            pl.when(z < 3)(lambda: start(time_z(True, 0)))
            pl.when(z > 0)(lambda: start(time_z(False, 0)))
        else:
            for left in (True, False):
                pl.when(from_left(j - 1) if left else from_right(j - 1))(lambda j=j, left=left: corners(j - 1, left))
    for left in (True, False):
        pl.when(from_left(2) if left else from_right(2))(lambda left=left: corners(2, left))
    for j in range(3):
        for left in (True, False):
            pl.when(from_left(j) if left else from_right(j))(lambda j=j, left=left: time_forward(j, left))

    for copy in keep:
        copy.wait()
    for r in (1, 2, 3):
        part = piece(1, 1, r, split=True)
        landed(copies(part[:1], part[:1], p_send.at[r], p_recv.at[r], near_x))
        landed(copies(part[1:], part[1:], q_send.at[r], q_recv.at[r], near_y))
        for group in (y_copies(r), x_copies(r), corner_x(r), corner_y(r), time_x(0, r)):
            sent(group)
        landed(time_x(1, r))
    for step in range(3):
        pl.when(jnp.logical_and(z >= step, z < 3))(lambda step=step: sent(z_copies(True, step) + time_z(True, step)))
        pl.when(jnp.logical_and(z + step <= 3, z > 0))(lambda step=step: sent(z_copies(False, step) + time_z(False, step)))
    for k in range(4):
        def finish_local(k=k):
            for copy in token_local(k):
                copy.wait()

        pl.when(stays(k))(finish_local)
        pl.when(jnp.logical_not(stays(k)))(lambda k=k: sent(token_copies(k)))
    for s in range(4):
        at = pl.ds(s * BLK, BLK)
        away = jnp.logical_not(jnp.logical_and(z == s, z // 2 == c))

        def arrived(s=s, at=at):
            for src, dst, send, recv in (
                (tok.at[0], rows_out.at[:, at], t_send, t_recv),
                (vec, vec_out.at[:, at], v_send, v_recv),
            ):
                pltpu.make_async_remote_copy(
                    src_ref=src, dst_ref=dst, send_sem=send.at[0], recv_sem=recv.at[s], device_id=near_y, device_id_type=MESH
                ).wait_recv()

        pl.when(away)(arrived)


def arrive(tok, vec, mine, later):
    own, width, half = tok.shape[1], 4 * tok.shape[2], mine.shape[1] // 4
    dma = pltpu.SemaphoreType.DMA
    anywhere = pl.BlockSpec(memory_space=pl.ANY)
    return pl.pallas_call(
        arrive_kernel,
        in_specs=[anywhere] * 4,
        out_specs=[anywhere] * 5,
        out_shape=[
            jax.ShapeDtypeStruct((own, width), BF16),
            jax.ShapeDtypeStruct((vec.shape[0], width), BF16),
            jax.ShapeDtypeStruct((width, 12 * half), BF16),
            jax.ShapeDtypeStruct((width, 4 * half), BF16),
            jax.ShapeDtypeStruct((width, 4 * later.shape[1]), BF16),
        ],
        scratch_shapes=[
            dma((2, 3, 2)), dma((4, 2)), dma((4, 2)), dma((4, 2)), dma((4, 2)), dma((4, 2)),
            dma((4, 1)), dma((4, 1)), dma((4, 2)), dma((4, 2)),
            dma((4,)), dma((4,)), dma((4,)), dma((4,)),
            dma((2, 3)), dma((4,)), dma((4,)), dma((4,)), dma((5,)),
        ],
        compiler_params=pltpu.CompilerParams(collective_id=0, has_side_effects=True),
        name="arrive",
    )(tok, vec, mine, later)


def dot_nn(a, b):
    return lax.dot_general(a, b, (((1,), (0,)), ((), ())), preferred_element_type=F32)


def dot_nt(a, b):
    return lax.dot_general(a, b, (((1,), (1,)), ((), ())), preferred_element_type=F32)


def dot_tn(a, b):
    return lax.dot_general(a, b, (((0,), (0,)), ((), ())), preferred_element_type=F32)


def attend_pair(q, k, v, bias, scale):
    mixed, totals = [], []
    for i in range(2):
        mine = slice(i * HEAD_DIM, (i + 1) * HEAD_DIM)
        scores = dot_nt(k[:, mine], q[:, mine]) * scale
        if bias is not None:
            scores = scores + bias
        highest = jnp.max(scores, axis=0, keepdims=True)
        exponent = jnp.exp(scores - highest)
        total = jnp.sum(exponent, axis=0, keepdims=True)
        totals.append(highest + jnp.log(total))
        mixed.append(dot_tn(v[:, mine], exponent.astype(BF16)) * (1.0 / total))
    return (jnp.concatenate(mixed, axis=0).T, totals)


def attend_pair_back(q, k, v, g, totals, bias, scale):
    grads = ([], [], [])
    for i in range(2):
        mine = slice(i * HEAD_DIM, (i + 1) * HEAD_DIM)
        scores = dot_nt(k[:, mine], q[:, mine]) * scale
        if bias is not None:
            scores = scores + bias
        p = jnp.exp(scores - totals[i])
        dp = dot_nt(v[:, mine], g[:, mine])
        ds = (p * (dp - jnp.sum(p * dp, axis=0, keepdims=True))).astype(BF16)
        grads[0].append(dot_tn(k[:, mine], ds) * scale)
        grads[1].append(dot_nn(ds, q[:, mine]) * scale)
        grads[2].append(dot_nn(p.astype(BF16), g[:, mine]))
    return (
        jnp.concatenate(grads[0], axis=0).T,
        jnp.concatenate(grads[1], axis=1),
        jnp.concatenate(grads[2], axis=1),
    )


PAIR = 2 * HEAD_DIM


def space_attend_kernel(scale, qkv_ref, out_ref, total_ref):
    for i in range(out_ref.shape[1] // PAIR):
        q, k, v = (qkv_ref[:, (3 * i + part) * PAIR : (3 * i + part + 1) * PAIR] for part in range(3))
        mixed, totals = attend_pair(q, k, v, None, scale)
        out_ref[:, i * PAIR : (i + 1) * PAIR] = mixed.astype(BF16)
        for h in range(2):
            total_ref[0, 2 * i + h : 2 * i + h + 1, :] = totals[h]


def space_attend_back_kernel(scale, qkv_ref, grad_ref, total_ref, out_ref):
    for i in range(grad_ref.shape[1] // PAIR):
        q, k, v = (qkv_ref[:, (3 * i + part) * PAIR : (3 * i + part + 1) * PAIR] for part in range(3))
        totals = [total_ref[0, 2 * i + h : 2 * i + h + 1, :] for h in range(2)]
        grads = attend_pair_back(q, k, v, grad_ref[:, i * PAIR : (i + 1) * PAIR], totals, None, scale)
        for part in range(3):
            out_ref[:, (3 * i + part) * PAIR : (3 * i + part + 1) * PAIR] = grads[part].astype(BF16)


def attention_cost(groups, rows, heads, products):
    return pl.CostEstimate(
        flops=8 * products * groups * heads * rows * rows * HEAD_DIM,
        transcendentals=groups * heads * rows * rows,
        bytes_accessed=2 * groups * rows * heads * HEAD_DIM * 2 * products,
    )


def space_attend(qkv, frames, patches, heads, scale):
    width = heads * HEAD_DIM
    return pl.pallas_call(
        functools.partial(space_attend_kernel, scale),
        grid=(frames,),
        in_specs=[pl.BlockSpec((patches, 3 * width), lambda i: (i, 0))],
        out_specs=[
            pl.BlockSpec((patches, width), lambda i: (i, 0)),
            pl.BlockSpec((1, heads, patches), lambda i: (i, 0, 0)),
        ],
        out_shape=[
            jax.ShapeDtypeStruct((frames * patches, width), BF16),
            jax.ShapeDtypeStruct((frames, heads, patches), F32),
        ],
        cost_estimate=attention_cost(frames, patches, heads, 2),
        name="space_attend",
    )(qkv)


def space_attend_back(qkv, grad, total, frames, patches, heads, scale):
    width = heads * HEAD_DIM
    return pl.pallas_call(
        functools.partial(space_attend_back_kernel, scale),
        grid=(frames,),
        in_specs=[
            pl.BlockSpec((patches, 3 * width), lambda i: (i, 0)),
            pl.BlockSpec((patches, width), lambda i: (i, 0)),
            pl.BlockSpec((1, heads, patches), lambda i: (i, 0, 0)),
        ],
        out_specs=pl.BlockSpec((patches, 3 * width), lambda i: (i, 0)),
        out_shape=jax.ShapeDtypeStruct((frames * patches, 3 * width), BF16),
        cost_estimate=attention_cost(frames, patches, heads, 5),
        name="space_attend_back",
    )(qkv, grad, total)


GROUP = 8
CHUNK = 32


def time_kernel(back, scale, heads, *refs):
    if back:
        (own_ref, rider_ref, joined_ref, total_ref, wide_ref, wq_ref, wo_ref, bias_ref) = refs[:8]
        (all_ref, out_ref, delta_ref, halved_ref, rider_out) = refs[8:13]
        (halved_in, halved_own, half_send, half_recv, half_local) = refs[-5:]
        refs = refs[13:-5]
    else:
        (own_ref, rider_ref, far_ref, near_ref, wq_ref, wo_ref, bias_ref) = refs[:7]
        (all_ref, out_ref, mixed_ref, total_ref, delta_ref, rider_out, spread_out) = refs[7:14]
        refs = refs[14:]
    (
        held, wide, narrow, kept, core_out, core_in, near_out, near_in,
        gy_send, gy_recv, gc_send, gc_recv, gd_send, gd_recv, sc_send, sc_recv, sy_send, sy_recv,
        r_send, r_recv, r_local, out_sem, wy_send, wy_recv, wx_send, wx_recv, wd_send, wd_recv, w_local,
    ) = refs
    y, x, c, z = (lax.axis_index(name) for name in AXES)
    near, pair, near_x = (1 - y, x, c, z), (y, x, 1 - c, z), (y, 1 - x, c, z)
    frames = held.shape[0] // 4
    chunks = held.shape[1] // CHUNK
    width = heads * HEAD_DIM
    groups = CHUNK // GROUP

    barrier = pltpu.get_barrier_semaphore()
    for dc in range(2):
        for dz in range(4):
            if dc or dz:
                pl.semaphore_signal(barrier, inc=1, device_id=(y, x, (c + dc) % 2, (z + dz) % 4), device_id_type=MESH)
    pl.semaphore_signal(barrier, inc=1, device_id=near, device_id_type=MESH)
    pl.semaphore_signal(barrier, inc=1, device_id=near_x, device_id_type=MESH)
    pl.semaphore_wait(barrier, 9)

    def remote(src, dst, send, recv, peer):
        return pltpu.make_async_remote_copy(
            src_ref=src, dst_ref=dst, send_sem=send, recv_sem=recv, device_id=peer, device_id_type=MESH
        )

    def patches(k):
        return pl.ds(pl.multiple_of(k * CHUNK, CHUNK), CHUNK)

    def block(b, k):
        return held.at[pl.ds(b * frames, frames), patches(k)]

    def gather_y(k):
        return remote(own_ref.at[:, patches(k)], block(1, k), gy_send.at[k], gy_recv.at[k], near)

    def gather_c(k):
        return remote(own_ref.at[:, patches(k)], block(2, k), gc_send.at[k], gc_recv.at[k], pair)

    def gather_d(k):
        return remote(block(1, k), block(3, k), gd_send.at[k], gd_recv.at[k], pair)

    def scatter_c(k):
        return remote(core_out.at[k], core_in.at[k], sc_send.at[k], sc_recv.at[k], pair)

    def scatter_y(k):
        return remote(near_out.at[k], near_in.at[k], sy_send.at[k], sy_recv.at[k], near)

    def save(k):
        return pltpu.make_async_copy(held.at[:, patches(k)], all_ref.at[:, patches(k)], out_sem.at[k])

    def columns(s):
        return pl.ds(pl.multiple_of(s * BLK, BLK), BLK)

    def stays(k):
        if back:
            return jnp.logical_and(z == k, z // 2 == c)
        return jnp.logical_and(2 * c + k // 2 == z, c == k % 2)

    def ride(k):
        if back:
            src, dst = rider_ref.at[:, columns(k)], rider_out.at[2 * (z % 2) + c]
            peer, slot = (y, x, z // 2, k), 2 * (z % 2) + c
        else:
            src, dst = rider_ref.at[k], rider_out.at[:, columns(z)]
            peer, slot = (y, x, k % 2, 2 * c + k // 2), z
        return src, dst, peer, slot

    def ride_remote(k):
        src, dst, peer, slot = ride(k)
        return remote(src, dst, r_send.at[k], r_recv.at[slot], peer)

    def ride_local(k):
        src, dst, _, _ = ride(k)
        return pltpu.make_async_copy(src, dst, r_local.at[0])

    def ride_landed(k):
        if back:
            src, dst = rider_ref.at[:, columns(k)], rider_out.at[k]
        else:
            src, dst = rider_ref.at[k], rider_out.at[:, columns(k)]
        return remote(src, dst, r_send.at[k], r_recv.at[k], near)

    def from_self(k):
        if back:
            return jnp.logical_and(2 * c + k // 2 == z, c == k % 2)
        return jnp.logical_and(z == k, z // 2 == c)

    def place(dy, dx, r):
        size = far_ref.shape[1]
        at = pl.multiple_of(size * (2 * ((y + dy) % 2) + (x + dx) % 2), size)
        return spread_out.at[(z + r) % 4, pl.ds(at, size)]

    def spread_y(r, dy=0):
        src = far_ref.at[r - 1] if dy == 0 else place(1, 0, r)
        return remote(src, place(dy, 0, r), wy_send.at[r], wy_recv.at[r], near)

    def spread_x(r, dx=0):
        src = far_ref.at[r - 1] if dx == 0 else place(0, 1, r)
        return remote(src, place(0, dx, r), wx_send.at[r], wx_recv.at[r], near_x)

    def spread_d(r, dx=0):
        return remote(place(1, dx, r), place(1, dx, r), wd_send.at[r], wd_recv.at[r], near_x)

    def spread_keep(r):
        if r == 0:
            size = 4 * far_ref.shape[1]
            here = near_ref.at[pl.ds(pl.multiple_of(c * size, size), size)]
            return pltpu.make_async_copy(here, spread_out.at[z], w_local.at[0])
        return pltpu.make_async_copy(far_ref.at[r - 1], place(0, 0, r), w_local.at[r])

    def spread_on(r):
        spread_y(r, 1).wait_recv()
        spread_d(r).start()

    gather_y(0).start()
    for k in range(chunks):
        if k > 0:
            gather_y(k).start()
        gather_c(k).start()
    def half_rows(yb, xb):
        return pl.ds(pl.multiple_of(BLK * (2 * yb + xb), BLK), BLK)

    def half_away(i):
        src = wide_ref.at[i % 4, half_rows(i // 4, 1 - x)]
        return remote(src, halved_in.at[i // 4, i % 4], half_send.at[i], half_recv.at[i], near_x)

    def half_here(i):
        src = wide_ref.at[i % 4, half_rows(i // 4, x)]
        return pltpu.make_async_copy(src, halved_own.at[i // 4, i % 4], half_local.at[i])

    if back:
        for i in range(8):
            half_away(i).start()
            half_here(i).start()
    else:
        for r in (1, 2, 3):
            spread_x(r).start()
            spread_y(r).start()
        for r in range(4):
            spread_keep(r).start()
    for k in range(4):
        pl.when(stays(k))(lambda k=k: ride_local(k).start())
        pl.when(jnp.logical_not(stays(k)))(lambda k=k: ride_remote(k).start())
    held[:frames] = own_ref[...]

    def finish(k):
        scatter_c(k).wait_recv()
        both = kept[:, patches(k)] + core_in[k].astype(F32)
        near_out[k] = both[frames:].astype(BF16)
        delta_ref[:, patches(k)] = both[:frames]
        scatter_y(k).start()

    def pass_on(k):
        gather_y(k).wait_recv()
        gather_d(k).start()

    def one_group(i, rows):
        at = pl.ds(pl.multiple_of(i * GROUP, GROUP), GROUP)
        count = 4 * frames * GROUP
        bias = bias_ref[...]
        for lo in range(0, width, PAIR):
            q, k, v = (
                wide[:, at, part * width + lo : part * width + lo + PAIR].reshape(count, PAIR).astype(BF16)
                for part in range(3)
            )
            h = lo // HEAD_DIM
            if back:
                g = narrow[:, at, lo : lo + PAIR].reshape(count, PAIR).astype(BF16)
                totals = [total_ref[rows * groups + i, h + j : h + j + 1, :] for j in range(2)]
                grads = attend_pair_back(q, k, v, g, totals, bias, scale)
                for part in range(3):
                    wide[:, at, part * width + lo : part * width + lo + PAIR] = grads[part].reshape(
                        4 * frames, GROUP, PAIR
                    )
            else:
                mixed, totals = attend_pair(q, k, v, bias, scale)
                narrow[:, at, lo : lo + PAIR] = mixed.reshape(4 * frames, GROUP, PAIR)
                for j in range(2):
                    total_ref[rows * groups + i, h + j : h + j + 1, :] = totals[j]

    def one_chunk(k, carry):
        pl.when(k + 1 < chunks)(lambda: pass_on(k + 1))
        gather_c(k).wait_recv()
        gather_d(k).wait_recv()
        count = 4 * frames * CHUNK
        lhs = held[:, patches(k)].reshape(count, held.shape[2])
        if back:
            wide[...] = joined_ref[:, patches(k)].astype(F32)
            narrow[...] = dot_nn(lhs, wo_ref[...]).astype(BF16).astype(F32).reshape(narrow.shape)
        else:
            joined = dot_nn(lhs, wq_ref[...]).astype(BF16)
            out_ref[:, patches(k)] = joined.reshape(wide.shape)
            wide[...] = joined.astype(F32).reshape(wide.shape)
        save(k).start()
        lax.fori_loop(0, groups, lambda i, carry: (one_group(i, k), carry)[1], 0)
        if back:
            grads = wide[...].astype(BF16)
            out_ref[:, patches(k)] = grads
            partial = dot_nt(grads.reshape(count, 3 * width), wq_ref[...])
        else:
            mixed = narrow[...].astype(BF16)
            mixed_ref[:, patches(k)] = mixed
            partial = dot_nt(mixed.reshape(count, width), wo_ref[...])
        partial = partial.reshape(4 * frames, CHUNK, held.shape[2])
        kept[:, patches(k)] = partial[: 2 * frames]
        core_out[k] = partial[2 * frames :].astype(BF16)
        scatter_c(k).start()
        pl.when(k > 0)(lambda: finish(k - 1))
        if not back:
            for r in (1, 2, 3):
                pl.when(k == r)(lambda r=r: spread_on(r))
        return carry

    pass_on(0)
    lax.fori_loop(0, chunks, one_chunk, 0)
    finish(chunks - 1)
    if back:
        for i in range(8):
            half_away(i).wait_recv()
            half_here(i).wait()
            at = (i // 4, i % 4)
            halved_ref[at] = (halved_own[at].astype(F32) + halved_in[at].astype(F32)).astype(BF16)
            half_away(i).wait_send()
    for k in range(chunks):
        scatter_y(k).wait_recv()
        delta_ref[:, patches(k)] = delta_ref[:, patches(k)] + near_in[k].astype(F32)
    for k in range(chunks):
        for copy in (gather_y(k), gather_c(k), gather_d(k), scatter_c(k), scatter_y(k)):
            copy.wait_send()
        save(k).wait()
    if not back:
        for r in (1, 2, 3):
            spread_x(r, 1).wait_recv()
            spread_d(r, 1).wait_recv()
            for copy in (spread_x(r), spread_y(r), spread_d(r)):
                copy.wait_send()
        for r in range(4):
            spread_keep(r).wait()
    for k in range(4):
        pl.when(stays(k))(lambda k=k: ride_local(k).wait())
        pl.when(jnp.logical_not(stays(k)))(lambda k=k: ride_remote(k).wait_send())
        pl.when(jnp.logical_not(from_self(k)))(lambda k=k: ride_landed(k).wait_recv())


def time_call(back, own, rider, saved, wq, wo, bias, scale):
    frames, patches, features = own.shape
    width = wo.shape[1]
    heads = width // HEAD_DIM
    chunks = patches // CHUNK
    rows = 4 * frames * GROUP
    dma = pltpu.SemaphoreType.DMA
    anywhere = pl.BlockSpec(memory_space=pl.ANY)
    whole = pl.BlockSpec(memory_space=pltpu.VMEM)
    out_shape = [
        jax.ShapeDtypeStruct((4 * frames, patches, features), BF16),
        jax.ShapeDtypeStruct((4 * frames, patches, 3 * width), BF16),
    ]
    if not back:
        out_shape += [
            jax.ShapeDtypeStruct((4 * frames, patches, width), BF16),
            jax.ShapeDtypeStruct((patches // GROUP, heads, rows), F32),
        ]
    rider_shape = (4, frames * patches, BLK) if back else (frames * patches, features)
    out_shape += [
        jax.ShapeDtypeStruct((frames, patches, features), F32),
        jax.ShapeDtypeStruct(rider_shape, BF16),
    ]
    held = 2
    halves = (2, 4, BLK, saved[2].shape[2]) if back else None
    if back:
        out_shape.insert(-1, jax.ShapeDtypeStruct(halves, BF16))
    else:
        out_shape.append(jax.ShapeDtypeStruct((4, 4 * saved[0].shape[1], features), BF16))
        held = 3
    return pl.pallas_call(
        functools.partial(time_kernel, back, scale, heads),
        in_specs=[whole, anywhere] + ([whole, whole, anywhere] if back else [anywhere] * 2) + [whole] * 3,
        out_specs=[anywhere] + [whole] * (len(out_shape) - held) + [anywhere] * (held - 1),
        out_shape=out_shape,
        scratch_shapes=[
            pltpu.VMEM((4 * frames, patches, features), BF16),
            pltpu.VMEM((4 * frames, CHUNK, 3 * width), F32),
            pltpu.VMEM((4 * frames, CHUNK, width), F32),
            pltpu.VMEM((2 * frames, patches, features), F32),
            pltpu.VMEM((chunks, 2 * frames, CHUNK, features), BF16),
            pltpu.VMEM((chunks, 2 * frames, CHUNK, features), BF16),
            pltpu.VMEM((chunks, frames, CHUNK, features), BF16),
            pltpu.VMEM((chunks, frames, CHUNK, features), BF16),
        ]
        + [dma((chunks,))] * 10
        + [dma((4,)), dma((4,)), dma((1,)), dma((chunks,))]
        + [dma((4,))] * 7
        + ([pltpu.VMEM(halves, BF16), pltpu.VMEM(halves, BF16), dma((8,)), dma((8,)), dma((8,))] if back else []),
        compiler_params=pltpu.CompilerParams(
            collective_id=2 if back else 1, has_side_effects=True, vmem_limit_bytes=48 * 1024 * 1024
        ),
        cost_estimate=pl.CostEstimate(flops=10**10, transcendentals=10**6, bytes_accessed=10**8),
        name="time_back" if back else "time_forward",
    )(own, rider, *saved, wq, wo, bias)


def feed_kernel(
    resid, delta, upstream, masked, gain, w_in_hbm, w_out_hbm,
    g_in_hbm, g_out_hbm, grad_out, low_out, rows_out, gain_out,
    w_in, w_out, standard, inverse, normed, grads, normed_t, grads_t, hidden, pulled, g_in, g_out, back, ahead,
    back_out, back_in, ahead_out, ahead_in,
    w_sem, g_sem, n_send, n_recv, b_send, b_recv,
):
    y, x, c, z = (lax.axis_index(name) for name in AXES)
    pair = (y, x, 1 - c, z)
    own = resid.shape[0]
    step = own // 2
    slab = 128

    def fetch(s):
        return (
            pltpu.make_async_copy(w_in_hbm.at[s], w_in.at[s], w_sem.at[0, s]),
            pltpu.make_async_copy(w_out_hbm.at[s], w_out.at[s], w_sem.at[1, s]),
        )

    for s in range(4):
        for copy in fetch(s):
            copy.start()
    barrier = pltpu.get_barrier_semaphore()
    pl.semaphore_signal(barrier, inc=1, device_id=pair, device_id_type=MESH)

    def remote(src, dst, send, recv):
        return pltpu.make_async_remote_copy(
            src_ref=src, dst_ref=dst, send_sem=send, recv_sem=recv, device_id=pair, device_id_type=MESH
        )

    def at(i, size):
        return pl.ds(pl.multiple_of(i * size, size), size)

    def prepare(i, carry):
        rows = at(i, step)
        grads[rows] = jnp.where(masked[rows] > 0.0, upstream[rows].astype(F32), 0.0).astype(BF16)
        std, inv = norm_rows(resid[rows] + delta[rows])
        standard[rows] = std
        inverse[rows] = inv
        normed[rows] = (std * gain[...]).astype(BF16)
        return carry

    lax.fori_loop(0, 2, prepare, 0)
    pl.semaphore_wait(barrier, 1)
    mine, theirs = pl.ds(0, own), pl.ds(own, own)
    give_grads = remote(grads.at[mine], grads.at[theirs], n_send.at[0], n_recv.at[0])
    give_normed = remote(normed.at[mine], normed.at[theirs], n_send.at[1], n_recv.at[1])
    give_normed.start()
    give_grads.start()

    def turn(i, carry):
        rows = at(i, slab)
        normed_t[:, rows] = normed[rows].T
        grads_t[:, rows] = grads[rows].T
        return carry

    lax.fori_loop(0, own // slab, turn, 0)
    back[...] = jnp.zeros_like(back)
    ahead[...] = jnp.zeros_like(ahead)
    rate = math.sqrt(2.0 / math.pi)

    def rows_step(s, rows):
        inner = dot_nn(normed[rows], w_in[s])
        square = inner * inner
        bend = jnp.tanh(rate * inner * (1.0 + 0.044715 * square))
        hidden[rows] = (0.5 * inner * (1.0 + bend)).astype(BF16)
        slope = 0.5 * (1.0 + bend) + 0.5 * inner * (1.0 - bend * bend) * (rate * (1.0 + 3.0 * 0.044715 * square))
        pulled[rows] = (dot_nt(grads[rows], w_out[s]) * slope).astype(BF16)
        ahead[rows] = ahead[rows] + dot_nn(hidden[rows], w_out[s])
        back[rows] = back[rows] + dot_nt(pulled[rows], w_in[s])

    def keep(s):
        return (
            pltpu.make_async_copy(g_in.at[s], g_in_hbm.at[s], g_sem.at[0, s]),
            pltpu.make_async_copy(g_out.at[s], g_out_hbm.at[s], g_sem.at[1, s]),
        )

    def meet():
        give_normed.wait_recv()
        give_grads.wait_recv()
        lax.fori_loop(own // slab, 2 * own // slab, turn, 0)

    def one_piece(s, carry):
        for copy in fetch(s):
            copy.wait()

        def one_half(t, carry):
            pl.when(jnp.logical_and(s == 0, t == 1))(meet)
            rows_step(s, at(t, own))
            return carry

        lax.fori_loop(0, 2, one_half, 0)
        g_out[s] = dot_nn(grads_t[...], hidden[...]).astype(BF16)
        g_in[s] = dot_nn(normed_t[...], pulled[...]).astype(BF16)
        for copy in keep(s):
            copy.start()
        return carry

    lax.fori_loop(0, 4, one_piece, 0)
    back_out[...] = back[theirs].astype(BF16)
    give_back = remote(back_out, back_in, b_send.at[0], b_recv.at[0])
    give_back.start()
    ahead_out[...] = ahead[theirs].astype(BF16)
    give_ahead = remote(ahead_out, ahead_in, b_send.at[1], b_recv.at[1])
    give_ahead.start()
    give_back.wait_recv()

    def finish(i, total):
        rows = at(i, step)
        grad = back[rows] + back_in[rows].astype(F32)
        std = standard[rows]
        inner = grad * gain[...]
        mean = jnp.mean(inner, axis=-1, keepdims=True)
        along = jnp.mean(inner * std, axis=-1, keepdims=True)
        full = grads[rows].astype(F32) + (inner - mean - std * along) * inverse[rows]
        grad_out[rows] = full
        low_out[rows] = full.astype(BF16)
        return total + jnp.sum(grad * std, axis=0, keepdims=True)

    gain_out[...] = lax.fori_loop(0, 2, finish, jnp.zeros((1, resid.shape[1]), F32))
    give_ahead.wait_recv()

    def emit(i, carry):
        rows = at(i, step)
        rows_out[rows] = (resid[rows] + delta[rows] + ahead[rows] + ahead_in[rows].astype(F32)).astype(BF16)
        return carry

    lax.fori_loop(0, 2, emit, 0)
    for copy in (give_normed, give_grads, give_back, give_ahead):
        copy.wait_send()
    for s in range(4):
        for copy in keep(s):
            copy.wait()


def feed(resid, delta, upstream, masked, gain, w_in, w_out):
    own, features = resid.shape
    units = w_in.shape[2]
    dma = pltpu.SemaphoreType.DMA
    anywhere = pl.BlockSpec(memory_space=pl.ANY)
    whole = pl.BlockSpec(memory_space=pltpu.VMEM)

    def low(*shape):
        return pltpu.VMEM(shape, BF16)

    def high(*shape):
        return pltpu.VMEM(shape, F32)

    return pl.pallas_call(
        feed_kernel,
        in_specs=[whole] * 5 + [anywhere] * 2,
        out_specs=[anywhere] * 2 + [whole] * 4,
        out_shape=[
            jax.ShapeDtypeStruct((4, features, units), BF16),
            jax.ShapeDtypeStruct((4, features, units), BF16),
            jax.ShapeDtypeStruct((own, features), F32),
            jax.ShapeDtypeStruct((own, features), BF16),
            jax.ShapeDtypeStruct((own, features), BF16),
            jax.ShapeDtypeStruct((1, features), F32),
        ],
        scratch_shapes=[
            low(4, features, units), low(4, units, features), high(own, features), high(own, 1),
            low(2 * own, features), low(2 * own, features), low(features, 2 * own), low(features, 2 * own),
            low(2 * own, units), low(2 * own, units), low(4, features, units), low(4, features, units),
            high(2 * own, features), high(2 * own, features),
            low(own, features), low(own, features), low(own, features), low(own, features),
            dma((2, 4)), dma((2, 4)), dma((2,)), dma((2,)), dma((2,)), dma((2,)),
        ],
        compiler_params=pltpu.CompilerParams(
            collective_id=4, has_side_effects=True, vmem_limit_bytes=60 * 1024 * 1024
        ),
        cost_estimate=pl.CostEstimate(flops=26 * 10**9, transcendentals=2 * 10**6, bytes_accessed=10**8),
        name="feed",
    )(resid, delta, upstream, masked, gain, w_in, w_out)


def settle_kernel(
    dj, go, lhs, weight_hbm, std_hbm, base_hbm, inverse, masked, gain, small_in,
    kept_out, landed_out, rows_out, small_out,
    weight, std, base, grads, a1_out, a1_in, b1_out, b1_in, a2_out, a2_in, b2_out, b2_in, z_out, z_in,
    half_out, half_in, ready, core_out, core_in, sums, sum_out, sum_in, share_in,
    a1_send, a1_recv, b1_send, b1_recv, a2_send, a2_recv, b2_send, b2_recv, z_send, z_recv,
    h_send, h_recv, r_send, r_recv, c_send, c_recv, s_send, s_recv, p_send, p_recv, local,
):
    y, x, c, z = (lax.axis_index(name) for name in AXES)
    near_y, near_x, pair = (1 - y, x, c, z), (y, 1 - x, c, z), (y, x, 1 - c, z)
    own = std.shape[0]
    third = go.shape[1] // 4
    wide = 3 * third
    two = 2 * third

    fetches = [
        pltpu.make_async_copy(weight_hbm, weight, local.at[0]),
        pltpu.make_async_copy(std_hbm, std, local.at[1]),
        pltpu.make_async_copy(base_hbm, base, local.at[2]),
    ]
    for copy in fetches:
        copy.start()

    barrier = pltpu.get_barrier_semaphore()
    for dc in range(2):
        for dz in range(4):
            if dc or dz:
                pl.semaphore_signal(barrier, inc=1, device_id=(y, x, (c + dc) % 2, (z + dz) % 4), device_id_type=MESH)
    for peer in (near_y, near_x):
        pl.semaphore_signal(barrier, inc=1, device_id=peer, device_id_type=MESH)
    pl.semaphore_wait(barrier, 9)

    def remote(src, dst, send, recv, peer):
        return pltpu.make_async_remote_copy(
            src_ref=src, dst_ref=dst, send_sem=send, recv_sem=recv, device_id=peer, device_id_type=MESH
        )

    def block(yb, xb):
        return pl.ds(pl.multiple_of(BLK * (2 * yb + xb), BLK), BLK)

    def a1(i):
        return remote(a1_out.at[i], a1_in.at[i], a1_send.at[i], a1_recv.at[i], near_x)

    def b1(i):
        return remote(b1_out.at[i], b1_in.at[i], b1_send.at[i], b1_recv.at[i], near_y)

    def a2(i):
        return remote(a2_out.at[i], a2_in.at[i], a2_send.at[i], a2_recv.at[i], near_y)

    def b2(i):
        return remote(b2_out.at[i], b2_in.at[i], b2_send.at[i], b2_recv.at[i], near_x)

    def to_z(r):
        return remote(z_out.at[r], z_in.at[r], z_send.at[r], z_recv.at[r], (y, x, c, (z + r) % 4))

    def piece(i, carry):
        s = (z + i + 1) % 4
        made = dot_nn(lhs[...], dj[:, pl.ds(pl.multiple_of(s * wide, third), wide)])
        grads[i, :, :wide] = made
        grads[i, :, wide:] = go[:, pl.ds(pl.multiple_of(s * third, third), third)].astype(F32)
        for b in range(2):
            a1_out[i, b] = grads[i, block(b, 1 - x), :two].astype(BF16)
            b1_out[i, b] = grads[i, block(1 - y, b), two:].astype(BF16)
        a1(i).start()
        b1(i).start()
        return carry

    lax.fori_loop(0, 4, piece, 0)

    def second(i):
        a1(i).wait_recv()
        a2_out[i] = (grads[i, block(1 - y, x), :two] + a1_in[i, 1 - y].astype(F32)).astype(BF16)
        a2(i).start()
        b1(i).wait_recv()
        b2_out[i] = (grads[i, block(y, 1 - x), two:] + b1_in[i, 1 - x].astype(F32)).astype(BF16)
        b2(i).start()
        grads[i, block(y, x), :two] = grads[i, block(y, x), :two] + a1_in[i, y].astype(F32)
        grads[i, block(y, x), two:] = grads[i, block(y, x), two:] + b1_in[i, x].astype(F32)

    def third_step(i):
        a2(i).wait_recv()
        b2(i).wait_recv()
        grads[i, block(y, x), :two] = grads[i, block(y, x), :two] + a2_in[i].astype(F32)
        grads[i, block(y, x), two:] = grads[i, block(y, x), two:] + b2_in[i].astype(F32)
        if i < 3:
            z_out[i + 1] = grads[i, block(y, x), :].astype(BF16)
            to_z(i + 1).start()

    step = own // 2
    fetches[0].wait()

    def away(i, carry):
        rows = pl.ds(pl.multiple_of(own + i * step, step), step)
        half_out[pl.ds(pl.multiple_of(i * step, step), step)] = dot_nt(dj[rows], weight[...]).astype(BF16)
        return carry

    lax.fori_loop(0, 2, away, 0)
    swap = remote(half_out, half_in, h_send.at[0], h_recv.at[0], pair)
    swap.start()
    second(0)
    for copy in fetches[1:]:
        copy.wait()
    sums[...] = small_in[...]
    swap.wait_recv()

    def home(i, totals):
        rows = pl.ds(pl.multiple_of(i * step, step), step)
        grad = dot_nt(dj[rows], weight[...]) + half_in[rows].astype(F32)
        standard = std[rows]
        inner = grad * gain[...]
        mean = jnp.mean(inner, axis=-1, keepdims=True)
        along = jnp.mean(inner * standard, axis=-1, keepdims=True)
        full = base[rows] + (inner - mean - standard * along) * inverse[rows]
        hide = masked[rows] > 0.0
        ready[rows] = jnp.where(hide, 0.0, full).astype(BF16)
        return (
            totals[0] + jnp.sum(grad * standard, axis=0, keepdims=True),
            totals[1] + jnp.sum(jnp.where(hide, full, 0.0), axis=0, keepdims=True),
        )

    zero = jnp.zeros((1, std.shape[1]), F32)
    gain_grad, embed_grad = lax.fori_loop(0, 2, home, (zero, zero))
    sums[0:1] = gain_grad
    sums[3:4] = embed_grad

    def columns(s):
        return pl.ds(pl.multiple_of(s * BLK, BLK), BLK)

    def stays(k):
        return jnp.logical_and(z == k, z // 2 == c)

    def ride(k):
        slot = 2 * (z % 2) + c
        return remote(ready.at[:, columns(k)], rows_out.at[slot], r_send.at[k], r_recv.at[slot], (y, x, z // 2, k))

    def ride_local(k):
        return pltpu.make_async_copy(ready.at[:, columns(k)], rows_out.at[2 * (z % 2) + c], local.at[3])

    for k in range(4):
        pl.when(stays(k))(lambda k=k: ride_local(k).start())
        pl.when(jnp.logical_not(stays(k)))(lambda k=k: ride(k).start())

    def share(h):
        peer = (pair, near_y, near_x)[h]
        return remote(sum_out.at[h], sum_in.at[h], s_send.at[h], s_recv.at[h], peer)

    def begin_share(h):
        sum_out[h] = sums[...]
        share(h).start()

    def end_share(h):
        share(h).wait_recv()
        sums[...] = sums[...] + sum_in[h]

    begin_share(0)
    second(1)
    third_step(0)
    end_share(0)
    begin_share(1)
    second(2)
    third_step(1)
    end_share(1)
    begin_share(2)
    second(3)
    third_step(2)
    end_share(2)
    sum_out[3] = sums[...]

    def deal(r):
        s = (z + r) % 4
        return remote(sum_out.at[3, :, columns(s)], share_in.at[r], p_send.at[r], p_recv.at[r], (y, x, c, s))

    for r in (1, 2, 3):
        deal(r).start()
    third_step(3)
    for r in (1, 2, 3):
        to_z(r).wait_recv()
    total = grads[3, block(y, x), :]
    for r in (1, 2, 3):
        total = total + z_in[r].astype(F32)
    grads[3, block(y, x), :] = total
    rows = BLK // 2

    def core_rows(core):
        return pl.ds(pl.multiple_of(BLK * (2 * y + x) + rows * core, rows), rows)

    core_out[...] = grads[3, core_rows(1 - c), :].astype(BF16)
    last = remote(core_out, core_in, c_send.at[0], c_recv.at[0], pair)
    last.start()
    kept_out[...] = grads[3, core_rows(c), :]
    result = sums[:, columns(z)]
    for r in (1, 2, 3):
        deal(r).wait_recv()
        result = result + share_in[r]
    small_out[...] = result
    last.wait_recv()
    landed_out[...] = core_in[...].astype(F32)

    last.wait_send()
    swap.wait_send()
    for i in range(4):
        for copy in (a1(i), b1(i), a2(i), b2(i)):
            copy.wait_send()
    for r in (1, 2, 3):
        to_z(r).wait_send()
        deal(r).wait_send()
    for h in range(3):
        share(h).wait_send()
    for k in range(4):
        pl.when(stays(k))(lambda k=k: ride_local(k).wait())
        pl.when(jnp.logical_not(stays(k)))(lambda k=k: ride(k).wait_send())
        from_self = jnp.logical_and(2 * c + k // 2 == z, c == k % 2)

        def landed(k=k):
            remote(ready.at[:, columns(k)], rows_out.at[k], r_send.at[k], r_recv.at[k], near_y).wait_recv()

        pl.when(jnp.logical_not(from_self))(landed)


def settle(dj, go, lhs, weight, std, base, inverse, masked, gain, small):
    own, features = std.shape
    cols4 = go.shape[1]
    quarter = cols4 // 4
    dma = pltpu.SemaphoreType.DMA
    anywhere = pl.BlockSpec(memory_space=pl.ANY)
    whole = pl.BlockSpec(memory_space=pltpu.VMEM)

    def low(*shape):
        return pltpu.VMEM(shape, BF16)

    def high(*shape):
        return pltpu.VMEM(shape, F32)

    return pl.pallas_call(
        settle_kernel,
        in_specs=[whole] * 3 + [anywhere] * 3 + [whole] * 4,
        out_specs=[whole, whole, anywhere, whole],
        out_shape=[
            jax.ShapeDtypeStruct((BLK // 2, cols4), F32),
            jax.ShapeDtypeStruct((BLK // 2, cols4), F32),
            jax.ShapeDtypeStruct((4, own, BLK), BF16),
            jax.ShapeDtypeStruct((8, BLK), F32),
        ],
        scratch_shapes=[
            low(*weight.shape), high(own, features), high(own, features), high(4, features, cols4),
            low(4, 2, BLK, 2 * quarter), low(4, 2, BLK, 2 * quarter), low(4, 2, BLK, 2 * quarter), low(4, 2, BLK, 2 * quarter),
            low(4, BLK, 2 * quarter), low(4, BLK, 2 * quarter), low(4, BLK, 2 * quarter), low(4, BLK, 2 * quarter),
            low(4, BLK, cols4), low(4, BLK, cols4),
            low(own, features), low(own, features), low(own, features),
            low(BLK // 2, cols4), low(BLK // 2, cols4),
            high(8, features), high(4, 8, features), high(3, 8, features), high(4, 8, BLK),
        ]
        + [dma((4,))] * 10
        + [dma((1,)), dma((1,)), dma((4,)), dma((4,)), dma((1,)), dma((1,)), dma((3,)), dma((3,)), dma((4,)), dma((4,)), dma((4,))],
        compiler_params=pltpu.CompilerParams(
            collective_id=3, has_side_effects=True, vmem_limit_bytes=56 * 1024 * 1024
        ),
        cost_estimate=pl.CostEstimate(flops=10**10, transcendentals=10**6, bytes_accessed=10**8),
        name="settle",
    )(dj, go, lhs, weight, std, base, inverse, masked, gain, small)


def tie(*values):
    return lax.optimization_barrier(values)


def norm_rows(resid):
    mean = jnp.mean(resid, axis=-1, keepdims=True)
    centered = resid - mean
    inverse = lax.rsqrt(jnp.mean(centered * centered, axis=-1, keepdims=True) + eps_norm)
    return (centered * inverse, inverse)


def norm_rows_back(grad, standardized, inverse, gain):
    gain_grad = jnp.sum(grad * standardized, axis=0)
    inner = grad * gain
    mean = jnp.mean(inner, axis=-1, keepdims=True)
    along = jnp.mean(inner * standardized, axis=-1, keepdims=True)
    return ((inner - mean - standardized * along) * inverse, gain_grad)


def cols(parts):
    return jnp.concatenate(parts, axis=1)


def rows_of(parts):
    return jnp.concatenate(parts, axis=0)


def token_parallel(
    tokens,
    cotangent,
    ratio,
    priority,
    frame_order,
    mask_embed,
    gains,
    qkv_space,
    out_space,
    qkv_time,
    out_time,
    w_in,
    w_out,
):
    scale = 1.0 / math.sqrt(HEAD_DIM)
    y, x, c, z = (lax.axis_index(name) for name in AXES)
    patches = tokens.shape[2]
    width = qkv_space.shape[0]
    frames_own = tokens.shape[0] * tokens.shape[1] // 4
    frames_all = frame_order.shape[1]
    own = frames_own * patches
    hidden_own = w_in.shape[1] // 2
    plane = 2 * y + x
    k_own = 2 * (z % 2) + c

    masked_here = (priority < ratio[:, None, None]).astype(jnp.int32).reshape(2, -1)
    info = cols([masked_here, frame_order])
    info = jnp.where(z // 2 == c, info, hop_c(info))
    info = lax.dynamic_index_in_dim(info, z % 2, 0, keepdims=False)
    masked = lax.dynamic_slice_in_dim(info, c * own, own, 0)[:, None] != 0
    order = info[2 * own :].reshape(2, 2, frames_own)
    order = jnp.where(y == 1, order[::-1], order)
    order = jnp.where(c == 1, order[:, ::-1], order).swapaxes(0, 1).reshape(frames_all)
    order = jnp.repeat(order, GROUP)
    patch = jnp.arange(frames_all * GROUP) % GROUP
    visible = (order[:, None] <= order[None, :]) & (patch[:, None] == patch[None, :])
    bias = jnp.where(visible, 0.0, -1e30).astype(F32)

    half = qkv_space.shape[2] // 2
    sp_own = cols(
        [
            lax.dynamic_slice_in_dim(qkv_space, c * half, half, 2).reshape(width, -1),
            lax.dynamic_slice_in_dim(out_space, c * half, half, 0).T,
        ]
    )
    vectors = rows_of([mask_embed[None], gains, jnp.zeros((4, BLK), BF16)])
    head = (2 * y + c) * HEAD_DIM
    ti_own = cols(
        [
            lax.dynamic_slice_in_dim(qkv_time, head, HEAD_DIM, 2).reshape(width, -1),
            lax.dynamic_slice_in_dim(out_time, head, HEAD_DIM, 0).T,
        ]
    )
    arrived, vectors, ws_qkv, ws_out, wt_all = arrive(tokens.reshape(4, own, BLK), vectors, sp_own, ti_own)
    wt_all = wt_all.reshape(width, 4, 4, HEAD_DIM)
    wt_qkv = jnp.swapaxes(wt_all[:, :, :3], 1, 2).reshape(width, 12 * HEAD_DIM)
    wt_out = wt_all[:, :, 3].reshape(width, 4 * HEAD_DIM)
    source = arrived.astype(F32)
    embed_row = vectors[:1].astype(F32)
    gain = [vectors[1 + i : 2 + i].astype(F32) for i in range(3)]

    ff_in = lax.dynamic_slice(w_in, (plane * BLK, c * hidden_own), (BLK, hidden_own))
    arrived, ff_in, w_out = tie(arrived, ff_in, w_out)
    out_size = hidden_own // 4
    out_slice = lax.dynamic_slice_in_dim(w_out, c * hidden_own + plane * out_size, out_size, 0)
    out_far = [hop_z(out_slice, -r) for r in (1, 2, 3)]
    wf_in = lax.all_gather(ff_in, ("mp", "tm", "x")).reshape(4, width, hidden_own)

    def pair_gather(v):
        return rows_of([v, hop_c(v)])

    def pair_scatter(v):
        return v[:own] + hop_c(v[own:].astype(BF16)).astype(F32)

    heads_s = 4 * half // HEAD_DIM
    frames_pair = 2 * frames_own
    resid0 = jnp.where(masked, embed_row, source)
    std0, inv0 = norm_rows(resid0)
    normed0 = pair_gather((std0 * gain[0]).astype(BF16))
    joined0 = dot_nn(normed0, ws_qkv).astype(BF16)
    mixed0, total0 = space_attend(joined0, frames_pair, patches, heads_s, scale)
    mixed0, out_far = tie(mixed0, out_far)
    resid1 = resid0 + pair_scatter(dot_nt(mixed0, ws_out))
    std1, inv1 = norm_rows(resid1)
    normed1, joined1, mixed1, total1, delta, upstream, wf_out = time_call(
        False,
        (std1 * gain[1]).astype(BF16).reshape(frames_own, patches, width),
        cotangent.reshape(4, own, BLK),
        [jnp.stack(out_far), w_out],
        wt_qkv,
        wt_out,
        bias,
        scale,
    )
    normed1 = normed1.reshape(4 * own, width)
    mixed1 = mixed1.reshape(4 * own, -1)
    g_w_in, g_w_out, grad2, grad2_low, block_rows, gain_grad2 = feed(
        resid1, delta.reshape(own, width), upstream, masked.astype(F32), gain[2], wf_in, wf_out
    )

    def line_scatter(parts):
        return lax.psum_scatter(parts, "mp", scatter_dimension=0)

    def plane_scatter(v):
        return lax.psum_scatter(v, ("tm", "x"), scatter_dimension=0, tiled=True).astype(F32)

    def send_x(lhs, rhs):
        there = jnp.where(x == 0, cols([lhs[:, BLK : 2 * BLK], lhs[:, 3 * BLK :]]), cols([lhs[:, :BLK], lhs[:, 2 * BLK : 3 * BLK]]))
        return hop_x(dot_tn(there, rhs).astype(BF16))

    def keep_x(lhs, rhs, landed):
        here = jnp.where(x == 1, cols([lhs[:, BLK : 2 * BLK], lhs[:, 3 * BLK :]]), cols([lhs[:, :BLK], lhs[:, 2 * BLK : 3 * BLK]]))
        return dot_tn(here, rhs) + landed.astype(F32)

    def mine_y(v):
        return jnp.where(y == 0, v[:BLK], v[BLK:])

    def other_y(v):
        return jnp.where(y == 1, v[:BLK], v[BLK:])

    def reduce_z(pieces):
        total = pieces[0]
        for r in (1, 2, 3):
            total = total + hop_z(pieces[r].astype(BF16), r).astype(F32)
        return total

    def swap_c(total):
        rows = BLK // 2
        kept = lax.dynamic_slice_in_dim(total, c * rows, rows, 0)
        sent = hop_c(lax.dynamic_slice_in_dim(total, (1 - c) * rows, rows, 0).astype(BF16))
        return (kept, sent.astype(F32))

    def by_core(kept, landed):
        return jnp.where(c == 0, jnp.concatenate([kept, landed], -1), jnp.concatenate([landed, kept], -1))

    w_in_part = line_scatter(g_w_in)
    gb2, djoined1, part1, w_out_part, block_out = time_call(
        True,
        grad2_low.reshape(frames_own, patches, width),
        block_rows,
        [joined1, total1, g_w_out],
        wt_qkv,
        wt_out,
        bias,
        scale,
    )
    block_out = block_out.reshape(tokens.shape)
    gb2 = gb2.reshape(4 * own, width)
    djoined1 = djoined1.reshape(4 * own, -1)
    part1 = part1.reshape(own, width)
    back1, gain_grad1 = norm_rows_back(part1, std1, inv1, gain[1])
    grad1 = grad2 + back1
    w_out_part, w_in_part = tie(w_out_part, w_in_part)
    gb1 = pair_gather(grad1.astype(BF16))
    w_out_part = lax.psum_scatter(w_out_part, "tm", scatter_dimension=0)
    g_w_out = lax.psum_scatter(w_out_part, "mp", scatter_dimension=0).astype(F32)
    t_out_x = send_x(gb2, mixed1)
    t_qkv_x = send_x(normed1, djoined1)
    dmixed0 = dot_nn(gb1, ws_out).astype(BF16)
    g_w_in = plane_scatter(w_in_part)
    go = dot_tn(gb1, mixed0).astype(BF16)
    djoined0 = space_attend_back(joined0, dmixed0, total0, frames_pair, patches, heads_s, scale)
    djoined0, t_out_x, t_qkv_x, go = tie(djoined0, t_out_x, t_qkv_x, go)
    g_t_out = keep_x(gb2, mixed1, t_out_x)
    g_t_qkv = keep_x(normed1, djoined1, t_qkv_x)
    z_at = [(z + r) % 4 for r in range(4)]
    span = 4 * HEAD_DIM
    g_time = reduce_z(
        [
            cols(
                [lax.dynamic_slice_in_dim(g_t_qkv, j * span + s * HEAD_DIM, HEAD_DIM, 1) for j in range(3)]
                + [lax.dynamic_slice_in_dim(g_t_out, s * HEAD_DIM, HEAD_DIM, 1)]
            )
            for s in z_at
        ]
    )
    small = rows_of([jnp.zeros((1, width), F32), gain_grad1[None], gain_grad2, jnp.zeros((5, width), F32)])
    kept, landed, grad_tokens, small = settle(
        djoined0, go, normed0.T, ws_qkv, std0, grad1, inv0, masked.astype(F32), gain[0], small
    )
    grad_tokens = grad_tokens.reshape(tokens.shape).astype(F32)

    rows = BLK // 2
    grad_qkv_space = by_core(
        kept[:, : 3 * half].reshape(rows, 3, half), landed[:, : 3 * half].reshape(rows, 3, half)
    )
    grad_out_space = by_core(kept[:, 3 * half :], landed[:, 3 * half :]).T
    kept, landed = swap_c(cols([g_w_in, g_w_out]))
    grad_w_in = by_core(kept[:, :hidden_own], landed[:, :hidden_own])
    grad_w_out = by_core(kept[:, hidden_own:], landed[:, hidden_own:]).T
    both = cols([mine_y(g_time), hop_y(other_y(g_time).astype(BF16)).astype(F32)])
    kept, landed = swap_c(both)
    quad = jnp.stack([kept, landed], 1).reshape(rows, 2, 2, 4, HEAD_DIM)
    quad = jnp.where(c == 1, quad[:, ::-1], quad)
    quad = jnp.where(y == 1, quad[:, :, ::-1], quad)
    quad = jnp.transpose(quad, (0, 3, 2, 1, 4)).reshape(rows, 4, 4 * HEAD_DIM)
    grad_qkv_time = quad[:, :3]
    grad_out_time = quad[:, 3].T
    return (
        block_out,
        grad_tokens,
        small[3],
        small[:3],
        grad_qkv_space,
        grad_out_space,
        grad_qkv_time,
        grad_out_time,
        grad_w_in,
        grad_w_out,
    )


def solution(mesh):
    sizes = (mesh.shape["tm"], mesh.shape["clip"], mesh.shape["mp"])
    if sizes == (2, 4, 4):
        mesh = jax.sharding.Mesh(mesh.devices.reshape(2, 2, 2, 4), AXES)
        step, clip = token_parallel, ("x", "c")
    else:
        step, clip = shards, ("clip",)
    return jax.shard_map(
        step,
        mesh=mesh,
        in_specs=(
            P(clip, "tm", None, "mp"),
            P(clip, "tm", None, "mp"),
            P(clip),
            P(clip, "tm", None),
            P(clip, None),
            P("mp"),
            P(None, "mp"),
            P(None, None, "mp"),
            P("mp", None),
            P(None, None, "mp"),
            P("mp", None),
            P(None, "mp"),
            P("mp", None),
        ),
        out_specs=(
            P(clip, "tm", None, "mp"),
            P(clip, "tm", None, "mp"),
            P("mp"),
            P(None, "mp"),
            P(("tm",) + clip, None, "mp"),
            P("mp", ("tm",) + clip),
            P(("tm",) + clip, None, "mp"),
            P("mp", ("tm",) + clip),
            P(("tm",) + clip, "mp"),
            P("mp", ("tm",) + clip),
        ),
        check_vma=False,
    )
```

```python
import functools
import math

import jax
import jax.numpy as jnp
from jax import lax
from jax.experimental import pallas as pl
from jax.experimental.pallas import tpu as pltpu
from jax.sharding import PartitionSpec as P

HEAD_DIM = 64
MICRO = 2


eps_norm = 1e-05


def gelu_tanh(values):
    return jax.nn.gelu(values, approximate=True)


def norm_forward_pass(residual_stream, gain_coefficients, complete_width):
    reduced_totals = lax.psum(
        (jnp.sum(residual_stream, axis=-1), jnp.sum(residual_stream * residual_stream, axis=-1)),
        "mp",
    )
    centered_rows = reduced_totals[0] / complete_width
    spread = reduced_totals[1] / complete_width - centered_rows * centered_rows
    inverse_scale = lax.rsqrt(spread + eps_norm)
    standardized_rows = (residual_stream - centered_rows[:, None]) * inverse_scale[:, None]
    shard_rows = (standardized_rows * gain_coefficients).astype(jnp.bfloat16)
    normalized_rows = lax.all_gather(shard_rows, "mp", axis=1, tiled=True)
    return (normalized_rows, standardized_rows, inverse_scale)


def norm_reverse_pass(
    normalized_gradient, standardized_rows, inverse_scale, gain_coefficients, complete_width
):
    gain_gradient = jnp.sum(normalized_gradient * standardized_rows, axis=0)
    standardized_gradient = normalized_gradient * gain_coefficients
    reduced_totals = lax.psum(
        (
            jnp.sum(standardized_gradient, axis=-1),
            jnp.sum(standardized_gradient * standardized_rows, axis=-1),
        ),
        "mp",
    )
    grad_resid = (
        standardized_gradient
        - reduced_totals[0][:, None] / complete_width
        - standardized_rows * (reduced_totals[1][:, None] / complete_width)
    ) * inverse_scale[:, None]
    return (grad_resid, gain_gradient)


def sum_features(grad_full):
    return lax.psum_scatter(
        grad_full.astype(jnp.bfloat16), "mp", scatter_dimension=1, tiled=True
    ).astype(jnp.float32)


def branch_out(hidden, weight):
    partial_rows = jnp.dot(hidden, weight, preferred_element_type=jnp.float32)
    return lax.psum_scatter(partial_rows, "mp", scatter_dimension=1, tiled=True)


def branch_back(grad_resid, hidden, weight):
    grad_rows = lax.all_gather(grad_resid.astype(jnp.bfloat16), "mp", axis=1, tiled=True)
    weight_grad = jnp.einsum("rk,rd->kd", hidden, grad_rows, preferred_element_type=jnp.float32)
    grad_hidden = jnp.einsum("rd,kd->rk", grad_rows, weight, preferred_element_type=jnp.float32)
    return (grad_hidden, weight_grad)


def qkv_back(normalized_rows, grad_joined, weight):
    weight_grad = jnp.einsum(
        "rd,trk->dtk", normalized_rows, grad_joined, preferred_element_type=jnp.float32
    )
    grad_full = jnp.einsum("trk,dtk->rd", grad_joined, weight, preferred_element_type=jnp.float32)
    return (weight_grad, sum_features(grad_full))


def reduce_grads(local_grads, small_grads):
    reduced = (
        lax.psum_scatter(local_grads[0], ("tm", "clip"), scatter_dimension=0, tiled=True),
        lax.psum_scatter(local_grads[1], ("tm", "clip"), scatter_dimension=1, tiled=True),
        lax.psum_scatter(local_grads[2], ("tm", "clip"), scatter_dimension=0, tiled=True),
        lax.psum_scatter(local_grads[3], ("tm", "clip"), scatter_dimension=1, tiled=True),
        lax.psum_scatter(local_grads[4], ("tm", "clip"), scatter_dimension=0, tiled=True),
        lax.psum_scatter(local_grads[5], ("tm", "clip"), scatter_dimension=1, tiled=True),
    )
    reduced_small = lax.psum((small_grads[0], small_grads[1]), ("tm", "clip"))
    return (reduced, reduced_small)


def space_forward(normalized_rows, weight, frame_count, patches, heads_local, scale):
    joined = jnp.einsum(
        "rd,dtk->trk", normalized_rows, weight, preferred_element_type=jnp.float32
    ).astype(jnp.bfloat16)
    shape_heads = (frame_count, patches, heads_local, HEAD_DIM)
    scores = (
        jnp.einsum(
            "bshd,bthd->bhst",
            joined[0].reshape(shape_heads),
            joined[1].reshape(shape_heads),
            preferred_element_type=jnp.float32,
        )
        * scale
    )
    highest = jnp.max(scores, axis=-1, keepdims=True)
    exponent = jnp.exp(scores - highest)
    reduced_totals = jnp.sum(exponent, axis=-1, keepdims=True)
    log_total = highest + jnp.log(reduced_totals)
    attention = (exponent / reduced_totals).astype(jnp.bfloat16)
    mixed = jnp.einsum(
        "bhst,bthd->bshd",
        attention,
        joined[2].reshape(shape_heads),
        preferred_element_type=jnp.float32,
    )
    return (
        joined,
        log_total,
        mixed.astype(jnp.bfloat16).reshape(frame_count * patches, heads_local * HEAD_DIM),
    )


def space_backward(grad_mixed, joined, log_total, frame_count, patches, heads_local, scale):
    shape_heads = (frame_count, patches, heads_local, HEAD_DIM)
    queries = joined[0].reshape(shape_heads)
    key_rows = joined[1].reshape(shape_heads)
    values = joined[2].reshape(shape_heads)
    grad_out = grad_mixed.reshape(shape_heads)
    scores = (
        jnp.einsum("bshd,bthd->bhst", queries, key_rows, preferred_element_type=jnp.float32) * scale
    )
    attention = jnp.exp(scores - log_total)
    grad_values = jnp.einsum(
        "bhst,bshd->bthd",
        attention.astype(jnp.bfloat16),
        grad_out,
        preferred_element_type=jnp.float32,
    )
    grad_att = jnp.einsum("bshd,bthd->bhst", grad_out, values, preferred_element_type=jnp.float32)
    grad_scores = (
        attention * (grad_att - jnp.sum(attention * grad_att, axis=-1, keepdims=True))
    ).astype(jnp.bfloat16)
    grad_queries = (
        jnp.einsum("bhst,bthd->bshd", grad_scores, key_rows, preferred_element_type=jnp.float32)
        * scale
    )
    grad_keys = (
        jnp.einsum("bhst,bshd->bthd", grad_scores, queries, preferred_element_type=jnp.float32)
        * scale
    )
    row_count = frame_count * patches
    stacked = jnp.stack(
        [
            grad_queries.reshape(row_count, -1),
            grad_keys.reshape(row_count, -1),
            grad_values.reshape(row_count, -1),
        ]
    )
    return stacked.astype(jnp.bfloat16)


def time_scores(queries, keys_all, visible, scale):
    scores = (
        jnp.einsum("cfshd,cgshd->chfgs", queries, keys_all, preferred_element_type=jnp.float32)
        * scale
    )
    return jnp.where(visible, scores, -1e30)


def time_forward(queries, keys_all, values_all, visible, scale):
    scores = time_scores(queries, keys_all, visible, scale)
    highest = jnp.max(scores, axis=3, keepdims=True)
    exponent = jnp.exp(scores - highest)
    reduced_totals = jnp.sum(exponent, axis=3, keepdims=True)
    log_total = highest + jnp.log(reduced_totals)
    attention = (exponent / reduced_totals).astype(jnp.bfloat16)
    mixed = jnp.einsum(
        "chfgs,cgshd->cfshd", attention, values_all, preferred_element_type=jnp.float32
    )
    return (log_total, mixed.astype(jnp.bfloat16))


def time_backward(grad_mixed, queries, keys_all, values_all, visible, log_total, scale):
    grad_out = grad_mixed.reshape(queries.shape)
    scores = time_scores(queries, keys_all, visible, scale)
    attention = jnp.exp(scores - log_total)
    grad_values = jnp.einsum(
        "chfgs,cfshd->cgshd",
        attention.astype(jnp.bfloat16),
        grad_out,
        preferred_element_type=jnp.float32,
    )
    grad_att = jnp.einsum(
        "cfshd,cgshd->chfgs", grad_out, values_all, preferred_element_type=jnp.float32
    )
    grad_scores = (
        attention * (grad_att - jnp.sum(attention * grad_att, axis=3, keepdims=True))
    ).astype(jnp.bfloat16)
    grad_queries = (
        jnp.einsum("chfgs,cgshd->cfshd", grad_scores, keys_all, preferred_element_type=jnp.float32)
        * scale
    )
    grad_keys = (
        jnp.einsum("chfgs,cfshd->cgshd", grad_scores, queries, preferred_element_type=jnp.float32)
        * scale
    )
    return (grad_queries, grad_keys, grad_values)


def shards(
    tokens,
    cotangent,
    ratio,
    priority,
    frame_order,
    mask_embed,
    gains,
    qkv_space,
    out_space,
    qkv_time,
    out_time,
    w_in,
    w_out,
):
    scale = 1.0 / math.sqrt(HEAD_DIM)
    clips_local = tokens.shape[0] // MICRO
    frames_local = tokens.shape[1]
    patches = tokens.shape[2]
    cols_local = tokens.shape[3]
    frames_all = frame_order.shape[1]
    hidden_width = qkv_space.shape[0]
    joined_local = qkv_space.shape[2]
    heads_local = joined_local // HEAD_DIM
    row_count = clips_local * frames_local * patches
    gain_broadcast = gains.astype(jnp.float32)
    embed_row = mask_embed.astype(jnp.float32)
    first_frame = lax.axis_index("tm") * frames_local
    shape_local = (clips_local, frames_local, patches, joined_local)
    shape_heads = (clips_local, frames_local, patches, heads_local, HEAD_DIM)
    shape_all = (clips_local, frames_all, patches, heads_local, HEAD_DIM)
    outputs = []
    input_grads = []
    weight_total = None
    small_total = None
    for batch_index in range(MICRO):
        lower = batch_index * clips_local
        upper = lower + clips_local
        source = tokens[lower:upper].reshape(row_count, cols_local).astype(jnp.float32)
        upstream = cotangent[lower:upper].reshape(row_count, cols_local).astype(jnp.float32)
        masked = (priority[lower:upper] < ratio[lower:upper][:, None, None]).reshape(row_count)
        order_rows = frame_order[lower:upper]
        residual_stream0 = jnp.where(masked[:, None], embed_row[None, :], source)
        normalized_rows0, standardized_rows0, inverse_deviation0 = norm_forward_pass(
            residual_stream0, gain_broadcast[0], hidden_width
        )
        joined0, total0, mixed0 = space_forward(
            normalized_rows0, qkv_space, clips_local * frames_local, patches, heads_local, scale
        )
        residual_stream1 = residual_stream0 + branch_out(mixed0, out_space)
        normalized_rows1, standardized_rows1, inverse_deviation1 = norm_forward_pass(
            residual_stream1, gain_broadcast[1], hidden_width
        )
        joined1 = jnp.einsum(
            "rd,dtk->trk", normalized_rows1, qkv_time, preferred_element_type=jnp.float32
        ).astype(jnp.bfloat16)
        queries_local = joined1[0].reshape(shape_local)
        keys_local = joined1[1].reshape(shape_local)
        values_local = joined1[2].reshape(shape_local)
        keys_all, values_all = (
            lax.all_gather(keys_local, "tm", axis=1, tiled=True),
            lax.all_gather(values_local, "tm", axis=1, tiled=True),
        )
        query_order = lax.dynamic_slice_in_dim(order_rows, first_frame, frames_local, axis=1)
        time_visible = (order_rows[:, None, :] <= query_order[:, :, None])[:, None, :, :, None]
        time_q = queries_local.reshape(shape_heads)
        time_k = keys_all.reshape(shape_all)
        time_v = values_all.reshape(shape_all)
        total1, mixed_frames = time_forward(time_q, time_k, time_v, time_visible, scale)
        mixed1 = mixed_frames.reshape(row_count, joined_local)
        residual_stream2 = residual_stream1 + branch_out(mixed1, out_time)
        normalized_rows2, standardized_rows2, inverse_deviation2 = norm_forward_pass(
            residual_stream2, gain_broadcast[2], hidden_width
        )
        projected = jnp.dot(normalized_rows2, w_in, preferred_element_type=jnp.float32)
        activated, gelu_pull = jax.vjp(gelu_tanh, projected)
        hidden = activated.astype(jnp.bfloat16)
        resid3 = residual_stream2 + branch_out(hidden, w_out)
        outputs.append(
            resid3.astype(jnp.bfloat16).reshape(clips_local, frames_local, patches, cols_local)
        )
        grad3 = jnp.where(masked[:, None], upstream, 0.0)
        grad_hidden, grad_w_out = branch_back(grad3, hidden, w_out)
        grad_inner = gelu_pull(grad_hidden)[0].astype(jnp.bfloat16)
        grad_w_in = jnp.einsum(
            "rd,rk->dk", normalized_rows2, grad_inner, preferred_element_type=jnp.float32
        )
        normalized_gradient2 = sum_features(
            jnp.einsum("rk,dk->rd", grad_inner, w_in, preferred_element_type=jnp.float32)
        )
        backward_third, gain_gradient2 = norm_reverse_pass(
            normalized_gradient2,
            standardized_rows2,
            inverse_deviation2,
            gain_broadcast[2],
            hidden_width,
        )
        grad2 = grad3 + backward_third
        grad_mixed1, grad_out_time = branch_back(grad2, mixed1, out_time)
        grad_mixed_low = grad_mixed1.astype(jnp.bfloat16).reshape(shape_local)
        grad_queries, grad_keys, grad_values = time_backward(
            grad_mixed_low, time_q, time_k, time_v, time_visible, total1, scale
        )
        key_part, value_part = (
            lax.psum_scatter(
                grad_keys.reshape(clips_local, frames_all, patches, joined_local).astype(
                    jnp.bfloat16
                ),
                "tm",
                scatter_dimension=1,
                tiled=True,
            ).astype(jnp.float32),
            lax.psum_scatter(
                grad_values.reshape(clips_local, frames_all, patches, joined_local).astype(
                    jnp.bfloat16
                ),
                "tm",
                scatter_dimension=1,
                tiled=True,
            ).astype(jnp.float32),
        )
        grad_joined1 = jnp.stack(
            [
                grad_queries.reshape(row_count, joined_local),
                key_part.reshape(row_count, joined_local),
                value_part.reshape(row_count, joined_local),
            ]
        ).astype(jnp.bfloat16)
        grad_qkv_time, normalized_gradient1 = qkv_back(normalized_rows1, grad_joined1, qkv_time)
        backward_second, gain_gradient1 = norm_reverse_pass(
            normalized_gradient1,
            standardized_rows1,
            inverse_deviation1,
            gain_broadcast[1],
            hidden_width,
        )
        grad1 = grad2 + backward_second
        grad_mixed0, grad_out_space = branch_back(grad1, mixed0, out_space)
        grad_joined0 = space_backward(
            grad_mixed0.astype(jnp.bfloat16),
            joined0,
            total0,
            clips_local * frames_local,
            patches,
            heads_local,
            scale,
        )
        grad_qkv_space, normalized_gradient0 = qkv_back(normalized_rows0, grad_joined0, qkv_space)
        backward_first, gain_gradient0 = norm_reverse_pass(
            normalized_gradient0,
            standardized_rows0,
            inverse_deviation0,
            gain_broadcast[0],
            hidden_width,
        )
        grad0 = grad1 + backward_first
        input_grads.append(
            jnp.where(masked[:, None], 0.0, grad0).reshape(
                clips_local, frames_local, patches, cols_local
            )
        )
        grad_embed = jnp.sum(jnp.where(masked[:, None], grad0, 0.0), axis=0)
        gain_grads = jnp.stack([gain_gradient0, gain_gradient1, gain_gradient2])
        local_grads = (
            grad_qkv_space,
            grad_out_space,
            grad_qkv_time,
            grad_out_time,
            grad_w_in,
            grad_w_out,
        )
        small_grads = (gain_grads, grad_embed)
        reduced, reduced_small = reduce_grads(local_grads, small_grads)
        if weight_total is None:
            weight_total = reduced
            small_total = reduced_small
        else:
            weight_total = tuple((total + grad for total, grad in zip(weight_total, reduced)))
            small_total = tuple((total + grad for total, grad in zip(small_total, reduced_small)))
    return (
        jnp.concatenate(outputs, axis=0),
        jnp.concatenate(input_grads, axis=0),
        small_total[1],
        small_total[0],
        weight_total[0],
        weight_total[1],
        weight_total[2],
        weight_total[3],
        weight_total[4],
        weight_total[5],
    )


AXES = ("tm", "x", "c", "mp")
F32 = jnp.float32
BF16 = jnp.bfloat16
BLK = 256
MESH = pl.DeviceIdType.MESH


def device_pairs(move):
    pairs = []
    for y in range(2):
        for x in range(2):
            for c in range(2):
                for z in range(4):
                    there = move(y, x, c, z)
                    pairs.append(tuple(((q[0] * 2 + q[1]) * 2 + q[2]) * 4 + q[3] for q in ((y, x, c, z), there)))
    return pairs


def hop_y(v):
    return lax.ppermute(v, AXES, device_pairs(lambda y, x, c, z: (1 - y, x, c, z)))


def hop_x(v):
    return lax.ppermute(v, AXES, device_pairs(lambda y, x, c, z: (y, 1 - x, c, z)))


def hop_c(v):
    return lax.ppermute(v, AXES, device_pairs(lambda y, x, c, z: (y, x, 1 - c, z)))


def hop_z(v, shift):
    return lax.ppermute(v, AXES, device_pairs(lambda y, x, c, z: (y, x, c, (z + shift) % 4)))


def spread_pairs(r):
    def move(y, x, c, z):
        k = z ^ r
        return (y, x, k & 1, 2 * c + (k >> 1))

    return device_pairs(move)


def dot_nn(a, b):
    return lax.dot_general(a, b, (((1,), (0,)), ((), ())), preferred_element_type=F32)


def dot_nt(a, b):
    return lax.dot_general(a, b, (((1,), (1,)), ((), ())), preferred_element_type=F32)


def dot_tn(a, b):
    return lax.dot_general(a, b, (((0,), (0,)), ((), ())), preferred_element_type=F32)


def attend_pair(q, k, v, bias, scale):
    mixed, totals = [], []
    for i in range(2):
        mine = slice(i * HEAD_DIM, (i + 1) * HEAD_DIM)
        scores = dot_nt(k[:, mine], q[:, mine]) * scale
        if bias is not None:
            scores = scores + bias
        highest = jnp.max(scores, axis=0, keepdims=True)
        exponent = jnp.exp(scores - highest)
        total = jnp.sum(exponent, axis=0, keepdims=True)
        totals.append(highest + jnp.log(total))
        mixed.append(dot_tn(v[:, mine], exponent.astype(BF16)) * (1.0 / total))
    return (jnp.concatenate(mixed, axis=0).T, totals)


def attend_pair_back(q, k, v, g, totals, bias, scale):
    grads = ([], [], [])
    for i in range(2):
        mine = slice(i * HEAD_DIM, (i + 1) * HEAD_DIM)
        scores = dot_nt(k[:, mine], q[:, mine]) * scale
        if bias is not None:
            scores = scores + bias
        p = jnp.exp(scores - totals[i])
        dp = dot_nt(v[:, mine], g[:, mine])
        ds = (p * (dp - jnp.sum(p * dp, axis=0, keepdims=True))).astype(BF16)
        grads[0].append(dot_tn(k[:, mine], ds) * scale)
        grads[1].append(dot_nn(ds, q[:, mine]) * scale)
        grads[2].append(dot_nn(p.astype(BF16), g[:, mine]))
    return (
        jnp.concatenate(grads[0], axis=0).T,
        jnp.concatenate(grads[1], axis=1),
        jnp.concatenate(grads[2], axis=1),
    )


PAIR = 2 * HEAD_DIM


def space_attend_back_kernel(scale, qkv_ref, grad_ref, total_ref, out_ref):
    for i in range(grad_ref.shape[1] // PAIR):
        q, k, v = (qkv_ref[:, (3 * i + part) * PAIR : (3 * i + part + 1) * PAIR] for part in range(3))
        totals = [total_ref[0, 2 * i + h : 2 * i + h + 1, :] for h in range(2)]
        grads = attend_pair_back(q, k, v, grad_ref[:, i * PAIR : (i + 1) * PAIR], totals, None, scale)
        for part in range(3):
            out_ref[:, (3 * i + part) * PAIR : (3 * i + part + 1) * PAIR] = grads[part].astype(BF16)


def attention_cost(groups, rows, heads, products):
    return pl.CostEstimate(
        flops=8 * products * groups * heads * rows * rows * HEAD_DIM,
        transcendentals=groups * heads * rows * rows,
        bytes_accessed=2 * groups * rows * heads * HEAD_DIM * 2 * products,
    )


def space_attend_back(qkv, grad, total, frames, patches, heads, scale):
    width = heads * HEAD_DIM
    return pl.pallas_call(
        functools.partial(space_attend_back_kernel, scale),
        grid=(frames,),
        in_specs=[
            pl.BlockSpec((patches, 3 * width), lambda i: (i, 0)),
            pl.BlockSpec((patches, width), lambda i: (i, 0)),
            pl.BlockSpec((1, heads, patches), lambda i: (i, 0, 0)),
        ],
        out_specs=pl.BlockSpec((patches, 3 * width), lambda i: (i, 0)),
        out_shape=jax.ShapeDtypeStruct((frames * patches, 3 * width), BF16),
        cost_estimate=attention_cost(frames, patches, heads, 5),
        name="space_attend_back",
    )(qkv, grad, total)


def enter_kernel(
    scale,
    tok, vec, qkv_hbm, out_hbm, later, feed_hbm, masked,
    wq_out, wo_out, wt, wf, joined_out, turned_out, std_out,
    mixed, total_out, inverse, resid, std_next, inverse_next, low_next, vec_out,
    rows_in, vec_in, wq, wo, normed, joined, turned, std, base, part, part_out, part_in,
    z_send, z_recv, y_send, y_recv, x_send, x_recv, p_send, p_recv, q_send, q_recv,
    t_send, t_recv, v_send, v_recv, u_send, u_recv, w_send, w_recv,
    f_send, f_recv, g_send, g_recv, n_send, n_recv, local, saved,
):
    y, x, c, z = (lax.axis_index(name) for name in AXES)
    half = wo.shape[0] // 4
    wide = 3 * half
    span = wt.shape[1] // 4
    size = wf.shape[1] // 4
    own = rows_in.shape[0]
    near_y, near_x, pair = (1 - y, x, c, z), (y, 1 - x, c, z), (y, x, 1 - c, z)
    right_z, left_z = (y, x, c, (z + 1) % 4), (y, x, c, (z + 3) % 4)

    def at(i, length):
        return pl.ds(pl.multiple_of(i * length, length), length)

    def remote(src, dst, send, recv, peer):
        return pltpu.make_async_remote_copy(
            src_ref=src, dst_ref=dst, send_sem=send, recv_sem=recv, device_id=peer, device_id_type=MESH
        )

    def start(all_copies):
        for copy in all_copies:
            copy.start()

    def landed(all_copies):
        for copy in all_copies:
            copy.wait_recv()

    def sent(all_copies):
        for copy in all_copies:
            copy.wait_send()

    core = at(c, half)
    keep = [
        pltpu.make_async_copy(
            qkv_hbm.at[j, :, core], wq.at[:, pl.ds(pl.multiple_of(z * wide + j * half, half), half)], local.at[j]
        )
        for j in range(3)
    ] + [pltpu.make_async_copy(out_hbm.at[core], wo.at[at(z, half)], local.at[3])]
    keep_later = [
        pltpu.make_async_copy(later, wt.at[:, at(z, span)], local.at[4]),
        pltpu.make_async_copy(feed_hbm.at[at(c, 4 * size)], wf.at[z], local.at[5]),
    ]
    start(keep + keep_later)

    barrier = pltpu.get_barrier_semaphore()
    for dc in range(2):
        for dz in range(4):
            if dc or dz:
                peer = (y, x, (c + dc) % 2, (z + dz) % 4)
                pl.semaphore_signal(barrier, inc=1, device_id=peer, device_id_type=MESH)
    for peer in (near_y, near_x):
        pl.semaphore_signal(barrier, inc=1, device_id=peer, device_id_type=MESH)
    pl.semaphore_wait(barrier, 9)

    def spot(dy, dx):
        return 2 * ((y + dy) % 2) + (x + dx) % 2

    def piece(dy, dx, r, split=False):
        s = (z + r) % 4
        rows = at(spot(dy, dx), BLK)
        first = pl.multiple_of(s * wide, half)
        out = wo.at[at(s, half), at(spot(dy, dx), BLK)]
        if split:
            last = pl.multiple_of(s * wide + 2 * half, half)
            return (wq.at[rows, pl.ds(first, 2 * half)], wq.at[rows, pl.ds(last, half)], out)
        return (wq.at[rows, pl.ds(first, wide)], out)

    def time_piece(dx, r):
        return wt.at[at((x + dx) % 2, 2 * BLK), at((z + r) % 4, span)]

    def feed_piece(dy, r):
        return wf.at[(z + r) % 4, at(spot(dy, 0), size)]

    def copies(parts, send, recv, peer):
        return [remote(ref, ref, send.at[i], recv.at[i], peer) for i, ref in enumerate(parts)]

    def leg(right, step):
        if right:
            return (0 if step == 0 else 4 - step), right_z, 3 - step
        return step, left_z, step + 1

    def z_copies(right, step):
        r, peer, lands = leg(right, step)
        return copies(piece(0, 0, r), z_send.at[int(right), step], z_recv.at[lands], peer)

    def time_z(right, step):
        r, peer, lands = leg(right, step)
        source = later.at[at(x, 2 * BLK)] if step == 0 else time_piece(0, r)
        return [remote(source, time_piece(0, r), u_send.at[int(right), step], u_recv.at[lands], peer)]

    def feed_z(right, step):
        r, peer, lands = leg(right, step)
        source = feed_hbm.at[at(4 * c + spot(0, 0), size)] if step == 0 else feed_piece(0, r)
        return [remote(source, feed_piece(0, r), f_send.at[int(right), step], f_recv.at[lands], peer)]

    def y_copies(r, dy=0):
        return copies(piece(dy, 0, r), y_send.at[r], y_recv.at[r], near_y)

    def x_copies(r, dx=0):
        return copies(piece(0, dx, r), x_send.at[r], x_recv.at[r], near_x)

    def corner_x(r, dx=0):
        return copies(piece(1, dx, r, split=True)[:1], p_send.at[r], p_recv.at[r], near_x)

    def corner_y(r, dy=0):
        return copies(piece(dy, 1, r, split=True)[1:], q_send.at[r], q_recv.at[r], near_y)

    def time_x(r, dx=0):
        return [remote(time_piece(dx, r), time_piece(dx, r), w_send.at[r], w_recv.at[r], near_x)]

    def feed_y(r, dy=0):
        return [remote(feed_piece(dy, r), feed_piece(dy, r), g_send.at[r], g_recv.at[r], near_y)]

    def token_copies(k):
        peer = (y, x, k % 2, 2 * c + k // 2)
        return [
            remote(tok.at[k], rows_in.at[:, at(z, BLK)], t_send.at[k], t_recv.at[z], peer),
            remote(vec, vec_in.at[:, at(z, BLK)], v_send.at[k], v_recv.at[z], peer),
        ]

    def token_local(k):
        return [
            pltpu.make_async_copy(tok.at[k], rows_in.at[:, at(z, BLK)], local.at[6]),
            pltpu.make_async_copy(vec, vec_in.at[:, at(z, BLK)], local.at[7]),
        ]

    def stays(k):
        return jnp.logical_and(2 * c + k // 2 == z, c == k % 2)

    def start_tokens(ks):
        for k in ks:
            pl.when(stays(k))(lambda k=k: start(token_local(k)))
            pl.when(jnp.logical_not(stays(k)))(lambda k=k: start(token_copies(k)))

    def each_side(j, act):
        pl.when(z >= j + 1)(lambda: act(3 - j, True))
        pl.when(z <= 2 - j)(lambda: act(j + 1, False))

    def begin(make):
        pl.when(z < 3)(lambda: start(make(True, 0)))
        pl.when(z > 0)(lambda: start(make(False, 0)))

    def onward(j, make, right):
        if j < 2:
            pl.when(z < 3 if right else z > 0)(lambda: start(make(right, j + 1)))

    def forward(j):
        def act(r, right):
            landed(copies(piece(0, 0, r), z_send.at[0, 0], z_recv.at[r], near_y))
            onward(j, z_copies, right)
            start(y_copies(r))
            start(x_copies(r))

        each_side(j, act)

    def corners(j):
        def act(r, right):
            landed(y_copies(r, 1))
            start(corner_x(r))
            landed(x_copies(r, 1))
            start(corner_y(r))

        each_side(j, act)

    def time_forward_step(j):
        def act(r, right):
            landed([remote(time_piece(0, r), time_piece(0, r), u_send.at[0, 0], u_recv.at[r], near_x)])
            onward(j, time_z, right)
            start(time_x(r))

        each_side(j, act)

    def feed_forward_step(j):
        def act(r, right):
            landed([remote(feed_piece(0, r), feed_piece(0, r), f_send.at[0, 0], f_recv.at[r], near_y)])
            onward(j, feed_z, right)
            start(feed_y(r))

        each_side(j, act)

    for copy in keep:
        copy.wait()
    begin(z_copies)
    forward(0)
    start_tokens((0, 1))
    forward(1)
    start_tokens((2, 3))
    begin(time_z)
    corners(0)
    forward(2)
    corners(1)
    for k in range(4):
        def finish_local(k=k):
            for copy in token_local(k):
                copy.wait()

        pl.when(stays(k))(finish_local)
    for s in range(4):
        def arrived(s=s):
            landed([
                remote(tok.at[0], rows_in.at[:, at(s, BLK)], t_send.at[0], t_recv.at[s], near_y),
                remote(vec, vec_in.at[:, at(s, BLK)], v_send.at[0], v_recv.at[s], near_y),
            ])

        pl.when(jnp.logical_not(jnp.logical_and(z == s, z // 2 == c)))(arrived)

    step = own // 2
    slab = 128
    vec_out[...] = vec_in[...].astype(F32)

    def first_norm(i, carry):
        rows = at(i, step)
        value = jnp.where(masked[rows] > 0.0, vec_out[0:1], rows_in[rows].astype(F32))
        base[rows] = value
        standard, inv = norm_rows(value)
        std[rows] = standard
        inverse[rows] = inv
        normed[rows] = (standard * vec_out[1:2]).astype(BF16)
        return carry

    lax.fori_loop(0, 2, first_norm, 0)
    give_normed = remote(normed.at[pl.ds(0, own)], normed.at[pl.ds(own, own)], n_send.at[0], n_recv.at[0], pair)
    give_normed.start()
    corners(2)

    def turn(i, carry):
        turned[:, at(i, slab)] = normed[at(i, slab)].T
        return carry

    lax.fori_loop(0, own // slab, turn, 0)
    for r in (1, 2, 3):
        landed(corner_x(r, 1))
        landed(corner_y(r, 1))
    saves = [
        pltpu.make_async_copy(wq, wq_out, saved.at[0]),
        pltpu.make_async_copy(wo, wo_out, saved.at[1]),
        pltpu.make_async_copy(std, std_out, saved.at[2]),
    ]
    start(saves)
    time_forward_step(0)

    def attend(i, carry):
        rows = at(i, slab)
        for h in range(wo.shape[0] // PAIR):
            q, k, v = (joined[rows, (3 * h + j) * PAIR : (3 * h + j + 1) * PAIR] for j in range(3))
            out, totals = attend_pair(q, k, v, None, scale)
            mixed[rows, h * PAIR : (h + 1) * PAIR] = out.astype(BF16)
            for j in range(2):
                total_out[i, 2 * h + j : 2 * h + j + 1, :] = totals[j]
        return carry

    def project(t):
        rows = pl.ds(t * own, own)
        joined[rows] = dot_nn(normed[rows], wq[...]).astype(BF16)

    frames = own // slab
    project(0)
    time_forward_step(1)
    begin(feed_z)
    lax.fori_loop(0, frames, attend, 0)
    part[...] = dot_nn(mixed[pl.ds(0, own)], wo[...])
    time_forward_step(2)
    give_normed.wait_recv()
    project(1)
    saves.append(pltpu.make_async_copy(joined, joined_out, saved.at[3]))
    saves[3].start()
    lax.fori_loop(frames, 2 * frames, attend, 0)
    part_out[...] = dot_nn(mixed[pl.ds(own, own)], wo[...]).astype(BF16)
    give_part = remote(part_out, part_in, n_send.at[1], n_recv.at[1], pair)
    give_part.start()
    feed_forward_step(0)
    lax.fori_loop(own // slab, 2 * own // slab, turn, 0)
    saves.append(pltpu.make_async_copy(turned, turned_out, saved.at[4]))
    saves[4].start()
    give_part.wait_recv()
    feed_forward_step(1)

    def second_norm(i, carry):
        rows = at(i, step)
        value = base[rows] + part[rows] + part_in[rows].astype(F32)
        resid[rows] = value
        standard, inv = norm_rows(value)
        std_next[rows] = standard
        inverse_next[rows] = inv
        low_next[rows] = (standard * vec_out[2:3]).astype(BF16)
        return carry

    lax.fori_loop(0, 2, second_norm, 0)
    feed_forward_step(2)

    for copy in keep_later + saves:
        copy.wait()
    give_normed.wait_send()
    give_part.wait_send()
    for r in (1, 2, 3):
        landed(time_x(r, 1))
        landed(feed_y(r, 1))
        for group in (y_copies(r), x_copies(r), corner_x(r), corner_y(r), time_x(r), feed_y(r)):
            sent(group)
    for step_z in range(3):
        for make in (z_copies, time_z, feed_z):
            pl.when(jnp.logical_and(z >= step_z, z < 3))(lambda step_z=step_z, make=make: sent(make(True, step_z)))
            pl.when(jnp.logical_and(z + step_z <= 3, z > 0))(lambda step_z=step_z, make=make: sent(make(False, step_z)))
    for k in range(4):
        pl.when(jnp.logical_not(stays(k)))(lambda k=k: sent(token_copies(k)))


def enter(tok, vec, qkv, out, later, feed_weight, masked, scale):
    own, width, half = tok.shape[1], 4 * tok.shape[2], out.shape[0] // 2
    size = feed_weight.shape[0] // 2
    dma = pltpu.SemaphoreType.DMA
    anywhere = pl.BlockSpec(memory_space=pl.ANY)
    whole = pl.BlockSpec(memory_space=pltpu.VMEM)
    heads = 4 * half // HEAD_DIM

    def low(*shape):
        return pltpu.VMEM(shape, BF16)

    def high(*shape):
        return pltpu.VMEM(shape, F32)

    shapes = [
        ((width, 12 * half), BF16), ((4 * half, width), BF16), ((width, 4 * later.shape[1]), BF16),
        ((4, size, width), BF16), ((2 * own, 12 * half), BF16), ((width, 2 * own), BF16), ((own, width), F32),
        ((2 * own, 4 * half), BF16), ((2 * own // 128, heads, 128), F32), ((own, 1), F32), ((own, width), F32),
        ((own, width), F32), ((own, 1), F32), ((own, width), BF16), ((vec.shape[0], width), F32),
    ]
    return pl.pallas_call(
        functools.partial(enter_kernel, scale),
        in_specs=[anywhere] * 6 + [whole],
        out_specs=[anywhere] * 7 + [whole] * 8,
        out_shape=[jax.ShapeDtypeStruct(shape, kind) for shape, kind in shapes],
        scratch_shapes=[
            low(own, width), low(vec.shape[0], width), low(width, 12 * half), low(4 * half, width),
            low(2 * own, width), low(2 * own, 12 * half), low(width, 2 * own), high(own, width), high(own, width),
            high(own, width), low(own, width), low(own, width),
            dma((2, 3, 2)), dma((4, 2)), dma((4, 2)), dma((4, 2)), dma((4, 2)), dma((4, 2)),
            dma((4, 1)), dma((4, 1)), dma((4, 2)), dma((4, 2)),
            dma((4,)), dma((4,)), dma((4,)), dma((4,)), dma((2, 3)), dma((4,)), dma((4,)), dma((4,)),
            dma((2, 3)), dma((4,)), dma((4,)), dma((4,)), dma((2,)), dma((2,)), dma((8,)), dma((5,)),
        ],
        compiler_params=pltpu.CompilerParams(
            collective_id=0, has_side_effects=True, vmem_limit_bytes=56 * 1024 * 1024
        ),
        cost_estimate=pl.CostEstimate(flops=10**10, transcendentals=10**6, bytes_accessed=10**8),
        name="enter",
    )(tok, vec, qkv, out, later, feed_weight, masked)


GROUP = 8
CHUNK = 32


def time_kernel(back, scale, heads, *refs):
    if back:
        (own_ref, rider_ref, joined_ref, total_ref, wide_ref, wq_ref, wo_ref, bias_ref) = refs[:8]
        (all_ref, out_ref, delta_ref, reduced_ref, rider_out) = refs[8:13]
        (half_in, half_own, line_out, line_in, half_send, half_recv, half_local, line_send, line_recv) = refs[-9:]
        refs = refs[13:-9]
    else:
        (own_ref, rider_ref, far_ref, wq_ref, wo_ref, bias_ref) = refs[:6]
        (all_ref, out_ref, mixed_ref, total_ref, delta_ref, rider_out, spread_out) = refs[6:13]
        refs = refs[13:]
    (
        held, wide, narrow, kept, core_out, core_in, near_out, near_in,
        gy_send, gy_recv, gc_send, gc_recv, gd_send, gd_recv, sc_send, sc_recv, sy_send, sy_recv,
        r_send, r_recv, r_local, out_sem, wx_send, wx_recv,
    ) = refs
    y, x, c, z = (lax.axis_index(name) for name in AXES)
    near, pair, near_x = (1 - y, x, c, z), (y, x, 1 - c, z), (y, 1 - x, c, z)
    frames = held.shape[0] // 4
    chunks = held.shape[1] // CHUNK
    width = heads * HEAD_DIM
    groups = CHUNK // GROUP

    barrier = pltpu.get_barrier_semaphore()
    for dc in range(2):
        for dz in range(4):
            if dc or dz:
                pl.semaphore_signal(barrier, inc=1, device_id=(y, x, (c + dc) % 2, (z + dz) % 4), device_id_type=MESH)
    pl.semaphore_signal(barrier, inc=1, device_id=near, device_id_type=MESH)
    pl.semaphore_signal(barrier, inc=1, device_id=near_x, device_id_type=MESH)
    pl.semaphore_wait(barrier, 9)

    def remote(src, dst, send, recv, peer):
        return pltpu.make_async_remote_copy(
            src_ref=src, dst_ref=dst, send_sem=send, recv_sem=recv, device_id=peer, device_id_type=MESH
        )

    def patches(k):
        return pl.ds(pl.multiple_of(k * CHUNK, CHUNK), CHUNK)

    def block(b, k):
        return held.at[pl.ds(b * frames, frames), patches(k)]

    def gather_y(k):
        return remote(own_ref.at[:, patches(k)], block(1, k), gy_send.at[k], gy_recv.at[k], near)

    def gather_c(k):
        return remote(own_ref.at[:, patches(k)], block(2, k), gc_send.at[k], gc_recv.at[k], pair)

    def gather_d(k):
        return remote(block(1, k), block(3, k), gd_send.at[k], gd_recv.at[k], pair)

    def scatter_c(k):
        return remote(core_out.at[k], core_in.at[k], sc_send.at[k], sc_recv.at[k], pair)

    def scatter_y(k):
        return remote(near_out.at[k], near_in.at[k], sy_send.at[k], sy_recv.at[k], near)

    def save(k):
        return pltpu.make_async_copy(held.at[:, patches(k)], all_ref.at[:, patches(k)], out_sem.at[k])

    def columns(s):
        return pl.ds(pl.multiple_of(s * BLK, BLK), BLK)

    def stays(k):
        if back:
            return jnp.logical_and(z == k, z // 2 == c)
        return jnp.logical_and(2 * c + k // 2 == z, c == k % 2)

    def ride(k):
        if back:
            src, dst = rider_ref.at[:, columns(k)], rider_out.at[2 * (z % 2) + c]
            peer, slot = (y, x, z // 2, k), 2 * (z % 2) + c
        else:
            src, dst = rider_ref.at[k], rider_out.at[:, columns(z)]
            peer, slot = (y, x, k % 2, 2 * c + k // 2), z
        return src, dst, peer, slot

    def ride_remote(k):
        src, dst, peer, slot = ride(k)
        return remote(src, dst, r_send.at[k], r_recv.at[slot], peer)

    def ride_local(k):
        src, dst, _, _ = ride(k)
        return pltpu.make_async_copy(src, dst, r_local.at[0])

    def ride_landed(k):
        if back:
            src, dst = rider_ref.at[:, columns(k)], rider_out.at[k]
        else:
            src, dst = rider_ref.at[k], rider_out.at[:, columns(k)]
        return remote(src, dst, r_send.at[k], r_recv.at[k], near)

    def from_self(k):
        if back:
            return jnp.logical_and(2 * c + k // 2 == z, c == k % 2)
        return jnp.logical_and(z == k, z // 2 == c)

    def spread_x(i, dx=0):
        r, yb = i // 2 + 1, i % 2
        size = far_ref.shape[1] // 4
        at = pl.multiple_of(size * (2 * yb + (x + dx) % 2), size)
        src = far_ref.at[(z + r) % 4, pl.ds(at, size)]
        return remote(src, spread_out.at[(z + r) % 4, pl.ds(at, size)], wx_send.at[i], wx_recv.at[i], near_x)

    gather_y(0).start()
    for k in range(chunks):
        if k > 0:
            gather_y(k).start()
        gather_c(k).start()
    def half_away(s):
        return remote(wide_ref.at[1 - x, s], half_in.at[s], half_send.at[s], half_recv.at[s], near_x)

    def half_here(s):
        return pltpu.make_async_copy(wide_ref.at[x, s], half_own.at[s], half_local.at[s])

    def line_away(r):
        return remote(line_out.at[r], line_in.at[r], line_send.at[r], line_recv.at[r], (y, x, c, (z + r) % 4))

    def halve():
        for s in range(4):
            half_away(s).wait_recv()
            half_here(s).wait()
        for r in range(4):
            s = (z + r) % 4
            whole = half_own[s].astype(F32) + half_in[s].astype(F32)
            if r == 0:
                reduced_ref[...] = whole
            else:
                line_out[r] = whole.astype(BF16)
                line_away(r).start()

    if back:
        for s in range(4):
            half_away(s).start()
            half_here(s).start()
    else:
        for i in range(6):
            spread_x(i).start()
    for k in range(4):
        pl.when(stays(k))(lambda k=k: ride_local(k).start())
        pl.when(jnp.logical_not(stays(k)))(lambda k=k: ride_remote(k).start())
    held[:frames] = own_ref[...]

    def finish(k):
        scatter_c(k).wait_recv()
        both = kept[:, patches(k)] + core_in[k].astype(F32)
        near_out[k] = both[frames:].astype(BF16)
        delta_ref[:, patches(k)] = both[:frames]
        scatter_y(k).start()

    def pass_on(k):
        gather_y(k).wait_recv()
        gather_d(k).start()

    def one_group(i, rows):
        at = pl.ds(pl.multiple_of(i * GROUP, GROUP), GROUP)
        count = 4 * frames * GROUP
        bias = bias_ref[...]
        for lo in range(0, width, PAIR):
            q, k, v = (
                wide[:, at, part * width + lo : part * width + lo + PAIR].reshape(count, PAIR).astype(BF16)
                for part in range(3)
            )
            h = lo // HEAD_DIM
            if back:
                g = narrow[:, at, lo : lo + PAIR].reshape(count, PAIR).astype(BF16)
                totals = [total_ref[rows * groups + i, h + j : h + j + 1, :] for j in range(2)]
                grads = attend_pair_back(q, k, v, g, totals, bias, scale)
                for part in range(3):
                    wide[:, at, part * width + lo : part * width + lo + PAIR] = grads[part].reshape(
                        4 * frames, GROUP, PAIR
                    )
            else:
                mixed, totals = attend_pair(q, k, v, bias, scale)
                narrow[:, at, lo : lo + PAIR] = mixed.reshape(4 * frames, GROUP, PAIR)
                for j in range(2):
                    total_ref[rows * groups + i, h + j : h + j + 1, :] = totals[j]

    def one_chunk(k, carry):
        pl.when(k + 1 < chunks)(lambda: pass_on(k + 1))
        gather_c(k).wait_recv()
        gather_d(k).wait_recv()
        count = 4 * frames * CHUNK
        lhs = held[:, patches(k)].reshape(count, held.shape[2])
        if back:
            wide[...] = joined_ref[:, patches(k)].astype(F32)
            narrow[...] = dot_nn(lhs, wo_ref[...]).astype(BF16).astype(F32).reshape(narrow.shape)
        else:
            joined = dot_nn(lhs, wq_ref[...]).astype(BF16)
            out_ref[:, patches(k)] = joined.reshape(wide.shape)
            wide[...] = joined.astype(F32).reshape(wide.shape)
        save(k).start()
        lax.fori_loop(0, groups, lambda i, carry: (one_group(i, k), carry)[1], 0)
        if back:
            grads = wide[...].astype(BF16)
            out_ref[:, patches(k)] = grads
            partial = dot_nt(grads.reshape(count, 3 * width), wq_ref[...])
        else:
            mixed = narrow[...].astype(BF16)
            mixed_ref[:, patches(k)] = mixed
            partial = dot_nt(mixed.reshape(count, width), wo_ref[...])
        partial = partial.reshape(4 * frames, CHUNK, held.shape[2])
        kept[:, patches(k)] = partial[: 2 * frames]
        core_out[k] = partial[2 * frames :].astype(BF16)
        scatter_c(k).start()
        pl.when(k > 0)(lambda: finish(k - 1))
        if back:
            pl.when(k == 1)(halve)
        return carry

    pass_on(0)
    lax.fori_loop(0, chunks, one_chunk, 0)
    finish(chunks - 1)
    for k in range(chunks):
        scatter_y(k).wait_recv()
        delta_ref[:, patches(k)] = delta_ref[:, patches(k)] + near_in[k].astype(F32)
    if back:
        for r in (1, 2, 3):
            line_away(r).wait_recv()
            reduced_ref[...] = reduced_ref[...] + line_in[r].astype(F32)
        for r in (1, 2, 3):
            line_away(r).wait_send()
        for s in range(4):
            half_away(s).wait_send()
    for k in range(chunks):
        for copy in (gather_y(k), gather_c(k), gather_d(k), scatter_c(k), scatter_y(k)):
            copy.wait_send()
        save(k).wait()
    if not back:
        for i in range(6):
            spread_x(i, 1).wait_recv()
            spread_x(i).wait_send()
    for k in range(4):
        pl.when(stays(k))(lambda k=k: ride_local(k).wait())
        pl.when(jnp.logical_not(stays(k)))(lambda k=k: ride_remote(k).wait_send())
        pl.when(jnp.logical_not(from_self(k)))(lambda k=k: ride_landed(k).wait_recv())


def time_call(back, own, rider, saved, wq, wo, bias, scale):
    frames, patches, features = own.shape
    width = wo.shape[1]
    heads = width // HEAD_DIM
    chunks = patches // CHUNK
    rows = 4 * frames * GROUP
    dma = pltpu.SemaphoreType.DMA
    anywhere = pl.BlockSpec(memory_space=pl.ANY)
    whole = pl.BlockSpec(memory_space=pltpu.VMEM)
    out_shape = [
        jax.ShapeDtypeStruct((4 * frames, patches, features), BF16),
        jax.ShapeDtypeStruct((4 * frames, patches, 3 * width), BF16),
    ]
    if not back:
        out_shape += [
            jax.ShapeDtypeStruct((4 * frames, patches, width), BF16),
            jax.ShapeDtypeStruct((patches // GROUP, heads, rows), F32),
        ]
    rider_shape = (4, frames * patches, BLK) if back else (frames * patches, features)
    out_shape += [
        jax.ShapeDtypeStruct((frames, patches, features), F32),
        jax.ShapeDtypeStruct(rider_shape, BF16),
    ]
    held = 2
    half = saved[2].shape[1:] if back else None
    if back:
        out_shape.insert(-1, jax.ShapeDtypeStruct(half[1:], F32))
    else:
        out_shape.append(jax.ShapeDtypeStruct(saved[0].shape, BF16))
        held = 3
    return pl.pallas_call(
        functools.partial(time_kernel, back, scale, heads),
        in_specs=[whole, anywhere] + ([whole, whole, anywhere] if back else [anywhere]) + [whole] * 3,
        out_specs=[anywhere] + [whole] * (len(out_shape) - held) + [anywhere] * (held - 1),
        out_shape=out_shape,
        scratch_shapes=[
            pltpu.VMEM((4 * frames, patches, features), BF16),
            pltpu.VMEM((4 * frames, CHUNK, 3 * width), F32),
            pltpu.VMEM((4 * frames, CHUNK, width), F32),
            pltpu.VMEM((2 * frames, patches, features), F32),
            pltpu.VMEM((chunks, 2 * frames, CHUNK, features), BF16),
            pltpu.VMEM((chunks, 2 * frames, CHUNK, features), BF16),
            pltpu.VMEM((chunks, frames, CHUNK, features), BF16),
            pltpu.VMEM((chunks, frames, CHUNK, features), BF16),
        ]
        + [dma((chunks,))] * 10
        + [dma((4,)), dma((4,)), dma((1,)), dma((chunks,))]
        + [dma((6,))] * 2
        + ([pltpu.VMEM(half, BF16)] * 4 + [dma((4,))] * 5 if back else []),
        compiler_params=pltpu.CompilerParams(
            collective_id=2 if back else 1, has_side_effects=True, vmem_limit_bytes=48 * 1024 * 1024
        ),
        cost_estimate=pl.CostEstimate(flops=10**10, transcendentals=10**6, bytes_accessed=10**8),
        name="time_back" if back else "time_forward",
    )(own, rider, *saved, wq, wo, bias)


def feed_kernel(
    resid, delta, upstream, masked, gain, w_in_hbm, w_out_hbm, w_far_hbm,
    half_in_hbm, half_out_hbm, grad_out, low_out, rows_out, gain_out,
    w_in, w_out, standard, inverse, normed, grads, normed_t, grads_t, hidden, pulled, g_in, g_out, back, ahead,
    back_out, back_in, ahead_out, ahead_in, from_x, from_y,
    w_sem, g_sem, n_send, n_recv, b_send, b_recv, hx_send, hx_recv, hy_send, hy_recv,
):
    y, x, c, z = (lax.axis_index(name) for name in AXES)
    pair, near_y, near_x = (y, x, 1 - c, z), (1 - y, x, c, z), (y, 1 - x, c, z)
    own = resid.shape[0]
    step = own // 2
    slab = 128

    def fetch(s, far):
        size = w_out.shape[1] // 4
        copies = [pltpu.make_async_copy(w_in_hbm.at[s], w_in.at[s], w_sem.at[0, s])]
        for i in range(4):
            rows = pl.ds(pl.multiple_of(size * (2 * (i // 2) + (x + i % 2) % 2), size), size)
            source = w_far_hbm if far and i % 2 else w_out_hbm
            copies.append(pltpu.make_async_copy(source.at[s, rows], w_out.at[s, rows], w_sem.at[1 + i, s]))
        return copies

    def fetch_now(s, far):
        for copy in fetch(s, far):
            copy.start()

    for s in range(4):
        pl.when(z == s)(lambda s=s: fetch_now(s, False))
        pl.when(z != s)(lambda s=s: fetch_now(s, True))
    barrier = pltpu.get_barrier_semaphore()
    for peer in (pair, near_y, near_x):
        pl.semaphore_signal(barrier, inc=1, device_id=peer, device_id_type=MESH)

    def remote(src, dst, send, recv, peer=pair):
        return pltpu.make_async_remote_copy(
            src_ref=src, dst_ref=dst, send_sem=send, recv_sem=recv, device_id=peer, device_id_type=MESH
        )

    def block(yb, xb):
        return pl.ds(pl.multiple_of(BLK * (2 * yb + xb), BLK), BLK)

    def away_x(s, i):
        return remote(g_out.at[s, block(i, 1 - x)], from_x.at[i, s], hx_send.at[i, s], hx_recv.at[i, s], near_x)

    def away_y(s, i):
        return remote(g_in.at[s, block(1 - y, i)], from_y.at[i, s], hy_send.at[i, s], hy_recv.at[i, s], near_y)

    def keep(s, i):
        return (
            pltpu.make_async_copy(g_out.at[s, block(i, x)], half_out_hbm.at[i, s], g_sem.at[0, i, s]),
            pltpu.make_async_copy(g_in.at[s, block(y, i)], half_in_hbm.at[i, s], g_sem.at[1, i, s]),
        )

    def combine(s):
        for i in range(2):
            away_x(s, i).wait_recv()
            g_out[s, block(i, x)] = (g_out[s, block(i, x)].astype(F32) + from_x[i, s].astype(F32)).astype(BF16)
            away_y(s, i).wait_recv()
            g_in[s, block(y, i)] = (g_in[s, block(y, i)].astype(F32) + from_y[i, s].astype(F32)).astype(BF16)
            for copy in keep(s, i):
                copy.start()

    def at(i, size):
        return pl.ds(pl.multiple_of(i * size, size), size)

    def prepare(i, carry):
        rows = at(i, step)
        grads[rows] = jnp.where(masked[rows] > 0.0, upstream[rows].astype(F32), 0.0).astype(BF16)
        std, inv = norm_rows(resid[rows] + delta[rows])
        standard[rows] = std
        inverse[rows] = inv
        normed[rows] = (std * gain[...]).astype(BF16)
        return carry

    lax.fori_loop(0, 2, prepare, 0)
    pl.semaphore_wait(barrier, 3)
    mine, theirs = pl.ds(0, own), pl.ds(own, own)
    give_grads = remote(grads.at[mine], grads.at[theirs], n_send.at[0], n_recv.at[0])
    give_normed = remote(normed.at[mine], normed.at[theirs], n_send.at[1], n_recv.at[1])
    give_normed.start()
    give_grads.start()

    def turn(i, carry):
        rows = at(i, slab)
        normed_t[:, rows] = normed[rows].T
        grads_t[:, rows] = grads[rows].T
        return carry

    lax.fori_loop(0, own // slab, turn, 0)
    back[...] = jnp.zeros_like(back)
    ahead[...] = jnp.zeros_like(ahead)
    rate = math.sqrt(2.0 / math.pi)

    def rows_step(s, rows):
        inner = dot_nn(normed[rows], w_in[s])
        square = inner * inner
        bend = jnp.tanh(rate * inner * (1.0 + 0.044715 * square))
        hidden[rows] = (0.5 * inner * (1.0 + bend)).astype(BF16)
        slope = 0.5 * (1.0 + bend) + 0.5 * inner * (1.0 - bend * bend) * (rate * (1.0 + 3.0 * 0.044715 * square))
        pulled[rows] = (dot_nt(grads[rows], w_out[s]) * slope).astype(BF16)
        ahead[rows] = ahead[rows] + dot_nn(hidden[rows], w_out[s])
        back[rows] = back[rows] + dot_nt(pulled[rows], w_in[s])

    def meet():
        give_normed.wait_recv()
        give_grads.wait_recv()
        lax.fori_loop(own // slab, 2 * own // slab, turn, 0)

    def one_piece(s, carry):
        for copy in fetch(s, False):
            copy.wait()

        def one_half(t, carry):
            pl.when(jnp.logical_and(s == 0, t == 1))(meet)
            rows_step(s, at(t, own))
            return carry

        lax.fori_loop(0, 2, one_half, 0)
        g_out[s] = dot_nn(grads_t[...], hidden[...]).astype(BF16)
        g_in[s] = dot_nn(normed_t[...], pulled[...]).astype(BF16)
        for i in range(2):
            away_x(s, i).start()
            away_y(s, i).start()
        return carry

    lax.fori_loop(0, 4, one_piece, 0)
    back_out[...] = back[theirs].astype(BF16)
    give_back = remote(back_out, back_in, b_send.at[0], b_recv.at[0])
    give_back.start()
    ahead_out[...] = ahead[theirs].astype(BF16)
    give_ahead = remote(ahead_out, ahead_in, b_send.at[1], b_recv.at[1])
    give_ahead.start()
    give_back.wait_recv()

    def finish(i, total):
        rows = at(i, step)
        grad = back[rows] + back_in[rows].astype(F32)
        std = standard[rows]
        inner = grad * gain[...]
        mean = jnp.mean(inner, axis=-1, keepdims=True)
        along = jnp.mean(inner * std, axis=-1, keepdims=True)
        full = grads[rows].astype(F32) + (inner - mean - std * along) * inverse[rows]
        grad_out[rows] = full
        low_out[rows] = full.astype(BF16)
        return total + jnp.sum(grad * std, axis=0, keepdims=True)

    gain_out[...] = lax.fori_loop(0, 2, finish, jnp.zeros((1, resid.shape[1]), F32))
    give_ahead.wait_recv()

    def emit(i, carry):
        rows = at(i, step)
        rows_out[rows] = (resid[rows] + delta[rows] + ahead[rows] + ahead_in[rows].astype(F32)).astype(BF16)
        return carry

    lax.fori_loop(0, 2, emit, 0)
    lax.fori_loop(0, 4, lambda s, carry: (combine(s), carry)[1], 0)
    for copy in (give_normed, give_grads, give_back, give_ahead):
        copy.wait_send()
    for s in range(4):
        for i in range(2):
            away_x(s, i).wait_send()
            away_y(s, i).wait_send()
            for copy in keep(s, i):
                copy.wait()


def feed(resid, delta, upstream, masked, gain, w_in, w_out, w_far):
    own, features = resid.shape
    units = w_in.shape[2]
    dma = pltpu.SemaphoreType.DMA
    anywhere = pl.BlockSpec(memory_space=pl.ANY)
    whole = pl.BlockSpec(memory_space=pltpu.VMEM)

    def low(*shape):
        return pltpu.VMEM(shape, BF16)

    def high(*shape):
        return pltpu.VMEM(shape, F32)

    return pl.pallas_call(
        feed_kernel,
        in_specs=[whole] * 5 + [anywhere] * 3,
        out_specs=[anywhere] * 2 + [whole] * 4,
        out_shape=[
            jax.ShapeDtypeStruct((2, 4, BLK, units), BF16),
            jax.ShapeDtypeStruct((2, 4, BLK, units), BF16),
            jax.ShapeDtypeStruct((own, features), F32),
            jax.ShapeDtypeStruct((own, features), BF16),
            jax.ShapeDtypeStruct((own, features), BF16),
            jax.ShapeDtypeStruct((1, features), F32),
        ],
        scratch_shapes=[
            low(4, features, units), low(4, units, features), high(own, features), high(own, 1),
            low(2 * own, features), low(2 * own, features), low(features, 2 * own), low(features, 2 * own),
            low(2 * own, units), low(2 * own, units), low(4, features, units), low(4, features, units),
            high(2 * own, features), high(2 * own, features),
            low(own, features), low(own, features), low(own, features), low(own, features),
            low(2, 4, BLK, units), low(2, 4, BLK, units),
            dma((5, 4)), dma((2, 2, 4)), dma((2,)), dma((2,)), dma((2,)), dma((2,)),
            dma((2, 4)), dma((2, 4)), dma((2, 4)), dma((2, 4)),
        ],
        compiler_params=pltpu.CompilerParams(
            collective_id=4, has_side_effects=True, vmem_limit_bytes=60 * 1024 * 1024
        ),
        cost_estimate=pl.CostEstimate(flops=26 * 10**9, transcendentals=2 * 10**6, bytes_accessed=10**8),
        name="feed",
    )(resid, delta, upstream, masked, gain, w_in, w_out, w_far)


def settle_kernel(
    dj, go, lhs, weight_hbm, std_hbm, base_hbm, inverse, masked, gain, small_in,
    kept_out, landed_out, rows_out, small_out,
    weight, std, base, grads, a1_out, a1_in, b1_out, b1_in, a2_out, a2_in, b2_out, b2_in, z_out, z_in,
    half_out, half_in, ready, core_out, core_in, sums, sum_out, sum_in, share_in,
    a1_send, a1_recv, b1_send, b1_recv, a2_send, a2_recv, b2_send, b2_recv, z_send, z_recv,
    h_send, h_recv, r_send, r_recv, c_send, c_recv, s_send, s_recv, p_send, p_recv, local,
):
    y, x, c, z = (lax.axis_index(name) for name in AXES)
    near_y, near_x, pair = (1 - y, x, c, z), (y, 1 - x, c, z), (y, x, 1 - c, z)
    own = std.shape[0]
    third = go.shape[1] // 4
    wide = 3 * third
    two = 2 * third

    fetches = [
        pltpu.make_async_copy(weight_hbm, weight, local.at[0]),
        pltpu.make_async_copy(std_hbm, std, local.at[1]),
        pltpu.make_async_copy(base_hbm, base, local.at[2]),
    ]
    for copy in fetches:
        copy.start()

    barrier = pltpu.get_barrier_semaphore()
    for dc in range(2):
        for dz in range(4):
            if dc or dz:
                pl.semaphore_signal(barrier, inc=1, device_id=(y, x, (c + dc) % 2, (z + dz) % 4), device_id_type=MESH)
    for peer in (near_y, near_x):
        pl.semaphore_signal(barrier, inc=1, device_id=peer, device_id_type=MESH)
    pl.semaphore_wait(barrier, 9)

    def remote(src, dst, send, recv, peer):
        return pltpu.make_async_remote_copy(
            src_ref=src, dst_ref=dst, send_sem=send, recv_sem=recv, device_id=peer, device_id_type=MESH
        )

    def block(yb, xb):
        return pl.ds(pl.multiple_of(BLK * (2 * yb + xb), BLK), BLK)

    def a1(i):
        return remote(a1_out.at[i], a1_in.at[i], a1_send.at[i], a1_recv.at[i], near_x)

    def b1(i):
        return remote(b1_out.at[i], b1_in.at[i], b1_send.at[i], b1_recv.at[i], near_y)

    def a2(i):
        return remote(a2_out.at[i], a2_in.at[i], a2_send.at[i], a2_recv.at[i], near_y)

    def b2(i):
        return remote(b2_out.at[i], b2_in.at[i], b2_send.at[i], b2_recv.at[i], near_x)

    def to_z(r):
        return remote(z_out.at[r], z_in.at[r], z_send.at[r], z_recv.at[r], (y, x, c, (z + r) % 4))

    def piece(i, carry):
        s = (z + i + 1) % 4
        made = dot_nn(lhs[...], dj[:, pl.ds(pl.multiple_of(s * wide, third), wide)])
        grads[i, :, :wide] = made
        grads[i, :, wide:] = go[:, pl.ds(pl.multiple_of(s * third, third), third)].astype(F32)
        for b in range(2):
            a1_out[i, b] = grads[i, block(b, 1 - x), :two].astype(BF16)
            b1_out[i, b] = grads[i, block(1 - y, b), two:].astype(BF16)
        a1(i).start()
        b1(i).start()
        return carry

    lax.fori_loop(0, 4, piece, 0)

    def second(i):
        a1(i).wait_recv()
        a2_out[i] = (grads[i, block(1 - y, x), :two] + a1_in[i, 1 - y].astype(F32)).astype(BF16)
        a2(i).start()
        b1(i).wait_recv()
        b2_out[i] = (grads[i, block(y, 1 - x), two:] + b1_in[i, 1 - x].astype(F32)).astype(BF16)
        b2(i).start()
        grads[i, block(y, x), :two] = grads[i, block(y, x), :two] + a1_in[i, y].astype(F32)
        grads[i, block(y, x), two:] = grads[i, block(y, x), two:] + b1_in[i, x].astype(F32)

    def third_step(i):
        a2(i).wait_recv()
        b2(i).wait_recv()
        grads[i, block(y, x), :two] = grads[i, block(y, x), :two] + a2_in[i].astype(F32)
        grads[i, block(y, x), two:] = grads[i, block(y, x), two:] + b2_in[i].astype(F32)
        if i < 3:
            z_out[i + 1] = grads[i, block(y, x), :].astype(BF16)
            to_z(i + 1).start()

    step = own // 2
    fetches[0].wait()

    def away(i, carry):
        rows = pl.ds(pl.multiple_of(own + i * step, step), step)
        half_out[pl.ds(pl.multiple_of(i * step, step), step)] = dot_nt(dj[rows], weight[...]).astype(BF16)
        return carry

    lax.fori_loop(0, 2, away, 0)
    swap = remote(half_out, half_in, h_send.at[0], h_recv.at[0], pair)
    swap.start()
    second(0)
    for copy in fetches[1:]:
        copy.wait()
    sums[...] = small_in[...]
    swap.wait_recv()

    def home(i, totals):
        rows = pl.ds(pl.multiple_of(i * step, step), step)
        grad = dot_nt(dj[rows], weight[...]) + half_in[rows].astype(F32)
        standard = std[rows]
        inner = grad * gain[...]
        mean = jnp.mean(inner, axis=-1, keepdims=True)
        along = jnp.mean(inner * standard, axis=-1, keepdims=True)
        full = base[rows] + (inner - mean - standard * along) * inverse[rows]
        hide = masked[rows] > 0.0
        ready[rows] = jnp.where(hide, 0.0, full).astype(BF16)
        return (
            totals[0] + jnp.sum(grad * standard, axis=0, keepdims=True),
            totals[1] + jnp.sum(jnp.where(hide, full, 0.0), axis=0, keepdims=True),
        )

    zero = jnp.zeros((1, std.shape[1]), F32)
    gain_grad, embed_grad = lax.fori_loop(0, 2, home, (zero, zero))
    sums[0:1] = gain_grad
    sums[3:4] = embed_grad

    def columns(s):
        return pl.ds(pl.multiple_of(s * BLK, BLK), BLK)

    def stays(k):
        return jnp.logical_and(z == k, z // 2 == c)

    def ride(k):
        slot = 2 * (z % 2) + c
        return remote(ready.at[:, columns(k)], rows_out.at[slot], r_send.at[k], r_recv.at[slot], (y, x, z // 2, k))

    def ride_local(k):
        return pltpu.make_async_copy(ready.at[:, columns(k)], rows_out.at[2 * (z % 2) + c], local.at[3])

    for k in range(4):
        pl.when(stays(k))(lambda k=k: ride_local(k).start())
        pl.when(jnp.logical_not(stays(k)))(lambda k=k: ride(k).start())

    def share(h):
        peer = (pair, near_y, near_x)[h]
        return remote(sum_out.at[h], sum_in.at[h], s_send.at[h], s_recv.at[h], peer)

    def begin_share(h):
        sum_out[h] = sums[...]
        share(h).start()

    def end_share(h):
        share(h).wait_recv()
        sums[...] = sums[...] + sum_in[h]

    begin_share(0)
    second(1)
    third_step(0)
    end_share(0)
    begin_share(1)
    second(2)
    third_step(1)
    end_share(1)
    begin_share(2)
    second(3)
    third_step(2)
    end_share(2)
    sum_out[3] = sums[...]

    def deal(r):
        s = (z + r) % 4
        return remote(sum_out.at[3, :, columns(s)], share_in.at[r], p_send.at[r], p_recv.at[r], (y, x, c, s))

    for r in (1, 2, 3):
        deal(r).start()
    third_step(3)
    for r in (1, 2, 3):
        to_z(r).wait_recv()
    total = grads[3, block(y, x), :]
    for r in (1, 2, 3):
        total = total + z_in[r].astype(F32)
    grads[3, block(y, x), :] = total
    rows = BLK // 2

    def core_rows(core):
        return pl.ds(pl.multiple_of(BLK * (2 * y + x) + rows * core, rows), rows)

    core_out[...] = grads[3, core_rows(1 - c), :].astype(BF16)
    last = remote(core_out, core_in, c_send.at[0], c_recv.at[0], pair)
    last.start()
    kept_out[...] = grads[3, core_rows(c), :]
    result = sums[:, columns(z)]
    for r in (1, 2, 3):
        deal(r).wait_recv()
        result = result + share_in[r]
    small_out[...] = result
    last.wait_recv()
    landed_out[...] = core_in[...].astype(F32)

    last.wait_send()
    swap.wait_send()
    for i in range(4):
        for copy in (a1(i), b1(i), a2(i), b2(i)):
            copy.wait_send()
    for r in (1, 2, 3):
        to_z(r).wait_send()
        deal(r).wait_send()
    for h in range(3):
        share(h).wait_send()
    for k in range(4):
        pl.when(stays(k))(lambda k=k: ride_local(k).wait())
        pl.when(jnp.logical_not(stays(k)))(lambda k=k: ride(k).wait_send())
        from_self = jnp.logical_and(2 * c + k // 2 == z, c == k % 2)

        def landed(k=k):
            remote(ready.at[:, columns(k)], rows_out.at[k], r_send.at[k], r_recv.at[k], near_y).wait_recv()

        pl.when(jnp.logical_not(from_self))(landed)


def settle(dj, go, lhs, weight, std, base, inverse, masked, gain, small):
    own, features = std.shape
    cols4 = go.shape[1]
    quarter = cols4 // 4
    dma = pltpu.SemaphoreType.DMA
    anywhere = pl.BlockSpec(memory_space=pl.ANY)
    whole = pl.BlockSpec(memory_space=pltpu.VMEM)

    def low(*shape):
        return pltpu.VMEM(shape, BF16)

    def high(*shape):
        return pltpu.VMEM(shape, F32)

    return pl.pallas_call(
        settle_kernel,
        in_specs=[whole] * 3 + [anywhere] * 3 + [whole] * 4,
        out_specs=[whole, whole, anywhere, whole],
        out_shape=[
            jax.ShapeDtypeStruct((BLK // 2, cols4), F32),
            jax.ShapeDtypeStruct((BLK // 2, cols4), F32),
            jax.ShapeDtypeStruct((4, own, BLK), BF16),
            jax.ShapeDtypeStruct((8, BLK), F32),
        ],
        scratch_shapes=[
            low(*weight.shape), high(own, features), high(own, features), high(4, features, cols4),
            low(4, 2, BLK, 2 * quarter), low(4, 2, BLK, 2 * quarter), low(4, 2, BLK, 2 * quarter), low(4, 2, BLK, 2 * quarter),
            low(4, BLK, 2 * quarter), low(4, BLK, 2 * quarter), low(4, BLK, 2 * quarter), low(4, BLK, 2 * quarter),
            low(4, BLK, cols4), low(4, BLK, cols4),
            low(own, features), low(own, features), low(own, features),
            low(BLK // 2, cols4), low(BLK // 2, cols4),
            high(8, features), high(4, 8, features), high(3, 8, features), high(4, 8, BLK),
        ]
        + [dma((4,))] * 10
        + [dma((1,)), dma((1,)), dma((4,)), dma((4,)), dma((1,)), dma((1,)), dma((3,)), dma((3,)), dma((4,)), dma((4,)), dma((4,))],
        compiler_params=pltpu.CompilerParams(
            collective_id=3, has_side_effects=True, vmem_limit_bytes=56 * 1024 * 1024
        ),
        cost_estimate=pl.CostEstimate(flops=10**10, transcendentals=10**6, bytes_accessed=10**8),
        name="settle",
    )(dj, go, lhs, weight, std, base, inverse, masked, gain, small)


def tie(*values):
    return lax.optimization_barrier(values)


def norm_rows(resid):
    mean = jnp.mean(resid, axis=-1, keepdims=True)
    centered = resid - mean
    inverse = lax.rsqrt(jnp.mean(centered * centered, axis=-1, keepdims=True) + eps_norm)
    return (centered * inverse, inverse)


def norm_rows_back(grad, standardized, inverse, gain):
    gain_grad = jnp.sum(grad * standardized, axis=0)
    inner = grad * gain
    mean = jnp.mean(inner, axis=-1, keepdims=True)
    along = jnp.mean(inner * standardized, axis=-1, keepdims=True)
    return ((inner - mean - standardized * along) * inverse, gain_grad)


def cols(parts):
    return jnp.concatenate(parts, axis=1)


def rows_of(parts):
    return jnp.concatenate(parts, axis=0)


def token_parallel(
    tokens,
    cotangent,
    ratio,
    priority,
    frame_order,
    mask_embed,
    gains,
    qkv_space,
    out_space,
    qkv_time,
    out_time,
    w_in,
    w_out,
):
    scale = 1.0 / math.sqrt(HEAD_DIM)
    y, x, c, z = (lax.axis_index(name) for name in AXES)
    patches = tokens.shape[2]
    width = qkv_space.shape[0]
    frames_own = tokens.shape[0] * tokens.shape[1] // 4
    frames_all = frame_order.shape[1]
    own = frames_own * patches
    hidden_own = w_in.shape[1] // 2
    plane = 2 * y + x
    k_own = 2 * (z % 2) + c

    masked_here = (priority < ratio[:, None, None]).astype(jnp.int32).reshape(2, -1)
    info = cols([masked_here, frame_order])
    info = jnp.where(z // 2 == c, info, hop_c(info))
    info = lax.dynamic_index_in_dim(info, z % 2, 0, keepdims=False)
    masked = lax.dynamic_slice_in_dim(info, c * own, own, 0)[:, None] != 0
    order = info[2 * own :].reshape(2, 2, frames_own)
    order = jnp.where(y == 1, order[::-1], order)
    order = jnp.where(c == 1, order[:, ::-1], order).swapaxes(0, 1).reshape(frames_all)
    order = jnp.repeat(order, GROUP)
    patch = jnp.arange(frames_all * GROUP) % GROUP
    visible = (order[:, None] <= order[None, :]) & (patch[:, None] == patch[None, :])
    bias = jnp.where(visible, 0.0, -1e30).astype(F32)

    vectors = rows_of([mask_embed[None], gains, jnp.zeros((4, BLK), BF16)])
    head = (2 * y + c) * HEAD_DIM
    ti_own = cols(
        [
            lax.dynamic_slice_in_dim(qkv_time, head, HEAD_DIM, 2).reshape(width, -1),
            lax.dynamic_slice_in_dim(out_time, head, HEAD_DIM, 0).T,
        ]
    )
    (
        ws_qkv, ws_out, wt_all, wf_out, joined0, turned0, std0,
        mixed0, total0, inv0, resid1, std1, inv1, normed1, vectors,
    ) = enter(
        tokens.reshape(4, own, BLK),
        vectors,
        jnp.swapaxes(qkv_space, 0, 1),
        out_space,
        ti_own,
        w_out,
        masked.astype(F32),
        scale,
    )
    gain = [vectors[1 + i : 2 + i] for i in range(3)]
    wt_all = wt_all.reshape(width, 4, 4, HEAD_DIM)
    wt_qkv = jnp.swapaxes(wt_all[:, :, :3], 1, 2).reshape(width, 12 * HEAD_DIM)
    wt_out = wt_all[:, :, 3].reshape(width, 4 * HEAD_DIM)

    ff_in = lax.dynamic_slice(w_in, (plane * BLK, c * hidden_own), (BLK, hidden_own))
    ff_in, normed1 = tie(ff_in, normed1)
    wf_in = lax.all_gather(ff_in, ("mp", "tm", "x")).reshape(4, width, hidden_own)

    def pair_gather(v):
        return rows_of([v, hop_c(v)])

    def pair_scatter(v):
        return v[:own] + hop_c(v[own:].astype(BF16)).astype(F32)

    half = qkv_space.shape[2] // 2
    heads_s = 4 * half // HEAD_DIM
    frames_pair = 2 * frames_own
    normed1, joined1, mixed1, total1, delta, upstream, wf_far = time_call(
        False,
        normed1.reshape(frames_own, patches, width),
        cotangent.reshape(4, own, BLK),
        [wf_out],
        wt_qkv,
        wt_out,
        bias,
        scale,
    )
    normed1 = normed1.reshape(4 * own, width)
    mixed1 = mixed1.reshape(4 * own, -1)
    w_in_half, w_out_half, grad2, grad2_low, block_rows, gain_grad2 = feed(
        resid1, delta.reshape(own, width), upstream, masked.astype(F32), gain[2], wf_in, wf_out, wf_far
    )

    def send_x(lhs, rhs):
        there = jnp.where(x == 0, cols([lhs[:, BLK : 2 * BLK], lhs[:, 3 * BLK :]]), cols([lhs[:, :BLK], lhs[:, 2 * BLK : 3 * BLK]]))
        return hop_x(dot_tn(there, rhs).astype(BF16))

    def keep_x(lhs, rhs, landed):
        here = jnp.where(x == 1, cols([lhs[:, BLK : 2 * BLK], lhs[:, 3 * BLK :]]), cols([lhs[:, :BLK], lhs[:, 2 * BLK : 3 * BLK]]))
        return dot_tn(here, rhs) + landed.astype(F32)

    def mine_y(v):
        return jnp.where(y == 0, v[:BLK], v[BLK:])

    def other_y(v):
        return jnp.where(y == 1, v[:BLK], v[BLK:])

    def reduce_z(pieces):
        total = pieces[0]
        for r in (1, 2, 3):
            total = total + hop_z(pieces[r].astype(BF16), r).astype(F32)
        return total

    def swap_c(total):
        rows = BLK // 2
        kept = lax.dynamic_slice_in_dim(total, c * rows, rows, 0)
        sent = hop_c(lax.dynamic_slice_in_dim(total, (1 - c) * rows, rows, 0).astype(BF16))
        return (kept, sent.astype(F32))

    def by_core(kept, landed):
        return jnp.where(c == 0, jnp.concatenate([kept, landed], -1), jnp.concatenate([landed, kept], -1))

    gb2, djoined1, part1, g_w_in, block_out = time_call(
        True,
        grad2_low.reshape(frames_own, patches, width),
        block_rows,
        [joined1, total1, w_in_half],
        wt_qkv,
        wt_out,
        bias,
        scale,
    )
    block_out = block_out.reshape(tokens.shape)
    gb2 = gb2.reshape(4 * own, width)
    djoined1 = djoined1.reshape(4 * own, -1)
    part1, w_out_half = tie(part1.reshape(own, width), w_out_half)
    g_w_out = lax.psum_scatter(w_out_half, "tm", scatter_dimension=0)
    g_w_out = lax.psum_scatter(g_w_out, "mp", scatter_dimension=0).astype(F32)
    back1, gain_grad1 = norm_rows_back(part1, std1, inv1, gain[1])
    grad1 = grad2 + back1
    gb1 = pair_gather(grad1.astype(BF16))
    t_out_x = send_x(gb2, mixed1)
    t_qkv_x = send_x(normed1, djoined1)
    dmixed0 = dot_nt(gb1, ws_out).astype(BF16)
    go = dot_tn(gb1, mixed0).astype(BF16)
    djoined0 = space_attend_back(joined0, dmixed0, total0, frames_pair, patches, heads_s, scale)
    djoined0, t_out_x, t_qkv_x, go = tie(djoined0, t_out_x, t_qkv_x, go)
    g_t_out = keep_x(gb2, mixed1, t_out_x)
    g_t_qkv = keep_x(normed1, djoined1, t_qkv_x)
    z_at = [(z + r) % 4 for r in range(4)]
    span = 4 * HEAD_DIM
    g_time = reduce_z(
        [
            cols(
                [lax.dynamic_slice_in_dim(g_t_qkv, j * span + s * HEAD_DIM, HEAD_DIM, 1) for j in range(3)]
                + [lax.dynamic_slice_in_dim(g_t_out, s * HEAD_DIM, HEAD_DIM, 1)]
            )
            for s in z_at
        ]
    )
    small = rows_of([jnp.zeros((1, width), F32), gain_grad1[None], gain_grad2, jnp.zeros((5, width), F32)])
    kept, landed, grad_tokens, small = settle(
        djoined0, go, turned0, ws_qkv, std0, grad1, inv0, masked.astype(F32), gain[0], small
    )
    grad_tokens = grad_tokens.reshape(tokens.shape).astype(F32)

    rows = BLK // 2
    grad_qkv_space = by_core(
        kept[:, : 3 * half].reshape(rows, 3, half), landed[:, : 3 * half].reshape(rows, 3, half)
    )
    grad_out_space = by_core(kept[:, 3 * half :], landed[:, 3 * half :]).T
    kept, landed = swap_c(cols([g_w_in, g_w_out]))
    grad_w_in = by_core(kept[:, :hidden_own], landed[:, :hidden_own])
    grad_w_out = by_core(kept[:, hidden_own:], landed[:, hidden_own:]).T
    both = cols([mine_y(g_time), hop_y(other_y(g_time).astype(BF16)).astype(F32)])
    kept, landed = swap_c(both)
    quad = jnp.stack([kept, landed], 1).reshape(rows, 2, 2, 4, HEAD_DIM)
    quad = jnp.where(c == 1, quad[:, ::-1], quad)
    quad = jnp.where(y == 1, quad[:, :, ::-1], quad)
    quad = jnp.transpose(quad, (0, 3, 2, 1, 4)).reshape(rows, 4, 4 * HEAD_DIM)
    grad_qkv_time = quad[:, :3]
    grad_out_time = quad[:, 3].T
    return (
        block_out,
        grad_tokens,
        small[3],
        small[:3],
        grad_qkv_space,
        grad_out_space,
        grad_qkv_time,
        grad_out_time,
        grad_w_in,
        grad_w_out,
    )


def solution(mesh):
    sizes = (mesh.shape["tm"], mesh.shape["clip"], mesh.shape["mp"])
    if sizes == (2, 4, 4):
        mesh = jax.sharding.Mesh(mesh.devices.reshape(2, 2, 2, 4), AXES)
        step, clip = token_parallel, ("x", "c")
    else:
        step, clip = shards, ("clip",)
    return jax.shard_map(
        step,
        mesh=mesh,
        in_specs=(
            P(clip, "tm", None, "mp"),
            P(clip, "tm", None, "mp"),
            P(clip),
            P(clip, "tm", None),
            P(clip, None),
            P("mp"),
            P(None, "mp"),
            P(None, None, "mp"),
            P("mp", None),
            P(None, None, "mp"),
            P("mp", None),
            P(None, "mp"),
            P("mp", None),
        ),
        out_specs=(
            P(clip, "tm", None, "mp"),
            P(clip, "tm", None, "mp"),
            P("mp"),
            P(None, "mp"),
            P(("tm",) + clip, None, "mp"),
            P("mp", ("tm",) + clip),
            P(("tm",) + clip, None, "mp"),
            P("mp", ("tm",) + clip),
            P(("tm",) + clip, "mp"),
            P("mp", ("tm",) + clip),
        ),
        check_vma=False,
    )
```

```python
import functools
import math

import jax
import jax.numpy as jnp
from jax import lax
from jax.experimental import pallas as pl
from jax.experimental.pallas import tpu as pltpu
from jax.sharding import PartitionSpec as P

HEAD_DIM = 64
MICRO = 2


eps_norm = 1e-05


def gelu_tanh(values):
    return jax.nn.gelu(values, approximate=True)


def norm_forward_pass(residual_stream, gain_coefficients, complete_width):
    reduced_totals = lax.psum(
        (jnp.sum(residual_stream, axis=-1), jnp.sum(residual_stream * residual_stream, axis=-1)),
        "mp",
    )
    centered_rows = reduced_totals[0] / complete_width
    spread = reduced_totals[1] / complete_width - centered_rows * centered_rows
    inverse_scale = lax.rsqrt(spread + eps_norm)
    standardized_rows = (residual_stream - centered_rows[:, None]) * inverse_scale[:, None]
    shard_rows = (standardized_rows * gain_coefficients).astype(jnp.bfloat16)
    normalized_rows = lax.all_gather(shard_rows, "mp", axis=1, tiled=True)
    return (normalized_rows, standardized_rows, inverse_scale)


def norm_reverse_pass(
    normalized_gradient, standardized_rows, inverse_scale, gain_coefficients, complete_width
):
    gain_gradient = jnp.sum(normalized_gradient * standardized_rows, axis=0)
    standardized_gradient = normalized_gradient * gain_coefficients
    reduced_totals = lax.psum(
        (
            jnp.sum(standardized_gradient, axis=-1),
            jnp.sum(standardized_gradient * standardized_rows, axis=-1),
        ),
        "mp",
    )
    grad_resid = (
        standardized_gradient
        - reduced_totals[0][:, None] / complete_width
        - standardized_rows * (reduced_totals[1][:, None] / complete_width)
    ) * inverse_scale[:, None]
    return (grad_resid, gain_gradient)


def sum_features(grad_full):
    return lax.psum_scatter(
        grad_full.astype(jnp.bfloat16), "mp", scatter_dimension=1, tiled=True
    ).astype(jnp.float32)


def branch_out(hidden, weight):
    partial_rows = jnp.dot(hidden, weight, preferred_element_type=jnp.float32)
    return lax.psum_scatter(partial_rows, "mp", scatter_dimension=1, tiled=True)


def branch_back(grad_resid, hidden, weight):
    grad_rows = lax.all_gather(grad_resid.astype(jnp.bfloat16), "mp", axis=1, tiled=True)
    weight_grad = jnp.einsum("rk,rd->kd", hidden, grad_rows, preferred_element_type=jnp.float32)
    grad_hidden = jnp.einsum("rd,kd->rk", grad_rows, weight, preferred_element_type=jnp.float32)
    return (grad_hidden, weight_grad)


def qkv_back(normalized_rows, grad_joined, weight):
    weight_grad = jnp.einsum(
        "rd,trk->dtk", normalized_rows, grad_joined, preferred_element_type=jnp.float32
    )
    grad_full = jnp.einsum("trk,dtk->rd", grad_joined, weight, preferred_element_type=jnp.float32)
    return (weight_grad, sum_features(grad_full))


def reduce_grads(local_grads, small_grads):
    reduced = (
        lax.psum_scatter(local_grads[0], ("tm", "clip"), scatter_dimension=0, tiled=True),
        lax.psum_scatter(local_grads[1], ("tm", "clip"), scatter_dimension=1, tiled=True),
        lax.psum_scatter(local_grads[2], ("tm", "clip"), scatter_dimension=0, tiled=True),
        lax.psum_scatter(local_grads[3], ("tm", "clip"), scatter_dimension=1, tiled=True),
        lax.psum_scatter(local_grads[4], ("tm", "clip"), scatter_dimension=0, tiled=True),
        lax.psum_scatter(local_grads[5], ("tm", "clip"), scatter_dimension=1, tiled=True),
    )
    reduced_small = lax.psum((small_grads[0], small_grads[1]), ("tm", "clip"))
    return (reduced, reduced_small)


def space_forward(normalized_rows, weight, frame_count, patches, heads_local, scale):
    joined = jnp.einsum(
        "rd,dtk->trk", normalized_rows, weight, preferred_element_type=jnp.float32
    ).astype(jnp.bfloat16)
    shape_heads = (frame_count, patches, heads_local, HEAD_DIM)
    scores = (
        jnp.einsum(
            "bshd,bthd->bhst",
            joined[0].reshape(shape_heads),
            joined[1].reshape(shape_heads),
            preferred_element_type=jnp.float32,
        )
        * scale
    )
    highest = jnp.max(scores, axis=-1, keepdims=True)
    exponent = jnp.exp(scores - highest)
    reduced_totals = jnp.sum(exponent, axis=-1, keepdims=True)
    log_total = highest + jnp.log(reduced_totals)
    attention = (exponent / reduced_totals).astype(jnp.bfloat16)
    mixed = jnp.einsum(
        "bhst,bthd->bshd",
        attention,
        joined[2].reshape(shape_heads),
        preferred_element_type=jnp.float32,
    )
    return (
        joined,
        log_total,
        mixed.astype(jnp.bfloat16).reshape(frame_count * patches, heads_local * HEAD_DIM),
    )


def space_backward(grad_mixed, joined, log_total, frame_count, patches, heads_local, scale):
    shape_heads = (frame_count, patches, heads_local, HEAD_DIM)
    queries = joined[0].reshape(shape_heads)
    key_rows = joined[1].reshape(shape_heads)
    values = joined[2].reshape(shape_heads)
    grad_out = grad_mixed.reshape(shape_heads)
    scores = (
        jnp.einsum("bshd,bthd->bhst", queries, key_rows, preferred_element_type=jnp.float32) * scale
    )
    attention = jnp.exp(scores - log_total)
    grad_values = jnp.einsum(
        "bhst,bshd->bthd",
        attention.astype(jnp.bfloat16),
        grad_out,
        preferred_element_type=jnp.float32,
    )
    grad_att = jnp.einsum("bshd,bthd->bhst", grad_out, values, preferred_element_type=jnp.float32)
    grad_scores = (
        attention * (grad_att - jnp.sum(attention * grad_att, axis=-1, keepdims=True))
    ).astype(jnp.bfloat16)
    grad_queries = (
        jnp.einsum("bhst,bthd->bshd", grad_scores, key_rows, preferred_element_type=jnp.float32)
        * scale
    )
    grad_keys = (
        jnp.einsum("bhst,bshd->bthd", grad_scores, queries, preferred_element_type=jnp.float32)
        * scale
    )
    row_count = frame_count * patches
    stacked = jnp.stack(
        [
            grad_queries.reshape(row_count, -1),
            grad_keys.reshape(row_count, -1),
            grad_values.reshape(row_count, -1),
        ]
    )
    return stacked.astype(jnp.bfloat16)


def time_scores(queries, keys_all, visible, scale):
    scores = (
        jnp.einsum("cfshd,cgshd->chfgs", queries, keys_all, preferred_element_type=jnp.float32)
        * scale
    )
    return jnp.where(visible, scores, -1e30)


def time_forward(queries, keys_all, values_all, visible, scale):
    scores = time_scores(queries, keys_all, visible, scale)
    highest = jnp.max(scores, axis=3, keepdims=True)
    exponent = jnp.exp(scores - highest)
    reduced_totals = jnp.sum(exponent, axis=3, keepdims=True)
    log_total = highest + jnp.log(reduced_totals)
    attention = (exponent / reduced_totals).astype(jnp.bfloat16)
    mixed = jnp.einsum(
        "chfgs,cgshd->cfshd", attention, values_all, preferred_element_type=jnp.float32
    )
    return (log_total, mixed.astype(jnp.bfloat16))


def time_backward(grad_mixed, queries, keys_all, values_all, visible, log_total, scale):
    grad_out = grad_mixed.reshape(queries.shape)
    scores = time_scores(queries, keys_all, visible, scale)
    attention = jnp.exp(scores - log_total)
    grad_values = jnp.einsum(
        "chfgs,cfshd->cgshd",
        attention.astype(jnp.bfloat16),
        grad_out,
        preferred_element_type=jnp.float32,
    )
    grad_att = jnp.einsum(
        "cfshd,cgshd->chfgs", grad_out, values_all, preferred_element_type=jnp.float32
    )
    grad_scores = (
        attention * (grad_att - jnp.sum(attention * grad_att, axis=3, keepdims=True))
    ).astype(jnp.bfloat16)
    grad_queries = (
        jnp.einsum("chfgs,cgshd->cfshd", grad_scores, keys_all, preferred_element_type=jnp.float32)
        * scale
    )
    grad_keys = (
        jnp.einsum("chfgs,cfshd->cgshd", grad_scores, queries, preferred_element_type=jnp.float32)
        * scale
    )
    return (grad_queries, grad_keys, grad_values)


def shards(
    tokens,
    cotangent,
    ratio,
    priority,
    frame_order,
    mask_embed,
    gains,
    qkv_space,
    out_space,
    qkv_time,
    out_time,
    w_in,
    w_out,
):
    scale = 1.0 / math.sqrt(HEAD_DIM)
    clips_local = tokens.shape[0] // MICRO
    frames_local = tokens.shape[1]
    patches = tokens.shape[2]
    cols_local = tokens.shape[3]
    frames_all = frame_order.shape[1]
    hidden_width = qkv_space.shape[0]
    joined_local = qkv_space.shape[2]
    heads_local = joined_local // HEAD_DIM
    row_count = clips_local * frames_local * patches
    gain_broadcast = gains.astype(jnp.float32)
    embed_row = mask_embed.astype(jnp.float32)
    first_frame = lax.axis_index("tm") * frames_local
    shape_local = (clips_local, frames_local, patches, joined_local)
    shape_heads = (clips_local, frames_local, patches, heads_local, HEAD_DIM)
    shape_all = (clips_local, frames_all, patches, heads_local, HEAD_DIM)
    outputs = []
    input_grads = []
    weight_total = None
    small_total = None
    for batch_index in range(MICRO):
        lower = batch_index * clips_local
        upper = lower + clips_local
        source = tokens[lower:upper].reshape(row_count, cols_local).astype(jnp.float32)
        upstream = cotangent[lower:upper].reshape(row_count, cols_local).astype(jnp.float32)
        masked = (priority[lower:upper] < ratio[lower:upper][:, None, None]).reshape(row_count)
        order_rows = frame_order[lower:upper]
        residual_stream0 = jnp.where(masked[:, None], embed_row[None, :], source)
        normalized_rows0, standardized_rows0, inverse_deviation0 = norm_forward_pass(
            residual_stream0, gain_broadcast[0], hidden_width
        )
        joined0, total0, mixed0 = space_forward(
            normalized_rows0, qkv_space, clips_local * frames_local, patches, heads_local, scale
        )
        residual_stream1 = residual_stream0 + branch_out(mixed0, out_space)
        normalized_rows1, standardized_rows1, inverse_deviation1 = norm_forward_pass(
            residual_stream1, gain_broadcast[1], hidden_width
        )
        joined1 = jnp.einsum(
            "rd,dtk->trk", normalized_rows1, qkv_time, preferred_element_type=jnp.float32
        ).astype(jnp.bfloat16)
        queries_local = joined1[0].reshape(shape_local)
        keys_local = joined1[1].reshape(shape_local)
        values_local = joined1[2].reshape(shape_local)
        keys_all, values_all = (
            lax.all_gather(keys_local, "tm", axis=1, tiled=True),
            lax.all_gather(values_local, "tm", axis=1, tiled=True),
        )
        query_order = lax.dynamic_slice_in_dim(order_rows, first_frame, frames_local, axis=1)
        time_visible = (order_rows[:, None, :] <= query_order[:, :, None])[:, None, :, :, None]
        time_q = queries_local.reshape(shape_heads)
        time_k = keys_all.reshape(shape_all)
        time_v = values_all.reshape(shape_all)
        total1, mixed_frames = time_forward(time_q, time_k, time_v, time_visible, scale)
        mixed1 = mixed_frames.reshape(row_count, joined_local)
        residual_stream2 = residual_stream1 + branch_out(mixed1, out_time)
        normalized_rows2, standardized_rows2, inverse_deviation2 = norm_forward_pass(
            residual_stream2, gain_broadcast[2], hidden_width
        )
        projected = jnp.dot(normalized_rows2, w_in, preferred_element_type=jnp.float32)
        activated, gelu_pull = jax.vjp(gelu_tanh, projected)
        hidden = activated.astype(jnp.bfloat16)
        resid3 = residual_stream2 + branch_out(hidden, w_out)
        outputs.append(
            resid3.astype(jnp.bfloat16).reshape(clips_local, frames_local, patches, cols_local)
        )
        grad3 = jnp.where(masked[:, None], upstream, 0.0)
        grad_hidden, grad_w_out = branch_back(grad3, hidden, w_out)
        grad_inner = gelu_pull(grad_hidden)[0].astype(jnp.bfloat16)
        grad_w_in = jnp.einsum(
            "rd,rk->dk", normalized_rows2, grad_inner, preferred_element_type=jnp.float32
        )
        normalized_gradient2 = sum_features(
            jnp.einsum("rk,dk->rd", grad_inner, w_in, preferred_element_type=jnp.float32)
        )
        backward_third, gain_gradient2 = norm_reverse_pass(
            normalized_gradient2,
            standardized_rows2,
            inverse_deviation2,
            gain_broadcast[2],
            hidden_width,
        )
        grad2 = grad3 + backward_third
        grad_mixed1, grad_out_time = branch_back(grad2, mixed1, out_time)
        grad_mixed_low = grad_mixed1.astype(jnp.bfloat16).reshape(shape_local)
        grad_queries, grad_keys, grad_values = time_backward(
            grad_mixed_low, time_q, time_k, time_v, time_visible, total1, scale
        )
        key_part, value_part = (
            lax.psum_scatter(
                grad_keys.reshape(clips_local, frames_all, patches, joined_local).astype(
                    jnp.bfloat16
                ),
                "tm",
                scatter_dimension=1,
                tiled=True,
            ).astype(jnp.float32),
            lax.psum_scatter(
                grad_values.reshape(clips_local, frames_all, patches, joined_local).astype(
                    jnp.bfloat16
                ),
                "tm",
                scatter_dimension=1,
                tiled=True,
            ).astype(jnp.float32),
        )
        grad_joined1 = jnp.stack(
            [
                grad_queries.reshape(row_count, joined_local),
                key_part.reshape(row_count, joined_local),
                value_part.reshape(row_count, joined_local),
            ]
        ).astype(jnp.bfloat16)
        grad_qkv_time, normalized_gradient1 = qkv_back(normalized_rows1, grad_joined1, qkv_time)
        backward_second, gain_gradient1 = norm_reverse_pass(
            normalized_gradient1,
            standardized_rows1,
            inverse_deviation1,
            gain_broadcast[1],
            hidden_width,
        )
        grad1 = grad2 + backward_second
        grad_mixed0, grad_out_space = branch_back(grad1, mixed0, out_space)
        grad_joined0 = space_backward(
            grad_mixed0.astype(jnp.bfloat16),
            joined0,
            total0,
            clips_local * frames_local,
            patches,
            heads_local,
            scale,
        )
        grad_qkv_space, normalized_gradient0 = qkv_back(normalized_rows0, grad_joined0, qkv_space)
        backward_first, gain_gradient0 = norm_reverse_pass(
            normalized_gradient0,
            standardized_rows0,
            inverse_deviation0,
            gain_broadcast[0],
            hidden_width,
        )
        grad0 = grad1 + backward_first
        input_grads.append(
            jnp.where(masked[:, None], 0.0, grad0).reshape(
                clips_local, frames_local, patches, cols_local
            )
        )
        grad_embed = jnp.sum(jnp.where(masked[:, None], grad0, 0.0), axis=0)
        gain_grads = jnp.stack([gain_gradient0, gain_gradient1, gain_gradient2])
        local_grads = (
            grad_qkv_space,
            grad_out_space,
            grad_qkv_time,
            grad_out_time,
            grad_w_in,
            grad_w_out,
        )
        small_grads = (gain_grads, grad_embed)
        reduced, reduced_small = reduce_grads(local_grads, small_grads)
        if weight_total is None:
            weight_total = reduced
            small_total = reduced_small
        else:
            weight_total = tuple((total + grad for total, grad in zip(weight_total, reduced)))
            small_total = tuple((total + grad for total, grad in zip(small_total, reduced_small)))
    return (
        jnp.concatenate(outputs, axis=0),
        jnp.concatenate(input_grads, axis=0),
        small_total[1],
        small_total[0],
        weight_total[0],
        weight_total[1],
        weight_total[2],
        weight_total[3],
        weight_total[4],
        weight_total[5],
    )


AXES = ("tm", "x", "c", "mp")
F32 = jnp.float32
BF16 = jnp.bfloat16
BLK = 256
MESH = pl.DeviceIdType.MESH


def device_pairs(move):
    pairs = []
    for y in range(2):
        for x in range(2):
            for c in range(2):
                for z in range(4):
                    there = move(y, x, c, z)
                    pairs.append(tuple(((q[0] * 2 + q[1]) * 2 + q[2]) * 4 + q[3] for q in ((y, x, c, z), there)))
    return pairs


def hop_y(v):
    return lax.ppermute(v, AXES, device_pairs(lambda y, x, c, z: (1 - y, x, c, z)))


def hop_x(v):
    return lax.ppermute(v, AXES, device_pairs(lambda y, x, c, z: (y, 1 - x, c, z)))


def hop_c(v):
    return lax.ppermute(v, AXES, device_pairs(lambda y, x, c, z: (y, x, 1 - c, z)))


def hop_z(v, shift):
    return lax.ppermute(v, AXES, device_pairs(lambda y, x, c, z: (y, x, c, (z + shift) % 4)))


def spread_pairs(r):
    def move(y, x, c, z):
        k = z ^ r
        return (y, x, k & 1, 2 * c + (k >> 1))

    return device_pairs(move)


def dot_nn(a, b):
    return lax.dot_general(a, b, (((1,), (0,)), ((), ())), preferred_element_type=F32)


def dot_nt(a, b):
    return lax.dot_general(a, b, (((1,), (1,)), ((), ())), preferred_element_type=F32)


def dot_tn(a, b):
    return lax.dot_general(a, b, (((0,), (0,)), ((), ())), preferred_element_type=F32)


def attend_pair(q, k, v, bias, scale):
    mixed, totals = [], []
    for i in range(2):
        mine = slice(i * HEAD_DIM, (i + 1) * HEAD_DIM)
        scores = dot_nt(k[:, mine], q[:, mine]) * scale
        if bias is not None:
            scores = scores + bias
        highest = jnp.max(scores, axis=0, keepdims=True)
        exponent = jnp.exp(scores - highest)
        total = jnp.sum(exponent, axis=0, keepdims=True)
        totals.append(highest + jnp.log(total))
        mixed.append(dot_tn(v[:, mine], exponent.astype(BF16)) * (1.0 / total))
    return (jnp.concatenate(mixed, axis=0).T, totals)


def attend_pair_back(q, k, v, g, totals, bias, scale):
    grads = ([], [], [])
    for i in range(2):
        mine = slice(i * HEAD_DIM, (i + 1) * HEAD_DIM)
        scores = dot_nt(k[:, mine], q[:, mine]) * scale
        if bias is not None:
            scores = scores + bias
        p = jnp.exp(scores - totals[i])
        dp = dot_nt(v[:, mine], g[:, mine])
        ds = (p * (dp - jnp.sum(p * dp, axis=0, keepdims=True))).astype(BF16)
        grads[0].append(dot_tn(k[:, mine], ds) * scale)
        grads[1].append(dot_nn(ds, q[:, mine]) * scale)
        grads[2].append(dot_nn(p.astype(BF16), g[:, mine]))
    return (
        jnp.concatenate(grads[0], axis=0).T,
        jnp.concatenate(grads[1], axis=1),
        jnp.concatenate(grads[2], axis=1),
    )


PAIR = 2 * HEAD_DIM


def enter_kernel(
    scale,
    tok, vec, qkv_hbm, out_hbm, later, feed_hbm, masked,
    wq_out, wo_out, wt, wf, joined_out, turned_out, std_out,
    mixed, total_out, inverse, resid, std_next, inverse_next, low_next, vec_out,
    rows_in, vec_in, wq, wo, normed, joined, turned, std, base, part, part_out, part_in,
    z_send, z_recv, y_send, y_recv, x_send, x_recv, p_send, p_recv, q_send, q_recv,
    t_send, t_recv, v_send, v_recv, u_send, u_recv, w_send, w_recv,
    f_send, f_recv, g_send, g_recv, n_send, n_recv, local, saved,
):
    y, x, c, z = (lax.axis_index(name) for name in AXES)
    half = wo.shape[0] // 4
    wide = 3 * half
    span = wt.shape[1] // 4
    size = wf.shape[1] // 4
    own = rows_in.shape[0]
    near_y, near_x, pair = (1 - y, x, c, z), (y, 1 - x, c, z), (y, x, 1 - c, z)
    right_z, left_z = (y, x, c, (z + 1) % 4), (y, x, c, (z + 3) % 4)

    def at(i, length):
        return pl.ds(pl.multiple_of(i * length, length), length)

    def remote(src, dst, send, recv, peer):
        return pltpu.make_async_remote_copy(
            src_ref=src, dst_ref=dst, send_sem=send, recv_sem=recv, device_id=peer, device_id_type=MESH
        )

    def start(all_copies):
        for copy in all_copies:
            copy.start()

    def landed(all_copies):
        for copy in all_copies:
            copy.wait_recv()

    def sent(all_copies):
        for copy in all_copies:
            copy.wait_send()

    core = at(c, half)
    keep = [
        pltpu.make_async_copy(
            qkv_hbm.at[j, :, core], wq.at[:, pl.ds(pl.multiple_of(z * wide + j * half, half), half)], local.at[j]
        )
        for j in range(3)
    ] + [pltpu.make_async_copy(out_hbm.at[core], wo.at[at(z, half)], local.at[3])]
    keep_later = [
        pltpu.make_async_copy(later, wt.at[:, at(z, span)], local.at[4]),
        pltpu.make_async_copy(feed_hbm.at[at(c, 4 * size)], wf.at[z], local.at[5]),
    ]
    start(keep + keep_later)

    barrier = pltpu.get_barrier_semaphore()
    for dc in range(2):
        for dz in range(4):
            if dc or dz:
                peer = (y, x, (c + dc) % 2, (z + dz) % 4)
                pl.semaphore_signal(barrier, inc=1, device_id=peer, device_id_type=MESH)
    for peer in (near_y, near_x):
        pl.semaphore_signal(barrier, inc=1, device_id=peer, device_id_type=MESH)
    pl.semaphore_wait(barrier, 9)

    def spot(dy, dx):
        return 2 * ((y + dy) % 2) + (x + dx) % 2

    def piece(dy, dx, r, split=False):
        s = (z + r) % 4
        rows = at(spot(dy, dx), BLK)
        first = pl.multiple_of(s * wide, half)
        out = wo.at[at(s, half), at(spot(dy, dx), BLK)]
        if split:
            last = pl.multiple_of(s * wide + 2 * half, half)
            return (wq.at[rows, pl.ds(first, 2 * half)], wq.at[rows, pl.ds(last, half)], out)
        return (wq.at[rows, pl.ds(first, wide)], out)

    def time_piece(dx, r):
        return wt.at[at((x + dx) % 2, 2 * BLK), at((z + r) % 4, span)]

    def feed_piece(dy, r):
        return wf.at[(z + r) % 4, at(spot(dy, 0), size)]

    def copies(parts, send, recv, peer):
        return [remote(ref, ref, send.at[i], recv.at[i], peer) for i, ref in enumerate(parts)]

    def leg(right, step):
        if right:
            return (0 if step == 0 else 4 - step), right_z, 3 - step
        return step, left_z, step + 1

    def z_copies(right, step):
        r, peer, lands = leg(right, step)
        return copies(piece(0, 0, r), z_send.at[int(right), step], z_recv.at[lands], peer)

    def time_z(right, step):
        r, peer, lands = leg(right, step)
        source = later.at[at(x, 2 * BLK)] if step == 0 else time_piece(0, r)
        return [remote(source, time_piece(0, r), u_send.at[int(right), step], u_recv.at[lands], peer)]

    def feed_z(right, step):
        r, peer, lands = leg(right, step)
        source = feed_hbm.at[at(4 * c + spot(0, 0), size)] if step == 0 else feed_piece(0, r)
        return [remote(source, feed_piece(0, r), f_send.at[int(right), step], f_recv.at[lands], peer)]

    def y_copies(r, dy=0):
        return copies(piece(dy, 0, r), y_send.at[r], y_recv.at[r], near_y)

    def x_copies(r, dx=0):
        return copies(piece(0, dx, r), x_send.at[r], x_recv.at[r], near_x)

    def corner_x(r, dx=0):
        return copies(piece(1, dx, r, split=True)[:1], p_send.at[r], p_recv.at[r], near_x)

    def corner_y(r, dy=0):
        return copies(piece(dy, 1, r, split=True)[1:], q_send.at[r], q_recv.at[r], near_y)

    def time_x(r, dx=0):
        return [remote(time_piece(dx, r), time_piece(dx, r), w_send.at[r], w_recv.at[r], near_x)]

    def feed_y(r, dy=0):
        return [remote(feed_piece(dy, r), feed_piece(dy, r), g_send.at[r], g_recv.at[r], near_y)]

    def token_copies(k):
        peer = (y, x, k % 2, 2 * c + k // 2)
        return [
            remote(tok.at[k], rows_in.at[:, at(z, BLK)], t_send.at[k], t_recv.at[z], peer),
            remote(vec, vec_in.at[:, at(z, BLK)], v_send.at[k], v_recv.at[z], peer),
        ]

    def token_local(k):
        return [
            pltpu.make_async_copy(tok.at[k], rows_in.at[:, at(z, BLK)], local.at[6]),
            pltpu.make_async_copy(vec, vec_in.at[:, at(z, BLK)], local.at[7]),
        ]

    def stays(k):
        return jnp.logical_and(2 * c + k // 2 == z, c == k % 2)

    def start_tokens(ks):
        for k in ks:
            pl.when(stays(k))(lambda k=k: start(token_local(k)))
            pl.when(jnp.logical_not(stays(k)))(lambda k=k: start(token_copies(k)))

    def each_side(j, act):
        pl.when(z >= j + 1)(lambda: act(3 - j, True))
        pl.when(z <= 2 - j)(lambda: act(j + 1, False))

    def begin(make):
        pl.when(z < 3)(lambda: start(make(True, 0)))
        pl.when(z > 0)(lambda: start(make(False, 0)))

    def onward(j, make, right):
        if j < 2:
            pl.when(z < 3 if right else z > 0)(lambda: start(make(right, j + 1)))

    def forward(j):
        def act(r, right):
            landed(copies(piece(0, 0, r), z_send.at[0, 0], z_recv.at[r], near_y))
            onward(j, z_copies, right)
            start(y_copies(r))
            start(x_copies(r))

        each_side(j, act)

    def corners(j):
        def act(r, right):
            landed(y_copies(r, 1))
            start(corner_x(r))
            landed(x_copies(r, 1))
            start(corner_y(r))

        each_side(j, act)

    def time_forward_step(j):
        def act(r, right):
            landed([remote(time_piece(0, r), time_piece(0, r), u_send.at[0, 0], u_recv.at[r], near_x)])
            onward(j, time_z, right)
            start(time_x(r))

        each_side(j, act)

    def feed_forward_step(j):
        def act(r, right):
            landed([remote(feed_piece(0, r), feed_piece(0, r), f_send.at[0, 0], f_recv.at[r], near_y)])
            onward(j, feed_z, right)
            start(feed_y(r))

        each_side(j, act)

    for copy in keep:
        copy.wait()
    begin(z_copies)
    forward(0)
    start_tokens((0, 1))
    forward(1)
    start_tokens((2, 3))
    begin(time_z)
    corners(0)
    forward(2)
    corners(1)
    for k in range(4):
        def finish_local(k=k):
            for copy in token_local(k):
                copy.wait()

        pl.when(stays(k))(finish_local)
    for s in range(4):
        def arrived(s=s):
            landed([
                remote(tok.at[0], rows_in.at[:, at(s, BLK)], t_send.at[0], t_recv.at[s], near_y),
                remote(vec, vec_in.at[:, at(s, BLK)], v_send.at[0], v_recv.at[s], near_y),
            ])

        pl.when(jnp.logical_not(jnp.logical_and(z == s, z // 2 == c)))(arrived)

    step = own // 2
    slab = 128
    vec_out[...] = vec_in[...].astype(F32)

    def first_norm(i, carry):
        rows = at(i, step)
        value = jnp.where(masked[rows] > 0.0, vec_out[0:1], rows_in[rows].astype(F32))
        base[rows] = value
        standard, inv = norm_rows(value)
        std[rows] = standard
        inverse[rows] = inv
        normed[rows] = (standard * vec_out[1:2]).astype(BF16)
        return carry

    lax.fori_loop(0, 2, first_norm, 0)
    give_normed = remote(normed.at[pl.ds(0, own)], normed.at[pl.ds(own, own)], n_send.at[0], n_recv.at[0], pair)
    give_normed.start()
    corners(2)

    def turn(i, carry):
        turned[:, at(i, slab)] = normed[at(i, slab)].T
        return carry

    lax.fori_loop(0, own // slab, turn, 0)
    for r in (1, 2, 3):
        landed(corner_x(r, 1))
        landed(corner_y(r, 1))
    saves = [
        pltpu.make_async_copy(wq, wq_out, saved.at[0]),
        pltpu.make_async_copy(wo, wo_out, saved.at[1]),
        pltpu.make_async_copy(std, std_out, saved.at[2]),
    ]
    start(saves)
    time_forward_step(0)

    def attend(i, carry):
        rows = at(i, slab)
        for h in range(wo.shape[0] // PAIR):
            q, k, v = (joined[rows, (3 * h + j) * PAIR : (3 * h + j + 1) * PAIR] for j in range(3))
            out, totals = attend_pair(q, k, v, None, scale)
            mixed[rows, h * PAIR : (h + 1) * PAIR] = out.astype(BF16)
            for j in range(2):
                total_out[i, 2 * h + j : 2 * h + j + 1, :] = totals[j]
        return carry

    def project(t):
        rows = pl.ds(t * own, own)
        joined[rows] = dot_nn(normed[rows], wq[...]).astype(BF16)

    frames = own // slab
    project(0)
    time_forward_step(1)
    begin(feed_z)
    lax.fori_loop(0, frames, attend, 0)
    part[...] = dot_nn(mixed[pl.ds(0, own)], wo[...])
    time_forward_step(2)
    give_normed.wait_recv()
    project(1)
    saves.append(pltpu.make_async_copy(joined, joined_out, saved.at[3]))
    saves[3].start()
    lax.fori_loop(frames, 2 * frames, attend, 0)
    part_out[...] = dot_nn(mixed[pl.ds(own, own)], wo[...]).astype(BF16)
    give_part = remote(part_out, part_in, n_send.at[1], n_recv.at[1], pair)
    give_part.start()
    feed_forward_step(0)
    lax.fori_loop(own // slab, 2 * own // slab, turn, 0)
    saves.append(pltpu.make_async_copy(turned, turned_out, saved.at[4]))
    saves[4].start()
    give_part.wait_recv()
    feed_forward_step(1)

    def second_norm(i, carry):
        rows = at(i, step)
        value = base[rows] + part[rows] + part_in[rows].astype(F32)
        resid[rows] = value
        standard, inv = norm_rows(value)
        std_next[rows] = standard
        inverse_next[rows] = inv
        low_next[rows] = (standard * vec_out[2:3]).astype(BF16)
        return carry

    lax.fori_loop(0, 2, second_norm, 0)
    feed_forward_step(2)

    for copy in keep_later + saves:
        copy.wait()
    give_normed.wait_send()
    give_part.wait_send()
    for r in (1, 2, 3):
        landed(time_x(r, 1))
        landed(feed_y(r, 1))
        for group in (y_copies(r), x_copies(r), corner_x(r), corner_y(r), time_x(r), feed_y(r)):
            sent(group)
    for step_z in range(3):
        for make in (z_copies, time_z, feed_z):
            pl.when(jnp.logical_and(z >= step_z, z < 3))(lambda step_z=step_z, make=make: sent(make(True, step_z)))
            pl.when(jnp.logical_and(z + step_z <= 3, z > 0))(lambda step_z=step_z, make=make: sent(make(False, step_z)))
    for k in range(4):
        pl.when(jnp.logical_not(stays(k)))(lambda k=k: sent(token_copies(k)))


def enter(tok, vec, qkv, out, later, feed_weight, masked, scale):
    own, width, half = tok.shape[1], 4 * tok.shape[2], out.shape[0] // 2
    size = feed_weight.shape[0] // 2
    dma = pltpu.SemaphoreType.DMA
    anywhere = pl.BlockSpec(memory_space=pl.ANY)
    whole = pl.BlockSpec(memory_space=pltpu.VMEM)
    heads = 4 * half // HEAD_DIM

    def low(*shape):
        return pltpu.VMEM(shape, BF16)

    def high(*shape):
        return pltpu.VMEM(shape, F32)

    shapes = [
        ((width, 12 * half), BF16), ((4 * half, width), BF16), ((width, 4 * later.shape[1]), BF16),
        ((4, size, width), BF16), ((2 * own, 12 * half), BF16), ((width, 2 * own), BF16), ((own, width), F32),
        ((2 * own, 4 * half), BF16), ((2 * own // 128, heads, 128), F32), ((own, 1), F32), ((own, width), F32),
        ((own, width), F32), ((own, 1), F32), ((own, width), BF16), ((vec.shape[0], width), F32),
    ]
    return pl.pallas_call(
        functools.partial(enter_kernel, scale),
        in_specs=[anywhere] * 6 + [whole],
        out_specs=[anywhere] * 7 + [whole] * 8,
        out_shape=[jax.ShapeDtypeStruct(shape, kind) for shape, kind in shapes],
        scratch_shapes=[
            low(own, width), low(vec.shape[0], width), low(width, 12 * half), low(4 * half, width),
            low(2 * own, width), low(2 * own, 12 * half), low(width, 2 * own), high(own, width), high(own, width),
            high(own, width), low(own, width), low(own, width),
            dma((2, 3, 2)), dma((4, 2)), dma((4, 2)), dma((4, 2)), dma((4, 2)), dma((4, 2)),
            dma((4, 1)), dma((4, 1)), dma((4, 2)), dma((4, 2)),
            dma((4,)), dma((4,)), dma((4,)), dma((4,)), dma((2, 3)), dma((4,)), dma((4,)), dma((4,)),
            dma((2, 3)), dma((4,)), dma((4,)), dma((4,)), dma((2,)), dma((2,)), dma((8,)), dma((5,)),
        ],
        compiler_params=pltpu.CompilerParams(
            collective_id=0, has_side_effects=True, vmem_limit_bytes=56 * 1024 * 1024
        ),
        cost_estimate=pl.CostEstimate(flops=10**10, transcendentals=10**6, bytes_accessed=10**8),
        name="enter",
    )(tok, vec, qkv, out, later, feed_weight, masked)


GROUP = 8
CHUNK = 32


def time_kernel(back, scale, heads, *refs):
    if back:
        (own_ref, rider_ref, joined_ref, total_ref, wide_ref, wq_ref, wo_ref, bias_ref) = refs[:8]
        (all_ref, out_ref, delta_ref, reduced_ref, rider_out) = refs[8:13]
        (half_in, half_own, line_out, line_in, half_send, half_recv, half_local, line_send, line_recv) = refs[-9:]
        refs = refs[13:-9]
    else:
        (own_ref, rider_ref, far_ref, wq_ref, wo_ref, bias_ref) = refs[:6]
        (all_ref, out_ref, mixed_ref, total_ref, delta_ref, rider_out, spread_out) = refs[6:13]
        refs = refs[13:]
    (
        held, wide, narrow, kept, core_out, core_in, near_out, near_in,
        gy_send, gy_recv, gc_send, gc_recv, gd_send, gd_recv, sc_send, sc_recv, sy_send, sy_recv,
        r_send, r_recv, r_local, out_sem, wx_send, wx_recv,
    ) = refs
    y, x, c, z = (lax.axis_index(name) for name in AXES)
    near, pair, near_x = (1 - y, x, c, z), (y, x, 1 - c, z), (y, 1 - x, c, z)
    frames = held.shape[0] // 4
    chunks = held.shape[1] // CHUNK
    width = heads * HEAD_DIM
    groups = CHUNK // GROUP

    barrier = pltpu.get_barrier_semaphore()
    for dc in range(2):
        for dz in range(4):
            if dc or dz:
                pl.semaphore_signal(barrier, inc=1, device_id=(y, x, (c + dc) % 2, (z + dz) % 4), device_id_type=MESH)
    pl.semaphore_signal(barrier, inc=1, device_id=near, device_id_type=MESH)
    pl.semaphore_signal(barrier, inc=1, device_id=near_x, device_id_type=MESH)
    pl.semaphore_wait(barrier, 9)

    def remote(src, dst, send, recv, peer):
        return pltpu.make_async_remote_copy(
            src_ref=src, dst_ref=dst, send_sem=send, recv_sem=recv, device_id=peer, device_id_type=MESH
        )

    def patches(k):
        return pl.ds(pl.multiple_of(k * CHUNK, CHUNK), CHUNK)

    def block(b, k):
        return held.at[pl.ds(b * frames, frames), patches(k)]

    def gather_y(k):
        return remote(own_ref.at[:, patches(k)], block(1, k), gy_send.at[k], gy_recv.at[k], near)

    def gather_c(k):
        return remote(own_ref.at[:, patches(k)], block(2, k), gc_send.at[k], gc_recv.at[k], pair)

    def gather_d(k):
        return remote(block(1, k), block(3, k), gd_send.at[k], gd_recv.at[k], pair)

    def scatter_c(k):
        return remote(core_out.at[k], core_in.at[k], sc_send.at[k], sc_recv.at[k], pair)

    def scatter_y(k):
        return remote(near_out.at[k], near_in.at[k], sy_send.at[k], sy_recv.at[k], near)

    def save(k):
        return pltpu.make_async_copy(held.at[:, patches(k)], all_ref.at[:, patches(k)], out_sem.at[k])

    def columns(s):
        return pl.ds(pl.multiple_of(s * BLK, BLK), BLK)

    def stays(k):
        if back:
            return jnp.logical_and(z == k, z // 2 == c)
        return jnp.logical_and(2 * c + k // 2 == z, c == k % 2)

    def ride(k):
        if back:
            src, dst = rider_ref.at[:, columns(k)], rider_out.at[2 * (z % 2) + c]
            peer, slot = (y, x, z // 2, k), 2 * (z % 2) + c
        else:
            src, dst = rider_ref.at[k], rider_out.at[:, columns(z)]
            peer, slot = (y, x, k % 2, 2 * c + k // 2), z
        return src, dst, peer, slot

    def ride_remote(k):
        src, dst, peer, slot = ride(k)
        return remote(src, dst, r_send.at[k], r_recv.at[slot], peer)

    def ride_local(k):
        src, dst, _, _ = ride(k)
        return pltpu.make_async_copy(src, dst, r_local.at[0])

    def ride_landed(k):
        if back:
            src, dst = rider_ref.at[:, columns(k)], rider_out.at[k]
        else:
            src, dst = rider_ref.at[k], rider_out.at[:, columns(k)]
        return remote(src, dst, r_send.at[k], r_recv.at[k], near)

    def from_self(k):
        if back:
            return jnp.logical_and(2 * c + k // 2 == z, c == k % 2)
        return jnp.logical_and(z == k, z // 2 == c)

    def spread_x(i, dx=0):
        r, yb = i // 2 + 1, i % 2
        size = far_ref.shape[1] // 4
        at = pl.multiple_of(size * (2 * yb + (x + dx) % 2), size)
        src = far_ref.at[(z + r) % 4, pl.ds(at, size)]
        return remote(src, spread_out.at[(z + r) % 4, pl.ds(at, size)], wx_send.at[i], wx_recv.at[i], near_x)

    gather_y(0).start()
    for k in range(chunks):
        if k > 0:
            gather_y(k).start()
        gather_c(k).start()
    def half_away(s):
        return remote(wide_ref.at[1 - x, s], half_in.at[s], half_send.at[s], half_recv.at[s], near_x)

    def half_here(s):
        return pltpu.make_async_copy(wide_ref.at[x, s], half_own.at[s], half_local.at[s])

    def line_away(r):
        return remote(line_out.at[r], line_in.at[r], line_send.at[r], line_recv.at[r], (y, x, c, (z + r) % 4))

    def halve():
        for s in range(4):
            half_away(s).wait_recv()
            half_here(s).wait()
        for r in range(4):
            s = (z + r) % 4
            whole = half_own[s].astype(F32) + half_in[s].astype(F32)
            if r == 0:
                reduced_ref[...] = whole
            else:
                line_out[r] = whole.astype(BF16)
                line_away(r).start()

    if back:
        for s in range(4):
            half_away(s).start()
            half_here(s).start()
    else:
        for i in range(6):
            spread_x(i).start()
    for k in range(4):
        pl.when(stays(k))(lambda k=k: ride_local(k).start())
        pl.when(jnp.logical_not(stays(k)))(lambda k=k: ride_remote(k).start())
    held[:frames] = own_ref[...]

    def finish(k):
        scatter_c(k).wait_recv()
        both = kept[:, patches(k)] + core_in[k].astype(F32)
        near_out[k] = both[frames:].astype(BF16)
        delta_ref[:, patches(k)] = both[:frames]
        scatter_y(k).start()

    def pass_on(k):
        gather_y(k).wait_recv()
        gather_d(k).start()

    def one_group(i, rows):
        at = pl.ds(pl.multiple_of(i * GROUP, GROUP), GROUP)
        count = 4 * frames * GROUP
        bias = bias_ref[...]
        for lo in range(0, width, PAIR):
            q, k, v = (
                wide[:, at, part * width + lo : part * width + lo + PAIR].reshape(count, PAIR).astype(BF16)
                for part in range(3)
            )
            h = lo // HEAD_DIM
            if back:
                g = narrow[:, at, lo : lo + PAIR].reshape(count, PAIR).astype(BF16)
                totals = [total_ref[rows * groups + i, h + j : h + j + 1, :] for j in range(2)]
                grads = attend_pair_back(q, k, v, g, totals, bias, scale)
                for part in range(3):
                    wide[:, at, part * width + lo : part * width + lo + PAIR] = grads[part].reshape(
                        4 * frames, GROUP, PAIR
                    )
            else:
                mixed, totals = attend_pair(q, k, v, bias, scale)
                narrow[:, at, lo : lo + PAIR] = mixed.reshape(4 * frames, GROUP, PAIR)
                for j in range(2):
                    total_ref[rows * groups + i, h + j : h + j + 1, :] = totals[j]

    def one_chunk(k, carry):
        pl.when(k + 1 < chunks)(lambda: pass_on(k + 1))
        gather_c(k).wait_recv()
        gather_d(k).wait_recv()
        count = 4 * frames * CHUNK
        lhs = held[:, patches(k)].reshape(count, held.shape[2])
        if back:
            wide[...] = joined_ref[:, patches(k)].astype(F32)
            narrow[...] = dot_nn(lhs, wo_ref[...]).astype(BF16).astype(F32).reshape(narrow.shape)
        else:
            joined = dot_nn(lhs, wq_ref[...]).astype(BF16)
            out_ref[:, patches(k)] = joined.reshape(wide.shape)
            wide[...] = joined.astype(F32).reshape(wide.shape)
        save(k).start()
        lax.fori_loop(0, groups, lambda i, carry: (one_group(i, k), carry)[1], 0)
        if back:
            grads = wide[...].astype(BF16)
            out_ref[:, patches(k)] = grads
            partial = dot_nt(grads.reshape(count, 3 * width), wq_ref[...])
        else:
            mixed = narrow[...].astype(BF16)
            mixed_ref[:, patches(k)] = mixed
            partial = dot_nt(mixed.reshape(count, width), wo_ref[...])
        partial = partial.reshape(4 * frames, CHUNK, held.shape[2])
        kept[:, patches(k)] = partial[: 2 * frames]
        core_out[k] = partial[2 * frames :].astype(BF16)
        scatter_c(k).start()
        pl.when(k > 0)(lambda: finish(k - 1))
        if back:
            pl.when(k == 1)(halve)
        return carry

    pass_on(0)
    lax.fori_loop(0, chunks, one_chunk, 0)
    finish(chunks - 1)
    for k in range(chunks):
        scatter_y(k).wait_recv()
        delta_ref[:, patches(k)] = delta_ref[:, patches(k)] + near_in[k].astype(F32)
    if back:
        for r in (1, 2, 3):
            line_away(r).wait_recv()
            reduced_ref[...] = reduced_ref[...] + line_in[r].astype(F32)
        for r in (1, 2, 3):
            line_away(r).wait_send()
        for s in range(4):
            half_away(s).wait_send()
    for k in range(chunks):
        for copy in (gather_y(k), gather_c(k), gather_d(k), scatter_c(k), scatter_y(k)):
            copy.wait_send()
        save(k).wait()
    if not back:
        for i in range(6):
            spread_x(i, 1).wait_recv()
            spread_x(i).wait_send()
    for k in range(4):
        pl.when(stays(k))(lambda k=k: ride_local(k).wait())
        pl.when(jnp.logical_not(stays(k)))(lambda k=k: ride_remote(k).wait_send())
        pl.when(jnp.logical_not(from_self(k)))(lambda k=k: ride_landed(k).wait_recv())


def time_call(back, own, rider, saved, wq, wo, bias, scale):
    frames, patches, features = own.shape
    width = wo.shape[1]
    heads = width // HEAD_DIM
    chunks = patches // CHUNK
    rows = 4 * frames * GROUP
    dma = pltpu.SemaphoreType.DMA
    anywhere = pl.BlockSpec(memory_space=pl.ANY)
    whole = pl.BlockSpec(memory_space=pltpu.VMEM)
    out_shape = [
        jax.ShapeDtypeStruct((4 * frames, patches, features), BF16),
        jax.ShapeDtypeStruct((4 * frames, patches, 3 * width), BF16),
    ]
    if not back:
        out_shape += [
            jax.ShapeDtypeStruct((4 * frames, patches, width), BF16),
            jax.ShapeDtypeStruct((patches // GROUP, heads, rows), F32),
        ]
    rider_shape = (4, frames * patches, BLK) if back else (frames * patches, features)
    out_shape += [
        jax.ShapeDtypeStruct((frames, patches, features), F32),
        jax.ShapeDtypeStruct(rider_shape, BF16),
    ]
    held = 2
    half = saved[2].shape[1:] if back else None
    if back:
        out_shape.insert(-1, jax.ShapeDtypeStruct(half[1:], F32))
    else:
        out_shape.append(jax.ShapeDtypeStruct(saved[0].shape, BF16))
        held = 3
    return pl.pallas_call(
        functools.partial(time_kernel, back, scale, heads),
        in_specs=[whole, anywhere] + ([whole, whole, anywhere] if back else [anywhere]) + [whole] * 3,
        out_specs=[anywhere] + [whole] * (len(out_shape) - held) + [anywhere] * (held - 1),
        out_shape=out_shape,
        scratch_shapes=[
            pltpu.VMEM((4 * frames, patches, features), BF16),
            pltpu.VMEM((4 * frames, CHUNK, 3 * width), F32),
            pltpu.VMEM((4 * frames, CHUNK, width), F32),
            pltpu.VMEM((2 * frames, patches, features), F32),
            pltpu.VMEM((chunks, 2 * frames, CHUNK, features), BF16),
            pltpu.VMEM((chunks, 2 * frames, CHUNK, features), BF16),
            pltpu.VMEM((chunks, frames, CHUNK, features), BF16),
            pltpu.VMEM((chunks, frames, CHUNK, features), BF16),
        ]
        + [dma((chunks,))] * 10
        + [dma((4,)), dma((4,)), dma((1,)), dma((chunks,))]
        + [dma((6,))] * 2
        + ([pltpu.VMEM(half, BF16)] * 4 + [dma((4,))] * 5 if back else []),
        compiler_params=pltpu.CompilerParams(
            collective_id=2 if back else 1, has_side_effects=True, vmem_limit_bytes=48 * 1024 * 1024
        ),
        cost_estimate=pl.CostEstimate(flops=10**10, transcendentals=10**6, bytes_accessed=10**8),
        name="time_back" if back else "time_forward",
    )(own, rider, *saved, wq, wo, bias)


def feed_kernel(
    resid, delta, upstream, masked, gain, w_in_hbm, w_out_hbm, w_far_hbm,
    half_in_hbm, half_out_hbm, grad_out, low_out, rows_out, gain_out,
    w_in, w_out, standard, inverse, normed, grads, normed_t, grads_t, hidden, pulled, g_in, g_out, back, ahead,
    back_out, back_in, ahead_out, ahead_in, from_x, from_y,
    w_sem, g_sem, n_send, n_recv, b_send, b_recv, hx_send, hx_recv, hy_send, hy_recv,
):
    y, x, c, z = (lax.axis_index(name) for name in AXES)
    pair, near_y, near_x = (y, x, 1 - c, z), (1 - y, x, c, z), (y, 1 - x, c, z)
    own = resid.shape[0]
    step = own // 2
    slab = 128

    def fetch(s, far):
        size = w_out.shape[1] // 4
        copies = [pltpu.make_async_copy(w_in_hbm.at[s], w_in.at[s], w_sem.at[0, s])]
        for i in range(4):
            rows = pl.ds(pl.multiple_of(size * (2 * (i // 2) + (x + i % 2) % 2), size), size)
            source = w_far_hbm if far and i % 2 else w_out_hbm
            copies.append(pltpu.make_async_copy(source.at[s, rows], w_out.at[s, rows], w_sem.at[1 + i, s]))
        return copies

    def fetch_now(s, far):
        for copy in fetch(s, far):
            copy.start()

    for s in range(4):
        pl.when(z == s)(lambda s=s: fetch_now(s, False))
        pl.when(z != s)(lambda s=s: fetch_now(s, True))
    barrier = pltpu.get_barrier_semaphore()
    for peer in (pair, near_y, near_x):
        pl.semaphore_signal(barrier, inc=1, device_id=peer, device_id_type=MESH)

    def remote(src, dst, send, recv, peer=pair):
        return pltpu.make_async_remote_copy(
            src_ref=src, dst_ref=dst, send_sem=send, recv_sem=recv, device_id=peer, device_id_type=MESH
        )

    def block(yb, xb):
        return pl.ds(pl.multiple_of(BLK * (2 * yb + xb), BLK), BLK)

    def away_x(s, i):
        return remote(g_out.at[s, block(i, 1 - x)], from_x.at[i, s], hx_send.at[i, s], hx_recv.at[i, s], near_x)

    def away_y(s, i):
        return remote(g_in.at[s, block(1 - y, i)], from_y.at[i, s], hy_send.at[i, s], hy_recv.at[i, s], near_y)

    def keep(s, i):
        return (
            pltpu.make_async_copy(g_out.at[s, block(i, x)], half_out_hbm.at[i, s], g_sem.at[0, i, s]),
            pltpu.make_async_copy(g_in.at[s, block(y, i)], half_in_hbm.at[i, s], g_sem.at[1, i, s]),
        )

    def combine(s):
        for i in range(2):
            away_x(s, i).wait_recv()
            g_out[s, block(i, x)] = (g_out[s, block(i, x)].astype(F32) + from_x[i, s].astype(F32)).astype(BF16)
            away_y(s, i).wait_recv()
            g_in[s, block(y, i)] = (g_in[s, block(y, i)].astype(F32) + from_y[i, s].astype(F32)).astype(BF16)
            for copy in keep(s, i):
                copy.start()

    def at(i, size):
        return pl.ds(pl.multiple_of(i * size, size), size)

    def prepare(i, carry):
        rows = at(i, step)
        grads[rows] = jnp.where(masked[rows] > 0.0, upstream[rows].astype(F32), 0.0).astype(BF16)
        std, inv = norm_rows(resid[rows] + delta[rows])
        standard[rows] = std
        inverse[rows] = inv
        normed[rows] = (std * gain[...]).astype(BF16)
        return carry

    lax.fori_loop(0, 2, prepare, 0)
    pl.semaphore_wait(barrier, 3)
    mine, theirs = pl.ds(0, own), pl.ds(own, own)
    give_grads = remote(grads.at[mine], grads.at[theirs], n_send.at[0], n_recv.at[0])
    give_normed = remote(normed.at[mine], normed.at[theirs], n_send.at[1], n_recv.at[1])
    give_normed.start()
    give_grads.start()

    def turn(i, carry):
        rows = at(i, slab)
        normed_t[:, rows] = normed[rows].T
        grads_t[:, rows] = grads[rows].T
        return carry

    lax.fori_loop(0, own // slab, turn, 0)
    back[...] = jnp.zeros_like(back)
    ahead[...] = jnp.zeros_like(ahead)
    rate = math.sqrt(2.0 / math.pi)

    def rows_step(s, rows):
        inner = dot_nn(normed[rows], w_in[s])
        square = inner * inner
        bend = jnp.tanh(rate * inner * (1.0 + 0.044715 * square))
        hidden[rows] = (0.5 * inner * (1.0 + bend)).astype(BF16)
        slope = 0.5 * (1.0 + bend) + 0.5 * inner * (1.0 - bend * bend) * (rate * (1.0 + 3.0 * 0.044715 * square))
        pulled[rows] = (dot_nt(grads[rows], w_out[s]) * slope).astype(BF16)
        ahead[rows] = ahead[rows] + dot_nn(hidden[rows], w_out[s])
        back[rows] = back[rows] + dot_nt(pulled[rows], w_in[s])

    def meet():
        give_normed.wait_recv()
        give_grads.wait_recv()
        lax.fori_loop(own // slab, 2 * own // slab, turn, 0)

    def one_piece(s, carry):
        for copy in fetch(s, False):
            copy.wait()

        def one_half(t, carry):
            pl.when(jnp.logical_and(s == 0, t == 1))(meet)
            rows_step(s, at(t, own))
            return carry

        lax.fori_loop(0, 2, one_half, 0)
        g_out[s] = dot_nn(grads_t[...], hidden[...]).astype(BF16)
        g_in[s] = dot_nn(normed_t[...], pulled[...]).astype(BF16)
        for i in range(2):
            away_x(s, i).start()
            away_y(s, i).start()
        return carry

    lax.fori_loop(0, 4, one_piece, 0)
    back_out[...] = back[theirs].astype(BF16)
    give_back = remote(back_out, back_in, b_send.at[0], b_recv.at[0])
    give_back.start()
    ahead_out[...] = ahead[theirs].astype(BF16)
    give_ahead = remote(ahead_out, ahead_in, b_send.at[1], b_recv.at[1])
    give_ahead.start()
    give_back.wait_recv()

    def finish(i, total):
        rows = at(i, step)
        grad = back[rows] + back_in[rows].astype(F32)
        std = standard[rows]
        inner = grad * gain[...]
        mean = jnp.mean(inner, axis=-1, keepdims=True)
        along = jnp.mean(inner * std, axis=-1, keepdims=True)
        full = grads[rows].astype(F32) + (inner - mean - std * along) * inverse[rows]
        grad_out[rows] = full
        low_out[rows] = full.astype(BF16)
        return total + jnp.sum(grad * std, axis=0, keepdims=True)

    gain_out[...] = lax.fori_loop(0, 2, finish, jnp.zeros((1, resid.shape[1]), F32))
    give_ahead.wait_recv()

    def emit(i, carry):
        rows = at(i, step)
        rows_out[rows] = (resid[rows] + delta[rows] + ahead[rows] + ahead_in[rows].astype(F32)).astype(BF16)
        return carry

    lax.fori_loop(0, 2, emit, 0)
    lax.fori_loop(0, 4, lambda s, carry: (combine(s), carry)[1], 0)
    for copy in (give_normed, give_grads, give_back, give_ahead):
        copy.wait_send()
    for s in range(4):
        for i in range(2):
            away_x(s, i).wait_send()
            away_y(s, i).wait_send()
            for copy in keep(s, i):
                copy.wait()


def feed(resid, delta, upstream, masked, gain, w_in, w_out, w_far):
    own, features = resid.shape
    units = w_in.shape[2]
    dma = pltpu.SemaphoreType.DMA
    anywhere = pl.BlockSpec(memory_space=pl.ANY)
    whole = pl.BlockSpec(memory_space=pltpu.VMEM)

    def low(*shape):
        return pltpu.VMEM(shape, BF16)

    def high(*shape):
        return pltpu.VMEM(shape, F32)

    return pl.pallas_call(
        feed_kernel,
        in_specs=[whole] * 5 + [anywhere] * 3,
        out_specs=[anywhere] * 2 + [whole] * 4,
        out_shape=[
            jax.ShapeDtypeStruct((2, 4, BLK, units), BF16),
            jax.ShapeDtypeStruct((2, 4, BLK, units), BF16),
            jax.ShapeDtypeStruct((own, features), F32),
            jax.ShapeDtypeStruct((own, features), BF16),
            jax.ShapeDtypeStruct((own, features), BF16),
            jax.ShapeDtypeStruct((1, features), F32),
        ],
        scratch_shapes=[
            low(4, features, units), low(4, units, features), high(own, features), high(own, 1),
            low(2 * own, features), low(2 * own, features), low(features, 2 * own), low(features, 2 * own),
            low(2 * own, units), low(2 * own, units), low(4, features, units), low(4, features, units),
            high(2 * own, features), high(2 * own, features),
            low(own, features), low(own, features), low(own, features), low(own, features),
            low(2, 4, BLK, units), low(2, 4, BLK, units),
            dma((5, 4)), dma((2, 2, 4)), dma((2,)), dma((2,)), dma((2,)), dma((2,)),
            dma((2, 4)), dma((2, 4)), dma((2, 4)), dma((2, 4)),
        ],
        compiler_params=pltpu.CompilerParams(
            collective_id=4, has_side_effects=True, vmem_limit_bytes=60 * 1024 * 1024
        ),
        cost_estimate=pl.CostEstimate(flops=26 * 10**9, transcendentals=2 * 10**6, bytes_accessed=10**8),
        name="feed",
    )(resid, delta, upstream, masked, gain, w_in, w_out, w_far)


def leave_kernel(
    scale,
    part_hbm, next_hbm, grad_hbm, out_hbm, joined_hbm, mixed_hbm, lhs_hbm, weight_hbm, std_hbm, time_hbm, feed_hbm, feed_in_hbm,
    totals, inverse_next, inverse, masked, gain_next, gain, small_in,
    kept_out, landed_out, feed_kept, feed_landed, time_out, rows_out, small_out,
    part, std, base, w_out, dj, mixed, lhs, weight, low_grads, turned, dmixed, go,
    t_own, t_in, tz_out, tz_in, t_total, ty_out, ty_in, tc_out, tc_in,
    f_own, f_in, fz_out, fz_in, f_total, f_other, fc_out, fc_in,
    grads, a1_out, a1_in, b1_out, b1_in, a2_out, a2_in, b2_out, b2_in, z_out, z_in,
    half_out, half_in, ready, core_out, core_in, sums, sum_out, sum_in, share_in,
    a1_send, a1_recv, b1_send, b1_recv, a2_send, a2_recv, b2_send, b2_recv, z_send, z_recv,
    h_send, h_recv, r_send, r_recv, c_send, c_recv, s_send, s_recv, p_send, p_recv, local,
    g_send, g_recv, tx_send, tx_recv, tz_send, tz_recv, ty_send, ty_recv, fy_send, fy_recv, fz_send, fz_recv, t_local, f_local, fetched,
):
    y, x, c, z = (lax.axis_index(name) for name in AXES)
    near_y, near_x, pair = (1 - y, x, c, z), (y, 1 - x, c, z), (y, x, 1 - c, z)
    own = std.shape[0]
    third = go.shape[1] // 4
    wide = 3 * third
    two = 2 * third
    slab = 128

    fetches = [
        pltpu.make_async_copy(src, dst, fetched.at[i])
        for i, (src, dst) in enumerate((
            (part_hbm, part), (next_hbm, std), (grad_hbm, base), (out_hbm, w_out), (joined_hbm, dj), (mixed_hbm, mixed),
            (lhs_hbm, lhs), (weight_hbm, weight), (feed_in_hbm, f_other),
        ))
    ]
    for copy in fetches:
        copy.start()
    fetch_std = pltpu.make_async_copy(std_hbm, std, fetched.at[9])

    barrier = pltpu.get_barrier_semaphore()
    for dc in range(2):
        for dz in range(4):
            if dc or dz:
                pl.semaphore_signal(barrier, inc=1, device_id=(y, x, (c + dc) % 2, (z + dz) % 4), device_id_type=MESH)
    for peer in (near_y, near_x):
        pl.semaphore_signal(barrier, inc=1, device_id=peer, device_id_type=MESH)
    pl.semaphore_wait(barrier, 9)

    def remote(src, dst, send, recv, peer):
        return pltpu.make_async_remote_copy(
            src_ref=src, dst_ref=dst, send_sem=send, recv_sem=recv, device_id=peer, device_id_type=MESH
        )

    def at(i, length):
        return pl.ds(pl.multiple_of(i * length, length), length)

    def along(r):
        return (y, x, c, (z + r) % 4)

    def time_x(yb):
        return remote(time_hbm.at[at(2 * yb + 1 - x, BLK)], t_in.at[yb], tx_send.at[yb], tx_recv.at[yb], near_x)

    def time_keep(yb):
        return pltpu.make_async_copy(time_hbm.at[at(2 * yb + x, BLK)], t_own.at[yb], t_local.at[yb])

    def time_z(r):
        return remote(tz_out.at[r], tz_in.at[r], tz_send.at[r], tz_recv.at[r], along(r))

    def feed_y(r):
        s = (z + r) % 4
        return remote(feed_hbm.at[1 - y, s], f_in.at[r], fy_send.at[r], fy_recv.at[r], near_y)

    def feed_keep(r):
        return pltpu.make_async_copy(feed_hbm.at[y, (z + r) % 4], f_own.at[r], f_local.at[r])

    def feed_z(r):
        return remote(fz_out.at[r], fz_in.at[r], fz_send.at[r], fz_recv.at[r], along(r))

    for r in (1, 2, 3, 0):
        feed_y(r).start()
        feed_keep(r).start()
    for yb in range(2):
        time_x(yb).start()
        time_keep(yb).start()

    def feed_step(r):
        feed_y(r).wait_recv()
        feed_keep(r).wait()
        total = f_own[r].astype(F32) + f_in[r].astype(F32)
        if r == 0:
            f_total[...] = total
        else:
            fz_out[r] = total.astype(BF16)
            feed_z(r).start()

    def time_step():
        for yb in range(2):
            time_x(yb).wait_recv()
            time_keep(yb).wait()
        for r in (1, 2, 3, 0):
            piece_at = at((z + r) % 4, BLK)
            for yb in range(2):
                total = t_own[yb, :, piece_at].astype(F32) + t_in[yb, :, piece_at].astype(F32)
                if r == 0:
                    t_total[yb] = total
                else:
                    tz_out[r, yb] = total.astype(BF16)
            if r:
                time_z(r).start()

    step = own // 2
    for copy in fetches[:3]:
        copy.wait()

    def norm_back(grad, standard, weights, inv):
        inner = grad * weights
        mean = jnp.mean(inner, axis=-1, keepdims=True)
        slope = jnp.mean(inner * standard, axis=-1, keepdims=True)
        return (inner - mean - standard * slope) * inv

    def after_time(i, total):
        rows = at(i, step)
        grad, standard = part[rows], std[rows]
        full = base[rows] + norm_back(grad, standard, gain_next[...], inverse_next[rows])
        base[rows] = full
        low_grads[rows] = full.astype(BF16)
        return total + jnp.sum(grad * standard, axis=0, keepdims=True)

    zero = jnp.zeros((1, std.shape[1]), F32)
    next_grad = lax.fori_loop(0, 2, after_time, zero)
    give = remote(low_grads.at[pl.ds(0, own)], low_grads.at[pl.ds(own, own)], g_send.at[0], g_recv.at[0], pair)
    give.start()
    fetch_std.start()
    for copy in fetches[3:6]:
        copy.wait()

    def attend(i, carry):
        rows = at(i, slab)
        for h in range(mixed.shape[1] // PAIR):
            places = [pl.ds((3 * h + j) * PAIR, PAIR) for j in range(3)]
            q, k, v = (dj[rows, place] for place in places)
            lines = [totals[i, 2 * h + j : 2 * h + j + 1, :] for j in range(2)]
            found = attend_pair_back(q, k, v, dmixed[rows, h * PAIR : (h + 1) * PAIR], lines, None, scale)
            for place, value in zip(places, found):
                dj[rows, place] = value.astype(BF16)
        return carry

    def turn(i, carry):
        turned[:, at(i, slab)] = low_grads[at(i, slab)].T
        return carry

    def attend_half(t):
        rows = pl.ds(t * own, own)
        dmixed[rows] = dot_nt(low_grads[rows], w_out[...]).astype(BF16)
        lax.fori_loop(t * own // slab, (t + 1) * own // slab, attend, 0)
        lax.fori_loop(t * own // slab, (t + 1) * own // slab, turn, 0)

    attend_half(0)
    feed_step(1)
    feed_step(2)
    give.wait_recv()
    attend_half(1)
    feed_step(3)
    time_step()
    feed_step(0)
    for copy in fetches[6:]:
        copy.wait()
    go[...] = dot_nn(turned[...], mixed[...]).astype(BF16)

    def block(yb, xb):
        return pl.ds(pl.multiple_of(BLK * (2 * yb + xb), BLK), BLK)

    def a1(i):
        return remote(a1_out.at[i], a1_in.at[i], a1_send.at[i], a1_recv.at[i], near_x)

    def b1(i):
        return remote(b1_out.at[i], b1_in.at[i], b1_send.at[i], b1_recv.at[i], near_y)

    def a2(i):
        return remote(a2_out.at[i], a2_in.at[i], a2_send.at[i], a2_recv.at[i], near_y)

    def b2(i):
        return remote(b2_out.at[i], b2_in.at[i], b2_send.at[i], b2_recv.at[i], near_x)

    def to_z(r):
        return remote(z_out.at[r], z_in.at[r], z_send.at[r], z_recv.at[r], along(r))

    def piece(i, carry):
        s = (z + i + 1) % 4
        made = dot_nn(lhs[...], dj[:, pl.ds(pl.multiple_of(s * wide, third), wide)])
        grads[i, :, :wide] = made
        grads[i, :, wide:] = go[:, pl.ds(pl.multiple_of(s * third, third), third)].astype(F32)
        for b in range(2):
            a1_out[i, b] = grads[i, block(b, 1 - x), :two].astype(BF16)
            b1_out[i, b] = grads[i, block(1 - y, b), two:].astype(BF16)
        a1(i).start()
        b1(i).start()
        return carry

    lax.fori_loop(0, 4, piece, 0)

    def second(i):
        a1(i).wait_recv()
        a2_out[i] = (grads[i, block(1 - y, x), :two] + a1_in[i, 1 - y].astype(F32)).astype(BF16)
        a2(i).start()
        b1(i).wait_recv()
        b2_out[i] = (grads[i, block(y, 1 - x), two:] + b1_in[i, 1 - x].astype(F32)).astype(BF16)
        b2(i).start()
        grads[i, block(y, x), :two] = grads[i, block(y, x), :two] + a1_in[i, y].astype(F32)
        grads[i, block(y, x), two:] = grads[i, block(y, x), two:] + b1_in[i, x].astype(F32)

    def third_step(i):
        a2(i).wait_recv()
        b2(i).wait_recv()
        grads[i, block(y, x), :two] = grads[i, block(y, x), :two] + a2_in[i].astype(F32)
        grads[i, block(y, x), two:] = grads[i, block(y, x), two:] + b2_in[i].astype(F32)
        if i < 3:
            z_out[i + 1] = grads[i, block(y, x), :].astype(BF16)
            to_z(i + 1).start()

    def away(i, carry):
        rows = pl.ds(pl.multiple_of(own + i * step, step), step)
        half_out[pl.ds(pl.multiple_of(i * step, step), step)] = dot_nt(dj[rows], weight[...]).astype(BF16)
        return carry

    lax.fori_loop(0, 2, away, 0)
    swap = remote(half_out, half_in, h_send.at[0], h_recv.at[0], pair)
    swap.start()
    second(0)
    fetch_std.wait()
    sums[...] = small_in[...]
    sums[1:2] = next_grad
    swap.wait_recv()

    def home(i, totals):
        rows = pl.ds(pl.multiple_of(i * step, step), step)
        grad = dot_nt(dj[rows], weight[...]) + half_in[rows].astype(F32)
        standard = std[rows]
        full = base[rows] + norm_back(grad, standard, gain[...], inverse[rows])
        hide = masked[rows] > 0.0
        ready[rows] = jnp.where(hide, 0.0, full).astype(BF16)
        return (
            totals[0] + jnp.sum(grad * standard, axis=0, keepdims=True),
            totals[1] + jnp.sum(jnp.where(hide, full, 0.0), axis=0, keepdims=True),
        )

    gain_grad, embed_grad = lax.fori_loop(0, 2, home, (zero, zero))
    sums[0:1] = gain_grad
    sums[3:4] = embed_grad

    def columns(s):
        return pl.ds(pl.multiple_of(s * BLK, BLK), BLK)

    def stays(k):
        return jnp.logical_and(z == k, z // 2 == c)

    def ride(k):
        slot = 2 * (z % 2) + c
        return remote(ready.at[:, columns(k)], rows_out.at[slot], r_send.at[k], r_recv.at[slot], (y, x, z // 2, k))

    def ride_local(k):
        return pltpu.make_async_copy(ready.at[:, columns(k)], rows_out.at[2 * (z % 2) + c], local.at[3])

    for k in range(4):
        pl.when(stays(k))(lambda k=k: ride_local(k).start())
        pl.when(jnp.logical_not(stays(k)))(lambda k=k: ride(k).start())

    def share(h):
        peer = (pair, near_y, near_x)[h]
        return remote(sum_out.at[h], sum_in.at[h], s_send.at[h], s_recv.at[h], peer)

    def begin_share(h):
        sum_out[h] = sums[...]
        share(h).start()

    def end_share(h):
        share(h).wait_recv()
        sums[...] = sums[...] + sum_in[h]

    begin_share(0)
    second(1)
    third_step(0)
    end_share(0)
    begin_share(1)
    second(2)
    third_step(1)
    end_share(1)
    begin_share(2)
    second(3)
    third_step(2)
    end_share(2)
    sum_out[3] = sums[...]

    def deal(r):
        s = (z + r) % 4
        return remote(sum_out.at[3, :, columns(s)], share_in.at[r], p_send.at[r], p_recv.at[r], (y, x, c, s))

    for r in (1, 2, 3):
        deal(r).start()
    third_step(3)
    parity = BLK // 2

    for r in (1, 2, 3):
        time_z(r).wait_recv()
        t_total[...] = t_total[...] + tz_in[r].astype(F32)
    ty_out[...] = t_total[1 - y].astype(BF16)
    swap_y = remote(ty_out, ty_in, ty_send.at[0], ty_recv.at[0], near_y)
    swap_y.start()
    for r in (1, 2, 3):
        feed_z(r).wait_recv()
        f_total[...] = f_total[...] + fz_in[r].astype(F32)
    fc_out[0] = f_other[at(1 - c, parity)].astype(BF16)
    fc_out[1] = f_total[at(1 - c, parity)].astype(BF16)
    swap_feed = remote(fc_out, fc_in, c_send.at[1], c_recv.at[1], pair)
    swap_feed.start()
    feed_kept[0] = f_other[at(c, parity)]
    feed_kept[1] = f_total[at(c, parity)]
    swap_y.wait_recv()
    tc_out[0] = t_total[y, at(1 - c, parity)].astype(BF16)
    tc_out[1] = ty_in[at(1 - c, parity)]
    swap_time = remote(tc_out, tc_in, c_send.at[2], c_recv.at[2], pair)
    swap_time.start()
    time_out[0, 0] = t_total[y, at(c, parity)]
    time_out[0, 1] = ty_in[at(c, parity)].astype(F32)
    for r in (1, 2, 3):
        to_z(r).wait_recv()
    total = grads[3, block(y, x), :]
    for r in (1, 2, 3):
        total = total + z_in[r].astype(F32)
    grads[3, block(y, x), :] = total
    rows = BLK // 2

    def core_rows(core):
        return pl.ds(pl.multiple_of(BLK * (2 * y + x) + rows * core, rows), rows)

    core_out[...] = grads[3, core_rows(1 - c), :].astype(BF16)
    last = remote(core_out, core_in, c_send.at[0], c_recv.at[0], pair)
    last.start()
    kept_out[...] = grads[3, core_rows(c), :]
    result = sums[:, columns(z)]
    for r in (1, 2, 3):
        deal(r).wait_recv()
        result = result + share_in[r]
    small_out[...] = result
    swap_feed.wait_recv()
    feed_landed[...] = fc_in[...].astype(F32)
    swap_time.wait_recv()
    time_out[1] = tc_in[...].astype(F32)
    last.wait_recv()
    landed_out[...] = core_in[...].astype(F32)

    for copy in (last, swap, give, swap_y, swap_feed, swap_time):
        copy.wait_send()
    for yb in range(2):
        time_x(yb).wait_send()
    for r in range(4):
        feed_y(r).wait_send()
    for r in (1, 2, 3):
        time_z(r).wait_send()
        feed_z(r).wait_send()
    for i in range(4):
        for copy in (a1(i), b1(i), a2(i), b2(i)):
            copy.wait_send()
    for r in (1, 2, 3):
        to_z(r).wait_send()
        deal(r).wait_send()
    for h in range(3):
        share(h).wait_send()
    for k in range(4):
        pl.when(stays(k))(lambda k=k: ride_local(k).wait())
        pl.when(jnp.logical_not(stays(k)))(lambda k=k: ride(k).wait_send())
        from_self = jnp.logical_and(2 * c + k // 2 == z, c == k % 2)

        def landed(k=k):
            remote(ready.at[:, columns(k)], rows_out.at[k], r_send.at[k], r_recv.at[k], near_y).wait_recv()

        pl.when(jnp.logical_not(from_self))(landed)


def leave(
    part, std_next, grad, w_out, joined, mixed, lhs, weight, std, g_time, g_out, g_in,
    totals, inverse_next, inverse, masked, gain_next, gain, small, scale,
):
    own, features = std.shape
    cols4 = mixed.shape[1]
    quarter = cols4 // 4
    units = g_in.shape[1]
    dma = pltpu.SemaphoreType.DMA
    anywhere = pl.BlockSpec(memory_space=pl.ANY)
    whole = pl.BlockSpec(memory_space=pltpu.VMEM)
    parity = BLK // 2

    def low(*shape):
        return pltpu.VMEM(shape, BF16)

    def high(*shape):
        return pltpu.VMEM(shape, F32)

    return pl.pallas_call(
        functools.partial(leave_kernel, scale),
        in_specs=[anywhere] * 12 + [whole] * 7,
        out_specs=[whole] * 5 + [anywhere, whole],
        out_shape=[
            jax.ShapeDtypeStruct((parity, cols4), F32),
            jax.ShapeDtypeStruct((parity, cols4), F32),
            jax.ShapeDtypeStruct((2, parity, units), F32),
            jax.ShapeDtypeStruct((2, parity, units), F32),
            jax.ShapeDtypeStruct((2, 2, parity, BLK), F32),
            jax.ShapeDtypeStruct((4, own, BLK), BF16),
            jax.ShapeDtypeStruct((8, BLK), F32),
        ],
        scratch_shapes=[
            high(own, features), high(own, features), high(own, features), low(*w_out.shape), low(*joined.shape),
            low(*mixed.shape), low(*lhs.shape), low(*weight.shape), low(2 * own, features), low(features, 2 * own),
            low(*mixed.shape), low(features, cols4),
            low(2, BLK, features), low(2, BLK, features), low(4, 2, BLK, BLK), low(4, 2, BLK, BLK), high(2, BLK, BLK),
            low(BLK, BLK), low(BLK, BLK), low(2, parity, BLK), low(2, parity, BLK),
            low(4, BLK, units), low(4, BLK, units), low(4, BLK, units), low(4, BLK, units),
            high(BLK, units), high(BLK, units), low(2, parity, units), low(2, parity, units),
            high(4, features, cols4),
            low(4, 2, BLK, 2 * quarter), low(4, 2, BLK, 2 * quarter), low(4, 2, BLK, 2 * quarter), low(4, 2, BLK, 2 * quarter),
            low(4, BLK, 2 * quarter), low(4, BLK, 2 * quarter), low(4, BLK, 2 * quarter), low(4, BLK, 2 * quarter),
            low(4, BLK, cols4), low(4, BLK, cols4),
            low(own, features), low(own, features), low(own, features),
            low(parity, cols4), low(parity, cols4),
            high(8, features), high(4, 8, features), high(3, 8, features), high(4, 8, BLK),
        ]
        + [dma((4,))] * 10
        + [dma((1,)), dma((1,)), dma((4,)), dma((4,)), dma((3,)), dma((3,)), dma((3,)), dma((3,)), dma((4,)), dma((4,)), dma((4,))]
        + [dma((1,)), dma((1,)), dma((2,)), dma((2,)), dma((4,)), dma((4,)), dma((1,)), dma((1,))]
        + [dma((4,)), dma((4,)), dma((4,)), dma((4,)), dma((2,)), dma((4,)), dma((10,))],
        compiler_params=pltpu.CompilerParams(
            collective_id=3, has_side_effects=True, vmem_limit_bytes=62 * 1024 * 1024
        ),
        cost_estimate=pl.CostEstimate(flops=2 * 10**10, transcendentals=10**6, bytes_accessed=10**8),
        name="leave",
    )(
        part, std_next, grad, w_out, joined, mixed, lhs, weight, std, g_time, g_out, g_in,
        totals, inverse_next, inverse, masked, gain_next, gain, small,
    )


def tie(*values):
    return lax.optimization_barrier(values)


def norm_rows(resid):
    mean = jnp.mean(resid, axis=-1, keepdims=True)
    centered = resid - mean
    inverse = lax.rsqrt(jnp.mean(centered * centered, axis=-1, keepdims=True) + eps_norm)
    return (centered * inverse, inverse)


def norm_rows_back(grad, standardized, inverse, gain):
    gain_grad = jnp.sum(grad * standardized, axis=0)
    inner = grad * gain
    mean = jnp.mean(inner, axis=-1, keepdims=True)
    along = jnp.mean(inner * standardized, axis=-1, keepdims=True)
    return ((inner - mean - standardized * along) * inverse, gain_grad)


def cols(parts):
    return jnp.concatenate(parts, axis=1)


def rows_of(parts):
    return jnp.concatenate(parts, axis=0)


def token_parallel(
    tokens,
    cotangent,
    ratio,
    priority,
    frame_order,
    mask_embed,
    gains,
    qkv_space,
    out_space,
    qkv_time,
    out_time,
    w_in,
    w_out,
):
    scale = 1.0 / math.sqrt(HEAD_DIM)
    y, x, c, z = (lax.axis_index(name) for name in AXES)
    patches = tokens.shape[2]
    width = qkv_space.shape[0]
    frames_own = tokens.shape[0] * tokens.shape[1] // 4
    frames_all = frame_order.shape[1]
    own = frames_own * patches
    hidden_own = w_in.shape[1] // 2
    plane = 2 * y + x
    k_own = 2 * (z % 2) + c

    masked_here = (priority < ratio[:, None, None]).astype(jnp.int32).reshape(2, -1)
    info = cols([masked_here, frame_order])
    info = jnp.where(z // 2 == c, info, hop_c(info))
    info = lax.dynamic_index_in_dim(info, z % 2, 0, keepdims=False)
    masked = lax.dynamic_slice_in_dim(info, c * own, own, 0)[:, None] != 0
    order = info[2 * own :].reshape(2, 2, frames_own)
    order = jnp.where(y == 1, order[::-1], order)
    order = jnp.where(c == 1, order[:, ::-1], order).swapaxes(0, 1).reshape(frames_all)
    order = jnp.repeat(order, GROUP)
    patch = jnp.arange(frames_all * GROUP) % GROUP
    visible = (order[:, None] <= order[None, :]) & (patch[:, None] == patch[None, :])
    bias = jnp.where(visible, 0.0, -1e30).astype(F32)

    vectors = rows_of([mask_embed[None], gains, jnp.zeros((4, BLK), BF16)])
    head = (2 * y + c) * HEAD_DIM
    ti_own = cols(
        [
            lax.dynamic_slice_in_dim(qkv_time, head, HEAD_DIM, 2).reshape(width, -1),
            lax.dynamic_slice_in_dim(out_time, head, HEAD_DIM, 0).T,
        ]
    )
    (
        ws_qkv, ws_out, wt_all, wf_out, joined0, turned0, std0,
        mixed0, total0, inv0, resid1, std1, inv1, normed1, vectors,
    ) = enter(
        tokens.reshape(4, own, BLK),
        vectors,
        jnp.swapaxes(qkv_space, 0, 1),
        out_space,
        ti_own,
        w_out,
        masked.astype(F32),
        scale,
    )
    gain = [vectors[1 + i : 2 + i] for i in range(3)]
    wt_all = wt_all.reshape(width, 4, 4, HEAD_DIM)
    wt_qkv = jnp.swapaxes(wt_all[:, :, :3], 1, 2).reshape(width, 12 * HEAD_DIM)
    wt_out = wt_all[:, :, 3].reshape(width, 4 * HEAD_DIM)

    ff_in = lax.dynamic_slice(w_in, (plane * BLK, c * hidden_own), (BLK, hidden_own))
    ff_in, normed1 = tie(ff_in, normed1)
    wf_in = lax.all_gather(ff_in, ("mp", "tm", "x")).reshape(4, width, hidden_own)

    def pair_gather(v):
        return rows_of([v, hop_c(v)])

    def pair_scatter(v):
        return v[:own] + hop_c(v[own:].astype(BF16)).astype(F32)

    half = qkv_space.shape[2] // 2
    normed1, joined1, mixed1, total1, delta, upstream, wf_far = time_call(
        False,
        normed1.reshape(frames_own, patches, width),
        cotangent.reshape(4, own, BLK),
        [wf_out],
        wt_qkv,
        wt_out,
        bias,
        scale,
    )
    normed1 = normed1.reshape(4 * own, width)
    mixed1 = mixed1.reshape(4 * own, -1)
    w_in_half, w_out_half, grad2, grad2_low, block_rows, gain_grad2 = feed(
        resid1, delta.reshape(own, width), upstream, masked.astype(F32), gain[2], wf_in, wf_out, wf_far
    )

    def by_core(kept, landed):
        return jnp.where(c == 0, jnp.concatenate([kept, landed], -1), jnp.concatenate([landed, kept], -1))

    gb2, djoined1, part1, g_w_in, block_out = time_call(
        True,
        grad2_low.reshape(frames_own, patches, width),
        block_rows,
        [joined1, total1, w_in_half],
        wt_qkv,
        wt_out,
        bias,
        scale,
    )
    block_out = block_out.reshape(tokens.shape)
    gb2 = gb2.reshape(4 * own, width)
    djoined1 = djoined1.reshape(4 * own, -1)
    g_t_qkv = dot_tn(normed1, djoined1).astype(BF16).reshape(width, 3, 4, HEAD_DIM)
    g_t_out = dot_tn(gb2, mixed1).astype(BF16).reshape(width, 1, 4, HEAD_DIM)
    g_time = jnp.swapaxes(jnp.concatenate([g_t_qkv, g_t_out], axis=1), 1, 2).reshape(width, width)
    small = rows_of([jnp.zeros((2, width), F32), gain_grad2, jnp.zeros((5, width), F32)])
    kept, landed, feed_kept, feed_landed, quad, grad_tokens, small = leave(
        part1.reshape(own, width), std1, grad2, ws_out, joined0, mixed0, turned0, ws_qkv, std0, g_time, w_out_half, g_w_in,
        total0, inv1, inv0, masked.astype(F32), gain[1], gain[0], small, scale,
    )
    grad_tokens = grad_tokens.reshape(tokens.shape).astype(F32)

    rows = BLK // 2
    grad_qkv_space = by_core(
        kept[:, : 3 * half].reshape(rows, 3, half), landed[:, : 3 * half].reshape(rows, 3, half)
    )
    grad_out_space = by_core(kept[:, 3 * half :], landed[:, 3 * half :]).T
    grad_w_in = by_core(feed_kept[0], feed_landed[0])
    grad_w_out = by_core(feed_kept[1], feed_landed[1]).T
    quad = jnp.transpose(quad, (2, 0, 1, 3)).reshape(rows, 2, 2, 4, HEAD_DIM)
    quad = jnp.where(c == 1, quad[:, ::-1], quad)
    quad = jnp.where(y == 1, quad[:, :, ::-1], quad)
    quad = jnp.transpose(quad, (0, 3, 2, 1, 4)).reshape(rows, 4, 4 * HEAD_DIM)
    grad_qkv_time = quad[:, :3]
    grad_out_time = quad[:, 3].T
    return (
        block_out,
        grad_tokens,
        small[3],
        small[:3],
        grad_qkv_space,
        grad_out_space,
        grad_qkv_time,
        grad_out_time,
        grad_w_in,
        grad_w_out,
    )


def solution(mesh):
    sizes = (mesh.shape["tm"], mesh.shape["clip"], mesh.shape["mp"])
    if sizes == (2, 4, 4):
        mesh = jax.sharding.Mesh(mesh.devices.reshape(2, 2, 2, 4), AXES)
        step, clip = token_parallel, ("x", "c")
    else:
        step, clip = shards, ("clip",)
    return jax.shard_map(
        step,
        mesh=mesh,
        in_specs=(
            P(clip, "tm", None, "mp"),
            P(clip, "tm", None, "mp"),
            P(clip),
            P(clip, "tm", None),
            P(clip, None),
            P("mp"),
            P(None, "mp"),
            P(None, None, "mp"),
            P("mp", None),
            P(None, None, "mp"),
            P("mp", None),
            P(None, "mp"),
            P("mp", None),
        ),
        out_specs=(
            P(clip, "tm", None, "mp"),
            P(clip, "tm", None, "mp"),
            P("mp"),
            P(None, "mp"),
            P(("tm",) + clip, None, "mp"),
            P("mp", ("tm",) + clip),
            P(("tm",) + clip, None, "mp"),
            P("mp", ("tm",) + clip),
            P(("tm",) + clip, "mp"),
            P("mp", ("tm",) + clip),
        ),
        check_vma=False,
    )
```

```python
import functools
import math

import jax
import jax.numpy as jnp
from jax import lax
from jax.experimental import pallas as pl
from jax.experimental.pallas import tpu as pltpu
from jax.sharding import PartitionSpec as P

HEAD_DIM = 64
MICRO = 2


eps_norm = 1e-05


def gelu_tanh(values):
    return jax.nn.gelu(values, approximate=True)


def norm_forward_pass(residual_stream, gain_coefficients, complete_width):
    reduced_totals = lax.psum(
        (jnp.sum(residual_stream, axis=-1), jnp.sum(residual_stream * residual_stream, axis=-1)),
        "mp",
    )
    centered_rows = reduced_totals[0] / complete_width
    spread = reduced_totals[1] / complete_width - centered_rows * centered_rows
    inverse_scale = lax.rsqrt(spread + eps_norm)
    standardized_rows = (residual_stream - centered_rows[:, None]) * inverse_scale[:, None]
    shard_rows = (standardized_rows * gain_coefficients).astype(jnp.bfloat16)
    normalized_rows = lax.all_gather(shard_rows, "mp", axis=1, tiled=True)
    return (normalized_rows, standardized_rows, inverse_scale)


def norm_reverse_pass(
    normalized_gradient, standardized_rows, inverse_scale, gain_coefficients, complete_width
):
    gain_gradient = jnp.sum(normalized_gradient * standardized_rows, axis=0)
    standardized_gradient = normalized_gradient * gain_coefficients
    reduced_totals = lax.psum(
        (
            jnp.sum(standardized_gradient, axis=-1),
            jnp.sum(standardized_gradient * standardized_rows, axis=-1),
        ),
        "mp",
    )
    grad_resid = (
        standardized_gradient
        - reduced_totals[0][:, None] / complete_width
        - standardized_rows * (reduced_totals[1][:, None] / complete_width)
    ) * inverse_scale[:, None]
    return (grad_resid, gain_gradient)


def sum_features(grad_full):
    return lax.psum_scatter(
        grad_full.astype(jnp.bfloat16), "mp", scatter_dimension=1, tiled=True
    ).astype(jnp.float32)


def branch_out(hidden, weight):
    partial_rows = jnp.dot(hidden, weight, preferred_element_type=jnp.float32)
    return lax.psum_scatter(partial_rows, "mp", scatter_dimension=1, tiled=True)


def branch_back(grad_resid, hidden, weight):
    grad_rows = lax.all_gather(grad_resid.astype(jnp.bfloat16), "mp", axis=1, tiled=True)
    weight_grad = jnp.einsum("rk,rd->kd", hidden, grad_rows, preferred_element_type=jnp.float32)
    grad_hidden = jnp.einsum("rd,kd->rk", grad_rows, weight, preferred_element_type=jnp.float32)
    return (grad_hidden, weight_grad)


def qkv_back(normalized_rows, grad_joined, weight):
    weight_grad = jnp.einsum(
        "rd,trk->dtk", normalized_rows, grad_joined, preferred_element_type=jnp.float32
    )
    grad_full = jnp.einsum("trk,dtk->rd", grad_joined, weight, preferred_element_type=jnp.float32)
    return (weight_grad, sum_features(grad_full))


def reduce_grads(local_grads, small_grads):
    reduced = (
        lax.psum_scatter(local_grads[0], ("tm", "clip"), scatter_dimension=0, tiled=True),
        lax.psum_scatter(local_grads[1], ("tm", "clip"), scatter_dimension=1, tiled=True),
        lax.psum_scatter(local_grads[2], ("tm", "clip"), scatter_dimension=0, tiled=True),
        lax.psum_scatter(local_grads[3], ("tm", "clip"), scatter_dimension=1, tiled=True),
        lax.psum_scatter(local_grads[4], ("tm", "clip"), scatter_dimension=0, tiled=True),
        lax.psum_scatter(local_grads[5], ("tm", "clip"), scatter_dimension=1, tiled=True),
    )
    reduced_small = lax.psum((small_grads[0], small_grads[1]), ("tm", "clip"))
    return (reduced, reduced_small)


def space_forward(normalized_rows, weight, frame_count, patches, heads_local, scale):
    joined = jnp.einsum(
        "rd,dtk->trk", normalized_rows, weight, preferred_element_type=jnp.float32
    ).astype(jnp.bfloat16)
    shape_heads = (frame_count, patches, heads_local, HEAD_DIM)
    scores = (
        jnp.einsum(
            "bshd,bthd->bhst",
            joined[0].reshape(shape_heads),
            joined[1].reshape(shape_heads),
            preferred_element_type=jnp.float32,
        )
        * scale
    )
    highest = jnp.max(scores, axis=-1, keepdims=True)
    exponent = jnp.exp(scores - highest)
    reduced_totals = jnp.sum(exponent, axis=-1, keepdims=True)
    log_total = highest + jnp.log(reduced_totals)
    attention = (exponent / reduced_totals).astype(jnp.bfloat16)
    mixed = jnp.einsum(
        "bhst,bthd->bshd",
        attention,
        joined[2].reshape(shape_heads),
        preferred_element_type=jnp.float32,
    )
    return (
        joined,
        log_total,
        mixed.astype(jnp.bfloat16).reshape(frame_count * patches, heads_local * HEAD_DIM),
    )


def space_backward(grad_mixed, joined, log_total, frame_count, patches, heads_local, scale):
    shape_heads = (frame_count, patches, heads_local, HEAD_DIM)
    queries = joined[0].reshape(shape_heads)
    key_rows = joined[1].reshape(shape_heads)
    values = joined[2].reshape(shape_heads)
    grad_out = grad_mixed.reshape(shape_heads)
    scores = (
        jnp.einsum("bshd,bthd->bhst", queries, key_rows, preferred_element_type=jnp.float32) * scale
    )
    attention = jnp.exp(scores - log_total)
    grad_values = jnp.einsum(
        "bhst,bshd->bthd",
        attention.astype(jnp.bfloat16),
        grad_out,
        preferred_element_type=jnp.float32,
    )
    grad_att = jnp.einsum("bshd,bthd->bhst", grad_out, values, preferred_element_type=jnp.float32)
    grad_scores = (
        attention * (grad_att - jnp.sum(attention * grad_att, axis=-1, keepdims=True))
    ).astype(jnp.bfloat16)
    grad_queries = (
        jnp.einsum("bhst,bthd->bshd", grad_scores, key_rows, preferred_element_type=jnp.float32)
        * scale
    )
    grad_keys = (
        jnp.einsum("bhst,bshd->bthd", grad_scores, queries, preferred_element_type=jnp.float32)
        * scale
    )
    row_count = frame_count * patches
    stacked = jnp.stack(
        [
            grad_queries.reshape(row_count, -1),
            grad_keys.reshape(row_count, -1),
            grad_values.reshape(row_count, -1),
        ]
    )
    return stacked.astype(jnp.bfloat16)


def time_scores(queries, keys_all, visible, scale):
    scores = (
        jnp.einsum("cfshd,cgshd->chfgs", queries, keys_all, preferred_element_type=jnp.float32)
        * scale
    )
    return jnp.where(visible, scores, -1e30)


def time_forward(queries, keys_all, values_all, visible, scale):
    scores = time_scores(queries, keys_all, visible, scale)
    highest = jnp.max(scores, axis=3, keepdims=True)
    exponent = jnp.exp(scores - highest)
    reduced_totals = jnp.sum(exponent, axis=3, keepdims=True)
    log_total = highest + jnp.log(reduced_totals)
    attention = (exponent / reduced_totals).astype(jnp.bfloat16)
    mixed = jnp.einsum(
        "chfgs,cgshd->cfshd", attention, values_all, preferred_element_type=jnp.float32
    )
    return (log_total, mixed.astype(jnp.bfloat16))


def time_backward(grad_mixed, queries, keys_all, values_all, visible, log_total, scale):
    grad_out = grad_mixed.reshape(queries.shape)
    scores = time_scores(queries, keys_all, visible, scale)
    attention = jnp.exp(scores - log_total)
    grad_values = jnp.einsum(
        "chfgs,cfshd->cgshd",
        attention.astype(jnp.bfloat16),
        grad_out,
        preferred_element_type=jnp.float32,
    )
    grad_att = jnp.einsum(
        "cfshd,cgshd->chfgs", grad_out, values_all, preferred_element_type=jnp.float32
    )
    grad_scores = (
        attention * (grad_att - jnp.sum(attention * grad_att, axis=3, keepdims=True))
    ).astype(jnp.bfloat16)
    grad_queries = (
        jnp.einsum("chfgs,cgshd->cfshd", grad_scores, keys_all, preferred_element_type=jnp.float32)
        * scale
    )
    grad_keys = (
        jnp.einsum("chfgs,cfshd->cgshd", grad_scores, queries, preferred_element_type=jnp.float32)
        * scale
    )
    return (grad_queries, grad_keys, grad_values)


def shards(
    tokens,
    cotangent,
    ratio,
    priority,
    frame_order,
    mask_embed,
    gains,
    qkv_space,
    out_space,
    qkv_time,
    out_time,
    w_in,
    w_out,
):
    scale = 1.0 / math.sqrt(HEAD_DIM)
    clips_local = tokens.shape[0] // MICRO
    frames_local = tokens.shape[1]
    patches = tokens.shape[2]
    cols_local = tokens.shape[3]
    frames_all = frame_order.shape[1]
    hidden_width = qkv_space.shape[0]
    joined_local = qkv_space.shape[2]
    heads_local = joined_local // HEAD_DIM
    row_count = clips_local * frames_local * patches
    gain_broadcast = gains.astype(jnp.float32)
    embed_row = mask_embed.astype(jnp.float32)
    first_frame = lax.axis_index("tm") * frames_local
    shape_local = (clips_local, frames_local, patches, joined_local)
    shape_heads = (clips_local, frames_local, patches, heads_local, HEAD_DIM)
    shape_all = (clips_local, frames_all, patches, heads_local, HEAD_DIM)
    outputs = []
    input_grads = []
    weight_total = None
    small_total = None
    for batch_index in range(MICRO):
        lower = batch_index * clips_local
        upper = lower + clips_local
        source = tokens[lower:upper].reshape(row_count, cols_local).astype(jnp.float32)
        upstream = cotangent[lower:upper].reshape(row_count, cols_local).astype(jnp.float32)
        masked = (priority[lower:upper] < ratio[lower:upper][:, None, None]).reshape(row_count)
        order_rows = frame_order[lower:upper]
        residual_stream0 = jnp.where(masked[:, None], embed_row[None, :], source)
        normalized_rows0, standardized_rows0, inverse_deviation0 = norm_forward_pass(
            residual_stream0, gain_broadcast[0], hidden_width
        )
        joined0, total0, mixed0 = space_forward(
            normalized_rows0, qkv_space, clips_local * frames_local, patches, heads_local, scale
        )
        residual_stream1 = residual_stream0 + branch_out(mixed0, out_space)
        normalized_rows1, standardized_rows1, inverse_deviation1 = norm_forward_pass(
            residual_stream1, gain_broadcast[1], hidden_width
        )
        joined1 = jnp.einsum(
            "rd,dtk->trk", normalized_rows1, qkv_time, preferred_element_type=jnp.float32
        ).astype(jnp.bfloat16)
        queries_local = joined1[0].reshape(shape_local)
        keys_local = joined1[1].reshape(shape_local)
        values_local = joined1[2].reshape(shape_local)
        keys_all, values_all = (
            lax.all_gather(keys_local, "tm", axis=1, tiled=True),
            lax.all_gather(values_local, "tm", axis=1, tiled=True),
        )
        query_order = lax.dynamic_slice_in_dim(order_rows, first_frame, frames_local, axis=1)
        time_visible = (order_rows[:, None, :] <= query_order[:, :, None])[:, None, :, :, None]
        time_q = queries_local.reshape(shape_heads)
        time_k = keys_all.reshape(shape_all)
        time_v = values_all.reshape(shape_all)
        total1, mixed_frames = time_forward(time_q, time_k, time_v, time_visible, scale)
        mixed1 = mixed_frames.reshape(row_count, joined_local)
        residual_stream2 = residual_stream1 + branch_out(mixed1, out_time)
        normalized_rows2, standardized_rows2, inverse_deviation2 = norm_forward_pass(
            residual_stream2, gain_broadcast[2], hidden_width
        )
        projected = jnp.dot(normalized_rows2, w_in, preferred_element_type=jnp.float32)
        activated, gelu_pull = jax.vjp(gelu_tanh, projected)
        hidden = activated.astype(jnp.bfloat16)
        resid3 = residual_stream2 + branch_out(hidden, w_out)
        outputs.append(
            resid3.astype(jnp.bfloat16).reshape(clips_local, frames_local, patches, cols_local)
        )
        grad3 = jnp.where(masked[:, None], upstream, 0.0)
        grad_hidden, grad_w_out = branch_back(grad3, hidden, w_out)
        grad_inner = gelu_pull(grad_hidden)[0].astype(jnp.bfloat16)
        grad_w_in = jnp.einsum(
            "rd,rk->dk", normalized_rows2, grad_inner, preferred_element_type=jnp.float32
        )
        normalized_gradient2 = sum_features(
            jnp.einsum("rk,dk->rd", grad_inner, w_in, preferred_element_type=jnp.float32)
        )
        backward_third, gain_gradient2 = norm_reverse_pass(
            normalized_gradient2,
            standardized_rows2,
            inverse_deviation2,
            gain_broadcast[2],
            hidden_width,
        )
        grad2 = grad3 + backward_third
        grad_mixed1, grad_out_time = branch_back(grad2, mixed1, out_time)
        grad_mixed_low = grad_mixed1.astype(jnp.bfloat16).reshape(shape_local)
        grad_queries, grad_keys, grad_values = time_backward(
            grad_mixed_low, time_q, time_k, time_v, time_visible, total1, scale
        )
        key_part, value_part = (
            lax.psum_scatter(
                grad_keys.reshape(clips_local, frames_all, patches, joined_local).astype(
                    jnp.bfloat16
                ),
                "tm",
                scatter_dimension=1,
                tiled=True,
            ).astype(jnp.float32),
            lax.psum_scatter(
                grad_values.reshape(clips_local, frames_all, patches, joined_local).astype(
                    jnp.bfloat16
                ),
                "tm",
                scatter_dimension=1,
                tiled=True,
            ).astype(jnp.float32),
        )
        grad_joined1 = jnp.stack(
            [
                grad_queries.reshape(row_count, joined_local),
                key_part.reshape(row_count, joined_local),
                value_part.reshape(row_count, joined_local),
            ]
        ).astype(jnp.bfloat16)
        grad_qkv_time, normalized_gradient1 = qkv_back(normalized_rows1, grad_joined1, qkv_time)
        backward_second, gain_gradient1 = norm_reverse_pass(
            normalized_gradient1,
            standardized_rows1,
            inverse_deviation1,
            gain_broadcast[1],
            hidden_width,
        )
        grad1 = grad2 + backward_second
        grad_mixed0, grad_out_space = branch_back(grad1, mixed0, out_space)
        grad_joined0 = space_backward(
            grad_mixed0.astype(jnp.bfloat16),
            joined0,
            total0,
            clips_local * frames_local,
            patches,
            heads_local,
            scale,
        )
        grad_qkv_space, normalized_gradient0 = qkv_back(normalized_rows0, grad_joined0, qkv_space)
        backward_first, gain_gradient0 = norm_reverse_pass(
            normalized_gradient0,
            standardized_rows0,
            inverse_deviation0,
            gain_broadcast[0],
            hidden_width,
        )
        grad0 = grad1 + backward_first
        input_grads.append(
            jnp.where(masked[:, None], 0.0, grad0).reshape(
                clips_local, frames_local, patches, cols_local
            )
        )
        grad_embed = jnp.sum(jnp.where(masked[:, None], grad0, 0.0), axis=0)
        gain_grads = jnp.stack([gain_gradient0, gain_gradient1, gain_gradient2])
        local_grads = (
            grad_qkv_space,
            grad_out_space,
            grad_qkv_time,
            grad_out_time,
            grad_w_in,
            grad_w_out,
        )
        small_grads = (gain_grads, grad_embed)
        reduced, reduced_small = reduce_grads(local_grads, small_grads)
        if weight_total is None:
            weight_total = reduced
            small_total = reduced_small
        else:
            weight_total = tuple((total + grad for total, grad in zip(weight_total, reduced)))
            small_total = tuple((total + grad for total, grad in zip(small_total, reduced_small)))
    return (
        jnp.concatenate(outputs, axis=0),
        jnp.concatenate(input_grads, axis=0),
        small_total[1],
        small_total[0],
        weight_total[0],
        weight_total[1],
        weight_total[2],
        weight_total[3],
        weight_total[4],
        weight_total[5],
    )


AXES = ("tm", "x", "c", "mp")
F32 = jnp.float32
BF16 = jnp.bfloat16
BLK = 256
MESH = pl.DeviceIdType.MESH


def device_pairs(move):
    pairs = []
    for y in range(2):
        for x in range(2):
            for c in range(2):
                for z in range(4):
                    there = move(y, x, c, z)
                    pairs.append(tuple(((q[0] * 2 + q[1]) * 2 + q[2]) * 4 + q[3] for q in ((y, x, c, z), there)))
    return pairs


def hop_y(v):
    return lax.ppermute(v, AXES, device_pairs(lambda y, x, c, z: (1 - y, x, c, z)))


def hop_x(v):
    return lax.ppermute(v, AXES, device_pairs(lambda y, x, c, z: (y, 1 - x, c, z)))


def hop_c(v):
    return lax.ppermute(v, AXES, device_pairs(lambda y, x, c, z: (y, x, 1 - c, z)))


def hop_z(v, shift):
    return lax.ppermute(v, AXES, device_pairs(lambda y, x, c, z: (y, x, c, (z + shift) % 4)))


def spread_pairs(r):
    def move(y, x, c, z):
        k = z ^ r
        return (y, x, k & 1, 2 * c + (k >> 1))

    return device_pairs(move)


def dot_nn(a, b):
    return lax.dot_general(a, b, (((1,), (0,)), ((), ())), preferred_element_type=F32)


def dot_nt(a, b):
    return lax.dot_general(a, b, (((1,), (1,)), ((), ())), preferred_element_type=F32)


def dot_tn(a, b):
    return lax.dot_general(a, b, (((0,), (0,)), ((), ())), preferred_element_type=F32)


def attend_pair(q, k, v, bias, scale):
    mixed, totals = [], []
    for i in range(2):
        mine = slice(i * HEAD_DIM, (i + 1) * HEAD_DIM)
        scores = dot_nt(k[:, mine], q[:, mine]) * scale
        if bias is not None:
            scores = scores + bias
        highest = jnp.max(scores, axis=0, keepdims=True)
        exponent = jnp.exp(scores - highest)
        total = jnp.sum(exponent, axis=0, keepdims=True)
        totals.append(highest + jnp.log(total))
        mixed.append(dot_tn(v[:, mine], exponent.astype(BF16)) * (1.0 / total))
    return (jnp.concatenate(mixed, axis=0).T, totals)


def attend_pair_back(q, k, v, g, totals, bias, scale):
    grads = ([], [], [])
    for i in range(2):
        mine = slice(i * HEAD_DIM, (i + 1) * HEAD_DIM)
        scores = dot_nt(k[:, mine], q[:, mine]) * scale
        if bias is not None:
            scores = scores + bias
        p = jnp.exp(scores - totals[i])
        dp = dot_nt(v[:, mine], g[:, mine])
        ds = (p * (dp - jnp.sum(p * dp, axis=0, keepdims=True))).astype(BF16)
        grads[0].append(dot_tn(k[:, mine], ds) * scale)
        grads[1].append(dot_nn(ds, q[:, mine]) * scale)
        grads[2].append(dot_nn(p.astype(BF16), g[:, mine]))
    return (
        jnp.concatenate(grads[0], axis=0).T,
        jnp.concatenate(grads[1], axis=1),
        jnp.concatenate(grads[2], axis=1),
    )


PAIR = 2 * HEAD_DIM


def enter_kernel(
    scale,
    tok, vec, qkv_hbm, out_hbm, later, feed_hbm, first_hbm, masked,
    wq_out, wo_out, wt, wf, wi, joined_out, turned_out, std_out,
    mixed, total_out, inverse, resid, std_next, inverse_next, low_next, vec_out,
    rows_in, vec_in, wq, wo, normed, joined, turned, std, base, part, part_out, part_in,
    z_send, z_recv, y_send, y_recv, x_send, x_recv, p_send, p_recv, q_send, q_recv,
    t_send, t_recv, v_send, v_recv, u_send, u_recv, w_send, w_recv,
    f_send, f_recv, g_send, g_recv, n_send, n_recv, local, saved,
    i_send, i_recv, j_send, j_recv, k_send, k_recv,
):
    y, x, c, z = (lax.axis_index(name) for name in AXES)
    half = wo.shape[0] // 4
    wide = 3 * half
    span = wt.shape[1] // 4
    size = wf.shape[1] // 4
    own = rows_in.shape[0]
    near_y, near_x, pair = (1 - y, x, c, z), (y, 1 - x, c, z), (y, x, 1 - c, z)
    right_z, left_z = (y, x, c, (z + 1) % 4), (y, x, c, (z + 3) % 4)

    def at(i, length):
        return pl.ds(pl.multiple_of(i * length, length), length)

    def remote(src, dst, send, recv, peer):
        return pltpu.make_async_remote_copy(
            src_ref=src, dst_ref=dst, send_sem=send, recv_sem=recv, device_id=peer, device_id_type=MESH
        )

    def start(all_copies):
        for copy in all_copies:
            copy.start()

    def landed(all_copies):
        for copy in all_copies:
            copy.wait_recv()

    def sent(all_copies):
        for copy in all_copies:
            copy.wait_send()

    core = at(c, half)
    keep = [
        pltpu.make_async_copy(
            qkv_hbm.at[j, :, core], wq.at[:, pl.ds(pl.multiple_of(z * wide + j * half, half), half)], local.at[j]
        )
        for j in range(3)
    ] + [pltpu.make_async_copy(out_hbm.at[core], wo.at[at(z, half)], local.at[3])]
    keep_later = [
        pltpu.make_async_copy(later, wt.at[:, at(z, span)], local.at[4]),
        pltpu.make_async_copy(feed_hbm.at[at(c, 4 * size)], wf.at[z], local.at[5]),
        pltpu.make_async_copy(first_hbm.at[:, at(c, 4 * size)], wi.at[z], local.at[8]),
    ]
    start(keep + keep_later)

    barrier = pltpu.get_barrier_semaphore()
    for dc in range(2):
        for dz in range(4):
            if dc or dz:
                peer = (y, x, (c + dc) % 2, (z + dz) % 4)
                pl.semaphore_signal(barrier, inc=1, device_id=peer, device_id_type=MESH)
    for peer in (near_y, near_x):
        pl.semaphore_signal(barrier, inc=1, device_id=peer, device_id_type=MESH)
    pl.semaphore_wait(barrier, 9)

    def spot(dy, dx):
        return 2 * ((y + dy) % 2) + (x + dx) % 2

    def piece(dy, dx, r, split=False):
        s = (z + r) % 4
        rows = at(spot(dy, dx), BLK)
        first = pl.multiple_of(s * wide, half)
        out = wo.at[at(s, half), at(spot(dy, dx), BLK)]
        if split:
            last = pl.multiple_of(s * wide + 2 * half, half)
            return (wq.at[rows, pl.ds(first, 2 * half)], wq.at[rows, pl.ds(last, half)], out)
        return (wq.at[rows, pl.ds(first, wide)], out)

    def time_piece(dx, r):
        return wt.at[at((x + dx) % 2, 2 * BLK), at((z + r) % 4, span)]

    def feed_piece(dy, r):
        return wf.at[(z + r) % 4, at(spot(dy, 0), size)]

    def copies(parts, send, recv, peer):
        return [remote(ref, ref, send.at[i], recv.at[i], peer) for i, ref in enumerate(parts)]

    def leg(right, step):
        if right:
            return (0 if step == 0 else 4 - step), right_z, 3 - step
        return step, left_z, step + 1

    def z_copies(right, step):
        r, peer, lands = leg(right, step)
        return copies(piece(0, 0, r), z_send.at[int(right), step], z_recv.at[lands], peer)

    def time_z(right, step):
        r, peer, lands = leg(right, step)
        source = later.at[at(x, 2 * BLK)] if step == 0 else time_piece(0, r)
        return [remote(source, time_piece(0, r), u_send.at[int(right), step], u_recv.at[lands], peer)]

    def feed_z(right, step):
        r, peer, lands = leg(right, step)
        source = feed_hbm.at[at(4 * c + spot(0, 0), size)] if step == 0 else feed_piece(0, r)
        return [remote(source, feed_piece(0, r), f_send.at[int(right), step], f_recv.at[lands], peer)]

    def first_piece(dy, dx, r):
        return wi.at[(z + r) % 4, at(spot(dy, dx), BLK)]

    def first_z(right, step):
        r, peer, lands = leg(right, step)
        source = first_hbm.at[at(spot(0, 0), BLK), at(c, 4 * size)] if step == 0 else first_piece(0, 0, r)
        return [remote(source, first_piece(0, 0, r), i_send.at[int(right), step], i_recv.at[lands], peer)]

    def first_y(r, dy=0):
        return [remote(first_piece(dy, 0, r), first_piece(dy, 0, r), j_send.at[r], j_recv.at[r], near_y)]

    def first_x(r, dx=0):
        return [remote(first_piece(0, dx, r), first_piece(0, dx, r), k_send.at[r], k_recv.at[r], near_x)]

    def y_copies(r, dy=0):
        return copies(piece(dy, 0, r), y_send.at[r], y_recv.at[r], near_y)

    def x_copies(r, dx=0):
        return copies(piece(0, dx, r), x_send.at[r], x_recv.at[r], near_x)

    def corner_x(r, dx=0):
        return copies(piece(1, dx, r, split=True)[:1], p_send.at[r], p_recv.at[r], near_x)

    def corner_y(r, dy=0):
        return copies(piece(dy, 1, r, split=True)[1:], q_send.at[r], q_recv.at[r], near_y)

    def time_x(r, dx=0):
        return [remote(time_piece(dx, r), time_piece(dx, r), w_send.at[r], w_recv.at[r], near_x)]

    def feed_y(r, dy=0):
        return [remote(feed_piece(dy, r), feed_piece(dy, r), g_send.at[r], g_recv.at[r], near_y)]

    def token_copies(k):
        peer = (y, x, k % 2, 2 * c + k // 2)
        return [
            remote(tok.at[k], rows_in.at[:, at(z, BLK)], t_send.at[k], t_recv.at[z], peer),
            remote(vec, vec_in.at[:, at(z, BLK)], v_send.at[k], v_recv.at[z], peer),
        ]

    def token_local(k):
        return [
            pltpu.make_async_copy(tok.at[k], rows_in.at[:, at(z, BLK)], local.at[6]),
            pltpu.make_async_copy(vec, vec_in.at[:, at(z, BLK)], local.at[7]),
        ]

    def stays(k):
        return jnp.logical_and(2 * c + k // 2 == z, c == k % 2)

    def start_tokens(ks):
        for k in ks:
            pl.when(stays(k))(lambda k=k: start(token_local(k)))
            pl.when(jnp.logical_not(stays(k)))(lambda k=k: start(token_copies(k)))

    def each_side(j, act):
        pl.when(z >= j + 1)(lambda: act(3 - j, True))
        pl.when(z <= 2 - j)(lambda: act(j + 1, False))

    def begin(make):
        pl.when(z < 3)(lambda: start(make(True, 0)))
        pl.when(z > 0)(lambda: start(make(False, 0)))

    def onward(j, make, right):
        if j < 2:
            pl.when(z < 3 if right else z > 0)(lambda: start(make(right, j + 1)))

    def forward(j):
        def act(r, right):
            landed(copies(piece(0, 0, r), z_send.at[0, 0], z_recv.at[r], near_y))
            onward(j, z_copies, right)
            start(y_copies(r))
            start(x_copies(r))

        each_side(j, act)

    def corners(j):
        def act(r, right):
            landed(y_copies(r, 1))
            start(corner_x(r))
            landed(x_copies(r, 1))
            start(corner_y(r))

        each_side(j, act)

    def time_forward_step(j):
        def act(r, right):
            landed([remote(time_piece(0, r), time_piece(0, r), u_send.at[0, 0], u_recv.at[r], near_x)])
            onward(j, time_z, right)
            start(time_x(r))

        each_side(j, act)

    def feed_forward_step(j):
        def act(r, right):
            landed([remote(feed_piece(0, r), feed_piece(0, r), f_send.at[0, 0], f_recv.at[r], near_y)])
            onward(j, feed_z, right)
            start(feed_y(r))

        each_side(j, act)

    def first_forward_step(j):
        def act(r, right):
            landed([remote(first_piece(0, 0, r), first_piece(0, 0, r), i_send.at[0, 0], i_recv.at[r], near_y)])
            onward(j, first_z, right)
            start(first_y(r))
            start(first_x(r))

        each_side(j, act)

    for copy in keep:
        copy.wait()
    begin(z_copies)
    forward(0)
    start_tokens((0, 1))
    forward(1)
    start_tokens((2, 3))
    begin(time_z)
    corners(0)
    forward(2)
    corners(1)
    for k in range(4):
        def finish_local(k=k):
            for copy in token_local(k):
                copy.wait()

        pl.when(stays(k))(finish_local)
    for s in range(4):
        def arrived(s=s):
            landed([
                remote(tok.at[0], rows_in.at[:, at(s, BLK)], t_send.at[0], t_recv.at[s], near_y),
                remote(vec, vec_in.at[:, at(s, BLK)], v_send.at[0], v_recv.at[s], near_y),
            ])

        pl.when(jnp.logical_not(jnp.logical_and(z == s, z // 2 == c)))(arrived)

    step = own // 2
    slab = 128
    vec_out[...] = vec_in[...].astype(F32)

    def first_norm(i, carry):
        rows = at(i, step)
        value = jnp.where(masked[rows] > 0.0, vec_out[0:1], rows_in[rows].astype(F32))
        base[rows] = value
        standard, inv = norm_rows(value)
        std[rows] = standard
        inverse[rows] = inv
        normed[rows] = (standard * vec_out[1:2]).astype(BF16)
        return carry

    lax.fori_loop(0, 2, first_norm, 0)
    give_normed = remote(normed.at[pl.ds(0, own)], normed.at[pl.ds(own, own)], n_send.at[0], n_recv.at[0], pair)
    give_normed.start()
    corners(2)

    def turn(i, carry):
        turned[:, at(i, slab)] = normed[at(i, slab)].T
        return carry

    lax.fori_loop(0, own // slab, turn, 0)
    for r in (1, 2, 3):
        landed(corner_x(r, 1))
        landed(corner_y(r, 1))
    saves = [
        pltpu.make_async_copy(wq, wq_out, saved.at[0]),
        pltpu.make_async_copy(wo, wo_out, saved.at[1]),
        pltpu.make_async_copy(std, std_out, saved.at[2]),
    ]
    start(saves)
    time_forward_step(0)

    def attend(i, carry):
        rows = at(i, slab)
        for h in range(wo.shape[0] // PAIR):
            q, k, v = (joined[rows, (3 * h + j) * PAIR : (3 * h + j + 1) * PAIR] for j in range(3))
            out, totals = attend_pair(q, k, v, None, scale)
            mixed[rows, h * PAIR : (h + 1) * PAIR] = out.astype(BF16)
            for j in range(2):
                total_out[i, 2 * h + j : 2 * h + j + 1, :] = totals[j]
        return carry

    def project(t):
        rows = pl.ds(t * own, own)
        joined[rows] = dot_nn(normed[rows], wq[...]).astype(BF16)

    frames = own // slab
    project(0)
    time_forward_step(1)
    begin(first_z)
    lax.fori_loop(0, frames, attend, 0)
    part[...] = dot_nn(mixed[pl.ds(0, own)], wo[...])
    time_forward_step(2)
    give_normed.wait_recv()
    project(1)
    saves.append(pltpu.make_async_copy(joined, joined_out, saved.at[3]))
    saves[3].start()
    first_forward_step(0)
    lax.fori_loop(frames, 2 * frames, attend, 0)
    part_out[...] = dot_nn(mixed[pl.ds(own, own)], wo[...]).astype(BF16)
    give_part = remote(part_out, part_in, n_send.at[1], n_recv.at[1], pair)
    give_part.start()
    first_forward_step(1)
    begin(feed_z)
    lax.fori_loop(own // slab, 2 * own // slab, turn, 0)
    saves.append(pltpu.make_async_copy(turned, turned_out, saved.at[4]))
    saves[4].start()
    give_part.wait_recv()
    first_forward_step(2)

    def second_norm(i, carry):
        rows = at(i, step)
        value = base[rows] + part[rows] + part_in[rows].astype(F32)
        resid[rows] = value
        standard, inv = norm_rows(value)
        std_next[rows] = standard
        inverse_next[rows] = inv
        low_next[rows] = (standard * vec_out[2:3]).astype(BF16)
        return carry

    lax.fori_loop(0, 2, second_norm, 0)
    for j in range(3):
        feed_forward_step(j)

    for copy in keep_later + saves:
        copy.wait()
    give_normed.wait_send()
    give_part.wait_send()
    for r in (1, 2, 3):
        landed(time_x(r, 1))
        landed(feed_y(r, 1))
        landed(first_y(r, 1))
        landed(first_x(r, 1))
        for group in (y_copies(r), x_copies(r), corner_x(r), corner_y(r), time_x(r), feed_y(r), first_y(r), first_x(r)):
            sent(group)
    for step_z in range(3):
        for make in (z_copies, time_z, first_z, feed_z):
            pl.when(jnp.logical_and(z >= step_z, z < 3))(lambda step_z=step_z, make=make: sent(make(True, step_z)))
            pl.when(jnp.logical_and(z + step_z <= 3, z > 0))(lambda step_z=step_z, make=make: sent(make(False, step_z)))
    for k in range(4):
        pl.when(jnp.logical_not(stays(k)))(lambda k=k: sent(token_copies(k)))


def enter(tok, vec, qkv, out, later, feed_weight, first_weight, masked, scale):
    own, width, half = tok.shape[1], 4 * tok.shape[2], out.shape[0] // 2
    size = feed_weight.shape[0] // 2
    dma = pltpu.SemaphoreType.DMA
    anywhere = pl.BlockSpec(memory_space=pl.ANY)
    whole = pl.BlockSpec(memory_space=pltpu.VMEM)
    heads = 4 * half // HEAD_DIM

    def low(*shape):
        return pltpu.VMEM(shape, BF16)

    def high(*shape):
        return pltpu.VMEM(shape, F32)

    shapes = [
        ((width, 12 * half), BF16), ((4 * half, width), BF16), ((width, 4 * later.shape[1]), BF16),
        ((4, size, width), BF16), ((4, width, size), BF16), ((2 * own, 12 * half), BF16), ((width, 2 * own), BF16), ((own, width), F32),
        ((2 * own, 4 * half), BF16), ((2 * own // 128, heads, 128), F32), ((own, 1), F32), ((own, width), F32),
        ((own, width), F32), ((own, 1), F32), ((own, width), BF16), ((vec.shape[0], width), F32),
    ]
    return pl.pallas_call(
        functools.partial(enter_kernel, scale),
        in_specs=[anywhere] * 7 + [whole],
        out_specs=[anywhere] * 8 + [whole] * 8,
        out_shape=[jax.ShapeDtypeStruct(shape, kind) for shape, kind in shapes],
        scratch_shapes=[
            low(own, width), low(vec.shape[0], width), low(width, 12 * half), low(4 * half, width),
            low(2 * own, width), low(2 * own, 12 * half), low(width, 2 * own), high(own, width), high(own, width),
            high(own, width), low(own, width), low(own, width),
            dma((2, 3, 2)), dma((4, 2)), dma((4, 2)), dma((4, 2)), dma((4, 2)), dma((4, 2)),
            dma((4, 1)), dma((4, 1)), dma((4, 2)), dma((4, 2)),
            dma((4,)), dma((4,)), dma((4,)), dma((4,)), dma((2, 3)), dma((4,)), dma((4,)), dma((4,)),
            dma((2, 3)), dma((4,)), dma((4,)), dma((4,)), dma((2,)), dma((2,)), dma((9,)), dma((5,)),
            dma((2, 3)), dma((4,)), dma((4,)), dma((4,)), dma((4,)), dma((4,)),
        ],
        compiler_params=pltpu.CompilerParams(
            collective_id=0, has_side_effects=True, vmem_limit_bytes=56 * 1024 * 1024
        ),
        cost_estimate=pl.CostEstimate(flops=10**10, transcendentals=10**6, bytes_accessed=10**8),
        name="enter",
    )(tok, vec, qkv, out, later, feed_weight, first_weight, masked)


GROUP = 8
CHUNK = 32


def time_kernel(back, scale, heads, *refs):
    if back:
        (own_ref, rider_ref, joined_ref, total_ref, wide_ref, wt_ref, bias_ref) = refs[:7]
        (all_ref, out_ref, delta_ref, reduced_ref, rider_out) = refs[7:12]
        (half_in, half_own, line_out, line_in, half_send, half_recv, half_local, line_send, line_recv) = refs[-9:]
        refs = refs[12:-9]
    else:
        (own_ref, rider_ref, far_ref, in_ref, wt_ref, bias_ref) = refs[:6]
        (all_ref, out_ref, mixed_ref, total_ref, delta_ref, rider_out, spread_out, in_out) = refs[6:14]
        refs = refs[14:]
    (
        wq_ref, wo_ref, held, wide, narrow, kept, core_out, core_in, near_out, near_in,
        gy_send, gy_recv, gc_send, gc_recv, gd_send, gd_recv, sc_send, sc_recv, sy_send, sy_recv,
        r_send, r_recv, r_local, out_sem, wx_send, wx_recv,
    ) = refs
    y, x, c, z = (lax.axis_index(name) for name in AXES)
    near, pair, near_x = (1 - y, x, c, z), (y, x, 1 - c, z), (y, 1 - x, c, z)
    frames = held.shape[0] // 4
    chunks = held.shape[1] // CHUNK
    width = heads * HEAD_DIM
    groups = CHUNK // GROUP

    barrier = pltpu.get_barrier_semaphore()
    for dc in range(2):
        for dz in range(4):
            if dc or dz:
                pl.semaphore_signal(barrier, inc=1, device_id=(y, x, (c + dc) % 2, (z + dz) % 4), device_id_type=MESH)
    pl.semaphore_signal(barrier, inc=1, device_id=near, device_id_type=MESH)
    pl.semaphore_signal(barrier, inc=1, device_id=near_x, device_id_type=MESH)
    pl.semaphore_wait(barrier, 9)

    def remote(src, dst, send, recv, peer):
        return pltpu.make_async_remote_copy(
            src_ref=src, dst_ref=dst, send_sem=send, recv_sem=recv, device_id=peer, device_id_type=MESH
        )

    def patches(k):
        return pl.ds(pl.multiple_of(k * CHUNK, CHUNK), CHUNK)

    def block(b, k):
        return held.at[pl.ds(b * frames, frames), patches(k)]

    def gather_y(k):
        return remote(own_ref.at[:, patches(k)], block(1, k), gy_send.at[k], gy_recv.at[k], near)

    def gather_c(k):
        return remote(own_ref.at[:, patches(k)], block(2, k), gc_send.at[k], gc_recv.at[k], pair)

    def gather_d(k):
        return remote(block(1, k), block(3, k), gd_send.at[k], gd_recv.at[k], pair)

    def scatter_c(k):
        return remote(core_out.at[k], core_in.at[k], sc_send.at[k], sc_recv.at[k], pair)

    def scatter_y(k):
        return remote(near_out.at[k], near_in.at[k], sy_send.at[k], sy_recv.at[k], near)

    def save(k):
        return pltpu.make_async_copy(held.at[:, patches(k)], all_ref.at[:, patches(k)], out_sem.at[k])

    def columns(s):
        return pl.ds(pl.multiple_of(s * BLK, BLK), BLK)

    def stays(k):
        if back:
            return jnp.logical_and(z == k, z // 2 == c)
        return jnp.logical_and(2 * c + k // 2 == z, c == k % 2)

    def ride(k):
        if back:
            src, dst = rider_ref.at[:, columns(k)], rider_out.at[2 * (z % 2) + c]
            peer, slot = (y, x, z // 2, k), 2 * (z % 2) + c
        else:
            src, dst = rider_ref.at[k], rider_out.at[:, columns(z)]
            peer, slot = (y, x, k % 2, 2 * c + k // 2), z
        return src, dst, peer, slot

    def ride_remote(k):
        src, dst, peer, slot = ride(k)
        return remote(src, dst, r_send.at[k], r_recv.at[slot], peer)

    def ride_local(k):
        src, dst, _, _ = ride(k)
        return pltpu.make_async_copy(src, dst, r_local.at[0])

    def ride_landed(k):
        if back:
            src, dst = rider_ref.at[:, columns(k)], rider_out.at[k]
        else:
            src, dst = rider_ref.at[k], rider_out.at[:, columns(k)]
        return remote(src, dst, r_send.at[k], r_recv.at[k], near)

    def from_self(k):
        if back:
            return jnp.logical_and(2 * c + k // 2 == z, c == k % 2)
        return jnp.logical_and(z == k, z // 2 == c)

    def spread_x(i, dx=0):
        r, yb = i // 2 + 1, i % 2
        size = far_ref.shape[1] // 4
        at = pl.multiple_of(size * (2 * yb + (x + dx) % 2), size)
        src = far_ref.at[(z + r) % 4, pl.ds(at, size)]
        return remote(src, spread_out.at[(z + r) % 4, pl.ds(at, size)], wx_send.at[i], wx_recv.at[i], near_x)

    gather_y(0).start()
    for k in range(chunks):
        if k > 0:
            gather_y(k).start()
        gather_c(k).start()
    def spread_in(r, dx=0):
        at = pl.multiple_of(BLK * (2 * (1 - y) + (x + dx) % 2), BLK)
        there = in_out.at[(z + r) % 4, pl.ds(at, BLK)]
        return remote(in_ref.at[(z + r) % 4, pl.ds(at, BLK)], there, wx_send.at[5 + r], wx_recv.at[5 + r], near_x)

    def half_away(s):
        return remote(wide_ref.at[1 - x, s], half_in.at[s], half_send.at[s], half_recv.at[s], near_x)

    def half_here(s):
        return pltpu.make_async_copy(wide_ref.at[x, s], half_own.at[s], half_local.at[s])

    def line_away(r):
        return remote(line_out.at[r], line_in.at[r], line_send.at[r], line_recv.at[r], (y, x, c, (z + r) % 4))

    def halve():
        for s in range(4):
            half_away(s).wait_recv()
            half_here(s).wait()
        for r in range(4):
            s = (z + r) % 4
            whole = half_own[s].astype(F32) + half_in[s].astype(F32)
            if r == 0:
                reduced_ref[...] = whole
            else:
                line_out[r] = whole.astype(BF16)
                line_away(r).start()

    if back:
        for s in range(4):
            half_away(s).start()
            half_here(s).start()
    else:
        for r in (1, 2, 3):
            spread_in(r).start()
        for i in range(6):
            spread_x(i).start()
    for k in range(4):
        pl.when(stays(k))(lambda k=k: ride_local(k).start())
        pl.when(jnp.logical_not(stays(k)))(lambda k=k: ride_remote(k).start())
    held[:frames] = own_ref[...]

    def assemble(i, carry):
        rows = pl.ds(pl.multiple_of(i * BLK, BLK), BLK)
        for s in range(0, heads, 2):
            for part in range(4):
                both = [
                    wt_ref[rows, (s + j) * 4 * HEAD_DIM + part * HEAD_DIM : (s + j) * 4 * HEAD_DIM + (part + 1) * HEAD_DIM]
                    for j in range(2)
                ]
                both = jnp.concatenate(both, axis=1)
                if part < 3:
                    wq_ref[rows, part * width + s * HEAD_DIM : part * width + s * HEAD_DIM + PAIR] = both
                else:
                    wo_ref[rows, s * HEAD_DIM : s * HEAD_DIM + PAIR] = both
        return carry

    lax.fori_loop(0, wt_ref.shape[0] // BLK, assemble, 0)

    def finish(k):
        scatter_c(k).wait_recv()
        both = kept[:, patches(k)] + core_in[k].astype(F32)
        near_out[k] = both[frames:].astype(BF16)
        delta_ref[:, patches(k)] = both[:frames]
        scatter_y(k).start()

    def pass_on(k):
        gather_y(k).wait_recv()
        gather_d(k).start()

    def one_group(i, rows):
        at = pl.ds(pl.multiple_of(i * GROUP, GROUP), GROUP)
        count = 4 * frames * GROUP
        bias = bias_ref[...]
        for lo in range(0, width, PAIR):
            q, k, v = (
                wide[:, at, part * width + lo : part * width + lo + PAIR].reshape(count, PAIR).astype(BF16)
                for part in range(3)
            )
            h = lo // HEAD_DIM
            if back:
                g = narrow[:, at, lo : lo + PAIR].reshape(count, PAIR).astype(BF16)
                totals = [total_ref[rows * groups + i, h + j : h + j + 1, :] for j in range(2)]
                grads = attend_pair_back(q, k, v, g, totals, bias, scale)
                for part in range(3):
                    wide[:, at, part * width + lo : part * width + lo + PAIR] = grads[part].reshape(
                        4 * frames, GROUP, PAIR
                    )
            else:
                mixed, totals = attend_pair(q, k, v, bias, scale)
                narrow[:, at, lo : lo + PAIR] = mixed.reshape(4 * frames, GROUP, PAIR)
                for j in range(2):
                    total_ref[rows * groups + i, h + j : h + j + 1, :] = totals[j]

    def one_chunk(k, carry):
        pl.when(k + 1 < chunks)(lambda: pass_on(k + 1))
        gather_c(k).wait_recv()
        gather_d(k).wait_recv()
        count = 4 * frames * CHUNK
        lhs = held[:, patches(k)].reshape(count, held.shape[2])
        if back:
            wide[...] = joined_ref[:, patches(k)].astype(F32)
            narrow[...] = dot_nn(lhs, wo_ref[...]).astype(BF16).astype(F32).reshape(narrow.shape)
        else:
            joined = dot_nn(lhs, wq_ref[...]).astype(BF16)
            out_ref[:, patches(k)] = joined.reshape(wide.shape)
            wide[...] = joined.astype(F32).reshape(wide.shape)
        save(k).start()
        lax.fori_loop(0, groups, lambda i, carry: (one_group(i, k), carry)[1], 0)
        if back:
            grads = wide[...].astype(BF16)
            out_ref[:, patches(k)] = grads
            partial = dot_nt(grads.reshape(count, 3 * width), wq_ref[...])
        else:
            mixed = narrow[...].astype(BF16)
            mixed_ref[:, patches(k)] = mixed
            partial = dot_nt(mixed.reshape(count, width), wo_ref[...])
        partial = partial.reshape(4 * frames, CHUNK, held.shape[2])
        kept[:, patches(k)] = partial[: 2 * frames]
        core_out[k] = partial[2 * frames :].astype(BF16)
        scatter_c(k).start()
        pl.when(k > 0)(lambda: finish(k - 1))
        if back:
            pl.when(k == 1)(halve)
        return carry

    pass_on(0)
    lax.fori_loop(0, chunks, one_chunk, 0)
    finish(chunks - 1)
    for k in range(chunks):
        scatter_y(k).wait_recv()
        delta_ref[:, patches(k)] = delta_ref[:, patches(k)] + near_in[k].astype(F32)
    if back:
        for r in (1, 2, 3):
            line_away(r).wait_recv()
            reduced_ref[...] = reduced_ref[...] + line_in[r].astype(F32)
        for r in (1, 2, 3):
            line_away(r).wait_send()
        for s in range(4):
            half_away(s).wait_send()
    for k in range(chunks):
        for copy in (gather_y(k), gather_c(k), gather_d(k), scatter_c(k), scatter_y(k)):
            copy.wait_send()
        save(k).wait()
    if not back:
        for i in range(6):
            spread_x(i, 1).wait_recv()
            spread_x(i).wait_send()
        for r in (1, 2, 3):
            spread_in(r, 1).wait_recv()
            spread_in(r).wait_send()
    for k in range(4):
        pl.when(stays(k))(lambda k=k: ride_local(k).wait())
        pl.when(jnp.logical_not(stays(k)))(lambda k=k: ride_remote(k).wait_send())
        pl.when(jnp.logical_not(from_self(k)))(lambda k=k: ride_landed(k).wait_recv())


def time_call(back, own, rider, saved, weights, bias, scale):
    frames, patches, features = own.shape
    width = weights.shape[1] // 4
    heads = width // HEAD_DIM
    chunks = patches // CHUNK
    rows = 4 * frames * GROUP
    dma = pltpu.SemaphoreType.DMA
    anywhere = pl.BlockSpec(memory_space=pl.ANY)
    whole = pl.BlockSpec(memory_space=pltpu.VMEM)
    out_shape = [
        jax.ShapeDtypeStruct((4 * frames, patches, features), BF16),
        jax.ShapeDtypeStruct((4 * frames, patches, 3 * width), BF16),
    ]
    if not back:
        out_shape += [
            jax.ShapeDtypeStruct((4 * frames, patches, width), BF16),
            jax.ShapeDtypeStruct((patches // GROUP, heads, rows), F32),
        ]
    rider_shape = (4, frames * patches, BLK) if back else (frames * patches, features)
    out_shape += [
        jax.ShapeDtypeStruct((frames, patches, features), F32),
        jax.ShapeDtypeStruct(rider_shape, BF16),
    ]
    held = 2
    half = saved[2].shape[1:] if back else None
    if back:
        out_shape.insert(-1, jax.ShapeDtypeStruct(half[1:], F32))
    else:
        out_shape += [jax.ShapeDtypeStruct(w.shape, BF16) for w in saved]
        held = 4
    return pl.pallas_call(
        functools.partial(time_kernel, back, scale, heads),
        in_specs=[whole, anywhere] + ([whole, whole, anywhere] if back else [anywhere] * 2) + [whole] * 2,
        out_specs=[anywhere] + [whole] * (len(out_shape) - held) + [anywhere] * (held - 1),
        out_shape=out_shape,
        scratch_shapes=[
            pltpu.VMEM((features, 3 * width), BF16),
            pltpu.VMEM((features, width), BF16),
            pltpu.VMEM((4 * frames, patches, features), BF16),
            pltpu.VMEM((4 * frames, CHUNK, 3 * width), F32),
            pltpu.VMEM((4 * frames, CHUNK, width), F32),
            pltpu.VMEM((2 * frames, patches, features), F32),
            pltpu.VMEM((chunks, 2 * frames, CHUNK, features), BF16),
            pltpu.VMEM((chunks, 2 * frames, CHUNK, features), BF16),
            pltpu.VMEM((chunks, frames, CHUNK, features), BF16),
            pltpu.VMEM((chunks, frames, CHUNK, features), BF16),
        ]
        + [dma((chunks,))] * 10
        + [dma((4,)), dma((4,)), dma((1,)), dma((chunks,))]
        + [dma((9,))] * 2
        + ([pltpu.VMEM(half, BF16)] * 4 + [dma((4,))] * 5 if back else []),
        compiler_params=pltpu.CompilerParams(
            collective_id=2 if back else 1, has_side_effects=True, vmem_limit_bytes=48 * 1024 * 1024
        ),
        cost_estimate=pl.CostEstimate(flops=10**10, transcendentals=10**6, bytes_accessed=10**8),
        name="time_back" if back else "time_forward",
    )(own, rider, *saved, weights, bias)


def feed_kernel(
    resid, delta, upstream, masked, gain, w_in_hbm, w_in_far_hbm, w_out_hbm, w_far_hbm,
    half_in_hbm, half_out_hbm, grad_out, low_out, rows_out, gain_out,
    w_in, w_out, standard, inverse, normed, grads, normed_t, grads_t, hidden, pulled, g_in, g_out, back, ahead,
    back_out, back_in, ahead_out, ahead_in, from_x, from_y,
    w_sem, g_sem, n_send, n_recv, b_send, b_recv, hx_send, hx_recv, hy_send, hy_recv,
):
    y, x, c, z = (lax.axis_index(name) for name in AXES)
    pair, near_y, near_x = (y, x, 1 - c, z), (1 - y, x, c, z), (y, 1 - x, c, z)
    own = resid.shape[0]
    step = own // 2
    slab = 128

    def fetch(s, far):
        size = w_out.shape[1] // 4
        copies = []
        for i in range(4):
            rows = pl.ds(pl.multiple_of(BLK * (2 * ((y + i // 2) % 2) + (x + i % 2) % 2), BLK), BLK)
            source = w_in_far_hbm if far and i == 3 else w_in_hbm
            copies.append(pltpu.make_async_copy(source.at[s, rows], w_in.at[s, rows], w_sem.at[5 + i, s]))
        for i in range(4):
            rows = pl.ds(pl.multiple_of(size * (2 * (i // 2) + (x + i % 2) % 2), size), size)
            source = w_far_hbm if far and i % 2 else w_out_hbm
            copies.append(pltpu.make_async_copy(source.at[s, rows], w_out.at[s, rows], w_sem.at[i, s]))
        return copies

    def fetch_now(s, far):
        for copy in fetch(s, far):
            copy.start()

    for s in range(4):
        pl.when(z == s)(lambda s=s: fetch_now(s, False))
        pl.when(z != s)(lambda s=s: fetch_now(s, True))
    barrier = pltpu.get_barrier_semaphore()
    for peer in (pair, near_y, near_x):
        pl.semaphore_signal(barrier, inc=1, device_id=peer, device_id_type=MESH)

    def remote(src, dst, send, recv, peer=pair):
        return pltpu.make_async_remote_copy(
            src_ref=src, dst_ref=dst, send_sem=send, recv_sem=recv, device_id=peer, device_id_type=MESH
        )

    def block(yb, xb):
        return pl.ds(pl.multiple_of(BLK * (2 * yb + xb), BLK), BLK)

    def away_x(s, i):
        return remote(g_out.at[s, block(i, 1 - x)], from_x.at[i, s], hx_send.at[i, s], hx_recv.at[i, s], near_x)

    def away_y(s, i):
        return remote(g_in.at[s, block(1 - y, i)], from_y.at[i, s], hy_send.at[i, s], hy_recv.at[i, s], near_y)

    def keep(s, i):
        return (
            pltpu.make_async_copy(g_out.at[s, block(i, x)], half_out_hbm.at[i, s], g_sem.at[0, i, s]),
            pltpu.make_async_copy(g_in.at[s, block(y, i)], half_in_hbm.at[i, s], g_sem.at[1, i, s]),
        )

    def combine(s):
        for i in range(2):
            away_x(s, i).wait_recv()
            g_out[s, block(i, x)] = (g_out[s, block(i, x)].astype(F32) + from_x[i, s].astype(F32)).astype(BF16)
            away_y(s, i).wait_recv()
            g_in[s, block(y, i)] = (g_in[s, block(y, i)].astype(F32) + from_y[i, s].astype(F32)).astype(BF16)
            for copy in keep(s, i):
                copy.start()

    def at(i, size):
        return pl.ds(pl.multiple_of(i * size, size), size)

    def prepare(i, carry):
        rows = at(i, step)
        grads[rows] = jnp.where(masked[rows] > 0.0, upstream[rows].astype(F32), 0.0).astype(BF16)
        std, inv = norm_rows(resid[rows] + delta[rows])
        standard[rows] = std
        inverse[rows] = inv
        normed[rows] = (std * gain[...]).astype(BF16)
        return carry

    lax.fori_loop(0, 2, prepare, 0)
    pl.semaphore_wait(barrier, 3)
    mine, theirs = pl.ds(0, own), pl.ds(own, own)
    give_grads = remote(grads.at[mine], grads.at[theirs], n_send.at[0], n_recv.at[0])
    give_normed = remote(normed.at[mine], normed.at[theirs], n_send.at[1], n_recv.at[1])
    give_normed.start()
    give_grads.start()

    def turn(i, carry):
        rows = at(i, slab)
        normed_t[:, rows] = normed[rows].T
        grads_t[:, rows] = grads[rows].T
        return carry

    lax.fori_loop(0, own // slab, turn, 0)
    back[...] = jnp.zeros_like(back)
    ahead[...] = jnp.zeros_like(ahead)
    rate = math.sqrt(2.0 / math.pi)

    def rows_step(s, rows):
        inner = dot_nn(normed[rows], w_in[s])
        square = inner * inner
        bend = jnp.tanh(rate * inner * (1.0 + 0.044715 * square))
        hidden[rows] = (0.5 * inner * (1.0 + bend)).astype(BF16)
        slope = 0.5 * (1.0 + bend) + 0.5 * inner * (1.0 - bend * bend) * (rate * (1.0 + 3.0 * 0.044715 * square))
        pulled[rows] = (dot_nt(grads[rows], w_out[s]) * slope).astype(BF16)
        ahead[rows] = ahead[rows] + dot_nn(hidden[rows], w_out[s])
        back[rows] = back[rows] + dot_nt(pulled[rows], w_in[s])

    def meet():
        give_normed.wait_recv()
        give_grads.wait_recv()
        lax.fori_loop(own // slab, 2 * own // slab, turn, 0)

    def one_piece(s, carry):
        for copy in fetch(s, False):
            copy.wait()

        def one_half(t, carry):
            pl.when(jnp.logical_and(s == 0, t == 1))(meet)
            rows_step(s, at(t, own))
            return carry

        lax.fori_loop(0, 2, one_half, 0)
        g_out[s] = dot_nn(grads_t[...], hidden[...]).astype(BF16)
        g_in[s] = dot_nn(normed_t[...], pulled[...]).astype(BF16)
        for i in range(2):
            away_x(s, i).start()
            away_y(s, i).start()
        return carry

    lax.fori_loop(0, 4, one_piece, 0)
    back_out[...] = back[theirs].astype(BF16)
    give_back = remote(back_out, back_in, b_send.at[0], b_recv.at[0])
    give_back.start()
    ahead_out[...] = ahead[theirs].astype(BF16)
    give_ahead = remote(ahead_out, ahead_in, b_send.at[1], b_recv.at[1])
    give_ahead.start()
    give_back.wait_recv()

    def finish(i, total):
        rows = at(i, step)
        grad = back[rows] + back_in[rows].astype(F32)
        std = standard[rows]
        inner = grad * gain[...]
        mean = jnp.mean(inner, axis=-1, keepdims=True)
        along = jnp.mean(inner * std, axis=-1, keepdims=True)
        full = grads[rows].astype(F32) + (inner - mean - std * along) * inverse[rows]
        grad_out[rows] = full
        low_out[rows] = full.astype(BF16)
        return total + jnp.sum(grad * std, axis=0, keepdims=True)

    gain_out[...] = lax.fori_loop(0, 2, finish, jnp.zeros((1, resid.shape[1]), F32))
    give_ahead.wait_recv()

    def emit(i, carry):
        rows = at(i, step)
        rows_out[rows] = (resid[rows] + delta[rows] + ahead[rows] + ahead_in[rows].astype(F32)).astype(BF16)
        return carry

    lax.fori_loop(0, 2, emit, 0)
    lax.fori_loop(0, 4, lambda s, carry: (combine(s), carry)[1], 0)
    for copy in (give_normed, give_grads, give_back, give_ahead):
        copy.wait_send()
    for s in range(4):
        for i in range(2):
            away_x(s, i).wait_send()
            away_y(s, i).wait_send()
            for copy in keep(s, i):
                copy.wait()


def feed(resid, delta, upstream, masked, gain, w_in, w_in_far, w_out, w_far):
    own, features = resid.shape
    units = w_in.shape[2]
    dma = pltpu.SemaphoreType.DMA
    anywhere = pl.BlockSpec(memory_space=pl.ANY)
    whole = pl.BlockSpec(memory_space=pltpu.VMEM)

    def low(*shape):
        return pltpu.VMEM(shape, BF16)

    def high(*shape):
        return pltpu.VMEM(shape, F32)

    return pl.pallas_call(
        feed_kernel,
        in_specs=[whole] * 5 + [anywhere] * 4,
        out_specs=[anywhere] * 2 + [whole] * 4,
        out_shape=[
            jax.ShapeDtypeStruct((2, 4, BLK, units), BF16),
            jax.ShapeDtypeStruct((2, 4, BLK, units), BF16),
            jax.ShapeDtypeStruct((own, features), F32),
            jax.ShapeDtypeStruct((own, features), BF16),
            jax.ShapeDtypeStruct((own, features), BF16),
            jax.ShapeDtypeStruct((1, features), F32),
        ],
        scratch_shapes=[
            low(4, features, units), low(4, units, features), high(own, features), high(own, 1),
            low(2 * own, features), low(2 * own, features), low(features, 2 * own), low(features, 2 * own),
            low(2 * own, units), low(2 * own, units), low(4, features, units), low(4, features, units),
            high(2 * own, features), high(2 * own, features),
            low(own, features), low(own, features), low(own, features), low(own, features),
            low(2, 4, BLK, units), low(2, 4, BLK, units),
            dma((9, 4)), dma((2, 2, 4)), dma((2,)), dma((2,)), dma((2,)), dma((2,)),
            dma((2, 4)), dma((2, 4)), dma((2, 4)), dma((2, 4)),
        ],
        compiler_params=pltpu.CompilerParams(
            collective_id=4, has_side_effects=True, vmem_limit_bytes=60 * 1024 * 1024
        ),
        cost_estimate=pl.CostEstimate(flops=26 * 10**9, transcendentals=2 * 10**6, bytes_accessed=10**8),
        name="feed",
    )(resid, delta, upstream, masked, gain, w_in, w_in_far, w_out, w_far)


def leave_kernel(
    scale,
    part_hbm, next_hbm, grad_hbm, out_hbm, joined_hbm, mixed_hbm, lhs_hbm, weight_hbm, std_hbm, time_hbm, feed_hbm, feed_in_hbm,
    totals, inverse_next, inverse, masked, gain_next, gain, small_in,
    kept_out, landed_out, feed_kept, feed_landed, time_out, rows_out, small_out,
    part, std, base, w_out, dj, mixed, lhs, weight, low_grads, turned, dmixed, go,
    t_own, t_in, tz_out, tz_in, t_total, ty_out, ty_in, tc_out, tc_in,
    f_own, f_in, fz_out, fz_in, f_total, f_other, fc_out, fc_in,
    grads, a1_out, a1_in, b1_out, b1_in, a2_out, a2_in, b2_out, b2_in, z_out, z_in,
    half_out, half_in, ready, core_out, core_in, sums, sum_out, sum_in, share_in,
    a1_send, a1_recv, b1_send, b1_recv, a2_send, a2_recv, b2_send, b2_recv, z_send, z_recv,
    h_send, h_recv, r_send, r_recv, c_send, c_recv, s_send, s_recv, p_send, p_recv, local,
    g_send, g_recv, tx_send, tx_recv, tz_send, tz_recv, ty_send, ty_recv, fy_send, fy_recv, fz_send, fz_recv, t_local, f_local, fetched,
):
    y, x, c, z = (lax.axis_index(name) for name in AXES)
    near_y, near_x, pair = (1 - y, x, c, z), (y, 1 - x, c, z), (y, x, 1 - c, z)
    own = std.shape[0]
    third = go.shape[1] // 4
    wide = 3 * third
    two = 2 * third
    slab = 128

    fetches = [
        pltpu.make_async_copy(src, dst, fetched.at[i])
        for i, (src, dst) in enumerate((
            (part_hbm, part), (next_hbm, std), (grad_hbm, base), (out_hbm, w_out), (joined_hbm, dj), (mixed_hbm, mixed),
            (lhs_hbm, lhs), (weight_hbm, weight), (feed_in_hbm, f_other),
        ))
    ]
    for copy in fetches:
        copy.start()
    fetch_std = pltpu.make_async_copy(std_hbm, std, fetched.at[9])

    barrier = pltpu.get_barrier_semaphore()
    for dc in range(2):
        for dz in range(4):
            if dc or dz:
                pl.semaphore_signal(barrier, inc=1, device_id=(y, x, (c + dc) % 2, (z + dz) % 4), device_id_type=MESH)
    for peer in (near_y, near_x):
        pl.semaphore_signal(barrier, inc=1, device_id=peer, device_id_type=MESH)
    pl.semaphore_wait(barrier, 9)

    def remote(src, dst, send, recv, peer):
        return pltpu.make_async_remote_copy(
            src_ref=src, dst_ref=dst, send_sem=send, recv_sem=recv, device_id=peer, device_id_type=MESH
        )

    def at(i, length):
        return pl.ds(pl.multiple_of(i * length, length), length)

    def along(r):
        return (y, x, c, (z + r) % 4)

    def time_x(yb):
        return remote(time_hbm.at[at(2 * yb + 1 - x, BLK)], t_in.at[yb], tx_send.at[yb], tx_recv.at[yb], near_x)

    def time_keep(yb):
        return pltpu.make_async_copy(time_hbm.at[at(2 * yb + x, BLK)], t_own.at[yb], t_local.at[yb])

    def time_z(r):
        return remote(tz_out.at[r], tz_in.at[r], tz_send.at[r], tz_recv.at[r], along(r))

    def feed_y(r):
        s = (z + r) % 4
        return remote(feed_hbm.at[1 - y, s], f_in.at[r], fy_send.at[r], fy_recv.at[r], near_y)

    def feed_keep(r):
        return pltpu.make_async_copy(feed_hbm.at[y, (z + r) % 4], f_own.at[r], f_local.at[r])

    def feed_z(r):
        return remote(fz_out.at[r], fz_in.at[r], fz_send.at[r], fz_recv.at[r], along(r))

    for r in (1, 2, 3, 0):
        feed_y(r).start()
        feed_keep(r).start()
    for yb in range(2):
        time_x(yb).start()
        time_keep(yb).start()

    def feed_step(r):
        feed_y(r).wait_recv()
        feed_keep(r).wait()
        total = f_own[r].astype(F32) + f_in[r].astype(F32)
        if r == 0:
            f_total[...] = total
        else:
            fz_out[r] = total.astype(BF16)
            feed_z(r).start()

    def time_step():
        for yb in range(2):
            time_x(yb).wait_recv()
            time_keep(yb).wait()
        for r in (1, 2, 3, 0):
            piece_at = at((z + r) % 4, BLK)
            for yb in range(2):
                total = t_own[yb, :, piece_at].astype(F32) + t_in[yb, :, piece_at].astype(F32)
                if r == 0:
                    t_total[yb] = total
                else:
                    tz_out[r, yb] = total.astype(BF16)
            if r:
                time_z(r).start()

    step = own // 2
    for copy in fetches[:3]:
        copy.wait()

    def norm_back(grad, standard, weights, inv):
        inner = grad * weights
        mean = jnp.mean(inner, axis=-1, keepdims=True)
        slope = jnp.mean(inner * standard, axis=-1, keepdims=True)
        return (inner - mean - standard * slope) * inv

    def after_time(i, total):
        rows = at(i, step)
        grad, standard = part[rows], std[rows]
        full = base[rows] + norm_back(grad, standard, gain_next[...], inverse_next[rows])
        base[rows] = full
        low_grads[rows] = full.astype(BF16)
        return total + jnp.sum(grad * standard, axis=0, keepdims=True)

    zero = jnp.zeros((1, std.shape[1]), F32)
    next_grad = lax.fori_loop(0, 2, after_time, zero)
    give = remote(low_grads.at[pl.ds(0, own)], low_grads.at[pl.ds(own, own)], g_send.at[0], g_recv.at[0], pair)
    give.start()
    fetch_std.start()
    for copy in fetches[3:6]:
        copy.wait()

    def attend(i, carry):
        rows = at(i, slab)
        for h in range(mixed.shape[1] // PAIR):
            places = [pl.ds((3 * h + j) * PAIR, PAIR) for j in range(3)]
            q, k, v = (dj[rows, place] for place in places)
            lines = [totals[i, 2 * h + j : 2 * h + j + 1, :] for j in range(2)]
            found = attend_pair_back(q, k, v, dmixed[rows, h * PAIR : (h + 1) * PAIR], lines, None, scale)
            for place, value in zip(places, found):
                dj[rows, place] = value.astype(BF16)
        return carry

    def turn(i, carry):
        turned[:, at(i, slab)] = low_grads[at(i, slab)].T
        return carry

    def attend_half(t):
        rows = pl.ds(t * own, own)
        dmixed[rows] = dot_nt(low_grads[rows], w_out[...]).astype(BF16)
        lax.fori_loop(t * own // slab, (t + 1) * own // slab, attend, 0)
        lax.fori_loop(t * own // slab, (t + 1) * own // slab, turn, 0)

    attend_half(0)
    feed_step(1)
    feed_step(2)
    give.wait_recv()
    attend_half(1)
    feed_step(3)
    time_step()
    feed_step(0)
    for copy in fetches[6:]:
        copy.wait()
    go[...] = dot_nn(turned[...], mixed[...]).astype(BF16)

    def block(yb, xb):
        return pl.ds(pl.multiple_of(BLK * (2 * yb + xb), BLK), BLK)

    def a1(i):
        return remote(a1_out.at[i], a1_in.at[i], a1_send.at[i], a1_recv.at[i], near_x)

    def b1(i):
        return remote(b1_out.at[i], b1_in.at[i], b1_send.at[i], b1_recv.at[i], near_y)

    def a2(i):
        return remote(a2_out.at[i], a2_in.at[i], a2_send.at[i], a2_recv.at[i], near_y)

    def b2(i):
        return remote(b2_out.at[i], b2_in.at[i], b2_send.at[i], b2_recv.at[i], near_x)

    def to_z(r):
        return remote(z_out.at[r], z_in.at[r], z_send.at[r], z_recv.at[r], along(r))

    def piece(i, carry):
        s = (z + i + 1) % 4
        made = dot_nn(lhs[...], dj[:, pl.ds(pl.multiple_of(s * wide, third), wide)])
        grads[i, :, :wide] = made
        grads[i, :, wide:] = go[:, pl.ds(pl.multiple_of(s * third, third), third)].astype(F32)
        for b in range(2):
            a1_out[i, b] = grads[i, block(b, 1 - x), :two].astype(BF16)
            b1_out[i, b] = grads[i, block(1 - y, b), two:].astype(BF16)
        a1(i).start()
        b1(i).start()
        return carry

    lax.fori_loop(0, 4, piece, 0)

    def second(i):
        a1(i).wait_recv()
        a2_out[i] = (grads[i, block(1 - y, x), :two] + a1_in[i, 1 - y].astype(F32)).astype(BF16)
        a2(i).start()
        b1(i).wait_recv()
        b2_out[i] = (grads[i, block(y, 1 - x), two:] + b1_in[i, 1 - x].astype(F32)).astype(BF16)
        b2(i).start()
        grads[i, block(y, x), :two] = grads[i, block(y, x), :two] + a1_in[i, y].astype(F32)
        grads[i, block(y, x), two:] = grads[i, block(y, x), two:] + b1_in[i, x].astype(F32)

    def third_step(i):
        a2(i).wait_recv()
        b2(i).wait_recv()
        grads[i, block(y, x), :two] = grads[i, block(y, x), :two] + a2_in[i].astype(F32)
        grads[i, block(y, x), two:] = grads[i, block(y, x), two:] + b2_in[i].astype(F32)
        if i < 3:
            z_out[i + 1] = grads[i, block(y, x), :].astype(BF16)
            to_z(i + 1).start()

    def away(i, carry):
        rows = pl.ds(pl.multiple_of(own + i * step, step), step)
        half_out[pl.ds(pl.multiple_of(i * step, step), step)] = dot_nt(dj[rows], weight[...]).astype(BF16)
        return carry

    lax.fori_loop(0, 2, away, 0)
    swap = remote(half_out, half_in, h_send.at[0], h_recv.at[0], pair)
    swap.start()
    second(0)
    fetch_std.wait()
    sums[...] = small_in[...]
    sums[1:2] = next_grad
    swap.wait_recv()

    def home(i, totals):
        rows = pl.ds(pl.multiple_of(i * step, step), step)
        grad = dot_nt(dj[rows], weight[...]) + half_in[rows].astype(F32)
        standard = std[rows]
        full = base[rows] + norm_back(grad, standard, gain[...], inverse[rows])
        hide = masked[rows] > 0.0
        ready[rows] = jnp.where(hide, 0.0, full).astype(BF16)
        return (
            totals[0] + jnp.sum(grad * standard, axis=0, keepdims=True),
            totals[1] + jnp.sum(jnp.where(hide, full, 0.0), axis=0, keepdims=True),
        )

    gain_grad, embed_grad = lax.fori_loop(0, 2, home, (zero, zero))
    sums[0:1] = gain_grad
    sums[3:4] = embed_grad

    def columns(s):
        return pl.ds(pl.multiple_of(s * BLK, BLK), BLK)

    def stays(k):
        return jnp.logical_and(z == k, z // 2 == c)

    def ride(k):
        slot = 2 * (z % 2) + c
        return remote(ready.at[:, columns(k)], rows_out.at[slot], r_send.at[k], r_recv.at[slot], (y, x, z // 2, k))

    def ride_local(k):
        return pltpu.make_async_copy(ready.at[:, columns(k)], rows_out.at[2 * (z % 2) + c], local.at[3])

    for k in range(4):
        pl.when(stays(k))(lambda k=k: ride_local(k).start())
        pl.when(jnp.logical_not(stays(k)))(lambda k=k: ride(k).start())

    def share(h):
        peer = (pair, near_y, near_x)[h]
        return remote(sum_out.at[h], sum_in.at[h], s_send.at[h], s_recv.at[h], peer)

    def begin_share(h):
        sum_out[h] = sums[...]
        share(h).start()

    def end_share(h):
        share(h).wait_recv()
        sums[...] = sums[...] + sum_in[h]

    begin_share(0)
    second(1)
    third_step(0)
    end_share(0)
    begin_share(1)
    second(2)
    third_step(1)
    end_share(1)
    begin_share(2)
    second(3)
    third_step(2)
    end_share(2)
    sum_out[3] = sums[...]

    def deal(r):
        s = (z + r) % 4
        return remote(sum_out.at[3, :, columns(s)], share_in.at[r], p_send.at[r], p_recv.at[r], (y, x, c, s))

    for r in (1, 2, 3):
        deal(r).start()
    third_step(3)
    parity = BLK // 2

    for r in (1, 2, 3):
        time_z(r).wait_recv()
        t_total[...] = t_total[...] + tz_in[r].astype(F32)
    ty_out[...] = t_total[1 - y].astype(BF16)
    swap_y = remote(ty_out, ty_in, ty_send.at[0], ty_recv.at[0], near_y)
    swap_y.start()
    for r in (1, 2, 3):
        feed_z(r).wait_recv()
        f_total[...] = f_total[...] + fz_in[r].astype(F32)
    fc_out[0] = f_other[at(1 - c, parity)].astype(BF16)
    fc_out[1] = f_total[at(1 - c, parity)].astype(BF16)
    swap_feed = remote(fc_out, fc_in, c_send.at[1], c_recv.at[1], pair)
    swap_feed.start()
    feed_kept[0] = f_other[at(c, parity)]
    feed_kept[1] = f_total[at(c, parity)]
    swap_y.wait_recv()
    tc_out[0] = t_total[y, at(1 - c, parity)].astype(BF16)
    tc_out[1] = ty_in[at(1 - c, parity)]
    swap_time = remote(tc_out, tc_in, c_send.at[2], c_recv.at[2], pair)
    swap_time.start()
    time_out[0, 0] = t_total[y, at(c, parity)]
    time_out[0, 1] = ty_in[at(c, parity)].astype(F32)
    for r in (1, 2, 3):
        to_z(r).wait_recv()
    total = grads[3, block(y, x), :]
    for r in (1, 2, 3):
        total = total + z_in[r].astype(F32)
    grads[3, block(y, x), :] = total
    rows = BLK // 2

    def core_rows(core):
        return pl.ds(pl.multiple_of(BLK * (2 * y + x) + rows * core, rows), rows)

    core_out[...] = grads[3, core_rows(1 - c), :].astype(BF16)
    last = remote(core_out, core_in, c_send.at[0], c_recv.at[0], pair)
    last.start()
    kept_out[...] = grads[3, core_rows(c), :]
    result = sums[:, columns(z)]
    for r in (1, 2, 3):
        deal(r).wait_recv()
        result = result + share_in[r]
    small_out[...] = result
    swap_feed.wait_recv()
    feed_landed[...] = fc_in[...].astype(F32)
    swap_time.wait_recv()
    time_out[1] = tc_in[...].astype(F32)
    last.wait_recv()
    landed_out[...] = core_in[...].astype(F32)

    for copy in (last, swap, give, swap_y, swap_feed, swap_time):
        copy.wait_send()
    for yb in range(2):
        time_x(yb).wait_send()
    for r in range(4):
        feed_y(r).wait_send()
    for r in (1, 2, 3):
        time_z(r).wait_send()
        feed_z(r).wait_send()
    for i in range(4):
        for copy in (a1(i), b1(i), a2(i), b2(i)):
            copy.wait_send()
    for r in (1, 2, 3):
        to_z(r).wait_send()
        deal(r).wait_send()
    for h in range(3):
        share(h).wait_send()
    for k in range(4):
        pl.when(stays(k))(lambda k=k: ride_local(k).wait())
        pl.when(jnp.logical_not(stays(k)))(lambda k=k: ride(k).wait_send())
        from_self = jnp.logical_and(2 * c + k // 2 == z, c == k % 2)

        def landed(k=k):
            remote(ready.at[:, columns(k)], rows_out.at[k], r_send.at[k], r_recv.at[k], near_y).wait_recv()

        pl.when(jnp.logical_not(from_self))(landed)


def leave(
    part, std_next, grad, w_out, joined, mixed, lhs, weight, std, g_time, g_out, g_in,
    totals, inverse_next, inverse, masked, gain_next, gain, small, scale,
):
    own, features = std.shape
    cols4 = mixed.shape[1]
    quarter = cols4 // 4
    units = g_in.shape[1]
    dma = pltpu.SemaphoreType.DMA
    anywhere = pl.BlockSpec(memory_space=pl.ANY)
    whole = pl.BlockSpec(memory_space=pltpu.VMEM)
    parity = BLK // 2

    def low(*shape):
        return pltpu.VMEM(shape, BF16)

    def high(*shape):
        return pltpu.VMEM(shape, F32)

    return pl.pallas_call(
        functools.partial(leave_kernel, scale),
        in_specs=[anywhere] * 12 + [whole] * 7,
        out_specs=[whole] * 5 + [anywhere, whole],
        out_shape=[
            jax.ShapeDtypeStruct((parity, cols4), F32),
            jax.ShapeDtypeStruct((parity, cols4), F32),
            jax.ShapeDtypeStruct((2, parity, units), F32),
            jax.ShapeDtypeStruct((2, parity, units), F32),
            jax.ShapeDtypeStruct((2, 2, parity, BLK), F32),
            jax.ShapeDtypeStruct((4, own, BLK), BF16),
            jax.ShapeDtypeStruct((8, BLK), F32),
        ],
        scratch_shapes=[
            high(own, features), high(own, features), high(own, features), low(*w_out.shape), low(*joined.shape),
            low(*mixed.shape), low(*lhs.shape), low(*weight.shape), low(2 * own, features), low(features, 2 * own),
            low(*mixed.shape), low(features, cols4),
            low(2, BLK, features), low(2, BLK, features), low(4, 2, BLK, BLK), low(4, 2, BLK, BLK), high(2, BLK, BLK),
            low(BLK, BLK), low(BLK, BLK), low(2, parity, BLK), low(2, parity, BLK),
            low(4, BLK, units), low(4, BLK, units), low(4, BLK, units), low(4, BLK, units),
            high(BLK, units), high(BLK, units), low(2, parity, units), low(2, parity, units),
            high(4, features, cols4),
            low(4, 2, BLK, 2 * quarter), low(4, 2, BLK, 2 * quarter), low(4, 2, BLK, 2 * quarter), low(4, 2, BLK, 2 * quarter),
            low(4, BLK, 2 * quarter), low(4, BLK, 2 * quarter), low(4, BLK, 2 * quarter), low(4, BLK, 2 * quarter),
            low(4, BLK, cols4), low(4, BLK, cols4),
            low(own, features), low(own, features), low(own, features),
            low(parity, cols4), low(parity, cols4),
            high(8, features), high(4, 8, features), high(3, 8, features), high(4, 8, BLK),
        ]
        + [dma((4,))] * 10
        + [dma((1,)), dma((1,)), dma((4,)), dma((4,)), dma((3,)), dma((3,)), dma((3,)), dma((3,)), dma((4,)), dma((4,)), dma((4,))]
        + [dma((1,)), dma((1,)), dma((2,)), dma((2,)), dma((4,)), dma((4,)), dma((1,)), dma((1,))]
        + [dma((4,)), dma((4,)), dma((4,)), dma((4,)), dma((2,)), dma((4,)), dma((10,))],
        compiler_params=pltpu.CompilerParams(
            collective_id=3, has_side_effects=True, vmem_limit_bytes=62 * 1024 * 1024
        ),
        cost_estimate=pl.CostEstimate(flops=2 * 10**10, transcendentals=10**6, bytes_accessed=10**8),
        name="leave",
    )(
        part, std_next, grad, w_out, joined, mixed, lhs, weight, std, g_time, g_out, g_in,
        totals, inverse_next, inverse, masked, gain_next, gain, small,
    )


def tie(*values):
    return lax.optimization_barrier(values)


def norm_rows(resid):
    mean = jnp.mean(resid, axis=-1, keepdims=True)
    centered = resid - mean
    inverse = lax.rsqrt(jnp.mean(centered * centered, axis=-1, keepdims=True) + eps_norm)
    return (centered * inverse, inverse)


def norm_rows_back(grad, standardized, inverse, gain):
    gain_grad = jnp.sum(grad * standardized, axis=0)
    inner = grad * gain
    mean = jnp.mean(inner, axis=-1, keepdims=True)
    along = jnp.mean(inner * standardized, axis=-1, keepdims=True)
    return ((inner - mean - standardized * along) * inverse, gain_grad)


def cols(parts):
    return jnp.concatenate(parts, axis=1)


def rows_of(parts):
    return jnp.concatenate(parts, axis=0)


def token_parallel(
    tokens,
    cotangent,
    ratio,
    priority,
    frame_order,
    mask_embed,
    gains,
    qkv_space,
    out_space,
    qkv_time,
    out_time,
    w_in,
    w_out,
):
    scale = 1.0 / math.sqrt(HEAD_DIM)
    y, x, c, z = (lax.axis_index(name) for name in AXES)
    patches = tokens.shape[2]
    width = qkv_space.shape[0]
    frames_own = tokens.shape[0] * tokens.shape[1] // 4
    frames_all = frame_order.shape[1]
    own = frames_own * patches
    hidden_own = w_in.shape[1] // 2
    plane = 2 * y + x
    k_own = 2 * (z % 2) + c

    masked_here = (priority < ratio[:, None, None]).astype(jnp.int32).reshape(2, -1)
    info = cols([masked_here, frame_order])
    info = jnp.where(z // 2 == c, info, hop_c(info))
    info = lax.dynamic_index_in_dim(info, z % 2, 0, keepdims=False)
    masked = lax.dynamic_slice_in_dim(info, c * own, own, 0)[:, None] != 0
    order = info[2 * own :].reshape(2, 2, frames_own)
    order = jnp.where(y == 1, order[::-1], order)
    order = jnp.where(c == 1, order[:, ::-1], order).swapaxes(0, 1).reshape(frames_all)
    order = jnp.repeat(order, GROUP)
    patch = jnp.arange(frames_all * GROUP) % GROUP
    visible = (order[:, None] <= order[None, :]) & (patch[:, None] == patch[None, :])
    bias = jnp.where(visible, 0.0, -1e30).astype(F32)

    vectors = rows_of([mask_embed[None], gains, jnp.zeros((4, BLK), BF16)])
    head = (2 * y + c) * HEAD_DIM
    ti_own = cols(
        [
            lax.dynamic_slice_in_dim(qkv_time, head, HEAD_DIM, 2).reshape(width, -1),
            lax.dynamic_slice_in_dim(out_time, head, HEAD_DIM, 0).T,
        ]
    )
    (
        ws_qkv, ws_out, wt_all, wf_out, wf_in, joined0, turned0, std0,
        mixed0, total0, inv0, resid1, std1, inv1, normed1, vectors,
    ) = enter(
        tokens.reshape(4, own, BLK),
        vectors,
        jnp.swapaxes(qkv_space, 0, 1),
        out_space,
        ti_own,
        w_out,
        w_in,
        masked.astype(F32),
        scale,
    )
    gain = [vectors[1 + i : 2 + i] for i in range(3)]

    half = qkv_space.shape[2] // 2
    normed1, joined1, mixed1, total1, delta, upstream, wf_far, wf_in_far = time_call(
        False,
        normed1.reshape(frames_own, patches, width),
        cotangent.reshape(4, own, BLK),
        [wf_out, wf_in],
        wt_all,
        bias,
        scale,
    )
    normed1 = normed1.reshape(4 * own, width)
    mixed1 = mixed1.reshape(4 * own, -1)
    w_in_half, w_out_half, grad2, grad2_low, block_rows, gain_grad2 = feed(
        resid1, delta.reshape(own, width), upstream, masked.astype(F32), gain[2], wf_in, wf_in_far, wf_out, wf_far
    )

    def by_core(kept, landed):
        return jnp.where(c == 0, jnp.concatenate([kept, landed], -1), jnp.concatenate([landed, kept], -1))

    gb2, djoined1, part1, g_w_in, block_out = time_call(
        True,
        grad2_low.reshape(frames_own, patches, width),
        block_rows,
        [joined1, total1, w_in_half],
        wt_all,
        bias,
        scale,
    )
    block_out = block_out.reshape(tokens.shape)
    gb2 = gb2.reshape(4 * own, width)
    djoined1 = djoined1.reshape(4 * own, -1)
    g_t_qkv = dot_tn(normed1, djoined1).astype(BF16).reshape(width, 3, 4, HEAD_DIM)
    g_t_out = dot_tn(gb2, mixed1).astype(BF16).reshape(width, 1, 4, HEAD_DIM)
    g_time = jnp.swapaxes(jnp.concatenate([g_t_qkv, g_t_out], axis=1), 1, 2).reshape(width, width)
    small = rows_of([jnp.zeros((2, width), F32), gain_grad2, jnp.zeros((5, width), F32)])
    kept, landed, feed_kept, feed_landed, quad, grad_tokens, small = leave(
        part1.reshape(own, width), std1, grad2, ws_out, joined0, mixed0, turned0, ws_qkv, std0, g_time, w_out_half, g_w_in,
        total0, inv1, inv0, masked.astype(F32), gain[1], gain[0], small, scale,
    )
    grad_tokens = grad_tokens.reshape(tokens.shape).astype(F32)

    rows = BLK // 2
    grad_qkv_space = by_core(
        kept[:, : 3 * half].reshape(rows, 3, half), landed[:, : 3 * half].reshape(rows, 3, half)
    )
    grad_out_space = by_core(kept[:, 3 * half :], landed[:, 3 * half :]).T
    grad_w_in = by_core(feed_kept[0], feed_landed[0])
    grad_w_out = by_core(feed_kept[1], feed_landed[1]).T
    quad = jnp.transpose(quad, (2, 0, 1, 3)).reshape(rows, 2, 2, 4, HEAD_DIM)
    quad = jnp.where(c == 1, quad[:, ::-1], quad)
    quad = jnp.where(y == 1, quad[:, :, ::-1], quad)
    quad = jnp.transpose(quad, (0, 3, 2, 1, 4)).reshape(rows, 4, 4 * HEAD_DIM)
    grad_qkv_time = quad[:, :3]
    grad_out_time = quad[:, 3].T
    return (
        block_out,
        grad_tokens,
        small[3],
        small[:3],
        grad_qkv_space,
        grad_out_space,
        grad_qkv_time,
        grad_out_time,
        grad_w_in,
        grad_w_out,
    )


def solution(mesh):
    sizes = (mesh.shape["tm"], mesh.shape["clip"], mesh.shape["mp"])
    if sizes == (2, 4, 4):
        mesh = jax.sharding.Mesh(mesh.devices.reshape(2, 2, 2, 4), AXES)
        step, clip = token_parallel, ("x", "c")
    else:
        step, clip = shards, ("clip",)
    return jax.shard_map(
        step,
        mesh=mesh,
        in_specs=(
            P(clip, "tm", None, "mp"),
            P(clip, "tm", None, "mp"),
            P(clip),
            P(clip, "tm", None),
            P(clip, None),
            P("mp"),
            P(None, "mp"),
            P(None, None, "mp"),
            P("mp", None),
            P(None, None, "mp"),
            P("mp", None),
            P(None, "mp"),
            P("mp", None),
        ),
        out_specs=(
            P(clip, "tm", None, "mp"),
            P(clip, "tm", None, "mp"),
            P("mp"),
            P(None, "mp"),
            P(("tm",) + clip, None, "mp"),
            P("mp", ("tm",) + clip),
            P(("tm",) + clip, None, "mp"),
            P("mp", ("tm",) + clip),
            P(("tm",) + clip, "mp"),
            P("mp", ("tm",) + clip),
        ),
        check_vma=False,
    )
```

```python
import functools
import math

import jax
import jax.numpy as jnp
from jax import lax
from jax.experimental import pallas as pl
from jax.experimental.pallas import tpu as pltpu
from jax.sharding import PartitionSpec as P

HEAD_DIM = 64
MICRO = 2


eps_norm = 1e-05


def gelu_tanh(values):
    return jax.nn.gelu(values, approximate=True)


def norm_forward_pass(residual_stream, gain_coefficients, complete_width):
    reduced_totals = lax.psum(
        (jnp.sum(residual_stream, axis=-1), jnp.sum(residual_stream * residual_stream, axis=-1)),
        "mp",
    )
    centered_rows = reduced_totals[0] / complete_width
    spread = reduced_totals[1] / complete_width - centered_rows * centered_rows
    inverse_scale = lax.rsqrt(spread + eps_norm)
    standardized_rows = (residual_stream - centered_rows[:, None]) * inverse_scale[:, None]
    shard_rows = (standardized_rows * gain_coefficients).astype(jnp.bfloat16)
    normalized_rows = lax.all_gather(shard_rows, "mp", axis=1, tiled=True)
    return (normalized_rows, standardized_rows, inverse_scale)


def norm_reverse_pass(
    normalized_gradient, standardized_rows, inverse_scale, gain_coefficients, complete_width
):
    gain_gradient = jnp.sum(normalized_gradient * standardized_rows, axis=0)
    standardized_gradient = normalized_gradient * gain_coefficients
    reduced_totals = lax.psum(
        (
            jnp.sum(standardized_gradient, axis=-1),
            jnp.sum(standardized_gradient * standardized_rows, axis=-1),
        ),
        "mp",
    )
    grad_resid = (
        standardized_gradient
        - reduced_totals[0][:, None] / complete_width
        - standardized_rows * (reduced_totals[1][:, None] / complete_width)
    ) * inverse_scale[:, None]
    return (grad_resid, gain_gradient)


def sum_features(grad_full):
    return lax.psum_scatter(
        grad_full.astype(jnp.bfloat16), "mp", scatter_dimension=1, tiled=True
    ).astype(jnp.float32)


def branch_out(hidden, weight):
    partial_rows = jnp.dot(hidden, weight, preferred_element_type=jnp.float32)
    return lax.psum_scatter(partial_rows, "mp", scatter_dimension=1, tiled=True)


def branch_back(grad_resid, hidden, weight):
    grad_rows = lax.all_gather(grad_resid.astype(jnp.bfloat16), "mp", axis=1, tiled=True)
    weight_grad = jnp.einsum("rk,rd->kd", hidden, grad_rows, preferred_element_type=jnp.float32)
    grad_hidden = jnp.einsum("rd,kd->rk", grad_rows, weight, preferred_element_type=jnp.float32)
    return (grad_hidden, weight_grad)


def qkv_back(normalized_rows, grad_joined, weight):
    weight_grad = jnp.einsum(
        "rd,trk->dtk", normalized_rows, grad_joined, preferred_element_type=jnp.float32
    )
    grad_full = jnp.einsum("trk,dtk->rd", grad_joined, weight, preferred_element_type=jnp.float32)
    return (weight_grad, sum_features(grad_full))


def reduce_grads(local_grads, small_grads):
    reduced = (
        lax.psum_scatter(local_grads[0], ("tm", "clip"), scatter_dimension=0, tiled=True),
        lax.psum_scatter(local_grads[1], ("tm", "clip"), scatter_dimension=1, tiled=True),
        lax.psum_scatter(local_grads[2], ("tm", "clip"), scatter_dimension=0, tiled=True),
        lax.psum_scatter(local_grads[3], ("tm", "clip"), scatter_dimension=1, tiled=True),
        lax.psum_scatter(local_grads[4], ("tm", "clip"), scatter_dimension=0, tiled=True),
        lax.psum_scatter(local_grads[5], ("tm", "clip"), scatter_dimension=1, tiled=True),
    )
    reduced_small = lax.psum((small_grads[0], small_grads[1]), ("tm", "clip"))
    return (reduced, reduced_small)


def space_forward(normalized_rows, weight, frame_count, patches, heads_local, scale):
    joined = jnp.einsum(
        "rd,dtk->trk", normalized_rows, weight, preferred_element_type=jnp.float32
    ).astype(jnp.bfloat16)
    shape_heads = (frame_count, patches, heads_local, HEAD_DIM)
    scores = (
        jnp.einsum(
            "bshd,bthd->bhst",
            joined[0].reshape(shape_heads),
            joined[1].reshape(shape_heads),
            preferred_element_type=jnp.float32,
        )
        * scale
    )
    highest = jnp.max(scores, axis=-1, keepdims=True)
    exponent = jnp.exp(scores - highest)
    reduced_totals = jnp.sum(exponent, axis=-1, keepdims=True)
    log_total = highest + jnp.log(reduced_totals)
    attention = (exponent / reduced_totals).astype(jnp.bfloat16)
    mixed = jnp.einsum(
        "bhst,bthd->bshd",
        attention,
        joined[2].reshape(shape_heads),
        preferred_element_type=jnp.float32,
    )
    return (
        joined,
        log_total,
        mixed.astype(jnp.bfloat16).reshape(frame_count * patches, heads_local * HEAD_DIM),
    )


def space_backward(grad_mixed, joined, log_total, frame_count, patches, heads_local, scale):
    shape_heads = (frame_count, patches, heads_local, HEAD_DIM)
    queries = joined[0].reshape(shape_heads)
    key_rows = joined[1].reshape(shape_heads)
    values = joined[2].reshape(shape_heads)
    grad_out = grad_mixed.reshape(shape_heads)
    scores = (
        jnp.einsum("bshd,bthd->bhst", queries, key_rows, preferred_element_type=jnp.float32) * scale
    )
    attention = jnp.exp(scores - log_total)
    grad_values = jnp.einsum(
        "bhst,bshd->bthd",
        attention.astype(jnp.bfloat16),
        grad_out,
        preferred_element_type=jnp.float32,
    )
    grad_att = jnp.einsum("bshd,bthd->bhst", grad_out, values, preferred_element_type=jnp.float32)
    grad_scores = (
        attention * (grad_att - jnp.sum(attention * grad_att, axis=-1, keepdims=True))
    ).astype(jnp.bfloat16)
    grad_queries = (
        jnp.einsum("bhst,bthd->bshd", grad_scores, key_rows, preferred_element_type=jnp.float32)
        * scale
    )
    grad_keys = (
        jnp.einsum("bhst,bshd->bthd", grad_scores, queries, preferred_element_type=jnp.float32)
        * scale
    )
    row_count = frame_count * patches
    stacked = jnp.stack(
        [
            grad_queries.reshape(row_count, -1),
            grad_keys.reshape(row_count, -1),
            grad_values.reshape(row_count, -1),
        ]
    )
    return stacked.astype(jnp.bfloat16)


def time_scores(queries, keys_all, visible, scale):
    scores = (
        jnp.einsum("cfshd,cgshd->chfgs", queries, keys_all, preferred_element_type=jnp.float32)
        * scale
    )
    return jnp.where(visible, scores, -1e30)


def time_forward(queries, keys_all, values_all, visible, scale):
    scores = time_scores(queries, keys_all, visible, scale)
    highest = jnp.max(scores, axis=3, keepdims=True)
    exponent = jnp.exp(scores - highest)
    reduced_totals = jnp.sum(exponent, axis=3, keepdims=True)
    log_total = highest + jnp.log(reduced_totals)
    attention = (exponent / reduced_totals).astype(jnp.bfloat16)
    mixed = jnp.einsum(
        "chfgs,cgshd->cfshd", attention, values_all, preferred_element_type=jnp.float32
    )
    return (log_total, mixed.astype(jnp.bfloat16))


def time_backward(grad_mixed, queries, keys_all, values_all, visible, log_total, scale):
    grad_out = grad_mixed.reshape(queries.shape)
    scores = time_scores(queries, keys_all, visible, scale)
    attention = jnp.exp(scores - log_total)
    grad_values = jnp.einsum(
        "chfgs,cfshd->cgshd",
        attention.astype(jnp.bfloat16),
        grad_out,
        preferred_element_type=jnp.float32,
    )
    grad_att = jnp.einsum(
        "cfshd,cgshd->chfgs", grad_out, values_all, preferred_element_type=jnp.float32
    )
    grad_scores = (
        attention * (grad_att - jnp.sum(attention * grad_att, axis=3, keepdims=True))
    ).astype(jnp.bfloat16)
    grad_queries = (
        jnp.einsum("chfgs,cgshd->cfshd", grad_scores, keys_all, preferred_element_type=jnp.float32)
        * scale
    )
    grad_keys = (
        jnp.einsum("chfgs,cfshd->cgshd", grad_scores, queries, preferred_element_type=jnp.float32)
        * scale
    )
    return (grad_queries, grad_keys, grad_values)


def shards(
    tokens,
    cotangent,
    ratio,
    priority,
    frame_order,
    mask_embed,
    gains,
    qkv_space,
    out_space,
    qkv_time,
    out_time,
    w_in,
    w_out,
):
    scale = 1.0 / math.sqrt(HEAD_DIM)
    clips_local = tokens.shape[0] // MICRO
    frames_local = tokens.shape[1]
    patches = tokens.shape[2]
    cols_local = tokens.shape[3]
    frames_all = frame_order.shape[1]
    hidden_width = qkv_space.shape[0]
    joined_local = qkv_space.shape[2]
    heads_local = joined_local // HEAD_DIM
    row_count = clips_local * frames_local * patches
    gain_broadcast = gains.astype(jnp.float32)
    embed_row = mask_embed.astype(jnp.float32)
    first_frame = lax.axis_index("tm") * frames_local
    shape_local = (clips_local, frames_local, patches, joined_local)
    shape_heads = (clips_local, frames_local, patches, heads_local, HEAD_DIM)
    shape_all = (clips_local, frames_all, patches, heads_local, HEAD_DIM)
    outputs = []
    input_grads = []
    weight_total = None
    small_total = None
    for batch_index in range(MICRO):
        lower = batch_index * clips_local
        upper = lower + clips_local
        source = tokens[lower:upper].reshape(row_count, cols_local).astype(jnp.float32)
        upstream = cotangent[lower:upper].reshape(row_count, cols_local).astype(jnp.float32)
        masked = (priority[lower:upper] < ratio[lower:upper][:, None, None]).reshape(row_count)
        order_rows = frame_order[lower:upper]
        residual_stream0 = jnp.where(masked[:, None], embed_row[None, :], source)
        normalized_rows0, standardized_rows0, inverse_deviation0 = norm_forward_pass(
            residual_stream0, gain_broadcast[0], hidden_width
        )
        joined0, total0, mixed0 = space_forward(
            normalized_rows0, qkv_space, clips_local * frames_local, patches, heads_local, scale
        )
        residual_stream1 = residual_stream0 + branch_out(mixed0, out_space)
        normalized_rows1, standardized_rows1, inverse_deviation1 = norm_forward_pass(
            residual_stream1, gain_broadcast[1], hidden_width
        )
        joined1 = jnp.einsum(
            "rd,dtk->trk", normalized_rows1, qkv_time, preferred_element_type=jnp.float32
        ).astype(jnp.bfloat16)
        queries_local = joined1[0].reshape(shape_local)
        keys_local = joined1[1].reshape(shape_local)
        values_local = joined1[2].reshape(shape_local)
        keys_all, values_all = (
            lax.all_gather(keys_local, "tm", axis=1, tiled=True),
            lax.all_gather(values_local, "tm", axis=1, tiled=True),
        )
        query_order = lax.dynamic_slice_in_dim(order_rows, first_frame, frames_local, axis=1)
        time_visible = (order_rows[:, None, :] <= query_order[:, :, None])[:, None, :, :, None]
        time_q = queries_local.reshape(shape_heads)
        time_k = keys_all.reshape(shape_all)
        time_v = values_all.reshape(shape_all)
        total1, mixed_frames = time_forward(time_q, time_k, time_v, time_visible, scale)
        mixed1 = mixed_frames.reshape(row_count, joined_local)
        residual_stream2 = residual_stream1 + branch_out(mixed1, out_time)
        normalized_rows2, standardized_rows2, inverse_deviation2 = norm_forward_pass(
            residual_stream2, gain_broadcast[2], hidden_width
        )
        projected = jnp.dot(normalized_rows2, w_in, preferred_element_type=jnp.float32)
        activated, gelu_pull = jax.vjp(gelu_tanh, projected)
        hidden = activated.astype(jnp.bfloat16)
        resid3 = residual_stream2 + branch_out(hidden, w_out)
        outputs.append(
            resid3.astype(jnp.bfloat16).reshape(clips_local, frames_local, patches, cols_local)
        )
        grad3 = jnp.where(masked[:, None], upstream, 0.0)
        grad_hidden, grad_w_out = branch_back(grad3, hidden, w_out)
        grad_inner = gelu_pull(grad_hidden)[0].astype(jnp.bfloat16)
        grad_w_in = jnp.einsum(
            "rd,rk->dk", normalized_rows2, grad_inner, preferred_element_type=jnp.float32
        )
        normalized_gradient2 = sum_features(
            jnp.einsum("rk,dk->rd", grad_inner, w_in, preferred_element_type=jnp.float32)
        )
        backward_third, gain_gradient2 = norm_reverse_pass(
            normalized_gradient2,
            standardized_rows2,
            inverse_deviation2,
            gain_broadcast[2],
            hidden_width,
        )
        grad2 = grad3 + backward_third
        grad_mixed1, grad_out_time = branch_back(grad2, mixed1, out_time)
        grad_mixed_low = grad_mixed1.astype(jnp.bfloat16).reshape(shape_local)
        grad_queries, grad_keys, grad_values = time_backward(
            grad_mixed_low, time_q, time_k, time_v, time_visible, total1, scale
        )
        key_part, value_part = (
            lax.psum_scatter(
                grad_keys.reshape(clips_local, frames_all, patches, joined_local).astype(
                    jnp.bfloat16
                ),
                "tm",
                scatter_dimension=1,
                tiled=True,
            ).astype(jnp.float32),
            lax.psum_scatter(
                grad_values.reshape(clips_local, frames_all, patches, joined_local).astype(
                    jnp.bfloat16
                ),
                "tm",
                scatter_dimension=1,
                tiled=True,
            ).astype(jnp.float32),
        )
        grad_joined1 = jnp.stack(
            [
                grad_queries.reshape(row_count, joined_local),
                key_part.reshape(row_count, joined_local),
                value_part.reshape(row_count, joined_local),
            ]
        ).astype(jnp.bfloat16)
        grad_qkv_time, normalized_gradient1 = qkv_back(normalized_rows1, grad_joined1, qkv_time)
        backward_second, gain_gradient1 = norm_reverse_pass(
            normalized_gradient1,
            standardized_rows1,
            inverse_deviation1,
            gain_broadcast[1],
            hidden_width,
        )
        grad1 = grad2 + backward_second
        grad_mixed0, grad_out_space = branch_back(grad1, mixed0, out_space)
        grad_joined0 = space_backward(
            grad_mixed0.astype(jnp.bfloat16),
            joined0,
            total0,
            clips_local * frames_local,
            patches,
            heads_local,
            scale,
        )
        grad_qkv_space, normalized_gradient0 = qkv_back(normalized_rows0, grad_joined0, qkv_space)
        backward_first, gain_gradient0 = norm_reverse_pass(
            normalized_gradient0,
            standardized_rows0,
            inverse_deviation0,
            gain_broadcast[0],
            hidden_width,
        )
        grad0 = grad1 + backward_first
        input_grads.append(
            jnp.where(masked[:, None], 0.0, grad0).reshape(
                clips_local, frames_local, patches, cols_local
            )
        )
        grad_embed = jnp.sum(jnp.where(masked[:, None], grad0, 0.0), axis=0)
        gain_grads = jnp.stack([gain_gradient0, gain_gradient1, gain_gradient2])
        local_grads = (
            grad_qkv_space,
            grad_out_space,
            grad_qkv_time,
            grad_out_time,
            grad_w_in,
            grad_w_out,
        )
        small_grads = (gain_grads, grad_embed)
        reduced, reduced_small = reduce_grads(local_grads, small_grads)
        if weight_total is None:
            weight_total = reduced
            small_total = reduced_small
        else:
            weight_total = tuple((total + grad for total, grad in zip(weight_total, reduced)))
            small_total = tuple((total + grad for total, grad in zip(small_total, reduced_small)))
    return (
        jnp.concatenate(outputs, axis=0),
        jnp.concatenate(input_grads, axis=0),
        small_total[1],
        small_total[0],
        weight_total[0],
        weight_total[1],
        weight_total[2],
        weight_total[3],
        weight_total[4],
        weight_total[5],
    )


AXES = ("tm", "x", "c", "mp")
F32 = jnp.float32
BF16 = jnp.bfloat16
BLK = 256
MESH = pl.DeviceIdType.MESH


def device_pairs(move):
    pairs = []
    for y in range(2):
        for x in range(2):
            for c in range(2):
                for z in range(4):
                    there = move(y, x, c, z)
                    pairs.append(tuple(((q[0] * 2 + q[1]) * 2 + q[2]) * 4 + q[3] for q in ((y, x, c, z), there)))
    return pairs


def hop_y(v):
    return lax.ppermute(v, AXES, device_pairs(lambda y, x, c, z: (1 - y, x, c, z)))


def hop_x(v):
    return lax.ppermute(v, AXES, device_pairs(lambda y, x, c, z: (y, 1 - x, c, z)))


def hop_c(v):
    return lax.ppermute(v, AXES, device_pairs(lambda y, x, c, z: (y, x, 1 - c, z)))


def hop_z(v, shift):
    return lax.ppermute(v, AXES, device_pairs(lambda y, x, c, z: (y, x, c, (z + shift) % 4)))


def spread_pairs(r):
    def move(y, x, c, z):
        k = z ^ r
        return (y, x, k & 1, 2 * c + (k >> 1))

    return device_pairs(move)


def dot_nn(a, b):
    return lax.dot_general(a, b, (((1,), (0,)), ((), ())), preferred_element_type=F32)


def dot_nt(a, b):
    return lax.dot_general(a, b, (((1,), (1,)), ((), ())), preferred_element_type=F32)


def dot_tn(a, b):
    return lax.dot_general(a, b, (((0,), (0,)), ((), ())), preferred_element_type=F32)


def attend_pair(q, k, v, bias, scale):
    mixed, totals = [], []
    for i in range(2):
        mine = slice(i * HEAD_DIM, (i + 1) * HEAD_DIM)
        scores = dot_nt(k[:, mine], q[:, mine]) * scale
        if bias is not None:
            scores = scores + bias
        highest = jnp.max(scores, axis=0, keepdims=True)
        exponent = jnp.exp(scores - highest)
        total = jnp.sum(exponent, axis=0, keepdims=True)
        totals.append(highest + jnp.log(total))
        mixed.append(dot_tn(v[:, mine], exponent.astype(BF16)) * (1.0 / total))
    return (jnp.concatenate(mixed, axis=0).T, totals)


def attend_pair_back(q, k, v, g, totals, bias, scale):
    grads = ([], [], [])
    for i in range(2):
        mine = slice(i * HEAD_DIM, (i + 1) * HEAD_DIM)
        scores = dot_nt(k[:, mine], q[:, mine]) * scale
        if bias is not None:
            scores = scores + bias
        p = jnp.exp(scores - totals[i])
        dp = dot_nt(v[:, mine], g[:, mine])
        ds = (p * (dp - jnp.sum(p * dp, axis=0, keepdims=True))).astype(BF16)
        grads[0].append(dot_tn(k[:, mine], ds) * scale)
        grads[1].append(dot_nn(ds, q[:, mine]) * scale)
        grads[2].append(dot_nn(p.astype(BF16), g[:, mine]))
    return (
        jnp.concatenate(grads[0], axis=0).T,
        jnp.concatenate(grads[1], axis=1),
        jnp.concatenate(grads[2], axis=1),
    )


PAIR = 2 * HEAD_DIM


def enter_kernel(
    scale,
    tok, vec, qkv_hbm, out_hbm, later, feed_hbm, first_hbm, masked,
    wq_out, wo_out, wt, wf, wi, joined_out, turned_out, std_out,
    mixed, total_out, inverse, resid, std_next, inverse_next, low_next, vec_out,
    rows_in, vec_in, wq, wo, normed, joined, turned, std, base, part, part_out, part_in,
    z_send, z_recv, y_send, y_recv, x_send, x_recv, p_send, p_recv, q_send, q_recv,
    t_send, t_recv, v_send, v_recv, u_send, u_recv, w_send, w_recv,
    f_send, f_recv, g_send, g_recv, n_send, n_recv, local, saved,
    i_send, i_recv, j_send, j_recv, k_send, k_recv,
):
    y, x, c, z = (lax.axis_index(name) for name in AXES)
    half = wo.shape[0] // 4
    wide = 3 * half
    span = wt.shape[1] // 4
    size = wf.shape[1] // 4
    own = rows_in.shape[0]
    near_y, near_x, pair = (1 - y, x, c, z), (y, 1 - x, c, z), (y, x, 1 - c, z)
    right_z, left_z = (y, x, c, (z + 1) % 4), (y, x, c, (z + 3) % 4)

    def at(i, length):
        return pl.ds(pl.multiple_of(i * length, length), length)

    def remote(src, dst, send, recv, peer):
        return pltpu.make_async_remote_copy(
            src_ref=src, dst_ref=dst, send_sem=send, recv_sem=recv, device_id=peer, device_id_type=MESH
        )

    def start(all_copies):
        for copy in all_copies:
            copy.start()

    def landed(all_copies):
        for copy in all_copies:
            copy.wait_recv()

    def sent(all_copies):
        for copy in all_copies:
            copy.wait_send()

    core = at(c, half)
    keep = [
        pltpu.make_async_copy(
            qkv_hbm.at[j, :, core], wq.at[:, pl.ds(pl.multiple_of(z * wide + j * half, half), half)], local.at[j]
        )
        for j in range(3)
    ] + [pltpu.make_async_copy(out_hbm.at[core], wo.at[at(z, half)], local.at[3])]
    keep_later = [
        pltpu.make_async_copy(later, wt.at[:, at(z, span)], local.at[4]),
        pltpu.make_async_copy(feed_hbm.at[at(c, 4 * size)], wf.at[z], local.at[5]),
        pltpu.make_async_copy(first_hbm.at[:, at(c, 4 * size)], wi.at[z], local.at[8]),
    ]
    start(keep + keep_later)

    barrier = pltpu.get_barrier_semaphore()
    for dc in range(2):
        for dz in range(4):
            if dc or dz:
                peer = (y, x, (c + dc) % 2, (z + dz) % 4)
                pl.semaphore_signal(barrier, inc=1, device_id=peer, device_id_type=MESH)
    for peer in (near_y, near_x):
        pl.semaphore_signal(barrier, inc=1, device_id=peer, device_id_type=MESH)
    pl.semaphore_wait(barrier, 9)

    def spot(dy, dx):
        return 2 * ((y + dy) % 2) + (x + dx) % 2

    def piece(dy, dx, r, split=False):
        s = (z + r) % 4
        rows = at(spot(dy, dx), BLK)
        first = pl.multiple_of(s * wide, half)
        out = wo.at[at(s, half), at(spot(dy, dx), BLK)]
        if split:
            last = pl.multiple_of(s * wide + 2 * half, half)
            return (wq.at[rows, pl.ds(first, 2 * half)], wq.at[rows, pl.ds(last, half)], out)
        return (wq.at[rows, pl.ds(first, wide)], out)

    def time_piece(dx, r):
        return wt.at[at((x + dx) % 2, 2 * BLK), at((z + r) % 4, span)]

    def feed_piece(dy, r):
        return wf.at[(z + r) % 4, at(spot(dy, 0), size)]

    def copies(parts, send, recv, peer):
        return [remote(ref, ref, send.at[i], recv.at[i], peer) for i, ref in enumerate(parts)]

    def leg(right, step):
        if right:
            return (0 if step == 0 else 4 - step), right_z, 3 - step
        return step, left_z, step + 1

    def z_copies(right, step):
        r, peer, lands = leg(right, step)
        return copies(piece(0, 0, r), z_send.at[int(right), step], z_recv.at[lands], peer)

    def time_z(right, step):
        r, peer, lands = leg(right, step)
        source = later.at[at(x, 2 * BLK)] if step == 0 else time_piece(0, r)
        return [remote(source, time_piece(0, r), u_send.at[int(right), step], u_recv.at[lands], peer)]

    def feed_z(right, step):
        r, peer, lands = leg(right, step)
        source = feed_hbm.at[at(4 * c + spot(0, 0), size)] if step == 0 else feed_piece(0, r)
        return [remote(source, feed_piece(0, r), f_send.at[int(right), step], f_recv.at[lands], peer)]

    def first_piece(dy, dx, r):
        return wi.at[(z + r) % 4, at(spot(dy, dx), BLK)]

    def first_z(right, step):
        r, peer, lands = leg(right, step)
        source = first_hbm.at[at(spot(0, 0), BLK), at(c, 4 * size)] if step == 0 else first_piece(0, 0, r)
        return [remote(source, first_piece(0, 0, r), i_send.at[int(right), step], i_recv.at[lands], peer)]

    def first_y(r, dy=0):
        return [remote(first_piece(dy, 0, r), first_piece(dy, 0, r), j_send.at[r], j_recv.at[r], near_y)]

    def first_x(r, dx=0):
        return [remote(first_piece(0, dx, r), first_piece(0, dx, r), k_send.at[r], k_recv.at[r], near_x)]

    def y_copies(r, dy=0):
        return copies(piece(dy, 0, r), y_send.at[r], y_recv.at[r], near_y)

    def x_copies(r, dx=0):
        return copies(piece(0, dx, r), x_send.at[r], x_recv.at[r], near_x)

    def corner_x(r, dx=0):
        return copies(piece(1, dx, r, split=True)[:1], p_send.at[r], p_recv.at[r], near_x)

    def corner_y(r, dy=0):
        return copies(piece(dy, 1, r, split=True)[1:], q_send.at[r], q_recv.at[r], near_y)

    def time_x(r, dx=0):
        return [remote(time_piece(dx, r), time_piece(dx, r), w_send.at[r], w_recv.at[r], near_x)]

    def feed_y(r, dy=0):
        return [remote(feed_piece(dy, r), feed_piece(dy, r), g_send.at[r], g_recv.at[r], near_y)]

    def token_copies(k):
        peer = (y, x, k % 2, 2 * c + k // 2)
        return [
            remote(tok.at[k], rows_in.at[:, at(z, BLK)], t_send.at[k], t_recv.at[z], peer),
            remote(vec, vec_in.at[:, at(z, BLK)], v_send.at[k], v_recv.at[z], peer),
        ]

    def token_local(k):
        return [
            pltpu.make_async_copy(tok.at[k], rows_in.at[:, at(z, BLK)], local.at[6]),
            pltpu.make_async_copy(vec, vec_in.at[:, at(z, BLK)], local.at[7]),
        ]

    def stays(k):
        return jnp.logical_and(2 * c + k // 2 == z, c == k % 2)

    def start_tokens(ks):
        for k in ks:
            pl.when(stays(k))(lambda k=k: start(token_local(k)))
            pl.when(jnp.logical_not(stays(k)))(lambda k=k: start(token_copies(k)))

    def each_side(j, act):
        pl.when(z >= j + 1)(lambda: act(3 - j, True))
        pl.when(z <= 2 - j)(lambda: act(j + 1, False))

    def begin(make):
        pl.when(z < 3)(lambda: start(make(True, 0)))
        pl.when(z > 0)(lambda: start(make(False, 0)))

    def onward(j, make, right):
        if j < 2:
            pl.when(z < 3 if right else z > 0)(lambda: start(make(right, j + 1)))

    def forward(j):
        def act(r, right):
            landed(copies(piece(0, 0, r), z_send.at[0, 0], z_recv.at[r], near_y))
            onward(j, z_copies, right)
            start(y_copies(r))
            start(x_copies(r))

        each_side(j, act)

    def corners(j):
        def act(r, right):
            landed(y_copies(r, 1))
            start(corner_x(r))
            landed(x_copies(r, 1))
            start(corner_y(r))

        each_side(j, act)

    def time_forward_step(j):
        def act(r, right):
            landed([remote(time_piece(0, r), time_piece(0, r), u_send.at[0, 0], u_recv.at[r], near_x)])
            onward(j, time_z, right)
            start(time_x(r))

        each_side(j, act)

    def feed_forward_step(j):
        def act(r, right):
            landed([remote(feed_piece(0, r), feed_piece(0, r), f_send.at[0, 0], f_recv.at[r], near_y)])
            onward(j, feed_z, right)
            start(feed_y(r))

        each_side(j, act)

    def first_forward_step(j):
        def act(r, right):
            landed([remote(first_piece(0, 0, r), first_piece(0, 0, r), i_send.at[0, 0], i_recv.at[r], near_y)])
            onward(j, first_z, right)
            start(first_y(r))
            start(first_x(r))

        each_side(j, act)

    for copy in keep:
        copy.wait()
    begin(z_copies)
    forward(0)
    start_tokens((0, 1))
    forward(1)
    start_tokens((2, 3))
    begin(time_z)
    corners(0)
    forward(2)
    corners(1)
    for k in range(4):
        def finish_local(k=k):
            for copy in token_local(k):
                copy.wait()

        pl.when(stays(k))(finish_local)
    for s in range(4):
        def arrived(s=s):
            landed([
                remote(tok.at[0], rows_in.at[:, at(s, BLK)], t_send.at[0], t_recv.at[s], near_y),
                remote(vec, vec_in.at[:, at(s, BLK)], v_send.at[0], v_recv.at[s], near_y),
            ])

        pl.when(jnp.logical_not(jnp.logical_and(z == s, z // 2 == c)))(arrived)

    step = own // 2
    slab = 128
    vec_out[...] = vec_in[...].astype(F32)

    def first_norm(i, carry):
        rows = at(i, step)
        value = jnp.where(masked[rows] > 0.0, vec_out[0:1], rows_in[rows].astype(F32))
        base[rows] = value
        standard, inv = norm_rows(value)
        std[rows] = standard
        inverse[rows] = inv
        normed[rows] = (standard * vec_out[1:2]).astype(BF16)
        return carry

    lax.fori_loop(0, 2, first_norm, 0)
    give_normed = remote(normed.at[pl.ds(0, own)], normed.at[pl.ds(own, own)], n_send.at[0], n_recv.at[0], pair)
    give_normed.start()
    corners(2)

    def turn(i, carry):
        turned[:, at(i, slab)] = normed[at(i, slab)].T
        return carry

    lax.fori_loop(0, own // slab, turn, 0)
    for r in (1, 2, 3):
        landed(corner_x(r, 1))
        landed(corner_y(r, 1))
    saves = [
        pltpu.make_async_copy(wq, wq_out, saved.at[0]),
        pltpu.make_async_copy(wo, wo_out, saved.at[1]),
        pltpu.make_async_copy(std, std_out, saved.at[2]),
    ]
    start(saves)
    time_forward_step(0)

    def attend(i, carry):
        rows = at(i, slab)
        for h in range(wo.shape[0] // PAIR):
            q, k, v = (joined[rows, (3 * h + j) * PAIR : (3 * h + j + 1) * PAIR] for j in range(3))
            out, totals = attend_pair(q, k, v, None, scale)
            mixed[rows, h * PAIR : (h + 1) * PAIR] = out.astype(BF16)
            for j in range(2):
                total_out[i, 2 * h + j : 2 * h + j + 1, :] = totals[j]
        return carry

    def project(t):
        rows = pl.ds(t * own, own)
        joined[rows] = dot_nn(normed[rows], wq[...]).astype(BF16)

    frames = own // slab
    project(0)
    time_forward_step(1)
    begin(first_z)
    lax.fori_loop(0, frames, attend, 0)
    part[...] = dot_nn(mixed[pl.ds(0, own)], wo[...])
    time_forward_step(2)
    give_normed.wait_recv()
    project(1)
    saves.append(pltpu.make_async_copy(joined, joined_out, saved.at[3]))
    saves[3].start()
    first_forward_step(0)
    lax.fori_loop(frames, 2 * frames, attend, 0)
    part_out[...] = dot_nn(mixed[pl.ds(own, own)], wo[...]).astype(BF16)
    give_part = remote(part_out, part_in, n_send.at[1], n_recv.at[1], pair)
    give_part.start()
    first_forward_step(1)
    begin(feed_z)
    lax.fori_loop(own // slab, 2 * own // slab, turn, 0)
    saves.append(pltpu.make_async_copy(turned, turned_out, saved.at[4]))
    saves[4].start()
    give_part.wait_recv()
    first_forward_step(2)

    def second_norm(i, carry):
        rows = at(i, step)
        value = base[rows] + part[rows] + part_in[rows].astype(F32)
        resid[rows] = value
        standard, inv = norm_rows(value)
        std_next[rows] = standard
        inverse_next[rows] = inv
        low_next[rows] = (standard * vec_out[2:3]).astype(BF16)
        return carry

    lax.fori_loop(0, 2, second_norm, 0)
    for j in range(3):
        feed_forward_step(j)

    for copy in keep_later + saves:
        copy.wait()
    give_normed.wait_send()
    give_part.wait_send()
    for r in (1, 2, 3):
        landed(time_x(r, 1))
        landed(feed_y(r, 1))
        landed(first_y(r, 1))
        landed(first_x(r, 1))
        for group in (y_copies(r), x_copies(r), corner_x(r), corner_y(r), time_x(r), feed_y(r), first_y(r), first_x(r)):
            sent(group)
    for step_z in range(3):
        for make in (z_copies, time_z, first_z, feed_z):
            pl.when(jnp.logical_and(z >= step_z, z < 3))(lambda step_z=step_z, make=make: sent(make(True, step_z)))
            pl.when(jnp.logical_and(z + step_z <= 3, z > 0))(lambda step_z=step_z, make=make: sent(make(False, step_z)))
    for k in range(4):
        pl.when(jnp.logical_not(stays(k)))(lambda k=k: sent(token_copies(k)))


def enter(tok, vec, qkv, out, later, feed_weight, first_weight, masked, scale):
    own, width, half = tok.shape[1], 4 * tok.shape[2], out.shape[0] // 2
    size = feed_weight.shape[0] // 2
    dma = pltpu.SemaphoreType.DMA
    anywhere = pl.BlockSpec(memory_space=pl.ANY)
    whole = pl.BlockSpec(memory_space=pltpu.VMEM)
    heads = 4 * half // HEAD_DIM

    def low(*shape):
        return pltpu.VMEM(shape, BF16)

    def high(*shape):
        return pltpu.VMEM(shape, F32)

    shapes = [
        ((width, 12 * half), BF16), ((4 * half, width), BF16), ((width, 4 * later.shape[1]), BF16),
        ((4, size, width), BF16), ((4, width, size), BF16), ((2 * own, 12 * half), BF16), ((width, 2 * own), BF16), ((own, width), F32),
        ((2 * own, 4 * half), BF16), ((2 * own // 128, heads, 128), F32), ((own, 1), F32), ((own, width), F32),
        ((own, width), F32), ((own, 1), F32), ((own, width), BF16), ((vec.shape[0], width), F32),
    ]
    return pl.pallas_call(
        functools.partial(enter_kernel, scale),
        in_specs=[anywhere] * 7 + [whole],
        out_specs=[anywhere] * 8 + [whole] * 8,
        out_shape=[jax.ShapeDtypeStruct(shape, kind) for shape, kind in shapes],
        scratch_shapes=[
            low(own, width), low(vec.shape[0], width), low(width, 12 * half), low(4 * half, width),
            low(2 * own, width), low(2 * own, 12 * half), low(width, 2 * own), high(own, width), high(own, width),
            high(own, width), low(own, width), low(own, width),
            dma((2, 3, 2)), dma((4, 2)), dma((4, 2)), dma((4, 2)), dma((4, 2)), dma((4, 2)),
            dma((4, 1)), dma((4, 1)), dma((4, 2)), dma((4, 2)),
            dma((4,)), dma((4,)), dma((4,)), dma((4,)), dma((2, 3)), dma((4,)), dma((4,)), dma((4,)),
            dma((2, 3)), dma((4,)), dma((4,)), dma((4,)), dma((2,)), dma((2,)), dma((9,)), dma((5,)),
            dma((2, 3)), dma((4,)), dma((4,)), dma((4,)), dma((4,)), dma((4,)),
        ],
        compiler_params=pltpu.CompilerParams(
            collective_id=0, has_side_effects=True, vmem_limit_bytes=56 * 1024 * 1024
        ),
        cost_estimate=pl.CostEstimate(flops=10**10, transcendentals=10**6, bytes_accessed=10**8),
        name="enter",
    )(tok, vec, qkv, out, later, feed_weight, first_weight, masked)


GROUP = 8
CHUNK = 32


def time_kernel(back, scale, heads, *refs):
    if back:
        (own_ref, rider_ref, joined_ref, total_ref, wide_ref, turned_ref, mixed_ref, wt_ref, bias_ref) = refs[:9]
        (delta_ref, grad_ref, reduced_ref, rider_out) = refs[9:13]
        (half_in, half_own, line_out, line_in, half_send, half_recv, half_local, line_send, line_recv) = refs[-13:-4]
        (out_ref, turned, grad_qkv, grad_out) = refs[-4:]
        refs = refs[13:-13]
    else:
        (own_ref, rider_ref, far_ref, in_ref, wt_ref, bias_ref) = refs[:6]
        (turned_ref, out_ref, mixed_ref, total_ref, delta_ref, rider_out, spread_out, in_out) = refs[6:14]
        turned = refs[-1]
        refs = refs[14:-1]
    (
        wq_ref, wo_ref, held, wide, narrow, kept, core_out, core_in, near_out, near_in,
        gy_send, gy_recv, gc_send, gc_recv, gd_send, gd_recv, sc_send, sc_recv, sy_send, sy_recv,
        r_send, r_recv, r_local, out_sem, wx_send, wx_recv,
    ) = refs
    y, x, c, z = (lax.axis_index(name) for name in AXES)
    near, pair, near_x = (1 - y, x, c, z), (y, x, 1 - c, z), (y, 1 - x, c, z)
    frames = held.shape[0] // 4
    chunks = held.shape[1] // CHUNK
    width = heads * HEAD_DIM
    groups = CHUNK // GROUP

    barrier = pltpu.get_barrier_semaphore()
    for dc in range(2):
        for dz in range(4):
            if dc or dz:
                pl.semaphore_signal(barrier, inc=1, device_id=(y, x, (c + dc) % 2, (z + dz) % 4), device_id_type=MESH)
    pl.semaphore_signal(barrier, inc=1, device_id=near, device_id_type=MESH)
    pl.semaphore_signal(barrier, inc=1, device_id=near_x, device_id_type=MESH)
    pl.semaphore_wait(barrier, 9)

    def remote(src, dst, send, recv, peer):
        return pltpu.make_async_remote_copy(
            src_ref=src, dst_ref=dst, send_sem=send, recv_sem=recv, device_id=peer, device_id_type=MESH
        )

    def patches(k):
        return pl.ds(pl.multiple_of(k * CHUNK, CHUNK), CHUNK)

    def block(b, k):
        return held.at[pl.ds(b * frames, frames), patches(k)]

    def gather_y(k):
        return remote(own_ref.at[:, patches(k)], block(1, k), gy_send.at[k], gy_recv.at[k], near)

    def gather_c(k):
        return remote(own_ref.at[:, patches(k)], block(2, k), gc_send.at[k], gc_recv.at[k], pair)

    def gather_d(k):
        return remote(block(1, k), block(3, k), gd_send.at[k], gd_recv.at[k], pair)

    def scatter_c(k):
        return remote(core_out.at[k], core_in.at[k], sc_send.at[k], sc_recv.at[k], pair)

    def scatter_y(k):
        return remote(near_out.at[k], near_in.at[k], sy_send.at[k], sy_recv.at[k], near)

    def save(k):
        there = (turned_ref.at[k], turned.at[k]) if back else (turned.at[k], turned_ref.at[k])
        return pltpu.make_async_copy(*there, out_sem.at[k])

    def columns(s):
        return pl.ds(pl.multiple_of(s * BLK, BLK), BLK)

    def stays(k):
        if back:
            return jnp.logical_and(z == k, z // 2 == c)
        return jnp.logical_and(2 * c + k // 2 == z, c == k % 2)

    def ride(k):
        if back:
            src, dst = rider_ref.at[:, columns(k)], rider_out.at[2 * (z % 2) + c]
            peer, slot = (y, x, z // 2, k), 2 * (z % 2) + c
        else:
            src, dst = rider_ref.at[k], rider_out.at[:, columns(z)]
            peer, slot = (y, x, k % 2, 2 * c + k // 2), z
        return src, dst, peer, slot

    def ride_remote(k):
        src, dst, peer, slot = ride(k)
        return remote(src, dst, r_send.at[k], r_recv.at[slot], peer)

    def ride_local(k):
        src, dst, _, _ = ride(k)
        return pltpu.make_async_copy(src, dst, r_local.at[0])

    def ride_landed(k):
        if back:
            src, dst = rider_ref.at[:, columns(k)], rider_out.at[k]
        else:
            src, dst = rider_ref.at[k], rider_out.at[:, columns(k)]
        return remote(src, dst, r_send.at[k], r_recv.at[k], near)

    def from_self(k):
        if back:
            return jnp.logical_and(2 * c + k // 2 == z, c == k % 2)
        return jnp.logical_and(z == k, z // 2 == c)

    def spread_x(i, dx=0):
        r, yb = i // 2 + 1, i % 2
        size = far_ref.shape[1] // 4
        at = pl.multiple_of(size * (2 * yb + (x + dx) % 2), size)
        src = far_ref.at[(z + r) % 4, pl.ds(at, size)]
        return remote(src, spread_out.at[(z + r) % 4, pl.ds(at, size)], wx_send.at[i], wx_recv.at[i], near_x)

    gather_y(0).start()
    for k in range(chunks):
        if k > 0:
            gather_y(k).start()
        gather_c(k).start()
    def spread_in(r, dx=0):
        at = pl.multiple_of(BLK * (2 * (1 - y) + (x + dx) % 2), BLK)
        there = in_out.at[(z + r) % 4, pl.ds(at, BLK)]
        return remote(in_ref.at[(z + r) % 4, pl.ds(at, BLK)], there, wx_send.at[5 + r], wx_recv.at[5 + r], near_x)

    def half_away(s):
        return remote(wide_ref.at[1 - x, s], half_in.at[s], half_send.at[s], half_recv.at[s], near_x)

    def half_here(s):
        return pltpu.make_async_copy(wide_ref.at[x, s], half_own.at[s], half_local.at[s])

    def line_away(r):
        return remote(line_out.at[r], line_in.at[r], line_send.at[r], line_recv.at[r], (y, x, c, (z + r) % 4))

    def halve():
        for s in range(4):
            half_away(s).wait_recv()
            half_here(s).wait()
        for r in range(4):
            s = (z + r) % 4
            whole = half_own[s].astype(F32) + half_in[s].astype(F32)
            if r == 0:
                reduced_ref[...] = whole
            else:
                line_out[r] = whole.astype(BF16)
                line_away(r).start()

    if back:
        for s in range(4):
            half_away(s).start()
            half_here(s).start()
    else:
        for r in (1, 2, 3):
            spread_in(r).start()
        for i in range(6):
            spread_x(i).start()
    for k in range(4):
        pl.when(stays(k))(lambda k=k: ride_local(k).start())
        pl.when(jnp.logical_not(stays(k)))(lambda k=k: ride_remote(k).start())
    held[:frames] = own_ref[...]
    if back:
        for k in range(chunks):
            save(k).start()

    def assemble(i, carry):
        rows = pl.ds(pl.multiple_of(i * BLK, BLK), BLK)
        for s in range(0, heads, 2):
            for part in range(4):
                both = [
                    wt_ref[rows, (s + j) * 4 * HEAD_DIM + part * HEAD_DIM : (s + j) * 4 * HEAD_DIM + (part + 1) * HEAD_DIM]
                    for j in range(2)
                ]
                both = jnp.concatenate(both, axis=1)
                if part < 3:
                    wq_ref[rows, part * width + s * HEAD_DIM : part * width + s * HEAD_DIM + PAIR] = both
                else:
                    wo_ref[rows, s * HEAD_DIM : s * HEAD_DIM + PAIR] = both
        return carry

    lax.fori_loop(0, wt_ref.shape[0] // BLK, assemble, 0)

    def finish(k):
        scatter_c(k).wait_recv()
        both = kept[:, patches(k)] + core_in[k].astype(F32)
        near_out[k] = both[frames:].astype(BF16)
        delta_ref[:, patches(k)] = both[:frames]
        scatter_y(k).start()

    def pass_on(k):
        gather_y(k).wait_recv()
        gather_d(k).start()

    def one_group(i, rows):
        at = pl.ds(pl.multiple_of(i * GROUP, GROUP), GROUP)
        count = 4 * frames * GROUP
        bias = bias_ref[...]
        for lo in range(0, width, PAIR):
            q, k, v = (
                wide[:, at, part * width + lo : part * width + lo + PAIR].reshape(count, PAIR).astype(BF16)
                for part in range(3)
            )
            h = lo // HEAD_DIM
            if back:
                g = narrow[:, at, lo : lo + PAIR].reshape(count, PAIR).astype(BF16)
                totals = [total_ref[rows * groups + i, h + j : h + j + 1, :] for j in range(2)]
                grads = attend_pair_back(q, k, v, g, totals, bias, scale)
                for part in range(3):
                    wide[:, at, part * width + lo : part * width + lo + PAIR] = grads[part].reshape(
                        4 * frames, GROUP, PAIR
                    )
            else:
                mixed, totals = attend_pair(q, k, v, bias, scale)
                narrow[:, at, lo : lo + PAIR] = mixed.reshape(4 * frames, GROUP, PAIR)
                for j in range(2):
                    total_ref[rows * groups + i, h + j : h + j + 1, :] = totals[j]

    def one_chunk(k, carry):
        pl.when(k + 1 < chunks)(lambda: pass_on(k + 1))
        gather_c(k).wait_recv()
        gather_d(k).wait_recv()
        count = 4 * frames * CHUNK
        lhs = held[:, patches(k)].reshape(count, held.shape[2])
        if back:
            wide[...] = joined_ref[:, patches(k)].astype(F32)
            narrow[...] = dot_nn(lhs, wo_ref[...]).astype(BF16).astype(F32).reshape(narrow.shape)
        else:
            joined = dot_nn(lhs, wq_ref[...]).astype(BF16)
            out_ref[:, patches(k)] = joined.reshape(wide.shape)
            wide[...] = joined.astype(F32).reshape(wide.shape)
        lax.fori_loop(0, groups, lambda i, carry: (one_group(i, k), carry)[1], 0)
        if back:
            grads = wide[...].astype(BF16)
            out_ref[:, patches(k)] = grads
            partial = dot_nt(grads.reshape(count, 3 * width), wq_ref[...])
        else:
            mixed = narrow[...].astype(BF16)
            mixed_ref[:, patches(k)] = mixed
            partial = dot_nt(mixed.reshape(count, width), wo_ref[...])
        partial = partial.reshape(4 * frames, CHUNK, held.shape[2])
        kept[:, patches(k)] = partial[: 2 * frames]
        core_out[k] = partial[2 * frames :].astype(BF16)
        scatter_c(k).start()
        pl.when(k > 0)(lambda: finish(k - 1))
        if not back:
            for b in range(4):
                slab = held[b * frames : (b + 1) * frames, patches(k)].reshape(frames * CHUNK, held.shape[2])
                turned[k, :, b * frames * CHUNK : (b + 1) * frames * CHUNK] = slab.T
            save(k).start()
        if back:
            pl.when(k == 1)(halve)
        return carry

    pass_on(0)
    lax.fori_loop(0, chunks, one_chunk, 0)
    finish(chunks - 1)

    def weigh(k, carry):
        count = 4 * frames * CHUNK
        save(k).wait()
        grad_qkv[...] = grad_qkv[...] + dot_nn(turned[k], out_ref[:, patches(k)].reshape(count, 3 * width))
        grad_out[...] = grad_out[...] + dot_tn(
            mixed_ref[:, patches(k)].reshape(count, width), held[:, patches(k)].reshape(count, held.shape[2])
        )
        return carry

    def arrange(i, carry):
        rows = pl.ds(pl.multiple_of(i * BLK, BLK), BLK)
        last = grad_out[:, rows].T
        for s in range(heads):
            mine = slice(s * HEAD_DIM, (s + 1) * HEAD_DIM)
            parts = [grad_qkv[rows, j * width : (j + 1) * width][:, mine] for j in range(3)] + [last[:, mine]]
            grad_ref[rows, 2 * s * PAIR : (2 * s + 1) * PAIR] = jnp.concatenate(parts[:2], axis=1).astype(BF16)
            grad_ref[rows, (2 * s + 1) * PAIR : (2 * s + 2) * PAIR] = jnp.concatenate(parts[2:], axis=1).astype(BF16)
        return carry

    if back:
        grad_qkv[...] = jnp.zeros_like(grad_qkv)
        grad_out[...] = jnp.zeros_like(grad_out)
        lax.fori_loop(0, chunks, weigh, 0)
        lax.fori_loop(0, grad_ref.shape[0] // BLK, arrange, 0)
    for k in range(chunks):
        scatter_y(k).wait_recv()
        delta_ref[:, patches(k)] = delta_ref[:, patches(k)] + near_in[k].astype(F32)
    if back:
        for r in (1, 2, 3):
            line_away(r).wait_recv()
            reduced_ref[...] = reduced_ref[...] + line_in[r].astype(F32)
        for r in (1, 2, 3):
            line_away(r).wait_send()
        for s in range(4):
            half_away(s).wait_send()
    for k in range(chunks):
        for copy in (gather_y(k), gather_c(k), gather_d(k), scatter_c(k), scatter_y(k)):
            copy.wait_send()
        if not back:
            save(k).wait()
    if not back:
        for i in range(6):
            spread_x(i, 1).wait_recv()
            spread_x(i).wait_send()
        for r in (1, 2, 3):
            spread_in(r, 1).wait_recv()
            spread_in(r).wait_send()
    for k in range(4):
        pl.when(stays(k))(lambda k=k: ride_local(k).wait())
        pl.when(jnp.logical_not(stays(k)))(lambda k=k: ride_remote(k).wait_send())
        pl.when(jnp.logical_not(from_self(k)))(lambda k=k: ride_landed(k).wait_recv())


def time_call(back, own, rider, saved, weights, bias, scale):
    frames, patches, features = own.shape
    width = weights.shape[1] // 4
    heads = width // HEAD_DIM
    chunks = patches // CHUNK
    rows = 4 * frames * GROUP
    dma = pltpu.SemaphoreType.DMA
    anywhere = pl.BlockSpec(memory_space=pl.ANY)
    whole = pl.BlockSpec(memory_space=pltpu.VMEM)
    turned = (chunks, features, 4 * frames * CHUNK)
    if back:
        out_shape = []
    else:
        out_shape = [
            jax.ShapeDtypeStruct(turned, BF16),
            jax.ShapeDtypeStruct((4 * frames, patches, 3 * width), BF16),
            jax.ShapeDtypeStruct((4 * frames, patches, width), BF16),
            jax.ShapeDtypeStruct((patches // GROUP, heads, rows), F32),
        ]
    rider_shape = (4, frames * patches, BLK) if back else (frames * patches, features)
    out_shape += [
        jax.ShapeDtypeStruct((frames, patches, features), F32),
        jax.ShapeDtypeStruct(rider_shape, BF16),
    ]
    held = 2
    half = saved[2].shape[1:] if back else None
    if back:
        out_shape.insert(-1, jax.ShapeDtypeStruct((features, features), BF16))
        out_shape.insert(-1, jax.ShapeDtypeStruct(half[1:], F32))
    else:
        out_shape += [jax.ShapeDtypeStruct(w.shape, BF16) for w in saved]
        held = 4
    return pl.pallas_call(
        functools.partial(time_kernel, back, scale, heads),
        in_specs=[whole, anywhere] + ([whole, whole, anywhere, anywhere, whole] if back else [anywhere] * 2) + [whole] * 2,
        out_specs=([] if back else [anywhere]) + [whole] * (len(out_shape) - held + back) + [anywhere] * (held - 1),
        out_shape=out_shape,
        scratch_shapes=[
            pltpu.VMEM((features, 3 * width), BF16),
            pltpu.VMEM((features, width), BF16),
            pltpu.VMEM((4 * frames, patches, features), BF16),
            pltpu.VMEM((4 * frames, CHUNK, 3 * width), F32),
            pltpu.VMEM((4 * frames, CHUNK, width), F32),
            pltpu.VMEM((2 * frames, patches, features), F32),
            pltpu.VMEM((chunks, 2 * frames, CHUNK, features), BF16),
            pltpu.VMEM((chunks, 2 * frames, CHUNK, features), BF16),
            pltpu.VMEM((chunks, frames, CHUNK, features), BF16),
            pltpu.VMEM((chunks, frames, CHUNK, features), BF16),
        ]
        + [dma((chunks,))] * 10
        + [dma((4,)), dma((4,)), dma((1,)), dma((chunks,))]
        + [dma((9,))] * 2
        + ([pltpu.VMEM(half, BF16)] * 4 + [dma((4,))] * 5 if back else [])
        + ([pltpu.VMEM((4 * frames, patches, 3 * width), BF16)] if back else [])
        + [pltpu.VMEM(turned, BF16)]
        + ([pltpu.VMEM((features, 3 * width), F32), pltpu.VMEM((width, features), F32)] if back else []),
        compiler_params=pltpu.CompilerParams(
            collective_id=2 if back else 1, has_side_effects=True, vmem_limit_bytes=60 * 1024 * 1024
        ),
        cost_estimate=pl.CostEstimate(flops=10**10, transcendentals=10**6, bytes_accessed=10**8),
        name="time_back" if back else "time_forward",
    )(own, rider, *saved, weights, bias)


def feed_kernel(
    resid, delta, upstream, masked, gain, w_in_hbm, w_in_far_hbm, w_out_hbm, w_far_hbm,
    half_in_hbm, half_out_hbm, grad_out, low_out, rows_out, gain_out,
    w_in, w_out, standard, inverse, normed, grads, normed_t, grads_t, hidden, pulled, g_in, g_out, back, ahead,
    back_out, back_in, ahead_out, ahead_in, from_x, from_y,
    w_sem, g_sem, n_send, n_recv, b_send, b_recv, hx_send, hx_recv, hy_send, hy_recv,
):
    y, x, c, z = (lax.axis_index(name) for name in AXES)
    pair, near_y, near_x = (y, x, 1 - c, z), (1 - y, x, c, z), (y, 1 - x, c, z)
    own = resid.shape[0]
    step = own // 2
    slab = 128

    def fetch(s, far):
        size = w_out.shape[1] // 4
        copies = []
        for i in range(4):
            rows = pl.ds(pl.multiple_of(BLK * (2 * ((y + i // 2) % 2) + (x + i % 2) % 2), BLK), BLK)
            source = w_in_far_hbm if far and i == 3 else w_in_hbm
            copies.append(pltpu.make_async_copy(source.at[s, rows], w_in.at[s, rows], w_sem.at[5 + i, s]))
        for i in range(4):
            rows = pl.ds(pl.multiple_of(size * (2 * (i // 2) + (x + i % 2) % 2), size), size)
            source = w_far_hbm if far and i % 2 else w_out_hbm
            copies.append(pltpu.make_async_copy(source.at[s, rows], w_out.at[s, rows], w_sem.at[i, s]))
        return copies

    def fetch_now(s, far):
        for copy in fetch(s, far):
            copy.start()

    for s in range(4):
        pl.when(z == s)(lambda s=s: fetch_now(s, False))
        pl.when(z != s)(lambda s=s: fetch_now(s, True))
    barrier = pltpu.get_barrier_semaphore()
    for peer in (pair, near_y, near_x):
        pl.semaphore_signal(barrier, inc=1, device_id=peer, device_id_type=MESH)

    def remote(src, dst, send, recv, peer=pair):
        return pltpu.make_async_remote_copy(
            src_ref=src, dst_ref=dst, send_sem=send, recv_sem=recv, device_id=peer, device_id_type=MESH
        )

    def block(yb, xb):
        return pl.ds(pl.multiple_of(BLK * (2 * yb + xb), BLK), BLK)

    def away_x(s, i):
        return remote(g_out.at[s, block(i, 1 - x)], from_x.at[i, s], hx_send.at[i, s], hx_recv.at[i, s], near_x)

    def away_y(s, i):
        return remote(g_in.at[s, block(1 - y, i)], from_y.at[i, s], hy_send.at[i, s], hy_recv.at[i, s], near_y)

    def keep(s, i):
        return (
            pltpu.make_async_copy(g_out.at[s, block(i, x)], half_out_hbm.at[i, s], g_sem.at[0, i, s]),
            pltpu.make_async_copy(g_in.at[s, block(y, i)], half_in_hbm.at[i, s], g_sem.at[1, i, s]),
        )

    def combine(s):
        for i in range(2):
            away_x(s, i).wait_recv()
            g_out[s, block(i, x)] = (g_out[s, block(i, x)].astype(F32) + from_x[i, s].astype(F32)).astype(BF16)
            away_y(s, i).wait_recv()
            g_in[s, block(y, i)] = (g_in[s, block(y, i)].astype(F32) + from_y[i, s].astype(F32)).astype(BF16)
            for copy in keep(s, i):
                copy.start()

    def at(i, size):
        return pl.ds(pl.multiple_of(i * size, size), size)

    def prepare(i, carry):
        rows = at(i, step)
        grads[rows] = jnp.where(masked[rows] > 0.0, upstream[rows].astype(F32), 0.0).astype(BF16)
        std, inv = norm_rows(resid[rows] + delta[rows])
        standard[rows] = std
        inverse[rows] = inv
        normed[rows] = (std * gain[...]).astype(BF16)
        return carry

    lax.fori_loop(0, 2, prepare, 0)
    pl.semaphore_wait(barrier, 3)
    mine, theirs = pl.ds(0, own), pl.ds(own, own)
    give_grads = remote(grads.at[mine], grads.at[theirs], n_send.at[0], n_recv.at[0])
    give_normed = remote(normed.at[mine], normed.at[theirs], n_send.at[1], n_recv.at[1])
    give_normed.start()
    give_grads.start()

    def turn(i, carry):
        rows = at(i, slab)
        normed_t[:, rows] = normed[rows].T
        grads_t[:, rows] = grads[rows].T
        return carry

    lax.fori_loop(0, own // slab, turn, 0)
    back[...] = jnp.zeros_like(back)
    ahead[...] = jnp.zeros_like(ahead)
    rate = math.sqrt(2.0 / math.pi)

    def rows_step(s, rows):
        inner = dot_nn(normed[rows], w_in[s])
        square = inner * inner
        bend = jnp.tanh(rate * inner * (1.0 + 0.044715 * square))
        hidden[rows] = (0.5 * inner * (1.0 + bend)).astype(BF16)
        slope = 0.5 * (1.0 + bend) + 0.5 * inner * (1.0 - bend * bend) * (rate * (1.0 + 3.0 * 0.044715 * square))
        pulled[rows] = (dot_nt(grads[rows], w_out[s]) * slope).astype(BF16)
        ahead[rows] = ahead[rows] + dot_nn(hidden[rows], w_out[s])
        back[rows] = back[rows] + dot_nt(pulled[rows], w_in[s])

    def meet():
        give_normed.wait_recv()
        give_grads.wait_recv()
        lax.fori_loop(own // slab, 2 * own // slab, turn, 0)

    def one_piece(s, carry):
        for copy in fetch(s, False):
            copy.wait()

        def one_half(t, carry):
            pl.when(jnp.logical_and(s == 0, t == 1))(meet)
            rows_step(s, at(t, own))
            return carry

        lax.fori_loop(0, 2, one_half, 0)
        g_out[s] = dot_nn(grads_t[...], hidden[...]).astype(BF16)
        g_in[s] = dot_nn(normed_t[...], pulled[...]).astype(BF16)
        for i in range(2):
            away_x(s, i).start()
            away_y(s, i).start()
        return carry

    lax.fori_loop(0, 4, one_piece, 0)
    back_out[...] = back[theirs].astype(BF16)
    give_back = remote(back_out, back_in, b_send.at[0], b_recv.at[0])
    give_back.start()
    ahead_out[...] = ahead[theirs].astype(BF16)
    give_ahead = remote(ahead_out, ahead_in, b_send.at[1], b_recv.at[1])
    give_ahead.start()
    give_back.wait_recv()

    def finish(i, total):
        rows = at(i, step)
        grad = back[rows] + back_in[rows].astype(F32)
        std = standard[rows]
        inner = grad * gain[...]
        mean = jnp.mean(inner, axis=-1, keepdims=True)
        along = jnp.mean(inner * std, axis=-1, keepdims=True)
        full = grads[rows].astype(F32) + (inner - mean - std * along) * inverse[rows]
        grad_out[rows] = full
        low_out[rows] = full.astype(BF16)
        return total + jnp.sum(grad * std, axis=0, keepdims=True)

    gain_out[...] = lax.fori_loop(0, 2, finish, jnp.zeros((1, resid.shape[1]), F32))
    give_ahead.wait_recv()

    def emit(i, carry):
        rows = at(i, step)
        rows_out[rows] = (resid[rows] + delta[rows] + ahead[rows] + ahead_in[rows].astype(F32)).astype(BF16)
        return carry

    lax.fori_loop(0, 2, emit, 0)
    lax.fori_loop(0, 4, lambda s, carry: (combine(s), carry)[1], 0)
    for copy in (give_normed, give_grads, give_back, give_ahead):
        copy.wait_send()
    for s in range(4):
        for i in range(2):
            away_x(s, i).wait_send()
            away_y(s, i).wait_send()
            for copy in keep(s, i):
                copy.wait()


def feed(resid, delta, upstream, masked, gain, w_in, w_in_far, w_out, w_far):
    own, features = resid.shape
    units = w_in.shape[2]
    dma = pltpu.SemaphoreType.DMA
    anywhere = pl.BlockSpec(memory_space=pl.ANY)
    whole = pl.BlockSpec(memory_space=pltpu.VMEM)

    def low(*shape):
        return pltpu.VMEM(shape, BF16)

    def high(*shape):
        return pltpu.VMEM(shape, F32)

    return pl.pallas_call(
        feed_kernel,
        in_specs=[whole] * 5 + [anywhere] * 4,
        out_specs=[anywhere] * 2 + [whole] * 4,
        out_shape=[
            jax.ShapeDtypeStruct((2, 4, BLK, units), BF16),
            jax.ShapeDtypeStruct((2, 4, BLK, units), BF16),
            jax.ShapeDtypeStruct((own, features), F32),
            jax.ShapeDtypeStruct((own, features), BF16),
            jax.ShapeDtypeStruct((own, features), BF16),
            jax.ShapeDtypeStruct((1, features), F32),
        ],
        scratch_shapes=[
            low(4, features, units), low(4, units, features), high(own, features), high(own, 1),
            low(2 * own, features), low(2 * own, features), low(features, 2 * own), low(features, 2 * own),
            low(2 * own, units), low(2 * own, units), low(4, features, units), low(4, features, units),
            high(2 * own, features), high(2 * own, features),
            low(own, features), low(own, features), low(own, features), low(own, features),
            low(2, 4, BLK, units), low(2, 4, BLK, units),
            dma((9, 4)), dma((2, 2, 4)), dma((2,)), dma((2,)), dma((2,)), dma((2,)),
            dma((2, 4)), dma((2, 4)), dma((2, 4)), dma((2, 4)),
        ],
        compiler_params=pltpu.CompilerParams(
            collective_id=4, has_side_effects=True, vmem_limit_bytes=60 * 1024 * 1024
        ),
        cost_estimate=pl.CostEstimate(flops=26 * 10**9, transcendentals=2 * 10**6, bytes_accessed=10**8),
        name="feed",
    )(resid, delta, upstream, masked, gain, w_in, w_in_far, w_out, w_far)


def leave_kernel(
    scale,
    part_hbm, next_hbm, grad_hbm, out_hbm, joined_hbm, mixed_hbm, lhs_hbm, weight_hbm, std_hbm, time_hbm, feed_hbm, feed_in_hbm,
    totals, inverse_next, inverse, masked, gain_next, gain, small_in,
    space_qkv, space_out, feed_in_out, feed_out_out, time_qkv, time_out, rows_out, small_out,
    rows_in,
    part, std, base, w_out, dj, mixed, lhs, weight, low_grads, turned, dmixed, go,
    t_own, t_in, tz_out, tz_in, t_total, ty_out, ty_in, tc_out, tc_in,
    f_own, f_in, fz_out, fz_in, f_total, f_other, fc_out, fc_in,
    grads, a1_out, a1_in, b1_out, b1_in, a2_out, a2_in, b2_out, b2_in, z_out, z_in,
    half_out, half_in, ready, core_out, core_in, sums, sum_out, sum_in, share_in,
    a1_send, a1_recv, b1_send, b1_recv, a2_send, a2_recv, b2_send, b2_recv, z_send, z_recv,
    h_send, h_recv, r_send, r_recv, c_send, c_recv, s_send, s_recv, p_send, p_recv, local,
    g_send, g_recv, tx_send, tx_recv, tz_send, tz_recv, ty_send, ty_recv, fy_send, fy_recv, fz_send, fz_recv, t_local, f_local, fetched,
):
    y, x, c, z = (lax.axis_index(name) for name in AXES)
    near_y, near_x, pair = (1 - y, x, c, z), (y, 1 - x, c, z), (y, x, 1 - c, z)
    own = std.shape[0]
    third = go.shape[1] // 4
    wide = 3 * third
    two = 2 * third
    slab = 128

    fetches = [
        pltpu.make_async_copy(src, dst, fetched.at[i])
        for i, (src, dst) in enumerate((
            (part_hbm, part), (next_hbm, std), (grad_hbm, base), (out_hbm, w_out), (joined_hbm, dj), (mixed_hbm, mixed),
            (lhs_hbm, lhs), (weight_hbm, weight), (feed_in_hbm, f_other),
        ))
    ]
    for copy in fetches:
        copy.start()
    fetch_std = pltpu.make_async_copy(std_hbm, std, fetched.at[9])

    barrier = pltpu.get_barrier_semaphore()
    for dc in range(2):
        for dz in range(4):
            if dc or dz:
                pl.semaphore_signal(barrier, inc=1, device_id=(y, x, (c + dc) % 2, (z + dz) % 4), device_id_type=MESH)
    for peer in (near_y, near_x):
        pl.semaphore_signal(barrier, inc=1, device_id=peer, device_id_type=MESH)
    pl.semaphore_wait(barrier, 9)

    def remote(src, dst, send, recv, peer):
        return pltpu.make_async_remote_copy(
            src_ref=src, dst_ref=dst, send_sem=send, recv_sem=recv, device_id=peer, device_id_type=MESH
        )

    def at(i, length):
        return pl.ds(pl.multiple_of(i * length, length), length)

    def along(r):
        return (y, x, c, (z + r) % 4)

    def time_x(yb):
        return remote(time_hbm.at[at(2 * yb + 1 - x, BLK)], t_in.at[yb], tx_send.at[yb], tx_recv.at[yb], near_x)

    def time_keep(yb):
        return pltpu.make_async_copy(time_hbm.at[at(2 * yb + x, BLK)], t_own.at[yb], t_local.at[yb])

    def time_z(r):
        return remote(tz_out.at[r], tz_in.at[r], tz_send.at[r], tz_recv.at[r], along(r))

    def feed_y(r):
        s = (z + r) % 4
        return remote(feed_hbm.at[1 - y, s], f_in.at[r], fy_send.at[r], fy_recv.at[r], near_y)

    def feed_keep(r):
        return pltpu.make_async_copy(feed_hbm.at[y, (z + r) % 4], f_own.at[r], f_local.at[r])

    def feed_z(r):
        return remote(fz_out.at[r], fz_in.at[r], fz_send.at[r], fz_recv.at[r], along(r))

    for r in (1, 2, 3, 0):
        feed_y(r).start()
        feed_keep(r).start()
    for yb in range(2):
        time_x(yb).start()
        time_keep(yb).start()

    def feed_step(r):
        feed_y(r).wait_recv()
        feed_keep(r).wait()
        total = f_own[r].astype(F32) + f_in[r].astype(F32)
        if r == 0:
            f_total[...] = total
        else:
            fz_out[r] = total.astype(BF16)
            feed_z(r).start()

    def time_step():
        for yb in range(2):
            time_x(yb).wait_recv()
            time_keep(yb).wait()
        for r in (1, 2, 3, 0):
            piece_at = at((z + r) % 4, BLK)
            for yb in range(2):
                total = t_own[yb, :, piece_at].astype(F32) + t_in[yb, :, piece_at].astype(F32)
                if r == 0:
                    t_total[yb] = total
                else:
                    tz_out[r, yb] = total.astype(BF16)
            if r:
                time_z(r).start()

    step = own // 2
    for copy in fetches[:3]:
        copy.wait()

    def norm_back(grad, standard, weights, inv):
        inner = grad * weights
        mean = jnp.mean(inner, axis=-1, keepdims=True)
        slope = jnp.mean(inner * standard, axis=-1, keepdims=True)
        return (inner - mean - standard * slope) * inv

    def after_time(i, total):
        rows = at(i, step)
        grad, standard = part[rows], std[rows]
        full = base[rows] + norm_back(grad, standard, gain_next[...], inverse_next[rows])
        base[rows] = full
        low_grads[rows] = full.astype(BF16)
        return total + jnp.sum(grad * standard, axis=0, keepdims=True)

    zero = jnp.zeros((1, std.shape[1]), F32)
    next_grad = lax.fori_loop(0, 2, after_time, zero)
    give = remote(low_grads.at[pl.ds(0, own)], low_grads.at[pl.ds(own, own)], g_send.at[0], g_recv.at[0], pair)
    give.start()
    fetch_std.start()
    for copy in fetches[3:6]:
        copy.wait()

    def attend(i, carry):
        rows = at(i, slab)
        for h in range(mixed.shape[1] // PAIR):
            places = [pl.ds((3 * h + j) * PAIR, PAIR) for j in range(3)]
            q, k, v = (dj[rows, place] for place in places)
            lines = [totals[i, 2 * h + j : 2 * h + j + 1, :] for j in range(2)]
            found = attend_pair_back(q, k, v, dmixed[rows, h * PAIR : (h + 1) * PAIR], lines, None, scale)
            for place, value in zip(places, found):
                dj[rows, place] = value.astype(BF16)
        return carry

    def turn(i, carry):
        turned[:, at(i, slab)] = low_grads[at(i, slab)].T
        return carry

    def attend_half(t, *between):
        rows = pl.ds(t * own, own)
        first, count = t * own // slab, own // slab
        dmixed[rows] = dot_nt(low_grads[rows], w_out[...]).astype(BF16)
        between[0]()
        lax.fori_loop(first, first + count // 2, attend, 0)
        between[1]()
        lax.fori_loop(first + count // 2, first + count, attend, 0)
        between[2]()
        lax.fori_loop(first, first + count, turn, 0)

    def nothing():
        pass

    attend_half(0, lambda: feed_step(1), lambda: feed_step(2), lambda: feed_step(3))
    give.wait_recv()
    attend_half(1, nothing, time_step, lambda: feed_step(0))
    for copy in fetches[6:]:
        copy.wait()
    go[...] = dot_nn(turned[...], mixed[...]).astype(BF16)

    def block(yb, xb):
        return pl.ds(pl.multiple_of(BLK * (2 * yb + xb), BLK), BLK)

    def a1(i):
        return remote(a1_out.at[i], a1_in.at[i], a1_send.at[i], a1_recv.at[i], near_x)

    def b1(i):
        return remote(b1_out.at[i], b1_in.at[i], b1_send.at[i], b1_recv.at[i], near_y)

    def a2(i):
        return remote(a2_out.at[i], a2_in.at[i], a2_send.at[i], a2_recv.at[i], near_y)

    def b2(i):
        return remote(b2_out.at[i], b2_in.at[i], b2_send.at[i], b2_recv.at[i], near_x)

    def to_z(r):
        return remote(z_out.at[r], z_in.at[r], z_send.at[r], z_recv.at[r], along(r))

    def piece(i, carry):
        s = (z + i + 1) % 4
        made = dot_nn(lhs[...], dj[:, pl.ds(pl.multiple_of(s * wide, third), wide)])
        grads[i, :, :wide] = made
        grads[i, :, wide:] = go[:, pl.ds(pl.multiple_of(s * third, third), third)].astype(F32)
        for b in range(2):
            a1_out[i, b] = grads[i, block(b, 1 - x), :two].astype(BF16)
            b1_out[i, b] = grads[i, block(1 - y, b), two:].astype(BF16)
        a1(i).start()
        b1(i).start()
        return carry

    lax.fori_loop(0, 4, piece, 0)

    def second(i):
        a1(i).wait_recv()
        a2_out[i] = (grads[i, block(1 - y, x), :two] + a1_in[i, 1 - y].astype(F32)).astype(BF16)
        a2(i).start()
        b1(i).wait_recv()
        b2_out[i] = (grads[i, block(y, 1 - x), two:] + b1_in[i, 1 - x].astype(F32)).astype(BF16)
        b2(i).start()
        grads[i, block(y, x), :two] = grads[i, block(y, x), :two] + a1_in[i, y].astype(F32)
        grads[i, block(y, x), two:] = grads[i, block(y, x), two:] + b1_in[i, x].astype(F32)

    def third_step(i):
        a2(i).wait_recv()
        b2(i).wait_recv()
        grads[i, block(y, x), :two] = grads[i, block(y, x), :two] + a2_in[i].astype(F32)
        grads[i, block(y, x), two:] = grads[i, block(y, x), two:] + b2_in[i].astype(F32)
        if i < 3:
            z_out[i + 1] = grads[i, block(y, x), :].astype(BF16)
            to_z(i + 1).start()

    def away(i, carry):
        rows = pl.ds(pl.multiple_of(own + i * step, step), step)
        half_out[pl.ds(pl.multiple_of(i * step, step), step)] = dot_nt(dj[rows], weight[...]).astype(BF16)
        return carry

    lax.fori_loop(0, 2, away, 0)
    swap = remote(half_out, half_in, h_send.at[0], h_recv.at[0], pair)
    swap.start()
    second(0)
    fetch_std.wait()
    sums[...] = small_in[...]
    sums[1:2] = next_grad
    swap.wait_recv()

    def home(i, totals):
        rows = pl.ds(pl.multiple_of(i * step, step), step)
        grad = dot_nt(dj[rows], weight[...]) + half_in[rows].astype(F32)
        standard = std[rows]
        full = base[rows] + norm_back(grad, standard, gain[...], inverse[rows])
        hide = masked[rows] > 0.0
        ready[rows] = jnp.where(hide, 0.0, full).astype(BF16)
        return (
            totals[0] + jnp.sum(grad * standard, axis=0, keepdims=True),
            totals[1] + jnp.sum(jnp.where(hide, full, 0.0), axis=0, keepdims=True),
        )

    gain_grad, embed_grad = lax.fori_loop(0, 2, home, (zero, zero))
    sums[0:1] = gain_grad
    sums[3:4] = embed_grad

    def columns(s):
        return pl.ds(pl.multiple_of(s * BLK, BLK), BLK)

    def stays(k):
        return jnp.logical_and(z == k, z // 2 == c)

    def ride(k):
        slot = 2 * (z % 2) + c
        return remote(ready.at[:, columns(k)], rows_in.at[slot], r_send.at[k], r_recv.at[slot], (y, x, z // 2, k))

    def ride_local(k):
        return pltpu.make_async_copy(ready.at[:, columns(k)], rows_in.at[2 * (z % 2) + c], local.at[3])

    for k in range(4):
        pl.when(stays(k))(lambda k=k: ride_local(k).start())
        pl.when(jnp.logical_not(stays(k)))(lambda k=k: ride(k).start())

    def share(h):
        peer = (pair, near_y, near_x)[h]
        return remote(sum_out.at[h], sum_in.at[h], s_send.at[h], s_recv.at[h], peer)

    def begin_share(h):
        sum_out[h] = sums[...]
        share(h).start()

    def end_share(h):
        share(h).wait_recv()
        sums[...] = sums[...] + sum_in[h]

    begin_share(0)
    second(1)
    third_step(0)
    end_share(0)
    begin_share(1)
    second(2)
    third_step(1)
    end_share(1)
    begin_share(2)
    second(3)
    third_step(2)
    end_share(2)
    sum_out[3] = sums[...]

    def deal(r):
        s = (z + r) % 4
        return remote(sum_out.at[3, :, columns(s)], share_in.at[r], p_send.at[r], p_recv.at[r], (y, x, c, s))

    for r in (1, 2, 3):
        deal(r).start()
    third_step(3)
    parity = BLK // 2

    for r in (1, 2, 3):
        time_z(r).wait_recv()
        t_total[...] = t_total[...] + tz_in[r].astype(F32)
    ty_out[...] = t_total[1 - y].astype(BF16)
    swap_y = remote(ty_out, ty_in, ty_send.at[0], ty_recv.at[0], near_y)
    swap_y.start()
    for r in (1, 2, 3):
        feed_z(r).wait_recv()
        f_total[...] = f_total[...] + fz_in[r].astype(F32)
    fc_out[0] = f_other[at(1 - c, parity)].astype(BF16)
    fc_out[1] = f_total[at(1 - c, parity)].astype(BF16)
    swap_feed = remote(fc_out, fc_in, c_send.at[1], c_recv.at[1], pair)
    swap_feed.start()
    units = f_total.shape[1]
    feed_in_out[:, at(c, units)] = f_other[at(c, parity)]
    feed_out_out[at(c, units)] = f_total[at(c, parity)].T
    swap_y.wait_recv()
    tc_out[0] = t_total[y, at(1 - c, parity)].astype(BF16)
    tc_out[1] = ty_in[at(1 - c, parity)]
    swap_time = remote(tc_out, tc_in, c_send.at[2], c_recv.at[2], pair)
    swap_time.start()
    for k in range(4):
        pl.when(stays(k))(lambda k=k: ride_local(k).wait())
        from_self = jnp.logical_and(2 * c + k // 2 == z, c == k % 2)

        def landed(k=k):
            remote(ready.at[:, columns(k)], rows_in.at[k], r_send.at[k], r_recv.at[k], near_y).wait_recv()

        pl.when(jnp.logical_not(from_self))(landed)
    rows_out[...] = rows_in[...].astype(F32)
    for r in (1, 2, 3):
        to_z(r).wait_recv()
    total = grads[3, block(y, x), :]
    for r in (1, 2, 3):
        total = total + z_in[r].astype(F32)
    grads[3, block(y, x), :] = total
    rows = BLK // 2

    def core_rows(core):
        return pl.ds(pl.multiple_of(BLK * (2 * y + x) + rows * core, rows), rows)

    core_out[...] = grads[3, core_rows(1 - c), :].astype(BF16)
    last = remote(core_out, core_in, c_send.at[0], c_recv.at[0], pair)
    last.start()
    def place(core, value):
        for j in range(3):
            space_qkv[j, :, at(core, third)] = value[:, j * third : (j + 1) * third]
        space_out[at(core, third)] = value[:, 3 * third :].T

    place(c, grads[3, core_rows(c), :])
    result = sums[:, columns(z)]
    for r in (1, 2, 3):
        deal(r).wait_recv()
        result = result + share_in[r]
    small_out[...] = result
    swap_feed.wait_recv()
    feed_in_out[:, at(1 - c, units)] = fc_in[0].astype(F32)
    feed_out_out[at(1 - c, units)] = fc_in[1].astype(F32).T
    swap_time.wait_recv()
    mine = (t_total[y, at(c, parity)], ty_in[at(c, parity)].astype(F32))
    other = (tc_in[0].astype(F32), tc_in[1].astype(F32))
    by_head = []
    for yb in range(2):
        for cb in range(2):
            by_head.append(
                jnp.where(
                    c == cb,
                    jnp.where(y == yb, mine[0], mine[1]),
                    jnp.where(y == yb, other[0], other[1]),
                )
            )
    for j in range(4):
        made = jnp.concatenate([v[:, j * HEAD_DIM : (j + 1) * HEAD_DIM] for v in by_head], axis=1)
        if j < 3:
            time_qkv[j] = made
        else:
            time_out[...] = made.T
    last.wait_recv()
    place(1 - c, core_in[...].astype(F32))

    for copy in (last, swap, give, swap_y, swap_feed, swap_time):
        copy.wait_send()
    for yb in range(2):
        time_x(yb).wait_send()
    for r in range(4):
        feed_y(r).wait_send()
    for r in (1, 2, 3):
        time_z(r).wait_send()
        feed_z(r).wait_send()
    for i in range(4):
        for copy in (a1(i), b1(i), a2(i), b2(i)):
            copy.wait_send()
    for r in (1, 2, 3):
        to_z(r).wait_send()
        deal(r).wait_send()
    for h in range(3):
        share(h).wait_send()
    for k in range(4):
        pl.when(jnp.logical_not(stays(k)))(lambda k=k: ride(k).wait_send())


def leave(
    part, std_next, grad, w_out, joined, mixed, lhs, weight, std, g_time, g_out, g_in,
    totals, inverse_next, inverse, masked, gain_next, gain, small, scale,
):
    own, features = std.shape
    cols4 = mixed.shape[1]
    quarter = cols4 // 4
    units = g_in.shape[1]
    dma = pltpu.SemaphoreType.DMA
    anywhere = pl.BlockSpec(memory_space=pl.ANY)
    whole = pl.BlockSpec(memory_space=pltpu.VMEM)
    parity = BLK // 2

    def low(*shape):
        return pltpu.VMEM(shape, BF16)

    def high(*shape):
        return pltpu.VMEM(shape, F32)

    return pl.pallas_call(
        functools.partial(leave_kernel, scale),
        in_specs=[anywhere] * 12 + [whole] * 7,
        out_specs=[whole] * 8,
        out_shape=[
            jax.ShapeDtypeStruct(shape, F32)
            for shape in (
                (3, parity, 2 * quarter), (2 * quarter, parity), (parity, 2 * units), (2 * units, parity),
                (3, parity, BLK), (BLK, parity), (4, own, BLK), (8, BLK),
            )
        ],
        scratch_shapes=[
            low(4, own, BLK),
            high(own, features), high(own, features), high(own, features), low(*w_out.shape), low(*joined.shape),
            low(*mixed.shape), low(*lhs.shape), low(*weight.shape), low(2 * own, features), low(features, 2 * own),
            low(*mixed.shape), low(features, cols4),
            low(2, BLK, features), low(2, BLK, features), low(4, 2, BLK, BLK), low(4, 2, BLK, BLK), high(2, BLK, BLK),
            low(BLK, BLK), low(BLK, BLK), low(2, parity, BLK), low(2, parity, BLK),
            low(4, BLK, units), low(4, BLK, units), low(4, BLK, units), low(4, BLK, units),
            high(BLK, units), high(BLK, units), low(2, parity, units), low(2, parity, units),
            high(4, features, cols4),
            low(4, 2, BLK, 2 * quarter), low(4, 2, BLK, 2 * quarter), low(4, 2, BLK, 2 * quarter), low(4, 2, BLK, 2 * quarter),
            low(4, BLK, 2 * quarter), low(4, BLK, 2 * quarter), low(4, BLK, 2 * quarter), low(4, BLK, 2 * quarter),
            low(4, BLK, cols4), low(4, BLK, cols4),
            low(own, features), low(own, features), low(own, features),
            low(parity, cols4), low(parity, cols4),
            high(8, features), high(4, 8, features), high(3, 8, features), high(4, 8, BLK),
        ]
        + [dma((4,))] * 10
        + [dma((1,)), dma((1,)), dma((4,)), dma((4,)), dma((3,)), dma((3,)), dma((3,)), dma((3,)), dma((4,)), dma((4,)), dma((4,))]
        + [dma((1,)), dma((1,)), dma((2,)), dma((2,)), dma((4,)), dma((4,)), dma((1,)), dma((1,))]
        + [dma((4,)), dma((4,)), dma((4,)), dma((4,)), dma((2,)), dma((4,)), dma((10,))],
        compiler_params=pltpu.CompilerParams(
            collective_id=3, has_side_effects=True, vmem_limit_bytes=62 * 1024 * 1024
        ),
        cost_estimate=pl.CostEstimate(flops=2 * 10**10, transcendentals=10**6, bytes_accessed=10**8),
        name="leave",
    )(
        part, std_next, grad, w_out, joined, mixed, lhs, weight, std, g_time, g_out, g_in,
        totals, inverse_next, inverse, masked, gain_next, gain, small,
    )


def tie(*values):
    return lax.optimization_barrier(values)


def norm_rows(resid):
    mean = jnp.mean(resid, axis=-1, keepdims=True)
    centered = resid - mean
    inverse = lax.rsqrt(jnp.mean(centered * centered, axis=-1, keepdims=True) + eps_norm)
    return (centered * inverse, inverse)


def norm_rows_back(grad, standardized, inverse, gain):
    gain_grad = jnp.sum(grad * standardized, axis=0)
    inner = grad * gain
    mean = jnp.mean(inner, axis=-1, keepdims=True)
    along = jnp.mean(inner * standardized, axis=-1, keepdims=True)
    return ((inner - mean - standardized * along) * inverse, gain_grad)


def cols(parts):
    return jnp.concatenate(parts, axis=1)


def rows_of(parts):
    return jnp.concatenate(parts, axis=0)


def token_parallel(
    tokens,
    cotangent,
    ratio,
    priority,
    frame_order,
    mask_embed,
    gains,
    qkv_space,
    out_space,
    qkv_time,
    out_time,
    w_in,
    w_out,
):
    scale = 1.0 / math.sqrt(HEAD_DIM)
    y, x, c, z = (lax.axis_index(name) for name in AXES)
    patches = tokens.shape[2]
    width = qkv_space.shape[0]
    frames_own = tokens.shape[0] * tokens.shape[1] // 4
    frames_all = frame_order.shape[1]
    own = frames_own * patches
    hidden_own = w_in.shape[1] // 2
    plane = 2 * y + x
    k_own = 2 * (z % 2) + c

    masked_here = (priority < ratio[:, None, None]).astype(jnp.int32).reshape(2, -1)
    info = cols([masked_here, frame_order])
    info = jnp.where(z // 2 == c, info, hop_c(info))
    info = lax.dynamic_index_in_dim(info, z % 2, 0, keepdims=False)
    masked = lax.dynamic_slice_in_dim(info, c * own, own, 0)[:, None] != 0
    order = info[2 * own :].reshape(2, 2, frames_own)
    order = jnp.where(y == 1, order[::-1], order)
    order = jnp.where(c == 1, order[:, ::-1], order).swapaxes(0, 1).reshape(frames_all)
    order = jnp.repeat(order, GROUP)
    patch = jnp.arange(frames_all * GROUP) % GROUP
    visible = (order[:, None] <= order[None, :]) & (patch[:, None] == patch[None, :])
    bias = jnp.where(visible, 0.0, -1e30).astype(F32)

    vectors = rows_of([mask_embed[None], gains, jnp.zeros((4, BLK), BF16)])
    head = (2 * y + c) * HEAD_DIM
    ti_own = cols(
        [
            lax.dynamic_slice_in_dim(qkv_time, head, HEAD_DIM, 2).reshape(width, -1),
            lax.dynamic_slice_in_dim(out_time, head, HEAD_DIM, 0).T,
        ]
    )
    (
        ws_qkv, ws_out, wt_all, wf_out, wf_in, joined0, turned0, std0,
        mixed0, total0, inv0, resid1, std1, inv1, normed1, vectors,
    ) = enter(
        tokens.reshape(4, own, BLK),
        vectors,
        jnp.swapaxes(qkv_space, 0, 1),
        out_space,
        ti_own,
        w_out,
        w_in,
        masked.astype(F32),
        scale,
    )
    gain = [vectors[1 + i : 2 + i] for i in range(3)]

    half = qkv_space.shape[2] // 2
    turned1, joined1, mixed1, total1, delta, upstream, wf_far, wf_in_far = time_call(
        False,
        normed1.reshape(frames_own, patches, width),
        cotangent.reshape(4, own, BLK),
        [wf_out, wf_in],
        wt_all,
        bias,
        scale,
    )
    w_in_half, w_out_half, grad2, grad2_low, block_rows, gain_grad2 = feed(
        resid1, delta.reshape(own, width), upstream, masked.astype(F32), gain[2], wf_in, wf_in_far, wf_out, wf_far
    )

    part1, g_time, g_w_in, block_out = time_call(
        True,
        grad2_low.reshape(frames_own, patches, width),
        block_rows,
        [joined1, total1, w_in_half, turned1, mixed1],
        wt_all,
        bias,
        scale,
    )
    block_out = block_out.reshape(tokens.shape)
    small = rows_of([jnp.zeros((2, width), F32), gain_grad2, jnp.zeros((5, width), F32)])
    grad_qkv_space, grad_out_space, grad_w_in, grad_w_out, grad_qkv_time, grad_out_time, grad_tokens, small = leave(
        part1.reshape(own, width), std1, grad2, ws_out, joined0, mixed0, turned0, ws_qkv, std0, g_time, w_out_half, g_w_in,
        total0, inv1, inv0, masked.astype(F32), gain[1], gain[0], small, scale,
    )
    small = small[:4]
    return (
        block_out,
        grad_tokens.reshape(tokens.shape),
        small[3],
        small[:3],
        jnp.swapaxes(grad_qkv_space, 0, 1),
        grad_out_space,
        jnp.swapaxes(grad_qkv_time, 0, 1),
        grad_out_time,
        grad_w_in,
        grad_w_out,
    )


def solution(mesh):
    sizes = (mesh.shape["tm"], mesh.shape["clip"], mesh.shape["mp"])
    if sizes == (2, 4, 4):
        mesh = jax.sharding.Mesh(mesh.devices.reshape(2, 2, 2, 4), AXES)
        step, clip = token_parallel, ("x", "c")
    else:
        step, clip = shards, ("clip",)
    return jax.shard_map(
        step,
        mesh=mesh,
        in_specs=(
            P(clip, "tm", None, "mp"),
            P(clip, "tm", None, "mp"),
            P(clip),
            P(clip, "tm", None),
            P(clip, None),
            P("mp"),
            P(None, "mp"),
            P(None, None, "mp"),
            P("mp", None),
            P(None, None, "mp"),
            P("mp", None),
            P(None, "mp"),
            P("mp", None),
        ),
        out_specs=(
            P(clip, "tm", None, "mp"),
            P(clip, "tm", None, "mp"),
            P("mp"),
            P(None, "mp"),
            P(("tm",) + clip, None, "mp"),
            P("mp", ("tm",) + clip),
            P(("tm",) + clip, None, "mp"),
            P("mp", ("tm",) + clip),
            P(("tm",) + clip, "mp"),
            P("mp", ("tm",) + clip),
        ),
        check_vma=False,
    )
```

```python
import functools
import math

import jax
import jax.numpy as jnp
from jax import lax
from jax.experimental import pallas as pl
from jax.experimental.pallas import tpu as pltpu
from jax.sharding import PartitionSpec as P

HEAD_DIM = 64
MICRO = 2


eps_norm = 1e-05


def gelu_tanh(values):
    return jax.nn.gelu(values, approximate=True)


def norm_forward_pass(residual_stream, gain_coefficients, complete_width):
    reduced_totals = lax.psum(
        (jnp.sum(residual_stream, axis=-1), jnp.sum(residual_stream * residual_stream, axis=-1)),
        "mp",
    )
    centered_rows = reduced_totals[0] / complete_width
    spread = reduced_totals[1] / complete_width - centered_rows * centered_rows
    inverse_scale = lax.rsqrt(spread + eps_norm)
    standardized_rows = (residual_stream - centered_rows[:, None]) * inverse_scale[:, None]
    shard_rows = (standardized_rows * gain_coefficients).astype(jnp.bfloat16)
    normalized_rows = lax.all_gather(shard_rows, "mp", axis=1, tiled=True)
    return (normalized_rows, standardized_rows, inverse_scale)


def norm_reverse_pass(
    normalized_gradient, standardized_rows, inverse_scale, gain_coefficients, complete_width
):
    gain_gradient = jnp.sum(normalized_gradient * standardized_rows, axis=0)
    standardized_gradient = normalized_gradient * gain_coefficients
    reduced_totals = lax.psum(
        (
            jnp.sum(standardized_gradient, axis=-1),
            jnp.sum(standardized_gradient * standardized_rows, axis=-1),
        ),
        "mp",
    )
    grad_resid = (
        standardized_gradient
        - reduced_totals[0][:, None] / complete_width
        - standardized_rows * (reduced_totals[1][:, None] / complete_width)
    ) * inverse_scale[:, None]
    return (grad_resid, gain_gradient)


def sum_features(grad_full):
    return lax.psum_scatter(
        grad_full.astype(jnp.bfloat16), "mp", scatter_dimension=1, tiled=True
    ).astype(jnp.float32)


def branch_out(hidden, weight):
    partial_rows = jnp.dot(hidden, weight, preferred_element_type=jnp.float32)
    return lax.psum_scatter(partial_rows, "mp", scatter_dimension=1, tiled=True)


def branch_back(grad_resid, hidden, weight):
    grad_rows = lax.all_gather(grad_resid.astype(jnp.bfloat16), "mp", axis=1, tiled=True)
    weight_grad = jnp.einsum("rk,rd->kd", hidden, grad_rows, preferred_element_type=jnp.float32)
    grad_hidden = jnp.einsum("rd,kd->rk", grad_rows, weight, preferred_element_type=jnp.float32)
    return (grad_hidden, weight_grad)


def qkv_back(normalized_rows, grad_joined, weight):
    weight_grad = jnp.einsum(
        "rd,trk->dtk", normalized_rows, grad_joined, preferred_element_type=jnp.float32
    )
    grad_full = jnp.einsum("trk,dtk->rd", grad_joined, weight, preferred_element_type=jnp.float32)
    return (weight_grad, sum_features(grad_full))


def reduce_grads(local_grads, small_grads):
    reduced = (
        lax.psum_scatter(local_grads[0], ("tm", "clip"), scatter_dimension=0, tiled=True),
        lax.psum_scatter(local_grads[1], ("tm", "clip"), scatter_dimension=1, tiled=True),
        lax.psum_scatter(local_grads[2], ("tm", "clip"), scatter_dimension=0, tiled=True),
        lax.psum_scatter(local_grads[3], ("tm", "clip"), scatter_dimension=1, tiled=True),
        lax.psum_scatter(local_grads[4], ("tm", "clip"), scatter_dimension=0, tiled=True),
        lax.psum_scatter(local_grads[5], ("tm", "clip"), scatter_dimension=1, tiled=True),
    )
    reduced_small = lax.psum((small_grads[0], small_grads[1]), ("tm", "clip"))
    return (reduced, reduced_small)


def space_forward(normalized_rows, weight, frame_count, patches, heads_local, scale):
    joined = jnp.einsum(
        "rd,dtk->trk", normalized_rows, weight, preferred_element_type=jnp.float32
    ).astype(jnp.bfloat16)
    shape_heads = (frame_count, patches, heads_local, HEAD_DIM)
    scores = (
        jnp.einsum(
            "bshd,bthd->bhst",
            joined[0].reshape(shape_heads),
            joined[1].reshape(shape_heads),
            preferred_element_type=jnp.float32,
        )
        * scale
    )
    highest = jnp.max(scores, axis=-1, keepdims=True)
    exponent = jnp.exp(scores - highest)
    reduced_totals = jnp.sum(exponent, axis=-1, keepdims=True)
    log_total = highest + jnp.log(reduced_totals)
    attention = (exponent / reduced_totals).astype(jnp.bfloat16)
    mixed = jnp.einsum(
        "bhst,bthd->bshd",
        attention,
        joined[2].reshape(shape_heads),
        preferred_element_type=jnp.float32,
    )
    return (
        joined,
        log_total,
        mixed.astype(jnp.bfloat16).reshape(frame_count * patches, heads_local * HEAD_DIM),
    )


def space_backward(grad_mixed, joined, log_total, frame_count, patches, heads_local, scale):
    shape_heads = (frame_count, patches, heads_local, HEAD_DIM)
    queries = joined[0].reshape(shape_heads)
    key_rows = joined[1].reshape(shape_heads)
    values = joined[2].reshape(shape_heads)
    grad_out = grad_mixed.reshape(shape_heads)
    scores = (
        jnp.einsum("bshd,bthd->bhst", queries, key_rows, preferred_element_type=jnp.float32) * scale
    )
    attention = jnp.exp(scores - log_total)
    grad_values = jnp.einsum(
        "bhst,bshd->bthd",
        attention.astype(jnp.bfloat16),
        grad_out,
        preferred_element_type=jnp.float32,
    )
    grad_att = jnp.einsum("bshd,bthd->bhst", grad_out, values, preferred_element_type=jnp.float32)
    grad_scores = (
        attention * (grad_att - jnp.sum(attention * grad_att, axis=-1, keepdims=True))
    ).astype(jnp.bfloat16)
    grad_queries = (
        jnp.einsum("bhst,bthd->bshd", grad_scores, key_rows, preferred_element_type=jnp.float32)
        * scale
    )
    grad_keys = (
        jnp.einsum("bhst,bshd->bthd", grad_scores, queries, preferred_element_type=jnp.float32)
        * scale
    )
    row_count = frame_count * patches
    stacked = jnp.stack(
        [
            grad_queries.reshape(row_count, -1),
            grad_keys.reshape(row_count, -1),
            grad_values.reshape(row_count, -1),
        ]
    )
    return stacked.astype(jnp.bfloat16)


def time_scores(queries, keys_all, visible, scale):
    scores = (
        jnp.einsum("cfshd,cgshd->chfgs", queries, keys_all, preferred_element_type=jnp.float32)
        * scale
    )
    return jnp.where(visible, scores, -1e30)


def time_forward(queries, keys_all, values_all, visible, scale):
    scores = time_scores(queries, keys_all, visible, scale)
    highest = jnp.max(scores, axis=3, keepdims=True)
    exponent = jnp.exp(scores - highest)
    reduced_totals = jnp.sum(exponent, axis=3, keepdims=True)
    log_total = highest + jnp.log(reduced_totals)
    attention = (exponent / reduced_totals).astype(jnp.bfloat16)
    mixed = jnp.einsum(
        "chfgs,cgshd->cfshd", attention, values_all, preferred_element_type=jnp.float32
    )
    return (log_total, mixed.astype(jnp.bfloat16))


def time_backward(grad_mixed, queries, keys_all, values_all, visible, log_total, scale):
    grad_out = grad_mixed.reshape(queries.shape)
    scores = time_scores(queries, keys_all, visible, scale)
    attention = jnp.exp(scores - log_total)
    grad_values = jnp.einsum(
        "chfgs,cfshd->cgshd",
        attention.astype(jnp.bfloat16),
        grad_out,
        preferred_element_type=jnp.float32,
    )
    grad_att = jnp.einsum(
        "cfshd,cgshd->chfgs", grad_out, values_all, preferred_element_type=jnp.float32
    )
    grad_scores = (
        attention * (grad_att - jnp.sum(attention * grad_att, axis=3, keepdims=True))
    ).astype(jnp.bfloat16)
    grad_queries = (
        jnp.einsum("chfgs,cgshd->cfshd", grad_scores, keys_all, preferred_element_type=jnp.float32)
        * scale
    )
    grad_keys = (
        jnp.einsum("chfgs,cfshd->cgshd", grad_scores, queries, preferred_element_type=jnp.float32)
        * scale
    )
    return (grad_queries, grad_keys, grad_values)


def shards(
    tokens,
    cotangent,
    ratio,
    priority,
    frame_order,
    mask_embed,
    gains,
    qkv_space,
    out_space,
    qkv_time,
    out_time,
    w_in,
    w_out,
):
    scale = 1.0 / math.sqrt(HEAD_DIM)
    clips_local = tokens.shape[0] // MICRO
    frames_local = tokens.shape[1]
    patches = tokens.shape[2]
    cols_local = tokens.shape[3]
    frames_all = frame_order.shape[1]
    hidden_width = qkv_space.shape[0]
    joined_local = qkv_space.shape[2]
    heads_local = joined_local // HEAD_DIM
    row_count = clips_local * frames_local * patches
    gain_broadcast = gains.astype(jnp.float32)
    embed_row = mask_embed.astype(jnp.float32)
    first_frame = lax.axis_index("tm") * frames_local
    shape_local = (clips_local, frames_local, patches, joined_local)
    shape_heads = (clips_local, frames_local, patches, heads_local, HEAD_DIM)
    shape_all = (clips_local, frames_all, patches, heads_local, HEAD_DIM)
    outputs = []
    input_grads = []
    weight_total = None
    small_total = None
    for batch_index in range(MICRO):
        lower = batch_index * clips_local
        upper = lower + clips_local
        source = tokens[lower:upper].reshape(row_count, cols_local).astype(jnp.float32)
        upstream = cotangent[lower:upper].reshape(row_count, cols_local).astype(jnp.float32)
        masked = (priority[lower:upper] < ratio[lower:upper][:, None, None]).reshape(row_count)
        order_rows = frame_order[lower:upper]
        residual_stream0 = jnp.where(masked[:, None], embed_row[None, :], source)
        normalized_rows0, standardized_rows0, inverse_deviation0 = norm_forward_pass(
            residual_stream0, gain_broadcast[0], hidden_width
        )
        joined0, total0, mixed0 = space_forward(
            normalized_rows0, qkv_space, clips_local * frames_local, patches, heads_local, scale
        )
        residual_stream1 = residual_stream0 + branch_out(mixed0, out_space)
        normalized_rows1, standardized_rows1, inverse_deviation1 = norm_forward_pass(
            residual_stream1, gain_broadcast[1], hidden_width
        )
        joined1 = jnp.einsum(
            "rd,dtk->trk", normalized_rows1, qkv_time, preferred_element_type=jnp.float32
        ).astype(jnp.bfloat16)
        queries_local = joined1[0].reshape(shape_local)
        keys_local = joined1[1].reshape(shape_local)
        values_local = joined1[2].reshape(shape_local)
        keys_all, values_all = (
            lax.all_gather(keys_local, "tm", axis=1, tiled=True),
            lax.all_gather(values_local, "tm", axis=1, tiled=True),
        )
        query_order = lax.dynamic_slice_in_dim(order_rows, first_frame, frames_local, axis=1)
        time_visible = (order_rows[:, None, :] <= query_order[:, :, None])[:, None, :, :, None]
        time_q = queries_local.reshape(shape_heads)
        time_k = keys_all.reshape(shape_all)
        time_v = values_all.reshape(shape_all)
        total1, mixed_frames = time_forward(time_q, time_k, time_v, time_visible, scale)
        mixed1 = mixed_frames.reshape(row_count, joined_local)
        residual_stream2 = residual_stream1 + branch_out(mixed1, out_time)
        normalized_rows2, standardized_rows2, inverse_deviation2 = norm_forward_pass(
            residual_stream2, gain_broadcast[2], hidden_width
        )
        projected = jnp.dot(normalized_rows2, w_in, preferred_element_type=jnp.float32)
        activated, gelu_pull = jax.vjp(gelu_tanh, projected)
        hidden = activated.astype(jnp.bfloat16)
        resid3 = residual_stream2 + branch_out(hidden, w_out)
        outputs.append(
            resid3.astype(jnp.bfloat16).reshape(clips_local, frames_local, patches, cols_local)
        )
        grad3 = jnp.where(masked[:, None], upstream, 0.0)
        grad_hidden, grad_w_out = branch_back(grad3, hidden, w_out)
        grad_inner = gelu_pull(grad_hidden)[0].astype(jnp.bfloat16)
        grad_w_in = jnp.einsum(
            "rd,rk->dk", normalized_rows2, grad_inner, preferred_element_type=jnp.float32
        )
        normalized_gradient2 = sum_features(
            jnp.einsum("rk,dk->rd", grad_inner, w_in, preferred_element_type=jnp.float32)
        )
        backward_third, gain_gradient2 = norm_reverse_pass(
            normalized_gradient2,
            standardized_rows2,
            inverse_deviation2,
            gain_broadcast[2],
            hidden_width,
        )
        grad2 = grad3 + backward_third
        grad_mixed1, grad_out_time = branch_back(grad2, mixed1, out_time)
        grad_mixed_low = grad_mixed1.astype(jnp.bfloat16).reshape(shape_local)
        grad_queries, grad_keys, grad_values = time_backward(
            grad_mixed_low, time_q, time_k, time_v, time_visible, total1, scale
        )
        key_part, value_part = (
            lax.psum_scatter(
                grad_keys.reshape(clips_local, frames_all, patches, joined_local).astype(
                    jnp.bfloat16
                ),
                "tm",
                scatter_dimension=1,
                tiled=True,
            ).astype(jnp.float32),
            lax.psum_scatter(
                grad_values.reshape(clips_local, frames_all, patches, joined_local).astype(
                    jnp.bfloat16
                ),
                "tm",
                scatter_dimension=1,
                tiled=True,
            ).astype(jnp.float32),
        )
        grad_joined1 = jnp.stack(
            [
                grad_queries.reshape(row_count, joined_local),
                key_part.reshape(row_count, joined_local),
                value_part.reshape(row_count, joined_local),
            ]
        ).astype(jnp.bfloat16)
        grad_qkv_time, normalized_gradient1 = qkv_back(normalized_rows1, grad_joined1, qkv_time)
        backward_second, gain_gradient1 = norm_reverse_pass(
            normalized_gradient1,
            standardized_rows1,
            inverse_deviation1,
            gain_broadcast[1],
            hidden_width,
        )
        grad1 = grad2 + backward_second
        grad_mixed0, grad_out_space = branch_back(grad1, mixed0, out_space)
        grad_joined0 = space_backward(
            grad_mixed0.astype(jnp.bfloat16),
            joined0,
            total0,
            clips_local * frames_local,
            patches,
            heads_local,
            scale,
        )
        grad_qkv_space, normalized_gradient0 = qkv_back(normalized_rows0, grad_joined0, qkv_space)
        backward_first, gain_gradient0 = norm_reverse_pass(
            normalized_gradient0,
            standardized_rows0,
            inverse_deviation0,
            gain_broadcast[0],
            hidden_width,
        )
        grad0 = grad1 + backward_first
        input_grads.append(
            jnp.where(masked[:, None], 0.0, grad0).reshape(
                clips_local, frames_local, patches, cols_local
            )
        )
        grad_embed = jnp.sum(jnp.where(masked[:, None], grad0, 0.0), axis=0)
        gain_grads = jnp.stack([gain_gradient0, gain_gradient1, gain_gradient2])
        local_grads = (
            grad_qkv_space,
            grad_out_space,
            grad_qkv_time,
            grad_out_time,
            grad_w_in,
            grad_w_out,
        )
        small_grads = (gain_grads, grad_embed)
        reduced, reduced_small = reduce_grads(local_grads, small_grads)
        if weight_total is None:
            weight_total = reduced
            small_total = reduced_small
        else:
            weight_total = tuple((total + grad for total, grad in zip(weight_total, reduced)))
            small_total = tuple((total + grad for total, grad in zip(small_total, reduced_small)))
    return (
        jnp.concatenate(outputs, axis=0),
        jnp.concatenate(input_grads, axis=0),
        small_total[1],
        small_total[0],
        weight_total[0],
        weight_total[1],
        weight_total[2],
        weight_total[3],
        weight_total[4],
        weight_total[5],
    )


AXES = ("tm", "x", "c", "mp")
F32 = jnp.float32
BF16 = jnp.bfloat16
BLK = 256
MESH = pl.DeviceIdType.MESH


def device_pairs(move):
    pairs = []
    for y in range(2):
        for x in range(2):
            for c in range(2):
                for z in range(4):
                    there = move(y, x, c, z)
                    pairs.append(tuple(((q[0] * 2 + q[1]) * 2 + q[2]) * 4 + q[3] for q in ((y, x, c, z), there)))
    return pairs


def hop_y(v):
    return lax.ppermute(v, AXES, device_pairs(lambda y, x, c, z: (1 - y, x, c, z)))


def hop_x(v):
    return lax.ppermute(v, AXES, device_pairs(lambda y, x, c, z: (y, 1 - x, c, z)))


def hop_c(v):
    return lax.ppermute(v, AXES, device_pairs(lambda y, x, c, z: (y, x, 1 - c, z)))


def hop_z(v, shift):
    return lax.ppermute(v, AXES, device_pairs(lambda y, x, c, z: (y, x, c, (z + shift) % 4)))


def spread_pairs(r):
    def move(y, x, c, z):
        k = z ^ r
        return (y, x, k & 1, 2 * c + (k >> 1))

    return device_pairs(move)


def dot_nn(a, b):
    return lax.dot_general(a, b, (((1,), (0,)), ((), ())), preferred_element_type=F32)


def dot_nt(a, b):
    return lax.dot_general(a, b, (((1,), (1,)), ((), ())), preferred_element_type=F32)


def dot_tn(a, b):
    return lax.dot_general(a, b, (((0,), (0,)), ((), ())), preferred_element_type=F32)


def attend_pair(q, k, v, bias, scale):
    mixed, totals = [], []
    for i in range(2):
        mine = slice(i * HEAD_DIM, (i + 1) * HEAD_DIM)
        scores = dot_nt(k[:, mine], q[:, mine]) * scale
        if bias is not None:
            scores = scores + bias
        highest = jnp.max(scores, axis=0, keepdims=True)
        exponent = jnp.exp(scores - highest)
        total = jnp.sum(exponent, axis=0, keepdims=True)
        totals.append(highest + jnp.log(total))
        mixed.append(dot_tn(v[:, mine], exponent.astype(BF16)) * (1.0 / total))
    return (jnp.concatenate(mixed, axis=0).T, totals)


def attend_pair_back(q, k, v, g, totals, bias, scale):
    grads = ([], [], [])
    for i in range(2):
        mine = slice(i * HEAD_DIM, (i + 1) * HEAD_DIM)
        scores = dot_nt(k[:, mine], q[:, mine]) * scale
        if bias is not None:
            scores = scores + bias
        p = jnp.exp(scores - totals[i])
        dp = dot_nt(v[:, mine], g[:, mine])
        ds = (p * (dp - jnp.sum(p * dp, axis=0, keepdims=True))).astype(BF16)
        grads[0].append(dot_tn(k[:, mine], ds) * scale)
        grads[1].append(dot_nn(ds, q[:, mine]) * scale)
        grads[2].append(dot_nn(p.astype(BF16), g[:, mine]))
    return (
        jnp.concatenate(grads[0], axis=0).T,
        jnp.concatenate(grads[1], axis=1),
        jnp.concatenate(grads[2], axis=1),
    )


PAIR = 2 * HEAD_DIM


def enter_kernel(
    scale,
    tok, vec, qkv_hbm, out_hbm, later, feed_hbm, first_hbm, masked,
    wq_out, wo_out, wt, wf, wi, joined_out, turned_out, std_out,
    mixed, total_out, inverse, resid, std_next, inverse_next, low_next, vec_out,
    rows_in, vec_in, wq, wo, normed, joined, turned, std, base, part, part_out, part_in,
    z_send, z_recv, y_send, y_recv, x_send, x_recv, p_send, p_recv, q_send, q_recv,
    t_send, t_recv, v_send, v_recv, u_send, u_recv, w_send, w_recv,
    f_send, f_recv, g_send, g_recv, n_send, n_recv, local, saved,
    i_send, i_recv, j_send, j_recv, k_send, k_recv, l_send, l_recv,
):
    y, x, c, z = (lax.axis_index(name) for name in AXES)
    half = wo.shape[0] // 4
    wide = 3 * half
    span = wt.shape[1] // 4
    size = wf.shape[1] // 4
    own = rows_in.shape[0]
    near_y, near_x, pair = (1 - y, x, c, z), (y, 1 - x, c, z), (y, x, 1 - c, z)
    right_z, left_z = (y, x, c, (z + 1) % 4), (y, x, c, (z + 3) % 4)

    def at(i, length):
        return pl.ds(pl.multiple_of(i * length, length), length)

    def remote(src, dst, send, recv, peer):
        return pltpu.make_async_remote_copy(
            src_ref=src, dst_ref=dst, send_sem=send, recv_sem=recv, device_id=peer, device_id_type=MESH
        )

    def start(all_copies):
        for copy in all_copies:
            copy.start()

    def landed(all_copies):
        for copy in all_copies:
            copy.wait_recv()

    def sent(all_copies):
        for copy in all_copies:
            copy.wait_send()

    core = at(c, half)
    keep = [
        pltpu.make_async_copy(
            qkv_hbm.at[j, :, core], wq.at[:, pl.ds(pl.multiple_of(z * wide + j * half, half), half)], local.at[j]
        )
        for j in range(3)
    ] + [pltpu.make_async_copy(out_hbm.at[core], wo.at[at(z, half)], local.at[3])]
    keep_later = [
        pltpu.make_async_copy(later, wt.at[:, at(z, span)], local.at[4]),
        pltpu.make_async_copy(feed_hbm.at[at(c, 4 * size)], wf.at[z], local.at[5]),
        pltpu.make_async_copy(first_hbm.at[:, at(c, 4 * size)], wi.at[z], local.at[8]),
    ]
    start(keep + keep_later)

    barrier = pltpu.get_barrier_semaphore()
    for dc in range(2):
        for dz in range(4):
            if dc or dz:
                peer = (y, x, (c + dc) % 2, (z + dz) % 4)
                pl.semaphore_signal(barrier, inc=1, device_id=peer, device_id_type=MESH)
    for peer in (near_y, near_x):
        pl.semaphore_signal(barrier, inc=1, device_id=peer, device_id_type=MESH)
    pl.semaphore_wait(barrier, 9)

    def spot(dy, dx):
        return 2 * ((y + dy) % 2) + (x + dx) % 2

    def piece(dy, dx, r, split=False):
        s = (z + r) % 4
        rows = at(spot(dy, dx), BLK)
        first = pl.multiple_of(s * wide, half)
        out = wo.at[at(s, half), at(spot(dy, dx), BLK)]
        if split:
            last = pl.multiple_of(s * wide + 2 * half, half)
            return (wq.at[rows, pl.ds(first, 2 * half)], wq.at[rows, pl.ds(last, half)], out)
        return (wq.at[rows, pl.ds(first, wide)], out)

    def time_piece(dx, r):
        return wt.at[at((x + dx) % 2, 2 * BLK), at((z + r) % 4, span)]

    def feed_piece(dy, r):
        return wf.at[(z + r) % 4, at(spot(dy, 0), size)]

    def copies(parts, send, recv, peer):
        return [remote(ref, ref, send.at[i], recv.at[i], peer) for i, ref in enumerate(parts)]

    def leg(right, step):
        if right:
            return (0 if step == 0 else 4 - step), right_z, 3 - step
        return step, left_z, step + 1

    def z_copies(right, step):
        r, peer, lands = leg(right, step)
        return copies(piece(0, 0, r), z_send.at[int(right), step], z_recv.at[lands], peer)

    def time_z(right, step):
        r, peer, lands = leg(right, step)
        source = later.at[at(x, 2 * BLK)] if step == 0 else time_piece(0, r)
        return [remote(source, time_piece(0, r), u_send.at[int(right), step], u_recv.at[lands], peer)]

    def feed_z(right, step):
        r, peer, lands = leg(right, step)
        source = feed_hbm.at[at(4 * c + spot(0, 0), size)] if step == 0 else feed_piece(0, r)
        return [remote(source, feed_piece(0, r), f_send.at[int(right), step], f_recv.at[lands], peer)]

    def first_piece(dy, dx, r):
        return wi.at[(z + r) % 4, at(spot(dy, dx), BLK)]

    def first_z(right, step):
        r, peer, lands = leg(right, step)
        source = first_hbm.at[at(spot(0, 0), BLK), at(c, 4 * size)] if step == 0 else first_piece(0, 0, r)
        return [remote(source, first_piece(0, 0, r), i_send.at[int(right), step], i_recv.at[lands], peer)]

    def first_y(r, dy=0):
        return [remote(first_piece(dy, 0, r), first_piece(dy, 0, r), j_send.at[r], j_recv.at[r], near_y)]

    def first_x(r, dx=0):
        return [remote(first_piece(0, dx, r), first_piece(0, dx, r), k_send.at[r], k_recv.at[r], near_x)]

    def y_copies(r, dy=0):
        return copies(piece(dy, 0, r), y_send.at[r], y_recv.at[r], near_y)

    def x_copies(r, dx=0):
        return copies(piece(0, dx, r), x_send.at[r], x_recv.at[r], near_x)

    def corner_x(r, dx=0):
        return copies(piece(1, dx, r, split=True)[:1], p_send.at[r], p_recv.at[r], near_x)

    def corner_y(r, dy=0):
        return copies(piece(dy, 1, r, split=True)[1:], q_send.at[r], q_recv.at[r], near_y)

    def time_x(r, dx=0):
        return [remote(time_piece(dx, r), time_piece(dx, r), w_send.at[r], w_recv.at[r], near_x)]

    def feed_y(r, dy=0):
        return [remote(feed_piece(dy, r), feed_piece(dy, r), g_send.at[r], g_recv.at[r], near_y)]

    def token_copies(k):
        peer = (y, x, k % 2, 2 * c + k // 2)
        return [
            remote(tok.at[k], rows_in.at[:, at(z, BLK)], t_send.at[k], t_recv.at[z], peer),
            remote(vec, vec_in.at[:, at(z, BLK)], v_send.at[k], v_recv.at[z], peer),
        ]

    def token_local(k):
        return [
            pltpu.make_async_copy(tok.at[k], rows_in.at[:, at(z, BLK)], local.at[6]),
            pltpu.make_async_copy(vec, vec_in.at[:, at(z, BLK)], local.at[7]),
        ]

    def stays(k):
        return jnp.logical_and(2 * c + k // 2 == z, c == k % 2)

    def start_tokens(ks):
        for k in ks:
            pl.when(stays(k))(lambda k=k: start(token_local(k)))
            pl.when(jnp.logical_not(stays(k)))(lambda k=k: start(token_copies(k)))

    def each_side(j, act):
        pl.when(z >= j + 1)(lambda: act(3 - j, True))
        pl.when(z <= 2 - j)(lambda: act(j + 1, False))

    def begin(make):
        pl.when(z < 3)(lambda: start(make(True, 0)))
        pl.when(z > 0)(lambda: start(make(False, 0)))

    def onward(j, make, right):
        if j < 2:
            pl.when(z < 3 if right else z > 0)(lambda: start(make(right, j + 1)))

    def forward(j):
        def act(r, right):
            landed(copies(piece(0, 0, r), z_send.at[0, 0], z_recv.at[r], near_y))
            onward(j, z_copies, right)
            start(y_copies(r))
            start(x_copies(r))

        each_side(j, act)

    def corners(j):
        def act(r, right):
            landed(y_copies(r, 1))
            start(corner_x(r))
            landed(x_copies(r, 1))
            start(corner_y(r))

        each_side(j, act)

    def time_forward_step(j):
        def act(r, right):
            landed([remote(time_piece(0, r), time_piece(0, r), u_send.at[0, 0], u_recv.at[r], near_x)])
            onward(j, time_z, right)
            start(time_x(r))

        each_side(j, act)

    def feed_forward_step(j):
        def act(r, right):
            landed([remote(feed_piece(0, r), feed_piece(0, r), f_send.at[0, 0], f_recv.at[r], near_y)])
            onward(j, feed_z, right)
            start(feed_y(r))

        each_side(j, act)

    def first_corner_copy(r, dx=0):
        return [remote(first_piece(1, dx, r), first_piece(1, dx, r), l_send.at[r], l_recv.at[r], near_x)]

    def first_corner(j):
        def act(r, right):
            landed(first_y(r, 1))
            start(first_corner_copy(r))

        each_side(j, act)

    def first_forward_step(j):
        def act(r, right):
            landed([remote(first_piece(0, 0, r), first_piece(0, 0, r), i_send.at[0, 0], i_recv.at[r], near_y)])
            onward(j, first_z, right)
            start(first_y(r))
            start(first_x(r))

        each_side(j, act)

    for copy in keep:
        copy.wait()
    begin(z_copies)
    forward(0)
    start_tokens((0, 1))
    forward(1)
    start_tokens((2, 3))
    begin(first_z)
    begin(time_z)
    begin(feed_z)
    corners(0)
    forward(2)
    corners(1)
    for k in range(4):
        def finish_local(k=k):
            for copy in token_local(k):
                copy.wait()

        pl.when(stays(k))(finish_local)
    for s in range(4):
        def arrived(s=s):
            landed([
                remote(tok.at[0], rows_in.at[:, at(s, BLK)], t_send.at[0], t_recv.at[s], near_y),
                remote(vec, vec_in.at[:, at(s, BLK)], v_send.at[0], v_recv.at[s], near_y),
            ])

        pl.when(jnp.logical_not(jnp.logical_and(z == s, z // 2 == c)))(arrived)

    step = own // 2
    slab = 128
    vec_out[...] = vec_in[...].astype(F32)

    def first_norm(i, carry):
        rows = at(i, step)
        value = jnp.where(masked[rows] > 0.0, vec_out[0:1], rows_in[rows].astype(F32))
        base[rows] = value
        standard, inv = norm_rows(value)
        std[rows] = standard
        inverse[rows] = inv
        normed[rows] = (standard * vec_out[1:2]).astype(BF16)
        return carry

    lax.fori_loop(0, 2, first_norm, 0)
    give_normed = remote(normed.at[pl.ds(0, own)], normed.at[pl.ds(own, own)], n_send.at[0], n_recv.at[0], pair)
    give_normed.start()
    corners(2)

    def turn(i, carry):
        turned[:, at(i, slab)] = normed[at(i, slab)].T
        return carry

    lax.fori_loop(0, own // slab, turn, 0)
    for r in (1, 2, 3):
        landed(corner_x(r, 1))
        landed(corner_y(r, 1))
    saves = [
        pltpu.make_async_copy(wq, wq_out, saved.at[0]),
        pltpu.make_async_copy(wo, wo_out, saved.at[1]),
        pltpu.make_async_copy(std, std_out, saved.at[2]),
    ]
    start(saves)
    first_forward_step(0)

    def attend(i, carry):
        rows = at(i, slab)
        for h in range(wo.shape[0] // PAIR):
            q, k, v = (joined[rows, (3 * h + j) * PAIR : (3 * h + j + 1) * PAIR] for j in range(3))
            out, totals = attend_pair(q, k, v, None, scale)
            mixed[rows, h * PAIR : (h + 1) * PAIR] = out.astype(BF16)
            for j in range(2):
                total_out[i, 2 * h + j : 2 * h + j + 1, :] = totals[j]
        return carry

    def project(t):
        rows = pl.ds(t * own, own)
        joined[rows] = dot_nn(normed[rows], wq[...]).astype(BF16)

    frames = own // slab
    project(0)
    time_forward_step(0)
    lax.fori_loop(0, frames, attend, 0)
    part[...] = dot_nn(mixed[pl.ds(0, own)], wo[...])
    feed_forward_step(0)
    first_forward_step(1)
    first_corner(0)
    give_normed.wait_recv()
    project(1)
    saves.append(pltpu.make_async_copy(joined, joined_out, saved.at[3]))
    saves[3].start()
    lax.fori_loop(frames, 2 * frames, attend, 0)
    part_out[...] = dot_nn(mixed[pl.ds(own, own)], wo[...]).astype(BF16)
    give_part = remote(part_out, part_in, n_send.at[1], n_recv.at[1], pair)
    give_part.start()
    time_forward_step(1)
    feed_forward_step(1)
    first_corner(1)
    lax.fori_loop(own // slab, 2 * own // slab, turn, 0)
    saves.append(pltpu.make_async_copy(turned, turned_out, saved.at[4]))
    saves[4].start()
    give_part.wait_recv()
    first_forward_step(2)

    def second_norm(i, carry):
        rows = at(i, step)
        value = base[rows] + part[rows] + part_in[rows].astype(F32)
        resid[rows] = value
        standard, inv = norm_rows(value)
        std_next[rows] = standard
        inverse_next[rows] = inv
        low_next[rows] = (standard * vec_out[2:3]).astype(BF16)
        return carry

    lax.fori_loop(0, 2, second_norm, 0)
    time_forward_step(2)
    feed_forward_step(2)

    def first_ends(j):
        def act(r, right):
            if j == 2:
                landed(first_y(r, 1))
            else:
                landed(first_corner_copy(r, 1))
                sent(first_corner_copy(r))

        each_side(j, act)

    for j in range(3):
        first_ends(j)
    for copy in keep_later + saves:
        copy.wait()
    give_normed.wait_send()
    give_part.wait_send()
    for r in (1, 2, 3):
        landed(time_x(r, 1))
        landed(feed_y(r, 1))
        landed(first_x(r, 1))
        for group in (y_copies(r), x_copies(r), corner_x(r), corner_y(r), time_x(r), feed_y(r), first_y(r), first_x(r)):
            sent(group)
    for step_z in range(3):
        for make in (z_copies, time_z, first_z, feed_z):
            pl.when(jnp.logical_and(z >= step_z, z < 3))(lambda step_z=step_z, make=make: sent(make(True, step_z)))
            pl.when(jnp.logical_and(z + step_z <= 3, z > 0))(lambda step_z=step_z, make=make: sent(make(False, step_z)))
    for k in range(4):
        pl.when(jnp.logical_not(stays(k)))(lambda k=k: sent(token_copies(k)))


def enter(tok, vec, qkv, out, later, feed_weight, first_weight, masked, scale):
    own, width, half = tok.shape[1], 4 * tok.shape[2], out.shape[0] // 2
    size = feed_weight.shape[0] // 2
    dma = pltpu.SemaphoreType.DMA
    anywhere = pl.BlockSpec(memory_space=pl.ANY)
    whole = pl.BlockSpec(memory_space=pltpu.VMEM)
    heads = 4 * half // HEAD_DIM

    def low(*shape):
        return pltpu.VMEM(shape, BF16)

    def high(*shape):
        return pltpu.VMEM(shape, F32)

    shapes = [
        ((width, 12 * half), BF16), ((4 * half, width), BF16), ((width, 4 * later.shape[1]), BF16),
        ((4, size, width), BF16), ((4, width, size), BF16), ((2 * own, 12 * half), BF16), ((width, 2 * own), BF16), ((own, width), F32),
        ((2 * own, 4 * half), BF16), ((2 * own // 128, heads, 128), F32), ((own, 1), F32), ((own, width), F32),
        ((own, width), F32), ((own, 1), F32), ((own, width), BF16), ((vec.shape[0], width), F32),
    ]
    return pl.pallas_call(
        functools.partial(enter_kernel, scale),
        in_specs=[anywhere] * 7 + [whole],
        out_specs=[anywhere] * 8 + [whole] * 8,
        out_shape=[jax.ShapeDtypeStruct(shape, kind) for shape, kind in shapes],
        scratch_shapes=[
            low(own, width), low(vec.shape[0], width), low(width, 12 * half), low(4 * half, width),
            low(2 * own, width), low(2 * own, 12 * half), low(width, 2 * own), high(own, width), high(own, width),
            high(own, width), low(own, width), low(own, width),
            dma((2, 3, 2)), dma((4, 2)), dma((4, 2)), dma((4, 2)), dma((4, 2)), dma((4, 2)),
            dma((4, 1)), dma((4, 1)), dma((4, 2)), dma((4, 2)),
            dma((4,)), dma((4,)), dma((4,)), dma((4,)), dma((2, 3)), dma((4,)), dma((4,)), dma((4,)),
            dma((2, 3)), dma((4,)), dma((4,)), dma((4,)), dma((2,)), dma((2,)), dma((9,)), dma((5,)),
            dma((2, 3)), dma((4,)), dma((4,)), dma((4,)), dma((4,)), dma((4,)), dma((4,)), dma((4,)),
        ],
        compiler_params=pltpu.CompilerParams(
            collective_id=0, has_side_effects=True, vmem_limit_bytes=56 * 1024 * 1024
        ),
        cost_estimate=pl.CostEstimate(flops=10**10, transcendentals=10**6, bytes_accessed=10**8),
        name="enter",
    )(tok, vec, qkv, out, later, feed_weight, first_weight, masked)


GROUP = 8
CHUNK = 16


def time_kernel(back, scale, heads, *refs):
    if back:
        (own_ref, rider_ref, joined_ref, total_ref, wide_ref, turned_ref, mixed_ref, wt_ref, bias_ref) = refs[:9]
        (delta_ref, grad_ref, reduced_ref, rider_out) = refs[9:13]
        (half_in, half_own, line_out, line_in, half_send, half_recv, half_local, line_send, line_recv) = refs[-13:-4]
        (out_ref, turned, grad_qkv, grad_out) = refs[-4:]
        refs = refs[13:-13]
    else:
        (own_ref, rider_ref, far_ref, in_ref, wt_ref, bias_ref) = refs[:6]
        (turned_ref, out_ref, mixed_ref, total_ref, delta_ref, rider_out, spread_out, in_out) = refs[6:14]
        turned = refs[-1]
        refs = refs[14:-1]
    (
        wq_ref, wo_ref, held, wide, narrow, kept, core_out, core_in, near_out, near_in,
        gy_send, gy_recv, gc_send, gc_recv, gd_send, gd_recv, sc_send, sc_recv, sy_send, sy_recv,
        r_send, r_recv, r_local, out_sem, wx_send, wx_recv,
    ) = refs
    y, x, c, z = (lax.axis_index(name) for name in AXES)
    near, pair, near_x = (1 - y, x, c, z), (y, x, 1 - c, z), (y, 1 - x, c, z)
    frames = held.shape[0] // 4
    chunks = held.shape[1] // CHUNK
    width = heads * HEAD_DIM
    groups = CHUNK // GROUP

    barrier = pltpu.get_barrier_semaphore()
    for dc in range(2):
        for dz in range(4):
            if dc or dz:
                pl.semaphore_signal(barrier, inc=1, device_id=(y, x, (c + dc) % 2, (z + dz) % 4), device_id_type=MESH)
    pl.semaphore_signal(barrier, inc=1, device_id=near, device_id_type=MESH)
    pl.semaphore_signal(barrier, inc=1, device_id=near_x, device_id_type=MESH)
    pl.semaphore_wait(barrier, 9)

    def remote(src, dst, send, recv, peer):
        return pltpu.make_async_remote_copy(
            src_ref=src, dst_ref=dst, send_sem=send, recv_sem=recv, device_id=peer, device_id_type=MESH
        )

    def patches(k):
        return pl.ds(pl.multiple_of(k * CHUNK, CHUNK), CHUNK)

    def block(b, k):
        return held.at[pl.ds(b * frames, frames), patches(k)]

    def gather_y(k):
        return remote(own_ref.at[:, patches(k)], block(1, k), gy_send.at[k], gy_recv.at[k], near)

    def gather_c(k):
        return remote(own_ref.at[:, patches(k)], block(2, k), gc_send.at[k], gc_recv.at[k], pair)

    def gather_d(k):
        return remote(block(1, k), block(3, k), gd_send.at[k], gd_recv.at[k], pair)

    def scatter_c(k):
        return remote(core_out.at[k], core_in.at[k], sc_send.at[k], sc_recv.at[k], pair)

    def scatter_y(k):
        return remote(near_out.at[k], near_in.at[k], sy_send.at[k], sy_recv.at[k], near)

    def save(k):
        there = (turned_ref.at[k], turned.at[k]) if back else (turned.at[k], turned_ref.at[k])
        return pltpu.make_async_copy(*there, out_sem.at[k])

    def columns(s):
        return pl.ds(pl.multiple_of(s * BLK, BLK), BLK)

    def stays(k):
        if back:
            return jnp.logical_and(z == k, z // 2 == c)
        return jnp.logical_and(2 * c + k // 2 == z, c == k % 2)

    def ride(k):
        if back:
            src, dst = rider_ref.at[:, columns(k)], rider_out.at[2 * (z % 2) + c]
            peer, slot = (y, x, z // 2, k), 2 * (z % 2) + c
        else:
            src, dst = rider_ref.at[k], rider_out.at[:, columns(z)]
            peer, slot = (y, x, k % 2, 2 * c + k // 2), z
        return src, dst, peer, slot

    def ride_remote(k):
        src, dst, peer, slot = ride(k)
        return remote(src, dst, r_send.at[k], r_recv.at[slot], peer)

    def ride_local(k):
        src, dst, _, _ = ride(k)
        return pltpu.make_async_copy(src, dst, r_local.at[0])

    def ride_landed(k):
        if back:
            src, dst = rider_ref.at[:, columns(k)], rider_out.at[k]
        else:
            src, dst = rider_ref.at[k], rider_out.at[:, columns(k)]
        return remote(src, dst, r_send.at[k], r_recv.at[k], near)

    def from_self(k):
        if back:
            return jnp.logical_and(2 * c + k // 2 == z, c == k % 2)
        return jnp.logical_and(z == k, z // 2 == c)

    def spread_x(i, dx=0):
        r, yb = i // 2 + 1, i % 2
        size = far_ref.shape[1] // 4
        at = pl.multiple_of(size * (2 * yb + (x + dx) % 2), size)
        src = far_ref.at[(z + r) % 4, pl.ds(at, size)]
        return remote(src, spread_out.at[(z + r) % 4, pl.ds(at, size)], wx_send.at[i], wx_recv.at[i], near_x)

    gather_y(0).start()
    for k in range(chunks):
        if k > 0:
            gather_y(k).start()
        gather_c(k).start()
    def spread_in(dx=0):
        at = pl.multiple_of(BLK * (2 * (1 - y) + (x + dx) % 2), BLK)
        there = in_out.at[3 - z, pl.ds(at, BLK)]
        return remote(in_ref.at[3 - z, pl.ds(at, BLK)], there, wx_send.at[6], wx_recv.at[6], near_x)

    at_end = jnp.logical_or(z == 0, z == 3)

    def half_away(s):
        return remote(wide_ref.at[1 - x, s], half_in.at[s], half_send.at[s], half_recv.at[s], near_x)

    def half_here(s):
        return pltpu.make_async_copy(wide_ref.at[x, s], half_own.at[s], half_local.at[s])

    def line_away(r):
        return remote(line_out.at[r], line_in.at[r], line_send.at[r], line_recv.at[r], (y, x, c, (z + r) % 4))

    def halve():
        for s in range(4):
            half_away(s).wait_recv()
            half_here(s).wait()
        for r in range(4):
            s = (z + r) % 4
            whole = half_own[s].astype(F32) + half_in[s].astype(F32)
            if r == 0:
                reduced_ref[...] = whole
            else:
                line_out[r] = whole.astype(BF16)
                line_away(r).start()

    if back:
        for s in range(4):
            half_away(s).start()
            half_here(s).start()
    else:
        pl.when(at_end)(lambda: spread_in().start())
        for i in range(6):
            spread_x(i).start()
    for k in range(4):
        pl.when(stays(k))(lambda k=k: ride_local(k).start())
        pl.when(jnp.logical_not(stays(k)))(lambda k=k: ride_remote(k).start())
    held[:frames] = own_ref[...]
    if back:
        for k in range(chunks):
            save(k).start()

    def assemble(i, carry):
        rows = pl.ds(pl.multiple_of(i * BLK, BLK), BLK)
        for s in range(0, heads, 2):
            for part in range(4):
                both = [
                    wt_ref[rows, (s + j) * 4 * HEAD_DIM + part * HEAD_DIM : (s + j) * 4 * HEAD_DIM + (part + 1) * HEAD_DIM]
                    for j in range(2)
                ]
                both = jnp.concatenate(both, axis=1)
                if part < 3:
                    wq_ref[rows, part * width + s * HEAD_DIM : part * width + s * HEAD_DIM + PAIR] = both
                else:
                    wo_ref[rows, s * HEAD_DIM : s * HEAD_DIM + PAIR] = both
        return carry

    lax.fori_loop(0, wt_ref.shape[0] // BLK, assemble, 0)

    def finish(k):
        scatter_c(k).wait_recv()
        both = kept[:, patches(k)] + core_in[k].astype(F32)
        near_out[k] = both[frames:].astype(BF16)
        delta_ref[:, patches(k)] = both[:frames]
        scatter_y(k).start()

    def pass_on(k):
        gather_y(k).wait_recv()
        gather_d(k).start()

    def one_group(i, rows):
        at = pl.ds(pl.multiple_of(i * GROUP, GROUP), GROUP)
        count = 4 * frames * GROUP
        bias = bias_ref[...]
        for lo in range(0, width, PAIR):
            q, k, v = (
                wide[:, at, part * width + lo : part * width + lo + PAIR].reshape(count, PAIR).astype(BF16)
                for part in range(3)
            )
            h = lo // HEAD_DIM
            if back:
                g = narrow[:, at, lo : lo + PAIR].reshape(count, PAIR).astype(BF16)
                totals = [total_ref[rows * groups + i, h + j : h + j + 1, :] for j in range(2)]
                grads = attend_pair_back(q, k, v, g, totals, bias, scale)
                for part in range(3):
                    wide[:, at, part * width + lo : part * width + lo + PAIR] = grads[part].reshape(
                        4 * frames, GROUP, PAIR
                    )
            else:
                mixed, totals = attend_pair(q, k, v, bias, scale)
                narrow[:, at, lo : lo + PAIR] = mixed.reshape(4 * frames, GROUP, PAIR)
                for j in range(2):
                    total_ref[rows * groups + i, h + j : h + j + 1, :] = totals[j]

    def one_chunk(k, carry):
        pl.when(k + 1 < chunks)(lambda: pass_on(k + 1))
        gather_c(k).wait_recv()
        gather_d(k).wait_recv()
        count = 4 * frames * CHUNK
        lhs = held[:, patches(k)].reshape(count, held.shape[2])
        if back:
            wide[...] = joined_ref[:, patches(k)].astype(F32)
            narrow[...] = dot_nn(lhs, wo_ref[...]).astype(BF16).astype(F32).reshape(narrow.shape)
        else:
            joined = dot_nn(lhs, wq_ref[...]).astype(BF16)
            out_ref[:, patches(k)] = joined.reshape(wide.shape)
            wide[...] = joined.astype(F32).reshape(wide.shape)
        lax.fori_loop(0, groups, lambda i, carry: (one_group(i, k), carry)[1], 0)
        if back:
            grads = wide[...].astype(BF16)
            out_ref[:, patches(k)] = grads
            partial = dot_nt(grads.reshape(count, 3 * width), wq_ref[...])
        else:
            mixed = narrow[...].astype(BF16)
            mixed_ref[:, patches(k)] = mixed
            partial = dot_nt(mixed.reshape(count, width), wo_ref[...])
        partial = partial.reshape(4 * frames, CHUNK, held.shape[2])
        kept[:, patches(k)] = partial[: 2 * frames]
        core_out[k] = partial[2 * frames :].astype(BF16)
        scatter_c(k).start()
        pl.when(k > 0)(lambda: finish(k - 1))
        if not back:
            for b in range(4):
                slab = held[b * frames : (b + 1) * frames, patches(k)].reshape(frames * CHUNK, held.shape[2])
                turned[k, :, b * frames * CHUNK : (b + 1) * frames * CHUNK] = slab.T
            save(k).start()
        if back:
            pl.when(k == chunks // 2 - 1)(halve)
        return carry

    pass_on(0)
    lax.fori_loop(0, chunks, one_chunk, 0)
    finish(chunks - 1)

    def weigh(k, carry):
        count = 4 * frames * CHUNK
        save(k).wait()
        grad_qkv[...] = grad_qkv[...] + dot_nn(turned[k], out_ref[:, patches(k)].reshape(count, 3 * width))
        grad_out[...] = grad_out[...] + dot_tn(
            mixed_ref[:, patches(k)].reshape(count, width), held[:, patches(k)].reshape(count, held.shape[2])
        )
        return carry

    def arrange(i, carry):
        rows = pl.ds(pl.multiple_of(i * BLK, BLK), BLK)
        last = grad_out[:, rows].T
        for s in range(heads):
            mine = slice(s * HEAD_DIM, (s + 1) * HEAD_DIM)
            parts = [grad_qkv[rows, j * width : (j + 1) * width][:, mine] for j in range(3)] + [last[:, mine]]
            grad_ref[rows, 2 * s * PAIR : (2 * s + 1) * PAIR] = jnp.concatenate(parts[:2], axis=1).astype(BF16)
            grad_ref[rows, (2 * s + 1) * PAIR : (2 * s + 2) * PAIR] = jnp.concatenate(parts[2:], axis=1).astype(BF16)
        return carry

    if back:
        grad_qkv[...] = jnp.zeros_like(grad_qkv)
        grad_out[...] = jnp.zeros_like(grad_out)
        lax.fori_loop(0, chunks, weigh, 0)
        lax.fori_loop(0, grad_ref.shape[0] // BLK, arrange, 0)
    for k in range(chunks):
        scatter_y(k).wait_recv()
        delta_ref[:, patches(k)] = delta_ref[:, patches(k)] + near_in[k].astype(F32)
    if back:
        for r in (1, 2, 3):
            line_away(r).wait_recv()
            reduced_ref[...] = reduced_ref[...] + line_in[r].astype(F32)
        for r in (1, 2, 3):
            line_away(r).wait_send()
        for s in range(4):
            half_away(s).wait_send()
    for k in range(chunks):
        for copy in (gather_y(k), gather_c(k), gather_d(k), scatter_c(k), scatter_y(k)):
            copy.wait_send()
        if not back:
            save(k).wait()
    if not back:
        for i in range(6):
            spread_x(i, 1).wait_recv()
            spread_x(i).wait_send()

        def spread_in_end():
            spread_in(1).wait_recv()
            spread_in().wait_send()

        pl.when(at_end)(spread_in_end)
    for k in range(4):
        pl.when(stays(k))(lambda k=k: ride_local(k).wait())
        pl.when(jnp.logical_not(stays(k)))(lambda k=k: ride_remote(k).wait_send())
        pl.when(jnp.logical_not(from_self(k)))(lambda k=k: ride_landed(k).wait_recv())


def time_call(back, own, rider, saved, weights, bias, scale):
    frames, patches, features = own.shape
    width = weights.shape[1] // 4
    heads = width // HEAD_DIM
    chunks = patches // CHUNK
    rows = 4 * frames * GROUP
    dma = pltpu.SemaphoreType.DMA
    anywhere = pl.BlockSpec(memory_space=pl.ANY)
    whole = pl.BlockSpec(memory_space=pltpu.VMEM)
    turned = (chunks, features, 4 * frames * CHUNK)
    if back:
        out_shape = []
    else:
        out_shape = [
            jax.ShapeDtypeStruct(turned, BF16),
            jax.ShapeDtypeStruct((4 * frames, patches, 3 * width), BF16),
            jax.ShapeDtypeStruct((4 * frames, patches, width), BF16),
            jax.ShapeDtypeStruct((patches // GROUP, heads, rows), F32),
        ]
    rider_shape = (4, frames * patches, BLK) if back else (frames * patches, features)
    out_shape += [
        jax.ShapeDtypeStruct((frames, patches, features), F32),
        jax.ShapeDtypeStruct(rider_shape, BF16),
    ]
    held = 2
    half = saved[2].shape[1:] if back else None
    if back:
        out_shape.insert(-1, jax.ShapeDtypeStruct((features, features), BF16))
        out_shape.insert(-1, jax.ShapeDtypeStruct(half[1:], F32))
    else:
        out_shape += [jax.ShapeDtypeStruct(w.shape, BF16) for w in saved]
        held = 4
    return pl.pallas_call(
        functools.partial(time_kernel, back, scale, heads),
        in_specs=[whole, anywhere] + ([whole, whole, anywhere, anywhere, whole] if back else [anywhere] * 2) + [whole] * 2,
        out_specs=([] if back else [anywhere]) + [whole] * (len(out_shape) - held + back) + [anywhere] * (held - 1),
        out_shape=out_shape,
        scratch_shapes=[
            pltpu.VMEM((features, 3 * width), BF16),
            pltpu.VMEM((features, width), BF16),
            pltpu.VMEM((4 * frames, patches, features), BF16),
            pltpu.VMEM((4 * frames, CHUNK, 3 * width), F32),
            pltpu.VMEM((4 * frames, CHUNK, width), F32),
            pltpu.VMEM((2 * frames, patches, features), F32),
            pltpu.VMEM((chunks, 2 * frames, CHUNK, features), BF16),
            pltpu.VMEM((chunks, 2 * frames, CHUNK, features), BF16),
            pltpu.VMEM((chunks, frames, CHUNK, features), BF16),
            pltpu.VMEM((chunks, frames, CHUNK, features), BF16),
        ]
        + [dma((chunks,))] * 10
        + [dma((4,)), dma((4,)), dma((1,)), dma((chunks,))]
        + [dma((7,))] * 2
        + ([pltpu.VMEM(half, BF16)] * 4 + [dma((4,))] * 5 if back else [])
        + ([pltpu.VMEM((4 * frames, patches, 3 * width), BF16)] if back else [])
        + [pltpu.VMEM(turned, BF16)]
        + ([pltpu.VMEM((features, 3 * width), F32), pltpu.VMEM((width, features), F32)] if back else []),
        compiler_params=pltpu.CompilerParams(
            collective_id=2 if back else 1, has_side_effects=True, vmem_limit_bytes=60 * 1024 * 1024
        ),
        cost_estimate=pl.CostEstimate(flops=10**10, transcendentals=10**6, bytes_accessed=10**8),
        name="time_back" if back else "time_forward",
    )(own, rider, *saved, weights, bias)


def feed_kernel(
    resid, delta, upstream, masked, gain, w_in_hbm, w_in_far_hbm, w_out_hbm, w_far_hbm,
    half_in_hbm, half_out_hbm, grad_out, low_out, rows_out, gain_out,
    w_in, w_out, standard, inverse, normed, grads, normed_t, grads_t, hidden, pulled, g_in, g_out, back, ahead,
    back_out, back_in, ahead_out, ahead_in, from_x, from_y,
    w_sem, g_sem, n_send, n_recv, b_send, b_recv, hx_send, hx_recv, hy_send, hy_recv,
):
    y, x, c, z = (lax.axis_index(name) for name in AXES)
    pair, near_y, near_x = (y, x, 1 - c, z), (1 - y, x, c, z), (y, 1 - x, c, z)
    own = resid.shape[0]
    step = own // 2
    slab = 128

    def fetch(s, far, last=False):
        size = w_out.shape[1] // 4
        copies = []
        for i in range(4):
            rows = pl.ds(pl.multiple_of(BLK * (2 * ((y + i // 2) % 2) + (x + i % 2) % 2), BLK), BLK)
            source = w_in_far_hbm if last and i == 3 else w_in_hbm
            copies.append(pltpu.make_async_copy(source.at[s, rows], w_in.at[s, rows], w_sem.at[5 + i, s]))
        for i in range(4):
            rows = pl.ds(pl.multiple_of(size * (2 * (i // 2) + (x + i % 2) % 2), size), size)
            source = w_far_hbm if far and i % 2 else w_out_hbm
            copies.append(pltpu.make_async_copy(source.at[s, rows], w_out.at[s, rows], w_sem.at[i, s]))
        return copies

    def fetch_now(s, far, last):
        for copy in fetch(s, far, last):
            copy.start()

    for s in range(4):
        pl.when(z == s)(lambda s=s: fetch_now(s, False, False))
        if s in (0, 3):
            pl.when(z == 3 - s)(lambda s=s: fetch_now(s, True, True))
            pl.when(jnp.logical_and(z != s, z != 3 - s))(lambda s=s: fetch_now(s, True, False))
        else:
            pl.when(z != s)(lambda s=s: fetch_now(s, True, False))
    barrier = pltpu.get_barrier_semaphore()
    for peer in (pair, near_y, near_x):
        pl.semaphore_signal(barrier, inc=1, device_id=peer, device_id_type=MESH)

    def remote(src, dst, send, recv, peer=pair):
        return pltpu.make_async_remote_copy(
            src_ref=src, dst_ref=dst, send_sem=send, recv_sem=recv, device_id=peer, device_id_type=MESH
        )

    def block(yb, xb):
        return pl.ds(pl.multiple_of(BLK * (2 * yb + xb), BLK), BLK)

    def away_x(s, i):
        return remote(g_out.at[s, block(i, 1 - x)], from_x.at[i, s], hx_send.at[i, s], hx_recv.at[i, s], near_x)

    def away_y(s, i):
        return remote(g_in.at[s, block(1 - y, i)], from_y.at[i, s], hy_send.at[i, s], hy_recv.at[i, s], near_y)

    def keep(s, i):
        return (
            pltpu.make_async_copy(g_out.at[s, block(i, x)], half_out_hbm.at[i, s], g_sem.at[0, i, s]),
            pltpu.make_async_copy(g_in.at[s, block(y, i)], half_in_hbm.at[i, s], g_sem.at[1, i, s]),
        )

    def combine(s):
        for i in range(2):
            away_x(s, i).wait_recv()
            g_out[s, block(i, x)] = (g_out[s, block(i, x)].astype(F32) + from_x[i, s].astype(F32)).astype(BF16)
            away_y(s, i).wait_recv()
            g_in[s, block(y, i)] = (g_in[s, block(y, i)].astype(F32) + from_y[i, s].astype(F32)).astype(BF16)
            for copy in keep(s, i):
                copy.start()

    def at(i, size):
        return pl.ds(pl.multiple_of(i * size, size), size)

    def prepare(i, carry):
        rows = at(i, step)
        grads[rows] = jnp.where(masked[rows] > 0.0, upstream[rows].astype(F32), 0.0).astype(BF16)
        std, inv = norm_rows(resid[rows] + delta[rows])
        standard[rows] = std
        inverse[rows] = inv
        normed[rows] = (std * gain[3:4]).astype(BF16)
        return carry

    lax.fori_loop(0, 2, prepare, 0)
    pl.semaphore_wait(barrier, 3)
    mine, theirs = pl.ds(0, own), pl.ds(own, own)
    give_grads = remote(grads.at[mine], grads.at[theirs], n_send.at[0], n_recv.at[0])
    give_normed = remote(normed.at[mine], normed.at[theirs], n_send.at[1], n_recv.at[1])
    give_normed.start()
    give_grads.start()

    def turn(i, carry):
        rows = at(i, slab)
        normed_t[:, rows] = normed[rows].T
        grads_t[:, rows] = grads[rows].T
        return carry

    lax.fori_loop(0, own // slab, turn, 0)
    back[...] = jnp.zeros_like(back)
    ahead[...] = jnp.zeros_like(ahead)
    rate = math.sqrt(2.0 / math.pi)

    def rows_step(s, rows):
        inner = dot_nn(normed[rows], w_in[s])
        square = inner * inner
        bend = jnp.tanh(rate * inner * (1.0 + 0.044715 * square))
        hidden[rows] = (0.5 * inner * (1.0 + bend)).astype(BF16)
        slope = 0.5 * (1.0 + bend) + 0.5 * inner * (1.0 - bend * bend) * (rate * (1.0 + 3.0 * 0.044715 * square))
        pulled[rows] = (dot_nt(grads[rows], w_out[s]) * slope).astype(BF16)
        ahead[rows] = ahead[rows] + dot_nn(hidden[rows], w_out[s])
        back[rows] = back[rows] + dot_nt(pulled[rows], w_in[s])

    def meet():
        give_normed.wait_recv()
        give_grads.wait_recv()
        lax.fori_loop(own // slab, 2 * own // slab, turn, 0)

    def one_piece(s, carry):
        for copy in fetch(s, False):
            copy.wait()

        def one_half(t, carry):
            pl.when(jnp.logical_and(s == 0, t == 1))(meet)
            rows_step(s, at(t, own))
            return carry

        lax.fori_loop(0, 2, one_half, 0)
        g_out[s] = dot_nn(grads_t[...], hidden[...]).astype(BF16)
        g_in[s] = dot_nn(normed_t[...], pulled[...]).astype(BF16)
        for i in range(2):
            away_x(s, i).start()
            away_y(s, i).start()
        return carry

    lax.fori_loop(0, 4, one_piece, 0)
    back_out[...] = back[theirs].astype(BF16)
    give_back = remote(back_out, back_in, b_send.at[0], b_recv.at[0])
    give_back.start()
    ahead_out[...] = ahead[theirs].astype(BF16)
    give_ahead = remote(ahead_out, ahead_in, b_send.at[1], b_recv.at[1])
    give_ahead.start()
    give_back.wait_recv()

    def finish(i, total):
        rows = at(i, step)
        grad = back[rows] + back_in[rows].astype(F32)
        std = standard[rows]
        inner = grad * gain[3:4]
        mean = jnp.mean(inner, axis=-1, keepdims=True)
        along = jnp.mean(inner * std, axis=-1, keepdims=True)
        full = grads[rows].astype(F32) + (inner - mean - std * along) * inverse[rows]
        grad_out[rows] = full
        low_out[rows] = full.astype(BF16)
        return total + jnp.sum(grad * std, axis=0, keepdims=True)

    gain_out[...] = lax.fori_loop(0, 2, finish, jnp.zeros((1, resid.shape[1]), F32))
    give_ahead.wait_recv()

    def emit(i, carry):
        rows = at(i, step)
        rows_out[rows] = (resid[rows] + delta[rows] + ahead[rows] + ahead_in[rows].astype(F32)).astype(BF16)
        return carry

    lax.fori_loop(0, 2, emit, 0)
    lax.fori_loop(0, 4, lambda s, carry: (combine(s), carry)[1], 0)
    for copy in (give_normed, give_grads, give_back, give_ahead):
        copy.wait_send()
    for s in range(4):
        for i in range(2):
            away_x(s, i).wait_send()
            away_y(s, i).wait_send()
            for copy in keep(s, i):
                copy.wait()


def feed(resid, delta, upstream, masked, gain, w_in, w_in_far, w_out, w_far):
    own, features = resid.shape
    units = w_in.shape[2]
    dma = pltpu.SemaphoreType.DMA
    anywhere = pl.BlockSpec(memory_space=pl.ANY)
    whole = pl.BlockSpec(memory_space=pltpu.VMEM)

    def low(*shape):
        return pltpu.VMEM(shape, BF16)

    def high(*shape):
        return pltpu.VMEM(shape, F32)

    return pl.pallas_call(
        feed_kernel,
        in_specs=[whole] * 5 + [anywhere] * 4,
        out_specs=[anywhere] * 2 + [whole] * 4,
        out_shape=[
            jax.ShapeDtypeStruct((2, 4, BLK, units), BF16),
            jax.ShapeDtypeStruct((2, 4, BLK, units), BF16),
            jax.ShapeDtypeStruct((own, features), F32),
            jax.ShapeDtypeStruct((own, features), BF16),
            jax.ShapeDtypeStruct((own, features), BF16),
            jax.ShapeDtypeStruct((1, features), F32),
        ],
        scratch_shapes=[
            low(4, features, units), low(4, units, features), high(own, features), high(own, 1),
            low(2 * own, features), low(2 * own, features), low(features, 2 * own), low(features, 2 * own),
            low(2 * own, units), low(2 * own, units), low(4, features, units), low(4, features, units),
            high(2 * own, features), high(2 * own, features),
            low(own, features), low(own, features), low(own, features), low(own, features),
            low(2, 4, BLK, units), low(2, 4, BLK, units),
            dma((9, 4)), dma((2, 2, 4)), dma((2,)), dma((2,)), dma((2,)), dma((2,)),
            dma((2, 4)), dma((2, 4)), dma((2, 4)), dma((2, 4)),
        ],
        compiler_params=pltpu.CompilerParams(
            collective_id=4, has_side_effects=True, vmem_limit_bytes=60 * 1024 * 1024
        ),
        cost_estimate=pl.CostEstimate(flops=26 * 10**9, transcendentals=2 * 10**6, bytes_accessed=10**8),
        name="feed",
    )(resid, delta, upstream, masked, gain, w_in, w_in_far, w_out, w_far)


def leave_kernel(
    scale,
    part_hbm, next_hbm, grad_hbm, out_hbm, joined_hbm, mixed_hbm, lhs_hbm, weight_hbm, std_hbm, time_hbm, feed_hbm, feed_in_hbm,
    totals, inverse_next, inverse, masked, gains, later_grad,
    space_qkv, space_out, feed_in_out, feed_out_out, time_qkv, time_out, rows_out, small_out,
    rows_in,
    part, std, base, w_out, dj, mixed, lhs, weight, low_grads, turned, dmixed, go,
    t_own, t_in, tz_out, tz_in, t_total, ty_out, ty_in, tc_out, tc_in,
    f_own, f_in, fz_out, fz_in, f_total, f_other, fc_out, fc_in,
    grads, a1_out, a1_in, b1_out, b1_in, a2_out, a2_in, b2_out, b2_in, z_out, z_in,
    half_out, half_in, ready, core_out, core_in, sums, sum_out, sum_in, share_in,
    a1_send, a1_recv, b1_send, b1_recv, a2_send, a2_recv, b2_send, b2_recv, z_send, z_recv,
    h_send, h_recv, r_send, r_recv, c_send, c_recv, s_send, s_recv, p_send, p_recv, local,
    g_send, g_recv, tx_send, tx_recv, tz_send, tz_recv, ty_send, ty_recv, fy_send, fy_recv, fz_send, fz_recv, t_local, f_local, fetched,
):
    y, x, c, z = (lax.axis_index(name) for name in AXES)
    near_y, near_x, pair = (1 - y, x, c, z), (y, 1 - x, c, z), (y, x, 1 - c, z)
    own = std.shape[0]
    third = go.shape[1] // 4
    wide = 3 * third
    two = 2 * third
    slab = 128

    fetches = [
        pltpu.make_async_copy(src, dst, fetched.at[i])
        for i, (src, dst) in enumerate((
            (part_hbm, part), (next_hbm, std), (grad_hbm, base), (out_hbm, w_out), (joined_hbm, dj), (mixed_hbm, mixed),
            (lhs_hbm, lhs), (weight_hbm, weight), (feed_in_hbm, f_other),
        ))
    ]
    for copy in fetches:
        copy.start()
    fetch_std = pltpu.make_async_copy(std_hbm, std, fetched.at[9])

    barrier = pltpu.get_barrier_semaphore()
    for dc in range(2):
        for dz in range(4):
            if dc or dz:
                pl.semaphore_signal(barrier, inc=1, device_id=(y, x, (c + dc) % 2, (z + dz) % 4), device_id_type=MESH)
    for peer in (near_y, near_x):
        pl.semaphore_signal(barrier, inc=1, device_id=peer, device_id_type=MESH)
    pl.semaphore_wait(barrier, 9)

    def remote(src, dst, send, recv, peer):
        return pltpu.make_async_remote_copy(
            src_ref=src, dst_ref=dst, send_sem=send, recv_sem=recv, device_id=peer, device_id_type=MESH
        )

    def at(i, length):
        return pl.ds(pl.multiple_of(i * length, length), length)

    def along(r):
        return (y, x, c, (z + r) % 4)

    def time_x(yb):
        return remote(time_hbm.at[at(2 * yb + 1 - x, BLK)], t_in.at[yb], tx_send.at[yb], tx_recv.at[yb], near_x)

    def time_keep(yb):
        return pltpu.make_async_copy(time_hbm.at[at(2 * yb + x, BLK)], t_own.at[yb], t_local.at[yb])

    def time_z(r):
        return remote(tz_out.at[r], tz_in.at[r], tz_send.at[r], tz_recv.at[r], along(r))

    def feed_y(r):
        s = (z + r) % 4
        return remote(feed_hbm.at[1 - y, s], f_in.at[r], fy_send.at[r], fy_recv.at[r], near_y)

    def feed_keep(r):
        return pltpu.make_async_copy(feed_hbm.at[y, (z + r) % 4], f_own.at[r], f_local.at[r])

    def feed_z(r):
        return remote(fz_out.at[r], fz_in.at[r], fz_send.at[r], fz_recv.at[r], along(r))

    for r in (1, 2, 3, 0):
        feed_y(r).start()
        feed_keep(r).start()
    for yb in range(2):
        time_x(yb).start()
        time_keep(yb).start()

    def feed_step(r):
        feed_y(r).wait_recv()
        feed_keep(r).wait()
        total = f_own[r].astype(F32) + f_in[r].astype(F32)
        if r == 0:
            f_total[...] = total
        else:
            fz_out[r] = total.astype(BF16)
            feed_z(r).start()

    def time_step():
        for yb in range(2):
            time_x(yb).wait_recv()
            time_keep(yb).wait()
        for r in (1, 2, 3, 0):
            piece_at = at((z + r) % 4, BLK)
            for yb in range(2):
                total = t_own[yb, :, piece_at].astype(F32) + t_in[yb, :, piece_at].astype(F32)
                if r == 0:
                    t_total[yb] = total
                else:
                    tz_out[r, yb] = total.astype(BF16)
            if r:
                time_z(r).start()

    step = own // 2
    for copy in fetches[:3]:
        copy.wait()

    def norm_back(grad, standard, weights, inv):
        inner = grad * weights
        mean = jnp.mean(inner, axis=-1, keepdims=True)
        slope = jnp.mean(inner * standard, axis=-1, keepdims=True)
        return (inner - mean - standard * slope) * inv

    def after_time(i, total):
        rows = at(i, step)
        grad, standard = part[rows], std[rows]
        full = base[rows] + norm_back(grad, standard, gains[2:3], inverse_next[rows])
        base[rows] = full
        low_grads[rows] = full.astype(BF16)
        return total + jnp.sum(grad * standard, axis=0, keepdims=True)

    zero = jnp.zeros((1, std.shape[1]), F32)
    next_grad = lax.fori_loop(0, 2, after_time, zero)
    give = remote(low_grads.at[pl.ds(0, own)], low_grads.at[pl.ds(own, own)], g_send.at[0], g_recv.at[0], pair)
    give.start()
    fetch_std.start()
    for copy in fetches[3:6]:
        copy.wait()

    def attend(i, carry):
        rows = at(i, slab)
        for h in range(mixed.shape[1] // PAIR):
            places = [pl.ds((3 * h + j) * PAIR, PAIR) for j in range(3)]
            q, k, v = (dj[rows, place] for place in places)
            lines = [totals[i, 2 * h + j : 2 * h + j + 1, :] for j in range(2)]
            found = attend_pair_back(q, k, v, dmixed[rows, h * PAIR : (h + 1) * PAIR], lines, None, scale)
            for place, value in zip(places, found):
                dj[rows, place] = value.astype(BF16)
        return carry

    def turn(i, carry):
        turned[:, at(i, slab)] = low_grads[at(i, slab)].T
        return carry

    def attend_half(t, *between):
        rows = pl.ds(t * own, own)
        first, count = t * own // slab, own // slab
        dmixed[rows] = dot_nt(low_grads[rows], w_out[...]).astype(BF16)
        between[0]()
        lax.fori_loop(first, first + count // 2, attend, 0)
        between[1]()
        lax.fori_loop(first + count // 2, first + count, attend, 0)
        between[2]()
        lax.fori_loop(first, first + count, turn, 0)

    def nothing():
        pass

    attend_half(0, lambda: feed_step(1), lambda: feed_step(2), lambda: feed_step(3))
    give.wait_recv()
    attend_half(1, nothing, time_step, lambda: feed_step(0))
    for copy in fetches[6:]:
        copy.wait()
    def away(i, carry):
        rows = pl.ds(pl.multiple_of(own + i * step, step), step)
        half_out[pl.ds(pl.multiple_of(i * step, step), step)] = dot_nt(dj[rows], weight[...]).astype(BF16)
        return carry

    lax.fori_loop(0, 2, away, 0)
    swap = remote(half_out, half_in, h_send.at[0], h_recv.at[0], pair)
    swap.start()
    go[...] = dot_nn(turned[...], mixed[...]).astype(BF16)

    def block(yb, xb):
        return pl.ds(pl.multiple_of(BLK * (2 * yb + xb), BLK), BLK)

    def a1(i):
        return remote(a1_out.at[i], a1_in.at[i], a1_send.at[i], a1_recv.at[i], near_x)

    def b1(i):
        return remote(b1_out.at[i], b1_in.at[i], b1_send.at[i], b1_recv.at[i], near_y)

    def a2(i):
        return remote(a2_out.at[i], a2_in.at[i], a2_send.at[i], a2_recv.at[i], near_y)

    def b2(i):
        return remote(b2_out.at[i], b2_in.at[i], b2_send.at[i], b2_recv.at[i], near_x)

    def to_z(r):
        return remote(z_out.at[r], z_in.at[r], z_send.at[r], z_recv.at[r], along(r))

    def piece(i, carry):
        s = (z + i + 1) % 4
        made = dot_nn(lhs[...], dj[:, pl.ds(pl.multiple_of(s * wide, third), wide)])
        grads[i, :, :wide] = made
        grads[i, :, wide:] = go[:, pl.ds(pl.multiple_of(s * third, third), third)].astype(F32)
        for b in range(2):
            a1_out[i, b] = grads[i, block(b, 1 - x), :two].astype(BF16)
            b1_out[i, b] = grads[i, block(1 - y, b), two:].astype(BF16)
        a1(i).start()
        b1(i).start()
        return carry

    lax.fori_loop(0, 4, piece, 0)

    def second(i):
        a1(i).wait_recv()
        a2_out[i] = (grads[i, block(1 - y, x), :two] + a1_in[i, 1 - y].astype(F32)).astype(BF16)
        a2(i).start()
        b1(i).wait_recv()
        b2_out[i] = (grads[i, block(y, 1 - x), two:] + b1_in[i, 1 - x].astype(F32)).astype(BF16)
        b2(i).start()
        grads[i, block(y, x), :two] = grads[i, block(y, x), :two] + a1_in[i, y].astype(F32)
        grads[i, block(y, x), two:] = grads[i, block(y, x), two:] + b1_in[i, x].astype(F32)

    def third_step(i):
        a2(i).wait_recv()
        b2(i).wait_recv()
        grads[i, block(y, x), :two] = grads[i, block(y, x), :two] + a2_in[i].astype(F32)
        grads[i, block(y, x), two:] = grads[i, block(y, x), two:] + b2_in[i].astype(F32)
        if i < 3:
            z_out[i + 1] = grads[i, block(y, x), :].astype(BF16)
            to_z(i + 1).start()

    second(0)
    fetch_std.wait()
    sums[...] = jnp.zeros_like(sums)
    sums[1:2] = next_grad
    sums[2:3] = later_grad[...]
    swap.wait_recv()

    def home(i, totals):
        rows = pl.ds(pl.multiple_of(i * step, step), step)
        grad = dot_nt(dj[rows], weight[...]) + half_in[rows].astype(F32)
        standard = std[rows]
        full = base[rows] + norm_back(grad, standard, gains[1:2], inverse[rows])
        hide = masked[rows] > 0.0
        ready[rows] = jnp.where(hide, 0.0, full).astype(BF16)
        return (
            totals[0] + jnp.sum(grad * standard, axis=0, keepdims=True),
            totals[1] + jnp.sum(jnp.where(hide, full, 0.0), axis=0, keepdims=True),
        )

    gain_grad, embed_grad = lax.fori_loop(0, 2, home, (zero, zero))
    sums[0:1] = gain_grad
    sums[3:4] = embed_grad

    def columns(s):
        return pl.ds(pl.multiple_of(s * BLK, BLK), BLK)

    def stays(k):
        return jnp.logical_and(z == k, z // 2 == c)

    def ride(k):
        slot = 2 * (z % 2) + c
        return remote(ready.at[:, columns(k)], rows_in.at[slot], r_send.at[k], r_recv.at[slot], (y, x, z // 2, k))

    def ride_local(k):
        return pltpu.make_async_copy(ready.at[:, columns(k)], rows_in.at[2 * (z % 2) + c], local.at[3])

    for k in range(4):
        pl.when(stays(k))(lambda k=k: ride_local(k).start())
        pl.when(jnp.logical_not(stays(k)))(lambda k=k: ride(k).start())

    def share(h):
        peer = (pair, near_y, near_x)[h]
        return remote(sum_out.at[h], sum_in.at[h], s_send.at[h], s_recv.at[h], peer)

    def begin_share(h):
        sum_out[h] = sums[...]
        share(h).start()

    def end_share(h):
        share(h).wait_recv()
        sums[...] = sums[...] + sum_in[h]

    begin_share(0)
    second(1)
    third_step(0)
    end_share(0)
    begin_share(1)
    second(2)
    third_step(1)
    end_share(1)
    begin_share(2)
    second(3)
    third_step(2)
    end_share(2)
    sum_out[3] = sums[...]

    def deal(r):
        s = (z + r) % 4
        return remote(sum_out.at[3, :, columns(s)], share_in.at[r], p_send.at[r], p_recv.at[r], (y, x, c, s))

    for r in (1, 2, 3):
        deal(r).start()
    third_step(3)
    parity = BLK // 2

    for r in (1, 2, 3):
        time_z(r).wait_recv()
        t_total[...] = t_total[...] + tz_in[r].astype(F32)
    ty_out[...] = t_total[1 - y].astype(BF16)
    swap_y = remote(ty_out, ty_in, ty_send.at[0], ty_recv.at[0], near_y)
    swap_y.start()
    for r in (1, 2, 3):
        feed_z(r).wait_recv()
        f_total[...] = f_total[...] + fz_in[r].astype(F32)
    fc_out[0] = f_other[at(1 - c, parity)].astype(BF16)
    fc_out[1] = f_total[at(1 - c, parity)].astype(BF16)
    swap_feed = remote(fc_out, fc_in, c_send.at[1], c_recv.at[1], pair)
    swap_feed.start()
    units = f_total.shape[1]
    feed_in_out[:, at(c, units)] = f_other[at(c, parity)]
    feed_out_out[at(c, units)] = f_total[at(c, parity)].T
    swap_y.wait_recv()
    tc_out[0] = t_total[y, at(1 - c, parity)].astype(BF16)
    tc_out[1] = ty_in[at(1 - c, parity)]
    swap_time = remote(tc_out, tc_in, c_send.at[2], c_recv.at[2], pair)
    swap_time.start()
    for k in range(4):
        pl.when(stays(k))(lambda k=k: ride_local(k).wait())
        from_self = jnp.logical_and(2 * c + k // 2 == z, c == k % 2)

        def landed(k=k):
            remote(ready.at[:, columns(k)], rows_in.at[k], r_send.at[k], r_recv.at[k], near_y).wait_recv()

        pl.when(jnp.logical_not(from_self))(landed)
    rows_out[...] = rows_in[...].astype(F32)
    for r in (1, 2, 3):
        to_z(r).wait_recv()
    total = grads[3, block(y, x), :]
    for r in (1, 2, 3):
        total = total + z_in[r].astype(F32)
    grads[3, block(y, x), :] = total
    rows = BLK // 2

    def core_rows(core):
        return pl.ds(pl.multiple_of(BLK * (2 * y + x) + rows * core, rows), rows)

    core_out[...] = grads[3, core_rows(1 - c), :].astype(BF16)
    last = remote(core_out, core_in, c_send.at[0], c_recv.at[0], pair)
    last.start()
    def place(core, value):
        for j in range(3):
            space_qkv[j, :, at(core, third)] = value[:, j * third : (j + 1) * third]
        space_out[at(core, third)] = value[:, 3 * third :].T

    place(c, grads[3, core_rows(c), :])
    result = sums[:, columns(z)]
    for r in (1, 2, 3):
        deal(r).wait_recv()
        result = result + share_in[r]
    small_out[...] = result
    swap_feed.wait_recv()
    feed_in_out[:, at(1 - c, units)] = fc_in[0].astype(F32)
    feed_out_out[at(1 - c, units)] = fc_in[1].astype(F32).T
    swap_time.wait_recv()
    mine = (t_total[y, at(c, parity)], ty_in[at(c, parity)].astype(F32))
    other = (tc_in[0].astype(F32), tc_in[1].astype(F32))
    by_head = []
    for yb in range(2):
        for cb in range(2):
            by_head.append(
                jnp.where(
                    c == cb,
                    jnp.where(y == yb, mine[0], mine[1]),
                    jnp.where(y == yb, other[0], other[1]),
                )
            )
    for j in range(4):
        made = jnp.concatenate([v[:, j * HEAD_DIM : (j + 1) * HEAD_DIM] for v in by_head], axis=1)
        if j < 3:
            time_qkv[j] = made
        else:
            time_out[...] = made.T
    last.wait_recv()
    place(1 - c, core_in[...].astype(F32))

    for copy in (last, swap, give, swap_y, swap_feed, swap_time):
        copy.wait_send()
    for yb in range(2):
        time_x(yb).wait_send()
    for r in range(4):
        feed_y(r).wait_send()
    for r in (1, 2, 3):
        time_z(r).wait_send()
        feed_z(r).wait_send()
    for i in range(4):
        for copy in (a1(i), b1(i), a2(i), b2(i)):
            copy.wait_send()
    for r in (1, 2, 3):
        to_z(r).wait_send()
        deal(r).wait_send()
    for h in range(3):
        share(h).wait_send()
    for k in range(4):
        pl.when(jnp.logical_not(stays(k)))(lambda k=k: ride(k).wait_send())


def leave(
    part, std_next, grad, w_out, joined, mixed, lhs, weight, std, g_time, g_out, g_in,
    totals, inverse_next, inverse, masked, gains, later_grad, scale,
):
    own, features = std.shape
    cols4 = mixed.shape[1]
    quarter = cols4 // 4
    units = g_in.shape[1]
    dma = pltpu.SemaphoreType.DMA
    anywhere = pl.BlockSpec(memory_space=pl.ANY)
    whole = pl.BlockSpec(memory_space=pltpu.VMEM)
    parity = BLK // 2

    def low(*shape):
        return pltpu.VMEM(shape, BF16)

    def high(*shape):
        return pltpu.VMEM(shape, F32)

    return pl.pallas_call(
        functools.partial(leave_kernel, scale),
        in_specs=[anywhere] * 12 + [whole] * 6,
        out_specs=[whole] * 8,
        out_shape=[
            jax.ShapeDtypeStruct(shape, F32)
            for shape in (
                (3, parity, 2 * quarter), (2 * quarter, parity), (parity, 2 * units), (2 * units, parity),
                (3, parity, BLK), (BLK, parity), (4, own, BLK), (8, BLK),
            )
        ],
        scratch_shapes=[
            low(4, own, BLK),
            high(own, features), high(own, features), high(own, features), low(*w_out.shape), low(*joined.shape),
            low(*mixed.shape), low(*lhs.shape), low(*weight.shape), low(2 * own, features), low(features, 2 * own),
            low(*mixed.shape), low(features, cols4),
            low(2, BLK, features), low(2, BLK, features), low(4, 2, BLK, BLK), low(4, 2, BLK, BLK), high(2, BLK, BLK),
            low(BLK, BLK), low(BLK, BLK), low(2, parity, BLK), low(2, parity, BLK),
            low(4, BLK, units), low(4, BLK, units), low(4, BLK, units), low(4, BLK, units),
            high(BLK, units), high(BLK, units), low(2, parity, units), low(2, parity, units),
            high(4, features, cols4),
            low(4, 2, BLK, 2 * quarter), low(4, 2, BLK, 2 * quarter), low(4, 2, BLK, 2 * quarter), low(4, 2, BLK, 2 * quarter),
            low(4, BLK, 2 * quarter), low(4, BLK, 2 * quarter), low(4, BLK, 2 * quarter), low(4, BLK, 2 * quarter),
            low(4, BLK, cols4), low(4, BLK, cols4),
            low(own, features), low(own, features), low(own, features),
            low(parity, cols4), low(parity, cols4),
            high(8, features), high(4, 8, features), high(3, 8, features), high(4, 8, BLK),
        ]
        + [dma((4,))] * 10
        + [dma((1,)), dma((1,)), dma((4,)), dma((4,)), dma((3,)), dma((3,)), dma((3,)), dma((3,)), dma((4,)), dma((4,)), dma((4,))]
        + [dma((1,)), dma((1,)), dma((2,)), dma((2,)), dma((4,)), dma((4,)), dma((1,)), dma((1,))]
        + [dma((4,)), dma((4,)), dma((4,)), dma((4,)), dma((2,)), dma((4,)), dma((10,))],
        compiler_params=pltpu.CompilerParams(
            collective_id=3, has_side_effects=True, vmem_limit_bytes=62 * 1024 * 1024
        ),
        cost_estimate=pl.CostEstimate(flops=2 * 10**10, transcendentals=10**6, bytes_accessed=10**8),
        name="leave",
    )(
        part, std_next, grad, w_out, joined, mixed, lhs, weight, std, g_time, g_out, g_in,
        totals, inverse_next, inverse, masked, gains, later_grad,
    )


def tie(*values):
    return lax.optimization_barrier(values)


def norm_rows(resid):
    mean = jnp.mean(resid, axis=-1, keepdims=True)
    centered = resid - mean
    inverse = lax.rsqrt(jnp.mean(centered * centered, axis=-1, keepdims=True) + eps_norm)
    return (centered * inverse, inverse)


def norm_rows_back(grad, standardized, inverse, gain):
    gain_grad = jnp.sum(grad * standardized, axis=0)
    inner = grad * gain
    mean = jnp.mean(inner, axis=-1, keepdims=True)
    along = jnp.mean(inner * standardized, axis=-1, keepdims=True)
    return ((inner - mean - standardized * along) * inverse, gain_grad)


def cols(parts):
    return jnp.concatenate(parts, axis=1)


def rows_of(parts):
    return jnp.concatenate(parts, axis=0)


def token_parallel(
    tokens,
    cotangent,
    ratio,
    priority,
    frame_order,
    mask_embed,
    gains,
    qkv_space,
    out_space,
    qkv_time,
    out_time,
    w_in,
    w_out,
):
    scale = 1.0 / math.sqrt(HEAD_DIM)
    y, x, c, z = (lax.axis_index(name) for name in AXES)
    patches = tokens.shape[2]
    width = qkv_space.shape[0]
    frames_own = tokens.shape[0] * tokens.shape[1] // 4
    frames_all = frame_order.shape[1]
    own = frames_own * patches
    hidden_own = w_in.shape[1] // 2
    plane = 2 * y + x
    k_own = 2 * (z % 2) + c

    masked_here = (priority < ratio[:, None, None]).astype(jnp.int32).reshape(2, -1)
    info = cols([masked_here, frame_order])
    info = jnp.where(z // 2 == c, info, hop_c(info))
    info = lax.dynamic_index_in_dim(info, z % 2, 0, keepdims=False)
    masked = lax.dynamic_slice_in_dim(info, c * own, own, 0)[:, None] != 0
    order = info[2 * own :].reshape(2, 2, frames_own)
    order = jnp.where(y == 1, order[::-1], order)
    order = jnp.where(c == 1, order[:, ::-1], order).swapaxes(0, 1).reshape(frames_all)
    order = jnp.repeat(order, GROUP)
    patch = jnp.arange(frames_all * GROUP) % GROUP
    visible = (order[:, None] <= order[None, :]) & (patch[:, None] == patch[None, :])
    bias = jnp.where(visible, 0.0, -1e30).astype(F32)

    vectors = rows_of([mask_embed[None], gains, jnp.zeros((4, BLK), BF16)])
    head = (2 * y + c) * HEAD_DIM
    ti_own = cols(
        [
            lax.dynamic_slice_in_dim(qkv_time, head, HEAD_DIM, 2).reshape(width, -1),
            lax.dynamic_slice_in_dim(out_time, head, HEAD_DIM, 0).T,
        ]
    )
    (
        ws_qkv, ws_out, wt_all, wf_out, wf_in, joined0, turned0, std0,
        mixed0, total0, inv0, resid1, std1, inv1, normed1, vectors,
    ) = enter(
        tokens.reshape(4, own, BLK),
        vectors,
        jnp.swapaxes(qkv_space, 0, 1),
        out_space,
        ti_own,
        w_out,
        w_in,
        masked.astype(F32),
        scale,
    )

    half = qkv_space.shape[2] // 2
    turned1, joined1, mixed1, total1, delta, upstream, wf_far, wf_in_far = time_call(
        False,
        normed1.reshape(frames_own, patches, width),
        cotangent.reshape(4, own, BLK),
        [wf_out, wf_in],
        wt_all,
        bias,
        scale,
    )
    w_in_half, w_out_half, grad2, grad2_low, block_rows, gain_grad2 = feed(
        resid1, delta.reshape(own, width), upstream, masked.astype(F32), vectors, wf_in, wf_in_far, wf_out, wf_far
    )

    part1, g_time, g_w_in, block_out = time_call(
        True,
        grad2_low.reshape(frames_own, patches, width),
        block_rows,
        [joined1, total1, w_in_half, turned1, mixed1],
        wt_all,
        bias,
        scale,
    )
    block_out = block_out.reshape(tokens.shape)
    grad_qkv_space, grad_out_space, grad_w_in, grad_w_out, grad_qkv_time, grad_out_time, grad_tokens, small = leave(
        part1.reshape(own, width), std1, grad2, ws_out, joined0, mixed0, turned0, ws_qkv, std0, g_time, w_out_half, g_w_in,
        total0, inv1, inv0, masked.astype(F32), vectors, gain_grad2, scale,
    )
    small = small[:4]
    return (
        block_out,
        grad_tokens.reshape(tokens.shape),
        small[3],
        small[:3],
        jnp.swapaxes(grad_qkv_space, 0, 1),
        grad_out_space,
        jnp.swapaxes(grad_qkv_time, 0, 1),
        grad_out_time,
        grad_w_in,
        grad_w_out,
    )


def solution(mesh):
    sizes = (mesh.shape["tm"], mesh.shape["clip"], mesh.shape["mp"])
    if sizes == (2, 4, 4):
        mesh = jax.sharding.Mesh(mesh.devices.reshape(2, 2, 2, 4), AXES)
        step, clip = token_parallel, ("x", "c")
    else:
        step, clip = shards, ("clip",)
    return jax.shard_map(
        step,
        mesh=mesh,
        in_specs=(
            P(clip, "tm", None, "mp"),
            P(clip, "tm", None, "mp"),
            P(clip),
            P(clip, "tm", None),
            P(clip, None),
            P("mp"),
            P(None, "mp"),
            P(None, None, "mp"),
            P("mp", None),
            P(None, None, "mp"),
            P("mp", None),
            P(None, "mp"),
            P("mp", None),
        ),
        out_specs=(
            P(clip, "tm", None, "mp"),
            P(clip, "tm", None, "mp"),
            P("mp"),
            P(None, "mp"),
            P(("tm",) + clip, None, "mp"),
            P("mp", ("tm",) + clip),
            P(("tm",) + clip, None, "mp"),
            P("mp", ("tm",) + clip),
            P(("tm",) + clip, "mp"),
            P("mp", ("tm",) + clip),
        ),
        check_vma=False,
    )
```

```python
import functools
import math

import jax
import jax.numpy as jnp
from jax import lax
from jax.experimental import pallas as pl
from jax.experimental.pallas import tpu as pltpu
from jax.sharding import PartitionSpec as P

HEAD_DIM = 64
MICRO = 2


eps_norm = 1e-05


def gelu_tanh(values):
    return jax.nn.gelu(values, approximate=True)


def norm_forward_pass(residual_stream, gain_coefficients, complete_width):
    reduced_totals = lax.psum(
        (jnp.sum(residual_stream, axis=-1), jnp.sum(residual_stream * residual_stream, axis=-1)),
        "mp",
    )
    centered_rows = reduced_totals[0] / complete_width
    spread = reduced_totals[1] / complete_width - centered_rows * centered_rows
    inverse_scale = lax.rsqrt(spread + eps_norm)
    standardized_rows = (residual_stream - centered_rows[:, None]) * inverse_scale[:, None]
    shard_rows = (standardized_rows * gain_coefficients).astype(jnp.bfloat16)
    normalized_rows = lax.all_gather(shard_rows, "mp", axis=1, tiled=True)
    return (normalized_rows, standardized_rows, inverse_scale)


def norm_reverse_pass(
    normalized_gradient, standardized_rows, inverse_scale, gain_coefficients, complete_width
):
    gain_gradient = jnp.sum(normalized_gradient * standardized_rows, axis=0)
    standardized_gradient = normalized_gradient * gain_coefficients
    reduced_totals = lax.psum(
        (
            jnp.sum(standardized_gradient, axis=-1),
            jnp.sum(standardized_gradient * standardized_rows, axis=-1),
        ),
        "mp",
    )
    grad_resid = (
        standardized_gradient
        - reduced_totals[0][:, None] / complete_width
        - standardized_rows * (reduced_totals[1][:, None] / complete_width)
    ) * inverse_scale[:, None]
    return (grad_resid, gain_gradient)


def sum_features(grad_full):
    return lax.psum_scatter(
        grad_full.astype(jnp.bfloat16), "mp", scatter_dimension=1, tiled=True
    ).astype(jnp.float32)


def branch_out(hidden, weight):
    partial_rows = jnp.dot(hidden, weight, preferred_element_type=jnp.float32)
    return lax.psum_scatter(partial_rows, "mp", scatter_dimension=1, tiled=True)


def branch_back(grad_resid, hidden, weight):
    grad_rows = lax.all_gather(grad_resid.astype(jnp.bfloat16), "mp", axis=1, tiled=True)
    weight_grad = jnp.einsum("rk,rd->kd", hidden, grad_rows, preferred_element_type=jnp.float32)
    grad_hidden = jnp.einsum("rd,kd->rk", grad_rows, weight, preferred_element_type=jnp.float32)
    return (grad_hidden, weight_grad)


def qkv_back(normalized_rows, grad_joined, weight):
    weight_grad = jnp.einsum(
        "rd,trk->dtk", normalized_rows, grad_joined, preferred_element_type=jnp.float32
    )
    grad_full = jnp.einsum("trk,dtk->rd", grad_joined, weight, preferred_element_type=jnp.float32)
    return (weight_grad, sum_features(grad_full))


def reduce_grads(local_grads, small_grads):
    reduced = (
        lax.psum_scatter(local_grads[0], ("tm", "clip"), scatter_dimension=0, tiled=True),
        lax.psum_scatter(local_grads[1], ("tm", "clip"), scatter_dimension=1, tiled=True),
        lax.psum_scatter(local_grads[2], ("tm", "clip"), scatter_dimension=0, tiled=True),
        lax.psum_scatter(local_grads[3], ("tm", "clip"), scatter_dimension=1, tiled=True),
        lax.psum_scatter(local_grads[4], ("tm", "clip"), scatter_dimension=0, tiled=True),
        lax.psum_scatter(local_grads[5], ("tm", "clip"), scatter_dimension=1, tiled=True),
    )
    reduced_small = lax.psum((small_grads[0], small_grads[1]), ("tm", "clip"))
    return (reduced, reduced_small)


def space_forward(normalized_rows, weight, frame_count, patches, heads_local, scale):
    joined = jnp.einsum(
        "rd,dtk->trk", normalized_rows, weight, preferred_element_type=jnp.float32
    ).astype(jnp.bfloat16)
    shape_heads = (frame_count, patches, heads_local, HEAD_DIM)
    scores = (
        jnp.einsum(
            "bshd,bthd->bhst",
            joined[0].reshape(shape_heads),
            joined[1].reshape(shape_heads),
            preferred_element_type=jnp.float32,
        )
        * scale
    )
    highest = jnp.max(scores, axis=-1, keepdims=True)
    exponent = jnp.exp(scores - highest)
    reduced_totals = jnp.sum(exponent, axis=-1, keepdims=True)
    log_total = highest + jnp.log(reduced_totals)
    attention = (exponent / reduced_totals).astype(jnp.bfloat16)
    mixed = jnp.einsum(
        "bhst,bthd->bshd",
        attention,
        joined[2].reshape(shape_heads),
        preferred_element_type=jnp.float32,
    )
    return (
        joined,
        log_total,
        mixed.astype(jnp.bfloat16).reshape(frame_count * patches, heads_local * HEAD_DIM),
    )


def space_backward(grad_mixed, joined, log_total, frame_count, patches, heads_local, scale):
    shape_heads = (frame_count, patches, heads_local, HEAD_DIM)
    queries = joined[0].reshape(shape_heads)
    key_rows = joined[1].reshape(shape_heads)
    values = joined[2].reshape(shape_heads)
    grad_out = grad_mixed.reshape(shape_heads)
    scores = (
        jnp.einsum("bshd,bthd->bhst", queries, key_rows, preferred_element_type=jnp.float32) * scale
    )
    attention = jnp.exp(scores - log_total)
    grad_values = jnp.einsum(
        "bhst,bshd->bthd",
        attention.astype(jnp.bfloat16),
        grad_out,
        preferred_element_type=jnp.float32,
    )
    grad_att = jnp.einsum("bshd,bthd->bhst", grad_out, values, preferred_element_type=jnp.float32)
    grad_scores = (
        attention * (grad_att - jnp.sum(attention * grad_att, axis=-1, keepdims=True))
    ).astype(jnp.bfloat16)
    grad_queries = (
        jnp.einsum("bhst,bthd->bshd", grad_scores, key_rows, preferred_element_type=jnp.float32)
        * scale
    )
    grad_keys = (
        jnp.einsum("bhst,bshd->bthd", grad_scores, queries, preferred_element_type=jnp.float32)
        * scale
    )
    row_count = frame_count * patches
    stacked = jnp.stack(
        [
            grad_queries.reshape(row_count, -1),
            grad_keys.reshape(row_count, -1),
            grad_values.reshape(row_count, -1),
        ]
    )
    return stacked.astype(jnp.bfloat16)


def time_scores(queries, keys_all, visible, scale):
    scores = (
        jnp.einsum("cfshd,cgshd->chfgs", queries, keys_all, preferred_element_type=jnp.float32)
        * scale
    )
    return jnp.where(visible, scores, -1e30)


def time_forward(queries, keys_all, values_all, visible, scale):
    scores = time_scores(queries, keys_all, visible, scale)
    highest = jnp.max(scores, axis=3, keepdims=True)
    exponent = jnp.exp(scores - highest)
    reduced_totals = jnp.sum(exponent, axis=3, keepdims=True)
    log_total = highest + jnp.log(reduced_totals)
    attention = (exponent / reduced_totals).astype(jnp.bfloat16)
    mixed = jnp.einsum(
        "chfgs,cgshd->cfshd", attention, values_all, preferred_element_type=jnp.float32
    )
    return (log_total, mixed.astype(jnp.bfloat16))


def time_backward(grad_mixed, queries, keys_all, values_all, visible, log_total, scale):
    grad_out = grad_mixed.reshape(queries.shape)
    scores = time_scores(queries, keys_all, visible, scale)
    attention = jnp.exp(scores - log_total)
    grad_values = jnp.einsum(
        "chfgs,cfshd->cgshd",
        attention.astype(jnp.bfloat16),
        grad_out,
        preferred_element_type=jnp.float32,
    )
    grad_att = jnp.einsum(
        "cfshd,cgshd->chfgs", grad_out, values_all, preferred_element_type=jnp.float32
    )
    grad_scores = (
        attention * (grad_att - jnp.sum(attention * grad_att, axis=3, keepdims=True))
    ).astype(jnp.bfloat16)
    grad_queries = (
        jnp.einsum("chfgs,cgshd->cfshd", grad_scores, keys_all, preferred_element_type=jnp.float32)
        * scale
    )
    grad_keys = (
        jnp.einsum("chfgs,cfshd->cgshd", grad_scores, queries, preferred_element_type=jnp.float32)
        * scale
    )
    return (grad_queries, grad_keys, grad_values)


def shards(
    tokens,
    cotangent,
    ratio,
    priority,
    frame_order,
    mask_embed,
    gains,
    qkv_space,
    out_space,
    qkv_time,
    out_time,
    w_in,
    w_out,
):
    scale = 1.0 / math.sqrt(HEAD_DIM)
    clips_local = tokens.shape[0] // MICRO
    frames_local = tokens.shape[1]
    patches = tokens.shape[2]
    cols_local = tokens.shape[3]
    frames_all = frame_order.shape[1]
    hidden_width = qkv_space.shape[0]
    joined_local = qkv_space.shape[2]
    heads_local = joined_local // HEAD_DIM
    row_count = clips_local * frames_local * patches
    gain_broadcast = gains.astype(jnp.float32)
    embed_row = mask_embed.astype(jnp.float32)
    first_frame = lax.axis_index("tm") * frames_local
    shape_local = (clips_local, frames_local, patches, joined_local)
    shape_heads = (clips_local, frames_local, patches, heads_local, HEAD_DIM)
    shape_all = (clips_local, frames_all, patches, heads_local, HEAD_DIM)
    outputs = []
    input_grads = []
    weight_total = None
    small_total = None
    for batch_index in range(MICRO):
        lower = batch_index * clips_local
        upper = lower + clips_local
        source = tokens[lower:upper].reshape(row_count, cols_local).astype(jnp.float32)
        upstream = cotangent[lower:upper].reshape(row_count, cols_local).astype(jnp.float32)
        masked = (priority[lower:upper] < ratio[lower:upper][:, None, None]).reshape(row_count)
        order_rows = frame_order[lower:upper]
        residual_stream0 = jnp.where(masked[:, None], embed_row[None, :], source)
        normalized_rows0, standardized_rows0, inverse_deviation0 = norm_forward_pass(
            residual_stream0, gain_broadcast[0], hidden_width
        )
        joined0, total0, mixed0 = space_forward(
            normalized_rows0, qkv_space, clips_local * frames_local, patches, heads_local, scale
        )
        residual_stream1 = residual_stream0 + branch_out(mixed0, out_space)
        normalized_rows1, standardized_rows1, inverse_deviation1 = norm_forward_pass(
            residual_stream1, gain_broadcast[1], hidden_width
        )
        joined1 = jnp.einsum(
            "rd,dtk->trk", normalized_rows1, qkv_time, preferred_element_type=jnp.float32
        ).astype(jnp.bfloat16)
        queries_local = joined1[0].reshape(shape_local)
        keys_local = joined1[1].reshape(shape_local)
        values_local = joined1[2].reshape(shape_local)
        keys_all, values_all = (
            lax.all_gather(keys_local, "tm", axis=1, tiled=True),
            lax.all_gather(values_local, "tm", axis=1, tiled=True),
        )
        query_order = lax.dynamic_slice_in_dim(order_rows, first_frame, frames_local, axis=1)
        time_visible = (order_rows[:, None, :] <= query_order[:, :, None])[:, None, :, :, None]
        time_q = queries_local.reshape(shape_heads)
        time_k = keys_all.reshape(shape_all)
        time_v = values_all.reshape(shape_all)
        total1, mixed_frames = time_forward(time_q, time_k, time_v, time_visible, scale)
        mixed1 = mixed_frames.reshape(row_count, joined_local)
        residual_stream2 = residual_stream1 + branch_out(mixed1, out_time)
        normalized_rows2, standardized_rows2, inverse_deviation2 = norm_forward_pass(
            residual_stream2, gain_broadcast[2], hidden_width
        )
        projected = jnp.dot(normalized_rows2, w_in, preferred_element_type=jnp.float32)
        activated, gelu_pull = jax.vjp(gelu_tanh, projected)
        hidden = activated.astype(jnp.bfloat16)
        resid3 = residual_stream2 + branch_out(hidden, w_out)
        outputs.append(
            resid3.astype(jnp.bfloat16).reshape(clips_local, frames_local, patches, cols_local)
        )
        grad3 = jnp.where(masked[:, None], upstream, 0.0)
        grad_hidden, grad_w_out = branch_back(grad3, hidden, w_out)
        grad_inner = gelu_pull(grad_hidden)[0].astype(jnp.bfloat16)
        grad_w_in = jnp.einsum(
            "rd,rk->dk", normalized_rows2, grad_inner, preferred_element_type=jnp.float32
        )
        normalized_gradient2 = sum_features(
            jnp.einsum("rk,dk->rd", grad_inner, w_in, preferred_element_type=jnp.float32)
        )
        backward_third, gain_gradient2 = norm_reverse_pass(
            normalized_gradient2,
            standardized_rows2,
            inverse_deviation2,
            gain_broadcast[2],
            hidden_width,
        )
        grad2 = grad3 + backward_third
        grad_mixed1, grad_out_time = branch_back(grad2, mixed1, out_time)
        grad_mixed_low = grad_mixed1.astype(jnp.bfloat16).reshape(shape_local)
        grad_queries, grad_keys, grad_values = time_backward(
            grad_mixed_low, time_q, time_k, time_v, time_visible, total1, scale
        )
        key_part, value_part = (
            lax.psum_scatter(
                grad_keys.reshape(clips_local, frames_all, patches, joined_local).astype(
                    jnp.bfloat16
                ),
                "tm",
                scatter_dimension=1,
                tiled=True,
            ).astype(jnp.float32),
            lax.psum_scatter(
                grad_values.reshape(clips_local, frames_all, patches, joined_local).astype(
                    jnp.bfloat16
                ),
                "tm",
                scatter_dimension=1,
                tiled=True,
            ).astype(jnp.float32),
        )
        grad_joined1 = jnp.stack(
            [
                grad_queries.reshape(row_count, joined_local),
                key_part.reshape(row_count, joined_local),
                value_part.reshape(row_count, joined_local),
            ]
        ).astype(jnp.bfloat16)
        grad_qkv_time, normalized_gradient1 = qkv_back(normalized_rows1, grad_joined1, qkv_time)
        backward_second, gain_gradient1 = norm_reverse_pass(
            normalized_gradient1,
            standardized_rows1,
            inverse_deviation1,
            gain_broadcast[1],
            hidden_width,
        )
        grad1 = grad2 + backward_second
        grad_mixed0, grad_out_space = branch_back(grad1, mixed0, out_space)
        grad_joined0 = space_backward(
            grad_mixed0.astype(jnp.bfloat16),
            joined0,
            total0,
            clips_local * frames_local,
            patches,
            heads_local,
            scale,
        )
        grad_qkv_space, normalized_gradient0 = qkv_back(normalized_rows0, grad_joined0, qkv_space)
        backward_first, gain_gradient0 = norm_reverse_pass(
            normalized_gradient0,
            standardized_rows0,
            inverse_deviation0,
            gain_broadcast[0],
            hidden_width,
        )
        grad0 = grad1 + backward_first
        input_grads.append(
            jnp.where(masked[:, None], 0.0, grad0).reshape(
                clips_local, frames_local, patches, cols_local
            )
        )
        grad_embed = jnp.sum(jnp.where(masked[:, None], grad0, 0.0), axis=0)
        gain_grads = jnp.stack([gain_gradient0, gain_gradient1, gain_gradient2])
        local_grads = (
            grad_qkv_space,
            grad_out_space,
            grad_qkv_time,
            grad_out_time,
            grad_w_in,
            grad_w_out,
        )
        small_grads = (gain_grads, grad_embed)
        reduced, reduced_small = reduce_grads(local_grads, small_grads)
        if weight_total is None:
            weight_total = reduced
            small_total = reduced_small
        else:
            weight_total = tuple((total + grad for total, grad in zip(weight_total, reduced)))
            small_total = tuple((total + grad for total, grad in zip(small_total, reduced_small)))
    return (
        jnp.concatenate(outputs, axis=0),
        jnp.concatenate(input_grads, axis=0),
        small_total[1],
        small_total[0],
        weight_total[0],
        weight_total[1],
        weight_total[2],
        weight_total[3],
        weight_total[4],
        weight_total[5],
    )


AXES = ("tm", "x", "c", "mp")
F32 = jnp.float32
BF16 = jnp.bfloat16
BLK = 256
MESH = pl.DeviceIdType.MESH


def device_pairs(move):
    pairs = []
    for y in range(2):
        for x in range(2):
            for c in range(2):
                for z in range(4):
                    there = move(y, x, c, z)
                    pairs.append(tuple(((q[0] * 2 + q[1]) * 2 + q[2]) * 4 + q[3] for q in ((y, x, c, z), there)))
    return pairs


def hop_y(v):
    return lax.ppermute(v, AXES, device_pairs(lambda y, x, c, z: (1 - y, x, c, z)))


def hop_x(v):
    return lax.ppermute(v, AXES, device_pairs(lambda y, x, c, z: (y, 1 - x, c, z)))


def hop_c(v):
    return lax.ppermute(v, AXES, device_pairs(lambda y, x, c, z: (y, x, 1 - c, z)))


def hop_z(v, shift):
    return lax.ppermute(v, AXES, device_pairs(lambda y, x, c, z: (y, x, c, (z + shift) % 4)))


def spread_pairs(r):
    def move(y, x, c, z):
        k = z ^ r
        return (y, x, k & 1, 2 * c + (k >> 1))

    return device_pairs(move)


def dot_nn(a, b):
    return lax.dot_general(a, b, (((1,), (0,)), ((), ())), preferred_element_type=F32)


def dot_nt(a, b):
    return lax.dot_general(a, b, (((1,), (1,)), ((), ())), preferred_element_type=F32)


def dot_tn(a, b):
    return lax.dot_general(a, b, (((0,), (0,)), ((), ())), preferred_element_type=F32)


def attend_pair(q, k, v, bias, scale):
    mixed, totals = [], []
    for i in range(2):
        mine = slice(i * HEAD_DIM, (i + 1) * HEAD_DIM)
        scores = dot_nt(k[:, mine], q[:, mine]) * scale
        if bias is not None:
            scores = scores + bias
        highest = jnp.max(scores, axis=0, keepdims=True)
        exponent = jnp.exp(scores - highest)
        total = jnp.sum(exponent, axis=0, keepdims=True)
        totals.append(highest + jnp.log(total))
        mixed.append(dot_tn(v[:, mine], exponent.astype(BF16)) * (1.0 / total))
    return (jnp.concatenate(mixed, axis=0).T, totals)


def attend_pair_back(q, k, v, g, totals, bias, scale):
    grads = ([], [], [])
    for i in range(2):
        mine = slice(i * HEAD_DIM, (i + 1) * HEAD_DIM)
        scores = dot_nt(k[:, mine], q[:, mine]) * scale
        if bias is not None:
            scores = scores + bias
        p = jnp.exp(scores - totals[i])
        dp = dot_nt(v[:, mine], g[:, mine])
        ds = (p * (dp - jnp.sum(p * dp, axis=0, keepdims=True))).astype(BF16)
        grads[0].append(dot_tn(k[:, mine], ds) * scale)
        grads[1].append(dot_nn(ds, q[:, mine]) * scale)
        grads[2].append(dot_nn(p.astype(BF16), g[:, mine]))
    return (
        jnp.concatenate(grads[0], axis=0).T,
        jnp.concatenate(grads[1], axis=1),
        jnp.concatenate(grads[2], axis=1),
    )


PAIR = 2 * HEAD_DIM


def enter_kernel(
    scale,
    tok, vec, qkv_hbm, out_hbm, later, feed_hbm, first_hbm, masked,
    wq_out, wo_out, wt, wf, wi, joined_out, turned_out, std_out,
    mixed, total_out, inverse, resid_out, next_out, inverse_next, low_out, vec_out,
    rows_in, vec_in, wq, wo, normed, joined, turned, std, base, part, part_out, part_in, resid, std_next, low_next,
    z_send, z_recv, y_send, y_recv, x_send, x_recv, p_send, p_recv, q_send, q_recv,
    t_send, t_recv, v_send, v_recv, u_send, u_recv, w_send, w_recv,
    f_send, f_recv, g_send, g_recv, n_send, n_recv, local, saved,
    i_send, i_recv, j_send, j_recv, k_send, k_recv, l_send, l_recv,
):
    y, x, c, z = (lax.axis_index(name) for name in AXES)
    half = wo.shape[0] // 4
    wide = 3 * half
    span = wt.shape[1] // 4
    size = wf.shape[1] // 4
    own = rows_in.shape[0]
    near_y, near_x, pair = (1 - y, x, c, z), (y, 1 - x, c, z), (y, x, 1 - c, z)
    right_z, left_z = (y, x, c, (z + 1) % 4), (y, x, c, (z + 3) % 4)

    def at(i, length):
        return pl.ds(pl.multiple_of(i * length, length), length)

    def remote(src, dst, send, recv, peer):
        return pltpu.make_async_remote_copy(
            src_ref=src, dst_ref=dst, send_sem=send, recv_sem=recv, device_id=peer, device_id_type=MESH
        )

    def start(all_copies):
        for copy in all_copies:
            copy.start()

    def landed(all_copies):
        for copy in all_copies:
            copy.wait_recv()

    def sent(all_copies):
        for copy in all_copies:
            copy.wait_send()

    core = at(c, half)
    keep = [
        pltpu.make_async_copy(
            qkv_hbm.at[j, :, core], wq.at[:, pl.ds(pl.multiple_of(z * wide + j * half, half), half)], local.at[j]
        )
        for j in range(3)
    ] + [pltpu.make_async_copy(out_hbm.at[core], wo.at[at(z, half)], local.at[3])]
    keep_later = [
        pltpu.make_async_copy(later, wt.at[:, at(z, span)], local.at[4]),
        pltpu.make_async_copy(feed_hbm.at[at(c, 4 * size)], wf.at[z], local.at[5]),
        pltpu.make_async_copy(first_hbm.at[:, at(c, 4 * size)], wi.at[z], local.at[8]),
    ]
    start(keep + keep_later)

    barrier = pltpu.get_barrier_semaphore()
    for dc in range(2):
        for dz in range(4):
            if dc or dz:
                peer = (y, x, (c + dc) % 2, (z + dz) % 4)
                pl.semaphore_signal(barrier, inc=1, device_id=peer, device_id_type=MESH)
    for peer in (near_y, near_x):
        pl.semaphore_signal(barrier, inc=1, device_id=peer, device_id_type=MESH)
    pl.semaphore_wait(barrier, 9)

    def spot(dy, dx):
        return 2 * ((y + dy) % 2) + (x + dx) % 2

    def piece(dy, dx, r, split=False):
        s = (z + r) % 4
        rows = at(spot(dy, dx), BLK)
        first = pl.multiple_of(s * wide, half)
        out = wo.at[at(s, half), at(spot(dy, dx), BLK)]
        if split:
            last = pl.multiple_of(s * wide + 2 * half, half)
            return (wq.at[rows, pl.ds(first, 2 * half)], wq.at[rows, pl.ds(last, half)], out)
        return (wq.at[rows, pl.ds(first, wide)], out)

    def time_piece(dx, r):
        return wt.at[at((x + dx) % 2, 2 * BLK), at((z + r) % 4, span)]

    def feed_piece(dy, r):
        return wf.at[(z + r) % 4, at(spot(dy, 0), size)]

    def copies(parts, send, recv, peer):
        return [remote(ref, ref, send.at[i], recv.at[i], peer) for i, ref in enumerate(parts)]

    def leg(right, step):
        if right:
            return (0 if step == 0 else 4 - step), right_z, 3 - step
        return step, left_z, step + 1

    def z_copies(right, step):
        r, peer, lands = leg(right, step)
        return copies(piece(0, 0, r), z_send.at[int(right), step], z_recv.at[lands], peer)

    def time_z(right, step):
        r, peer, lands = leg(right, step)
        source = later.at[at(x, 2 * BLK)] if step == 0 else time_piece(0, r)
        return [remote(source, time_piece(0, r), u_send.at[int(right), step], u_recv.at[lands], peer)]

    def feed_z(right, step):
        r, peer, lands = leg(right, step)
        source = feed_hbm.at[at(4 * c + spot(0, 0), size)] if step == 0 else feed_piece(0, r)
        return [remote(source, feed_piece(0, r), f_send.at[int(right), step], f_recv.at[lands], peer)]

    def first_piece(dy, dx, r):
        return wi.at[(z + r) % 4, at(spot(dy, dx), BLK)]

    def first_z(right, step):
        r, peer, lands = leg(right, step)
        source = first_hbm.at[at(spot(0, 0), BLK), at(c, 4 * size)] if step == 0 else first_piece(0, 0, r)
        return [remote(source, first_piece(0, 0, r), i_send.at[int(right), step], i_recv.at[lands], peer)]

    def first_y(r, dy=0):
        return [remote(first_piece(dy, 0, r), first_piece(dy, 0, r), j_send.at[r], j_recv.at[r], near_y)]

    def first_x(r, dx=0):
        return [remote(first_piece(0, dx, r), first_piece(0, dx, r), k_send.at[r], k_recv.at[r], near_x)]

    def y_copies(r, dy=0):
        return copies(piece(dy, 0, r), y_send.at[r], y_recv.at[r], near_y)

    def x_copies(r, dx=0):
        return copies(piece(0, dx, r), x_send.at[r], x_recv.at[r], near_x)

    def corner_x(r, dx=0):
        return copies(piece(1, dx, r, split=True)[:1], p_send.at[r], p_recv.at[r], near_x)

    def corner_y(r, dy=0):
        return copies(piece(dy, 1, r, split=True)[1:], q_send.at[r], q_recv.at[r], near_y)

    def time_x(r, dx=0):
        return [remote(time_piece(dx, r), time_piece(dx, r), w_send.at[r], w_recv.at[r], near_x)]

    def feed_y(r, dy=0):
        return [remote(feed_piece(dy, r), feed_piece(dy, r), g_send.at[r], g_recv.at[r], near_y)]

    def token_copies(k):
        peer = (y, x, k % 2, 2 * c + k // 2)
        return [
            remote(tok.at[k], rows_in.at[:, at(z, BLK)], t_send.at[k], t_recv.at[z], peer),
            remote(vec, vec_in.at[:, at(z, BLK)], v_send.at[k], v_recv.at[z], peer),
        ]

    def token_local(k):
        return [
            pltpu.make_async_copy(tok.at[k], rows_in.at[:, at(z, BLK)], local.at[6]),
            pltpu.make_async_copy(vec, vec_in.at[:, at(z, BLK)], local.at[7]),
        ]

    def stays(k):
        return jnp.logical_and(2 * c + k // 2 == z, c == k % 2)

    def start_tokens(ks):
        for k in ks:
            pl.when(stays(k))(lambda k=k: start(token_local(k)))
            pl.when(jnp.logical_not(stays(k)))(lambda k=k: start(token_copies(k)))

    def each_side(j, act):
        pl.when(z >= j + 1)(lambda: act(3 - j, True))
        pl.when(z <= 2 - j)(lambda: act(j + 1, False))

    def begin(make):
        pl.when(z < 3)(lambda: start(make(True, 0)))
        pl.when(z > 0)(lambda: start(make(False, 0)))

    def onward(j, make, right):
        if j < 2:
            pl.when(z < 3 if right else z > 0)(lambda: start(make(right, j + 1)))

    def forward(j):
        def act(r, right):
            landed(copies(piece(0, 0, r), z_send.at[0, 0], z_recv.at[r], near_y))
            onward(j, z_copies, right)
            start(y_copies(r))
            start(x_copies(r))

        each_side(j, act)

    def corners(j):
        def act(r, right):
            landed(y_copies(r, 1))
            start(corner_x(r))
            landed(x_copies(r, 1))
            start(corner_y(r))

        each_side(j, act)

    def time_forward_step(j):
        def act(r, right):
            landed([remote(time_piece(0, r), time_piece(0, r), u_send.at[0, 0], u_recv.at[r], near_x)])
            onward(j, time_z, right)
            start(time_x(r))

        each_side(j, act)

    def feed_forward_step(j):
        def act(r, right):
            landed([remote(feed_piece(0, r), feed_piece(0, r), f_send.at[0, 0], f_recv.at[r], near_y)])
            onward(j, feed_z, right)
            start(feed_y(r))

        each_side(j, act)

    def first_corner_copy(r, dx=0):
        return [remote(first_piece(1, dx, r), first_piece(1, dx, r), l_send.at[r], l_recv.at[r], near_x)]

    def first_corner(j):
        def act(r, right):
            landed(first_y(r, 1))
            start(first_corner_copy(r))

        each_side(j, act)

    def first_forward_step(j):
        def act(r, right):
            landed([remote(first_piece(0, 0, r), first_piece(0, 0, r), i_send.at[0, 0], i_recv.at[r], near_y)])
            onward(j, first_z, right)
            start(first_y(r))
            start(first_x(r))

        each_side(j, act)

    for copy in keep:
        copy.wait()
    begin(z_copies)
    forward(0)
    start_tokens((0, 1))
    forward(1)
    start_tokens((2, 3))
    begin(first_z)
    begin(time_z)
    begin(feed_z)
    corners(0)
    forward(2)
    corners(1)
    for k in range(4):
        def finish_local(k=k):
            for copy in token_local(k):
                copy.wait()

        pl.when(stays(k))(finish_local)
    for s in range(4):
        def arrived(s=s):
            landed([
                remote(tok.at[0], rows_in.at[:, at(s, BLK)], t_send.at[0], t_recv.at[s], near_y),
                remote(vec, vec_in.at[:, at(s, BLK)], v_send.at[0], v_recv.at[s], near_y),
            ])

        pl.when(jnp.logical_not(jnp.logical_and(z == s, z // 2 == c)))(arrived)

    step = own // 2
    slab = 128
    vec_out[...] = vec_in[...].astype(F32)

    def first_norm(i, carry):
        rows = at(i, step)
        value = jnp.where(masked[rows] > 0.0, vec_out[0:1], rows_in[rows].astype(F32))
        base[rows] = value
        standard, inv = norm_rows(value)
        std[rows] = standard
        inverse[rows] = inv
        normed[rows] = (standard * vec_out[1:2]).astype(BF16)
        return carry

    lax.fori_loop(0, 2, first_norm, 0)
    give_normed = remote(normed.at[pl.ds(0, own)], normed.at[pl.ds(own, own)], n_send.at[0], n_recv.at[0], pair)
    give_normed.start()
    corners(2)

    def turn(i, carry):
        turned[:, at(i, slab)] = normed[at(i, slab)].T
        return carry

    lax.fori_loop(0, own // slab, turn, 0)
    for r in (1, 2, 3):
        landed(corner_x(r, 1))
        landed(corner_y(r, 1))
    saves = [
        pltpu.make_async_copy(wq, wq_out, saved.at[0]),
        pltpu.make_async_copy(wo, wo_out, saved.at[1]),
        pltpu.make_async_copy(std, std_out, saved.at[2]),
    ]
    start(saves)
    first_forward_step(0)

    def attend(i, carry):
        rows = at(i, slab)
        for h in range(wo.shape[0] // PAIR):
            q, k, v = (joined[rows, (3 * h + j) * PAIR : (3 * h + j + 1) * PAIR] for j in range(3))
            out, totals = attend_pair(q, k, v, None, scale)
            mixed[rows, h * PAIR : (h + 1) * PAIR] = out.astype(BF16)
            for j in range(2):
                total_out[i, 2 * h + j : 2 * h + j + 1, :] = totals[j]
        return carry

    def project(t):
        rows = pl.ds(t * own, own)
        joined[rows] = dot_nn(normed[rows], wq[...]).astype(BF16)

    frames = own // slab
    project(0)
    time_forward_step(0)
    lax.fori_loop(0, frames, attend, 0)
    part[...] = dot_nn(mixed[pl.ds(0, own)], wo[...])
    feed_forward_step(0)
    first_forward_step(1)
    first_corner(0)
    give_normed.wait_recv()
    project(1)
    saves.append(pltpu.make_async_copy(joined, joined_out, saved.at[3]))
    saves[3].start()
    lax.fori_loop(frames, 2 * frames, attend, 0)
    part_out[...] = dot_nn(mixed[pl.ds(own, own)], wo[...]).astype(BF16)
    give_part = remote(part_out, part_in, n_send.at[1], n_recv.at[1], pair)
    give_part.start()
    time_forward_step(1)
    feed_forward_step(1)
    first_corner(1)
    lax.fori_loop(own // slab, 2 * own // slab, turn, 0)
    saves.append(pltpu.make_async_copy(turned, turned_out, saved.at[4]))
    saves[4].start()
    give_part.wait_recv()
    first_forward_step(2)

    def second_norm(i, carry):
        rows = at(i, step)
        value = base[rows] + part[rows] + part_in[rows].astype(F32)
        resid[rows] = value
        standard, inv = norm_rows(value)
        std_next[rows] = standard
        inverse_next[rows] = inv
        low_next[rows] = (standard * vec_out[2:3]).astype(BF16)
        return carry

    lax.fori_loop(0, 2, second_norm, 0)
    for i, (src, dst) in enumerate(((resid, resid_out), (std_next, next_out), (low_next, low_out))):
        saves.append(pltpu.make_async_copy(src, dst, saved.at[5 + i]))
        saves[-1].start()
    time_forward_step(2)
    feed_forward_step(2)

    def first_ends(j):
        def act(r, right):
            if j == 2:
                landed(first_y(r, 1))
            else:
                landed(first_corner_copy(r, 1))
                sent(first_corner_copy(r))

        each_side(j, act)

    for j in range(3):
        first_ends(j)
    for copy in keep_later + saves:
        copy.wait()
    give_normed.wait_send()
    give_part.wait_send()
    for r in (1, 2, 3):
        landed(time_x(r, 1))
        landed(feed_y(r, 1))
        landed(first_x(r, 1))
        for group in (y_copies(r), x_copies(r), corner_x(r), corner_y(r), time_x(r), feed_y(r), first_y(r), first_x(r)):
            sent(group)
    for step_z in range(3):
        for make in (z_copies, time_z, first_z, feed_z):
            pl.when(jnp.logical_and(z >= step_z, z < 3))(lambda step_z=step_z, make=make: sent(make(True, step_z)))
            pl.when(jnp.logical_and(z + step_z <= 3, z > 0))(lambda step_z=step_z, make=make: sent(make(False, step_z)))
    for k in range(4):
        pl.when(jnp.logical_not(stays(k)))(lambda k=k: sent(token_copies(k)))


def enter(tok, vec, qkv, out, later, feed_weight, first_weight, masked, scale):
    own, width, half = tok.shape[1], 4 * tok.shape[2], out.shape[0] // 2
    size = feed_weight.shape[0] // 2
    dma = pltpu.SemaphoreType.DMA
    anywhere = pl.BlockSpec(memory_space=pl.ANY)
    whole = pl.BlockSpec(memory_space=pltpu.VMEM)
    heads = 4 * half // HEAD_DIM

    def low(*shape):
        return pltpu.VMEM(shape, BF16)

    def high(*shape):
        return pltpu.VMEM(shape, F32)

    shapes = [
        ((width, 12 * half), BF16), ((4 * half, width), BF16), ((width, 4 * later.shape[1]), BF16),
        ((4, size, width), BF16), ((4, width, size), BF16), ((2 * own, 12 * half), BF16), ((width, 2 * own), BF16), ((own, width), F32),
        ((2 * own, 4 * half), BF16), ((2 * own // 128, heads, 128), F32), ((own, 1), F32), ((own, width), F32),
        ((own, width), F32), ((own, 1), F32), ((own, width), BF16), ((vec.shape[0], width), F32),
    ]
    return pl.pallas_call(
        functools.partial(enter_kernel, scale),
        in_specs=[anywhere] * 7 + [whole],
        out_specs=[anywhere] * 8 + [whole] * 3 + [anywhere] * 2 + [whole, anywhere, whole],
        out_shape=[jax.ShapeDtypeStruct(shape, kind) for shape, kind in shapes],
        scratch_shapes=[
            low(own, width), low(vec.shape[0], width), low(width, 12 * half), low(4 * half, width),
            low(2 * own, width), low(2 * own, 12 * half), low(width, 2 * own), high(own, width), high(own, width),
            high(own, width), low(own, width), low(own, width), high(own, width), high(own, width), low(own, width),
            dma((2, 3, 2)), dma((4, 2)), dma((4, 2)), dma((4, 2)), dma((4, 2)), dma((4, 2)),
            dma((4, 1)), dma((4, 1)), dma((4, 2)), dma((4, 2)),
            dma((4,)), dma((4,)), dma((4,)), dma((4,)), dma((2, 3)), dma((4,)), dma((4,)), dma((4,)),
            dma((2, 3)), dma((4,)), dma((4,)), dma((4,)), dma((2,)), dma((2,)), dma((9,)), dma((8,)),
            dma((2, 3)), dma((4,)), dma((4,)), dma((4,)), dma((4,)), dma((4,)), dma((4,)), dma((4,)),
        ],
        compiler_params=pltpu.CompilerParams(
            collective_id=0, has_side_effects=True, vmem_limit_bytes=56 * 1024 * 1024
        ),
        cost_estimate=pl.CostEstimate(flops=10**10, transcendentals=10**6, bytes_accessed=10**8),
        name="enter",
    )(tok, vec, qkv, out, later, feed_weight, first_weight, masked)


GROUP = 8
CHUNK = 16


def time_kernel(back, scale, heads, *refs):
    if back:
        (own_ref, rider_ref, joined_hbm, total_ref, wide_ref, turned_ref, mixed_hbm, wt_hbm, bias_ref) = refs[:9]
        (delta_ref, grad_ref, reduced_ref, rider_out) = refs[9:13]
        (half_in, half_own, line_out, line_in, half_send, half_recv, half_local, line_send, line_recv) = refs[-17:-8]
        (out_ref, turned, grad_qkv, grad_out, wt_ref, joined_ref, mixed_ref, load_sem) = refs[-8:]
        refs = refs[13:-17]
    else:
        (own_ref, rider_ref, far_ref, in_ref, wt_hbm, bias_ref) = refs[:6]
        (turned_ref, out_ref, mixed_ref, total_ref, delta_ref, rider_out, spread_out, in_out) = refs[6:14]
        (turned, wt_ref, load_sem) = refs[-3:]
        refs = refs[14:-3]
    (
        wq_ref, wo_ref, held, wide, narrow, kept, core_out, core_in, near_out, near_in,
        gy_send, gy_recv, gc_send, gc_recv, gd_send, gd_recv, sc_send, sc_recv, sy_send, sy_recv,
        r_send, r_recv, r_local, out_sem, wx_send, wx_recv,
    ) = refs
    y, x, c, z = (lax.axis_index(name) for name in AXES)
    near, pair, near_x = (1 - y, x, c, z), (y, x, 1 - c, z), (y, 1 - x, c, z)
    frames = held.shape[0] // 4
    chunks = held.shape[1] // CHUNK
    width = heads * HEAD_DIM
    groups = CHUNK // GROUP

    loads = [(wt_hbm, wt_ref), (own_ref, held.at[pl.ds(0, frames)])]
    if back:
        loads += [(joined_hbm, joined_ref), (mixed_hbm, mixed_ref)]
    loads = [pltpu.make_async_copy(src, dst, load_sem.at[i]) for i, (src, dst) in enumerate(loads)]
    for copy in loads:
        copy.start()
    barrier = pltpu.get_barrier_semaphore()
    for dc in range(2):
        for dz in range(4):
            if dc or dz:
                pl.semaphore_signal(barrier, inc=1, device_id=(y, x, (c + dc) % 2, (z + dz) % 4), device_id_type=MESH)
    pl.semaphore_signal(barrier, inc=1, device_id=near, device_id_type=MESH)
    pl.semaphore_signal(barrier, inc=1, device_id=near_x, device_id_type=MESH)
    pl.semaphore_wait(barrier, 9)

    def remote(src, dst, send, recv, peer):
        return pltpu.make_async_remote_copy(
            src_ref=src, dst_ref=dst, send_sem=send, recv_sem=recv, device_id=peer, device_id_type=MESH
        )

    def patches(k):
        return pl.ds(pl.multiple_of(k * CHUNK, CHUNK), CHUNK)

    def block(b, k):
        return held.at[pl.ds(b * frames, frames), patches(k)]

    def gather_y(k):
        return remote(own_ref.at[:, patches(k)], block(1, k), gy_send.at[k], gy_recv.at[k], near)

    def gather_c(k):
        return remote(own_ref.at[:, patches(k)], block(2, k), gc_send.at[k], gc_recv.at[k], pair)

    def gather_d(k):
        return remote(block(1, k), block(3, k), gd_send.at[k], gd_recv.at[k], pair)

    def scatter_c(k):
        return remote(core_out.at[k], core_in.at[k], sc_send.at[k], sc_recv.at[k], pair)

    def scatter_y(k):
        return remote(near_out.at[k], near_in.at[k], sy_send.at[k], sy_recv.at[k], near)

    def save(k):
        there = (turned_ref.at[k], turned.at[k]) if back else (turned.at[k], turned_ref.at[k])
        return pltpu.make_async_copy(*there, out_sem.at[k])

    def columns(s):
        return pl.ds(pl.multiple_of(s * BLK, BLK), BLK)

    def stays(k):
        if back:
            return jnp.logical_and(z == k, z // 2 == c)
        return jnp.logical_and(2 * c + k // 2 == z, c == k % 2)

    def ride(k):
        if back:
            src, dst = rider_ref.at[:, columns(k)], rider_out.at[2 * (z % 2) + c]
            peer, slot = (y, x, z // 2, k), 2 * (z % 2) + c
        else:
            src, dst = rider_ref.at[k], rider_out.at[:, columns(z)]
            peer, slot = (y, x, k % 2, 2 * c + k // 2), z
        return src, dst, peer, slot

    def ride_remote(k):
        src, dst, peer, slot = ride(k)
        return remote(src, dst, r_send.at[k], r_recv.at[slot], peer)

    def ride_local(k):
        src, dst, _, _ = ride(k)
        return pltpu.make_async_copy(src, dst, r_local.at[0])

    def ride_landed(k):
        if back:
            src, dst = rider_ref.at[:, columns(k)], rider_out.at[k]
        else:
            src, dst = rider_ref.at[k], rider_out.at[:, columns(k)]
        return remote(src, dst, r_send.at[k], r_recv.at[k], near)

    def from_self(k):
        if back:
            return jnp.logical_and(2 * c + k // 2 == z, c == k % 2)
        return jnp.logical_and(z == k, z // 2 == c)

    def spread_x(i, dx=0):
        r, yb = i // 2 + 1, i % 2
        size = far_ref.shape[1] // 4
        at = pl.multiple_of(size * (2 * yb + (x + dx) % 2), size)
        src = far_ref.at[(z + r) % 4, pl.ds(at, size)]
        return remote(src, spread_out.at[(z + r) % 4, pl.ds(at, size)], wx_send.at[i], wx_recv.at[i], near_x)

    gather_y(0).start()
    for k in range(chunks):
        if k > 0:
            gather_y(k).start()
        gather_c(k).start()
    def spread_in(dx=0):
        at = pl.multiple_of(BLK * (2 * (1 - y) + (x + dx) % 2), BLK)
        there = in_out.at[3 - z, pl.ds(at, BLK)]
        return remote(in_ref.at[3 - z, pl.ds(at, BLK)], there, wx_send.at[6], wx_recv.at[6], near_x)

    at_end = jnp.logical_or(z == 0, z == 3)

    def half_away(s):
        return remote(wide_ref.at[1 - x, s], half_in.at[s], half_send.at[s], half_recv.at[s], near_x)

    def half_here(s):
        return pltpu.make_async_copy(wide_ref.at[x, s], half_own.at[s], half_local.at[s])

    def line_away(r):
        return remote(line_out.at[r], line_in.at[r], line_send.at[r], line_recv.at[r], (y, x, c, (z + r) % 4))

    def halve():
        for s in range(4):
            half_away(s).wait_recv()
            half_here(s).wait()
        for r in range(4):
            s = (z + r) % 4
            whole = half_own[s].astype(F32) + half_in[s].astype(F32)
            if r == 0:
                reduced_ref[...] = whole
            else:
                line_out[r] = whole.astype(BF16)
                line_away(r).start()

    if back:
        for s in range(4):
            half_away(s).start()
            half_here(s).start()
    else:
        pl.when(at_end)(lambda: spread_in().start())
        for i in range(6):
            spread_x(i).start()
    for k in range(4):
        pl.when(stays(k))(lambda k=k: ride_local(k).start())
        pl.when(jnp.logical_not(stays(k)))(lambda k=k: ride_remote(k).start())
    if back:
        for k in range(chunks):
            save(k).start()

    def assemble(i, carry):
        rows = pl.ds(pl.multiple_of(i * BLK, BLK), BLK)
        for s in range(0, heads, 2):
            for part in range(4):
                both = [
                    wt_ref[rows, (s + j) * 4 * HEAD_DIM + part * HEAD_DIM : (s + j) * 4 * HEAD_DIM + (part + 1) * HEAD_DIM]
                    for j in range(2)
                ]
                both = jnp.concatenate(both, axis=1)
                if part < 3:
                    wq_ref[rows, part * width + s * HEAD_DIM : part * width + s * HEAD_DIM + PAIR] = both
                else:
                    wo_ref[rows, s * HEAD_DIM : s * HEAD_DIM + PAIR] = both
        return carry

    loads[0].wait()
    lax.fori_loop(0, wt_ref.shape[0] // BLK, assemble, 0)
    for copy in loads[1:]:
        copy.wait()

    def finish(k):
        scatter_c(k).wait_recv()
        both = kept[:, patches(k)] + core_in[k].astype(F32)
        near_out[k] = both[frames:].astype(BF16)
        delta_ref[:, patches(k)] = both[:frames]
        scatter_y(k).start()

    def pass_on(k):
        gather_y(k).wait_recv()
        gather_d(k).start()

    def one_group(i, rows):
        at = pl.ds(pl.multiple_of(i * GROUP, GROUP), GROUP)
        count = 4 * frames * GROUP
        bias = bias_ref[...]
        for lo in range(0, width, PAIR):
            q, k, v = (
                wide[:, at, part * width + lo : part * width + lo + PAIR].reshape(count, PAIR).astype(BF16)
                for part in range(3)
            )
            h = lo // HEAD_DIM
            if back:
                g = narrow[:, at, lo : lo + PAIR].reshape(count, PAIR).astype(BF16)
                totals = [total_ref[rows * groups + i, h + j : h + j + 1, :] for j in range(2)]
                grads = attend_pair_back(q, k, v, g, totals, bias, scale)
                for part in range(3):
                    wide[:, at, part * width + lo : part * width + lo + PAIR] = grads[part].reshape(
                        4 * frames, GROUP, PAIR
                    )
            else:
                mixed, totals = attend_pair(q, k, v, bias, scale)
                narrow[:, at, lo : lo + PAIR] = mixed.reshape(4 * frames, GROUP, PAIR)
                for j in range(2):
                    total_ref[rows * groups + i, h + j : h + j + 1, :] = totals[j]

    def one_chunk(k, carry):
        pl.when(k + 1 < chunks)(lambda: pass_on(k + 1))
        gather_c(k).wait_recv()
        gather_d(k).wait_recv()
        count = 4 * frames * CHUNK
        lhs = held[:, patches(k)].reshape(count, held.shape[2])
        if back:
            wide[...] = joined_ref[:, patches(k)].astype(F32)
            narrow[...] = dot_nn(lhs, wo_ref[...]).astype(BF16).astype(F32).reshape(narrow.shape)
        else:
            joined = dot_nn(lhs, wq_ref[...]).astype(BF16)
            out_ref[:, patches(k)] = joined.reshape(wide.shape)
            wide[...] = joined.astype(F32).reshape(wide.shape)
        lax.fori_loop(0, groups, lambda i, carry: (one_group(i, k), carry)[1], 0)
        if back:
            grads = wide[...].astype(BF16)
            out_ref[:, patches(k)] = grads
            partial = dot_nt(grads.reshape(count, 3 * width), wq_ref[...])
        else:
            mixed = narrow[...].astype(BF16)
            mixed_ref[:, patches(k)] = mixed
            partial = dot_nt(mixed.reshape(count, width), wo_ref[...])
        partial = partial.reshape(4 * frames, CHUNK, held.shape[2])
        kept[:, patches(k)] = partial[: 2 * frames]
        core_out[k] = partial[2 * frames :].astype(BF16)
        scatter_c(k).start()
        pl.when(k > 0)(lambda: finish(k - 1))
        if not back:
            for b in range(4):
                slab = held[b * frames : (b + 1) * frames, patches(k)].reshape(frames * CHUNK, held.shape[2])
                turned[k, :, b * frames * CHUNK : (b + 1) * frames * CHUNK] = slab.T
            save(k).start()
        if back:
            pl.when(k == chunks // 2 - 1)(halve)
        return carry

    pass_on(0)
    lax.fori_loop(0, chunks, one_chunk, 0)
    finish(chunks - 1)

    def weigh(k, carry):
        count = 4 * frames * CHUNK
        save(k).wait()
        grad_qkv[...] = grad_qkv[...] + dot_nn(turned[k], out_ref[:, patches(k)].reshape(count, 3 * width))
        grad_out[...] = grad_out[...] + dot_tn(
            mixed_ref[:, patches(k)].reshape(count, width), held[:, patches(k)].reshape(count, held.shape[2])
        )
        return carry

    def arrange(i, carry):
        rows = pl.ds(pl.multiple_of(i * BLK, BLK), BLK)
        last = grad_out[:, rows].T
        for s in range(heads):
            mine = slice(s * HEAD_DIM, (s + 1) * HEAD_DIM)
            parts = [grad_qkv[rows, j * width : (j + 1) * width][:, mine] for j in range(3)] + [last[:, mine]]
            grad_ref[rows, 2 * s * PAIR : (2 * s + 1) * PAIR] = jnp.concatenate(parts[:2], axis=1).astype(BF16)
            grad_ref[rows, (2 * s + 1) * PAIR : (2 * s + 2) * PAIR] = jnp.concatenate(parts[2:], axis=1).astype(BF16)
        return carry

    if back:
        grad_qkv[...] = jnp.zeros_like(grad_qkv)
        grad_out[...] = jnp.zeros_like(grad_out)
        lax.fori_loop(0, chunks, weigh, 0)
        lax.fori_loop(0, grad_ref.shape[0] // BLK, arrange, 0)
    for k in range(chunks):
        scatter_y(k).wait_recv()
        delta_ref[:, patches(k)] = delta_ref[:, patches(k)] + near_in[k].astype(F32)
    if back:
        for r in (1, 2, 3):
            line_away(r).wait_recv()
            reduced_ref[...] = reduced_ref[...] + line_in[r].astype(F32)
        for r in (1, 2, 3):
            line_away(r).wait_send()
        for s in range(4):
            half_away(s).wait_send()
    for k in range(chunks):
        for copy in (gather_y(k), gather_c(k), gather_d(k), scatter_c(k), scatter_y(k)):
            copy.wait_send()
        if not back:
            save(k).wait()
    if not back:
        for i in range(6):
            spread_x(i, 1).wait_recv()
            spread_x(i).wait_send()

        def spread_in_end():
            spread_in(1).wait_recv()
            spread_in().wait_send()

        pl.when(at_end)(spread_in_end)
    for k in range(4):
        pl.when(stays(k))(lambda k=k: ride_local(k).wait())
        pl.when(jnp.logical_not(stays(k)))(lambda k=k: ride_remote(k).wait_send())
        pl.when(jnp.logical_not(from_self(k)))(lambda k=k: ride_landed(k).wait_recv())


def time_call(back, own, rider, saved, weights, bias, scale):
    frames, patches, features = own.shape
    width = weights.shape[1] // 4
    heads = width // HEAD_DIM
    chunks = patches // CHUNK
    rows = 4 * frames * GROUP
    dma = pltpu.SemaphoreType.DMA
    anywhere = pl.BlockSpec(memory_space=pl.ANY)
    whole = pl.BlockSpec(memory_space=pltpu.VMEM)
    turned = (chunks, features, 4 * frames * CHUNK)
    if back:
        out_shape = []
    else:
        out_shape = [
            jax.ShapeDtypeStruct(turned, BF16),
            jax.ShapeDtypeStruct((4 * frames, patches, 3 * width), BF16),
            jax.ShapeDtypeStruct((4 * frames, patches, width), BF16),
            jax.ShapeDtypeStruct((patches // GROUP, heads, rows), F32),
        ]
    rider_shape = (4, frames * patches, BLK) if back else (frames * patches, features)
    out_shape += [
        jax.ShapeDtypeStruct((frames, patches, features), F32),
        jax.ShapeDtypeStruct(rider_shape, BF16),
    ]
    held = 2
    half = saved[2].shape[1:] if back else None
    if back:
        out_shape.insert(-1, jax.ShapeDtypeStruct((features, features), BF16))
        out_shape.insert(-1, jax.ShapeDtypeStruct(half[1:], F32))
    else:
        out_shape += [jax.ShapeDtypeStruct(w.shape, BF16) for w in saved]
        held = 4
    return pl.pallas_call(
        functools.partial(time_kernel, back, scale, heads),
        in_specs=[anywhere] * 2
        + ([anywhere, whole, anywhere, anywhere, anywhere] if back else [anywhere] * 2)
        + [anywhere, whole],
        out_specs=([] if back else [anywhere]) + [whole] * (len(out_shape) - held + back) + [anywhere] * (held - 1),
        out_shape=out_shape,
        scratch_shapes=[
            pltpu.VMEM((features, 3 * width), BF16),
            pltpu.VMEM((features, width), BF16),
            pltpu.VMEM((4 * frames, patches, features), BF16),
            pltpu.VMEM((4 * frames, CHUNK, 3 * width), F32),
            pltpu.VMEM((4 * frames, CHUNK, width), F32),
            pltpu.VMEM((2 * frames, patches, features), F32),
            pltpu.VMEM((chunks, 2 * frames, CHUNK, features), BF16),
            pltpu.VMEM((chunks, 2 * frames, CHUNK, features), BF16),
            pltpu.VMEM((chunks, frames, CHUNK, features), BF16),
            pltpu.VMEM((chunks, frames, CHUNK, features), BF16),
        ]
        + [dma((chunks,))] * 10
        + [dma((4,)), dma((4,)), dma((1,)), dma((chunks,))]
        + [dma((7,))] * 2
        + ([pltpu.VMEM(half, BF16)] * 4 + [dma((4,))] * 5 if back else [])
        + ([pltpu.VMEM((4 * frames, patches, 3 * width), BF16)] if back else [])
        + [pltpu.VMEM(turned, BF16)]
        + ([pltpu.VMEM((features, 3 * width), F32), pltpu.VMEM((width, features), F32)] if back else [])
        + [pltpu.VMEM(weights.shape, BF16)]
        + ([pltpu.VMEM(saved[0].shape, BF16), pltpu.VMEM(saved[4].shape, BF16)] if back else [])
        + [dma((4,))],
        compiler_params=pltpu.CompilerParams(
            collective_id=2 if back else 1, has_side_effects=True, vmem_limit_bytes=60 * 1024 * 1024
        ),
        cost_estimate=pl.CostEstimate(flops=10**10, transcendentals=10**6, bytes_accessed=10**8),
        name="time_back" if back else "time_forward",
    )(own, rider, *saved, weights, bias)


def feed_kernel(
    resid_hbm, delta_hbm, upstream_hbm, masked, gain, w_in_hbm, w_in_far_hbm, w_out_hbm, w_far_hbm,
    half_in_hbm, half_out_hbm, grad_hbm, low_hbm, rows_hbm, gain_out,
    resid, delta, upstream, grad_out, low_out, rows_out, move_sem,
    w_in, w_out, standard, inverse, normed, grads, normed_t, grads_t, hidden, pulled, g_in, g_out, back, ahead,
    back_out, back_in, ahead_out, ahead_in, from_x, from_y,
    w_sem, g_sem, n_send, n_recv, b_send, b_recv, hx_send, hx_recv, hy_send, hy_recv,
):
    y, x, c, z = (lax.axis_index(name) for name in AXES)
    pair, near_y, near_x = (y, x, 1 - c, z), (1 - y, x, c, z), (y, 1 - x, c, z)
    own = resid.shape[0]
    moves = [
        pltpu.make_async_copy(src, dst, move_sem.at[i])
        for i, (src, dst) in enumerate((
            (resid_hbm, resid), (delta_hbm, delta), (upstream_hbm, upstream),
            (grad_out, grad_hbm), (low_out, low_hbm), (rows_out, rows_hbm),
        ))
    ]
    for copy in moves[:3]:
        copy.start()
    step = own // 2
    slab = 128

    def fetch(s, far, last=False):
        size = w_out.shape[1] // 4
        copies = []
        for i in range(4):
            rows = pl.ds(pl.multiple_of(BLK * (2 * ((y + i // 2) % 2) + (x + i % 2) % 2), BLK), BLK)
            source = w_in_far_hbm if last and i == 3 else w_in_hbm
            copies.append(pltpu.make_async_copy(source.at[s, rows], w_in.at[s, rows], w_sem.at[5 + i, s]))
        for i in range(4):
            rows = pl.ds(pl.multiple_of(size * (2 * (i // 2) + (x + i % 2) % 2), size), size)
            source = w_far_hbm if far and i % 2 else w_out_hbm
            copies.append(pltpu.make_async_copy(source.at[s, rows], w_out.at[s, rows], w_sem.at[i, s]))
        return copies

    def fetch_now(s, far, last):
        for copy in fetch(s, far, last):
            copy.start()

    for s in range(4):
        pl.when(z == s)(lambda s=s: fetch_now(s, False, False))
        if s in (0, 3):
            pl.when(z == 3 - s)(lambda s=s: fetch_now(s, True, True))
            pl.when(jnp.logical_and(z != s, z != 3 - s))(lambda s=s: fetch_now(s, True, False))
        else:
            pl.when(z != s)(lambda s=s: fetch_now(s, True, False))
    barrier = pltpu.get_barrier_semaphore()
    for peer in (pair, near_y, near_x):
        pl.semaphore_signal(barrier, inc=1, device_id=peer, device_id_type=MESH)

    def remote(src, dst, send, recv, peer=pair):
        return pltpu.make_async_remote_copy(
            src_ref=src, dst_ref=dst, send_sem=send, recv_sem=recv, device_id=peer, device_id_type=MESH
        )

    def block(yb, xb):
        return pl.ds(pl.multiple_of(BLK * (2 * yb + xb), BLK), BLK)

    def away_x(s, i):
        return remote(g_out.at[s, block(i, 1 - x)], from_x.at[i, s], hx_send.at[i, s], hx_recv.at[i, s], near_x)

    def away_y(s, i):
        return remote(g_in.at[s, block(1 - y, i)], from_y.at[i, s], hy_send.at[i, s], hy_recv.at[i, s], near_y)

    def keep(s, i):
        return (
            pltpu.make_async_copy(g_out.at[s, block(i, x)], half_out_hbm.at[i, s], g_sem.at[0, i, s]),
            pltpu.make_async_copy(g_in.at[s, block(y, i)], half_in_hbm.at[i, s], g_sem.at[1, i, s]),
        )

    def combine(s):
        for i in range(2):
            away_x(s, i).wait_recv()
            g_out[s, block(i, x)] = (g_out[s, block(i, x)].astype(F32) + from_x[i, s].astype(F32)).astype(BF16)
            away_y(s, i).wait_recv()
            g_in[s, block(y, i)] = (g_in[s, block(y, i)].astype(F32) + from_y[i, s].astype(F32)).astype(BF16)
            for copy in keep(s, i):
                copy.start()

    def at(i, size):
        return pl.ds(pl.multiple_of(i * size, size), size)

    def prepare(i, carry):
        rows = at(i, step)
        grads[rows] = jnp.where(masked[rows] > 0.0, upstream[rows].astype(F32), 0.0).astype(BF16)
        std, inv = norm_rows(resid[rows] + delta[rows])
        standard[rows] = std
        inverse[rows] = inv
        normed[rows] = (std * gain[3:4]).astype(BF16)
        return carry

    for copy in moves[:3]:
        copy.wait()
    lax.fori_loop(0, 2, prepare, 0)
    pl.semaphore_wait(barrier, 3)
    mine, theirs = pl.ds(0, own), pl.ds(own, own)
    give_grads = remote(grads.at[mine], grads.at[theirs], n_send.at[0], n_recv.at[0])
    give_normed = remote(normed.at[mine], normed.at[theirs], n_send.at[1], n_recv.at[1])
    give_normed.start()
    give_grads.start()

    def turn(i, carry):
        rows = at(i, slab)
        normed_t[:, rows] = normed[rows].T
        grads_t[:, rows] = grads[rows].T
        return carry

    lax.fori_loop(0, own // slab, turn, 0)
    back[...] = jnp.zeros_like(back)
    ahead[...] = jnp.zeros_like(ahead)
    rate = math.sqrt(2.0 / math.pi)

    def rows_step(s, rows):
        inner = dot_nn(normed[rows], w_in[s])
        square = inner * inner
        bend = jnp.tanh(rate * inner * (1.0 + 0.044715 * square))
        hidden[rows] = (0.5 * inner * (1.0 + bend)).astype(BF16)
        slope = 0.5 * (1.0 + bend) + 0.5 * inner * (1.0 - bend * bend) * (rate * (1.0 + 3.0 * 0.044715 * square))
        pulled[rows] = (dot_nt(grads[rows], w_out[s]) * slope).astype(BF16)
        ahead[rows] = ahead[rows] + dot_nn(hidden[rows], w_out[s])
        back[rows] = back[rows] + dot_nt(pulled[rows], w_in[s])

    def meet():
        give_normed.wait_recv()
        give_grads.wait_recv()
        lax.fori_loop(own // slab, 2 * own // slab, turn, 0)

    def one_piece(s, carry):
        for copy in fetch(s, False):
            copy.wait()

        def one_half(t, carry):
            pl.when(jnp.logical_and(s == 0, t == 1))(meet)
            rows_step(s, at(t, own))
            return carry

        lax.fori_loop(0, 2, one_half, 0)
        g_out[s] = dot_nn(grads_t[...], hidden[...]).astype(BF16)
        g_in[s] = dot_nn(normed_t[...], pulled[...]).astype(BF16)
        for i in range(2):
            away_x(s, i).start()
            away_y(s, i).start()
        return carry

    lax.fori_loop(0, 4, one_piece, 0)
    back_out[...] = back[theirs].astype(BF16)
    give_back = remote(back_out, back_in, b_send.at[0], b_recv.at[0])
    give_back.start()
    ahead_out[...] = ahead[theirs].astype(BF16)
    give_ahead = remote(ahead_out, ahead_in, b_send.at[1], b_recv.at[1])
    give_ahead.start()
    give_back.wait_recv()

    def finish(i, total):
        rows = at(i, step)
        grad = back[rows] + back_in[rows].astype(F32)
        std = standard[rows]
        inner = grad * gain[3:4]
        mean = jnp.mean(inner, axis=-1, keepdims=True)
        along = jnp.mean(inner * std, axis=-1, keepdims=True)
        full = grads[rows].astype(F32) + (inner - mean - std * along) * inverse[rows]
        grad_out[rows] = full
        low_out[rows] = full.astype(BF16)
        return total + jnp.sum(grad * std, axis=0, keepdims=True)

    gain_out[...] = lax.fori_loop(0, 2, finish, jnp.zeros((1, resid.shape[1]), F32))
    moves[3].start()
    moves[4].start()
    give_ahead.wait_recv()

    def emit(i, carry):
        rows = at(i, step)
        rows_out[rows] = (resid[rows] + delta[rows] + ahead[rows] + ahead_in[rows].astype(F32)).astype(BF16)
        return carry

    lax.fori_loop(0, 2, emit, 0)
    moves[5].start()
    lax.fori_loop(0, 4, lambda s, carry: (combine(s), carry)[1], 0)
    for copy in (give_normed, give_grads, give_back, give_ahead):
        copy.wait_send()
    for s in range(4):
        for i in range(2):
            away_x(s, i).wait_send()
            away_y(s, i).wait_send()
            for copy in keep(s, i):
                copy.wait()
    for copy in moves[3:]:
        copy.wait()


def feed(resid, delta, upstream, masked, gain, w_in, w_in_far, w_out, w_far):
    own, features = resid.shape
    units = w_in.shape[2]
    dma = pltpu.SemaphoreType.DMA
    anywhere = pl.BlockSpec(memory_space=pl.ANY)
    whole = pl.BlockSpec(memory_space=pltpu.VMEM)

    def low(*shape):
        return pltpu.VMEM(shape, BF16)

    def high(*shape):
        return pltpu.VMEM(shape, F32)

    return pl.pallas_call(
        feed_kernel,
        in_specs=[anywhere] * 3 + [whole] * 2 + [anywhere] * 4,
        out_specs=[anywhere] * 5 + [whole],
        out_shape=[
            jax.ShapeDtypeStruct((2, 4, BLK, units), BF16),
            jax.ShapeDtypeStruct((2, 4, BLK, units), BF16),
            jax.ShapeDtypeStruct((own, features), F32),
            jax.ShapeDtypeStruct((own, features), BF16),
            jax.ShapeDtypeStruct((own, features), BF16),
            jax.ShapeDtypeStruct((1, features), F32),
        ],
        scratch_shapes=[
            high(own, features), high(own, features), low(own, features),
            high(own, features), low(own, features), low(own, features), dma((6,)),
            low(4, features, units), low(4, units, features), high(own, features), high(own, 1),
            low(2 * own, features), low(2 * own, features), low(features, 2 * own), low(features, 2 * own),
            low(2 * own, units), low(2 * own, units), low(4, features, units), low(4, features, units),
            high(2 * own, features), high(2 * own, features),
            low(own, features), low(own, features), low(own, features), low(own, features),
            low(2, 4, BLK, units), low(2, 4, BLK, units),
            dma((9, 4)), dma((2, 2, 4)), dma((2,)), dma((2,)), dma((2,)), dma((2,)),
            dma((2, 4)), dma((2, 4)), dma((2, 4)), dma((2, 4)),
        ],
        compiler_params=pltpu.CompilerParams(
            collective_id=4, has_side_effects=True, vmem_limit_bytes=60 * 1024 * 1024
        ),
        cost_estimate=pl.CostEstimate(flops=26 * 10**9, transcendentals=2 * 10**6, bytes_accessed=10**8),
        name="feed",
    )(resid, delta, upstream, masked, gain, w_in, w_in_far, w_out, w_far)


def leave_kernel(
    scale,
    part_hbm, next_hbm, grad_hbm, out_hbm, joined_hbm, mixed_hbm, lhs_hbm, weight_hbm, std_hbm, time_hbm, feed_hbm, feed_in_hbm,
    totals, inverse_next, inverse, masked, gains, later_grad,
    space_qkv, space_out, feed_in_out, feed_out_out, time_qkv, time_out, rows_out, small_out,
    rows_in,
    part, std, base, w_out, dj, mixed, lhs, weight, low_grads, turned, dmixed, go,
    t_own, t_in, tz_out, tz_in, t_total, ty_out, ty_in, tc_out, tc_in,
    f_own, f_in, fz_out, fz_in, f_total, f_other, fc_out, fc_in,
    grads, a1_out, a1_in, b1_out, b1_in, a2_out, a2_in, b2_out, b2_in, z_out, z_in,
    half_out, half_in, ready, core_out, core_in, sums, sum_out, sum_in, share_in,
    a1_send, a1_recv, b1_send, b1_recv, a2_send, a2_recv, b2_send, b2_recv, z_send, z_recv,
    h_send, h_recv, r_send, r_recv, c_send, c_recv, s_send, s_recv, p_send, p_recv, local,
    g_send, g_recv, tx_send, tx_recv, tz_send, tz_recv, ty_send, ty_recv, fy_send, fy_recv, fz_send, fz_recv, t_local, f_local, fetched,
):
    y, x, c, z = (lax.axis_index(name) for name in AXES)
    near_y, near_x, pair = (1 - y, x, c, z), (y, 1 - x, c, z), (y, x, 1 - c, z)
    own = std.shape[0]
    third = go.shape[1] // 4
    wide = 3 * third
    two = 2 * third
    slab = 128

    fetches = [
        pltpu.make_async_copy(src, dst, fetched.at[i])
        for i, (src, dst) in enumerate((
            (part_hbm, part), (next_hbm, std), (grad_hbm, base), (out_hbm, w_out), (joined_hbm, dj), (mixed_hbm, mixed),
            (lhs_hbm, lhs), (weight_hbm, weight), (feed_in_hbm, f_other),
        ))
    ]
    for copy in fetches:
        copy.start()
    fetch_std = pltpu.make_async_copy(std_hbm, std, fetched.at[9])

    barrier = pltpu.get_barrier_semaphore()
    for dc in range(2):
        for dz in range(4):
            if dc or dz:
                pl.semaphore_signal(barrier, inc=1, device_id=(y, x, (c + dc) % 2, (z + dz) % 4), device_id_type=MESH)
    for peer in (near_y, near_x):
        pl.semaphore_signal(barrier, inc=1, device_id=peer, device_id_type=MESH)
    pl.semaphore_wait(barrier, 9)

    def remote(src, dst, send, recv, peer):
        return pltpu.make_async_remote_copy(
            src_ref=src, dst_ref=dst, send_sem=send, recv_sem=recv, device_id=peer, device_id_type=MESH
        )

    def at(i, length):
        return pl.ds(pl.multiple_of(i * length, length), length)

    def along(r):
        return (y, x, c, (z + r) % 4)

    def time_x(yb):
        return remote(time_hbm.at[at(2 * yb + 1 - x, BLK)], t_in.at[yb], tx_send.at[yb], tx_recv.at[yb], near_x)

    def time_keep(yb):
        return pltpu.make_async_copy(time_hbm.at[at(2 * yb + x, BLK)], t_own.at[yb], t_local.at[yb])

    def time_z(r):
        return remote(tz_out.at[r], tz_in.at[r], tz_send.at[r], tz_recv.at[r], along(1))

    def feed_y(r):
        s = (z + r) % 4
        return remote(feed_hbm.at[1 - y, s], f_in.at[r], fy_send.at[r], fy_recv.at[r], near_y)

    def feed_keep(r):
        return pltpu.make_async_copy(feed_hbm.at[y, (z + r) % 4], f_own.at[r], f_local.at[r])

    def feed_z(r):
        return remote(fz_out.at[r], fz_in.at[r], fz_send.at[r], fz_recv.at[r], along(1))

    for r in (3, 2, 1, 0):
        feed_y(r).start()
        feed_keep(r).start()
    for yb in range(2):
        time_x(yb).start()
        time_keep(yb).start()

    def feed_step(t):
        r = 3 - t
        feed_y(r).wait_recv()
        feed_keep(r).wait()
        total = f_own[r].astype(F32) + f_in[r].astype(F32)
        if t > 0:
            feed_z(t - 1).wait_recv()
            total = total + fz_in[t - 1].astype(F32)
        if t == 3:
            f_total[...] = total
        else:
            fz_out[t] = total.astype(BF16)
            feed_z(t).start()

    def time_step(t):
        if t == 0:
            for yb in range(2):
                time_x(yb).wait_recv()
                time_keep(yb).wait()
        else:
            time_z(t - 1).wait_recv()
        piece_at = at((z + 3 - t) % 4, BLK)
        for yb in range(2):
            total = t_own[yb, :, piece_at].astype(F32) + t_in[yb, :, piece_at].astype(F32)
            if t > 0:
                total = total + tz_in[t - 1, yb].astype(F32)
            if t == 3:
                t_total[yb] = total
            else:
                tz_out[t, yb] = total.astype(BF16)
        if t < 3:
            time_z(t).start()

    step = own // 2
    for copy in fetches[:3]:
        copy.wait()

    def norm_back(grad, standard, weights, inv):
        inner = grad * weights
        mean = jnp.mean(inner, axis=-1, keepdims=True)
        slope = jnp.mean(inner * standard, axis=-1, keepdims=True)
        return (inner - mean - standard * slope) * inv

    def after_time(i, total):
        rows = at(i, step)
        grad, standard = part[rows], std[rows]
        full = base[rows] + norm_back(grad, standard, gains[2:3], inverse_next[rows])
        base[rows] = full
        low_grads[rows] = full.astype(BF16)
        return total + jnp.sum(grad * standard, axis=0, keepdims=True)

    zero = jnp.zeros((1, std.shape[1]), F32)
    next_grad = lax.fori_loop(0, 2, after_time, zero)
    give = remote(low_grads.at[pl.ds(0, own)], low_grads.at[pl.ds(own, own)], g_send.at[0], g_recv.at[0], pair)
    give.start()
    fetch_std.start()
    for copy in fetches[3:6]:
        copy.wait()

    def attend(i, carry):
        rows = at(i, slab)
        for h in range(mixed.shape[1] // PAIR):
            places = [pl.ds((3 * h + j) * PAIR, PAIR) for j in range(3)]
            q, k, v = (dj[rows, place] for place in places)
            lines = [totals[i, 2 * h + j : 2 * h + j + 1, :] for j in range(2)]
            found = attend_pair_back(q, k, v, dmixed[rows, h * PAIR : (h + 1) * PAIR], lines, None, scale)
            for place, value in zip(places, found):
                dj[rows, place] = value.astype(BF16)
        return carry

    def turn(i, carry):
        turned[:, at(i, slab)] = low_grads[at(i, slab)].T
        return carry

    def attend_half(t, *between):
        rows = pl.ds(t * own, own)
        first, count = t * own // slab, own // slab
        dmixed[rows] = dot_nt(low_grads[rows], w_out[...]).astype(BF16)
        between[0]()
        lax.fori_loop(first, first + count // 2, attend, 0)
        between[1]()
        lax.fori_loop(first + count // 2, first + count, attend, 0)
        between[2]()
        lax.fori_loop(first, first + count, turn, 0)

    def nothing():
        pass

    attend_half(0, lambda: feed_step(0), nothing, lambda: feed_step(1))
    give.wait_recv()
    attend_half(1, nothing, lambda: feed_step(2), lambda: time_step(0))
    for copy in fetches[6:]:
        copy.wait()
    def away(i, carry):
        rows = pl.ds(pl.multiple_of(own + i * step, step), step)
        half_out[pl.ds(pl.multiple_of(i * step, step), step)] = dot_nt(dj[rows], weight[...]).astype(BF16)
        return carry

    lax.fori_loop(0, 2, away, 0)
    swap = remote(half_out, half_in, h_send.at[0], h_recv.at[0], pair)
    swap.start()

    def block(yb, xb):
        return pl.ds(pl.multiple_of(BLK * (2 * yb + xb), BLK), BLK)

    def a1(i):
        return remote(a1_out.at[i], a1_in.at[i], a1_send.at[i], a1_recv.at[i], near_x)

    def b1(i):
        return remote(b1_out.at[i], b1_in.at[i], b1_send.at[i], b1_recv.at[i], near_y)

    def a2(i):
        return remote(a2_out.at[i], a2_in.at[i], a2_send.at[i], a2_recv.at[i], near_y)

    def b2(i):
        return remote(b2_out.at[i], b2_in.at[i], b2_send.at[i], b2_recv.at[i], near_x)

    def to_z(r):
        return remote(z_out.at[r], z_in.at[r], z_send.at[r], z_recv.at[r], along(r))

    def piece(i, carry):
        s = (z + i + 1) % 4
        made = dot_nn(lhs[...], dj[:, pl.ds(pl.multiple_of(s * wide, third), wide)])
        grads[i, :, :wide] = made
        grads[i, :, wide:] = go[:, pl.ds(pl.multiple_of(s * third, third), third)].astype(F32)
        for b in range(2):
            a1_out[i, b] = grads[i, block(b, 1 - x), :two].astype(BF16)
            b1_out[i, b] = grads[i, block(1 - y, b), two:].astype(BF16)
        a1(i).start()
        b1(i).start()
        return carry


    def second(i):
        a1(i).wait_recv()
        a2_out[i] = (grads[i, block(1 - y, x), :two] + a1_in[i, 1 - y].astype(F32)).astype(BF16)
        a2(i).start()
        b1(i).wait_recv()
        b2_out[i] = (grads[i, block(y, 1 - x), two:] + b1_in[i, 1 - x].astype(F32)).astype(BF16)
        b2(i).start()
        grads[i, block(y, x), :two] = grads[i, block(y, x), :two] + a1_in[i, y].astype(F32)
        grads[i, block(y, x), two:] = grads[i, block(y, x), two:] + b1_in[i, x].astype(F32)

    def third_step(i):
        a2(i).wait_recv()
        b2(i).wait_recv()
        grads[i, block(y, x), :two] = grads[i, block(y, x), :two] + a2_in[i].astype(F32)
        grads[i, block(y, x), two:] = grads[i, block(y, x), two:] + b2_in[i].astype(F32)
        if i < 3:
            z_out[i + 1] = grads[i, block(y, x), :].astype(BF16)
            to_z(i + 1).start()

    fetch_std.wait()
    sums[...] = jnp.zeros_like(sums)
    sums[1:2] = next_grad
    sums[2:3] = later_grad[...]
    swap.wait_recv()

    def home(i, totals):
        rows = pl.ds(pl.multiple_of(i * step, step), step)
        grad = dot_nt(dj[rows], weight[...]) + half_in[rows].astype(F32)
        standard = std[rows]
        full = base[rows] + norm_back(grad, standard, gains[1:2], inverse[rows])
        hide = masked[rows] > 0.0
        ready[rows] = jnp.where(hide, 0.0, full).astype(BF16)
        return (
            totals[0] + jnp.sum(grad * standard, axis=0, keepdims=True),
            totals[1] + jnp.sum(jnp.where(hide, full, 0.0), axis=0, keepdims=True),
        )

    gain_grad, embed_grad = lax.fori_loop(0, 2, home, (zero, zero))
    sums[0:1] = gain_grad
    sums[3:4] = embed_grad

    def columns(s):
        return pl.ds(pl.multiple_of(s * BLK, BLK), BLK)

    def stays(k):
        return jnp.logical_and(z == k, z // 2 == c)

    def ride(k):
        slot = 2 * (z % 2) + c
        return remote(ready.at[:, columns(k)], rows_in.at[slot], r_send.at[k], r_recv.at[slot], (y, x, z // 2, k))

    def ride_local(k):
        return pltpu.make_async_copy(ready.at[:, columns(k)], rows_in.at[2 * (z % 2) + c], local.at[3])

    time_step(1)
    for k in range(4):
        pl.when(stays(k))(lambda k=k: ride_local(k).start())
        pl.when(jnp.logical_not(stays(k)))(lambda k=k: ride(k).start())
    go[...] = dot_nn(turned[...], mixed[...]).astype(BF16)
    lax.fori_loop(0, 4, piece, 0)

    def share(h):
        peer = (pair, near_y, near_x)[h]
        return remote(sum_out.at[h], sum_in.at[h], s_send.at[h], s_recv.at[h], peer)

    def begin_share(h):
        sum_out[h] = sums[...]
        share(h).start()

    def end_share(h):
        share(h).wait_recv()
        sums[...] = sums[...] + sum_in[h]

    begin_share(0)
    second(0)
    time_step(2)
    second(1)
    third_step(0)
    end_share(0)
    begin_share(1)
    second(2)
    third_step(1)
    end_share(1)
    begin_share(2)
    second(3)
    third_step(2)
    end_share(2)
    sum_out[3] = sums[...]

    def deal(r):
        s = (z + r) % 4
        return remote(sum_out.at[3, :, columns(s)], share_in.at[r], p_send.at[r], p_recv.at[r], (y, x, c, s))

    for r in (1, 2, 3):
        deal(r).start()
    third_step(3)
    parity = BLK // 2

    time_step(3)
    ty_out[...] = t_total[1 - y].astype(BF16)
    swap_y = remote(ty_out, ty_in, ty_send.at[0], ty_recv.at[0], near_y)
    swap_y.start()
    feed_step(3)
    fc_out[0] = f_other[at(1 - c, parity)].astype(BF16)
    fc_out[1] = f_total[at(1 - c, parity)].astype(BF16)
    swap_feed = remote(fc_out, fc_in, c_send.at[1], c_recv.at[1], pair)
    swap_feed.start()
    units = f_total.shape[1]
    feed_in_out[:, at(c, units)] = f_other[at(c, parity)]
    feed_out_out[at(c, units)] = f_total[at(c, parity)].T
    swap_y.wait_recv()
    tc_out[0] = t_total[y, at(1 - c, parity)].astype(BF16)
    tc_out[1] = ty_in[at(1 - c, parity)]
    swap_time = remote(tc_out, tc_in, c_send.at[2], c_recv.at[2], pair)
    swap_time.start()
    for k in range(4):
        pl.when(stays(k))(lambda k=k: ride_local(k).wait())
        from_self = jnp.logical_and(2 * c + k // 2 == z, c == k % 2)

        def landed(k=k):
            remote(ready.at[:, columns(k)], rows_in.at[k], r_send.at[k], r_recv.at[k], near_y).wait_recv()

        pl.when(jnp.logical_not(from_self))(landed)
    rows_out[...] = rows_in[...].astype(F32)
    for r in (1, 2, 3):
        to_z(r).wait_recv()
    total = grads[3, block(y, x), :]
    for r in (1, 2, 3):
        total = total + z_in[r].astype(F32)
    grads[3, block(y, x), :] = total
    rows = BLK // 2

    def core_rows(core):
        return pl.ds(pl.multiple_of(BLK * (2 * y + x) + rows * core, rows), rows)

    core_out[...] = grads[3, core_rows(1 - c), :].astype(BF16)
    last = remote(core_out, core_in, c_send.at[0], c_recv.at[0], pair)
    last.start()
    def place(core, value):
        for j in range(3):
            space_qkv[j, :, at(core, third)] = value[:, j * third : (j + 1) * third]
        space_out[at(core, third)] = value[:, 3 * third :].T

    place(c, grads[3, core_rows(c), :])
    result = sums[:, columns(z)]
    for r in (1, 2, 3):
        deal(r).wait_recv()
        result = result + share_in[r]
    small_out[...] = result
    swap_feed.wait_recv()
    feed_in_out[:, at(1 - c, units)] = fc_in[0].astype(F32)
    feed_out_out[at(1 - c, units)] = fc_in[1].astype(F32).T
    swap_time.wait_recv()
    mine = (t_total[y, at(c, parity)], ty_in[at(c, parity)].astype(F32))
    other = (tc_in[0].astype(F32), tc_in[1].astype(F32))
    by_head = []
    for yb in range(2):
        for cb in range(2):
            by_head.append(
                jnp.where(
                    c == cb,
                    jnp.where(y == yb, mine[0], mine[1]),
                    jnp.where(y == yb, other[0], other[1]),
                )
            )
    for j in range(4):
        made = jnp.concatenate([v[:, j * HEAD_DIM : (j + 1) * HEAD_DIM] for v in by_head], axis=1)
        if j < 3:
            time_qkv[j] = made
        else:
            time_out[...] = made.T
    last.wait_recv()
    place(1 - c, core_in[...].astype(F32))

    for copy in (last, swap, give, swap_y, swap_feed, swap_time):
        copy.wait_send()
    for yb in range(2):
        time_x(yb).wait_send()
    for r in range(4):
        feed_y(r).wait_send()
    for t in range(3):
        time_z(t).wait_send()
        feed_z(t).wait_send()
    for i in range(4):
        for copy in (a1(i), b1(i), a2(i), b2(i)):
            copy.wait_send()
    for r in (1, 2, 3):
        to_z(r).wait_send()
        deal(r).wait_send()
    for h in range(3):
        share(h).wait_send()
    for k in range(4):
        pl.when(jnp.logical_not(stays(k)))(lambda k=k: ride(k).wait_send())


def leave(
    part, std_next, grad, w_out, joined, mixed, lhs, weight, std, g_time, g_out, g_in,
    totals, inverse_next, inverse, masked, gains, later_grad, scale,
):
    own, features = std.shape
    cols4 = mixed.shape[1]
    quarter = cols4 // 4
    units = g_in.shape[1]
    dma = pltpu.SemaphoreType.DMA
    anywhere = pl.BlockSpec(memory_space=pl.ANY)
    whole = pl.BlockSpec(memory_space=pltpu.VMEM)
    parity = BLK // 2

    def low(*shape):
        return pltpu.VMEM(shape, BF16)

    def high(*shape):
        return pltpu.VMEM(shape, F32)

    return pl.pallas_call(
        functools.partial(leave_kernel, scale),
        in_specs=[anywhere] * 12 + [whole] * 6,
        out_specs=[whole] * 8,
        out_shape=[
            jax.ShapeDtypeStruct(shape, F32)
            for shape in (
                (3, parity, 2 * quarter), (2 * quarter, parity), (parity, 2 * units), (2 * units, parity),
                (3, parity, BLK), (BLK, parity), (4, own, BLK), (8, BLK),
            )
        ],
        scratch_shapes=[
            low(4, own, BLK),
            high(own, features), high(own, features), high(own, features), low(*w_out.shape), low(*joined.shape),
            low(*mixed.shape), low(*lhs.shape), low(*weight.shape), low(2 * own, features), low(features, 2 * own),
            low(*mixed.shape), low(features, cols4),
            low(2, BLK, features), low(2, BLK, features), low(4, 2, BLK, BLK), low(4, 2, BLK, BLK), high(2, BLK, BLK),
            low(BLK, BLK), low(BLK, BLK), low(2, parity, BLK), low(2, parity, BLK),
            low(4, BLK, units), low(4, BLK, units), low(4, BLK, units), low(4, BLK, units),
            high(BLK, units), high(BLK, units), low(2, parity, units), low(2, parity, units),
            high(4, features, cols4),
            low(4, 2, BLK, 2 * quarter), low(4, 2, BLK, 2 * quarter), low(4, 2, BLK, 2 * quarter), low(4, 2, BLK, 2 * quarter),
            low(4, BLK, 2 * quarter), low(4, BLK, 2 * quarter), low(4, BLK, 2 * quarter), low(4, BLK, 2 * quarter),
            low(4, BLK, cols4), low(4, BLK, cols4),
            low(own, features), low(own, features), low(own, features),
            low(parity, cols4), low(parity, cols4),
            high(8, features), high(4, 8, features), high(3, 8, features), high(4, 8, BLK),
        ]
        + [dma((4,))] * 10
        + [dma((1,)), dma((1,)), dma((4,)), dma((4,)), dma((3,)), dma((3,)), dma((3,)), dma((3,)), dma((4,)), dma((4,)), dma((4,))]
        + [dma((1,)), dma((1,)), dma((2,)), dma((2,)), dma((4,)), dma((4,)), dma((1,)), dma((1,))]
        + [dma((4,)), dma((4,)), dma((4,)), dma((4,)), dma((2,)), dma((4,)), dma((10,))],
        compiler_params=pltpu.CompilerParams(
            collective_id=3, has_side_effects=True, vmem_limit_bytes=62 * 1024 * 1024
        ),
        cost_estimate=pl.CostEstimate(flops=2 * 10**10, transcendentals=10**6, bytes_accessed=10**8),
        name="leave",
    )(
        part, std_next, grad, w_out, joined, mixed, lhs, weight, std, g_time, g_out, g_in,
        totals, inverse_next, inverse, masked, gains, later_grad,
    )


def tie(*values):
    return lax.optimization_barrier(values)


def norm_rows(resid):
    mean = jnp.mean(resid, axis=-1, keepdims=True)
    centered = resid - mean
    inverse = lax.rsqrt(jnp.mean(centered * centered, axis=-1, keepdims=True) + eps_norm)
    return (centered * inverse, inverse)


def norm_rows_back(grad, standardized, inverse, gain):
    gain_grad = jnp.sum(grad * standardized, axis=0)
    inner = grad * gain
    mean = jnp.mean(inner, axis=-1, keepdims=True)
    along = jnp.mean(inner * standardized, axis=-1, keepdims=True)
    return ((inner - mean - standardized * along) * inverse, gain_grad)


def cols(parts):
    return jnp.concatenate(parts, axis=1)


def rows_of(parts):
    return jnp.concatenate(parts, axis=0)


def token_parallel(
    tokens,
    cotangent,
    ratio,
    priority,
    frame_order,
    mask_embed,
    gains,
    qkv_space,
    out_space,
    qkv_time,
    out_time,
    w_in,
    w_out,
):
    scale = 1.0 / math.sqrt(HEAD_DIM)
    y, x, c, z = (lax.axis_index(name) for name in AXES)
    patches = tokens.shape[2]
    width = qkv_space.shape[0]
    frames_own = tokens.shape[0] * tokens.shape[1] // 4
    frames_all = frame_order.shape[1]
    own = frames_own * patches
    hidden_own = w_in.shape[1] // 2
    plane = 2 * y + x
    k_own = 2 * (z % 2) + c

    masked_here = (priority < ratio[:, None, None]).astype(jnp.int32).reshape(2, -1)
    info = cols([masked_here, frame_order])
    info = jnp.where(z // 2 == c, info, hop_c(info))
    info = lax.dynamic_index_in_dim(info, z % 2, 0, keepdims=False)
    masked = lax.dynamic_slice_in_dim(info, c * own, own, 0)[:, None] != 0
    order = info[2 * own :].reshape(2, 2, frames_own)
    order = jnp.where(y == 1, order[::-1], order)
    order = jnp.where(c == 1, order[:, ::-1], order).swapaxes(0, 1).reshape(frames_all)
    order = jnp.repeat(order, GROUP)
    patch = jnp.arange(frames_all * GROUP) % GROUP
    visible = (order[:, None] <= order[None, :]) & (patch[:, None] == patch[None, :])
    bias = jnp.where(visible, 0.0, -1e30).astype(F32)

    vectors = rows_of([mask_embed[None], gains, jnp.zeros((4, BLK), BF16)])
    head = (2 * y + c) * HEAD_DIM
    ti_own = cols(
        [
            lax.dynamic_slice_in_dim(qkv_time, head, HEAD_DIM, 2).reshape(width, -1),
            lax.dynamic_slice_in_dim(out_time, head, HEAD_DIM, 0).T,
        ]
    )
    (
        ws_qkv, ws_out, wt_all, wf_out, wf_in, joined0, turned0, std0,
        mixed0, total0, inv0, resid1, std1, inv1, normed1, vectors,
    ) = enter(
        tokens.reshape(4, own, BLK),
        vectors,
        jnp.swapaxes(qkv_space, 0, 1),
        out_space,
        ti_own,
        w_out,
        w_in,
        masked.astype(F32),
        scale,
    )

    half = qkv_space.shape[2] // 2
    turned1, joined1, mixed1, total1, delta, upstream, wf_far, wf_in_far = time_call(
        False,
        normed1.reshape(frames_own, patches, width),
        cotangent.reshape(4, own, BLK),
        [wf_out, wf_in],
        wt_all,
        bias,
        scale,
    )
    w_in_half, w_out_half, grad2, grad2_low, block_rows, gain_grad2 = feed(
        resid1, delta.reshape(own, width), upstream, masked.astype(F32), vectors, wf_in, wf_in_far, wf_out, wf_far
    )

    part1, g_time, g_w_in, block_out = time_call(
        True,
        grad2_low.reshape(frames_own, patches, width),
        block_rows,
        [joined1, total1, w_in_half, turned1, mixed1],
        wt_all,
        bias,
        scale,
    )
    block_out = block_out.reshape(tokens.shape)
    grad_qkv_space, grad_out_space, grad_w_in, grad_w_out, grad_qkv_time, grad_out_time, grad_tokens, small = leave(
        part1.reshape(own, width), std1, grad2, ws_out, joined0, mixed0, turned0, ws_qkv, std0, g_time, w_out_half, g_w_in,
        total0, inv1, inv0, masked.astype(F32), vectors, gain_grad2, scale,
    )
    small = small[:4]
    return (
        block_out,
        grad_tokens.reshape(tokens.shape),
        small[3],
        small[:3],
        jnp.swapaxes(grad_qkv_space, 0, 1),
        grad_out_space,
        jnp.swapaxes(grad_qkv_time, 0, 1),
        grad_out_time,
        grad_w_in,
        grad_w_out,
    )


def solution(mesh):
    sizes = (mesh.shape["tm"], mesh.shape["clip"], mesh.shape["mp"])
    if sizes == (2, 4, 4):
        mesh = jax.sharding.Mesh(mesh.devices.reshape(2, 2, 2, 4), AXES)
        step, clip = token_parallel, ("x", "c")
    else:
        step, clip = shards, ("clip",)
    return jax.shard_map(
        step,
        mesh=mesh,
        in_specs=(
            P(clip, "tm", None, "mp"),
            P(clip, "tm", None, "mp"),
            P(clip),
            P(clip, "tm", None),
            P(clip, None),
            P("mp"),
            P(None, "mp"),
            P(None, None, "mp"),
            P("mp", None),
            P(None, None, "mp"),
            P("mp", None),
            P(None, "mp"),
            P("mp", None),
        ),
        out_specs=(
            P(clip, "tm", None, "mp"),
            P(clip, "tm", None, "mp"),
            P("mp"),
            P(None, "mp"),
            P(("tm",) + clip, None, "mp"),
            P("mp", ("tm",) + clip),
            P(("tm",) + clip, None, "mp"),
            P("mp", ("tm",) + clip),
            P(("tm",) + clip, "mp"),
            P("mp", ("tm",) + clip),
        ),
        check_vma=False,
    )
```

```python
import functools
import math

import jax
import jax.numpy as jnp
from jax import lax
from jax.experimental import pallas as pl
from jax.experimental.pallas import tpu as pltpu
from jax.sharding import PartitionSpec as P

HEAD_DIM = 64
MICRO = 2


eps_norm = 1e-05


def gelu_tanh(values):
    return jax.nn.gelu(values, approximate=True)


def norm_forward_pass(residual_stream, gain_coefficients, complete_width):
    reduced_totals = lax.psum(
        (jnp.sum(residual_stream, axis=-1), jnp.sum(residual_stream * residual_stream, axis=-1)),
        "mp",
    )
    centered_rows = reduced_totals[0] / complete_width
    spread = reduced_totals[1] / complete_width - centered_rows * centered_rows
    inverse_scale = lax.rsqrt(spread + eps_norm)
    standardized_rows = (residual_stream - centered_rows[:, None]) * inverse_scale[:, None]
    shard_rows = (standardized_rows * gain_coefficients).astype(jnp.bfloat16)
    normalized_rows = lax.all_gather(shard_rows, "mp", axis=1, tiled=True)
    return (normalized_rows, standardized_rows, inverse_scale)


def norm_reverse_pass(
    normalized_gradient, standardized_rows, inverse_scale, gain_coefficients, complete_width
):
    gain_gradient = jnp.sum(normalized_gradient * standardized_rows, axis=0)
    standardized_gradient = normalized_gradient * gain_coefficients
    reduced_totals = lax.psum(
        (
            jnp.sum(standardized_gradient, axis=-1),
            jnp.sum(standardized_gradient * standardized_rows, axis=-1),
        ),
        "mp",
    )
    grad_resid = (
        standardized_gradient
        - reduced_totals[0][:, None] / complete_width
        - standardized_rows * (reduced_totals[1][:, None] / complete_width)
    ) * inverse_scale[:, None]
    return (grad_resid, gain_gradient)


def sum_features(grad_full):
    return lax.psum_scatter(
        grad_full.astype(jnp.bfloat16), "mp", scatter_dimension=1, tiled=True
    ).astype(jnp.float32)


def branch_out(hidden, weight):
    partial_rows = jnp.dot(hidden, weight, preferred_element_type=jnp.float32)
    return lax.psum_scatter(partial_rows, "mp", scatter_dimension=1, tiled=True)


def branch_back(grad_resid, hidden, weight):
    grad_rows = lax.all_gather(grad_resid.astype(jnp.bfloat16), "mp", axis=1, tiled=True)
    weight_grad = jnp.einsum("rk,rd->kd", hidden, grad_rows, preferred_element_type=jnp.float32)
    grad_hidden = jnp.einsum("rd,kd->rk", grad_rows, weight, preferred_element_type=jnp.float32)
    return (grad_hidden, weight_grad)


def qkv_back(normalized_rows, grad_joined, weight):
    weight_grad = jnp.einsum(
        "rd,trk->dtk", normalized_rows, grad_joined, preferred_element_type=jnp.float32
    )
    grad_full = jnp.einsum("trk,dtk->rd", grad_joined, weight, preferred_element_type=jnp.float32)
    return (weight_grad, sum_features(grad_full))


def reduce_grads(local_grads, small_grads):
    reduced = (
        lax.psum_scatter(local_grads[0], ("tm", "clip"), scatter_dimension=0, tiled=True),
        lax.psum_scatter(local_grads[1], ("tm", "clip"), scatter_dimension=1, tiled=True),
        lax.psum_scatter(local_grads[2], ("tm", "clip"), scatter_dimension=0, tiled=True),
        lax.psum_scatter(local_grads[3], ("tm", "clip"), scatter_dimension=1, tiled=True),
        lax.psum_scatter(local_grads[4], ("tm", "clip"), scatter_dimension=0, tiled=True),
        lax.psum_scatter(local_grads[5], ("tm", "clip"), scatter_dimension=1, tiled=True),
    )
    reduced_small = lax.psum((small_grads[0], small_grads[1]), ("tm", "clip"))
    return (reduced, reduced_small)


def space_forward(normalized_rows, weight, frame_count, patches, heads_local, scale):
    joined = jnp.einsum(
        "rd,dtk->trk", normalized_rows, weight, preferred_element_type=jnp.float32
    ).astype(jnp.bfloat16)
    shape_heads = (frame_count, patches, heads_local, HEAD_DIM)
    scores = (
        jnp.einsum(
            "bshd,bthd->bhst",
            joined[0].reshape(shape_heads),
            joined[1].reshape(shape_heads),
            preferred_element_type=jnp.float32,
        )
        * scale
    )
    highest = jnp.max(scores, axis=-1, keepdims=True)
    exponent = jnp.exp(scores - highest)
    reduced_totals = jnp.sum(exponent, axis=-1, keepdims=True)
    log_total = highest + jnp.log(reduced_totals)
    attention = (exponent / reduced_totals).astype(jnp.bfloat16)
    mixed = jnp.einsum(
        "bhst,bthd->bshd",
        attention,
        joined[2].reshape(shape_heads),
        preferred_element_type=jnp.float32,
    )
    return (
        joined,
        log_total,
        mixed.astype(jnp.bfloat16).reshape(frame_count * patches, heads_local * HEAD_DIM),
    )


def space_backward(grad_mixed, joined, log_total, frame_count, patches, heads_local, scale):
    shape_heads = (frame_count, patches, heads_local, HEAD_DIM)
    queries = joined[0].reshape(shape_heads)
    key_rows = joined[1].reshape(shape_heads)
    values = joined[2].reshape(shape_heads)
    grad_out = grad_mixed.reshape(shape_heads)
    scores = (
        jnp.einsum("bshd,bthd->bhst", queries, key_rows, preferred_element_type=jnp.float32) * scale
    )
    attention = jnp.exp(scores - log_total)
    grad_values = jnp.einsum(
        "bhst,bshd->bthd",
        attention.astype(jnp.bfloat16),
        grad_out,
        preferred_element_type=jnp.float32,
    )
    grad_att = jnp.einsum("bshd,bthd->bhst", grad_out, values, preferred_element_type=jnp.float32)
    grad_scores = (
        attention * (grad_att - jnp.sum(attention * grad_att, axis=-1, keepdims=True))
    ).astype(jnp.bfloat16)
    grad_queries = (
        jnp.einsum("bhst,bthd->bshd", grad_scores, key_rows, preferred_element_type=jnp.float32)
        * scale
    )
    grad_keys = (
        jnp.einsum("bhst,bshd->bthd", grad_scores, queries, preferred_element_type=jnp.float32)
        * scale
    )
    row_count = frame_count * patches
    stacked = jnp.stack(
        [
            grad_queries.reshape(row_count, -1),
            grad_keys.reshape(row_count, -1),
            grad_values.reshape(row_count, -1),
        ]
    )
    return stacked.astype(jnp.bfloat16)


def time_scores(queries, keys_all, visible, scale):
    scores = (
        jnp.einsum("cfshd,cgshd->chfgs", queries, keys_all, preferred_element_type=jnp.float32)
        * scale
    )
    return jnp.where(visible, scores, -1e30)


def time_forward(queries, keys_all, values_all, visible, scale):
    scores = time_scores(queries, keys_all, visible, scale)
    highest = jnp.max(scores, axis=3, keepdims=True)
    exponent = jnp.exp(scores - highest)
    reduced_totals = jnp.sum(exponent, axis=3, keepdims=True)
    log_total = highest + jnp.log(reduced_totals)
    attention = (exponent / reduced_totals).astype(jnp.bfloat16)
    mixed = jnp.einsum(
        "chfgs,cgshd->cfshd", attention, values_all, preferred_element_type=jnp.float32
    )
    return (log_total, mixed.astype(jnp.bfloat16))


def time_backward(grad_mixed, queries, keys_all, values_all, visible, log_total, scale):
    grad_out = grad_mixed.reshape(queries.shape)
    scores = time_scores(queries, keys_all, visible, scale)
    attention = jnp.exp(scores - log_total)
    grad_values = jnp.einsum(
        "chfgs,cfshd->cgshd",
        attention.astype(jnp.bfloat16),
        grad_out,
        preferred_element_type=jnp.float32,
    )
    grad_att = jnp.einsum(
        "cfshd,cgshd->chfgs", grad_out, values_all, preferred_element_type=jnp.float32
    )
    grad_scores = (
        attention * (grad_att - jnp.sum(attention * grad_att, axis=3, keepdims=True))
    ).astype(jnp.bfloat16)
    grad_queries = (
        jnp.einsum("chfgs,cgshd->cfshd", grad_scores, keys_all, preferred_element_type=jnp.float32)
        * scale
    )
    grad_keys = (
        jnp.einsum("chfgs,cfshd->cgshd", grad_scores, queries, preferred_element_type=jnp.float32)
        * scale
    )
    return (grad_queries, grad_keys, grad_values)


def shards(
    tokens,
    cotangent,
    ratio,
    priority,
    frame_order,
    mask_embed,
    gains,
    qkv_space,
    out_space,
    qkv_time,
    out_time,
    w_in,
    w_out,
):
    scale = 1.0 / math.sqrt(HEAD_DIM)
    clips_local = tokens.shape[0] // MICRO
    frames_local = tokens.shape[1]
    patches = tokens.shape[2]
    cols_local = tokens.shape[3]
    frames_all = frame_order.shape[1]
    hidden_width = qkv_space.shape[0]
    joined_local = qkv_space.shape[2]
    heads_local = joined_local // HEAD_DIM
    row_count = clips_local * frames_local * patches
    gain_broadcast = gains.astype(jnp.float32)
    embed_row = mask_embed.astype(jnp.float32)
    first_frame = lax.axis_index("tm") * frames_local
    shape_local = (clips_local, frames_local, patches, joined_local)
    shape_heads = (clips_local, frames_local, patches, heads_local, HEAD_DIM)
    shape_all = (clips_local, frames_all, patches, heads_local, HEAD_DIM)
    outputs = []
    input_grads = []
    weight_total = None
    small_total = None
    for batch_index in range(MICRO):
        lower = batch_index * clips_local
        upper = lower + clips_local
        source = tokens[lower:upper].reshape(row_count, cols_local).astype(jnp.float32)
        upstream = cotangent[lower:upper].reshape(row_count, cols_local).astype(jnp.float32)
        masked = (priority[lower:upper] < ratio[lower:upper][:, None, None]).reshape(row_count)
        order_rows = frame_order[lower:upper]
        residual_stream0 = jnp.where(masked[:, None], embed_row[None, :], source)
        normalized_rows0, standardized_rows0, inverse_deviation0 = norm_forward_pass(
            residual_stream0, gain_broadcast[0], hidden_width
        )
        joined0, total0, mixed0 = space_forward(
            normalized_rows0, qkv_space, clips_local * frames_local, patches, heads_local, scale
        )
        residual_stream1 = residual_stream0 + branch_out(mixed0, out_space)
        normalized_rows1, standardized_rows1, inverse_deviation1 = norm_forward_pass(
            residual_stream1, gain_broadcast[1], hidden_width
        )
        joined1 = jnp.einsum(
            "rd,dtk->trk", normalized_rows1, qkv_time, preferred_element_type=jnp.float32
        ).astype(jnp.bfloat16)
        queries_local = joined1[0].reshape(shape_local)
        keys_local = joined1[1].reshape(shape_local)
        values_local = joined1[2].reshape(shape_local)
        keys_all, values_all = (
            lax.all_gather(keys_local, "tm", axis=1, tiled=True),
            lax.all_gather(values_local, "tm", axis=1, tiled=True),
        )
        query_order = lax.dynamic_slice_in_dim(order_rows, first_frame, frames_local, axis=1)
        time_visible = (order_rows[:, None, :] <= query_order[:, :, None])[:, None, :, :, None]
        time_q = queries_local.reshape(shape_heads)
        time_k = keys_all.reshape(shape_all)
        time_v = values_all.reshape(shape_all)
        total1, mixed_frames = time_forward(time_q, time_k, time_v, time_visible, scale)
        mixed1 = mixed_frames.reshape(row_count, joined_local)
        residual_stream2 = residual_stream1 + branch_out(mixed1, out_time)
        normalized_rows2, standardized_rows2, inverse_deviation2 = norm_forward_pass(
            residual_stream2, gain_broadcast[2], hidden_width
        )
        projected = jnp.dot(normalized_rows2, w_in, preferred_element_type=jnp.float32)
        activated, gelu_pull = jax.vjp(gelu_tanh, projected)
        hidden = activated.astype(jnp.bfloat16)
        resid3 = residual_stream2 + branch_out(hidden, w_out)
        outputs.append(
            resid3.astype(jnp.bfloat16).reshape(clips_local, frames_local, patches, cols_local)
        )
        grad3 = jnp.where(masked[:, None], upstream, 0.0)
        grad_hidden, grad_w_out = branch_back(grad3, hidden, w_out)
        grad_inner = gelu_pull(grad_hidden)[0].astype(jnp.bfloat16)
        grad_w_in = jnp.einsum(
            "rd,rk->dk", normalized_rows2, grad_inner, preferred_element_type=jnp.float32
        )
        normalized_gradient2 = sum_features(
            jnp.einsum("rk,dk->rd", grad_inner, w_in, preferred_element_type=jnp.float32)
        )
        backward_third, gain_gradient2 = norm_reverse_pass(
            normalized_gradient2,
            standardized_rows2,
            inverse_deviation2,
            gain_broadcast[2],
            hidden_width,
        )
        grad2 = grad3 + backward_third
        grad_mixed1, grad_out_time = branch_back(grad2, mixed1, out_time)
        grad_mixed_low = grad_mixed1.astype(jnp.bfloat16).reshape(shape_local)
        grad_queries, grad_keys, grad_values = time_backward(
            grad_mixed_low, time_q, time_k, time_v, time_visible, total1, scale
        )
        key_part, value_part = (
            lax.psum_scatter(
                grad_keys.reshape(clips_local, frames_all, patches, joined_local).astype(
                    jnp.bfloat16
                ),
                "tm",
                scatter_dimension=1,
                tiled=True,
            ).astype(jnp.float32),
            lax.psum_scatter(
                grad_values.reshape(clips_local, frames_all, patches, joined_local).astype(
                    jnp.bfloat16
                ),
                "tm",
                scatter_dimension=1,
                tiled=True,
            ).astype(jnp.float32),
        )
        grad_joined1 = jnp.stack(
            [
                grad_queries.reshape(row_count, joined_local),
                key_part.reshape(row_count, joined_local),
                value_part.reshape(row_count, joined_local),
            ]
        ).astype(jnp.bfloat16)
        grad_qkv_time, normalized_gradient1 = qkv_back(normalized_rows1, grad_joined1, qkv_time)
        backward_second, gain_gradient1 = norm_reverse_pass(
            normalized_gradient1,
            standardized_rows1,
            inverse_deviation1,
            gain_broadcast[1],
            hidden_width,
        )
        grad1 = grad2 + backward_second
        grad_mixed0, grad_out_space = branch_back(grad1, mixed0, out_space)
        grad_joined0 = space_backward(
            grad_mixed0.astype(jnp.bfloat16),
            joined0,
            total0,
            clips_local * frames_local,
            patches,
            heads_local,
            scale,
        )
        grad_qkv_space, normalized_gradient0 = qkv_back(normalized_rows0, grad_joined0, qkv_space)
        backward_first, gain_gradient0 = norm_reverse_pass(
            normalized_gradient0,
            standardized_rows0,
            inverse_deviation0,
            gain_broadcast[0],
            hidden_width,
        )
        grad0 = grad1 + backward_first
        input_grads.append(
            jnp.where(masked[:, None], 0.0, grad0).reshape(
                clips_local, frames_local, patches, cols_local
            )
        )
        grad_embed = jnp.sum(jnp.where(masked[:, None], grad0, 0.0), axis=0)
        gain_grads = jnp.stack([gain_gradient0, gain_gradient1, gain_gradient2])
        local_grads = (
            grad_qkv_space,
            grad_out_space,
            grad_qkv_time,
            grad_out_time,
            grad_w_in,
            grad_w_out,
        )
        small_grads = (gain_grads, grad_embed)
        reduced, reduced_small = reduce_grads(local_grads, small_grads)
        if weight_total is None:
            weight_total = reduced
            small_total = reduced_small
        else:
            weight_total = tuple((total + grad for total, grad in zip(weight_total, reduced)))
            small_total = tuple((total + grad for total, grad in zip(small_total, reduced_small)))
    return (
        jnp.concatenate(outputs, axis=0),
        jnp.concatenate(input_grads, axis=0),
        small_total[1],
        small_total[0],
        weight_total[0],
        weight_total[1],
        weight_total[2],
        weight_total[3],
        weight_total[4],
        weight_total[5],
    )


AXES = ("tm", "x", "c", "mp")
F32 = jnp.float32
BF16 = jnp.bfloat16
BLK = 256
MESH = pl.DeviceIdType.MESH


def device_pairs(move):
    pairs = []
    for y in range(2):
        for x in range(2):
            for c in range(2):
                for z in range(4):
                    there = move(y, x, c, z)
                    pairs.append(tuple(((q[0] * 2 + q[1]) * 2 + q[2]) * 4 + q[3] for q in ((y, x, c, z), there)))
    return pairs


def hop_y(v):
    return lax.ppermute(v, AXES, device_pairs(lambda y, x, c, z: (1 - y, x, c, z)))


def hop_x(v):
    return lax.ppermute(v, AXES, device_pairs(lambda y, x, c, z: (y, 1 - x, c, z)))


def hop_c(v):
    return lax.ppermute(v, AXES, device_pairs(lambda y, x, c, z: (y, x, 1 - c, z)))


def hop_z(v, shift):
    return lax.ppermute(v, AXES, device_pairs(lambda y, x, c, z: (y, x, c, (z + shift) % 4)))


def spread_pairs(r):
    def move(y, x, c, z):
        k = z ^ r
        return (y, x, k & 1, 2 * c + (k >> 1))

    return device_pairs(move)


def dot_nn(a, b):
    return lax.dot_general(a, b, (((1,), (0,)), ((), ())), preferred_element_type=F32)


def dot_nt(a, b):
    return lax.dot_general(a, b, (((1,), (1,)), ((), ())), preferred_element_type=F32)


def dot_tn(a, b):
    return lax.dot_general(a, b, (((0,), (0,)), ((), ())), preferred_element_type=F32)


def attend_pair(q, k, v, bias, scale):
    mixed, totals = [], []
    for i in range(2):
        mine = slice(i * HEAD_DIM, (i + 1) * HEAD_DIM)
        scores = dot_nt(k[:, mine], q[:, mine]) * scale
        if bias is not None:
            scores = scores + bias
        highest = jnp.max(scores, axis=0, keepdims=True)
        exponent = jnp.exp(scores - highest)
        total = jnp.sum(exponent, axis=0, keepdims=True)
        totals.append(highest + jnp.log(total))
        mixed.append(dot_tn(v[:, mine], exponent.astype(BF16)) * (1.0 / total))
    return (jnp.concatenate(mixed, axis=0).T, totals)


def attend_pair_back(q, k, v, g, totals, bias, scale):
    grads = ([], [], [])
    for i in range(2):
        mine = slice(i * HEAD_DIM, (i + 1) * HEAD_DIM)
        scores = dot_nt(k[:, mine], q[:, mine]) * scale
        if bias is not None:
            scores = scores + bias
        p = jnp.exp(scores - totals[i])
        dp = dot_nt(v[:, mine], g[:, mine])
        ds = (p * (dp - jnp.sum(p * dp, axis=0, keepdims=True))).astype(BF16)
        grads[0].append(dot_tn(k[:, mine], ds) * scale)
        grads[1].append(dot_nn(ds, q[:, mine]) * scale)
        grads[2].append(dot_nn(p.astype(BF16), g[:, mine]))
    return (
        jnp.concatenate(grads[0], axis=0).T,
        jnp.concatenate(grads[1], axis=1),
        jnp.concatenate(grads[2], axis=1),
    )


PAIR = 2 * HEAD_DIM


def enter_kernel(
    scale,
    tok, vec, qkv_hbm, out_hbm, later, feed_hbm, first_hbm, masked,
    wq_out, wo_out, wt, wf, wi, joined_out, turned_out, std_out,
    mixed, total_out, inverse, resid_out, next_out, inverse_next, low_out, vec_out,
    rows_in, vec_in, wq, wo, normed, joined, turned, std, base, part, part_out, part_in, resid, std_next, low_next,
    z_send, z_recv, y_send, y_recv, x_send, x_recv, p_send, p_recv, q_send, q_recv,
    t_send, t_recv, v_send, v_recv, u_send, u_recv, w_send, w_recv,
    f_send, f_recv, g_send, g_recv, n_send, n_recv, local, saved,
    i_send, i_recv, j_send, j_recv, k_send, k_recv, l_send, l_recv,
):
    y, x, c, z = (lax.axis_index(name) for name in AXES)
    half = wo.shape[0] // 4
    wide = 3 * half
    span = wt.shape[1] // 4
    size = wf.shape[1] // 4
    own = rows_in.shape[0]
    near_y, near_x, pair = (1 - y, x, c, z), (y, 1 - x, c, z), (y, x, 1 - c, z)
    right_z, left_z = (y, x, c, (z + 1) % 4), (y, x, c, (z + 3) % 4)

    def at(i, length):
        return pl.ds(pl.multiple_of(i * length, length), length)

    def remote(src, dst, send, recv, peer):
        return pltpu.make_async_remote_copy(
            src_ref=src, dst_ref=dst, send_sem=send, recv_sem=recv, device_id=peer, device_id_type=MESH
        )

    def start(all_copies):
        for copy in all_copies:
            copy.start()

    def landed(all_copies):
        for copy in all_copies:
            copy.wait_recv()

    def sent(all_copies):
        for copy in all_copies:
            copy.wait_send()

    core = at(c, half)
    keep = [
        pltpu.make_async_copy(
            qkv_hbm.at[j, :, core], wq.at[:, pl.ds(pl.multiple_of(z * wide + j * half, half), half)], local.at[j]
        )
        for j in range(3)
    ] + [pltpu.make_async_copy(out_hbm.at[core], wo.at[at(z, half)], local.at[3])]
    keep_later = [
        pltpu.make_async_copy(later, wt.at[:, at(z, span)], local.at[4]),
        pltpu.make_async_copy(feed_hbm.at[at(c, 4 * size)], wf.at[z], local.at[5]),
        pltpu.make_async_copy(first_hbm.at[:, at(c, 4 * size)], wi.at[z], local.at[8]),
    ]
    start(keep + keep_later)

    barrier = pltpu.get_barrier_semaphore()
    for dc in range(2):
        for dz in range(4):
            if dc or dz:
                peer = (y, x, (c + dc) % 2, (z + dz) % 4)
                pl.semaphore_signal(barrier, inc=1, device_id=peer, device_id_type=MESH)
    for peer in (near_y, near_x):
        pl.semaphore_signal(barrier, inc=1, device_id=peer, device_id_type=MESH)
    pl.semaphore_wait(barrier, 9)

    def spot(dy, dx):
        return 2 * ((y + dy) % 2) + (x + dx) % 2

    def piece(dy, dx, r, split=False):
        s = (z + r) % 4
        rows = at(spot(dy, dx), BLK)
        first = pl.multiple_of(s * wide, half)
        out = wo.at[at(s, half), at(spot(dy, dx), BLK)]
        if split:
            last = pl.multiple_of(s * wide + 2 * half, half)
            return (wq.at[rows, pl.ds(first, 2 * half)], wq.at[rows, pl.ds(last, half)], out)
        return (wq.at[rows, pl.ds(first, wide)], out)

    def time_piece(dx, r):
        return wt.at[at((x + dx) % 2, 2 * BLK), at((z + r) % 4, span)]

    def feed_piece(dy, r):
        return wf.at[(z + r) % 4, at(spot(dy, 0), size)]

    def copies(parts, send, recv, peer):
        return [remote(ref, ref, send.at[i], recv.at[i], peer) for i, ref in enumerate(parts)]

    def leg(right, step):
        if right:
            return (0 if step == 0 else 4 - step), right_z, 3 - step
        return step, left_z, step + 1

    def z_copies(right, step):
        r, peer, lands = leg(right, step)
        return copies(piece(0, 0, r), z_send.at[int(right), step], z_recv.at[lands], peer)

    def time_z(right, step):
        r, peer, lands = leg(right, step)
        source = later.at[at(x, 2 * BLK)] if step == 0 else time_piece(0, r)
        return [remote(source, time_piece(0, r), u_send.at[int(right), step], u_recv.at[lands], peer)]

    def feed_z(right, step):
        r, peer, lands = leg(right, step)
        source = feed_hbm.at[at(4 * c + spot(0, 0), size)] if step == 0 else feed_piece(0, r)
        return [remote(source, feed_piece(0, r), f_send.at[int(right), step], f_recv.at[lands], peer)]

    def first_piece(dy, dx, r):
        return wi.at[(z + r) % 4, at(spot(dy, dx), BLK)]

    def first_z(right, step):
        r, peer, lands = leg(right, step)
        source = first_hbm.at[at(spot(0, 0), BLK), at(c, 4 * size)] if step == 0 else first_piece(0, 0, r)
        return [remote(source, first_piece(0, 0, r), i_send.at[int(right), step], i_recv.at[lands], peer)]

    def first_y(r, dy=0):
        return [remote(first_piece(dy, 0, r), first_piece(dy, 0, r), j_send.at[r], j_recv.at[r], near_y)]

    def first_x(r, dx=0):
        return [remote(first_piece(0, dx, r), first_piece(0, dx, r), k_send.at[r], k_recv.at[r], near_x)]

    def y_copies(r, dy=0):
        return copies(piece(dy, 0, r), y_send.at[r], y_recv.at[r], near_y)

    def x_copies(r, dx=0):
        return copies(piece(0, dx, r), x_send.at[r], x_recv.at[r], near_x)

    def corner_x(r, dx=0):
        return copies(piece(1, dx, r, split=True)[:1], p_send.at[r], p_recv.at[r], near_x)

    def corner_y(r, dy=0):
        return copies(piece(dy, 1, r, split=True)[1:], q_send.at[r], q_recv.at[r], near_y)

    def time_x(r, dx=0):
        return [remote(time_piece(dx, r), time_piece(dx, r), w_send.at[r], w_recv.at[r], near_x)]

    def feed_y(r, dy=0):
        return [remote(feed_piece(dy, r), feed_piece(dy, r), g_send.at[r], g_recv.at[r], near_y)]

    def token_copies(k):
        peer = (y, x, k % 2, 2 * c + k // 2)
        return [
            remote(tok.at[k], rows_in.at[:, at(z, BLK)], t_send.at[k], t_recv.at[z], peer),
            remote(vec, vec_in.at[:, at(z, BLK)], v_send.at[k], v_recv.at[z], peer),
        ]

    def token_local(k):
        return [
            pltpu.make_async_copy(tok.at[k], rows_in.at[:, at(z, BLK)], local.at[6]),
            pltpu.make_async_copy(vec, vec_in.at[:, at(z, BLK)], local.at[7]),
        ]

    def stays(k):
        return jnp.logical_and(2 * c + k // 2 == z, c == k % 2)

    def start_tokens(ks):
        for k in ks:
            pl.when(stays(k))(lambda k=k: start(token_local(k)))
            pl.when(jnp.logical_not(stays(k)))(lambda k=k: start(token_copies(k)))

    def each_side(j, act):
        pl.when(z >= j + 1)(lambda: act(3 - j, True))
        pl.when(z <= 2 - j)(lambda: act(j + 1, False))

    def begin(make):
        pl.when(z < 3)(lambda: start(make(True, 0)))
        pl.when(z > 0)(lambda: start(make(False, 0)))

    def onward(j, make, right):
        if j < 2:
            pl.when(z < 3 if right else z > 0)(lambda: start(make(right, j + 1)))

    def forward(j):
        def act(r, right):
            landed(copies(piece(0, 0, r), z_send.at[0, 0], z_recv.at[r], near_y))
            onward(j, z_copies, right)
            start(y_copies(r))
            start(x_copies(r))

        each_side(j, act)

    def corners(j):
        def act(r, right):
            landed(y_copies(r, 1))
            start(corner_x(r))
            landed(x_copies(r, 1))
            start(corner_y(r))

        each_side(j, act)

    def time_forward_step(j):
        def act(r, right):
            landed([remote(time_piece(0, r), time_piece(0, r), u_send.at[0, 0], u_recv.at[r], near_x)])
            onward(j, time_z, right)
            start(time_x(r))

        each_side(j, act)

    def feed_forward_step(j):
        def act(r, right):
            landed([remote(feed_piece(0, r), feed_piece(0, r), f_send.at[0, 0], f_recv.at[r], near_y)])
            onward(j, feed_z, right)
            start(feed_y(r))

        each_side(j, act)

    def first_corner_copy(r, dx=0):
        return [remote(first_piece(1, dx, r), first_piece(1, dx, r), l_send.at[r], l_recv.at[r], near_x)]

    def first_corner(j):
        def act(r, right):
            landed(first_y(r, 1))
            start(first_corner_copy(r))

        each_side(j, act)

    def first_forward_step(j):
        def act(r, right):
            landed([remote(first_piece(0, 0, r), first_piece(0, 0, r), i_send.at[0, 0], i_recv.at[r], near_y)])
            onward(j, first_z, right)
            start(first_y(r))
            start(first_x(r))

        each_side(j, act)

    for copy in keep:
        copy.wait()
    begin(z_copies)
    forward(0)
    start_tokens((0, 1))
    forward(1)
    start_tokens((2, 3))
    begin(first_z)
    begin(time_z)
    begin(feed_z)
    corners(0)
    forward(2)
    corners(1)
    for k in range(4):
        def finish_local(k=k):
            for copy in token_local(k):
                copy.wait()

        pl.when(stays(k))(finish_local)
    for s in range(4):
        def arrived(s=s):
            landed([
                remote(tok.at[0], rows_in.at[:, at(s, BLK)], t_send.at[0], t_recv.at[s], near_y),
                remote(vec, vec_in.at[:, at(s, BLK)], v_send.at[0], v_recv.at[s], near_y),
            ])

        pl.when(jnp.logical_not(jnp.logical_and(z == s, z // 2 == c)))(arrived)

    step = own // 2
    slab = 128
    vec_out[...] = vec_in[...].astype(F32)

    def first_norm(i, carry):
        rows = at(i, step)
        value = jnp.where(masked[rows] > 0.0, vec_out[0:1], rows_in[rows].astype(F32))
        base[rows] = value
        standard, inv = norm_rows(value)
        std[rows] = standard
        inverse[rows] = inv
        normed[rows] = (standard * vec_out[1:2]).astype(BF16)
        return carry

    lax.fori_loop(0, 2, first_norm, 0)
    give_normed = remote(normed.at[pl.ds(0, own)], normed.at[pl.ds(own, own)], n_send.at[0], n_recv.at[0], pair)
    give_normed.start()
    corners(2)

    def turn(i, carry):
        turned[:, at(i, slab)] = normed[at(i, slab)].T
        return carry

    lax.fori_loop(0, own // slab, turn, 0)
    for r in (1, 2, 3):
        landed(corner_x(r, 1))
        landed(corner_y(r, 1))
    saves = [
        pltpu.make_async_copy(wq, wq_out, saved.at[0]),
        pltpu.make_async_copy(wo, wo_out, saved.at[1]),
        pltpu.make_async_copy(std, std_out, saved.at[2]),
    ]
    start(saves)
    first_forward_step(0)

    def attend(i, carry):
        rows = at(i, slab)
        for h in range(wo.shape[0] // PAIR):
            q, k, v = (joined[rows, (3 * h + j) * PAIR : (3 * h + j + 1) * PAIR] for j in range(3))
            out, totals = attend_pair(q, k, v, None, scale)
            mixed[rows, h * PAIR : (h + 1) * PAIR] = out.astype(BF16)
            for j in range(2):
                total_out[i, 2 * h + j : 2 * h + j + 1, :] = totals[j]
        return carry

    def project(t):
        rows = pl.ds(t * own, own)
        joined[rows] = dot_nn(normed[rows], wq[...]).astype(BF16)

    frames = own // slab
    project(0)
    time_forward_step(0)
    lax.fori_loop(0, frames, attend, 0)
    part[...] = dot_nn(mixed[pl.ds(0, own)], wo[...])
    feed_forward_step(0)
    first_forward_step(1)
    first_corner(0)
    give_normed.wait_recv()
    project(1)
    saves.append(pltpu.make_async_copy(joined, joined_out, saved.at[3]))
    saves[3].start()
    lax.fori_loop(frames, 2 * frames, attend, 0)
    part_out[...] = dot_nn(mixed[pl.ds(own, own)], wo[...]).astype(BF16)
    give_part = remote(part_out, part_in, n_send.at[1], n_recv.at[1], pair)
    give_part.start()
    time_forward_step(1)
    feed_forward_step(1)
    first_corner(1)
    lax.fori_loop(own // slab, 2 * own // slab, turn, 0)
    saves.append(pltpu.make_async_copy(turned, turned_out, saved.at[4]))
    saves[4].start()
    give_part.wait_recv()
    first_forward_step(2)

    def second_norm(i, carry):
        rows = at(i, step)
        value = base[rows] + part[rows] + part_in[rows].astype(F32)
        resid[rows] = value
        standard, inv = norm_rows(value)
        std_next[rows] = standard
        inverse_next[rows] = inv
        low_next[rows] = (standard * vec_out[2:3]).astype(BF16)
        return carry

    lax.fori_loop(0, 2, second_norm, 0)
    for i, (src, dst) in enumerate(((resid, resid_out), (std_next, next_out), (low_next, low_out))):
        saves.append(pltpu.make_async_copy(src, dst, saved.at[5 + i]))
        saves[-1].start()
    time_forward_step(2)
    feed_forward_step(2)

    def first_ends(j):
        def act(r, right):
            if j == 2:
                landed(first_y(r, 1))
            else:
                landed(first_corner_copy(r, 1))
                sent(first_corner_copy(r))

        each_side(j, act)

    for j in range(3):
        first_ends(j)
    for copy in keep_later + saves:
        copy.wait()
    give_normed.wait_send()
    give_part.wait_send()
    for r in (1, 2, 3):
        landed(time_x(r, 1))
        landed(feed_y(r, 1))
        landed(first_x(r, 1))
        for group in (y_copies(r), x_copies(r), corner_x(r), corner_y(r), time_x(r), feed_y(r), first_y(r), first_x(r)):
            sent(group)
    for step_z in range(3):
        for make in (z_copies, time_z, first_z, feed_z):
            pl.when(jnp.logical_and(z >= step_z, z < 3))(lambda step_z=step_z, make=make: sent(make(True, step_z)))
            pl.when(jnp.logical_and(z + step_z <= 3, z > 0))(lambda step_z=step_z, make=make: sent(make(False, step_z)))
    for k in range(4):
        pl.when(jnp.logical_not(stays(k)))(lambda k=k: sent(token_copies(k)))


def enter(tok, vec, qkv, out, later, feed_weight, first_weight, masked, scale):
    own, width, half = tok.shape[1], 4 * tok.shape[2], out.shape[0] // 2
    size = feed_weight.shape[0] // 2
    dma = pltpu.SemaphoreType.DMA
    anywhere = pl.BlockSpec(memory_space=pl.ANY)
    whole = pl.BlockSpec(memory_space=pltpu.VMEM)
    heads = 4 * half // HEAD_DIM

    def low(*shape):
        return pltpu.VMEM(shape, BF16)

    def high(*shape):
        return pltpu.VMEM(shape, F32)

    shapes = [
        ((width, 12 * half), BF16), ((4 * half, width), BF16), ((width, 4 * later.shape[1]), BF16),
        ((4, size, width), BF16), ((4, width, size), BF16), ((2 * own, 12 * half), BF16), ((width, 2 * own), BF16), ((own, width), F32),
        ((2 * own, 4 * half), BF16), ((2 * own // 128, heads, 128), F32), ((own, 1), F32), ((own, width), F32),
        ((own, width), F32), ((own, 1), F32), ((own, width), BF16), ((vec.shape[0], width), F32),
    ]
    return pl.pallas_call(
        functools.partial(enter_kernel, scale),
        in_specs=[anywhere] * 7 + [whole],
        out_specs=[anywhere] * 8 + [whole] * 3 + [anywhere] * 2 + [whole, anywhere, whole],
        out_shape=[jax.ShapeDtypeStruct(shape, kind) for shape, kind in shapes],
        scratch_shapes=[
            low(own, width), low(vec.shape[0], width), low(width, 12 * half), low(4 * half, width),
            low(2 * own, width), low(2 * own, 12 * half), low(width, 2 * own), high(own, width), high(own, width),
            high(own, width), low(own, width), low(own, width), high(own, width), high(own, width), low(own, width),
            dma((2, 3, 2)), dma((4, 2)), dma((4, 2)), dma((4, 2)), dma((4, 2)), dma((4, 2)),
            dma((4, 1)), dma((4, 1)), dma((4, 2)), dma((4, 2)),
            dma((4,)), dma((4,)), dma((4,)), dma((4,)), dma((2, 3)), dma((4,)), dma((4,)), dma((4,)),
            dma((2, 3)), dma((4,)), dma((4,)), dma((4,)), dma((2,)), dma((2,)), dma((9,)), dma((8,)),
            dma((2, 3)), dma((4,)), dma((4,)), dma((4,)), dma((4,)), dma((4,)), dma((4,)), dma((4,)),
        ],
        compiler_params=pltpu.CompilerParams(
            collective_id=0, has_side_effects=True, vmem_limit_bytes=56 * 1024 * 1024
        ),
        cost_estimate=pl.CostEstimate(flops=10**10, transcendentals=10**6, bytes_accessed=10**8),
        name="enter",
    )(tok, vec, qkv, out, later, feed_weight, first_weight, masked)


GROUP = 8
CHUNK = 16


def time_kernel(back, scale, heads, *refs):
    if back:
        (own_ref, rider_ref, joined_hbm, total_ref, wide_ref, turned_ref, mixed_hbm, wt_hbm, bias_ref) = refs[:9]
        (delta_ref, grad_ref, reduced_ref, rider_out) = refs[9:13]
        (half_in, half_own, line_out, line_in, half_send, half_recv, half_local, line_send, line_recv) = refs[-17:-8]
        (out_ref, turned, grad_qkv, grad_out, wt_ref, joined_ref, mixed_ref, load_sem) = refs[-8:]
        refs = refs[13:-17]
    else:
        (own_ref, rider_ref, far_ref, in_ref, wt_hbm, bias_ref) = refs[:6]
        (turned_ref, out_ref, mixed_ref, total_ref, delta_ref, rider_out, spread_out, in_out) = refs[6:14]
        (turned, wt_ref, load_sem) = refs[-3:]
        refs = refs[14:-3]
    (
        wq_ref, wo_ref, held, wide, narrow, kept, core_out, core_in, near_out, near_in,
        gy_send, gy_recv, gc_send, gc_recv, gd_send, gd_recv, sc_send, sc_recv, sy_send, sy_recv,
        r_send, r_recv, r_local, out_sem, wx_send, wx_recv,
    ) = refs
    y, x, c, z = (lax.axis_index(name) for name in AXES)
    near, pair, near_x = (1 - y, x, c, z), (y, x, 1 - c, z), (y, 1 - x, c, z)
    frames = held.shape[0] // 4
    chunks = held.shape[1] // CHUNK
    width = heads * HEAD_DIM
    groups = CHUNK // GROUP

    loads = [(wt_hbm, wt_ref), (own_ref, held.at[pl.ds(0, frames)])]
    if back:
        loads += [(joined_hbm, joined_ref), (mixed_hbm, mixed_ref)]
    loads = [pltpu.make_async_copy(src, dst, load_sem.at[i]) for i, (src, dst) in enumerate(loads)]
    for copy in loads:
        copy.start()
    barrier = pltpu.get_barrier_semaphore()
    for dc in range(2):
        for dz in range(4):
            if dc or dz:
                pl.semaphore_signal(barrier, inc=1, device_id=(y, x, (c + dc) % 2, (z + dz) % 4), device_id_type=MESH)
    pl.semaphore_signal(barrier, inc=1, device_id=near, device_id_type=MESH)
    pl.semaphore_signal(barrier, inc=1, device_id=near_x, device_id_type=MESH)
    pl.semaphore_wait(barrier, 9)

    def remote(src, dst, send, recv, peer):
        return pltpu.make_async_remote_copy(
            src_ref=src, dst_ref=dst, send_sem=send, recv_sem=recv, device_id=peer, device_id_type=MESH
        )

    def patches(k):
        return pl.ds(pl.multiple_of(k * CHUNK, CHUNK), CHUNK)

    def block(b, k):
        return held.at[pl.ds(b * frames, frames), patches(k)]

    def gather_y(k):
        return remote(own_ref.at[:, patches(k)], block(1, k), gy_send.at[k], gy_recv.at[k], near)

    def gather_c(k):
        return remote(own_ref.at[:, patches(k)], block(2, k), gc_send.at[k], gc_recv.at[k], pair)

    def gather_d(k):
        return remote(block(1, k), block(3, k), gd_send.at[k], gd_recv.at[k], pair)

    def scatter_c(k):
        return remote(core_out.at[k], core_in.at[k], sc_send.at[k], sc_recv.at[k], pair)

    def scatter_y(k):
        return remote(near_out.at[k], near_in.at[k], sy_send.at[k], sy_recv.at[k], near)

    def save(k):
        there = (turned_ref.at[k], turned.at[k]) if back else (turned.at[k], turned_ref.at[k])
        return pltpu.make_async_copy(*there, out_sem.at[k])

    def columns(s):
        return pl.ds(pl.multiple_of(s * BLK, BLK), BLK)

    def stays(k):
        if back:
            return jnp.logical_and(z == k, z // 2 == c)
        return jnp.logical_and(2 * c + k // 2 == z, c == k % 2)

    def ride(k):
        if back:
            src, dst = rider_ref.at[:, columns(k)], rider_out.at[2 * (z % 2) + c]
            peer, slot = (y, x, z // 2, k), 2 * (z % 2) + c
        else:
            src, dst = rider_ref.at[k], rider_out.at[:, columns(z)]
            peer, slot = (y, x, k % 2, 2 * c + k // 2), z
        return src, dst, peer, slot

    def ride_remote(k):
        src, dst, peer, slot = ride(k)
        return remote(src, dst, r_send.at[k], r_recv.at[slot], peer)

    def ride_local(k):
        src, dst, _, _ = ride(k)
        return pltpu.make_async_copy(src, dst, r_local.at[0])

    def ride_landed(k):
        if back:
            src, dst = rider_ref.at[:, columns(k)], rider_out.at[k]
        else:
            src, dst = rider_ref.at[k], rider_out.at[:, columns(k)]
        return remote(src, dst, r_send.at[k], r_recv.at[k], near)

    def from_self(k):
        if back:
            return jnp.logical_and(2 * c + k // 2 == z, c == k % 2)
        return jnp.logical_and(z == k, z // 2 == c)

    def spread_x(i, dx=0):
        r, yb = i // 2 + 1, i % 2
        size = far_ref.shape[1] // 4
        at = pl.multiple_of(size * (2 * yb + (x + dx) % 2), size)
        src = far_ref.at[(z + r) % 4, pl.ds(at, size)]
        return remote(src, spread_out.at[(z + r) % 4, pl.ds(at, size)], wx_send.at[i], wx_recv.at[i], near_x)

    gather_y(0).start()
    for k in range(chunks):
        if k > 0:
            gather_y(k).start()
        gather_c(k).start()
    def spread_in(dx=0):
        at = pl.multiple_of(BLK * (2 * (1 - y) + (x + dx) % 2), BLK)
        there = in_out.at[3 - z, pl.ds(at, BLK)]
        return remote(in_ref.at[3 - z, pl.ds(at, BLK)], there, wx_send.at[6], wx_recv.at[6], near_x)

    at_end = jnp.logical_or(z == 0, z == 3)

    def half_away(s):
        return remote(wide_ref.at[1 - x, s], half_in.at[s], half_send.at[s], half_recv.at[s], near_x)

    def half_here(s):
        return pltpu.make_async_copy(wide_ref.at[x, s], half_own.at[s], half_local.at[s])

    def line_away(r):
        return remote(line_out.at[r], line_in.at[r], line_send.at[r], line_recv.at[r], (y, x, c, (z + r) % 4))

    def halve():
        for s in range(4):
            half_away(s).wait_recv()
            half_here(s).wait()
        for r in range(4):
            s = (z + r) % 4
            whole = half_own[s].astype(F32) + half_in[s].astype(F32)
            if r == 0:
                reduced_ref[...] = whole
            else:
                line_out[r] = whole.astype(BF16)
                line_away(r).start()

    if back:
        for s in range(4):
            half_away(s).start()
            half_here(s).start()
    else:
        pl.when(at_end)(lambda: spread_in().start())
        for i in range(6):
            spread_x(i).start()
    for k in range(4):
        pl.when(stays(k))(lambda k=k: ride_local(k).start())
        pl.when(jnp.logical_not(stays(k)))(lambda k=k: ride_remote(k).start())
    if back:
        for k in range(chunks):
            save(k).start()

    def assemble(i, carry):
        rows = pl.ds(pl.multiple_of(i * BLK, BLK), BLK)
        for s in range(0, heads, 2):
            for part in range(4):
                both = [
                    wt_ref[rows, (s + j) * 4 * HEAD_DIM + part * HEAD_DIM : (s + j) * 4 * HEAD_DIM + (part + 1) * HEAD_DIM]
                    for j in range(2)
                ]
                both = jnp.concatenate(both, axis=1)
                if part < 3:
                    wq_ref[rows, part * width + s * HEAD_DIM : part * width + s * HEAD_DIM + PAIR] = both
                else:
                    wo_ref[rows, s * HEAD_DIM : s * HEAD_DIM + PAIR] = both
        return carry

    loads[0].wait()
    lax.fori_loop(0, wt_ref.shape[0] // BLK, assemble, 0)
    for copy in loads[1:]:
        copy.wait()

    def finish(k):
        scatter_c(k).wait_recv()
        both = kept[:, patches(k)] + core_in[k].astype(F32)
        near_out[k] = both[frames:].astype(BF16)
        delta_ref[:, patches(k)] = both[:frames]
        scatter_y(k).start()

    def pass_on(k):
        gather_y(k).wait_recv()
        gather_d(k).start()

    def one_group(i, rows):
        at = pl.ds(pl.multiple_of(i * GROUP, GROUP), GROUP)
        count = 4 * frames * GROUP
        bias = bias_ref[...]
        for lo in range(0, width, PAIR):
            q, k, v = (
                wide[:, at, part * width + lo : part * width + lo + PAIR].reshape(count, PAIR).astype(BF16)
                for part in range(3)
            )
            h = lo // HEAD_DIM
            if back:
                g = narrow[:, at, lo : lo + PAIR].reshape(count, PAIR).astype(BF16)
                totals = [total_ref[rows * groups + i, h + j : h + j + 1, :] for j in range(2)]
                grads = attend_pair_back(q, k, v, g, totals, bias, scale)
                for part in range(3):
                    wide[:, at, part * width + lo : part * width + lo + PAIR] = grads[part].reshape(
                        4 * frames, GROUP, PAIR
                    )
            else:
                mixed, totals = attend_pair(q, k, v, bias, scale)
                narrow[:, at, lo : lo + PAIR] = mixed.reshape(4 * frames, GROUP, PAIR)
                for j in range(2):
                    total_ref[rows * groups + i, h + j : h + j + 1, :] = totals[j]

    def one_chunk(k, carry):
        pl.when(k + 1 < chunks)(lambda: pass_on(k + 1))
        gather_c(k).wait_recv()
        gather_d(k).wait_recv()
        count = 4 * frames * CHUNK
        lhs = held[:, patches(k)].reshape(count, held.shape[2])
        if back:
            wide[...] = joined_ref[:, patches(k)].astype(F32)
            narrow[...] = dot_nn(lhs, wo_ref[...]).astype(BF16).astype(F32).reshape(narrow.shape)
        else:
            joined = dot_nn(lhs, wq_ref[...]).astype(BF16)
            out_ref[:, patches(k)] = joined.reshape(wide.shape)
            wide[...] = joined.astype(F32).reshape(wide.shape)
        lax.fori_loop(0, groups, lambda i, carry: (one_group(i, k), carry)[1], 0)
        if back:
            grads = wide[...].astype(BF16)
            out_ref[:, patches(k)] = grads
            partial = dot_nt(grads.reshape(count, 3 * width), wq_ref[...])
        else:
            mixed = narrow[...].astype(BF16)
            mixed_ref[:, patches(k)] = mixed
            partial = dot_nt(mixed.reshape(count, width), wo_ref[...])
        partial = partial.reshape(4 * frames, CHUNK, held.shape[2])
        kept[:, patches(k)] = partial[: 2 * frames]
        core_out[k] = partial[2 * frames :].astype(BF16)
        scatter_c(k).start()
        pl.when(k > 0)(lambda: finish(k - 1))
        if not back:
            for b in range(4):
                slab = held[b * frames : (b + 1) * frames, patches(k)].reshape(frames * CHUNK, held.shape[2])
                turned[k, :, b * frames * CHUNK : (b + 1) * frames * CHUNK] = slab.T
            save(k).start()
        if back:
            pl.when(k == chunks // 2 - 1)(halve)
        return carry

    pass_on(0)
    lax.fori_loop(0, chunks, one_chunk, 0)
    finish(chunks - 1)

    def weigh(k, carry):
        count = 4 * frames * CHUNK
        save(k).wait()
        grad_qkv[...] = grad_qkv[...] + dot_nn(turned[k], out_ref[:, patches(k)].reshape(count, 3 * width))
        grad_out[...] = grad_out[...] + dot_tn(
            mixed_ref[:, patches(k)].reshape(count, width), held[:, patches(k)].reshape(count, held.shape[2])
        )
        return carry

    def arrange(i, carry):
        rows = pl.ds(pl.multiple_of(i * BLK, BLK), BLK)
        last = grad_out[:, rows].T
        for s in range(heads):
            mine = slice(s * HEAD_DIM, (s + 1) * HEAD_DIM)
            parts = [grad_qkv[rows, j * width : (j + 1) * width][:, mine] for j in range(3)] + [last[:, mine]]
            grad_ref[rows, 2 * s * PAIR : (2 * s + 1) * PAIR] = jnp.concatenate(parts[:2], axis=1).astype(BF16)
            grad_ref[rows, (2 * s + 1) * PAIR : (2 * s + 2) * PAIR] = jnp.concatenate(parts[2:], axis=1).astype(BF16)
        return carry

    if back:
        grad_qkv[...] = jnp.zeros_like(grad_qkv)
        grad_out[...] = jnp.zeros_like(grad_out)
        lax.fori_loop(0, chunks, weigh, 0)
        lax.fori_loop(0, grad_ref.shape[0] // BLK, arrange, 0)
    for k in range(chunks):
        scatter_y(k).wait_recv()
        delta_ref[:, patches(k)] = delta_ref[:, patches(k)] + near_in[k].astype(F32)
    if back:
        for r in (1, 2, 3):
            line_away(r).wait_recv()
            reduced_ref[...] = reduced_ref[...] + line_in[r].astype(F32)
        for r in (1, 2, 3):
            line_away(r).wait_send()
        for s in range(4):
            half_away(s).wait_send()
    for k in range(chunks):
        for copy in (gather_y(k), gather_c(k), gather_d(k), scatter_c(k), scatter_y(k)):
            copy.wait_send()
        if not back:
            save(k).wait()
    if not back:
        for i in range(6):
            spread_x(i, 1).wait_recv()
            spread_x(i).wait_send()

        def spread_in_end():
            spread_in(1).wait_recv()
            spread_in().wait_send()

        pl.when(at_end)(spread_in_end)
    for k in range(4):
        pl.when(stays(k))(lambda k=k: ride_local(k).wait())
        pl.when(jnp.logical_not(stays(k)))(lambda k=k: ride_remote(k).wait_send())
        pl.when(jnp.logical_not(from_self(k)))(lambda k=k: ride_landed(k).wait_recv())


def time_call(back, own, rider, saved, weights, bias, scale):
    frames, patches, features = own.shape
    width = weights.shape[1] // 4
    heads = width // HEAD_DIM
    chunks = patches // CHUNK
    rows = 4 * frames * GROUP
    dma = pltpu.SemaphoreType.DMA
    anywhere = pl.BlockSpec(memory_space=pl.ANY)
    whole = pl.BlockSpec(memory_space=pltpu.VMEM)
    turned = (chunks, features, 4 * frames * CHUNK)
    if back:
        out_shape = []
    else:
        out_shape = [
            jax.ShapeDtypeStruct(turned, BF16),
            jax.ShapeDtypeStruct((4 * frames, patches, 3 * width), BF16),
            jax.ShapeDtypeStruct((4 * frames, patches, width), BF16),
            jax.ShapeDtypeStruct((patches // GROUP, heads, rows), F32),
        ]
    rider_shape = (4, frames * patches, BLK) if back else (frames * patches, features)
    out_shape += [
        jax.ShapeDtypeStruct((frames, patches, features), F32),
        jax.ShapeDtypeStruct(rider_shape, BF16),
    ]
    held = 2
    half = saved[2].shape[1:] if back else None
    if back:
        out_shape.insert(-1, jax.ShapeDtypeStruct((features, features), BF16))
        out_shape.insert(-1, jax.ShapeDtypeStruct(half[1:], F32))
    else:
        out_shape += [jax.ShapeDtypeStruct(w.shape, BF16) for w in saved]
        held = 4
    return pl.pallas_call(
        functools.partial(time_kernel, back, scale, heads),
        in_specs=[anywhere] * 2
        + ([anywhere, whole, anywhere, anywhere, anywhere] if back else [anywhere] * 2)
        + [anywhere, whole],
        out_specs=([] if back else [anywhere]) + [whole] * (len(out_shape) - held + back) + [anywhere] * (held - 1),
        out_shape=out_shape,
        scratch_shapes=[
            pltpu.VMEM((features, 3 * width), BF16),
            pltpu.VMEM((features, width), BF16),
            pltpu.VMEM((4 * frames, patches, features), BF16),
            pltpu.VMEM((4 * frames, CHUNK, 3 * width), F32),
            pltpu.VMEM((4 * frames, CHUNK, width), F32),
            pltpu.VMEM((2 * frames, patches, features), F32),
            pltpu.VMEM((chunks, 2 * frames, CHUNK, features), BF16),
            pltpu.VMEM((chunks, 2 * frames, CHUNK, features), BF16),
            pltpu.VMEM((chunks, frames, CHUNK, features), BF16),
            pltpu.VMEM((chunks, frames, CHUNK, features), BF16),
        ]
        + [dma((chunks,))] * 10
        + [dma((4,)), dma((4,)), dma((1,)), dma((chunks,))]
        + [dma((7,))] * 2
        + ([pltpu.VMEM(half, BF16)] * 4 + [dma((4,))] * 5 if back else [])
        + ([pltpu.VMEM((4 * frames, patches, 3 * width), BF16)] if back else [])
        + [pltpu.VMEM(turned, BF16)]
        + ([pltpu.VMEM((features, 3 * width), F32), pltpu.VMEM((width, features), F32)] if back else [])
        + [pltpu.VMEM(weights.shape, BF16)]
        + ([pltpu.VMEM(saved[0].shape, BF16), pltpu.VMEM(saved[4].shape, BF16)] if back else [])
        + [dma((4,))],
        compiler_params=pltpu.CompilerParams(
            collective_id=2 if back else 1, has_side_effects=True, vmem_limit_bytes=60 * 1024 * 1024
        ),
        cost_estimate=pl.CostEstimate(flops=10**10, transcendentals=10**6, bytes_accessed=10**8),
        name="time_back" if back else "time_forward",
    )(own, rider, *saved, weights, bias)


def feed_kernel(
    resid_hbm, delta_hbm, upstream_hbm, masked, gain, w_in_hbm, w_in_far_hbm, w_out_hbm, w_far_hbm,
    half_in_hbm, half_out_hbm, grad_hbm, low_hbm, rows_hbm, gain_out,
    resid, delta, upstream, grad_out, low_out, rows_out, move_sem,
    w_in, w_out, standard, inverse, normed, grads, normed_t, grads_t, hidden, pulled, g_in, g_out, back, ahead,
    back_out, back_in, ahead_out, ahead_in, from_x, from_y, slopes,
    w_sem, g_sem, n_send, n_recv, b_send, b_recv, hx_send, hx_recv, hy_send, hy_recv,
):
    y, x, c, z = (lax.axis_index(name) for name in AXES)
    pair, near_y, near_x = (y, x, 1 - c, z), (1 - y, x, c, z), (y, 1 - x, c, z)
    own = resid.shape[0]
    moves = [
        pltpu.make_async_copy(src, dst, move_sem.at[i])
        for i, (src, dst) in enumerate((
            (resid_hbm, resid), (delta_hbm, delta), (upstream_hbm, upstream),
            (grad_out, grad_hbm), (low_out, low_hbm), (rows_out, rows_hbm),
        ))
    ]
    for copy in moves[:3]:
        copy.start()
    step = own // 2
    slab = 128

    def fetch(s, far, last=False):
        size = w_out.shape[1] // 4
        copies = []
        for i in range(4):
            rows = pl.ds(pl.multiple_of(BLK * (2 * ((y + i // 2) % 2) + (x + i % 2) % 2), BLK), BLK)
            source = w_in_far_hbm if last and i == 3 else w_in_hbm
            copies.append(pltpu.make_async_copy(source.at[s, rows], w_in.at[s, rows], w_sem.at[5 + i, s]))
        for i in range(4):
            rows = pl.ds(pl.multiple_of(size * (2 * (i // 2) + (x + i % 2) % 2), size), size)
            source = w_far_hbm if far and i % 2 else w_out_hbm
            copies.append(pltpu.make_async_copy(source.at[s, rows], w_out.at[s, rows], w_sem.at[i, s]))
        return copies

    def fetch_now(s, far, last):
        for copy in fetch(s, far, last):
            copy.start()

    for s in range(4):
        pl.when(z == s)(lambda s=s: fetch_now(s, False, False))
        if s in (0, 3):
            pl.when(z == 3 - s)(lambda s=s: fetch_now(s, True, True))
            pl.when(jnp.logical_and(z != s, z != 3 - s))(lambda s=s: fetch_now(s, True, False))
        else:
            pl.when(z != s)(lambda s=s: fetch_now(s, True, False))
    barrier = pltpu.get_barrier_semaphore()
    for peer in (pair, near_y, near_x):
        pl.semaphore_signal(barrier, inc=1, device_id=peer, device_id_type=MESH)

    def remote(src, dst, send, recv, peer=pair):
        return pltpu.make_async_remote_copy(
            src_ref=src, dst_ref=dst, send_sem=send, recv_sem=recv, device_id=peer, device_id_type=MESH
        )

    def block(yb, xb):
        return pl.ds(pl.multiple_of(BLK * (2 * yb + xb), BLK), BLK)

    def away_x(s, i):
        return remote(g_out.at[s, block(i, 1 - x)], from_x.at[i, s], hx_send.at[i, s], hx_recv.at[i, s], near_x)

    def away_y(s, i):
        return remote(g_in.at[s, block(1 - y, i)], from_y.at[i, s], hy_send.at[i, s], hy_recv.at[i, s], near_y)

    def keep(s, i):
        return (
            pltpu.make_async_copy(g_out.at[s, block(i, x)], half_out_hbm.at[i, s], g_sem.at[0, i, s]),
            pltpu.make_async_copy(g_in.at[s, block(y, i)], half_in_hbm.at[i, s], g_sem.at[1, i, s]),
        )

    def combine(s):
        for i in range(2):
            away_x(s, i).wait_recv()
            g_out[s, block(i, x)] = (g_out[s, block(i, x)].astype(F32) + from_x[i, s].astype(F32)).astype(BF16)
            away_y(s, i).wait_recv()
            g_in[s, block(y, i)] = (g_in[s, block(y, i)].astype(F32) + from_y[i, s].astype(F32)).astype(BF16)
            for copy in keep(s, i):
                copy.start()

    def at(i, size):
        return pl.ds(pl.multiple_of(i * size, size), size)

    def prepare(i, carry):
        rows = at(i, step)
        grads[rows] = jnp.where(masked[rows] > 0.0, upstream[rows].astype(F32), 0.0).astype(BF16)
        std, inv = norm_rows(resid[rows] + delta[rows])
        standard[rows] = std
        inverse[rows] = inv
        normed[rows] = (std * gain[3:4]).astype(BF16)
        return carry

    for copy in moves[:3]:
        copy.wait()
    lax.fori_loop(0, 2, prepare, 0)
    pl.semaphore_wait(barrier, 3)
    mine, theirs = pl.ds(0, own), pl.ds(own, own)
    give_grads = remote(grads.at[mine], grads.at[theirs], n_send.at[0], n_recv.at[0])
    give_normed = remote(normed.at[mine], normed.at[theirs], n_send.at[1], n_recv.at[1])
    give_normed.start()
    give_grads.start()

    def turn(i, carry):
        rows = at(i, slab)
        normed_t[:, rows] = normed[rows].T
        grads_t[:, rows] = grads[rows].T
        return carry

    lax.fori_loop(0, own // slab, turn, 0)
    rate = math.sqrt(2.0 / math.pi)

    def bend_step(s, rows):
        inner = dot_nn(normed[rows], w_in[s])
        square = inner * inner
        bend = jnp.tanh(rate * inner * (1.0 + 0.044715 * square))
        hidden[rows] = (0.5 * inner * (1.0 + bend)).astype(BF16)
        slopes[rows] = 0.5 * (1.0 + bend) + 0.5 * inner * (1.0 - bend * bend) * (rate * (1.0 + 3.0 * 0.044715 * square))

    def pull_step(s, rows):
        pulled[rows] = (dot_nt(grads[rows], w_out[s]) * slopes[rows]).astype(BF16)

    def add_step(s, rows):
        ahead[rows] = ahead[rows] + dot_nn(hidden[rows], w_out[s])
        back[rows] = back[rows] + dot_nt(pulled[rows], w_in[s])

    def clear():
        back[...] = jnp.zeros_like(back)
        ahead[...] = jnp.zeros_like(ahead)

    def meet():
        give_normed.wait_recv()
        give_grads.wait_recv()
        lax.fori_loop(own // slab, 2 * own // slab, turn, 0)

    def one_piece(s, carry):
        for copy in fetch(s, False):
            copy.wait()

        def first_half(t, carry):
            pl.when(jnp.logical_and(s == 0, t == 1))(meet)
            bend_step(s, at(t, own))
            return carry

        lax.fori_loop(0, 2, first_half, 0)
        g_out[s] = dot_nn(grads_t[...], hidden[...]).astype(BF16)
        for i in range(2):
            away_x(s, i).start()
        lax.fori_loop(0, 2, lambda t, carry: (pull_step(s, at(t, own)), carry)[1], 0)
        g_in[s] = dot_nn(normed_t[...], pulled[...]).astype(BF16)
        for i in range(2):
            away_y(s, i).start()
        pl.when(s == 0)(clear)
        lax.fori_loop(0, 2, lambda t, carry: (add_step(s, at(t, own)), carry)[1], 0)
        return carry

    lax.fori_loop(0, 4, one_piece, 0)
    back_out[...] = back[theirs].astype(BF16)
    give_back = remote(back_out, back_in, b_send.at[0], b_recv.at[0])
    give_back.start()
    ahead_out[...] = ahead[theirs].astype(BF16)
    give_ahead = remote(ahead_out, ahead_in, b_send.at[1], b_recv.at[1])
    give_ahead.start()
    give_back.wait_recv()

    def finish(i, total):
        rows = at(i, step)
        grad = back[rows] + back_in[rows].astype(F32)
        std = standard[rows]
        inner = grad * gain[3:4]
        mean = jnp.mean(inner, axis=-1, keepdims=True)
        along = jnp.mean(inner * std, axis=-1, keepdims=True)
        full = grads[rows].astype(F32) + (inner - mean - std * along) * inverse[rows]
        grad_out[rows] = full
        low_out[rows] = full.astype(BF16)
        return total + jnp.sum(grad * std, axis=0, keepdims=True)

    gain_out[...] = lax.fori_loop(0, 2, finish, jnp.zeros((1, resid.shape[1]), F32))
    moves[3].start()
    moves[4].start()
    give_ahead.wait_recv()

    def emit(i, carry):
        rows = at(i, step)
        rows_out[rows] = (resid[rows] + delta[rows] + ahead[rows] + ahead_in[rows].astype(F32)).astype(BF16)
        return carry

    lax.fori_loop(0, 2, emit, 0)
    moves[5].start()
    lax.fori_loop(0, 4, lambda s, carry: (combine(s), carry)[1], 0)
    for copy in (give_normed, give_grads, give_back, give_ahead):
        copy.wait_send()
    for s in range(4):
        for i in range(2):
            away_x(s, i).wait_send()
            away_y(s, i).wait_send()
            for copy in keep(s, i):
                copy.wait()
    for copy in moves[3:]:
        copy.wait()


def feed(resid, delta, upstream, masked, gain, w_in, w_in_far, w_out, w_far):
    own, features = resid.shape
    units = w_in.shape[2]
    dma = pltpu.SemaphoreType.DMA
    anywhere = pl.BlockSpec(memory_space=pl.ANY)
    whole = pl.BlockSpec(memory_space=pltpu.VMEM)

    def low(*shape):
        return pltpu.VMEM(shape, BF16)

    def high(*shape):
        return pltpu.VMEM(shape, F32)

    return pl.pallas_call(
        feed_kernel,
        in_specs=[anywhere] * 3 + [whole] * 2 + [anywhere] * 4,
        out_specs=[anywhere] * 5 + [whole],
        out_shape=[
            jax.ShapeDtypeStruct((2, 4, BLK, units), BF16),
            jax.ShapeDtypeStruct((2, 4, BLK, units), BF16),
            jax.ShapeDtypeStruct((own, features), F32),
            jax.ShapeDtypeStruct((own, features), BF16),
            jax.ShapeDtypeStruct((own, features), BF16),
            jax.ShapeDtypeStruct((1, features), F32),
        ],
        scratch_shapes=[
            high(own, features), high(own, features), low(own, features),
            high(own, features), low(own, features), low(own, features), dma((6,)),
            low(4, features, units), low(4, units, features), high(own, features), high(own, 1),
            low(2 * own, features), low(2 * own, features), low(features, 2 * own), low(features, 2 * own),
            low(2 * own, units), low(2 * own, units), low(4, features, units), low(4, features, units),
            high(2 * own, features), high(2 * own, features),
            low(own, features), low(own, features), low(own, features), low(own, features),
            low(2, 4, BLK, units), low(2, 4, BLK, units), high(2 * own, units),
            dma((9, 4)), dma((2, 2, 4)), dma((2,)), dma((2,)), dma((2,)), dma((2,)),
            dma((2, 4)), dma((2, 4)), dma((2, 4)), dma((2, 4)),
        ],
        compiler_params=pltpu.CompilerParams(
            collective_id=4, has_side_effects=True, vmem_limit_bytes=60 * 1024 * 1024
        ),
        cost_estimate=pl.CostEstimate(flops=26 * 10**9, transcendentals=2 * 10**6, bytes_accessed=10**8),
        name="feed",
    )(resid, delta, upstream, masked, gain, w_in, w_in_far, w_out, w_far)


def leave_kernel(
    scale,
    part_hbm, next_hbm, grad_hbm, out_hbm, joined_hbm, mixed_hbm, lhs_hbm, weight_hbm, std_hbm, time_hbm, feed_hbm, feed_in_hbm,
    totals, inverse_next, inverse, masked, gains, later_grad,
    space_qkv, space_out, feed_in_out, feed_out_out, time_qkv, time_out, rows_out, gains_out, embed_out,
    rows_in,
    part, std, base, w_out, dj, mixed, lhs, weight, low_grads, turned, dmixed, go,
    t_own, t_in, tz_out, tz_in, t_total, ty_out, ty_in, tc_out, tc_in,
    f_own, f_in, fz_out, fz_in, f_total, f_other, fc_out, fc_in,
    grads, a1_out, a1_in, b1_out, b1_in, a2_out, a2_in, b2_out, b2_in, z_out, z_in,
    half_out, half_in, ready, core_out, core_in, sums, sum_out, sum_in, share_in,
    a1_send, a1_recv, b1_send, b1_recv, a2_send, a2_recv, b2_send, b2_recv, z_send, z_recv,
    h_send, h_recv, r_send, r_recv, c_send, c_recv, s_send, s_recv, p_send, p_recv, local,
    g_send, g_recv, tx_send, tx_recv, tz_send, tz_recv, ty_send, ty_recv, fy_send, fy_recv, fz_send, fz_recv, t_local, f_local, fetched,
):
    y, x, c, z = (lax.axis_index(name) for name in AXES)
    near_y, near_x, pair = (1 - y, x, c, z), (y, 1 - x, c, z), (y, x, 1 - c, z)
    own = std.shape[0]
    third = go.shape[1] // 4
    wide = 3 * third
    two = 2 * third
    slab = 128

    fetches = [
        pltpu.make_async_copy(src, dst, fetched.at[i])
        for i, (src, dst) in enumerate((
            (part_hbm, part), (next_hbm, std), (grad_hbm, base), (out_hbm, w_out), (joined_hbm, dj), (mixed_hbm, mixed),
            (lhs_hbm, lhs), (weight_hbm, weight), (feed_in_hbm, f_other),
        ))
    ]
    for copy in fetches:
        copy.start()
    fetch_std = pltpu.make_async_copy(std_hbm, std, fetched.at[9])

    barrier = pltpu.get_barrier_semaphore()
    for dc in range(2):
        for dz in range(4):
            if dc or dz:
                pl.semaphore_signal(barrier, inc=1, device_id=(y, x, (c + dc) % 2, (z + dz) % 4), device_id_type=MESH)
    for peer in (near_y, near_x):
        pl.semaphore_signal(barrier, inc=1, device_id=peer, device_id_type=MESH)
    pl.semaphore_wait(barrier, 9)

    def remote(src, dst, send, recv, peer):
        return pltpu.make_async_remote_copy(
            src_ref=src, dst_ref=dst, send_sem=send, recv_sem=recv, device_id=peer, device_id_type=MESH
        )

    def at(i, length):
        return pl.ds(pl.multiple_of(i * length, length), length)

    def along(r):
        return (y, x, c, (z + r) % 4)

    def time_x(yb):
        return remote(time_hbm.at[at(2 * yb + 1 - x, BLK)], t_in.at[yb], tx_send.at[yb], tx_recv.at[yb], near_x)

    def time_keep(yb):
        return pltpu.make_async_copy(time_hbm.at[at(2 * yb + x, BLK)], t_own.at[yb], t_local.at[yb])

    def time_z(r):
        return remote(tz_out.at[r], tz_in.at[r], tz_send.at[r], tz_recv.at[r], along(1))

    def feed_y(r):
        s = (z + r) % 4
        return remote(feed_hbm.at[1 - y, s], f_in.at[r], fy_send.at[r], fy_recv.at[r], near_y)

    def feed_keep(r):
        return pltpu.make_async_copy(feed_hbm.at[y, (z + r) % 4], f_own.at[r], f_local.at[r])

    def feed_z(r):
        return remote(fz_out.at[r], fz_in.at[r], fz_send.at[r], fz_recv.at[r], along(1))

    for r in (3, 2, 1, 0):
        feed_y(r).start()
        feed_keep(r).start()
    for yb in range(2):
        time_x(yb).start()
        time_keep(yb).start()

    def feed_step(t):
        r = 3 - t
        feed_y(r).wait_recv()
        feed_keep(r).wait()
        total = f_own[r].astype(F32) + f_in[r].astype(F32)
        if t > 0:
            feed_z(t - 1).wait_recv()
            total = total + fz_in[t - 1].astype(F32)
        if t == 3:
            f_total[...] = total
        else:
            fz_out[t] = total.astype(BF16)
            feed_z(t).start()

    def time_step(t):
        if t == 0:
            for yb in range(2):
                time_x(yb).wait_recv()
                time_keep(yb).wait()
        else:
            time_z(t - 1).wait_recv()
        piece_at = at((z + 3 - t) % 4, BLK)
        for yb in range(2):
            total = t_own[yb, :, piece_at].astype(F32) + t_in[yb, :, piece_at].astype(F32)
            if t > 0:
                total = total + tz_in[t - 1, yb].astype(F32)
            if t == 3:
                t_total[yb] = total
            else:
                tz_out[t, yb] = total.astype(BF16)
        if t < 3:
            time_z(t).start()

    step = own // 2
    for copy in fetches[:3]:
        copy.wait()

    def norm_back(grad, standard, weights, inv):
        inner = grad * weights
        mean = jnp.mean(inner, axis=-1, keepdims=True)
        slope = jnp.mean(inner * standard, axis=-1, keepdims=True)
        return (inner - mean - standard * slope) * inv

    def after_time(i, total):
        rows = at(i, step)
        grad, standard = part[rows], std[rows]
        full = base[rows] + norm_back(grad, standard, gains[2:3], inverse_next[rows])
        base[rows] = full
        low_grads[rows] = full.astype(BF16)
        return total + jnp.sum(grad * standard, axis=0, keepdims=True)

    zero = jnp.zeros((1, std.shape[1]), F32)
    next_grad = lax.fori_loop(0, 2, after_time, zero)
    give = remote(low_grads.at[pl.ds(0, own)], low_grads.at[pl.ds(own, own)], g_send.at[0], g_recv.at[0], pair)
    give.start()
    fetch_std.start()
    for copy in fetches[3:6]:
        copy.wait()

    def attend(i, carry):
        rows = at(i, slab)
        for h in range(mixed.shape[1] // PAIR):
            places = [pl.ds((3 * h + j) * PAIR, PAIR) for j in range(3)]
            q, k, v = (dj[rows, place] for place in places)
            lines = [totals[i, 2 * h + j : 2 * h + j + 1, :] for j in range(2)]
            found = attend_pair_back(q, k, v, dmixed[rows, h * PAIR : (h + 1) * PAIR], lines, None, scale)
            for place, value in zip(places, found):
                dj[rows, place] = value.astype(BF16)
        return carry

    def turn(i, carry):
        turned[:, at(i, slab)] = low_grads[at(i, slab)].T
        return carry

    def attend_half(t, *between):
        rows = pl.ds(t * own, own)
        first, count = t * own // slab, own // slab
        dmixed[rows] = dot_nt(low_grads[rows], w_out[...]).astype(BF16)
        between[0]()
        lax.fori_loop(first, first + count // 2, attend, 0)
        between[1]()
        lax.fori_loop(first + count // 2, first + count, attend, 0)
        between[2]()
        lax.fori_loop(first, first + count, turn, 0)

    def nothing():
        pass

    attend_half(0, lambda: feed_step(0), nothing, lambda: feed_step(1))
    give.wait_recv()
    attend_half(1, nothing, lambda: feed_step(2), lambda: time_step(0))
    for copy in fetches[6:]:
        copy.wait()
    def away(i, carry):
        rows = pl.ds(pl.multiple_of(own + i * step, step), step)
        half_out[pl.ds(pl.multiple_of(i * step, step), step)] = dot_nt(dj[rows], weight[...]).astype(BF16)
        return carry

    lax.fori_loop(0, 2, away, 0)
    swap = remote(half_out, half_in, h_send.at[0], h_recv.at[0], pair)
    swap.start()

    def block(yb, xb):
        return pl.ds(pl.multiple_of(BLK * (2 * yb + xb), BLK), BLK)

    def a1(i):
        return remote(a1_out.at[i], a1_in.at[i], a1_send.at[i], a1_recv.at[i], near_x)

    def b1(i):
        return remote(b1_out.at[i], b1_in.at[i], b1_send.at[i], b1_recv.at[i], near_y)

    def a2(i):
        return remote(a2_out.at[i], a2_in.at[i], a2_send.at[i], a2_recv.at[i], near_y)

    def b2(i):
        return remote(b2_out.at[i], b2_in.at[i], b2_send.at[i], b2_recv.at[i], near_x)

    def to_z(r):
        return remote(z_out.at[r], z_in.at[r], z_send.at[r], z_recv.at[r], along(r))

    def send_first(i):
        a1(i).start()
        b1(i).start()

    def piece(i, carry):
        s = (z + i + 1) % 4
        made = dot_nn(lhs[...], dj[:, pl.ds(pl.multiple_of(s * wide, third), wide)])
        grads[i, :, :wide] = made
        grads[i, :, wide:] = go[:, pl.ds(pl.multiple_of(s * third, third), third)].astype(F32)
        for b in range(2):
            a1_out[i, b] = grads[i, block(b, 1 - x), :two].astype(BF16)
            b1_out[i, b] = grads[i, block(1 - y, b), two:].astype(BF16)
        pl.when(i < 2)(lambda: send_first(i))
        return carry


    def second(i):
        a1(i).wait_recv()
        a2_out[i] = (grads[i, block(1 - y, x), :two] + a1_in[i, 1 - y].astype(F32)).astype(BF16)
        a2(i).start()
        b1(i).wait_recv()
        b2_out[i] = (grads[i, block(y, 1 - x), two:] + b1_in[i, 1 - x].astype(F32)).astype(BF16)
        b2(i).start()
        grads[i, block(y, x), :two] = grads[i, block(y, x), :two] + a1_in[i, y].astype(F32)
        grads[i, block(y, x), two:] = grads[i, block(y, x), two:] + b1_in[i, x].astype(F32)

    def third_step(i):
        a2(i).wait_recv()
        b2(i).wait_recv()
        grads[i, block(y, x), :two] = grads[i, block(y, x), :two] + a2_in[i].astype(F32)
        grads[i, block(y, x), two:] = grads[i, block(y, x), two:] + b2_in[i].astype(F32)
        if i < 3:
            z_out[i + 1] = grads[i, block(y, x), :].astype(BF16)
            to_z(i + 1).start()

    fetch_std.wait()
    sums[...] = jnp.zeros_like(sums)
    sums[1:2] = next_grad
    sums[2:3] = later_grad[...]
    swap.wait_recv()

    def home(i, totals):
        rows = pl.ds(pl.multiple_of(i * step, step), step)
        grad = dot_nt(dj[rows], weight[...]) + half_in[rows].astype(F32)
        standard = std[rows]
        full = base[rows] + norm_back(grad, standard, gains[1:2], inverse[rows])
        hide = masked[rows] > 0.0
        ready[rows] = jnp.where(hide, 0.0, full).astype(BF16)
        return (
            totals[0] + jnp.sum(grad * standard, axis=0, keepdims=True),
            totals[1] + jnp.sum(jnp.where(hide, full, 0.0), axis=0, keepdims=True),
        )

    gain_grad, embed_grad = lax.fori_loop(0, 2, home, (zero, zero))
    sums[0:1] = gain_grad
    sums[3:4] = embed_grad

    def columns(s):
        return pl.ds(pl.multiple_of(s * BLK, BLK), BLK)

    def stays(k):
        return jnp.logical_and(z == k, z // 2 == c)

    def ride(k):
        slot = 2 * (z % 2) + c
        return remote(ready.at[:, columns(k)], rows_in.at[slot], r_send.at[k], r_recv.at[slot], (y, x, z // 2, k))

    def ride_local(k):
        return pltpu.make_async_copy(ready.at[:, columns(k)], rows_in.at[2 * (z % 2) + c], local.at[3])

    for k in range(4):
        pl.when(stays(k))(lambda k=k: ride_local(k).start())
        pl.when(jnp.logical_not(stays(k)))(lambda k=k: ride(k).start())
    time_step(1)
    go[...] = dot_nn(turned[...], mixed[...]).astype(BF16)
    lax.fori_loop(0, 4, piece, 0)

    def share(h):
        peer = (pair, near_y, near_x)[h]
        return remote(sum_out.at[h], sum_in.at[h], s_send.at[h], s_recv.at[h], peer)

    def begin_share(h):
        sum_out[h] = sums[...]
        share(h).start()

    def end_share(h):
        share(h).wait_recv()
        sums[...] = sums[...] + sum_in[h]

    begin_share(0)
    second(0)
    send_first(2)
    time_step(2)
    second(1)
    send_first(3)
    third_step(0)
    end_share(0)
    begin_share(1)
    second(2)
    third_step(1)
    end_share(1)
    begin_share(2)
    second(3)
    third_step(2)
    end_share(2)
    sum_out[3] = sums[...]

    def deal(r):
        s = (z + r) % 4
        return remote(sum_out.at[3, :, columns(s)], share_in.at[r], p_send.at[r], p_recv.at[r], (y, x, c, s))

    for r in (1, 2, 3):
        deal(r).start()
    third_step(3)
    parity = BLK // 2

    time_step(3)
    ty_out[...] = t_total[1 - y].astype(BF16)
    swap_y = remote(ty_out, ty_in, ty_send.at[0], ty_recv.at[0], near_y)
    swap_y.start()
    feed_step(3)
    fc_out[0] = f_other[at(1 - c, parity)].astype(BF16)
    fc_out[1] = f_total[at(1 - c, parity)].astype(BF16)
    swap_feed = remote(fc_out, fc_in, c_send.at[1], c_recv.at[1], pair)
    swap_feed.start()
    units = f_total.shape[1]
    feed_in_out[:, at(c, units)] = f_other[at(c, parity)]
    feed_out_out[at(c, units)] = f_total[at(c, parity)].T
    swap_y.wait_recv()
    tc_out[0] = t_total[y, at(1 - c, parity)].astype(BF16)
    tc_out[1] = ty_in[at(1 - c, parity)]
    swap_time = remote(tc_out, tc_in, c_send.at[2], c_recv.at[2], pair)
    swap_time.start()
    for k in range(4):
        pl.when(stays(k))(lambda k=k: ride_local(k).wait())
        from_self = jnp.logical_and(2 * c + k // 2 == z, c == k % 2)

        def landed(k=k):
            remote(ready.at[:, columns(k)], rows_in.at[k], r_send.at[k], r_recv.at[k], near_y).wait_recv()

        pl.when(jnp.logical_not(from_self))(landed)
    rows_out[...] = rows_in[...].astype(F32)
    for r in (1, 2, 3):
        to_z(r).wait_recv()
    total = grads[3, block(y, x), :]
    for r in (1, 2, 3):
        total = total + z_in[r].astype(F32)
    grads[3, block(y, x), :] = total
    rows = BLK // 2

    def core_rows(core):
        return pl.ds(pl.multiple_of(BLK * (2 * y + x) + rows * core, rows), rows)

    core_out[...] = grads[3, core_rows(1 - c), :].astype(BF16)
    last = remote(core_out, core_in, c_send.at[0], c_recv.at[0], pair)
    last.start()
    def place(core, value):
        for j in range(3):
            space_qkv[j, :, at(core, third)] = value[:, j * third : (j + 1) * third]
        space_out[at(core, third)] = value[:, 3 * third :].T

    place(c, grads[3, core_rows(c), :])
    result = sums[:, columns(z)]
    for r in (1, 2, 3):
        deal(r).wait_recv()
        result = result + share_in[r]
    gains_out[...] = result[:3]
    embed_out[...] = result[3:4]
    swap_feed.wait_recv()
    feed_in_out[:, at(1 - c, units)] = fc_in[0].astype(F32)
    feed_out_out[at(1 - c, units)] = fc_in[1].astype(F32).T
    swap_time.wait_recv()
    mine = (t_total[y, at(c, parity)], ty_in[at(c, parity)].astype(F32))
    other = (tc_in[0].astype(F32), tc_in[1].astype(F32))
    by_head = []
    for yb in range(2):
        for cb in range(2):
            by_head.append(
                jnp.where(
                    c == cb,
                    jnp.where(y == yb, mine[0], mine[1]),
                    jnp.where(y == yb, other[0], other[1]),
                )
            )
    for j in range(4):
        made = jnp.concatenate([v[:, j * HEAD_DIM : (j + 1) * HEAD_DIM] for v in by_head], axis=1)
        if j < 3:
            time_qkv[j] = made
        else:
            time_out[...] = made.T
    last.wait_recv()
    place(1 - c, core_in[...].astype(F32))

    for copy in (last, swap, give, swap_y, swap_feed, swap_time):
        copy.wait_send()
    for yb in range(2):
        time_x(yb).wait_send()
    for r in range(4):
        feed_y(r).wait_send()
    for t in range(3):
        time_z(t).wait_send()
        feed_z(t).wait_send()
    for i in range(4):
        for copy in (a1(i), b1(i), a2(i), b2(i)):
            copy.wait_send()
    for r in (1, 2, 3):
        to_z(r).wait_send()
        deal(r).wait_send()
    for h in range(3):
        share(h).wait_send()
    for k in range(4):
        pl.when(jnp.logical_not(stays(k)))(lambda k=k: ride(k).wait_send())


def leave(
    part, std_next, grad, w_out, joined, mixed, lhs, weight, std, g_time, g_out, g_in,
    totals, inverse_next, inverse, masked, gains, later_grad, scale,
):
    own, features = std.shape
    cols4 = mixed.shape[1]
    quarter = cols4 // 4
    units = g_in.shape[1]
    dma = pltpu.SemaphoreType.DMA
    anywhere = pl.BlockSpec(memory_space=pl.ANY)
    whole = pl.BlockSpec(memory_space=pltpu.VMEM)
    parity = BLK // 2

    def low(*shape):
        return pltpu.VMEM(shape, BF16)

    def high(*shape):
        return pltpu.VMEM(shape, F32)

    return pl.pallas_call(
        functools.partial(leave_kernel, scale),
        in_specs=[anywhere] * 12 + [whole] * 6,
        out_specs=[whole] * 9,
        out_shape=[
            jax.ShapeDtypeStruct(shape, F32)
            for shape in (
                (3, parity, 2 * quarter), (2 * quarter, parity), (parity, 2 * units), (2 * units, parity),
                (3, parity, BLK), (BLK, parity), (4, own, BLK), (3, BLK), (1, BLK),
            )
        ],
        scratch_shapes=[
            low(4, own, BLK),
            high(own, features), high(own, features), high(own, features), low(*w_out.shape), low(*joined.shape),
            low(*mixed.shape), low(*lhs.shape), low(*weight.shape), low(2 * own, features), low(features, 2 * own),
            low(*mixed.shape), low(features, cols4),
            low(2, BLK, features), low(2, BLK, features), low(4, 2, BLK, BLK), low(4, 2, BLK, BLK), high(2, BLK, BLK),
            low(BLK, BLK), low(BLK, BLK), low(2, parity, BLK), low(2, parity, BLK),
            low(4, BLK, units), low(4, BLK, units), low(4, BLK, units), low(4, BLK, units),
            high(BLK, units), high(BLK, units), low(2, parity, units), low(2, parity, units),
            high(4, features, cols4),
            low(4, 2, BLK, 2 * quarter), low(4, 2, BLK, 2 * quarter), low(4, 2, BLK, 2 * quarter), low(4, 2, BLK, 2 * quarter),
            low(4, BLK, 2 * quarter), low(4, BLK, 2 * quarter), low(4, BLK, 2 * quarter), low(4, BLK, 2 * quarter),
            low(4, BLK, cols4), low(4, BLK, cols4),
            low(own, features), low(own, features), low(own, features),
            low(parity, cols4), low(parity, cols4),
            high(8, features), high(4, 8, features), high(3, 8, features), high(4, 8, BLK),
        ]
        + [dma((4,))] * 10
        + [dma((1,)), dma((1,)), dma((4,)), dma((4,)), dma((3,)), dma((3,)), dma((3,)), dma((3,)), dma((4,)), dma((4,)), dma((4,))]
        + [dma((1,)), dma((1,)), dma((2,)), dma((2,)), dma((4,)), dma((4,)), dma((1,)), dma((1,))]
        + [dma((4,)), dma((4,)), dma((4,)), dma((4,)), dma((2,)), dma((4,)), dma((10,))],
        compiler_params=pltpu.CompilerParams(
            collective_id=3, has_side_effects=True, vmem_limit_bytes=62 * 1024 * 1024
        ),
        cost_estimate=pl.CostEstimate(flops=2 * 10**10, transcendentals=10**6, bytes_accessed=10**8),
        name="leave",
    )(
        part, std_next, grad, w_out, joined, mixed, lhs, weight, std, g_time, g_out, g_in,
        totals, inverse_next, inverse, masked, gains, later_grad,
    )


def tie(*values):
    return lax.optimization_barrier(values)


def norm_rows(resid):
    mean = jnp.mean(resid, axis=-1, keepdims=True)
    centered = resid - mean
    inverse = lax.rsqrt(jnp.mean(centered * centered, axis=-1, keepdims=True) + eps_norm)
    return (centered * inverse, inverse)


def norm_rows_back(grad, standardized, inverse, gain):
    gain_grad = jnp.sum(grad * standardized, axis=0)
    inner = grad * gain
    mean = jnp.mean(inner, axis=-1, keepdims=True)
    along = jnp.mean(inner * standardized, axis=-1, keepdims=True)
    return ((inner - mean - standardized * along) * inverse, gain_grad)


def cols(parts):
    return jnp.concatenate(parts, axis=1)


def rows_of(parts):
    return jnp.concatenate(parts, axis=0)


def token_parallel(
    tokens,
    cotangent,
    ratio,
    priority,
    frame_order,
    mask_embed,
    gains,
    qkv_space,
    out_space,
    qkv_time,
    out_time,
    w_in,
    w_out,
):
    scale = 1.0 / math.sqrt(HEAD_DIM)
    y, x, c, z = (lax.axis_index(name) for name in AXES)
    patches = tokens.shape[2]
    width = qkv_space.shape[0]
    frames_own = tokens.shape[0] * tokens.shape[1] // 4
    frames_all = frame_order.shape[1]
    own = frames_own * patches
    hidden_own = w_in.shape[1] // 2
    plane = 2 * y + x
    k_own = 2 * (z % 2) + c

    masked_here = (priority < ratio[:, None, None]).astype(jnp.int32).reshape(2, -1)
    info = cols([masked_here, frame_order])
    info = jnp.where(z // 2 == c, info, hop_c(info))
    info = lax.dynamic_index_in_dim(info, z % 2, 0, keepdims=False)
    masked = lax.dynamic_slice_in_dim(info, c * own, own, 0)[:, None] != 0
    order = info[2 * own :].reshape(2, 2, frames_own)
    order = jnp.where(y == 1, order[::-1], order)
    order = jnp.where(c == 1, order[:, ::-1], order).swapaxes(0, 1).reshape(frames_all)
    order = jnp.repeat(order, GROUP)
    patch = jnp.arange(frames_all * GROUP) % GROUP
    visible = (order[:, None] <= order[None, :]) & (patch[:, None] == patch[None, :])
    bias = jnp.where(visible, 0.0, -1e30).astype(F32)

    vectors = rows_of([mask_embed[None], gains, jnp.zeros((4, BLK), BF16)])
    head = (2 * y + c) * HEAD_DIM
    ti_own = cols(
        [
            lax.dynamic_slice_in_dim(qkv_time, head, HEAD_DIM, 2).reshape(width, -1),
            lax.dynamic_slice_in_dim(out_time, head, HEAD_DIM, 0).T,
        ]
    )
    (
        ws_qkv, ws_out, wt_all, wf_out, wf_in, joined0, turned0, std0,
        mixed0, total0, inv0, resid1, std1, inv1, normed1, vectors,
    ) = enter(
        tokens.reshape(4, own, BLK),
        vectors,
        jnp.swapaxes(qkv_space, 0, 1),
        out_space,
        ti_own,
        w_out,
        w_in,
        masked.astype(F32),
        scale,
    )

    half = qkv_space.shape[2] // 2
    turned1, joined1, mixed1, total1, delta, upstream, wf_far, wf_in_far = time_call(
        False,
        normed1.reshape(frames_own, patches, width),
        cotangent.reshape(4, own, BLK),
        [wf_out, wf_in],
        wt_all,
        bias,
        scale,
    )
    w_in_half, w_out_half, grad2, grad2_low, block_rows, gain_grad2 = feed(
        resid1, delta.reshape(own, width), upstream, masked.astype(F32), vectors, wf_in, wf_in_far, wf_out, wf_far
    )

    part1, g_time, g_w_in, block_out = time_call(
        True,
        grad2_low.reshape(frames_own, patches, width),
        block_rows,
        [joined1, total1, w_in_half, turned1, mixed1],
        wt_all,
        bias,
        scale,
    )
    block_out = block_out.reshape(tokens.shape)
    grad_qkv_space, grad_out_space, grad_w_in, grad_w_out, grad_qkv_time, grad_out_time, grad_tokens, grad_gains, grad_embed = leave(
        part1.reshape(own, width), std1, grad2, ws_out, joined0, mixed0, turned0, ws_qkv, std0, g_time, w_out_half, g_w_in,
        total0, inv1, inv0, masked.astype(F32), vectors, gain_grad2, scale,
    )
    return (
        block_out,
        grad_tokens.reshape(tokens.shape),
        grad_embed.reshape(BLK),
        grad_gains,
        jnp.swapaxes(grad_qkv_space, 0, 1),
        grad_out_space,
        jnp.swapaxes(grad_qkv_time, 0, 1),
        grad_out_time,
        grad_w_in,
        grad_w_out,
    )


def solution(mesh):
    sizes = (mesh.shape["tm"], mesh.shape["clip"], mesh.shape["mp"])
    if sizes == (2, 4, 4):
        mesh = jax.sharding.Mesh(mesh.devices.reshape(2, 2, 2, 4), AXES)
        step, clip = token_parallel, ("x", "c")
    else:
        step, clip = shards, ("clip",)
    return jax.shard_map(
        step,
        mesh=mesh,
        in_specs=(
            P(clip, "tm", None, "mp"),
            P(clip, "tm", None, "mp"),
            P(clip),
            P(clip, "tm", None),
            P(clip, None),
            P("mp"),
            P(None, "mp"),
            P(None, None, "mp"),
            P("mp", None),
            P(None, None, "mp"),
            P("mp", None),
            P(None, "mp"),
            P("mp", None),
        ),
        out_specs=(
            P(clip, "tm", None, "mp"),
            P(clip, "tm", None, "mp"),
            P("mp"),
            P(None, "mp"),
            P(("tm",) + clip, None, "mp"),
            P("mp", ("tm",) + clip),
            P(("tm",) + clip, None, "mp"),
            P("mp", ("tm",) + clip),
            P(("tm",) + clip, "mp"),
            P("mp", ("tm",) + clip),
        ),
        check_vma=False,
    )
```

```python
import functools
import math

import jax
import jax.numpy as jnp
from jax import lax
from jax.experimental import pallas as pl
from jax.experimental.pallas import tpu as pltpu
from jax.sharding import PartitionSpec as P

HEAD_DIM = 64
MICRO = 2


eps_norm = 1e-05


def gelu_tanh(values):
    return jax.nn.gelu(values, approximate=True)


def norm_forward_pass(residual_stream, gain_coefficients, complete_width):
    reduced_totals = lax.psum(
        (jnp.sum(residual_stream, axis=-1), jnp.sum(residual_stream * residual_stream, axis=-1)),
        "mp",
    )
    centered_rows = reduced_totals[0] / complete_width
    spread = reduced_totals[1] / complete_width - centered_rows * centered_rows
    inverse_scale = lax.rsqrt(spread + eps_norm)
    standardized_rows = (residual_stream - centered_rows[:, None]) * inverse_scale[:, None]
    shard_rows = (standardized_rows * gain_coefficients).astype(jnp.bfloat16)
    normalized_rows = lax.all_gather(shard_rows, "mp", axis=1, tiled=True)
    return (normalized_rows, standardized_rows, inverse_scale)


def norm_reverse_pass(
    normalized_gradient, standardized_rows, inverse_scale, gain_coefficients, complete_width
):
    gain_gradient = jnp.sum(normalized_gradient * standardized_rows, axis=0)
    standardized_gradient = normalized_gradient * gain_coefficients
    reduced_totals = lax.psum(
        (
            jnp.sum(standardized_gradient, axis=-1),
            jnp.sum(standardized_gradient * standardized_rows, axis=-1),
        ),
        "mp",
    )
    grad_resid = (
        standardized_gradient
        - reduced_totals[0][:, None] / complete_width
        - standardized_rows * (reduced_totals[1][:, None] / complete_width)
    ) * inverse_scale[:, None]
    return (grad_resid, gain_gradient)


def sum_features(grad_full):
    return lax.psum_scatter(
        grad_full.astype(jnp.bfloat16), "mp", scatter_dimension=1, tiled=True
    ).astype(jnp.float32)


def branch_out(hidden, weight):
    partial_rows = jnp.dot(hidden, weight, preferred_element_type=jnp.float32)
    return lax.psum_scatter(partial_rows, "mp", scatter_dimension=1, tiled=True)


def branch_back(grad_resid, hidden, weight):
    grad_rows = lax.all_gather(grad_resid.astype(jnp.bfloat16), "mp", axis=1, tiled=True)
    weight_grad = jnp.einsum("rk,rd->kd", hidden, grad_rows, preferred_element_type=jnp.float32)
    grad_hidden = jnp.einsum("rd,kd->rk", grad_rows, weight, preferred_element_type=jnp.float32)
    return (grad_hidden, weight_grad)


def qkv_back(normalized_rows, grad_joined, weight):
    weight_grad = jnp.einsum(
        "rd,trk->dtk", normalized_rows, grad_joined, preferred_element_type=jnp.float32
    )
    grad_full = jnp.einsum("trk,dtk->rd", grad_joined, weight, preferred_element_type=jnp.float32)
    return (weight_grad, sum_features(grad_full))


def reduce_grads(local_grads, small_grads):
    reduced = (
        lax.psum_scatter(local_grads[0], ("tm", "clip"), scatter_dimension=0, tiled=True),
        lax.psum_scatter(local_grads[1], ("tm", "clip"), scatter_dimension=1, tiled=True),
        lax.psum_scatter(local_grads[2], ("tm", "clip"), scatter_dimension=0, tiled=True),
        lax.psum_scatter(local_grads[3], ("tm", "clip"), scatter_dimension=1, tiled=True),
        lax.psum_scatter(local_grads[4], ("tm", "clip"), scatter_dimension=0, tiled=True),
        lax.psum_scatter(local_grads[5], ("tm", "clip"), scatter_dimension=1, tiled=True),
    )
    reduced_small = lax.psum((small_grads[0], small_grads[1]), ("tm", "clip"))
    return (reduced, reduced_small)


def space_forward(normalized_rows, weight, frame_count, patches, heads_local, scale):
    joined = jnp.einsum(
        "rd,dtk->trk", normalized_rows, weight, preferred_element_type=jnp.float32
    ).astype(jnp.bfloat16)
    shape_heads = (frame_count, patches, heads_local, HEAD_DIM)
    scores = (
        jnp.einsum(
            "bshd,bthd->bhst",
            joined[0].reshape(shape_heads),
            joined[1].reshape(shape_heads),
            preferred_element_type=jnp.float32,
        )
        * scale
    )
    highest = jnp.max(scores, axis=-1, keepdims=True)
    exponent = jnp.exp(scores - highest)
    reduced_totals = jnp.sum(exponent, axis=-1, keepdims=True)
    log_total = highest + jnp.log(reduced_totals)
    attention = (exponent / reduced_totals).astype(jnp.bfloat16)
    mixed = jnp.einsum(
        "bhst,bthd->bshd",
        attention,
        joined[2].reshape(shape_heads),
        preferred_element_type=jnp.float32,
    )
    return (
        joined,
        log_total,
        mixed.astype(jnp.bfloat16).reshape(frame_count * patches, heads_local * HEAD_DIM),
    )


def space_backward(grad_mixed, joined, log_total, frame_count, patches, heads_local, scale):
    shape_heads = (frame_count, patches, heads_local, HEAD_DIM)
    queries = joined[0].reshape(shape_heads)
    key_rows = joined[1].reshape(shape_heads)
    values = joined[2].reshape(shape_heads)
    grad_out = grad_mixed.reshape(shape_heads)
    scores = (
        jnp.einsum("bshd,bthd->bhst", queries, key_rows, preferred_element_type=jnp.float32) * scale
    )
    attention = jnp.exp(scores - log_total)
    grad_values = jnp.einsum(
        "bhst,bshd->bthd",
        attention.astype(jnp.bfloat16),
        grad_out,
        preferred_element_type=jnp.float32,
    )
    grad_att = jnp.einsum("bshd,bthd->bhst", grad_out, values, preferred_element_type=jnp.float32)
    grad_scores = (
        attention * (grad_att - jnp.sum(attention * grad_att, axis=-1, keepdims=True))
    ).astype(jnp.bfloat16)
    grad_queries = (
        jnp.einsum("bhst,bthd->bshd", grad_scores, key_rows, preferred_element_type=jnp.float32)
        * scale
    )
    grad_keys = (
        jnp.einsum("bhst,bshd->bthd", grad_scores, queries, preferred_element_type=jnp.float32)
        * scale
    )
    row_count = frame_count * patches
    stacked = jnp.stack(
        [
            grad_queries.reshape(row_count, -1),
            grad_keys.reshape(row_count, -1),
            grad_values.reshape(row_count, -1),
        ]
    )
    return stacked.astype(jnp.bfloat16)


def time_scores(queries, keys_all, visible, scale):
    scores = (
        jnp.einsum("cfshd,cgshd->chfgs", queries, keys_all, preferred_element_type=jnp.float32)
        * scale
    )
    return jnp.where(visible, scores, -1e30)


def time_forward(queries, keys_all, values_all, visible, scale):
    scores = time_scores(queries, keys_all, visible, scale)
    highest = jnp.max(scores, axis=3, keepdims=True)
    exponent = jnp.exp(scores - highest)
    reduced_totals = jnp.sum(exponent, axis=3, keepdims=True)
    log_total = highest + jnp.log(reduced_totals)
    attention = (exponent / reduced_totals).astype(jnp.bfloat16)
    mixed = jnp.einsum(
        "chfgs,cgshd->cfshd", attention, values_all, preferred_element_type=jnp.float32
    )
    return (log_total, mixed.astype(jnp.bfloat16))


def time_backward(grad_mixed, queries, keys_all, values_all, visible, log_total, scale):
    grad_out = grad_mixed.reshape(queries.shape)
    scores = time_scores(queries, keys_all, visible, scale)
    attention = jnp.exp(scores - log_total)
    grad_values = jnp.einsum(
        "chfgs,cfshd->cgshd",
        attention.astype(jnp.bfloat16),
        grad_out,
        preferred_element_type=jnp.float32,
    )
    grad_att = jnp.einsum(
        "cfshd,cgshd->chfgs", grad_out, values_all, preferred_element_type=jnp.float32
    )
    grad_scores = (
        attention * (grad_att - jnp.sum(attention * grad_att, axis=3, keepdims=True))
    ).astype(jnp.bfloat16)
    grad_queries = (
        jnp.einsum("chfgs,cgshd->cfshd", grad_scores, keys_all, preferred_element_type=jnp.float32)
        * scale
    )
    grad_keys = (
        jnp.einsum("chfgs,cfshd->cgshd", grad_scores, queries, preferred_element_type=jnp.float32)
        * scale
    )
    return (grad_queries, grad_keys, grad_values)


def shards(
    tokens,
    cotangent,
    ratio,
    priority,
    frame_order,
    mask_embed,
    gains,
    qkv_space,
    out_space,
    qkv_time,
    out_time,
    w_in,
    w_out,
):
    scale = 1.0 / math.sqrt(HEAD_DIM)
    clips_local = tokens.shape[0] // MICRO
    frames_local = tokens.shape[1]
    patches = tokens.shape[2]
    cols_local = tokens.shape[3]
    frames_all = frame_order.shape[1]
    hidden_width = qkv_space.shape[0]
    joined_local = qkv_space.shape[2]
    heads_local = joined_local // HEAD_DIM
    row_count = clips_local * frames_local * patches
    gain_broadcast = gains.astype(jnp.float32)
    embed_row = mask_embed.astype(jnp.float32)
    first_frame = lax.axis_index("tm") * frames_local
    shape_local = (clips_local, frames_local, patches, joined_local)
    shape_heads = (clips_local, frames_local, patches, heads_local, HEAD_DIM)
    shape_all = (clips_local, frames_all, patches, heads_local, HEAD_DIM)
    outputs = []
    input_grads = []
    weight_total = None
    small_total = None
    for batch_index in range(MICRO):
        lower = batch_index * clips_local
        upper = lower + clips_local
        source = tokens[lower:upper].reshape(row_count, cols_local).astype(jnp.float32)
        upstream = cotangent[lower:upper].reshape(row_count, cols_local).astype(jnp.float32)
        masked = (priority[lower:upper] < ratio[lower:upper][:, None, None]).reshape(row_count)
        order_rows = frame_order[lower:upper]
        residual_stream0 = jnp.where(masked[:, None], embed_row[None, :], source)
        normalized_rows0, standardized_rows0, inverse_deviation0 = norm_forward_pass(
            residual_stream0, gain_broadcast[0], hidden_width
        )
        joined0, total0, mixed0 = space_forward(
            normalized_rows0, qkv_space, clips_local * frames_local, patches, heads_local, scale
        )
        residual_stream1 = residual_stream0 + branch_out(mixed0, out_space)
        normalized_rows1, standardized_rows1, inverse_deviation1 = norm_forward_pass(
            residual_stream1, gain_broadcast[1], hidden_width
        )
        joined1 = jnp.einsum(
            "rd,dtk->trk", normalized_rows1, qkv_time, preferred_element_type=jnp.float32
        ).astype(jnp.bfloat16)
        queries_local = joined1[0].reshape(shape_local)
        keys_local = joined1[1].reshape(shape_local)
        values_local = joined1[2].reshape(shape_local)
        keys_all, values_all = (
            lax.all_gather(keys_local, "tm", axis=1, tiled=True),
            lax.all_gather(values_local, "tm", axis=1, tiled=True),
        )
        query_order = lax.dynamic_slice_in_dim(order_rows, first_frame, frames_local, axis=1)
        time_visible = (order_rows[:, None, :] <= query_order[:, :, None])[:, None, :, :, None]
        time_q = queries_local.reshape(shape_heads)
        time_k = keys_all.reshape(shape_all)
        time_v = values_all.reshape(shape_all)
        total1, mixed_frames = time_forward(time_q, time_k, time_v, time_visible, scale)
        mixed1 = mixed_frames.reshape(row_count, joined_local)
        residual_stream2 = residual_stream1 + branch_out(mixed1, out_time)
        normalized_rows2, standardized_rows2, inverse_deviation2 = norm_forward_pass(
            residual_stream2, gain_broadcast[2], hidden_width
        )
        projected = jnp.dot(normalized_rows2, w_in, preferred_element_type=jnp.float32)
        activated, gelu_pull = jax.vjp(gelu_tanh, projected)
        hidden = activated.astype(jnp.bfloat16)
        resid3 = residual_stream2 + branch_out(hidden, w_out)
        outputs.append(
            resid3.astype(jnp.bfloat16).reshape(clips_local, frames_local, patches, cols_local)
        )
        grad3 = jnp.where(masked[:, None], upstream, 0.0)
        grad_hidden, grad_w_out = branch_back(grad3, hidden, w_out)
        grad_inner = gelu_pull(grad_hidden)[0].astype(jnp.bfloat16)
        grad_w_in = jnp.einsum(
            "rd,rk->dk", normalized_rows2, grad_inner, preferred_element_type=jnp.float32
        )
        normalized_gradient2 = sum_features(
            jnp.einsum("rk,dk->rd", grad_inner, w_in, preferred_element_type=jnp.float32)
        )
        backward_third, gain_gradient2 = norm_reverse_pass(
            normalized_gradient2,
            standardized_rows2,
            inverse_deviation2,
            gain_broadcast[2],
            hidden_width,
        )
        grad2 = grad3 + backward_third
        grad_mixed1, grad_out_time = branch_back(grad2, mixed1, out_time)
        grad_mixed_low = grad_mixed1.astype(jnp.bfloat16).reshape(shape_local)
        grad_queries, grad_keys, grad_values = time_backward(
            grad_mixed_low, time_q, time_k, time_v, time_visible, total1, scale
        )
        key_part, value_part = (
            lax.psum_scatter(
                grad_keys.reshape(clips_local, frames_all, patches, joined_local).astype(
                    jnp.bfloat16
                ),
                "tm",
                scatter_dimension=1,
                tiled=True,
            ).astype(jnp.float32),
            lax.psum_scatter(
                grad_values.reshape(clips_local, frames_all, patches, joined_local).astype(
                    jnp.bfloat16
                ),
                "tm",
                scatter_dimension=1,
                tiled=True,
            ).astype(jnp.float32),
        )
        grad_joined1 = jnp.stack(
            [
                grad_queries.reshape(row_count, joined_local),
                key_part.reshape(row_count, joined_local),
                value_part.reshape(row_count, joined_local),
            ]
        ).astype(jnp.bfloat16)
        grad_qkv_time, normalized_gradient1 = qkv_back(normalized_rows1, grad_joined1, qkv_time)
        backward_second, gain_gradient1 = norm_reverse_pass(
            normalized_gradient1,
            standardized_rows1,
            inverse_deviation1,
            gain_broadcast[1],
            hidden_width,
        )
        grad1 = grad2 + backward_second
        grad_mixed0, grad_out_space = branch_back(grad1, mixed0, out_space)
        grad_joined0 = space_backward(
            grad_mixed0.astype(jnp.bfloat16),
            joined0,
            total0,
            clips_local * frames_local,
            patches,
            heads_local,
            scale,
        )
        grad_qkv_space, normalized_gradient0 = qkv_back(normalized_rows0, grad_joined0, qkv_space)
        backward_first, gain_gradient0 = norm_reverse_pass(
            normalized_gradient0,
            standardized_rows0,
            inverse_deviation0,
            gain_broadcast[0],
            hidden_width,
        )
        grad0 = grad1 + backward_first
        input_grads.append(
            jnp.where(masked[:, None], 0.0, grad0).reshape(
                clips_local, frames_local, patches, cols_local
            )
        )
        grad_embed = jnp.sum(jnp.where(masked[:, None], grad0, 0.0), axis=0)
        gain_grads = jnp.stack([gain_gradient0, gain_gradient1, gain_gradient2])
        local_grads = (
            grad_qkv_space,
            grad_out_space,
            grad_qkv_time,
            grad_out_time,
            grad_w_in,
            grad_w_out,
        )
        small_grads = (gain_grads, grad_embed)
        reduced, reduced_small = reduce_grads(local_grads, small_grads)
        if weight_total is None:
            weight_total = reduced
            small_total = reduced_small
        else:
            weight_total = tuple((total + grad for total, grad in zip(weight_total, reduced)))
            small_total = tuple((total + grad for total, grad in zip(small_total, reduced_small)))
    return (
        jnp.concatenate(outputs, axis=0),
        jnp.concatenate(input_grads, axis=0),
        small_total[1],
        small_total[0],
        weight_total[0],
        weight_total[1],
        weight_total[2],
        weight_total[3],
        weight_total[4],
        weight_total[5],
    )


AXES = ("tm", "x", "c", "mp")
F32 = jnp.float32
BF16 = jnp.bfloat16
BLK = 256
MESH = pl.DeviceIdType.MESH


def device_pairs(move):
    pairs = []
    for y in range(2):
        for x in range(2):
            for c in range(2):
                for z in range(4):
                    there = move(y, x, c, z)
                    pairs.append(tuple(((q[0] * 2 + q[1]) * 2 + q[2]) * 4 + q[3] for q in ((y, x, c, z), there)))
    return pairs


def hop_y(v):
    return lax.ppermute(v, AXES, device_pairs(lambda y, x, c, z: (1 - y, x, c, z)))


def hop_x(v):
    return lax.ppermute(v, AXES, device_pairs(lambda y, x, c, z: (y, 1 - x, c, z)))


def hop_c(v):
    return lax.ppermute(v, AXES, device_pairs(lambda y, x, c, z: (y, x, 1 - c, z)))


def hop_z(v, shift):
    return lax.ppermute(v, AXES, device_pairs(lambda y, x, c, z: (y, x, c, (z + shift) % 4)))


def spread_pairs(r):
    def move(y, x, c, z):
        k = z ^ r
        return (y, x, k & 1, 2 * c + (k >> 1))

    return device_pairs(move)


def dot_nn(a, b):
    return lax.dot_general(a, b, (((1,), (0,)), ((), ())), preferred_element_type=F32)


def dot_nt(a, b):
    return lax.dot_general(a, b, (((1,), (1,)), ((), ())), preferred_element_type=F32)


def dot_tn(a, b):
    return lax.dot_general(a, b, (((0,), (0,)), ((), ())), preferred_element_type=F32)


def attend_pair(q, k, v, bias, scale):
    mixed, totals = [], []
    for i in range(2):
        mine = slice(i * HEAD_DIM, (i + 1) * HEAD_DIM)
        scores = dot_nt(k[:, mine], q[:, mine]) * scale
        if bias is not None:
            scores = scores + bias
        highest = jnp.max(scores, axis=0, keepdims=True)
        exponent = jnp.exp(scores - highest)
        total = jnp.sum(exponent, axis=0, keepdims=True)
        totals.append(highest + jnp.log(total))
        mixed.append(dot_tn(v[:, mine], exponent.astype(BF16)) * (1.0 / total))
    return (jnp.concatenate(mixed, axis=0).T, totals)


def attend_pair_back(q, k, v, g, totals, bias, scale):
    grads = ([], [], [])
    for i in range(2):
        mine = slice(i * HEAD_DIM, (i + 1) * HEAD_DIM)
        scores = dot_nt(k[:, mine], q[:, mine]) * scale
        if bias is not None:
            scores = scores + bias
        p = jnp.exp(scores - totals[i])
        dp = dot_nt(v[:, mine], g[:, mine])
        ds = (p * (dp - jnp.sum(p * dp, axis=0, keepdims=True))).astype(BF16)
        grads[0].append(dot_tn(k[:, mine], ds) * scale)
        grads[1].append(dot_nn(ds, q[:, mine]) * scale)
        grads[2].append(dot_nn(p.astype(BF16), g[:, mine]))
    return (
        jnp.concatenate(grads[0], axis=0).T,
        jnp.concatenate(grads[1], axis=1),
        jnp.concatenate(grads[2], axis=1),
    )


PAIR = 2 * HEAD_DIM


def enter_kernel(
    scale,
    tok, vec, qkv_hbm, out_hbm, time_hbm, time_out_hbm, feed_hbm, first_hbm, masked,
    wq_out, wo_out, wt, wf, wi, joined_out, turned_out, std_out,
    mixed, total_out, inverse, resid_out, next_out, inverse_next, low_out, vec_out,
    rows_in, vec_in, wq, wo, normed, joined, turned, std, base, part, part_out, part_in, resid, std_next, low_next,
    later, head_in, head_out,
    z_send, z_recv, y_send, y_recv, x_send, x_recv, p_send, p_recv, q_send, q_recv,
    t_send, t_recv, v_send, v_recv, u_send, u_recv, w_send, w_recv,
    f_send, f_recv, g_send, g_recv, n_send, n_recv, local, saved,
    i_send, i_recv, j_send, j_recv, k_send, k_recv, l_send, l_recv,
):
    y, x, c, z = (lax.axis_index(name) for name in AXES)
    half = wo.shape[0] // 4
    wide = 3 * half
    span = wt.shape[1] // 4
    size = wf.shape[1] // 4
    own = rows_in.shape[0]
    near_y, near_x, pair = (1 - y, x, c, z), (y, 1 - x, c, z), (y, x, 1 - c, z)
    right_z, left_z = (y, x, c, (z + 1) % 4), (y, x, c, (z + 3) % 4)

    def at(i, length):
        return pl.ds(pl.multiple_of(i * length, length), length)

    def remote(src, dst, send, recv, peer):
        return pltpu.make_async_remote_copy(
            src_ref=src, dst_ref=dst, send_sem=send, recv_sem=recv, device_id=peer, device_id_type=MESH
        )

    def start(all_copies):
        for copy in all_copies:
            copy.start()

    def landed(all_copies):
        for copy in all_copies:
            copy.wait_recv()

    def sent(all_copies):
        for copy in all_copies:
            copy.wait_send()

    core = at(c, half)
    keep = [
        pltpu.make_async_copy(
            qkv_hbm.at[j, :, core], wq.at[:, pl.ds(pl.multiple_of(z * wide + j * half, half), half)], local.at[j]
        )
        for j in range(3)
    ] + [pltpu.make_async_copy(out_hbm.at[core], wo.at[at(z, half)], local.at[3])]
    keep_later = [
        pltpu.make_async_copy(later, wt.at[:, at(z, span)], local.at[4]),
        pltpu.make_async_copy(feed_hbm.at[at(c, 4 * size)], wf.at[z], local.at[5]),
        pltpu.make_async_copy(first_hbm.at[:, at(c, 4 * size)], wi.at[z], local.at[8]),
    ]
    head = [
        pltpu.make_async_copy(time_hbm.at[:, :, at(y, PAIR)], head_in, local.at[9]),
        pltpu.make_async_copy(time_out_hbm.at[at(2 * y + c, HEAD_DIM)], head_out, local.at[10]),
    ]
    start(keep + keep_later[1:] + head)

    barrier = pltpu.get_barrier_semaphore()
    for dc in range(2):
        for dz in range(4):
            if dc or dz:
                peer = (y, x, (c + dc) % 2, (z + dz) % 4)
                pl.semaphore_signal(barrier, inc=1, device_id=peer, device_id_type=MESH)
    for peer in (near_y, near_x):
        pl.semaphore_signal(barrier, inc=1, device_id=peer, device_id_type=MESH)
    pl.semaphore_wait(barrier, 9)

    def spot(dy, dx):
        return 2 * ((y + dy) % 2) + (x + dx) % 2

    def piece(dy, dx, r, split=False):
        s = (z + r) % 4
        rows = at(spot(dy, dx), BLK)
        first = pl.multiple_of(s * wide, half)
        out = wo.at[at(s, half), at(spot(dy, dx), BLK)]
        if split:
            last = pl.multiple_of(s * wide + 2 * half, half)
            return (wq.at[rows, pl.ds(first, 2 * half)], wq.at[rows, pl.ds(last, half)], out)
        return (wq.at[rows, pl.ds(first, wide)], out)

    def time_piece(dx, r):
        return wt.at[at((x + dx) % 2, 2 * BLK), at((z + r) % 4, span)]

    def feed_piece(dy, r):
        return wf.at[(z + r) % 4, at(spot(dy, 0), size)]

    def copies(parts, send, recv, peer):
        return [remote(ref, ref, send.at[i], recv.at[i], peer) for i, ref in enumerate(parts)]

    def leg(right, step):
        if right:
            return (0 if step == 0 else 4 - step), right_z, 3 - step
        return step, left_z, step + 1

    def z_copies(right, step):
        r, peer, lands = leg(right, step)
        return copies(piece(0, 0, r), z_send.at[int(right), step], z_recv.at[lands], peer)

    def time_z(right, step):
        r, peer, lands = leg(right, step)
        source = later.at[at(x, 2 * BLK)] if step == 0 else time_piece(0, r)
        return [remote(source, time_piece(0, r), u_send.at[int(right), step], u_recv.at[lands], peer)]

    def feed_z(right, step):
        r, peer, lands = leg(right, step)
        source = feed_hbm.at[at(4 * c + spot(0, 0), size)] if step == 0 else feed_piece(0, r)
        return [remote(source, feed_piece(0, r), f_send.at[int(right), step], f_recv.at[lands], peer)]

    def first_piece(dy, dx, r):
        return wi.at[(z + r) % 4, at(spot(dy, dx), BLK)]

    def first_z(right, step):
        r, peer, lands = leg(right, step)
        source = first_hbm.at[at(spot(0, 0), BLK), at(c, 4 * size)] if step == 0 else first_piece(0, 0, r)
        return [remote(source, first_piece(0, 0, r), i_send.at[int(right), step], i_recv.at[lands], peer)]

    def first_y(r, dy=0):
        return [remote(first_piece(dy, 0, r), first_piece(dy, 0, r), j_send.at[r], j_recv.at[r], near_y)]

    def first_x(r, dx=0):
        return [remote(first_piece(0, dx, r), first_piece(0, dx, r), k_send.at[r], k_recv.at[r], near_x)]

    def y_copies(r, dy=0):
        return copies(piece(dy, 0, r), y_send.at[r], y_recv.at[r], near_y)

    def x_copies(r, dx=0):
        return copies(piece(0, dx, r), x_send.at[r], x_recv.at[r], near_x)

    def corner_x(r, dx=0):
        return copies(piece(1, dx, r, split=True)[:1], p_send.at[r], p_recv.at[r], near_x)

    def corner_y(r, dy=0):
        return copies(piece(dy, 1, r, split=True)[1:], q_send.at[r], q_recv.at[r], near_y)

    def time_x(r, dx=0):
        return [remote(time_piece(dx, r), time_piece(dx, r), w_send.at[r], w_recv.at[r], near_x)]

    def feed_y(r, dy=0):
        return [remote(feed_piece(dy, r), feed_piece(dy, r), g_send.at[r], g_recv.at[r], near_y)]

    def token_copies(k):
        peer = (y, x, k % 2, 2 * c + k // 2)
        return [
            remote(tok.at[k], rows_in.at[:, at(z, BLK)], t_send.at[k], t_recv.at[z], peer),
            remote(vec, vec_in.at[:, at(z, BLK)], v_send.at[k], v_recv.at[z], peer),
        ]

    def token_local(k):
        return [
            pltpu.make_async_copy(tok.at[k], rows_in.at[:, at(z, BLK)], local.at[6]),
            pltpu.make_async_copy(vec, vec_in.at[:, at(z, BLK)], local.at[7]),
        ]

    def stays(k):
        return jnp.logical_and(2 * c + k // 2 == z, c == k % 2)

    def start_tokens(ks):
        for k in ks:
            pl.when(stays(k))(lambda k=k: start(token_local(k)))
            pl.when(jnp.logical_not(stays(k)))(lambda k=k: start(token_copies(k)))

    def each_side(j, act):
        pl.when(z >= j + 1)(lambda: act(3 - j, True))
        pl.when(z <= 2 - j)(lambda: act(j + 1, False))

    def begin(make):
        pl.when(z < 3)(lambda: start(make(True, 0)))
        pl.when(z > 0)(lambda: start(make(False, 0)))

    def onward(j, make, right):
        if j < 2:
            pl.when(z < 3 if right else z > 0)(lambda: start(make(right, j + 1)))

    def forward(j):
        def act(r, right):
            landed(copies(piece(0, 0, r), z_send.at[0, 0], z_recv.at[r], near_y))
            onward(j, z_copies, right)
            start(y_copies(r))
            start(x_copies(r))

        each_side(j, act)

    def corners(j):
        def act(r, right):
            landed(y_copies(r, 1))
            start(corner_x(r))
            landed(x_copies(r, 1))
            start(corner_y(r))

        each_side(j, act)

    def time_forward_step(j):
        def act(r, right):
            landed([remote(time_piece(0, r), time_piece(0, r), u_send.at[0, 0], u_recv.at[r], near_x)])
            onward(j, time_z, right)
            start(time_x(r))

        each_side(j, act)

    def feed_forward_step(j):
        def act(r, right):
            landed([remote(feed_piece(0, r), feed_piece(0, r), f_send.at[0, 0], f_recv.at[r], near_y)])
            onward(j, feed_z, right)
            start(feed_y(r))

        each_side(j, act)

    def first_corner_copy(r, dx=0):
        return [remote(first_piece(1, dx, r), first_piece(1, dx, r), l_send.at[r], l_recv.at[r], near_x)]

    def first_corner(j):
        def act(r, right):
            landed(first_y(r, 1))
            start(first_corner_copy(r))

        each_side(j, act)

    def first_forward_step(j):
        def act(r, right):
            landed([remote(first_piece(0, 0, r), first_piece(0, 0, r), i_send.at[0, 0], i_recv.at[r], near_y)])
            onward(j, first_z, right)
            start(first_y(r))
            start(first_x(r))

        each_side(j, act)

    for copy in keep:
        copy.wait()
    begin(z_copies)

    def gather_head(i, carry):
        rows = at(i, BLK)
        parts = [head_in[j, rows].astype(F32) for j in range(3)]
        parts = [jnp.where(c == 0, v[:, :HEAD_DIM], v[:, HEAD_DIM:]) for v in parts]
        parts.append(head_out[:, rows].astype(F32).T)
        later[rows] = jnp.concatenate(parts, axis=1).astype(BF16)
        return carry

    for copy in head:
        copy.wait()
    lax.fori_loop(0, later.shape[0] // BLK, gather_head, 0)
    keep_later[0].start()
    forward(0)
    start_tokens((0, 1))
    forward(1)
    start_tokens((2, 3))
    begin(first_z)
    begin(time_z)
    begin(feed_z)
    corners(0)
    forward(2)
    corners(1)
    for k in range(4):
        def finish_local(k=k):
            for copy in token_local(k):
                copy.wait()

        pl.when(stays(k))(finish_local)
    for s in range(4):
        def arrived(s=s):
            landed([
                remote(tok.at[0], rows_in.at[:, at(s, BLK)], t_send.at[0], t_recv.at[s], near_y),
                remote(vec, vec_in.at[:, at(s, BLK)], v_send.at[0], v_recv.at[s], near_y),
            ])

        pl.when(jnp.logical_not(jnp.logical_and(z == s, z // 2 == c)))(arrived)

    step = own // 2
    slab = 128
    vec_out[...] = vec_in[...].astype(F32)

    def first_norm(i, carry):
        rows = at(i, step)
        value = jnp.where(masked[rows] > 0.0, vec_out[0:1], rows_in[rows].astype(F32))
        base[rows] = value
        standard, inv = norm_rows(value)
        std[rows] = standard
        inverse[rows] = inv
        normed[rows] = (standard * vec_out[1:2]).astype(BF16)
        return carry

    lax.fori_loop(0, 2, first_norm, 0)
    give_normed = remote(normed.at[pl.ds(0, own)], normed.at[pl.ds(own, own)], n_send.at[0], n_recv.at[0], pair)
    give_normed.start()
    corners(2)

    def turn(i, carry):
        turned[:, at(i, slab)] = normed[at(i, slab)].T
        return carry

    lax.fori_loop(0, own // slab, turn, 0)
    for r in (1, 2, 3):
        landed(corner_x(r, 1))
        landed(corner_y(r, 1))
    saves = [
        pltpu.make_async_copy(wq, wq_out, saved.at[0]),
        pltpu.make_async_copy(wo, wo_out, saved.at[1]),
        pltpu.make_async_copy(std, std_out, saved.at[2]),
    ]
    start(saves)
    first_forward_step(0)

    def attend(i, carry):
        rows = at(i, slab)
        for h in range(wo.shape[0] // PAIR):
            q, k, v = (joined[rows, (3 * h + j) * PAIR : (3 * h + j + 1) * PAIR] for j in range(3))
            out, totals = attend_pair(q, k, v, None, scale)
            mixed[rows, h * PAIR : (h + 1) * PAIR] = out.astype(BF16)
            for j in range(2):
                total_out[i, 2 * h + j : 2 * h + j + 1, :] = totals[j]
        return carry

    def project(t):
        rows = pl.ds(t * own, own)
        joined[rows] = dot_nn(normed[rows], wq[...]).astype(BF16)

    frames = own // slab
    project(0)
    time_forward_step(0)
    lax.fori_loop(0, frames, attend, 0)
    part[...] = dot_nn(mixed[pl.ds(0, own)], wo[...])
    feed_forward_step(0)
    first_forward_step(1)
    first_corner(0)
    give_normed.wait_recv()
    project(1)
    saves.append(pltpu.make_async_copy(joined, joined_out, saved.at[3]))
    saves[3].start()
    lax.fori_loop(frames, 2 * frames, attend, 0)
    part_out[...] = dot_nn(mixed[pl.ds(own, own)], wo[...]).astype(BF16)
    give_part = remote(part_out, part_in, n_send.at[1], n_recv.at[1], pair)
    give_part.start()
    time_forward_step(1)
    feed_forward_step(1)
    first_corner(1)
    lax.fori_loop(own // slab, 2 * own // slab, turn, 0)
    saves.append(pltpu.make_async_copy(turned, turned_out, saved.at[4]))
    saves[4].start()
    give_part.wait_recv()
    first_forward_step(2)

    def second_norm(i, carry):
        rows = at(i, step)
        value = base[rows] + part[rows] + part_in[rows].astype(F32)
        resid[rows] = value
        standard, inv = norm_rows(value)
        std_next[rows] = standard
        inverse_next[rows] = inv
        low_next[rows] = (standard * vec_out[2:3]).astype(BF16)
        return carry

    lax.fori_loop(0, 2, second_norm, 0)
    for i, (src, dst) in enumerate(((resid, resid_out), (std_next, next_out), (low_next, low_out))):
        saves.append(pltpu.make_async_copy(src, dst, saved.at[5 + i]))
        saves[-1].start()
    time_forward_step(2)
    feed_forward_step(2)

    def first_ends(j):
        def act(r, right):
            if j == 2:
                landed(first_y(r, 1))
            else:
                landed(first_corner_copy(r, 1))
                sent(first_corner_copy(r))

        each_side(j, act)

    for j in range(3):
        first_ends(j)
    for copy in keep_later + saves:
        copy.wait()
    give_normed.wait_send()
    give_part.wait_send()
    for r in (1, 2, 3):
        landed(time_x(r, 1))
        landed(feed_y(r, 1))
        landed(first_x(r, 1))
        for group in (y_copies(r), x_copies(r), corner_x(r), corner_y(r), time_x(r), feed_y(r), first_y(r), first_x(r)):
            sent(group)
    for step_z in range(3):
        for make in (z_copies, time_z, first_z, feed_z):
            pl.when(jnp.logical_and(z >= step_z, z < 3))(lambda step_z=step_z, make=make: sent(make(True, step_z)))
            pl.when(jnp.logical_and(z + step_z <= 3, z > 0))(lambda step_z=step_z, make=make: sent(make(False, step_z)))
    for k in range(4):
        pl.when(jnp.logical_not(stays(k)))(lambda k=k: sent(token_copies(k)))


def enter(tok, vec, qkv, out, time_qkv, time_out, feed_weight, first_weight, masked, scale):
    own, width, half = tok.shape[1], 4 * tok.shape[2], out.shape[0] // 2
    size = feed_weight.shape[0] // 2
    dma = pltpu.SemaphoreType.DMA
    anywhere = pl.BlockSpec(memory_space=pl.ANY)
    whole = pl.BlockSpec(memory_space=pltpu.VMEM)
    heads = 4 * half // HEAD_DIM

    def low(*shape):
        return pltpu.VMEM(shape, BF16)

    def high(*shape):
        return pltpu.VMEM(shape, F32)

    shapes = [
        ((width, 12 * half), BF16), ((4 * half, width), BF16), ((width, 16 * HEAD_DIM), BF16),
        ((4, size, width), BF16), ((4, width, size), BF16), ((2 * own, 12 * half), BF16), ((width, 2 * own), BF16), ((own, width), F32),
        ((2 * own, 4 * half), BF16), ((2 * own // 128, heads, 128), F32), ((own, 1), F32), ((own, width), F32),
        ((own, width), F32), ((own, 1), F32), ((own, width), BF16), ((vec.shape[0], width), F32),
    ]
    return pl.pallas_call(
        functools.partial(enter_kernel, scale),
        in_specs=[anywhere] * 8 + [whole],
        out_specs=[anywhere] * 8 + [whole] * 3 + [anywhere] * 2 + [whole, anywhere, whole],
        out_shape=[jax.ShapeDtypeStruct(shape, kind) for shape, kind in shapes],
        scratch_shapes=[
            low(own, width), low(vec.shape[0], width), low(width, 12 * half), low(4 * half, width),
            low(2 * own, width), low(2 * own, 12 * half), low(width, 2 * own), high(own, width), high(own, width),
            high(own, width), low(own, width), low(own, width), high(own, width), high(own, width), low(own, width),
            low(width, 4 * HEAD_DIM), low(3, width, PAIR), low(HEAD_DIM, width),
            dma((2, 3, 2)), dma((4, 2)), dma((4, 2)), dma((4, 2)), dma((4, 2)), dma((4, 2)),
            dma((4, 1)), dma((4, 1)), dma((4, 2)), dma((4, 2)),
            dma((4,)), dma((4,)), dma((4,)), dma((4,)), dma((2, 3)), dma((4,)), dma((4,)), dma((4,)),
            dma((2, 3)), dma((4,)), dma((4,)), dma((4,)), dma((2,)), dma((2,)), dma((11,)), dma((8,)),
            dma((2, 3)), dma((4,)), dma((4,)), dma((4,)), dma((4,)), dma((4,)), dma((4,)), dma((4,)),
        ],
        compiler_params=pltpu.CompilerParams(
            collective_id=0, has_side_effects=True, vmem_limit_bytes=56 * 1024 * 1024
        ),
        cost_estimate=pl.CostEstimate(flops=10**10, transcendentals=10**6, bytes_accessed=10**8),
        name="enter",
    )(tok, vec, qkv, out, time_qkv, time_out, feed_weight, first_weight, masked)


GROUP = 8
CHUNK = 16


def time_kernel(back, scale, heads, *refs):
    if back:
        (own_ref, rider_ref, joined_hbm, total_ref, wide_ref, turned_ref, mixed_hbm, wt_hbm, bias_ref) = refs[:9]
        (delta_ref, grad_ref, reduced_ref, rider_out) = refs[9:13]
        (half_in, half_own, line_out, line_in, half_send, half_recv, half_local, line_send, line_recv) = refs[-17:-8]
        (out_ref, turned, grad_qkv, grad_out, wt_ref, joined_ref, mixed_ref, load_sem) = refs[-8:]
        refs = refs[13:-17]
    else:
        (own_ref, rider_ref, far_ref, in_ref, wt_hbm, bias_ref) = refs[:6]
        (turned_ref, out_ref, mixed_ref, total_ref, delta_ref, rider_out, spread_out, in_out) = refs[6:14]
        (turned, wt_ref, load_sem) = refs[-3:]
        refs = refs[14:-3]
    (
        wq_ref, wo_ref, held, wide, narrow, kept, core_out, core_in, near_out, near_in,
        gy_send, gy_recv, gc_send, gc_recv, gd_send, gd_recv, sc_send, sc_recv, sy_send, sy_recv,
        r_send, r_recv, r_local, out_sem, wx_send, wx_recv,
    ) = refs
    y, x, c, z = (lax.axis_index(name) for name in AXES)
    near, pair, near_x = (1 - y, x, c, z), (y, x, 1 - c, z), (y, 1 - x, c, z)
    frames = held.shape[0] // 4
    chunks = held.shape[1] // CHUNK
    width = heads * HEAD_DIM
    groups = CHUNK // GROUP

    loads = [(wt_hbm, wt_ref), (own_ref, held.at[pl.ds(0, frames)])]
    if back:
        loads += [(joined_hbm, joined_ref), (mixed_hbm, mixed_ref)]
    loads = [pltpu.make_async_copy(src, dst, load_sem.at[i]) for i, (src, dst) in enumerate(loads)]
    for copy in loads:
        copy.start()
    barrier = pltpu.get_barrier_semaphore()
    for dc in range(2):
        for dz in range(4):
            if dc or dz:
                pl.semaphore_signal(barrier, inc=1, device_id=(y, x, (c + dc) % 2, (z + dz) % 4), device_id_type=MESH)
    pl.semaphore_signal(barrier, inc=1, device_id=near, device_id_type=MESH)
    pl.semaphore_signal(barrier, inc=1, device_id=near_x, device_id_type=MESH)
    pl.semaphore_wait(barrier, 9)

    def remote(src, dst, send, recv, peer):
        return pltpu.make_async_remote_copy(
            src_ref=src, dst_ref=dst, send_sem=send, recv_sem=recv, device_id=peer, device_id_type=MESH
        )

    def patches(k):
        return pl.ds(pl.multiple_of(k * CHUNK, CHUNK), CHUNK)

    def block(b, k):
        return held.at[pl.ds(b * frames, frames), patches(k)]

    def gather_y(k):
        return remote(own_ref.at[:, patches(k)], block(1, k), gy_send.at[k], gy_recv.at[k], near)

    def gather_c(k):
        return remote(own_ref.at[:, patches(k)], block(2, k), gc_send.at[k], gc_recv.at[k], pair)

    def gather_d(k):
        return remote(block(1, k), block(3, k), gd_send.at[k], gd_recv.at[k], pair)

    def scatter_c(k):
        return remote(core_out.at[k], core_in.at[k], sc_send.at[k], sc_recv.at[k], pair)

    def scatter_y(k):
        return remote(near_out.at[k], near_in.at[k], sy_send.at[k], sy_recv.at[k], near)

    def save(k):
        there = (turned_ref.at[k], turned.at[k]) if back else (turned.at[k], turned_ref.at[k])
        return pltpu.make_async_copy(*there, out_sem.at[k])

    def columns(s):
        return pl.ds(pl.multiple_of(s * BLK, BLK), BLK)

    def stays(k):
        if back:
            return jnp.logical_and(z == k, z // 2 == c)
        return jnp.logical_and(2 * c + k // 2 == z, c == k % 2)

    def ride(k):
        if back:
            src, dst = rider_ref.at[:, columns(k)], rider_out.at[2 * (z % 2) + c]
            peer, slot = (y, x, z // 2, k), 2 * (z % 2) + c
        else:
            src, dst = rider_ref.at[k], rider_out.at[:, columns(z)]
            peer, slot = (y, x, k % 2, 2 * c + k // 2), z
        return src, dst, peer, slot

    def ride_remote(k):
        src, dst, peer, slot = ride(k)
        return remote(src, dst, r_send.at[k], r_recv.at[slot], peer)

    def ride_local(k):
        src, dst, _, _ = ride(k)
        return pltpu.make_async_copy(src, dst, r_local.at[0])

    def ride_landed(k):
        if back:
            src, dst = rider_ref.at[:, columns(k)], rider_out.at[k]
        else:
            src, dst = rider_ref.at[k], rider_out.at[:, columns(k)]
        return remote(src, dst, r_send.at[k], r_recv.at[k], near)

    def from_self(k):
        if back:
            return jnp.logical_and(2 * c + k // 2 == z, c == k % 2)
        return jnp.logical_and(z == k, z // 2 == c)

    def spread_x(i, dx=0):
        r, yb = i // 2 + 1, i % 2
        size = far_ref.shape[1] // 4
        at = pl.multiple_of(size * (2 * yb + (x + dx) % 2), size)
        src = far_ref.at[(z + r) % 4, pl.ds(at, size)]
        return remote(src, spread_out.at[(z + r) % 4, pl.ds(at, size)], wx_send.at[i], wx_recv.at[i], near_x)

    gather_y(0).start()
    for k in range(chunks):
        if k > 0:
            gather_y(k).start()
        gather_c(k).start()
    def spread_in(dx=0):
        at = pl.multiple_of(BLK * (2 * (1 - y) + (x + dx) % 2), BLK)
        there = in_out.at[3 - z, pl.ds(at, BLK)]
        return remote(in_ref.at[3 - z, pl.ds(at, BLK)], there, wx_send.at[6], wx_recv.at[6], near_x)

    at_end = jnp.logical_or(z == 0, z == 3)

    def half_away(s):
        return remote(wide_ref.at[1 - x, s], half_in.at[s], half_send.at[s], half_recv.at[s], near_x)

    def half_here(s):
        return pltpu.make_async_copy(wide_ref.at[x, s], half_own.at[s], half_local.at[s])

    def line_away(r):
        return remote(line_out.at[r], line_in.at[r], line_send.at[r], line_recv.at[r], (y, x, c, (z + r) % 4))

    def halve():
        for s in range(4):
            half_away(s).wait_recv()
            half_here(s).wait()
        for r in range(4):
            s = (z + r) % 4
            whole = half_own[s].astype(F32) + half_in[s].astype(F32)
            if r == 0:
                reduced_ref[...] = whole
            else:
                line_out[r] = whole.astype(BF16)
                line_away(r).start()

    if back:
        for s in range(4):
            half_away(s).start()
            half_here(s).start()
    else:
        pl.when(at_end)(lambda: spread_in().start())
        for i in range(6):
            spread_x(i).start()
    for k in range(4):
        pl.when(stays(k))(lambda k=k: ride_local(k).start())
        pl.when(jnp.logical_not(stays(k)))(lambda k=k: ride_remote(k).start())
    if back:
        for k in range(chunks):
            save(k).start()

    def assemble(i, carry):
        rows = pl.ds(pl.multiple_of(i * BLK, BLK), BLK)
        for s in range(0, heads, 2):
            for part in range(4):
                both = [
                    wt_ref[rows, (s + j) * 4 * HEAD_DIM + part * HEAD_DIM : (s + j) * 4 * HEAD_DIM + (part + 1) * HEAD_DIM]
                    for j in range(2)
                ]
                both = jnp.concatenate(both, axis=1)
                if part < 3:
                    wq_ref[rows, part * width + s * HEAD_DIM : part * width + s * HEAD_DIM + PAIR] = both
                else:
                    wo_ref[rows, s * HEAD_DIM : s * HEAD_DIM + PAIR] = both
        return carry

    loads[0].wait()
    lax.fori_loop(0, wt_ref.shape[0] // BLK, assemble, 0)
    for copy in loads[1:]:
        copy.wait()

    def finish(k):
        scatter_c(k).wait_recv()
        both = kept[:, patches(k)] + core_in[k].astype(F32)
        near_out[k] = both[frames:].astype(BF16)
        delta_ref[:, patches(k)] = both[:frames]
        scatter_y(k).start()

    def pass_on(k):
        gather_y(k).wait_recv()
        gather_d(k).start()

    def one_group(i, rows):
        at = pl.ds(pl.multiple_of(i * GROUP, GROUP), GROUP)
        count = 4 * frames * GROUP
        bias = bias_ref[...]
        for lo in range(0, width, PAIR):
            q, k, v = (
                wide[:, at, part * width + lo : part * width + lo + PAIR].reshape(count, PAIR).astype(BF16)
                for part in range(3)
            )
            h = lo // HEAD_DIM
            if back:
                g = narrow[:, at, lo : lo + PAIR].reshape(count, PAIR).astype(BF16)
                totals = [total_ref[rows * groups + i, h + j : h + j + 1, :] for j in range(2)]
                grads = attend_pair_back(q, k, v, g, totals, bias, scale)
                for part in range(3):
                    wide[:, at, part * width + lo : part * width + lo + PAIR] = grads[part].reshape(
                        4 * frames, GROUP, PAIR
                    )
            else:
                mixed, totals = attend_pair(q, k, v, bias, scale)
                narrow[:, at, lo : lo + PAIR] = mixed.reshape(4 * frames, GROUP, PAIR)
                for j in range(2):
                    total_ref[rows * groups + i, h + j : h + j + 1, :] = totals[j]

    def one_chunk(k, carry):
        pl.when(k + 1 < chunks)(lambda: pass_on(k + 1))
        gather_c(k).wait_recv()
        gather_d(k).wait_recv()
        count = 4 * frames * CHUNK
        lhs = held[:, patches(k)].reshape(count, held.shape[2])
        if back:
            wide[...] = joined_ref[:, patches(k)].astype(F32)
            narrow[...] = dot_nn(lhs, wo_ref[...]).astype(BF16).astype(F32).reshape(narrow.shape)
        else:
            joined = dot_nn(lhs, wq_ref[...]).astype(BF16)
            out_ref[:, patches(k)] = joined.reshape(wide.shape)
            wide[...] = joined.astype(F32).reshape(wide.shape)
        lax.fori_loop(0, groups, lambda i, carry: (one_group(i, k), carry)[1], 0)
        if back:
            grads = wide[...].astype(BF16)
            out_ref[:, patches(k)] = grads
            partial = dot_nt(grads.reshape(count, 3 * width), wq_ref[...])
        else:
            mixed = narrow[...].astype(BF16)
            mixed_ref[:, patches(k)] = mixed
            partial = dot_nt(mixed.reshape(count, width), wo_ref[...])
        partial = partial.reshape(4 * frames, CHUNK, held.shape[2])
        kept[:, patches(k)] = partial[: 2 * frames]
        core_out[k] = partial[2 * frames :].astype(BF16)
        scatter_c(k).start()
        pl.when(k > 0)(lambda: finish(k - 1))
        if not back:
            for b in range(4):
                slab = held[b * frames : (b + 1) * frames, patches(k)].reshape(frames * CHUNK, held.shape[2])
                turned[k, :, b * frames * CHUNK : (b + 1) * frames * CHUNK] = slab.T
            save(k).start()
        if back:
            pl.when(k == chunks // 2 - 1)(halve)
        return carry

    pass_on(0)
    lax.fori_loop(0, chunks, one_chunk, 0)
    finish(chunks - 1)

    def weigh(k, carry):
        count = 4 * frames * CHUNK
        save(k).wait()
        grad_qkv[...] = grad_qkv[...] + dot_nn(turned[k], out_ref[:, patches(k)].reshape(count, 3 * width))
        grad_out[...] = grad_out[...] + dot_tn(
            mixed_ref[:, patches(k)].reshape(count, width), held[:, patches(k)].reshape(count, held.shape[2])
        )
        return carry

    def arrange(i, carry):
        rows = pl.ds(pl.multiple_of(i * BLK, BLK), BLK)
        last = grad_out[:, rows].T
        for s in range(heads):
            mine = slice(s * HEAD_DIM, (s + 1) * HEAD_DIM)
            parts = [grad_qkv[rows, j * width : (j + 1) * width][:, mine] for j in range(3)] + [last[:, mine]]
            grad_ref[rows, 2 * s * PAIR : (2 * s + 1) * PAIR] = jnp.concatenate(parts[:2], axis=1).astype(BF16)
            grad_ref[rows, (2 * s + 1) * PAIR : (2 * s + 2) * PAIR] = jnp.concatenate(parts[2:], axis=1).astype(BF16)
        return carry

    if back:
        grad_qkv[...] = jnp.zeros_like(grad_qkv)
        grad_out[...] = jnp.zeros_like(grad_out)
        lax.fori_loop(0, chunks, weigh, 0)
        lax.fori_loop(0, grad_ref.shape[0] // BLK, arrange, 0)
    for k in range(chunks):
        scatter_y(k).wait_recv()
        delta_ref[:, patches(k)] = delta_ref[:, patches(k)] + near_in[k].astype(F32)
    if back:
        for r in (1, 2, 3):
            line_away(r).wait_recv()
            reduced_ref[...] = reduced_ref[...] + line_in[r].astype(F32)
        for r in (1, 2, 3):
            line_away(r).wait_send()
        for s in range(4):
            half_away(s).wait_send()
    for k in range(chunks):
        for copy in (gather_y(k), gather_c(k), gather_d(k), scatter_c(k), scatter_y(k)):
            copy.wait_send()
        if not back:
            save(k).wait()
    if not back:
        for i in range(6):
            spread_x(i, 1).wait_recv()
            spread_x(i).wait_send()

        def spread_in_end():
            spread_in(1).wait_recv()
            spread_in().wait_send()

        pl.when(at_end)(spread_in_end)
    for k in range(4):
        pl.when(stays(k))(lambda k=k: ride_local(k).wait())
        pl.when(jnp.logical_not(stays(k)))(lambda k=k: ride_remote(k).wait_send())
        pl.when(jnp.logical_not(from_self(k)))(lambda k=k: ride_landed(k).wait_recv())


def time_call(back, own, rider, saved, weights, bias, scale):
    frames, patches, features = own.shape
    width = weights.shape[1] // 4
    heads = width // HEAD_DIM
    chunks = patches // CHUNK
    rows = 4 * frames * GROUP
    dma = pltpu.SemaphoreType.DMA
    anywhere = pl.BlockSpec(memory_space=pl.ANY)
    whole = pl.BlockSpec(memory_space=pltpu.VMEM)
    turned = (chunks, features, 4 * frames * CHUNK)
    if back:
        out_shape = []
    else:
        out_shape = [
            jax.ShapeDtypeStruct(turned, BF16),
            jax.ShapeDtypeStruct((4 * frames, patches, 3 * width), BF16),
            jax.ShapeDtypeStruct((4 * frames, patches, width), BF16),
            jax.ShapeDtypeStruct((patches // GROUP, heads, rows), F32),
        ]
    rider_shape = (4, frames * patches, BLK) if back else (frames * patches, features)
    out_shape += [
        jax.ShapeDtypeStruct((frames, patches, features), F32),
        jax.ShapeDtypeStruct(rider_shape, BF16),
    ]
    held = 2
    half = saved[2].shape[1:] if back else None
    if back:
        out_shape.insert(-1, jax.ShapeDtypeStruct((features, features), BF16))
        out_shape.insert(-1, jax.ShapeDtypeStruct(half[1:], F32))
    else:
        out_shape += [jax.ShapeDtypeStruct(w.shape, BF16) for w in saved]
        held = 4
    return pl.pallas_call(
        functools.partial(time_kernel, back, scale, heads),
        in_specs=[anywhere] * 2
        + ([anywhere, whole, anywhere, anywhere, anywhere] if back else [anywhere] * 2)
        + [anywhere, whole],
        out_specs=([] if back else [anywhere]) + [whole] * (len(out_shape) - held + back) + [anywhere] * (held - 1),
        out_shape=out_shape,
        scratch_shapes=[
            pltpu.VMEM((features, 3 * width), BF16),
            pltpu.VMEM((features, width), BF16),
            pltpu.VMEM((4 * frames, patches, features), BF16),
            pltpu.VMEM((4 * frames, CHUNK, 3 * width), F32),
            pltpu.VMEM((4 * frames, CHUNK, width), F32),
            pltpu.VMEM((2 * frames, patches, features), F32),
            pltpu.VMEM((chunks, 2 * frames, CHUNK, features), BF16),
            pltpu.VMEM((chunks, 2 * frames, CHUNK, features), BF16),
            pltpu.VMEM((chunks, frames, CHUNK, features), BF16),
            pltpu.VMEM((chunks, frames, CHUNK, features), BF16),
        ]
        + [dma((chunks,))] * 10
        + [dma((4,)), dma((4,)), dma((1,)), dma((chunks,))]
        + [dma((7,))] * 2
        + ([pltpu.VMEM(half, BF16)] * 4 + [dma((4,))] * 5 if back else [])
        + ([pltpu.VMEM((4 * frames, patches, 3 * width), BF16)] if back else [])
        + [pltpu.VMEM(turned, BF16)]
        + ([pltpu.VMEM((features, 3 * width), F32), pltpu.VMEM((width, features), F32)] if back else [])
        + [pltpu.VMEM(weights.shape, BF16)]
        + ([pltpu.VMEM(saved[0].shape, BF16), pltpu.VMEM(saved[4].shape, BF16)] if back else [])
        + [dma((4,))],
        compiler_params=pltpu.CompilerParams(
            collective_id=2 if back else 1, has_side_effects=True, vmem_limit_bytes=60 * 1024 * 1024
        ),
        cost_estimate=pl.CostEstimate(flops=10**10, transcendentals=10**6, bytes_accessed=10**8),
        name="time_back" if back else "time_forward",
    )(own, rider, *saved, weights, bias)


def feed_kernel(
    resid_hbm, delta_hbm, upstream_hbm, masked, gain, w_in_hbm, w_in_far_hbm, w_out_hbm, w_far_hbm,
    half_in_hbm, half_out_hbm, grad_hbm, low_hbm, rows_hbm, gain_out,
    resid, delta, upstream, grad_out, low_out, rows_out, move_sem,
    w_in, w_out, standard, inverse, normed, grads, normed_t, grads_t, hidden, pulled, g_in, g_out, back, ahead,
    back_out, back_in, ahead_out, ahead_in, from_x, from_y, slopes,
    w_sem, g_sem, n_send, n_recv, b_send, b_recv, hx_send, hx_recv, hy_send, hy_recv,
):
    y, x, c, z = (lax.axis_index(name) for name in AXES)
    pair, near_y, near_x = (y, x, 1 - c, z), (1 - y, x, c, z), (y, 1 - x, c, z)
    own = resid.shape[0]
    moves = [
        pltpu.make_async_copy(src, dst, move_sem.at[i])
        for i, (src, dst) in enumerate((
            (resid_hbm, resid), (delta_hbm, delta), (upstream_hbm, upstream),
            (grad_out, grad_hbm), (low_out, low_hbm), (rows_out, rows_hbm),
        ))
    ]
    for copy in moves[:3]:
        copy.start()
    step = own // 2
    slab = 128

    def fetch(s, far, last=False):
        size = w_out.shape[1] // 4
        copies = []
        for i in range(4):
            rows = pl.ds(pl.multiple_of(BLK * (2 * ((y + i // 2) % 2) + (x + i % 2) % 2), BLK), BLK)
            source = w_in_far_hbm if last and i == 3 else w_in_hbm
            copies.append(pltpu.make_async_copy(source.at[s, rows], w_in.at[s, rows], w_sem.at[5 + i, s]))
        for i in range(4):
            rows = pl.ds(pl.multiple_of(size * (2 * (i // 2) + (x + i % 2) % 2), size), size)
            source = w_far_hbm if far and i % 2 else w_out_hbm
            copies.append(pltpu.make_async_copy(source.at[s, rows], w_out.at[s, rows], w_sem.at[i, s]))
        return copies

    def fetch_now(s, far, last):
        for copy in fetch(s, far, last):
            copy.start()

    for s in range(4):
        pl.when(z == s)(lambda s=s: fetch_now(s, False, False))
        if s in (0, 3):
            pl.when(z == 3 - s)(lambda s=s: fetch_now(s, True, True))
            pl.when(jnp.logical_and(z != s, z != 3 - s))(lambda s=s: fetch_now(s, True, False))
        else:
            pl.when(z != s)(lambda s=s: fetch_now(s, True, False))
    barrier = pltpu.get_barrier_semaphore()
    for peer in (pair, near_y, near_x):
        pl.semaphore_signal(barrier, inc=1, device_id=peer, device_id_type=MESH)

    def remote(src, dst, send, recv, peer=pair):
        return pltpu.make_async_remote_copy(
            src_ref=src, dst_ref=dst, send_sem=send, recv_sem=recv, device_id=peer, device_id_type=MESH
        )

    def block(yb, xb):
        return pl.ds(pl.multiple_of(BLK * (2 * yb + xb), BLK), BLK)

    def away_x(s, i):
        return remote(g_out.at[s, block(i, 1 - x)], from_x.at[i, s], hx_send.at[i, s], hx_recv.at[i, s], near_x)

    def away_y(s, i):
        return remote(g_in.at[s, block(1 - y, i)], from_y.at[i, s], hy_send.at[i, s], hy_recv.at[i, s], near_y)

    def keep(s, i):
        return (
            pltpu.make_async_copy(g_out.at[s, block(i, x)], half_out_hbm.at[i, s], g_sem.at[0, i, s]),
            pltpu.make_async_copy(g_in.at[s, block(y, i)], half_in_hbm.at[i, s], g_sem.at[1, i, s]),
        )

    def combine(s):
        for i in range(2):
            away_x(s, i).wait_recv()
            g_out[s, block(i, x)] = (g_out[s, block(i, x)].astype(F32) + from_x[i, s].astype(F32)).astype(BF16)
            away_y(s, i).wait_recv()
            g_in[s, block(y, i)] = (g_in[s, block(y, i)].astype(F32) + from_y[i, s].astype(F32)).astype(BF16)
            for copy in keep(s, i):
                copy.start()

    def at(i, size):
        return pl.ds(pl.multiple_of(i * size, size), size)

    def prepare(i, carry):
        rows = at(i, step)
        grads[rows] = jnp.where(masked[rows] > 0.0, upstream[rows].astype(F32), 0.0).astype(BF16)
        std, inv = norm_rows(resid[rows] + delta[rows])
        standard[rows] = std
        inverse[rows] = inv
        normed[rows] = (std * gain[3:4]).astype(BF16)
        return carry

    for copy in moves[:3]:
        copy.wait()
    lax.fori_loop(0, 2, prepare, 0)
    pl.semaphore_wait(barrier, 3)
    mine, theirs = pl.ds(0, own), pl.ds(own, own)
    give_grads = remote(grads.at[mine], grads.at[theirs], n_send.at[0], n_recv.at[0])
    give_normed = remote(normed.at[mine], normed.at[theirs], n_send.at[1], n_recv.at[1])
    give_normed.start()
    give_grads.start()

    def turn(i, carry):
        rows = at(i, slab)
        normed_t[:, rows] = normed[rows].T
        grads_t[:, rows] = grads[rows].T
        return carry

    lax.fori_loop(0, own // slab, turn, 0)
    rate = math.sqrt(2.0 / math.pi)

    def bend_step(s, rows):
        inner = dot_nn(normed[rows], w_in[s])
        square = inner * inner
        bend = jnp.tanh(rate * inner * (1.0 + 0.044715 * square))
        hidden[rows] = (0.5 * inner * (1.0 + bend)).astype(BF16)
        slopes[rows] = 0.5 * (1.0 + bend) + 0.5 * inner * (1.0 - bend * bend) * (rate * (1.0 + 3.0 * 0.044715 * square))

    def pull_step(s, rows):
        pulled[rows] = (dot_nt(grads[rows], w_out[s]) * slopes[rows]).astype(BF16)

    def add_step(s, rows):
        ahead[rows] = ahead[rows] + dot_nn(hidden[rows], w_out[s])
        back[rows] = back[rows] + dot_nt(pulled[rows], w_in[s])

    def clear():
        back[...] = jnp.zeros_like(back)
        ahead[...] = jnp.zeros_like(ahead)

    def meet():
        give_normed.wait_recv()
        give_grads.wait_recv()
        lax.fori_loop(own // slab, 2 * own // slab, turn, 0)

    def one_piece(s, carry):
        for copy in fetch(s, False):
            copy.wait()

        def first_half(t, carry):
            pl.when(jnp.logical_and(s == 0, t == 1))(meet)
            bend_step(s, at(t, own))
            return carry

        lax.fori_loop(0, 2, first_half, 0)
        g_out[s] = dot_nn(grads_t[...], hidden[...]).astype(BF16)
        for i in range(2):
            away_x(s, i).start()
        lax.fori_loop(0, 2, lambda t, carry: (pull_step(s, at(t, own)), carry)[1], 0)
        g_in[s] = dot_nn(normed_t[...], pulled[...]).astype(BF16)
        for i in range(2):
            away_y(s, i).start()
        pl.when(s == 0)(clear)
        lax.fori_loop(0, 2, lambda t, carry: (add_step(s, at(t, own)), carry)[1], 0)
        return carry

    lax.fori_loop(0, 4, one_piece, 0)
    back_out[...] = back[theirs].astype(BF16)
    give_back = remote(back_out, back_in, b_send.at[0], b_recv.at[0])
    give_back.start()
    ahead_out[...] = ahead[theirs].astype(BF16)
    give_ahead = remote(ahead_out, ahead_in, b_send.at[1], b_recv.at[1])
    give_ahead.start()
    give_back.wait_recv()

    def finish(i, total):
        rows = at(i, step)
        grad = back[rows] + back_in[rows].astype(F32)
        std = standard[rows]
        inner = grad * gain[3:4]
        mean = jnp.mean(inner, axis=-1, keepdims=True)
        along = jnp.mean(inner * std, axis=-1, keepdims=True)
        full = grads[rows].astype(F32) + (inner - mean - std * along) * inverse[rows]
        grad_out[rows] = full
        low_out[rows] = full.astype(BF16)
        return total + jnp.sum(grad * std, axis=0, keepdims=True)

    gain_out[...] = lax.fori_loop(0, 2, finish, jnp.zeros((1, resid.shape[1]), F32))
    moves[3].start()
    moves[4].start()
    give_ahead.wait_recv()

    def emit(i, carry):
        rows = at(i, step)
        rows_out[rows] = (resid[rows] + delta[rows] + ahead[rows] + ahead_in[rows].astype(F32)).astype(BF16)
        return carry

    lax.fori_loop(0, 2, emit, 0)
    moves[5].start()
    lax.fori_loop(0, 4, lambda s, carry: (combine(s), carry)[1], 0)
    for copy in (give_normed, give_grads, give_back, give_ahead):
        copy.wait_send()
    for s in range(4):
        for i in range(2):
            away_x(s, i).wait_send()
            away_y(s, i).wait_send()
            for copy in keep(s, i):
                copy.wait()
    for copy in moves[3:]:
        copy.wait()


def feed(resid, delta, upstream, masked, gain, w_in, w_in_far, w_out, w_far):
    own, features = resid.shape
    units = w_in.shape[2]
    dma = pltpu.SemaphoreType.DMA
    anywhere = pl.BlockSpec(memory_space=pl.ANY)
    whole = pl.BlockSpec(memory_space=pltpu.VMEM)

    def low(*shape):
        return pltpu.VMEM(shape, BF16)

    def high(*shape):
        return pltpu.VMEM(shape, F32)

    return pl.pallas_call(
        feed_kernel,
        in_specs=[anywhere] * 3 + [whole] * 2 + [anywhere] * 4,
        out_specs=[anywhere] * 5 + [whole],
        out_shape=[
            jax.ShapeDtypeStruct((2, 4, BLK, units), BF16),
            jax.ShapeDtypeStruct((2, 4, BLK, units), BF16),
            jax.ShapeDtypeStruct((own, features), F32),
            jax.ShapeDtypeStruct((own, features), BF16),
            jax.ShapeDtypeStruct((own, features), BF16),
            jax.ShapeDtypeStruct((1, features), F32),
        ],
        scratch_shapes=[
            high(own, features), high(own, features), low(own, features),
            high(own, features), low(own, features), low(own, features), dma((6,)),
            low(4, features, units), low(4, units, features), high(own, features), high(own, 1),
            low(2 * own, features), low(2 * own, features), low(features, 2 * own), low(features, 2 * own),
            low(2 * own, units), low(2 * own, units), low(4, features, units), low(4, features, units),
            high(2 * own, features), high(2 * own, features),
            low(own, features), low(own, features), low(own, features), low(own, features),
            low(2, 4, BLK, units), low(2, 4, BLK, units), high(2 * own, units),
            dma((9, 4)), dma((2, 2, 4)), dma((2,)), dma((2,)), dma((2,)), dma((2,)),
            dma((2, 4)), dma((2, 4)), dma((2, 4)), dma((2, 4)),
        ],
        compiler_params=pltpu.CompilerParams(
            collective_id=4, has_side_effects=True, vmem_limit_bytes=60 * 1024 * 1024
        ),
        cost_estimate=pl.CostEstimate(flops=26 * 10**9, transcendentals=2 * 10**6, bytes_accessed=10**8),
        name="feed",
    )(resid, delta, upstream, masked, gain, w_in, w_in_far, w_out, w_far)


def leave_kernel(
    scale,
    part_hbm, next_hbm, grad_hbm, out_hbm, joined_hbm, mixed_hbm, lhs_hbm, weight_hbm, std_hbm, time_hbm, feed_hbm, feed_in_hbm,
    totals, inverse_next, inverse, masked, gains, later_grad,
    space_qkv, space_out, feed_in_out, feed_out_out, time_qkv, time_out, rows_out, gains_out, embed_out,
    rows_in,
    part, std, base, w_out, dj, mixed, lhs, weight, low_grads, turned, dmixed, go,
    t_own, t_in, tz_out, tz_in, t_total, ty_out, ty_in, tc_out, tc_in,
    f_own, f_in, fz_out, fz_in, f_total, f_other, fc_out, fc_in,
    grads, a1_out, a1_in, b1_out, b1_in, a2_out, a2_in, b2_out, b2_in, z_out, z_in,
    half_out, half_in, ready, core_out, core_in, sums, sum_out, sum_in, share_in,
    a1_send, a1_recv, b1_send, b1_recv, a2_send, a2_recv, b2_send, b2_recv, z_send, z_recv,
    h_send, h_recv, r_send, r_recv, c_send, c_recv, s_send, s_recv, p_send, p_recv, local,
    g_send, g_recv, tx_send, tx_recv, tz_send, tz_recv, ty_send, ty_recv, fy_send, fy_recv, fz_send, fz_recv, t_local, f_local, fetched,
):
    y, x, c, z = (lax.axis_index(name) for name in AXES)
    near_y, near_x, pair = (1 - y, x, c, z), (y, 1 - x, c, z), (y, x, 1 - c, z)
    own = std.shape[0]
    third = go.shape[1] // 4
    wide = 3 * third
    two = 2 * third
    slab = 128

    fetches = [
        pltpu.make_async_copy(src, dst, fetched.at[i])
        for i, (src, dst) in enumerate((
            (part_hbm, part), (next_hbm, std), (grad_hbm, base), (out_hbm, w_out), (joined_hbm, dj), (mixed_hbm, mixed),
            (lhs_hbm, lhs), (weight_hbm, weight), (feed_in_hbm, f_other),
        ))
    ]
    for copy in fetches:
        copy.start()
    fetch_std = pltpu.make_async_copy(std_hbm, std, fetched.at[9])

    barrier = pltpu.get_barrier_semaphore()
    for dc in range(2):
        for dz in range(4):
            if dc or dz:
                pl.semaphore_signal(barrier, inc=1, device_id=(y, x, (c + dc) % 2, (z + dz) % 4), device_id_type=MESH)
    for peer in (near_y, near_x):
        pl.semaphore_signal(barrier, inc=1, device_id=peer, device_id_type=MESH)
    pl.semaphore_wait(barrier, 9)

    def remote(src, dst, send, recv, peer):
        return pltpu.make_async_remote_copy(
            src_ref=src, dst_ref=dst, send_sem=send, recv_sem=recv, device_id=peer, device_id_type=MESH
        )

    def at(i, length):
        return pl.ds(pl.multiple_of(i * length, length), length)

    def along(r):
        return (y, x, c, (z + r) % 4)

    def time_x(yb):
        return remote(time_hbm.at[at(2 * yb + 1 - x, BLK)], t_in.at[yb], tx_send.at[yb], tx_recv.at[yb], near_x)

    def time_keep(yb):
        return pltpu.make_async_copy(time_hbm.at[at(2 * yb + x, BLK)], t_own.at[yb], t_local.at[yb])

    def time_z(r):
        return remote(tz_out.at[r], tz_in.at[r], tz_send.at[r], tz_recv.at[r], along(1))

    def feed_y(r):
        s = (z + r) % 4
        return remote(feed_hbm.at[1 - y, s], f_in.at[r], fy_send.at[r], fy_recv.at[r], near_y)

    def feed_keep(r):
        return pltpu.make_async_copy(feed_hbm.at[y, (z + r) % 4], f_own.at[r], f_local.at[r])

    def feed_z(r):
        return remote(fz_out.at[r], fz_in.at[r], fz_send.at[r], fz_recv.at[r], along(1))

    for r in (3, 2, 1, 0):
        feed_y(r).start()
        feed_keep(r).start()
    for yb in range(2):
        time_x(yb).start()
        time_keep(yb).start()

    def feed_step(t):
        r = 3 - t
        feed_y(r).wait_recv()
        feed_keep(r).wait()
        total = f_own[r].astype(F32) + f_in[r].astype(F32)
        if t > 0:
            feed_z(t - 1).wait_recv()
            total = total + fz_in[t - 1].astype(F32)
        if t == 3:
            f_total[...] = total
        else:
            fz_out[t] = total.astype(BF16)
            feed_z(t).start()

    def time_step(t):
        if t == 0:
            for yb in range(2):
                time_x(yb).wait_recv()
                time_keep(yb).wait()
        else:
            time_z(t - 1).wait_recv()
        piece_at = at((z + 3 - t) % 4, BLK)
        for yb in range(2):
            total = t_own[yb, :, piece_at].astype(F32) + t_in[yb, :, piece_at].astype(F32)
            if t > 0:
                total = total + tz_in[t - 1, yb].astype(F32)
            if t == 3:
                t_total[yb] = total
            else:
                tz_out[t, yb] = total.astype(BF16)
        if t < 3:
            time_z(t).start()

    step = own // 2
    for copy in fetches[:3]:
        copy.wait()

    def norm_back(grad, standard, weights, inv):
        inner = grad * weights
        mean = jnp.mean(inner, axis=-1, keepdims=True)
        slope = jnp.mean(inner * standard, axis=-1, keepdims=True)
        return (inner - mean - standard * slope) * inv

    def after_time(i, total):
        rows = at(i, step)
        grad, standard = part[rows], std[rows]
        full = base[rows] + norm_back(grad, standard, gains[2:3], inverse_next[rows])
        base[rows] = full
        low_grads[rows] = full.astype(BF16)
        return total + jnp.sum(grad * standard, axis=0, keepdims=True)

    zero = jnp.zeros((1, std.shape[1]), F32)
    next_grad = lax.fori_loop(0, 2, after_time, zero)
    give = remote(low_grads.at[pl.ds(0, own)], low_grads.at[pl.ds(own, own)], g_send.at[0], g_recv.at[0], pair)
    give.start()
    fetch_std.start()
    for copy in fetches[3:6]:
        copy.wait()

    def attend(i, carry):
        rows = at(i, slab)
        for h in range(mixed.shape[1] // PAIR):
            places = [pl.ds((3 * h + j) * PAIR, PAIR) for j in range(3)]
            q, k, v = (dj[rows, place] for place in places)
            lines = [totals[i, 2 * h + j : 2 * h + j + 1, :] for j in range(2)]
            found = attend_pair_back(q, k, v, dmixed[rows, h * PAIR : (h + 1) * PAIR], lines, None, scale)
            for place, value in zip(places, found):
                dj[rows, place] = value.astype(BF16)
        return carry

    def turn(i, carry):
        turned[:, at(i, slab)] = low_grads[at(i, slab)].T
        return carry

    def attend_half(t, *between):
        rows = pl.ds(t * own, own)
        first, count = t * own // slab, own // slab
        dmixed[rows] = dot_nt(low_grads[rows], w_out[...]).astype(BF16)
        between[0]()
        lax.fori_loop(first, first + count // 2, attend, 0)
        between[1]()
        lax.fori_loop(first + count // 2, first + count, attend, 0)
        between[2]()
        lax.fori_loop(first, first + count, turn, 0)

    def nothing():
        pass

    attend_half(0, lambda: feed_step(0), nothing, lambda: feed_step(1))
    give.wait_recv()
    attend_half(1, nothing, lambda: feed_step(2), lambda: time_step(0))
    for copy in fetches[6:]:
        copy.wait()
    def away(i, carry):
        rows = pl.ds(pl.multiple_of(own + i * step, step), step)
        half_out[pl.ds(pl.multiple_of(i * step, step), step)] = dot_nt(dj[rows], weight[...]).astype(BF16)
        return carry

    lax.fori_loop(0, 2, away, 0)
    swap = remote(half_out, half_in, h_send.at[0], h_recv.at[0], pair)
    swap.start()

    def block(yb, xb):
        return pl.ds(pl.multiple_of(BLK * (2 * yb + xb), BLK), BLK)

    def a1(i):
        return remote(a1_out.at[i], a1_in.at[i], a1_send.at[i], a1_recv.at[i], near_x)

    def b1(i):
        return remote(b1_out.at[i], b1_in.at[i], b1_send.at[i], b1_recv.at[i], near_y)

    def a2(i):
        return remote(a2_out.at[i], a2_in.at[i], a2_send.at[i], a2_recv.at[i], near_y)

    def b2(i):
        return remote(b2_out.at[i], b2_in.at[i], b2_send.at[i], b2_recv.at[i], near_x)

    def to_z(r):
        return remote(z_out.at[r], z_in.at[r], z_send.at[r], z_recv.at[r], along(r))

    def send_first(i):
        a1(i).start()
        b1(i).start()

    def piece(i, carry):
        s = (z + i + 1) % 4
        made = dot_nn(lhs[...], dj[:, pl.ds(pl.multiple_of(s * wide, third), wide)])
        grads[i, :, :wide] = made
        grads[i, :, wide:] = go[:, pl.ds(pl.multiple_of(s * third, third), third)].astype(F32)
        for b in range(2):
            a1_out[i, b] = grads[i, block(b, 1 - x), :two].astype(BF16)
            b1_out[i, b] = grads[i, block(1 - y, b), two:].astype(BF16)
        pl.when(i < 2)(lambda: send_first(i))
        return carry


    def second(i):
        a1(i).wait_recv()
        a2_out[i] = (grads[i, block(1 - y, x), :two] + a1_in[i, 1 - y].astype(F32)).astype(BF16)
        a2(i).start()
        b1(i).wait_recv()
        b2_out[i] = (grads[i, block(y, 1 - x), two:] + b1_in[i, 1 - x].astype(F32)).astype(BF16)
        b2(i).start()
        grads[i, block(y, x), :two] = grads[i, block(y, x), :two] + a1_in[i, y].astype(F32)
        grads[i, block(y, x), two:] = grads[i, block(y, x), two:] + b1_in[i, x].astype(F32)

    def third_step(i):
        a2(i).wait_recv()
        b2(i).wait_recv()
        grads[i, block(y, x), :two] = grads[i, block(y, x), :two] + a2_in[i].astype(F32)
        grads[i, block(y, x), two:] = grads[i, block(y, x), two:] + b2_in[i].astype(F32)
        if i < 3:
            z_out[i + 1] = grads[i, block(y, x), :].astype(BF16)
            to_z(i + 1).start()

    fetch_std.wait()
    sums[...] = jnp.zeros_like(sums)
    sums[1:2] = next_grad
    sums[2:3] = later_grad[...]
    swap.wait_recv()

    def home(i, totals):
        rows = pl.ds(pl.multiple_of(i * step, step), step)
        grad = dot_nt(dj[rows], weight[...]) + half_in[rows].astype(F32)
        standard = std[rows]
        full = base[rows] + norm_back(grad, standard, gains[1:2], inverse[rows])
        hide = masked[rows] > 0.0
        ready[rows] = jnp.where(hide, 0.0, full).astype(BF16)
        return (
            totals[0] + jnp.sum(grad * standard, axis=0, keepdims=True),
            totals[1] + jnp.sum(jnp.where(hide, full, 0.0), axis=0, keepdims=True),
        )

    gain_grad, embed_grad = lax.fori_loop(0, 2, home, (zero, zero))
    sums[0:1] = gain_grad
    sums[3:4] = embed_grad

    def columns(s):
        return pl.ds(pl.multiple_of(s * BLK, BLK), BLK)

    def stays(k):
        return jnp.logical_and(z == k, z // 2 == c)

    def ride(k):
        slot = 2 * (z % 2) + c
        return remote(ready.at[:, columns(k)], rows_in.at[slot], r_send.at[k], r_recv.at[slot], (y, x, z // 2, k))

    def ride_local(k):
        return pltpu.make_async_copy(ready.at[:, columns(k)], rows_in.at[2 * (z % 2) + c], local.at[3])

    for k in range(4):
        pl.when(stays(k))(lambda k=k: ride_local(k).start())
        pl.when(jnp.logical_not(stays(k)))(lambda k=k: ride(k).start())
    time_step(1)
    go[...] = dot_nn(turned[...], mixed[...]).astype(BF16)
    lax.fori_loop(0, 4, piece, 0)

    def share(h):
        peer = (pair, near_y, near_x)[h]
        return remote(sum_out.at[h], sum_in.at[h], s_send.at[h], s_recv.at[h], peer)

    def begin_share(h):
        sum_out[h] = sums[...]
        share(h).start()

    def end_share(h):
        share(h).wait_recv()
        sums[...] = sums[...] + sum_in[h]

    begin_share(0)
    second(0)
    send_first(2)
    time_step(2)
    second(1)
    send_first(3)
    third_step(0)
    end_share(0)
    begin_share(1)
    second(2)
    third_step(1)
    end_share(1)
    begin_share(2)
    second(3)
    third_step(2)
    end_share(2)
    sum_out[3] = sums[...]

    def deal(r):
        s = (z + r) % 4
        return remote(sum_out.at[3, :, columns(s)], share_in.at[r], p_send.at[r], p_recv.at[r], (y, x, c, s))

    for r in (1, 2, 3):
        deal(r).start()
    third_step(3)
    parity = BLK // 2

    time_step(3)
    ty_out[...] = t_total[1 - y].astype(BF16)
    swap_y = remote(ty_out, ty_in, ty_send.at[0], ty_recv.at[0], near_y)
    swap_y.start()
    feed_step(3)
    fc_out[0] = f_other[at(1 - c, parity)].astype(BF16)
    fc_out[1] = f_total[at(1 - c, parity)].astype(BF16)
    swap_feed = remote(fc_out, fc_in, c_send.at[1], c_recv.at[1], pair)
    swap_feed.start()
    units = f_total.shape[1]
    feed_in_out[:, at(c, units)] = f_other[at(c, parity)]
    feed_out_out[at(c, units)] = f_total[at(c, parity)].T
    swap_y.wait_recv()
    tc_out[0] = t_total[y, at(1 - c, parity)].astype(BF16)
    tc_out[1] = ty_in[at(1 - c, parity)]
    swap_time = remote(tc_out, tc_in, c_send.at[2], c_recv.at[2], pair)
    swap_time.start()
    for k in range(4):
        pl.when(stays(k))(lambda k=k: ride_local(k).wait())
        from_self = jnp.logical_and(2 * c + k // 2 == z, c == k % 2)

        def landed(k=k):
            remote(ready.at[:, columns(k)], rows_in.at[k], r_send.at[k], r_recv.at[k], near_y).wait_recv()

        pl.when(jnp.logical_not(from_self))(landed)
    rows_out[...] = rows_in[...].astype(F32)
    for r in (1, 2, 3):
        to_z(r).wait_recv()
    total = grads[3, block(y, x), :]
    for r in (1, 2, 3):
        total = total + z_in[r].astype(F32)
    grads[3, block(y, x), :] = total
    rows = BLK // 2

    def core_rows(core):
        return pl.ds(pl.multiple_of(BLK * (2 * y + x) + rows * core, rows), rows)

    core_out[...] = grads[3, core_rows(1 - c), :].astype(BF16)
    last = remote(core_out, core_in, c_send.at[0], c_recv.at[0], pair)
    last.start()
    def place(core, value):
        for j in range(3):
            space_qkv[j, :, at(core, third)] = value[:, j * third : (j + 1) * third]
        space_out[at(core, third)] = value[:, 3 * third :].T

    place(c, grads[3, core_rows(c), :])
    result = sums[:, columns(z)]
    for r in (1, 2, 3):
        deal(r).wait_recv()
        result = result + share_in[r]
    gains_out[...] = result[:3]
    embed_out[...] = result[3:4]
    swap_feed.wait_recv()
    feed_in_out[:, at(1 - c, units)] = fc_in[0].astype(F32)
    feed_out_out[at(1 - c, units)] = fc_in[1].astype(F32).T
    swap_time.wait_recv()
    mine = (t_total[y, at(c, parity)], ty_in[at(c, parity)].astype(F32))
    other = (tc_in[0].astype(F32), tc_in[1].astype(F32))
    by_head = []
    for yb in range(2):
        for cb in range(2):
            by_head.append(
                jnp.where(
                    c == cb,
                    jnp.where(y == yb, mine[0], mine[1]),
                    jnp.where(y == yb, other[0], other[1]),
                )
            )
    for j in range(4):
        made = jnp.concatenate([v[:, j * HEAD_DIM : (j + 1) * HEAD_DIM] for v in by_head], axis=1)
        if j < 3:
            time_qkv[j] = made
        else:
            time_out[...] = made.T
    last.wait_recv()
    place(1 - c, core_in[...].astype(F32))

    for copy in (last, swap, give, swap_y, swap_feed, swap_time):
        copy.wait_send()
    for yb in range(2):
        time_x(yb).wait_send()
    for r in range(4):
        feed_y(r).wait_send()
    for t in range(3):
        time_z(t).wait_send()
        feed_z(t).wait_send()
    for i in range(4):
        for copy in (a1(i), b1(i), a2(i), b2(i)):
            copy.wait_send()
    for r in (1, 2, 3):
        to_z(r).wait_send()
        deal(r).wait_send()
    for h in range(3):
        share(h).wait_send()
    for k in range(4):
        pl.when(jnp.logical_not(stays(k)))(lambda k=k: ride(k).wait_send())


def leave(
    part, std_next, grad, w_out, joined, mixed, lhs, weight, std, g_time, g_out, g_in,
    totals, inverse_next, inverse, masked, gains, later_grad, scale,
):
    own, features = std.shape
    cols4 = mixed.shape[1]
    quarter = cols4 // 4
    units = g_in.shape[1]
    dma = pltpu.SemaphoreType.DMA
    anywhere = pl.BlockSpec(memory_space=pl.ANY)
    whole = pl.BlockSpec(memory_space=pltpu.VMEM)
    parity = BLK // 2

    def low(*shape):
        return pltpu.VMEM(shape, BF16)

    def high(*shape):
        return pltpu.VMEM(shape, F32)

    return pl.pallas_call(
        functools.partial(leave_kernel, scale),
        in_specs=[anywhere] * 12 + [whole] * 6,
        out_specs=[whole] * 9,
        out_shape=[
            jax.ShapeDtypeStruct(shape, F32)
            for shape in (
                (3, parity, 2 * quarter), (2 * quarter, parity), (parity, 2 * units), (2 * units, parity),
                (3, parity, BLK), (BLK, parity), (4, own, BLK), (3, BLK), (1, BLK),
            )
        ],
        scratch_shapes=[
            low(4, own, BLK),
            high(own, features), high(own, features), high(own, features), low(*w_out.shape), low(*joined.shape),
            low(*mixed.shape), low(*lhs.shape), low(*weight.shape), low(2 * own, features), low(features, 2 * own),
            low(*mixed.shape), low(features, cols4),
            low(2, BLK, features), low(2, BLK, features), low(4, 2, BLK, BLK), low(4, 2, BLK, BLK), high(2, BLK, BLK),
            low(BLK, BLK), low(BLK, BLK), low(2, parity, BLK), low(2, parity, BLK),
            low(4, BLK, units), low(4, BLK, units), low(4, BLK, units), low(4, BLK, units),
            high(BLK, units), high(BLK, units), low(2, parity, units), low(2, parity, units),
            high(4, features, cols4),
            low(4, 2, BLK, 2 * quarter), low(4, 2, BLK, 2 * quarter), low(4, 2, BLK, 2 * quarter), low(4, 2, BLK, 2 * quarter),
            low(4, BLK, 2 * quarter), low(4, BLK, 2 * quarter), low(4, BLK, 2 * quarter), low(4, BLK, 2 * quarter),
            low(4, BLK, cols4), low(4, BLK, cols4),
            low(own, features), low(own, features), low(own, features),
            low(parity, cols4), low(parity, cols4),
            high(8, features), high(4, 8, features), high(3, 8, features), high(4, 8, BLK),
        ]
        + [dma((4,))] * 10
        + [dma((1,)), dma((1,)), dma((4,)), dma((4,)), dma((3,)), dma((3,)), dma((3,)), dma((3,)), dma((4,)), dma((4,)), dma((4,))]
        + [dma((1,)), dma((1,)), dma((2,)), dma((2,)), dma((4,)), dma((4,)), dma((1,)), dma((1,))]
        + [dma((4,)), dma((4,)), dma((4,)), dma((4,)), dma((2,)), dma((4,)), dma((10,))],
        compiler_params=pltpu.CompilerParams(
            collective_id=3, has_side_effects=True, vmem_limit_bytes=62 * 1024 * 1024
        ),
        cost_estimate=pl.CostEstimate(flops=2 * 10**10, transcendentals=10**6, bytes_accessed=10**8),
        name="leave",
    )(
        part, std_next, grad, w_out, joined, mixed, lhs, weight, std, g_time, g_out, g_in,
        totals, inverse_next, inverse, masked, gains, later_grad,
    )


def tie(*values):
    return lax.optimization_barrier(values)


def norm_rows(resid):
    mean = jnp.mean(resid, axis=-1, keepdims=True)
    centered = resid - mean
    inverse = lax.rsqrt(jnp.mean(centered * centered, axis=-1, keepdims=True) + eps_norm)
    return (centered * inverse, inverse)


def norm_rows_back(grad, standardized, inverse, gain):
    gain_grad = jnp.sum(grad * standardized, axis=0)
    inner = grad * gain
    mean = jnp.mean(inner, axis=-1, keepdims=True)
    along = jnp.mean(inner * standardized, axis=-1, keepdims=True)
    return ((inner - mean - standardized * along) * inverse, gain_grad)


def cols(parts):
    return jnp.concatenate(parts, axis=1)


def rows_of(parts):
    return jnp.concatenate(parts, axis=0)


def token_parallel(
    tokens,
    cotangent,
    ratio,
    priority,
    frame_order,
    mask_embed,
    gains,
    qkv_space,
    out_space,
    qkv_time,
    out_time,
    w_in,
    w_out,
):
    scale = 1.0 / math.sqrt(HEAD_DIM)
    y, x, c, z = (lax.axis_index(name) for name in AXES)
    patches = tokens.shape[2]
    width = qkv_space.shape[0]
    frames_own = tokens.shape[0] * tokens.shape[1] // 4
    frames_all = frame_order.shape[1]
    own = frames_own * patches
    hidden_own = w_in.shape[1] // 2
    plane = 2 * y + x
    k_own = 2 * (z % 2) + c

    masked_here = (priority < ratio[:, None, None]).astype(jnp.int32).reshape(2, -1)
    info = cols([masked_here, frame_order])
    info = jnp.where(z // 2 == c, info, hop_c(info))
    info = lax.dynamic_index_in_dim(info, z % 2, 0, keepdims=False)
    masked = lax.dynamic_slice_in_dim(info, c * own, own, 0)[:, None] != 0
    order = info[2 * own :].reshape(2, 2, frames_own)
    order = jnp.where(y == 1, order[::-1], order)
    order = jnp.where(c == 1, order[:, ::-1], order).swapaxes(0, 1).reshape(frames_all)
    order = jnp.repeat(order, GROUP)
    patch = jnp.arange(frames_all * GROUP) % GROUP
    visible = (order[:, None] <= order[None, :]) & (patch[:, None] == patch[None, :])
    bias = jnp.where(visible, 0.0, -1e30).astype(F32)

    vectors = rows_of([mask_embed[None], gains, jnp.zeros((4, BLK), BF16)])
    (
        ws_qkv, ws_out, wt_all, wf_out, wf_in, joined0, turned0, std0,
        mixed0, total0, inv0, resid1, std1, inv1, normed1, vectors,
    ) = enter(
        tokens.reshape(4, own, BLK),
        vectors,
        jnp.swapaxes(qkv_space, 0, 1),
        out_space,
        jnp.swapaxes(qkv_time, 0, 1),
        out_time,
        w_out,
        w_in,
        masked.astype(F32),
        scale,
    )

    half = qkv_space.shape[2] // 2
    turned1, joined1, mixed1, total1, delta, upstream, wf_far, wf_in_far = time_call(
        False,
        normed1.reshape(frames_own, patches, width),
        cotangent.reshape(4, own, BLK),
        [wf_out, wf_in],
        wt_all,
        bias,
        scale,
    )
    w_in_half, w_out_half, grad2, grad2_low, block_rows, gain_grad2 = feed(
        resid1, delta.reshape(own, width), upstream, masked.astype(F32), vectors, wf_in, wf_in_far, wf_out, wf_far
    )

    part1, g_time, g_w_in, block_out = time_call(
        True,
        grad2_low.reshape(frames_own, patches, width),
        block_rows,
        [joined1, total1, w_in_half, turned1, mixed1],
        wt_all,
        bias,
        scale,
    )
    block_out = block_out.reshape(tokens.shape)
    grad_qkv_space, grad_out_space, grad_w_in, grad_w_out, grad_qkv_time, grad_out_time, grad_tokens, grad_gains, grad_embed = leave(
        part1.reshape(own, width), std1, grad2, ws_out, joined0, mixed0, turned0, ws_qkv, std0, g_time, w_out_half, g_w_in,
        total0, inv1, inv0, masked.astype(F32), vectors, gain_grad2, scale,
    )
    return (
        block_out,
        grad_tokens.reshape(tokens.shape),
        grad_embed.reshape(BLK),
        grad_gains,
        jnp.swapaxes(grad_qkv_space, 0, 1),
        grad_out_space,
        jnp.swapaxes(grad_qkv_time, 0, 1),
        grad_out_time,
        grad_w_in,
        grad_w_out,
    )


def solution(mesh):
    sizes = (mesh.shape["tm"], mesh.shape["clip"], mesh.shape["mp"])
    if sizes == (2, 4, 4):
        mesh = jax.sharding.Mesh(mesh.devices.reshape(2, 2, 2, 4), AXES)
        step, clip = token_parallel, ("x", "c")
    else:
        step, clip = shards, ("clip",)
    return jax.shard_map(
        step,
        mesh=mesh,
        in_specs=(
            P(clip, "tm", None, "mp"),
            P(clip, "tm", None, "mp"),
            P(clip),
            P(clip, "tm", None),
            P(clip, None),
            P("mp"),
            P(None, "mp"),
            P(None, None, "mp"),
            P("mp", None),
            P(None, None, "mp"),
            P("mp", None),
            P(None, "mp"),
            P("mp", None),
        ),
        out_specs=(
            P(clip, "tm", None, "mp"),
            P(clip, "tm", None, "mp"),
            P("mp"),
            P(None, "mp"),
            P(("tm",) + clip, None, "mp"),
            P("mp", ("tm",) + clip),
            P(("tm",) + clip, None, "mp"),
            P("mp", ("tm",) + clip),
            P(("tm",) + clip, "mp"),
            P("mp", ("tm",) + clip),
        ),
        check_vma=False,
    )
```

```python
import functools
import math

import jax
import jax.numpy as jnp
from jax import lax
from jax.experimental import pallas as pl
from jax.experimental.pallas import tpu as pltpu
from jax.sharding import PartitionSpec as P

HEAD_DIM = 64
MICRO = 2


eps_norm = 1e-05


def gelu_tanh(values):
    return jax.nn.gelu(values, approximate=True)


def norm_forward_pass(residual_stream, gain_coefficients, complete_width):
    reduced_totals = lax.psum(
        (jnp.sum(residual_stream, axis=-1), jnp.sum(residual_stream * residual_stream, axis=-1)),
        "mp",
    )
    centered_rows = reduced_totals[0] / complete_width
    spread = reduced_totals[1] / complete_width - centered_rows * centered_rows
    inverse_scale = lax.rsqrt(spread + eps_norm)
    standardized_rows = (residual_stream - centered_rows[:, None]) * inverse_scale[:, None]
    shard_rows = (standardized_rows * gain_coefficients).astype(jnp.bfloat16)
    normalized_rows = lax.all_gather(shard_rows, "mp", axis=1, tiled=True)
    return (normalized_rows, standardized_rows, inverse_scale)


def norm_reverse_pass(
    normalized_gradient, standardized_rows, inverse_scale, gain_coefficients, complete_width
):
    gain_gradient = jnp.sum(normalized_gradient * standardized_rows, axis=0)
    standardized_gradient = normalized_gradient * gain_coefficients
    reduced_totals = lax.psum(
        (
            jnp.sum(standardized_gradient, axis=-1),
            jnp.sum(standardized_gradient * standardized_rows, axis=-1),
        ),
        "mp",
    )
    grad_resid = (
        standardized_gradient
        - reduced_totals[0][:, None] / complete_width
        - standardized_rows * (reduced_totals[1][:, None] / complete_width)
    ) * inverse_scale[:, None]
    return (grad_resid, gain_gradient)


def sum_features(grad_full):
    return lax.psum_scatter(
        grad_full.astype(jnp.bfloat16), "mp", scatter_dimension=1, tiled=True
    ).astype(jnp.float32)


def branch_out(hidden, weight):
    partial_rows = jnp.dot(hidden, weight, preferred_element_type=jnp.float32)
    return lax.psum_scatter(partial_rows, "mp", scatter_dimension=1, tiled=True)


def branch_back(grad_resid, hidden, weight):
    grad_rows = lax.all_gather(grad_resid.astype(jnp.bfloat16), "mp", axis=1, tiled=True)
    weight_grad = jnp.einsum("rk,rd->kd", hidden, grad_rows, preferred_element_type=jnp.float32)
    grad_hidden = jnp.einsum("rd,kd->rk", grad_rows, weight, preferred_element_type=jnp.float32)
    return (grad_hidden, weight_grad)


def qkv_back(normalized_rows, grad_joined, weight):
    weight_grad = jnp.einsum(
        "rd,trk->dtk", normalized_rows, grad_joined, preferred_element_type=jnp.float32
    )
    grad_full = jnp.einsum("trk,dtk->rd", grad_joined, weight, preferred_element_type=jnp.float32)
    return (weight_grad, sum_features(grad_full))


def reduce_grads(local_grads, small_grads):
    reduced = (
        lax.psum_scatter(local_grads[0], ("tm", "clip"), scatter_dimension=0, tiled=True),
        lax.psum_scatter(local_grads[1], ("tm", "clip"), scatter_dimension=1, tiled=True),
        lax.psum_scatter(local_grads[2], ("tm", "clip"), scatter_dimension=0, tiled=True),
        lax.psum_scatter(local_grads[3], ("tm", "clip"), scatter_dimension=1, tiled=True),
        lax.psum_scatter(local_grads[4], ("tm", "clip"), scatter_dimension=0, tiled=True),
        lax.psum_scatter(local_grads[5], ("tm", "clip"), scatter_dimension=1, tiled=True),
    )
    reduced_small = lax.psum((small_grads[0], small_grads[1]), ("tm", "clip"))
    return (reduced, reduced_small)


def space_forward(normalized_rows, weight, frame_count, patches, heads_local, scale):
    joined = jnp.einsum(
        "rd,dtk->trk", normalized_rows, weight, preferred_element_type=jnp.float32
    ).astype(jnp.bfloat16)
    shape_heads = (frame_count, patches, heads_local, HEAD_DIM)
    scores = (
        jnp.einsum(
            "bshd,bthd->bhst",
            joined[0].reshape(shape_heads),
            joined[1].reshape(shape_heads),
            preferred_element_type=jnp.float32,
        )
        * scale
    )
    highest = jnp.max(scores, axis=-1, keepdims=True)
    exponent = jnp.exp(scores - highest)
    reduced_totals = jnp.sum(exponent, axis=-1, keepdims=True)
    log_total = highest + jnp.log(reduced_totals)
    attention = (exponent / reduced_totals).astype(jnp.bfloat16)
    mixed = jnp.einsum(
        "bhst,bthd->bshd",
        attention,
        joined[2].reshape(shape_heads),
        preferred_element_type=jnp.float32,
    )
    return (
        joined,
        log_total,
        mixed.astype(jnp.bfloat16).reshape(frame_count * patches, heads_local * HEAD_DIM),
    )


def space_backward(grad_mixed, joined, log_total, frame_count, patches, heads_local, scale):
    shape_heads = (frame_count, patches, heads_local, HEAD_DIM)
    queries = joined[0].reshape(shape_heads)
    key_rows = joined[1].reshape(shape_heads)
    values = joined[2].reshape(shape_heads)
    grad_out = grad_mixed.reshape(shape_heads)
    scores = (
        jnp.einsum("bshd,bthd->bhst", queries, key_rows, preferred_element_type=jnp.float32) * scale
    )
    attention = jnp.exp(scores - log_total)
    grad_values = jnp.einsum(
        "bhst,bshd->bthd",
        attention.astype(jnp.bfloat16),
        grad_out,
        preferred_element_type=jnp.float32,
    )
    grad_att = jnp.einsum("bshd,bthd->bhst", grad_out, values, preferred_element_type=jnp.float32)
    grad_scores = (
        attention * (grad_att - jnp.sum(attention * grad_att, axis=-1, keepdims=True))
    ).astype(jnp.bfloat16)
    grad_queries = (
        jnp.einsum("bhst,bthd->bshd", grad_scores, key_rows, preferred_element_type=jnp.float32)
        * scale
    )
    grad_keys = (
        jnp.einsum("bhst,bshd->bthd", grad_scores, queries, preferred_element_type=jnp.float32)
        * scale
    )
    row_count = frame_count * patches
    stacked = jnp.stack(
        [
            grad_queries.reshape(row_count, -1),
            grad_keys.reshape(row_count, -1),
            grad_values.reshape(row_count, -1),
        ]
    )
    return stacked.astype(jnp.bfloat16)


def time_scores(queries, keys_all, visible, scale):
    scores = (
        jnp.einsum("cfshd,cgshd->chfgs", queries, keys_all, preferred_element_type=jnp.float32)
        * scale
    )
    return jnp.where(visible, scores, -1e30)


def time_forward(queries, keys_all, values_all, visible, scale):
    scores = time_scores(queries, keys_all, visible, scale)
    highest = jnp.max(scores, axis=3, keepdims=True)
    exponent = jnp.exp(scores - highest)
    reduced_totals = jnp.sum(exponent, axis=3, keepdims=True)
    log_total = highest + jnp.log(reduced_totals)
    attention = (exponent / reduced_totals).astype(jnp.bfloat16)
    mixed = jnp.einsum(
        "chfgs,cgshd->cfshd", attention, values_all, preferred_element_type=jnp.float32
    )
    return (log_total, mixed.astype(jnp.bfloat16))


def time_backward(grad_mixed, queries, keys_all, values_all, visible, log_total, scale):
    grad_out = grad_mixed.reshape(queries.shape)
    scores = time_scores(queries, keys_all, visible, scale)
    attention = jnp.exp(scores - log_total)
    grad_values = jnp.einsum(
        "chfgs,cfshd->cgshd",
        attention.astype(jnp.bfloat16),
        grad_out,
        preferred_element_type=jnp.float32,
    )
    grad_att = jnp.einsum(
        "cfshd,cgshd->chfgs", grad_out, values_all, preferred_element_type=jnp.float32
    )
    grad_scores = (
        attention * (grad_att - jnp.sum(attention * grad_att, axis=3, keepdims=True))
    ).astype(jnp.bfloat16)
    grad_queries = (
        jnp.einsum("chfgs,cgshd->cfshd", grad_scores, keys_all, preferred_element_type=jnp.float32)
        * scale
    )
    grad_keys = (
        jnp.einsum("chfgs,cfshd->cgshd", grad_scores, queries, preferred_element_type=jnp.float32)
        * scale
    )
    return (grad_queries, grad_keys, grad_values)


def shards(
    tokens,
    cotangent,
    ratio,
    priority,
    frame_order,
    mask_embed,
    gains,
    qkv_space,
    out_space,
    qkv_time,
    out_time,
    w_in,
    w_out,
):
    scale = 1.0 / math.sqrt(HEAD_DIM)
    clips_local = tokens.shape[0] // MICRO
    frames_local = tokens.shape[1]
    patches = tokens.shape[2]
    cols_local = tokens.shape[3]
    frames_all = frame_order.shape[1]
    hidden_width = qkv_space.shape[0]
    joined_local = qkv_space.shape[2]
    heads_local = joined_local // HEAD_DIM
    row_count = clips_local * frames_local * patches
    gain_broadcast = gains.astype(jnp.float32)
    embed_row = mask_embed.astype(jnp.float32)
    first_frame = lax.axis_index("tm") * frames_local
    shape_local = (clips_local, frames_local, patches, joined_local)
    shape_heads = (clips_local, frames_local, patches, heads_local, HEAD_DIM)
    shape_all = (clips_local, frames_all, patches, heads_local, HEAD_DIM)
    outputs = []
    input_grads = []
    weight_total = None
    small_total = None
    for batch_index in range(MICRO):
        lower = batch_index * clips_local
        upper = lower + clips_local
        source = tokens[lower:upper].reshape(row_count, cols_local).astype(jnp.float32)
        upstream = cotangent[lower:upper].reshape(row_count, cols_local).astype(jnp.float32)
        masked = (priority[lower:upper] < ratio[lower:upper][:, None, None]).reshape(row_count)
        order_rows = frame_order[lower:upper]
        residual_stream0 = jnp.where(masked[:, None], embed_row[None, :], source)
        normalized_rows0, standardized_rows0, inverse_deviation0 = norm_forward_pass(
            residual_stream0, gain_broadcast[0], hidden_width
        )
        joined0, total0, mixed0 = space_forward(
            normalized_rows0, qkv_space, clips_local * frames_local, patches, heads_local, scale
        )
        residual_stream1 = residual_stream0 + branch_out(mixed0, out_space)
        normalized_rows1, standardized_rows1, inverse_deviation1 = norm_forward_pass(
            residual_stream1, gain_broadcast[1], hidden_width
        )
        joined1 = jnp.einsum(
            "rd,dtk->trk", normalized_rows1, qkv_time, preferred_element_type=jnp.float32
        ).astype(jnp.bfloat16)
        queries_local = joined1[0].reshape(shape_local)
        keys_local = joined1[1].reshape(shape_local)
        values_local = joined1[2].reshape(shape_local)
        keys_all, values_all = (
            lax.all_gather(keys_local, "tm", axis=1, tiled=True),
            lax.all_gather(values_local, "tm", axis=1, tiled=True),
        )
        query_order = lax.dynamic_slice_in_dim(order_rows, first_frame, frames_local, axis=1)
        time_visible = (order_rows[:, None, :] <= query_order[:, :, None])[:, None, :, :, None]
        time_q = queries_local.reshape(shape_heads)
        time_k = keys_all.reshape(shape_all)
        time_v = values_all.reshape(shape_all)
        total1, mixed_frames = time_forward(time_q, time_k, time_v, time_visible, scale)
        mixed1 = mixed_frames.reshape(row_count, joined_local)
        residual_stream2 = residual_stream1 + branch_out(mixed1, out_time)
        normalized_rows2, standardized_rows2, inverse_deviation2 = norm_forward_pass(
            residual_stream2, gain_broadcast[2], hidden_width
        )
        projected = jnp.dot(normalized_rows2, w_in, preferred_element_type=jnp.float32)
        activated, gelu_pull = jax.vjp(gelu_tanh, projected)
        hidden = activated.astype(jnp.bfloat16)
        resid3 = residual_stream2 + branch_out(hidden, w_out)
        outputs.append(
            resid3.astype(jnp.bfloat16).reshape(clips_local, frames_local, patches, cols_local)
        )
        grad3 = jnp.where(masked[:, None], upstream, 0.0)
        grad_hidden, grad_w_out = branch_back(grad3, hidden, w_out)
        grad_inner = gelu_pull(grad_hidden)[0].astype(jnp.bfloat16)
        grad_w_in = jnp.einsum(
            "rd,rk->dk", normalized_rows2, grad_inner, preferred_element_type=jnp.float32
        )
        normalized_gradient2 = sum_features(
            jnp.einsum("rk,dk->rd", grad_inner, w_in, preferred_element_type=jnp.float32)
        )
        backward_third, gain_gradient2 = norm_reverse_pass(
            normalized_gradient2,
            standardized_rows2,
            inverse_deviation2,
            gain_broadcast[2],
            hidden_width,
        )
        grad2 = grad3 + backward_third
        grad_mixed1, grad_out_time = branch_back(grad2, mixed1, out_time)
        grad_mixed_low = grad_mixed1.astype(jnp.bfloat16).reshape(shape_local)
        grad_queries, grad_keys, grad_values = time_backward(
            grad_mixed_low, time_q, time_k, time_v, time_visible, total1, scale
        )
        key_part, value_part = (
            lax.psum_scatter(
                grad_keys.reshape(clips_local, frames_all, patches, joined_local).astype(
                    jnp.bfloat16
                ),
                "tm",
                scatter_dimension=1,
                tiled=True,
            ).astype(jnp.float32),
            lax.psum_scatter(
                grad_values.reshape(clips_local, frames_all, patches, joined_local).astype(
                    jnp.bfloat16
                ),
                "tm",
                scatter_dimension=1,
                tiled=True,
            ).astype(jnp.float32),
        )
        grad_joined1 = jnp.stack(
            [
                grad_queries.reshape(row_count, joined_local),
                key_part.reshape(row_count, joined_local),
                value_part.reshape(row_count, joined_local),
            ]
        ).astype(jnp.bfloat16)
        grad_qkv_time, normalized_gradient1 = qkv_back(normalized_rows1, grad_joined1, qkv_time)
        backward_second, gain_gradient1 = norm_reverse_pass(
            normalized_gradient1,
            standardized_rows1,
            inverse_deviation1,
            gain_broadcast[1],
            hidden_width,
        )
        grad1 = grad2 + backward_second
        grad_mixed0, grad_out_space = branch_back(grad1, mixed0, out_space)
        grad_joined0 = space_backward(
            grad_mixed0.astype(jnp.bfloat16),
            joined0,
            total0,
            clips_local * frames_local,
            patches,
            heads_local,
            scale,
        )
        grad_qkv_space, normalized_gradient0 = qkv_back(normalized_rows0, grad_joined0, qkv_space)
        backward_first, gain_gradient0 = norm_reverse_pass(
            normalized_gradient0,
            standardized_rows0,
            inverse_deviation0,
            gain_broadcast[0],
            hidden_width,
        )
        grad0 = grad1 + backward_first
        input_grads.append(
            jnp.where(masked[:, None], 0.0, grad0).reshape(
                clips_local, frames_local, patches, cols_local
            )
        )
        grad_embed = jnp.sum(jnp.where(masked[:, None], grad0, 0.0), axis=0)
        gain_grads = jnp.stack([gain_gradient0, gain_gradient1, gain_gradient2])
        local_grads = (
            grad_qkv_space,
            grad_out_space,
            grad_qkv_time,
            grad_out_time,
            grad_w_in,
            grad_w_out,
        )
        small_grads = (gain_grads, grad_embed)
        reduced, reduced_small = reduce_grads(local_grads, small_grads)
        if weight_total is None:
            weight_total = reduced
            small_total = reduced_small
        else:
            weight_total = tuple((total + grad for total, grad in zip(weight_total, reduced)))
            small_total = tuple((total + grad for total, grad in zip(small_total, reduced_small)))
    return (
        jnp.concatenate(outputs, axis=0),
        jnp.concatenate(input_grads, axis=0),
        small_total[1],
        small_total[0],
        weight_total[0],
        weight_total[1],
        weight_total[2],
        weight_total[3],
        weight_total[4],
        weight_total[5],
    )


AXES = ("tm", "x", "c", "mp")
F32 = jnp.float32
BF16 = jnp.bfloat16
BLK = 256
MESH = pl.DeviceIdType.MESH


def device_pairs(move):
    pairs = []
    for y in range(2):
        for x in range(2):
            for c in range(2):
                for z in range(4):
                    there = move(y, x, c, z)
                    pairs.append(tuple(((q[0] * 2 + q[1]) * 2 + q[2]) * 4 + q[3] for q in ((y, x, c, z), there)))
    return pairs


def hop_y(v):
    return lax.ppermute(v, AXES, device_pairs(lambda y, x, c, z: (1 - y, x, c, z)))


def hop_x(v):
    return lax.ppermute(v, AXES, device_pairs(lambda y, x, c, z: (y, 1 - x, c, z)))


def hop_c(v):
    return lax.ppermute(v, AXES, device_pairs(lambda y, x, c, z: (y, x, 1 - c, z)))


def hop_z(v, shift):
    return lax.ppermute(v, AXES, device_pairs(lambda y, x, c, z: (y, x, c, (z + shift) % 4)))


def spread_pairs(r):
    def move(y, x, c, z):
        k = z ^ r
        return (y, x, k & 1, 2 * c + (k >> 1))

    return device_pairs(move)


def dot_nn(a, b):
    return lax.dot_general(a, b, (((1,), (0,)), ((), ())), preferred_element_type=F32)


def dot_nt(a, b):
    return lax.dot_general(a, b, (((1,), (1,)), ((), ())), preferred_element_type=F32)


def dot_tn(a, b):
    return lax.dot_general(a, b, (((0,), (0,)), ((), ())), preferred_element_type=F32)


def attend_pair(q, k, v, bias, scale):
    mixed, totals = [], []
    for i in range(2):
        mine = slice(i * HEAD_DIM, (i + 1) * HEAD_DIM)
        scores = dot_nt(k[:, mine], q[:, mine]) * scale
        if bias is not None:
            scores = scores + bias
        highest = jnp.max(scores, axis=0, keepdims=True)
        exponent = jnp.exp(scores - highest)
        total = jnp.sum(exponent, axis=0, keepdims=True)
        totals.append(highest + jnp.log(total))
        mixed.append(dot_tn(v[:, mine], exponent.astype(BF16)) * (1.0 / total))
    return (jnp.concatenate(mixed, axis=0).T, totals)


def attend_pair_back(q, k, v, g, totals, bias, scale):
    grads = ([], [], [])
    for i in range(2):
        mine = slice(i * HEAD_DIM, (i + 1) * HEAD_DIM)
        scores = dot_nt(k[:, mine], q[:, mine]) * scale
        if bias is not None:
            scores = scores + bias
        p = jnp.exp(scores - totals[i])
        dp = dot_nt(v[:, mine], g[:, mine])
        ds = (p * (dp - jnp.sum(p * dp, axis=0, keepdims=True))).astype(BF16)
        grads[0].append(dot_tn(k[:, mine], ds) * scale)
        grads[1].append(dot_nn(ds, q[:, mine]) * scale)
        grads[2].append(dot_nn(p.astype(BF16), g[:, mine]))
    return (
        jnp.concatenate(grads[0], axis=0).T,
        jnp.concatenate(grads[1], axis=1),
        jnp.concatenate(grads[2], axis=1),
    )


PAIR = 2 * HEAD_DIM


def enter_kernel(
    scale,
    tok, vec, qkv_hbm, out_hbm, time_hbm, time_out_hbm, feed_hbm, first_hbm, masked,
    wq_out, wo_out, wt, wf, wi, joined_out, turned_out, std_out,
    mixed, total_out, inverse, resid_out, next_out, inverse_next, low_out, vec_out,
    rows_in, vec_in, wq, wo, normed, joined, turned, std, base, part, part_out, part_in, resid, std_next, low_next,
    later, head_in, head_out,
    z_send, z_recv, y_send, y_recv, x_send, x_recv, p_send, p_recv, q_send, q_recv,
    t_send, t_recv, v_send, v_recv, u_send, u_recv, w_send, w_recv,
    f_send, f_recv, g_send, g_recv, n_send, n_recv, local, saved,
    i_send, i_recv, j_send, j_recv, k_send, k_recv, l_send, l_recv,
):
    y, x, c, z = (lax.axis_index(name) for name in AXES)
    half = wo.shape[0] // 4
    wide = 3 * half
    span = wt.shape[1] // 4
    size = wf.shape[1] // 4
    own = rows_in.shape[0]
    near_y, near_x, pair = (1 - y, x, c, z), (y, 1 - x, c, z), (y, x, 1 - c, z)
    right_z, left_z = (y, x, c, (z + 1) % 4), (y, x, c, (z + 3) % 4)

    def at(i, length):
        return pl.ds(pl.multiple_of(i * length, length), length)

    def remote(src, dst, send, recv, peer):
        return pltpu.make_async_remote_copy(
            src_ref=src, dst_ref=dst, send_sem=send, recv_sem=recv, device_id=peer, device_id_type=MESH
        )

    def start(all_copies):
        for copy in all_copies:
            copy.start()

    def landed(all_copies):
        for copy in all_copies:
            copy.wait_recv()

    def sent(all_copies):
        for copy in all_copies:
            copy.wait_send()

    core = at(c, half)
    keep = [
        pltpu.make_async_copy(
            qkv_hbm.at[j, :, core], wq.at[:, pl.ds(pl.multiple_of(z * wide + j * half, half), half)], local.at[j]
        )
        for j in range(3)
    ] + [pltpu.make_async_copy(out_hbm.at[core], wo.at[at(z, half)], local.at[3])]
    keep_later = [
        pltpu.make_async_copy(later, wt.at[:, at(z, span)], local.at[4]),
        pltpu.make_async_copy(feed_hbm.at[at(c, 4 * size)], wf.at[z], local.at[5]),
        pltpu.make_async_copy(first_hbm.at[:, at(c, 4 * size)], wi.at[z], local.at[8]),
    ]
    head = [
        pltpu.make_async_copy(time_hbm.at[:, :, at(y, PAIR)], head_in, local.at[9]),
        pltpu.make_async_copy(time_out_hbm.at[at(2 * y + c, HEAD_DIM)], head_out, local.at[10]),
    ]
    start(keep + keep_later[1:] + head)

    barrier = pltpu.get_barrier_semaphore()
    for dc in range(2):
        for dz in range(4):
            if dc or dz:
                peer = (y, x, (c + dc) % 2, (z + dz) % 4)
                pl.semaphore_signal(barrier, inc=1, device_id=peer, device_id_type=MESH)
    for peer in (near_y, near_x):
        pl.semaphore_signal(barrier, inc=1, device_id=peer, device_id_type=MESH)
    pl.semaphore_wait(barrier, 9)

    def spot(dy, dx):
        return 2 * ((y + dy) % 2) + (x + dx) % 2

    def piece(dy, dx, r, split=False):
        s = (z + r) % 4
        rows = at(spot(dy, dx), BLK)
        first = pl.multiple_of(s * wide, half)
        out = wo.at[at(s, half), at(spot(dy, dx), BLK)]
        if split:
            last = pl.multiple_of(s * wide + 2 * half, half)
            return (wq.at[rows, pl.ds(first, 2 * half)], wq.at[rows, pl.ds(last, half)], out)
        return (wq.at[rows, pl.ds(first, wide)], out)

    def time_piece(dx, r):
        return wt.at[at((x + dx) % 2, 2 * BLK), at((z + r) % 4, span)]

    def feed_piece(dy, r):
        return wf.at[(z + r) % 4, at(spot(dy, 0), size)]

    def copies(parts, send, recv, peer):
        return [remote(ref, ref, send.at[i], recv.at[i], peer) for i, ref in enumerate(parts)]

    def leg(right, step):
        if right:
            return (0 if step == 0 else 4 - step), right_z, 3 - step
        return step, left_z, step + 1

    def z_copies(right, step):
        r, peer, lands = leg(right, step)
        return copies(piece(0, 0, r), z_send.at[int(right), step], z_recv.at[lands], peer)

    def time_z(right, step):
        r, peer, lands = leg(right, step)
        source = later.at[at(x, 2 * BLK)] if step == 0 else time_piece(0, r)
        return [remote(source, time_piece(0, r), u_send.at[int(right), step], u_recv.at[lands], peer)]

    def feed_z(right, step):
        r, peer, lands = leg(right, step)
        source = feed_hbm.at[at(4 * c + spot(0, 0), size)] if step == 0 else feed_piece(0, r)
        return [remote(source, feed_piece(0, r), f_send.at[int(right), step], f_recv.at[lands], peer)]

    def first_piece(dy, dx, r):
        return wi.at[(z + r) % 4, at(spot(dy, dx), BLK)]

    def first_z(right, step):
        r, peer, lands = leg(right, step)
        source = first_hbm.at[at(spot(0, 0), BLK), at(c, 4 * size)] if step == 0 else first_piece(0, 0, r)
        return [remote(source, first_piece(0, 0, r), i_send.at[int(right), step], i_recv.at[lands], peer)]

    def first_y(r, dy=0):
        return [remote(first_piece(dy, 0, r), first_piece(dy, 0, r), j_send.at[r], j_recv.at[r], near_y)]

    def first_x(r, dx=0):
        return [remote(first_piece(0, dx, r), first_piece(0, dx, r), k_send.at[r], k_recv.at[r], near_x)]

    def y_copies(r, dy=0):
        return copies(piece(dy, 0, r), y_send.at[r], y_recv.at[r], near_y)

    def x_copies(r, dx=0):
        return copies(piece(0, dx, r), x_send.at[r], x_recv.at[r], near_x)

    def corner_x(r, dx=0):
        return copies(piece(1, dx, r, split=True)[:1], p_send.at[r], p_recv.at[r], near_x)

    def corner_y(r, dy=0):
        return copies(piece(dy, 1, r, split=True)[1:], q_send.at[r], q_recv.at[r], near_y)

    def time_x(r, dx=0):
        return [remote(time_piece(dx, r), time_piece(dx, r), w_send.at[r], w_recv.at[r], near_x)]

    def feed_y(r, dy=0):
        return [remote(feed_piece(dy, r), feed_piece(dy, r), g_send.at[r], g_recv.at[r], near_y)]

    def token_copies(k):
        peer = (y, x, k % 2, 2 * c + k // 2)
        return [
            remote(tok.at[k], rows_in.at[:, at(z, BLK)], t_send.at[k], t_recv.at[z], peer),
            remote(vec, vec_in.at[:, at(z, BLK)], v_send.at[k], v_recv.at[z], peer),
        ]

    def token_local(k):
        return [
            pltpu.make_async_copy(tok.at[k], rows_in.at[:, at(z, BLK)], local.at[6]),
            pltpu.make_async_copy(vec, vec_in.at[:, at(z, BLK)], local.at[7]),
        ]

    def stays(k):
        return jnp.logical_and(2 * c + k // 2 == z, c == k % 2)

    def start_tokens(ks):
        for k in ks:
            pl.when(stays(k))(lambda k=k: start(token_local(k)))
            pl.when(jnp.logical_not(stays(k)))(lambda k=k: start(token_copies(k)))

    def each_side(j, act):
        pl.when(z >= j + 1)(lambda: act(3 - j, True))
        pl.when(z <= 2 - j)(lambda: act(j + 1, False))

    def begin(make):
        pl.when(z < 3)(lambda: start(make(True, 0)))
        pl.when(z > 0)(lambda: start(make(False, 0)))

    def onward(j, make, right):
        if j < 2:
            pl.when(z < 3 if right else z > 0)(lambda: start(make(right, j + 1)))

    def forward(j):
        def act(r, right):
            landed(copies(piece(0, 0, r), z_send.at[0, 0], z_recv.at[r], near_y))
            onward(j, z_copies, right)
            start(y_copies(r))
            start(x_copies(r))

        each_side(j, act)

    def corners(j):
        def act(r, right):
            landed(y_copies(r, 1))
            start(corner_x(r))
            landed(x_copies(r, 1))
            start(corner_y(r))

        each_side(j, act)

    def time_forward_step(j):
        def act(r, right):
            landed([remote(time_piece(0, r), time_piece(0, r), u_send.at[0, 0], u_recv.at[r], near_x)])
            onward(j, time_z, right)
            start(time_x(r))

        each_side(j, act)

    def feed_forward_step(j):
        def act(r, right):
            landed([remote(feed_piece(0, r), feed_piece(0, r), f_send.at[0, 0], f_recv.at[r], near_y)])
            onward(j, feed_z, right)
            start(feed_y(r))

        each_side(j, act)

    def first_corner_copy(r, dx=0):
        return [remote(first_piece(1, dx, r), first_piece(1, dx, r), l_send.at[r], l_recv.at[r], near_x)]

    def first_corner(j):
        def act(r, right):
            landed(first_y(r, 1))
            start(first_corner_copy(r))

        each_side(j, act)

    def first_forward_step(j):
        def act(r, right):
            landed([remote(first_piece(0, 0, r), first_piece(0, 0, r), i_send.at[0, 0], i_recv.at[r], near_y)])
            onward(j, first_z, right)
            start(first_y(r))
            start(first_x(r))

        each_side(j, act)

    for copy in keep:
        copy.wait()
    begin(z_copies)

    def gather_head(i, carry):
        rows = at(i, BLK)
        parts = [head_in[j, rows].astype(F32) for j in range(3)]
        parts = [jnp.where(c == 0, v[:, :HEAD_DIM], v[:, HEAD_DIM:]) for v in parts]
        parts.append(head_out[:, rows].astype(F32).T)
        later[rows] = jnp.concatenate(parts, axis=1).astype(BF16)
        return carry

    for copy in head:
        copy.wait()
    lax.fori_loop(0, later.shape[0] // BLK, gather_head, 0)
    keep_later[0].start()
    forward(0)
    start_tokens((0, 1))
    forward(1)
    start_tokens((2, 3))
    begin(first_z)
    begin(time_z)
    begin(feed_z)
    corners(0)
    forward(2)
    corners(1)
    for k in range(4):
        def finish_local(k=k):
            for copy in token_local(k):
                copy.wait()

        pl.when(stays(k))(finish_local)
    for s in range(4):
        def arrived(s=s):
            landed([
                remote(tok.at[0], rows_in.at[:, at(s, BLK)], t_send.at[0], t_recv.at[s], near_y),
                remote(vec, vec_in.at[:, at(s, BLK)], v_send.at[0], v_recv.at[s], near_y),
            ])

        pl.when(jnp.logical_not(jnp.logical_and(z == s, z // 2 == c)))(arrived)

    step = own // 2
    slab = 128
    vec_out[...] = vec_in[...].astype(F32)

    def first_norm(i, carry):
        rows = at(i, step)
        value = jnp.where(masked[rows] > 0.0, vec_out[0:1], rows_in[rows].astype(F32))
        base[rows] = value
        standard, inv = norm_rows(value)
        std[rows] = standard
        inverse[rows] = inv
        normed[rows] = (standard * vec_out[1:2]).astype(BF16)
        return carry

    lax.fori_loop(0, 2, first_norm, 0)
    give_normed = remote(normed.at[pl.ds(0, own)], normed.at[pl.ds(own, own)], n_send.at[0], n_recv.at[0], pair)
    give_normed.start()
    corners(2)

    def turn(i, carry):
        turned[:, at(i, slab)] = normed[at(i, slab)].T
        return carry

    lax.fori_loop(0, own // slab, turn, 0)
    for r in (1, 2, 3):
        landed(corner_x(r, 1))
        landed(corner_y(r, 1))
    saves = [
        pltpu.make_async_copy(wq, wq_out, saved.at[0]),
        pltpu.make_async_copy(wo, wo_out, saved.at[1]),
        pltpu.make_async_copy(std, std_out, saved.at[2]),
    ]
    start(saves)
    first_forward_step(0)

    def attend(i, carry):
        rows = at(i, slab)
        for h in range(wo.shape[0] // PAIR):
            q, k, v = (joined[rows, (3 * h + j) * PAIR : (3 * h + j + 1) * PAIR] for j in range(3))
            out, totals = attend_pair(q, k, v, None, scale)
            mixed[rows, h * PAIR : (h + 1) * PAIR] = out.astype(BF16)
            for j in range(2):
                total_out[i, 2 * h + j : 2 * h + j + 1, :] = totals[j]
        return carry

    def project(t):
        rows = pl.ds(t * own, own)
        joined[rows] = dot_nn(normed[rows], wq[...]).astype(BF16)

    frames = own // slab
    project(0)
    time_forward_step(0)
    lax.fori_loop(0, frames, attend, 0)
    part[...] = dot_nn(mixed[pl.ds(0, own)], wo[...])
    feed_forward_step(0)
    first_forward_step(1)
    first_corner(0)
    give_normed.wait_recv()
    project(1)
    saves.append(pltpu.make_async_copy(joined, joined_out, saved.at[3]))
    saves[3].start()
    lax.fori_loop(frames, 2 * frames, attend, 0)
    part_out[...] = dot_nn(mixed[pl.ds(own, own)], wo[...]).astype(BF16)
    give_part = remote(part_out, part_in, n_send.at[1], n_recv.at[1], pair)
    give_part.start()
    time_forward_step(1)
    feed_forward_step(1)
    first_corner(1)
    lax.fori_loop(own // slab, 2 * own // slab, turn, 0)
    saves.append(pltpu.make_async_copy(turned, turned_out, saved.at[4]))
    saves[4].start()
    give_part.wait_recv()
    first_forward_step(2)

    def second_norm(i, carry):
        rows = at(i, step)
        value = base[rows] + part[rows] + part_in[rows].astype(F32)
        resid[rows] = value
        standard, inv = norm_rows(value)
        std_next[rows] = standard
        inverse_next[rows] = inv
        low_next[rows] = (standard * vec_out[2:3]).astype(BF16)
        return carry

    lax.fori_loop(0, 2, second_norm, 0)
    for i, (src, dst) in enumerate(((resid, resid_out), (std_next, next_out), (low_next, low_out))):
        saves.append(pltpu.make_async_copy(src, dst, saved.at[5 + i]))
        saves[-1].start()
    time_forward_step(2)
    feed_forward_step(2)

    def first_ends(j):
        def act(r, right):
            if j == 2:
                landed(first_y(r, 1))
            else:
                landed(first_corner_copy(r, 1))
                sent(first_corner_copy(r))

        each_side(j, act)

    for j in range(3):
        first_ends(j)
    for copy in keep_later + saves:
        copy.wait()
    give_normed.wait_send()
    give_part.wait_send()
    for r in (1, 2, 3):
        landed(time_x(r, 1))
        landed(feed_y(r, 1))
        landed(first_x(r, 1))
        for group in (y_copies(r), x_copies(r), corner_x(r), corner_y(r), time_x(r), feed_y(r), first_y(r), first_x(r)):
            sent(group)
    for step_z in range(3):
        for make in (z_copies, time_z, first_z, feed_z):
            pl.when(jnp.logical_and(z >= step_z, z < 3))(lambda step_z=step_z, make=make: sent(make(True, step_z)))
            pl.when(jnp.logical_and(z + step_z <= 3, z > 0))(lambda step_z=step_z, make=make: sent(make(False, step_z)))
    for k in range(4):
        pl.when(jnp.logical_not(stays(k)))(lambda k=k: sent(token_copies(k)))


def enter(tok, vec, qkv, out, time_qkv, time_out, feed_weight, first_weight, masked, scale):
    own, width, half = tok.shape[1], 4 * tok.shape[2], out.shape[0] // 2
    size = feed_weight.shape[0] // 2
    dma = pltpu.SemaphoreType.DMA
    anywhere = pl.BlockSpec(memory_space=pl.ANY)
    whole = pl.BlockSpec(memory_space=pltpu.VMEM)
    heads = 4 * half // HEAD_DIM

    def low(*shape):
        return pltpu.VMEM(shape, BF16)

    def high(*shape):
        return pltpu.VMEM(shape, F32)

    shapes = [
        ((width, 12 * half), BF16), ((4 * half, width), BF16), ((width, 16 * HEAD_DIM), BF16),
        ((4, size, width), BF16), ((4, width, size), BF16), ((2 * own, 12 * half), BF16), ((width, 2 * own), BF16), ((own, width), F32),
        ((2 * own, 4 * half), BF16), ((2 * own // 128, heads, 128), F32), ((own, 1), F32), ((own, width), F32),
        ((own, width), F32), ((own, 1), F32), ((own, width), BF16), ((vec.shape[0], width), F32),
    ]
    return pl.pallas_call(
        functools.partial(enter_kernel, scale),
        in_specs=[anywhere] * 8 + [whole],
        out_specs=[anywhere] * 8 + [whole] * 3 + [anywhere] * 2 + [whole, anywhere, whole],
        out_shape=[jax.ShapeDtypeStruct(shape, kind) for shape, kind in shapes],
        scratch_shapes=[
            low(own, width), low(vec.shape[0], width), low(width, 12 * half), low(4 * half, width),
            low(2 * own, width), low(2 * own, 12 * half), low(width, 2 * own), high(own, width), high(own, width),
            high(own, width), low(own, width), low(own, width), high(own, width), high(own, width), low(own, width),
            low(width, 4 * HEAD_DIM), low(3, width, PAIR), low(HEAD_DIM, width),
            dma((2, 3, 2)), dma((4, 2)), dma((4, 2)), dma((4, 2)), dma((4, 2)), dma((4, 2)),
            dma((4, 1)), dma((4, 1)), dma((4, 2)), dma((4, 2)),
            dma((4,)), dma((4,)), dma((4,)), dma((4,)), dma((2, 3)), dma((4,)), dma((4,)), dma((4,)),
            dma((2, 3)), dma((4,)), dma((4,)), dma((4,)), dma((2,)), dma((2,)), dma((11,)), dma((8,)),
            dma((2, 3)), dma((4,)), dma((4,)), dma((4,)), dma((4,)), dma((4,)), dma((4,)), dma((4,)),
        ],
        compiler_params=pltpu.CompilerParams(
            collective_id=0, has_side_effects=True, vmem_limit_bytes=56 * 1024 * 1024
        ),
        cost_estimate=pl.CostEstimate(flops=10**10, transcendentals=10**6, bytes_accessed=10**8),
        name="enter",
    )(tok, vec, qkv, out, time_qkv, time_out, feed_weight, first_weight, masked)


GROUP = 8
CHUNK = 16


def time_kernel(back, scale, heads, *refs):
    if back:
        (own_ref, rider_ref, joined_hbm, total_ref, wide_ref, turned_ref, mixed_hbm, wt_hbm, bias_ref) = refs[:9]
        (delta_ref, grad_ref, reduced_ref, rider_out) = refs[9:13]
        (half_in, half_own, line_out, line_in, half_send, half_recv, half_local, line_send, line_recv) = refs[-17:-8]
        (out_ref, turned, grad_qkv, grad_out, wt_ref, joined_ref, mixed_ref, load_sem) = refs[-8:]
        refs = refs[13:-17]
    else:
        (own_ref, rider_ref, far_ref, in_ref, wt_hbm, bias_ref) = refs[:6]
        (turned_ref, out_hbm, mixed_hbm, total_ref, delta_ref, rider_out, spread_out, in_out) = refs[6:14]
        (turned, wt_ref, out_ref, mixed_ref, load_sem, keep_sem) = refs[-6:]
        refs = refs[14:-6]
    (
        wq_ref, wo_ref, held, wide, narrow, kept, core_out, core_in, near_out, near_in,
        gy_send, gy_recv, gc_send, gc_recv, gd_send, gd_recv, sc_send, sc_recv, sy_send, sy_recv,
        r_send, r_recv, r_local, out_sem, wx_send, wx_recv,
    ) = refs
    y, x, c, z = (lax.axis_index(name) for name in AXES)
    near, pair, near_x = (1 - y, x, c, z), (y, x, 1 - c, z), (y, 1 - x, c, z)
    frames = held.shape[0] // 4
    chunks = held.shape[1] // CHUNK
    width = heads * HEAD_DIM
    groups = CHUNK // GROUP

    loads = [(wt_hbm, wt_ref), (own_ref, held.at[pl.ds(0, frames)])]
    if back:
        loads += [(joined_hbm, joined_ref), (mixed_hbm, mixed_ref)]
    loads = [pltpu.make_async_copy(src, dst, load_sem.at[i]) for i, (src, dst) in enumerate(loads)]
    for copy in loads:
        copy.start()
    barrier = pltpu.get_barrier_semaphore()
    for dc in range(2):
        for dz in range(4):
            if dc or dz:
                pl.semaphore_signal(barrier, inc=1, device_id=(y, x, (c + dc) % 2, (z + dz) % 4), device_id_type=MESH)
    pl.semaphore_signal(barrier, inc=1, device_id=near, device_id_type=MESH)
    pl.semaphore_signal(barrier, inc=1, device_id=near_x, device_id_type=MESH)
    pl.semaphore_wait(barrier, 9)

    def remote(src, dst, send, recv, peer):
        return pltpu.make_async_remote_copy(
            src_ref=src, dst_ref=dst, send_sem=send, recv_sem=recv, device_id=peer, device_id_type=MESH
        )

    def patches(k):
        return pl.ds(pl.multiple_of(k * CHUNK, CHUNK), CHUNK)

    def block(b, k):
        return held.at[pl.ds(b * frames, frames), patches(k)]

    def gather_y(k):
        return remote(own_ref.at[:, patches(k)], block(1, k), gy_send.at[k], gy_recv.at[k], near)

    def gather_c(k):
        return remote(own_ref.at[:, patches(k)], block(2, k), gc_send.at[k], gc_recv.at[k], pair)

    def gather_d(k):
        return remote(block(1, k), block(3, k), gd_send.at[k], gd_recv.at[k], pair)

    def scatter_c(k):
        return remote(core_out.at[k], core_in.at[k], sc_send.at[k], sc_recv.at[k], pair)

    def scatter_y(k):
        return remote(near_out.at[k], near_in.at[k], sy_send.at[k], sy_recv.at[k], near)

    def save_results(k):
        return [
            pltpu.make_async_copy(src.at[:, patches(k)], dst.at[:, patches(k)], keep_sem.at[i, k])
            for i, (src, dst) in enumerate(((out_ref, out_hbm), (mixed_ref, mixed_hbm)))
        ]

    def save(k):
        there = (turned_ref.at[k], turned.at[k]) if back else (turned.at[k], turned_ref.at[k])
        return pltpu.make_async_copy(*there, out_sem.at[k])

    def columns(s):
        return pl.ds(pl.multiple_of(s * BLK, BLK), BLK)

    def stays(k):
        if back:
            return jnp.logical_and(z == k, z // 2 == c)
        return jnp.logical_and(2 * c + k // 2 == z, c == k % 2)

    def ride(k):
        if back:
            src, dst = rider_ref.at[:, columns(k)], rider_out.at[2 * (z % 2) + c]
            peer, slot = (y, x, z // 2, k), 2 * (z % 2) + c
        else:
            src, dst = rider_ref.at[k], rider_out.at[:, columns(z)]
            peer, slot = (y, x, k % 2, 2 * c + k // 2), z
        return src, dst, peer, slot

    def ride_remote(k):
        src, dst, peer, slot = ride(k)
        return remote(src, dst, r_send.at[k], r_recv.at[slot], peer)

    def ride_local(k):
        src, dst, _, _ = ride(k)
        return pltpu.make_async_copy(src, dst, r_local.at[0])

    def ride_landed(k):
        if back:
            src, dst = rider_ref.at[:, columns(k)], rider_out.at[k]
        else:
            src, dst = rider_ref.at[k], rider_out.at[:, columns(k)]
        return remote(src, dst, r_send.at[k], r_recv.at[k], near)

    def from_self(k):
        if back:
            return jnp.logical_and(2 * c + k // 2 == z, c == k % 2)
        return jnp.logical_and(z == k, z // 2 == c)

    def spread_x(i, dx=0):
        r, yb = i // 2 + 1, i % 2
        size = far_ref.shape[1] // 4
        at = pl.multiple_of(size * (2 * yb + (x + dx) % 2), size)
        src = far_ref.at[(z + r) % 4, pl.ds(at, size)]
        return remote(src, spread_out.at[(z + r) % 4, pl.ds(at, size)], wx_send.at[i], wx_recv.at[i], near_x)

    gather_y(0).start()
    for k in range(chunks):
        if k > 0:
            gather_y(k).start()
        gather_c(k).start()
    def spread_in(dx=0):
        at = pl.multiple_of(BLK * (2 * (1 - y) + (x + dx) % 2), BLK)
        there = in_out.at[3 - z, pl.ds(at, BLK)]
        return remote(in_ref.at[3 - z, pl.ds(at, BLK)], there, wx_send.at[6], wx_recv.at[6], near_x)

    at_end = jnp.logical_or(z == 0, z == 3)

    def half_away(s):
        return remote(wide_ref.at[1 - x, s], half_in.at[s], half_send.at[s], half_recv.at[s], near_x)

    def half_here(s):
        return pltpu.make_async_copy(wide_ref.at[x, s], half_own.at[s], half_local.at[s])

    def line_away(r):
        return remote(line_out.at[r], line_in.at[r], line_send.at[r], line_recv.at[r], (y, x, c, (z + r) % 4))

    def halve():
        for s in range(4):
            half_away(s).wait_recv()
            half_here(s).wait()
        for r in range(4):
            s = (z + r) % 4
            whole = half_own[s].astype(F32) + half_in[s].astype(F32)
            if r == 0:
                reduced_ref[...] = whole
            else:
                line_out[r] = whole.astype(BF16)
                line_away(r).start()

    if back:
        for s in range(4):
            half_away(s).start()
            half_here(s).start()
    else:
        pl.when(at_end)(lambda: spread_in().start())
        for i in range(6):
            spread_x(i).start()
    for k in range(4):
        pl.when(stays(k))(lambda k=k: ride_local(k).start())
        pl.when(jnp.logical_not(stays(k)))(lambda k=k: ride_remote(k).start())
    if back:
        for k in range(chunks):
            save(k).start()

    def assemble(i, carry):
        rows = pl.ds(pl.multiple_of(i * BLK, BLK), BLK)
        for s in range(0, heads, 2):
            for part in range(4):
                both = [
                    wt_ref[rows, (s + j) * 4 * HEAD_DIM + part * HEAD_DIM : (s + j) * 4 * HEAD_DIM + (part + 1) * HEAD_DIM]
                    for j in range(2)
                ]
                both = jnp.concatenate(both, axis=1)
                if part < 3:
                    wq_ref[rows, part * width + s * HEAD_DIM : part * width + s * HEAD_DIM + PAIR] = both
                else:
                    wo_ref[rows, s * HEAD_DIM : s * HEAD_DIM + PAIR] = both
        return carry

    loads[0].wait()
    lax.fori_loop(0, wt_ref.shape[0] // BLK, assemble, 0)
    for copy in loads[1:]:
        copy.wait()

    def finish(k):
        scatter_c(k).wait_recv()
        both = kept[:, patches(k)] + core_in[k].astype(F32)
        near_out[k] = both[frames:].astype(BF16)
        delta_ref[:, patches(k)] = both[:frames]
        scatter_y(k).start()

    def pass_on(k):
        gather_y(k).wait_recv()
        gather_d(k).start()

    def one_group(i, rows):
        at = pl.ds(pl.multiple_of(i * GROUP, GROUP), GROUP)
        count = 4 * frames * GROUP
        bias = bias_ref[...]
        for lo in range(0, width, PAIR):
            q, k, v = (
                wide[:, at, part * width + lo : part * width + lo + PAIR].reshape(count, PAIR).astype(BF16)
                for part in range(3)
            )
            h = lo // HEAD_DIM
            if back:
                g = narrow[:, at, lo : lo + PAIR].reshape(count, PAIR).astype(BF16)
                totals = [total_ref[rows * groups + i, h + j : h + j + 1, :] for j in range(2)]
                grads = attend_pair_back(q, k, v, g, totals, bias, scale)
                for part in range(3):
                    wide[:, at, part * width + lo : part * width + lo + PAIR] = grads[part].reshape(
                        4 * frames, GROUP, PAIR
                    )
            else:
                mixed, totals = attend_pair(q, k, v, bias, scale)
                narrow[:, at, lo : lo + PAIR] = mixed.reshape(4 * frames, GROUP, PAIR)
                for j in range(2):
                    total_ref[rows * groups + i, h + j : h + j + 1, :] = totals[j]

    def one_chunk(k, carry):
        pl.when(k + 1 < chunks)(lambda: pass_on(k + 1))
        gather_c(k).wait_recv()
        gather_d(k).wait_recv()
        count = 4 * frames * CHUNK
        lhs = held[:, patches(k)].reshape(count, held.shape[2])
        if back:
            wide[...] = joined_ref[:, patches(k)].astype(F32)
            narrow[...] = dot_nn(lhs, wo_ref[...]).astype(BF16).astype(F32).reshape(narrow.shape)
        else:
            joined = dot_nn(lhs, wq_ref[...]).astype(BF16)
            out_ref[:, patches(k)] = joined.reshape(wide.shape)
            wide[...] = joined.astype(F32).reshape(wide.shape)
        lax.fori_loop(0, groups, lambda i, carry: (one_group(i, k), carry)[1], 0)
        if back:
            grads = wide[...].astype(BF16)
            out_ref[:, patches(k)] = grads
            partial = dot_nt(grads.reshape(count, 3 * width), wq_ref[...])
        else:
            mixed = narrow[...].astype(BF16)
            mixed_ref[:, patches(k)] = mixed
            partial = dot_nt(mixed.reshape(count, width), wo_ref[...])
        partial = partial.reshape(4 * frames, CHUNK, held.shape[2])
        kept[:, patches(k)] = partial[: 2 * frames]
        core_out[k] = partial[2 * frames :].astype(BF16)
        scatter_c(k).start()
        pl.when(k > 0)(lambda: finish(k - 1))
        if not back:
            for b in range(4):
                slab = held[b * frames : (b + 1) * frames, patches(k)].reshape(frames * CHUNK, held.shape[2])
                turned[k, :, b * frames * CHUNK : (b + 1) * frames * CHUNK] = slab.T
            save(k).start()
            for copy in save_results(k):
                copy.start()
        if back:
            pl.when(k == chunks // 2 - 1)(halve)
        return carry

    pass_on(0)
    lax.fori_loop(0, chunks, one_chunk, 0)
    finish(chunks - 1)

    def weigh(k, carry):
        count = 4 * frames * CHUNK
        save(k).wait()
        grad_qkv[...] = grad_qkv[...] + dot_nn(turned[k], out_ref[:, patches(k)].reshape(count, 3 * width))
        grad_out[...] = grad_out[...] + dot_tn(
            mixed_ref[:, patches(k)].reshape(count, width), held[:, patches(k)].reshape(count, held.shape[2])
        )
        return carry

    def arrange(i, carry):
        rows = pl.ds(pl.multiple_of(i * BLK, BLK), BLK)
        last = grad_out[:, rows].T
        for s in range(heads):
            mine = slice(s * HEAD_DIM, (s + 1) * HEAD_DIM)
            parts = [grad_qkv[rows, j * width : (j + 1) * width][:, mine] for j in range(3)] + [last[:, mine]]
            grad_ref[rows, 2 * s * PAIR : (2 * s + 1) * PAIR] = jnp.concatenate(parts[:2], axis=1).astype(BF16)
            grad_ref[rows, (2 * s + 1) * PAIR : (2 * s + 2) * PAIR] = jnp.concatenate(parts[2:], axis=1).astype(BF16)
        return carry

    if back:
        grad_qkv[...] = jnp.zeros_like(grad_qkv)
        grad_out[...] = jnp.zeros_like(grad_out)
        lax.fori_loop(0, chunks, weigh, 0)
        lax.fori_loop(0, grad_ref.shape[0] // BLK, arrange, 0)
    for k in range(chunks):
        scatter_y(k).wait_recv()
        delta_ref[:, patches(k)] = delta_ref[:, patches(k)] + near_in[k].astype(F32)
    if back:
        for r in (1, 2, 3):
            line_away(r).wait_recv()
            reduced_ref[...] = reduced_ref[...] + line_in[r].astype(F32)
        for r in (1, 2, 3):
            line_away(r).wait_send()
        for s in range(4):
            half_away(s).wait_send()
    for k in range(chunks):
        for copy in (gather_y(k), gather_c(k), gather_d(k), scatter_c(k), scatter_y(k)):
            copy.wait_send()
        if not back:
            save(k).wait()
            for copy in save_results(k):
                copy.wait()
    if not back:
        for i in range(6):
            spread_x(i, 1).wait_recv()
            spread_x(i).wait_send()

        def spread_in_end():
            spread_in(1).wait_recv()
            spread_in().wait_send()

        pl.when(at_end)(spread_in_end)
    for k in range(4):
        pl.when(stays(k))(lambda k=k: ride_local(k).wait())
        pl.when(jnp.logical_not(stays(k)))(lambda k=k: ride_remote(k).wait_send())
        pl.when(jnp.logical_not(from_self(k)))(lambda k=k: ride_landed(k).wait_recv())


def time_call(back, own, rider, saved, weights, bias, scale):
    frames, patches, features = own.shape
    width = weights.shape[1] // 4
    heads = width // HEAD_DIM
    chunks = patches // CHUNK
    rows = 4 * frames * GROUP
    dma = pltpu.SemaphoreType.DMA
    anywhere = pl.BlockSpec(memory_space=pl.ANY)
    whole = pl.BlockSpec(memory_space=pltpu.VMEM)
    turned = (chunks, features, 4 * frames * CHUNK)
    if back:
        out_shape = []
    else:
        out_shape = [
            jax.ShapeDtypeStruct(turned, BF16),
            jax.ShapeDtypeStruct((4 * frames, patches, 3 * width), BF16),
            jax.ShapeDtypeStruct((4 * frames, patches, width), BF16),
            jax.ShapeDtypeStruct((patches // GROUP, heads, rows), F32),
        ]
    rider_shape = (4, frames * patches, BLK) if back else (frames * patches, features)
    out_shape += [
        jax.ShapeDtypeStruct((frames, patches, features), F32),
        jax.ShapeDtypeStruct(rider_shape, BF16),
    ]
    held = 2
    half = saved[2].shape[1:] if back else None
    if back:
        out_shape.insert(-1, jax.ShapeDtypeStruct((features, features), BF16))
        out_shape.insert(-1, jax.ShapeDtypeStruct(half[1:], F32))
    else:
        out_shape += [jax.ShapeDtypeStruct(w.shape, BF16) for w in saved]
        held = 4
    return pl.pallas_call(
        functools.partial(time_kernel, back, scale, heads),
        in_specs=[anywhere] * 2
        + ([anywhere, whole, anywhere, anywhere, anywhere] if back else [anywhere] * 2)
        + [anywhere, whole],
        out_specs=([] if back else [anywhere] * 3) + [whole] * (3 if back else 2) + [anywhere] * (held - 1),
        out_shape=out_shape,
        scratch_shapes=[
            pltpu.VMEM((features, 3 * width), BF16),
            pltpu.VMEM((features, width), BF16),
            pltpu.VMEM((4 * frames, patches, features), BF16),
            pltpu.VMEM((4 * frames, CHUNK, 3 * width), F32),
            pltpu.VMEM((4 * frames, CHUNK, width), F32),
            pltpu.VMEM((2 * frames, patches, features), F32),
            pltpu.VMEM((chunks, 2 * frames, CHUNK, features), BF16),
            pltpu.VMEM((chunks, 2 * frames, CHUNK, features), BF16),
            pltpu.VMEM((chunks, frames, CHUNK, features), BF16),
            pltpu.VMEM((chunks, frames, CHUNK, features), BF16),
        ]
        + [dma((chunks,))] * 10
        + [dma((4,)), dma((4,)), dma((1,)), dma((chunks,))]
        + [dma((7,))] * 2
        + ([pltpu.VMEM(half, BF16)] * 4 + [dma((4,))] * 5 if back else [])
        + ([pltpu.VMEM((4 * frames, patches, 3 * width), BF16)] if back else [])
        + [pltpu.VMEM(turned, BF16)]
        + ([pltpu.VMEM((features, 3 * width), F32), pltpu.VMEM((width, features), F32)] if back else [])
        + [pltpu.VMEM(weights.shape, BF16)]
        + ([pltpu.VMEM(saved[0].shape, BF16), pltpu.VMEM(saved[4].shape, BF16)] if back else [])
        + ([] if back else [pltpu.VMEM(out_shape[1].shape, BF16), pltpu.VMEM(out_shape[2].shape, BF16)])
        + [dma((4,))]
        + ([] if back else [dma((2, chunks))]),
        compiler_params=pltpu.CompilerParams(
            collective_id=2 if back else 1, has_side_effects=True, vmem_limit_bytes=60 * 1024 * 1024
        ),
        cost_estimate=pl.CostEstimate(flops=10**10, transcendentals=10**6, bytes_accessed=10**8),
        name="time_back" if back else "time_forward",
    )(own, rider, *saved, weights, bias)


def feed_kernel(
    resid_hbm, delta_hbm, upstream_hbm, masked, gain, w_in_hbm, w_in_far_hbm, w_out_hbm, w_far_hbm,
    half_in_hbm, half_out_hbm, grad_hbm, low_hbm, rows_hbm, gain_out,
    resid, delta, upstream, grad_out, low_out, rows_out, move_sem,
    w_in, w_out, standard, inverse, normed, grads, normed_t, grads_t, hidden, pulled, g_in, g_out, back, ahead,
    back_out, back_in, ahead_out, ahead_in, from_x, from_y, slopes,
    w_sem, g_sem, n_send, n_recv, b_send, b_recv, hx_send, hx_recv, hy_send, hy_recv,
):
    y, x, c, z = (lax.axis_index(name) for name in AXES)
    pair, near_y, near_x = (y, x, 1 - c, z), (1 - y, x, c, z), (y, 1 - x, c, z)
    own = resid.shape[0]
    moves = [
        pltpu.make_async_copy(src, dst, move_sem.at[i])
        for i, (src, dst) in enumerate((
            (resid_hbm, resid), (delta_hbm, delta), (upstream_hbm, upstream),
            (grad_out, grad_hbm), (low_out, low_hbm), (rows_out, rows_hbm),
        ))
    ]
    for copy in moves[:3]:
        copy.start()
    step = own // 2
    slab = 128

    def fetch(s, far, last=False):
        size = w_out.shape[1] // 4
        copies = []
        for i in range(4):
            rows = pl.ds(pl.multiple_of(BLK * (2 * ((y + i // 2) % 2) + (x + i % 2) % 2), BLK), BLK)
            source = w_in_far_hbm if last and i == 3 else w_in_hbm
            copies.append(pltpu.make_async_copy(source.at[s, rows], w_in.at[s, rows], w_sem.at[5 + i, s]))
        for i in range(4):
            rows = pl.ds(pl.multiple_of(size * (2 * (i // 2) + (x + i % 2) % 2), size), size)
            source = w_far_hbm if far and i % 2 else w_out_hbm
            copies.append(pltpu.make_async_copy(source.at[s, rows], w_out.at[s, rows], w_sem.at[i, s]))
        return copies

    def fetch_now(s, far, last):
        for copy in fetch(s, far, last):
            copy.start()

    for s in range(4):
        pl.when(z == s)(lambda s=s: fetch_now(s, False, False))
        if s in (0, 3):
            pl.when(z == 3 - s)(lambda s=s: fetch_now(s, True, True))
            pl.when(jnp.logical_and(z != s, z != 3 - s))(lambda s=s: fetch_now(s, True, False))
        else:
            pl.when(z != s)(lambda s=s: fetch_now(s, True, False))
    barrier = pltpu.get_barrier_semaphore()
    for peer in (pair, near_y, near_x):
        pl.semaphore_signal(barrier, inc=1, device_id=peer, device_id_type=MESH)

    def remote(src, dst, send, recv, peer=pair):
        return pltpu.make_async_remote_copy(
            src_ref=src, dst_ref=dst, send_sem=send, recv_sem=recv, device_id=peer, device_id_type=MESH
        )

    def block(yb, xb):
        return pl.ds(pl.multiple_of(BLK * (2 * yb + xb), BLK), BLK)

    def away_x(s, i):
        return remote(g_out.at[s, block(i, 1 - x)], from_x.at[i, s], hx_send.at[i, s], hx_recv.at[i, s], near_x)

    def away_y(s, i):
        return remote(g_in.at[s, block(1 - y, i)], from_y.at[i, s], hy_send.at[i, s], hy_recv.at[i, s], near_y)

    def keep(s, i):
        return (
            pltpu.make_async_copy(g_out.at[s, block(i, x)], half_out_hbm.at[i, s], g_sem.at[0, i, s]),
            pltpu.make_async_copy(g_in.at[s, block(y, i)], half_in_hbm.at[i, s], g_sem.at[1, i, s]),
        )

    def combine(s):
        for i in range(2):
            away_x(s, i).wait_recv()
            g_out[s, block(i, x)] = (g_out[s, block(i, x)].astype(F32) + from_x[i, s].astype(F32)).astype(BF16)
            away_y(s, i).wait_recv()
            g_in[s, block(y, i)] = (g_in[s, block(y, i)].astype(F32) + from_y[i, s].astype(F32)).astype(BF16)
            for copy in keep(s, i):
                copy.start()

    def at(i, size):
        return pl.ds(pl.multiple_of(i * size, size), size)

    def prepare(i, carry):
        rows = at(i, step)
        grads[rows] = jnp.where(masked[rows] > 0.0, upstream[rows].astype(F32), 0.0).astype(BF16)
        std, inv = norm_rows(resid[rows] + delta[rows])
        standard[rows] = std
        inverse[rows] = inv
        normed[rows] = (std * gain[3:4]).astype(BF16)
        return carry

    for copy in moves[:3]:
        copy.wait()
    lax.fori_loop(0, 2, prepare, 0)
    pl.semaphore_wait(barrier, 3)
    mine, theirs = pl.ds(0, own), pl.ds(own, own)
    give_grads = remote(grads.at[mine], grads.at[theirs], n_send.at[0], n_recv.at[0])
    give_normed = remote(normed.at[mine], normed.at[theirs], n_send.at[1], n_recv.at[1])
    give_normed.start()
    give_grads.start()

    def turn(i, carry):
        rows = at(i, slab)
        normed_t[:, rows] = normed[rows].T
        grads_t[:, rows] = grads[rows].T
        return carry

    lax.fori_loop(0, own // slab, turn, 0)
    rate = math.sqrt(2.0 / math.pi)

    def bend_step(s, rows):
        inner = dot_nn(normed[rows], w_in[s])
        square = inner * inner
        bend = jnp.tanh(rate * inner * (1.0 + 0.044715 * square))
        hidden[rows] = (0.5 * inner * (1.0 + bend)).astype(BF16)
        slopes[rows] = 0.5 * (1.0 + bend) + 0.5 * inner * (1.0 - bend * bend) * (rate * (1.0 + 3.0 * 0.044715 * square))

    def pull_step(s, rows):
        pulled[rows] = (dot_nt(grads[rows], w_out[s]) * slopes[rows]).astype(BF16)

    def add_step(s, rows):
        ahead[rows] = ahead[rows] + dot_nn(hidden[rows], w_out[s])
        back[rows] = back[rows] + dot_nt(pulled[rows], w_in[s])

    def clear():
        back[...] = jnp.zeros_like(back)
        ahead[...] = jnp.zeros_like(ahead)

    def meet():
        give_normed.wait_recv()
        give_grads.wait_recv()
        lax.fori_loop(own // slab, 2 * own // slab, turn, 0)

    def one_piece(s, carry):
        for copy in fetch(s, False):
            copy.wait()

        def first_half(t, carry):
            pl.when(jnp.logical_and(s == 0, t == 1))(meet)
            bend_step(s, at(t, own))
            return carry

        lax.fori_loop(0, 2, first_half, 0)
        g_out[s] = dot_nn(grads_t[...], hidden[...]).astype(BF16)
        for i in range(2):
            away_x(s, i).start()
        lax.fori_loop(0, 2, lambda t, carry: (pull_step(s, at(t, own)), carry)[1], 0)
        g_in[s] = dot_nn(normed_t[...], pulled[...]).astype(BF16)
        for i in range(2):
            away_y(s, i).start()
        pl.when(s == 0)(clear)
        lax.fori_loop(0, 2, lambda t, carry: (add_step(s, at(t, own)), carry)[1], 0)
        return carry

    lax.fori_loop(0, 4, one_piece, 0)
    back_out[...] = back[theirs].astype(BF16)
    give_back = remote(back_out, back_in, b_send.at[0], b_recv.at[0])
    give_back.start()
    ahead_out[...] = ahead[theirs].astype(BF16)
    give_ahead = remote(ahead_out, ahead_in, b_send.at[1], b_recv.at[1])
    give_ahead.start()
    give_back.wait_recv()

    def finish(i, total):
        rows = at(i, step)
        grad = back[rows] + back_in[rows].astype(F32)
        std = standard[rows]
        inner = grad * gain[3:4]
        mean = jnp.mean(inner, axis=-1, keepdims=True)
        along = jnp.mean(inner * std, axis=-1, keepdims=True)
        full = grads[rows].astype(F32) + (inner - mean - std * along) * inverse[rows]
        grad_out[rows] = full
        low_out[rows] = full.astype(BF16)
        return total + jnp.sum(grad * std, axis=0, keepdims=True)

    gain_out[...] = lax.fori_loop(0, 2, finish, jnp.zeros((1, resid.shape[1]), F32))
    moves[3].start()
    moves[4].start()
    give_ahead.wait_recv()

    def emit(i, carry):
        rows = at(i, step)
        rows_out[rows] = (resid[rows] + delta[rows] + ahead[rows] + ahead_in[rows].astype(F32)).astype(BF16)
        return carry

    lax.fori_loop(0, 2, emit, 0)
    moves[5].start()
    lax.fori_loop(0, 4, lambda s, carry: (combine(s), carry)[1], 0)
    for copy in (give_normed, give_grads, give_back, give_ahead):
        copy.wait_send()
    for s in range(4):
        for i in range(2):
            away_x(s, i).wait_send()
            away_y(s, i).wait_send()
            for copy in keep(s, i):
                copy.wait()
    for copy in moves[3:]:
        copy.wait()


def feed(resid, delta, upstream, masked, gain, w_in, w_in_far, w_out, w_far):
    own, features = resid.shape
    units = w_in.shape[2]
    dma = pltpu.SemaphoreType.DMA
    anywhere = pl.BlockSpec(memory_space=pl.ANY)
    whole = pl.BlockSpec(memory_space=pltpu.VMEM)

    def low(*shape):
        return pltpu.VMEM(shape, BF16)

    def high(*shape):
        return pltpu.VMEM(shape, F32)

    return pl.pallas_call(
        feed_kernel,
        in_specs=[anywhere] * 3 + [whole] * 2 + [anywhere] * 4,
        out_specs=[anywhere] * 5 + [whole],
        out_shape=[
            jax.ShapeDtypeStruct((2, 4, BLK, units), BF16),
            jax.ShapeDtypeStruct((2, 4, BLK, units), BF16),
            jax.ShapeDtypeStruct((own, features), F32),
            jax.ShapeDtypeStruct((own, features), BF16),
            jax.ShapeDtypeStruct((own, features), BF16),
            jax.ShapeDtypeStruct((1, features), F32),
        ],
        scratch_shapes=[
            high(own, features), high(own, features), low(own, features),
            high(own, features), low(own, features), low(own, features), dma((6,)),
            low(4, features, units), low(4, units, features), high(own, features), high(own, 1),
            low(2 * own, features), low(2 * own, features), low(features, 2 * own), low(features, 2 * own),
            low(2 * own, units), low(2 * own, units), low(4, features, units), low(4, features, units),
            high(2 * own, features), high(2 * own, features),
            low(own, features), low(own, features), low(own, features), low(own, features),
            low(2, 4, BLK, units), low(2, 4, BLK, units), high(2 * own, units),
            dma((9, 4)), dma((2, 2, 4)), dma((2,)), dma((2,)), dma((2,)), dma((2,)),
            dma((2, 4)), dma((2, 4)), dma((2, 4)), dma((2, 4)),
        ],
        compiler_params=pltpu.CompilerParams(
            collective_id=4, has_side_effects=True, vmem_limit_bytes=60 * 1024 * 1024
        ),
        cost_estimate=pl.CostEstimate(flops=26 * 10**9, transcendentals=2 * 10**6, bytes_accessed=10**8),
        name="feed",
    )(resid, delta, upstream, masked, gain, w_in, w_in_far, w_out, w_far)


def leave_kernel(
    scale,
    part_hbm, next_hbm, grad_hbm, out_hbm, joined_hbm, mixed_hbm, lhs_hbm, weight_hbm, std_hbm, time_hbm, feed_hbm, feed_in_hbm,
    totals, inverse_next, inverse, masked, gains, later_grad,
    space_qkv, space_out, feed_in_out, feed_out_out, time_qkv, time_out, rows_out, gains_out, embed_out,
    rows_in,
    part, std, base, w_out, dj, mixed, lhs, weight, low_grads, turned, dmixed, go,
    t_own, t_in, tz_out, tz_in, t_total, ty_out, ty_in, tc_out, tc_in,
    f_own, f_in, fz_out, fz_in, f_total, f_other, fc_out, fc_in,
    grads, a1_out, a1_in, b1_out, b1_in, a2_out, a2_in, b2_out, b2_in, z_out, z_in,
    half_out, half_in, ready, core_out, core_in, sums, sum_out, sum_in, share_in,
    a1_send, a1_recv, b1_send, b1_recv, a2_send, a2_recv, b2_send, b2_recv, z_send, z_recv,
    h_send, h_recv, r_send, r_recv, c_send, c_recv, s_send, s_recv, p_send, p_recv, local,
    g_send, g_recv, tx_send, tx_recv, tz_send, tz_recv, ty_send, ty_recv, fy_send, fy_recv, fz_send, fz_recv, t_local, f_local, fetched,
):
    y, x, c, z = (lax.axis_index(name) for name in AXES)
    near_y, near_x, pair = (1 - y, x, c, z), (y, 1 - x, c, z), (y, x, 1 - c, z)
    own = std.shape[0]
    third = go.shape[1] // 4
    wide = 3 * third
    two = 2 * third
    slab = 128

    fetches = [
        pltpu.make_async_copy(src, dst, fetched.at[i])
        for i, (src, dst) in enumerate((
            (part_hbm, part), (next_hbm, std), (grad_hbm, base), (out_hbm, w_out), (joined_hbm, dj), (mixed_hbm, mixed),
            (lhs_hbm, lhs), (weight_hbm, weight), (feed_in_hbm, f_other),
        ))
    ]
    for copy in fetches:
        copy.start()
    fetch_std = pltpu.make_async_copy(std_hbm, std, fetched.at[9])

    barrier = pltpu.get_barrier_semaphore()
    for dc in range(2):
        for dz in range(4):
            if dc or dz:
                pl.semaphore_signal(barrier, inc=1, device_id=(y, x, (c + dc) % 2, (z + dz) % 4), device_id_type=MESH)
    for peer in (near_y, near_x):
        pl.semaphore_signal(barrier, inc=1, device_id=peer, device_id_type=MESH)
    pl.semaphore_wait(barrier, 9)

    def remote(src, dst, send, recv, peer):
        return pltpu.make_async_remote_copy(
            src_ref=src, dst_ref=dst, send_sem=send, recv_sem=recv, device_id=peer, device_id_type=MESH
        )

    def at(i, length):
        return pl.ds(pl.multiple_of(i * length, length), length)

    def along(r):
        return (y, x, c, (z + r) % 4)

    def time_x(yb):
        return remote(time_hbm.at[at(2 * yb + 1 - x, BLK)], t_in.at[yb], tx_send.at[yb], tx_recv.at[yb], near_x)

    def time_keep(yb):
        return pltpu.make_async_copy(time_hbm.at[at(2 * yb + x, BLK)], t_own.at[yb], t_local.at[yb])

    def time_z(r):
        return remote(tz_out.at[r], tz_in.at[r], tz_send.at[r], tz_recv.at[r], along(1))

    def feed_y(r):
        s = (z + r) % 4
        return remote(feed_hbm.at[1 - y, s], f_in.at[r], fy_send.at[r], fy_recv.at[r], near_y)

    def feed_keep(r):
        return pltpu.make_async_copy(feed_hbm.at[y, (z + r) % 4], f_own.at[r], f_local.at[r])

    def feed_z(r):
        return remote(fz_out.at[r], fz_in.at[r], fz_send.at[r], fz_recv.at[r], along(1))

    for r in (3, 2, 1, 0):
        feed_y(r).start()
        feed_keep(r).start()
    for yb in range(2):
        time_x(yb).start()
        time_keep(yb).start()

    def feed_step(t):
        r = 3 - t
        feed_y(r).wait_recv()
        feed_keep(r).wait()
        total = f_own[r].astype(F32) + f_in[r].astype(F32)
        if t > 0:
            feed_z(t - 1).wait_recv()
            total = total + fz_in[t - 1].astype(F32)
        if t == 3:
            f_total[...] = total
        else:
            fz_out[t] = total.astype(BF16)
            feed_z(t).start()

    def time_step(t):
        if t == 0:
            for yb in range(2):
                time_x(yb).wait_recv()
                time_keep(yb).wait()
        else:
            time_z(t - 1).wait_recv()
        piece_at = at((z + 3 - t) % 4, BLK)
        for yb in range(2):
            total = t_own[yb, :, piece_at].astype(F32) + t_in[yb, :, piece_at].astype(F32)
            if t > 0:
                total = total + tz_in[t - 1, yb].astype(F32)
            if t == 3:
                t_total[yb] = total
            else:
                tz_out[t, yb] = total.astype(BF16)
        if t < 3:
            time_z(t).start()

    step = own // 2
    for copy in fetches[:3]:
        copy.wait()

    def norm_back(grad, standard, weights, inv):
        inner = grad * weights
        mean = jnp.mean(inner, axis=-1, keepdims=True)
        slope = jnp.mean(inner * standard, axis=-1, keepdims=True)
        return (inner - mean - standard * slope) * inv

    def after_time(i, total):
        rows = at(i, step)
        grad, standard = part[rows], std[rows]
        full = base[rows] + norm_back(grad, standard, gains[2:3], inverse_next[rows])
        base[rows] = full
        low_grads[rows] = full.astype(BF16)
        return total + jnp.sum(grad * standard, axis=0, keepdims=True)

    zero = jnp.zeros((1, std.shape[1]), F32)
    next_grad = lax.fori_loop(0, 2, after_time, zero)
    give = remote(low_grads.at[pl.ds(0, own)], low_grads.at[pl.ds(own, own)], g_send.at[0], g_recv.at[0], pair)
    give.start()
    fetch_std.start()
    for copy in fetches[3:6]:
        copy.wait()

    def attend(i, carry):
        rows = at(i, slab)
        for h in range(mixed.shape[1] // PAIR):
            places = [pl.ds((3 * h + j) * PAIR, PAIR) for j in range(3)]
            q, k, v = (dj[rows, place] for place in places)
            lines = [totals[i, 2 * h + j : 2 * h + j + 1, :] for j in range(2)]
            found = attend_pair_back(q, k, v, dmixed[rows, h * PAIR : (h + 1) * PAIR], lines, None, scale)
            for place, value in zip(places, found):
                dj[rows, place] = value.astype(BF16)
        return carry

    def turn(i, carry):
        turned[:, at(i, slab)] = low_grads[at(i, slab)].T
        return carry

    def attend_half(t, *between):
        rows = pl.ds(t * own, own)
        first, count = t * own // slab, own // slab
        dmixed[rows] = dot_nt(low_grads[rows], w_out[...]).astype(BF16)
        between[0]()
        lax.fori_loop(first, first + count // 2, attend, 0)
        between[1]()
        lax.fori_loop(first + count // 2, first + count, attend, 0)
        between[2]()
        lax.fori_loop(first, first + count, turn, 0)

    def nothing():
        pass

    attend_half(0, lambda: feed_step(0), nothing, lambda: feed_step(1))
    give.wait_recv()
    attend_half(1, nothing, lambda: feed_step(2), lambda: time_step(0))
    for copy in fetches[6:]:
        copy.wait()
    def away(i, carry):
        rows = pl.ds(pl.multiple_of(own + i * step, step), step)
        half_out[pl.ds(pl.multiple_of(i * step, step), step)] = dot_nt(dj[rows], weight[...]).astype(BF16)
        return carry

    lax.fori_loop(0, 2, away, 0)
    swap = remote(half_out, half_in, h_send.at[0], h_recv.at[0], pair)
    swap.start()

    def block(yb, xb):
        return pl.ds(pl.multiple_of(BLK * (2 * yb + xb), BLK), BLK)

    def a1(i):
        return remote(a1_out.at[i], a1_in.at[i], a1_send.at[i], a1_recv.at[i], near_x)

    def b1(i):
        return remote(b1_out.at[i], b1_in.at[i], b1_send.at[i], b1_recv.at[i], near_y)

    def a2(i):
        return remote(a2_out.at[i], a2_in.at[i], a2_send.at[i], a2_recv.at[i], near_y)

    def b2(i):
        return remote(b2_out.at[i], b2_in.at[i], b2_send.at[i], b2_recv.at[i], near_x)

    def to_z(r):
        return remote(z_out.at[r], z_in.at[r], z_send.at[r], z_recv.at[r], along(r))

    def send_first(i):
        a1(i).start()
        b1(i).start()

    def piece(i, carry):
        s = (z + i + 1) % 4
        made = dot_nn(lhs[...], dj[:, pl.ds(pl.multiple_of(s * wide, third), wide)])
        grads[i, :, :wide] = made
        grads[i, :, wide:] = go[:, pl.ds(pl.multiple_of(s * third, third), third)].astype(F32)
        for b in range(2):
            a1_out[i, b] = grads[i, block(b, 1 - x), :two].astype(BF16)
            b1_out[i, b] = grads[i, block(1 - y, b), two:].astype(BF16)
        pl.when(i < 2)(lambda: send_first(i))
        return carry


    def second(i):
        a1(i).wait_recv()
        a2_out[i] = (grads[i, block(1 - y, x), :two] + a1_in[i, 1 - y].astype(F32)).astype(BF16)
        a2(i).start()
        b1(i).wait_recv()
        b2_out[i] = (grads[i, block(y, 1 - x), two:] + b1_in[i, 1 - x].astype(F32)).astype(BF16)
        b2(i).start()
        grads[i, block(y, x), :two] = grads[i, block(y, x), :two] + a1_in[i, y].astype(F32)
        grads[i, block(y, x), two:] = grads[i, block(y, x), two:] + b1_in[i, x].astype(F32)

    def third_step(i):
        a2(i).wait_recv()
        b2(i).wait_recv()
        grads[i, block(y, x), :two] = grads[i, block(y, x), :two] + a2_in[i].astype(F32)
        grads[i, block(y, x), two:] = grads[i, block(y, x), two:] + b2_in[i].astype(F32)
        if i < 3:
            z_out[i + 1] = grads[i, block(y, x), :].astype(BF16)
            to_z(i + 1).start()

    fetch_std.wait()
    sums[...] = jnp.zeros_like(sums)
    sums[1:2] = next_grad
    sums[2:3] = later_grad[...]
    swap.wait_recv()

    def home(i, totals):
        rows = pl.ds(pl.multiple_of(i * step, step), step)
        grad = dot_nt(dj[rows], weight[...]) + half_in[rows].astype(F32)
        standard = std[rows]
        full = base[rows] + norm_back(grad, standard, gains[1:2], inverse[rows])
        hide = masked[rows] > 0.0
        ready[rows] = jnp.where(hide, 0.0, full).astype(BF16)
        return (
            totals[0] + jnp.sum(grad * standard, axis=0, keepdims=True),
            totals[1] + jnp.sum(jnp.where(hide, full, 0.0), axis=0, keepdims=True),
        )

    gain_grad, embed_grad = lax.fori_loop(0, 2, home, (zero, zero))
    sums[0:1] = gain_grad
    sums[3:4] = embed_grad

    def columns(s):
        return pl.ds(pl.multiple_of(s * BLK, BLK), BLK)

    def stays(k):
        return jnp.logical_and(z == k, z // 2 == c)

    def ride(k):
        slot = 2 * (z % 2) + c
        return remote(ready.at[:, columns(k)], rows_in.at[slot], r_send.at[k], r_recv.at[slot], (y, x, z // 2, k))

    def ride_local(k):
        return pltpu.make_async_copy(ready.at[:, columns(k)], rows_in.at[2 * (z % 2) + c], local.at[3])

    for k in range(4):
        pl.when(stays(k))(lambda k=k: ride_local(k).start())
        pl.when(jnp.logical_not(stays(k)))(lambda k=k: ride(k).start())
    time_step(1)
    go[...] = dot_nn(turned[...], mixed[...]).astype(BF16)
    lax.fori_loop(0, 4, piece, 0)

    def share(h):
        peer = (pair, near_y, near_x)[h]
        return remote(sum_out.at[h], sum_in.at[h], s_send.at[h], s_recv.at[h], peer)

    def begin_share(h):
        sum_out[h] = sums[...]
        share(h).start()

    def end_share(h):
        share(h).wait_recv()
        sums[...] = sums[...] + sum_in[h]

    begin_share(0)
    second(0)
    send_first(2)
    time_step(2)
    second(1)
    send_first(3)
    third_step(0)
    end_share(0)
    begin_share(1)
    second(2)
    third_step(1)
    end_share(1)
    begin_share(2)
    second(3)
    third_step(2)
    end_share(2)
    sum_out[3] = sums[...]

    def deal(r):
        s = (z + r) % 4
        return remote(sum_out.at[3, :, columns(s)], share_in.at[r], p_send.at[r], p_recv.at[r], (y, x, c, s))

    for r in (1, 2, 3):
        deal(r).start()
    third_step(3)
    parity = BLK // 2

    time_step(3)
    ty_out[...] = t_total[1 - y].astype(BF16)
    swap_y = remote(ty_out, ty_in, ty_send.at[0], ty_recv.at[0], near_y)
    swap_y.start()
    feed_step(3)
    fc_out[0] = f_other[at(1 - c, parity)].astype(BF16)
    fc_out[1] = f_total[at(1 - c, parity)].astype(BF16)
    swap_feed = remote(fc_out, fc_in, c_send.at[1], c_recv.at[1], pair)
    swap_feed.start()
    units = f_total.shape[1]
    feed_in_out[:, at(c, units)] = f_other[at(c, parity)]
    feed_out_out[at(c, units)] = f_total[at(c, parity)].T
    swap_y.wait_recv()
    tc_out[0] = t_total[y, at(1 - c, parity)].astype(BF16)
    tc_out[1] = ty_in[at(1 - c, parity)]
    swap_time = remote(tc_out, tc_in, c_send.at[2], c_recv.at[2], pair)
    swap_time.start()
    for k in range(4):
        pl.when(stays(k))(lambda k=k: ride_local(k).wait())
        from_self = jnp.logical_and(2 * c + k // 2 == z, c == k % 2)

        def landed(k=k):
            remote(ready.at[:, columns(k)], rows_in.at[k], r_send.at[k], r_recv.at[k], near_y).wait_recv()

        pl.when(jnp.logical_not(from_self))(landed)
    rows_out[...] = rows_in[...].astype(F32)
    for r in (1, 2, 3):
        to_z(r).wait_recv()
    total = grads[3, block(y, x), :]
    for r in (1, 2, 3):
        total = total + z_in[r].astype(F32)
    grads[3, block(y, x), :] = total
    rows = BLK // 2

    def core_rows(core):
        return pl.ds(pl.multiple_of(BLK * (2 * y + x) + rows * core, rows), rows)

    core_out[...] = grads[3, core_rows(1 - c), :].astype(BF16)
    last = remote(core_out, core_in, c_send.at[0], c_recv.at[0], pair)
    last.start()
    def place(core, value):
        for j in range(3):
            space_qkv[j, :, at(core, third)] = value[:, j * third : (j + 1) * third]
        space_out[at(core, third)] = value[:, 3 * third :].T

    place(c, grads[3, core_rows(c), :])
    result = sums[:, columns(z)]
    for r in (1, 2, 3):
        deal(r).wait_recv()
        result = result + share_in[r]
    gains_out[...] = result[:3]
    embed_out[...] = result[3:4]
    swap_feed.wait_recv()
    feed_in_out[:, at(1 - c, units)] = fc_in[0].astype(F32)
    feed_out_out[at(1 - c, units)] = fc_in[1].astype(F32).T
    swap_time.wait_recv()
    mine = (t_total[y, at(c, parity)], ty_in[at(c, parity)].astype(F32))
    other = (tc_in[0].astype(F32), tc_in[1].astype(F32))
    by_head = []
    for yb in range(2):
        for cb in range(2):
            by_head.append(
                jnp.where(
                    c == cb,
                    jnp.where(y == yb, mine[0], mine[1]),
                    jnp.where(y == yb, other[0], other[1]),
                )
            )
    for j in range(4):
        made = jnp.concatenate([v[:, j * HEAD_DIM : (j + 1) * HEAD_DIM] for v in by_head], axis=1)
        if j < 3:
            time_qkv[j] = made
        else:
            time_out[...] = made.T
    last.wait_recv()
    place(1 - c, core_in[...].astype(F32))

    for copy in (last, swap, give, swap_y, swap_feed, swap_time):
        copy.wait_send()
    for yb in range(2):
        time_x(yb).wait_send()
    for r in range(4):
        feed_y(r).wait_send()
    for t in range(3):
        time_z(t).wait_send()
        feed_z(t).wait_send()
    for i in range(4):
        for copy in (a1(i), b1(i), a2(i), b2(i)):
            copy.wait_send()
    for r in (1, 2, 3):
        to_z(r).wait_send()
        deal(r).wait_send()
    for h in range(3):
        share(h).wait_send()
    for k in range(4):
        pl.when(jnp.logical_not(stays(k)))(lambda k=k: ride(k).wait_send())


def leave(
    part, std_next, grad, w_out, joined, mixed, lhs, weight, std, g_time, g_out, g_in,
    totals, inverse_next, inverse, masked, gains, later_grad, scale,
):
    own, features = std.shape
    cols4 = mixed.shape[1]
    quarter = cols4 // 4
    units = g_in.shape[1]
    dma = pltpu.SemaphoreType.DMA
    anywhere = pl.BlockSpec(memory_space=pl.ANY)
    whole = pl.BlockSpec(memory_space=pltpu.VMEM)
    parity = BLK // 2

    def low(*shape):
        return pltpu.VMEM(shape, BF16)

    def high(*shape):
        return pltpu.VMEM(shape, F32)

    return pl.pallas_call(
        functools.partial(leave_kernel, scale),
        in_specs=[anywhere] * 12 + [whole] * 6,
        out_specs=[whole] * 9,
        out_shape=[
            jax.ShapeDtypeStruct(shape, F32)
            for shape in (
                (3, parity, 2 * quarter), (2 * quarter, parity), (parity, 2 * units), (2 * units, parity),
                (3, parity, BLK), (BLK, parity), (4, own, BLK), (3, BLK), (1, BLK),
            )
        ],
        scratch_shapes=[
            low(4, own, BLK),
            high(own, features), high(own, features), high(own, features), low(*w_out.shape), low(*joined.shape),
            low(*mixed.shape), low(*lhs.shape), low(*weight.shape), low(2 * own, features), low(features, 2 * own),
            low(*mixed.shape), low(features, cols4),
            low(2, BLK, features), low(2, BLK, features), low(4, 2, BLK, BLK), low(4, 2, BLK, BLK), high(2, BLK, BLK),
            low(BLK, BLK), low(BLK, BLK), low(2, parity, BLK), low(2, parity, BLK),
            low(4, BLK, units), low(4, BLK, units), low(4, BLK, units), low(4, BLK, units),
            high(BLK, units), high(BLK, units), low(2, parity, units), low(2, parity, units),
            high(4, features, cols4),
            low(4, 2, BLK, 2 * quarter), low(4, 2, BLK, 2 * quarter), low(4, 2, BLK, 2 * quarter), low(4, 2, BLK, 2 * quarter),
            low(4, BLK, 2 * quarter), low(4, BLK, 2 * quarter), low(4, BLK, 2 * quarter), low(4, BLK, 2 * quarter),
            low(4, BLK, cols4), low(4, BLK, cols4),
            low(own, features), low(own, features), low(own, features),
            low(parity, cols4), low(parity, cols4),
            high(8, features), high(4, 8, features), high(3, 8, features), high(4, 8, BLK),
        ]
        + [dma((4,))] * 10
        + [dma((1,)), dma((1,)), dma((4,)), dma((4,)), dma((3,)), dma((3,)), dma((3,)), dma((3,)), dma((4,)), dma((4,)), dma((4,))]
        + [dma((1,)), dma((1,)), dma((2,)), dma((2,)), dma((4,)), dma((4,)), dma((1,)), dma((1,))]
        + [dma((4,)), dma((4,)), dma((4,)), dma((4,)), dma((2,)), dma((4,)), dma((10,))],
        compiler_params=pltpu.CompilerParams(
            collective_id=3, has_side_effects=True, vmem_limit_bytes=62 * 1024 * 1024
        ),
        cost_estimate=pl.CostEstimate(flops=2 * 10**10, transcendentals=10**6, bytes_accessed=10**8),
        name="leave",
    )(
        part, std_next, grad, w_out, joined, mixed, lhs, weight, std, g_time, g_out, g_in,
        totals, inverse_next, inverse, masked, gains, later_grad,
    )


def tie(*values):
    return lax.optimization_barrier(values)


def norm_rows(resid):
    mean = jnp.mean(resid, axis=-1, keepdims=True)
    centered = resid - mean
    inverse = lax.rsqrt(jnp.mean(centered * centered, axis=-1, keepdims=True) + eps_norm)
    return (centered * inverse, inverse)


def norm_rows_back(grad, standardized, inverse, gain):
    gain_grad = jnp.sum(grad * standardized, axis=0)
    inner = grad * gain
    mean = jnp.mean(inner, axis=-1, keepdims=True)
    along = jnp.mean(inner * standardized, axis=-1, keepdims=True)
    return ((inner - mean - standardized * along) * inverse, gain_grad)


def cols(parts):
    return jnp.concatenate(parts, axis=1)


def rows_of(parts):
    return jnp.concatenate(parts, axis=0)


def token_parallel(
    tokens,
    cotangent,
    ratio,
    priority,
    frame_order,
    mask_embed,
    gains,
    qkv_space,
    out_space,
    qkv_time,
    out_time,
    w_in,
    w_out,
):
    scale = 1.0 / math.sqrt(HEAD_DIM)
    y, x, c, z = (lax.axis_index(name) for name in AXES)
    patches = tokens.shape[2]
    width = qkv_space.shape[0]
    frames_own = tokens.shape[0] * tokens.shape[1] // 4
    frames_all = frame_order.shape[1]
    own = frames_own * patches
    hidden_own = w_in.shape[1] // 2
    plane = 2 * y + x
    k_own = 2 * (z % 2) + c

    masked_here = (priority < ratio[:, None, None]).astype(jnp.int32).reshape(2, -1)
    info = cols([masked_here, frame_order])
    info = jnp.where(z // 2 == c, info, hop_c(info))
    info = lax.dynamic_index_in_dim(info, z % 2, 0, keepdims=False)
    masked = lax.dynamic_slice_in_dim(info, c * own, own, 0)[:, None] != 0
    order = info[2 * own :].reshape(2, 2, frames_own)
    order = jnp.where(y == 1, order[::-1], order)
    order = jnp.where(c == 1, order[:, ::-1], order).swapaxes(0, 1).reshape(frames_all)
    order = jnp.repeat(order, GROUP)
    patch = jnp.arange(frames_all * GROUP) % GROUP
    visible = (order[:, None] <= order[None, :]) & (patch[:, None] == patch[None, :])
    bias = jnp.where(visible, 0.0, -1e30).astype(F32)

    vectors = rows_of([mask_embed[None], gains, jnp.zeros((4, BLK), BF16)])
    (
        ws_qkv, ws_out, wt_all, wf_out, wf_in, joined0, turned0, std0,
        mixed0, total0, inv0, resid1, std1, inv1, normed1, vectors,
    ) = enter(
        tokens.reshape(4, own, BLK),
        vectors,
        jnp.swapaxes(qkv_space, 0, 1),
        out_space,
        jnp.swapaxes(qkv_time, 0, 1),
        out_time,
        w_out,
        w_in,
        masked.astype(F32),
        scale,
    )

    half = qkv_space.shape[2] // 2
    turned1, joined1, mixed1, total1, delta, upstream, wf_far, wf_in_far = time_call(
        False,
        normed1.reshape(frames_own, patches, width),
        cotangent.reshape(4, own, BLK),
        [wf_out, wf_in],
        wt_all,
        bias,
        scale,
    )
    w_in_half, w_out_half, grad2, grad2_low, block_rows, gain_grad2 = feed(
        resid1, delta.reshape(own, width), upstream, masked.astype(F32), vectors, wf_in, wf_in_far, wf_out, wf_far
    )

    part1, g_time, g_w_in, block_out = time_call(
        True,
        grad2_low.reshape(frames_own, patches, width),
        block_rows,
        [joined1, total1, w_in_half, turned1, mixed1],
        wt_all,
        bias,
        scale,
    )
    block_out = block_out.reshape(tokens.shape)
    grad_qkv_space, grad_out_space, grad_w_in, grad_w_out, grad_qkv_time, grad_out_time, grad_tokens, grad_gains, grad_embed = leave(
        part1.reshape(own, width), std1, grad2, ws_out, joined0, mixed0, turned0, ws_qkv, std0, g_time, w_out_half, g_w_in,
        total0, inv1, inv0, masked.astype(F32), vectors, gain_grad2, scale,
    )
    return (
        block_out,
        grad_tokens.reshape(tokens.shape),
        grad_embed.reshape(BLK),
        grad_gains,
        jnp.swapaxes(grad_qkv_space, 0, 1),
        grad_out_space,
        jnp.swapaxes(grad_qkv_time, 0, 1),
        grad_out_time,
        grad_w_in,
        grad_w_out,
    )


def solution(mesh):
    sizes = (mesh.shape["tm"], mesh.shape["clip"], mesh.shape["mp"])
    if sizes == (2, 4, 4):
        mesh = jax.sharding.Mesh(mesh.devices.reshape(2, 2, 2, 4), AXES)
        step, clip = token_parallel, ("x", "c")
    else:
        step, clip = shards, ("clip",)
    return jax.shard_map(
        step,
        mesh=mesh,
        in_specs=(
            P(clip, "tm", None, "mp"),
            P(clip, "tm", None, "mp"),
            P(clip),
            P(clip, "tm", None),
            P(clip, None),
            P("mp"),
            P(None, "mp"),
            P(None, None, "mp"),
            P("mp", None),
            P(None, None, "mp"),
            P("mp", None),
            P(None, "mp"),
            P("mp", None),
        ),
        out_specs=(
            P(clip, "tm", None, "mp"),
            P(clip, "tm", None, "mp"),
            P("mp"),
            P(None, "mp"),
            P(("tm",) + clip, None, "mp"),
            P("mp", ("tm",) + clip),
            P(("tm",) + clip, None, "mp"),
            P("mp", ("tm",) + clip),
            P(("tm",) + clip, "mp"),
            P("mp", ("tm",) + clip),
        ),
        check_vma=False,
    )
```

```python
import functools
import math

import jax
import jax.numpy as jnp
from jax import lax
from jax.experimental import pallas as pl
from jax.experimental.pallas import tpu as pltpu
from jax.sharding import PartitionSpec as P

HEAD_DIM = 64
MICRO = 2


eps_norm = 1e-05


def gelu_tanh(values):
    return jax.nn.gelu(values, approximate=True)


def norm_forward_pass(residual_stream, gain_coefficients, complete_width):
    reduced_totals = lax.psum(
        (jnp.sum(residual_stream, axis=-1), jnp.sum(residual_stream * residual_stream, axis=-1)),
        "mp",
    )
    centered_rows = reduced_totals[0] / complete_width
    spread = reduced_totals[1] / complete_width - centered_rows * centered_rows
    inverse_scale = lax.rsqrt(spread + eps_norm)
    standardized_rows = (residual_stream - centered_rows[:, None]) * inverse_scale[:, None]
    shard_rows = (standardized_rows * gain_coefficients).astype(jnp.bfloat16)
    normalized_rows = lax.all_gather(shard_rows, "mp", axis=1, tiled=True)
    return (normalized_rows, standardized_rows, inverse_scale)


def norm_reverse_pass(
    normalized_gradient, standardized_rows, inverse_scale, gain_coefficients, complete_width
):
    gain_gradient = jnp.sum(normalized_gradient * standardized_rows, axis=0)
    standardized_gradient = normalized_gradient * gain_coefficients
    reduced_totals = lax.psum(
        (
            jnp.sum(standardized_gradient, axis=-1),
            jnp.sum(standardized_gradient * standardized_rows, axis=-1),
        ),
        "mp",
    )
    grad_resid = (
        standardized_gradient
        - reduced_totals[0][:, None] / complete_width
        - standardized_rows * (reduced_totals[1][:, None] / complete_width)
    ) * inverse_scale[:, None]
    return (grad_resid, gain_gradient)


def sum_features(grad_full):
    return lax.psum_scatter(
        grad_full.astype(jnp.bfloat16), "mp", scatter_dimension=1, tiled=True
    ).astype(jnp.float32)


def branch_out(hidden, weight):
    partial_rows = jnp.dot(hidden, weight, preferred_element_type=jnp.float32)
    return lax.psum_scatter(partial_rows, "mp", scatter_dimension=1, tiled=True)


def branch_back(grad_resid, hidden, weight):
    grad_rows = lax.all_gather(grad_resid.astype(jnp.bfloat16), "mp", axis=1, tiled=True)
    weight_grad = jnp.einsum("rk,rd->kd", hidden, grad_rows, preferred_element_type=jnp.float32)
    grad_hidden = jnp.einsum("rd,kd->rk", grad_rows, weight, preferred_element_type=jnp.float32)
    return (grad_hidden, weight_grad)


def qkv_back(normalized_rows, grad_joined, weight):
    weight_grad = jnp.einsum(
        "rd,trk->dtk", normalized_rows, grad_joined, preferred_element_type=jnp.float32
    )
    grad_full = jnp.einsum("trk,dtk->rd", grad_joined, weight, preferred_element_type=jnp.float32)
    return (weight_grad, sum_features(grad_full))


def reduce_grads(local_grads, small_grads):
    reduced = (
        lax.psum_scatter(local_grads[0], ("tm", "clip"), scatter_dimension=0, tiled=True),
        lax.psum_scatter(local_grads[1], ("tm", "clip"), scatter_dimension=1, tiled=True),
        lax.psum_scatter(local_grads[2], ("tm", "clip"), scatter_dimension=0, tiled=True),
        lax.psum_scatter(local_grads[3], ("tm", "clip"), scatter_dimension=1, tiled=True),
        lax.psum_scatter(local_grads[4], ("tm", "clip"), scatter_dimension=0, tiled=True),
        lax.psum_scatter(local_grads[5], ("tm", "clip"), scatter_dimension=1, tiled=True),
    )
    reduced_small = lax.psum((small_grads[0], small_grads[1]), ("tm", "clip"))
    return (reduced, reduced_small)


def space_forward(normalized_rows, weight, frame_count, patches, heads_local, scale):
    joined = jnp.einsum(
        "rd,dtk->trk", normalized_rows, weight, preferred_element_type=jnp.float32
    ).astype(jnp.bfloat16)
    shape_heads = (frame_count, patches, heads_local, HEAD_DIM)
    scores = (
        jnp.einsum(
            "bshd,bthd->bhst",
            joined[0].reshape(shape_heads),
            joined[1].reshape(shape_heads),
            preferred_element_type=jnp.float32,
        )
        * scale
    )
    highest = jnp.max(scores, axis=-1, keepdims=True)
    exponent = jnp.exp(scores - highest)
    reduced_totals = jnp.sum(exponent, axis=-1, keepdims=True)
    log_total = highest + jnp.log(reduced_totals)
    attention = (exponent / reduced_totals).astype(jnp.bfloat16)
    mixed = jnp.einsum(
        "bhst,bthd->bshd",
        attention,
        joined[2].reshape(shape_heads),
        preferred_element_type=jnp.float32,
    )
    return (
        joined,
        log_total,
        mixed.astype(jnp.bfloat16).reshape(frame_count * patches, heads_local * HEAD_DIM),
    )


def space_backward(grad_mixed, joined, log_total, frame_count, patches, heads_local, scale):
    shape_heads = (frame_count, patches, heads_local, HEAD_DIM)
    queries = joined[0].reshape(shape_heads)
    key_rows = joined[1].reshape(shape_heads)
    values = joined[2].reshape(shape_heads)
    grad_out = grad_mixed.reshape(shape_heads)
    scores = (
        jnp.einsum("bshd,bthd->bhst", queries, key_rows, preferred_element_type=jnp.float32) * scale
    )
    attention = jnp.exp(scores - log_total)
    grad_values = jnp.einsum(
        "bhst,bshd->bthd",
        attention.astype(jnp.bfloat16),
        grad_out,
        preferred_element_type=jnp.float32,
    )
    grad_att = jnp.einsum("bshd,bthd->bhst", grad_out, values, preferred_element_type=jnp.float32)
    grad_scores = (
        attention * (grad_att - jnp.sum(attention * grad_att, axis=-1, keepdims=True))
    ).astype(jnp.bfloat16)
    grad_queries = (
        jnp.einsum("bhst,bthd->bshd", grad_scores, key_rows, preferred_element_type=jnp.float32)
        * scale
    )
    grad_keys = (
        jnp.einsum("bhst,bshd->bthd", grad_scores, queries, preferred_element_type=jnp.float32)
        * scale
    )
    row_count = frame_count * patches
    stacked = jnp.stack(
        [
            grad_queries.reshape(row_count, -1),
            grad_keys.reshape(row_count, -1),
            grad_values.reshape(row_count, -1),
        ]
    )
    return stacked.astype(jnp.bfloat16)


def time_scores(queries, keys_all, visible, scale):
    scores = (
        jnp.einsum("cfshd,cgshd->chfgs", queries, keys_all, preferred_element_type=jnp.float32)
        * scale
    )
    return jnp.where(visible, scores, -1e30)


def time_forward(queries, keys_all, values_all, visible, scale):
    scores = time_scores(queries, keys_all, visible, scale)
    highest = jnp.max(scores, axis=3, keepdims=True)
    exponent = jnp.exp(scores - highest)
    reduced_totals = jnp.sum(exponent, axis=3, keepdims=True)
    log_total = highest + jnp.log(reduced_totals)
    attention = (exponent / reduced_totals).astype(jnp.bfloat16)
    mixed = jnp.einsum(
        "chfgs,cgshd->cfshd", attention, values_all, preferred_element_type=jnp.float32
    )
    return (log_total, mixed.astype(jnp.bfloat16))


def time_backward(grad_mixed, queries, keys_all, values_all, visible, log_total, scale):
    grad_out = grad_mixed.reshape(queries.shape)
    scores = time_scores(queries, keys_all, visible, scale)
    attention = jnp.exp(scores - log_total)
    grad_values = jnp.einsum(
        "chfgs,cfshd->cgshd",
        attention.astype(jnp.bfloat16),
        grad_out,
        preferred_element_type=jnp.float32,
    )
    grad_att = jnp.einsum(
        "cfshd,cgshd->chfgs", grad_out, values_all, preferred_element_type=jnp.float32
    )
    grad_scores = (
        attention * (grad_att - jnp.sum(attention * grad_att, axis=3, keepdims=True))
    ).astype(jnp.bfloat16)
    grad_queries = (
        jnp.einsum("chfgs,cgshd->cfshd", grad_scores, keys_all, preferred_element_type=jnp.float32)
        * scale
    )
    grad_keys = (
        jnp.einsum("chfgs,cfshd->cgshd", grad_scores, queries, preferred_element_type=jnp.float32)
        * scale
    )
    return (grad_queries, grad_keys, grad_values)


def shards(
    tokens,
    cotangent,
    ratio,
    priority,
    frame_order,
    mask_embed,
    gains,
    qkv_space,
    out_space,
    qkv_time,
    out_time,
    w_in,
    w_out,
):
    scale = 1.0 / math.sqrt(HEAD_DIM)
    clips_local = tokens.shape[0] // MICRO
    frames_local = tokens.shape[1]
    patches = tokens.shape[2]
    cols_local = tokens.shape[3]
    frames_all = frame_order.shape[1]
    hidden_width = qkv_space.shape[0]
    joined_local = qkv_space.shape[2]
    heads_local = joined_local // HEAD_DIM
    row_count = clips_local * frames_local * patches
    gain_broadcast = gains.astype(jnp.float32)
    embed_row = mask_embed.astype(jnp.float32)
    first_frame = lax.axis_index("tm") * frames_local
    shape_local = (clips_local, frames_local, patches, joined_local)
    shape_heads = (clips_local, frames_local, patches, heads_local, HEAD_DIM)
    shape_all = (clips_local, frames_all, patches, heads_local, HEAD_DIM)
    outputs = []
    input_grads = []
    weight_total = None
    small_total = None
    for batch_index in range(MICRO):
        lower = batch_index * clips_local
        upper = lower + clips_local
        source = tokens[lower:upper].reshape(row_count, cols_local).astype(jnp.float32)
        upstream = cotangent[lower:upper].reshape(row_count, cols_local).astype(jnp.float32)
        masked = (priority[lower:upper] < ratio[lower:upper][:, None, None]).reshape(row_count)
        order_rows = frame_order[lower:upper]
        residual_stream0 = jnp.where(masked[:, None], embed_row[None, :], source)
        normalized_rows0, standardized_rows0, inverse_deviation0 = norm_forward_pass(
            residual_stream0, gain_broadcast[0], hidden_width
        )
        joined0, total0, mixed0 = space_forward(
            normalized_rows0, qkv_space, clips_local * frames_local, patches, heads_local, scale
        )
        residual_stream1 = residual_stream0 + branch_out(mixed0, out_space)
        normalized_rows1, standardized_rows1, inverse_deviation1 = norm_forward_pass(
            residual_stream1, gain_broadcast[1], hidden_width
        )
        joined1 = jnp.einsum(
            "rd,dtk->trk", normalized_rows1, qkv_time, preferred_element_type=jnp.float32
        ).astype(jnp.bfloat16)
        queries_local = joined1[0].reshape(shape_local)
        keys_local = joined1[1].reshape(shape_local)
        values_local = joined1[2].reshape(shape_local)
        keys_all, values_all = (
            lax.all_gather(keys_local, "tm", axis=1, tiled=True),
            lax.all_gather(values_local, "tm", axis=1, tiled=True),
        )
        query_order = lax.dynamic_slice_in_dim(order_rows, first_frame, frames_local, axis=1)
        time_visible = (order_rows[:, None, :] <= query_order[:, :, None])[:, None, :, :, None]
        time_q = queries_local.reshape(shape_heads)
        time_k = keys_all.reshape(shape_all)
        time_v = values_all.reshape(shape_all)
        total1, mixed_frames = time_forward(time_q, time_k, time_v, time_visible, scale)
        mixed1 = mixed_frames.reshape(row_count, joined_local)
        residual_stream2 = residual_stream1 + branch_out(mixed1, out_time)
        normalized_rows2, standardized_rows2, inverse_deviation2 = norm_forward_pass(
            residual_stream2, gain_broadcast[2], hidden_width
        )
        projected = jnp.dot(normalized_rows2, w_in, preferred_element_type=jnp.float32)
        activated, gelu_pull = jax.vjp(gelu_tanh, projected)
        hidden = activated.astype(jnp.bfloat16)
        resid3 = residual_stream2 + branch_out(hidden, w_out)
        outputs.append(
            resid3.astype(jnp.bfloat16).reshape(clips_local, frames_local, patches, cols_local)
        )
        grad3 = jnp.where(masked[:, None], upstream, 0.0)
        grad_hidden, grad_w_out = branch_back(grad3, hidden, w_out)
        grad_inner = gelu_pull(grad_hidden)[0].astype(jnp.bfloat16)
        grad_w_in = jnp.einsum(
            "rd,rk->dk", normalized_rows2, grad_inner, preferred_element_type=jnp.float32
        )
        normalized_gradient2 = sum_features(
            jnp.einsum("rk,dk->rd", grad_inner, w_in, preferred_element_type=jnp.float32)
        )
        backward_third, gain_gradient2 = norm_reverse_pass(
            normalized_gradient2,
            standardized_rows2,
            inverse_deviation2,
            gain_broadcast[2],
            hidden_width,
        )
        grad2 = grad3 + backward_third
        grad_mixed1, grad_out_time = branch_back(grad2, mixed1, out_time)
        grad_mixed_low = grad_mixed1.astype(jnp.bfloat16).reshape(shape_local)
        grad_queries, grad_keys, grad_values = time_backward(
            grad_mixed_low, time_q, time_k, time_v, time_visible, total1, scale
        )
        key_part, value_part = (
            lax.psum_scatter(
                grad_keys.reshape(clips_local, frames_all, patches, joined_local).astype(
                    jnp.bfloat16
                ),
                "tm",
                scatter_dimension=1,
                tiled=True,
            ).astype(jnp.float32),
            lax.psum_scatter(
                grad_values.reshape(clips_local, frames_all, patches, joined_local).astype(
                    jnp.bfloat16
                ),
                "tm",
                scatter_dimension=1,
                tiled=True,
            ).astype(jnp.float32),
        )
        grad_joined1 = jnp.stack(
            [
                grad_queries.reshape(row_count, joined_local),
                key_part.reshape(row_count, joined_local),
                value_part.reshape(row_count, joined_local),
            ]
        ).astype(jnp.bfloat16)
        grad_qkv_time, normalized_gradient1 = qkv_back(normalized_rows1, grad_joined1, qkv_time)
        backward_second, gain_gradient1 = norm_reverse_pass(
            normalized_gradient1,
            standardized_rows1,
            inverse_deviation1,
            gain_broadcast[1],
            hidden_width,
        )
        grad1 = grad2 + backward_second
        grad_mixed0, grad_out_space = branch_back(grad1, mixed0, out_space)
        grad_joined0 = space_backward(
            grad_mixed0.astype(jnp.bfloat16),
            joined0,
            total0,
            clips_local * frames_local,
            patches,
            heads_local,
            scale,
        )
        grad_qkv_space, normalized_gradient0 = qkv_back(normalized_rows0, grad_joined0, qkv_space)
        backward_first, gain_gradient0 = norm_reverse_pass(
            normalized_gradient0,
            standardized_rows0,
            inverse_deviation0,
            gain_broadcast[0],
            hidden_width,
        )
        grad0 = grad1 + backward_first
        input_grads.append(
            jnp.where(masked[:, None], 0.0, grad0).reshape(
                clips_local, frames_local, patches, cols_local
            )
        )
        grad_embed = jnp.sum(jnp.where(masked[:, None], grad0, 0.0), axis=0)
        gain_grads = jnp.stack([gain_gradient0, gain_gradient1, gain_gradient2])
        local_grads = (
            grad_qkv_space,
            grad_out_space,
            grad_qkv_time,
            grad_out_time,
            grad_w_in,
            grad_w_out,
        )
        small_grads = (gain_grads, grad_embed)
        reduced, reduced_small = reduce_grads(local_grads, small_grads)
        if weight_total is None:
            weight_total = reduced
            small_total = reduced_small
        else:
            weight_total = tuple((total + grad for total, grad in zip(weight_total, reduced)))
            small_total = tuple((total + grad for total, grad in zip(small_total, reduced_small)))
    return (
        jnp.concatenate(outputs, axis=0),
        jnp.concatenate(input_grads, axis=0),
        small_total[1],
        small_total[0],
        weight_total[0],
        weight_total[1],
        weight_total[2],
        weight_total[3],
        weight_total[4],
        weight_total[5],
    )


AXES = ("tm", "x", "c", "mp")
F32 = jnp.float32
BF16 = jnp.bfloat16
BLK = 256
MESH = pl.DeviceIdType.MESH


def device_pairs(move):
    pairs = []
    for y in range(2):
        for x in range(2):
            for c in range(2):
                for z in range(4):
                    there = move(y, x, c, z)
                    pairs.append(tuple(((q[0] * 2 + q[1]) * 2 + q[2]) * 4 + q[3] for q in ((y, x, c, z), there)))
    return pairs


def hop_y(v):
    return lax.ppermute(v, AXES, device_pairs(lambda y, x, c, z: (1 - y, x, c, z)))


def hop_x(v):
    return lax.ppermute(v, AXES, device_pairs(lambda y, x, c, z: (y, 1 - x, c, z)))


def hop_c(v):
    return lax.ppermute(v, AXES, device_pairs(lambda y, x, c, z: (y, x, 1 - c, z)))


def hop_z(v, shift):
    return lax.ppermute(v, AXES, device_pairs(lambda y, x, c, z: (y, x, c, (z + shift) % 4)))


def spread_pairs(r):
    def move(y, x, c, z):
        k = z ^ r
        return (y, x, k & 1, 2 * c + (k >> 1))

    return device_pairs(move)


def dot_nn(a, b):
    return lax.dot_general(a, b, (((1,), (0,)), ((), ())), preferred_element_type=F32)


def dot_nt(a, b):
    return lax.dot_general(a, b, (((1,), (1,)), ((), ())), preferred_element_type=F32)


def dot_tn(a, b):
    return lax.dot_general(a, b, (((0,), (0,)), ((), ())), preferred_element_type=F32)


def attend_pair(q, k, v, bias, scale):
    mixed, totals = [], []
    for i in range(2):
        mine = slice(i * HEAD_DIM, (i + 1) * HEAD_DIM)
        scores = dot_nt(k[:, mine], q[:, mine]) * scale
        if bias is not None:
            scores = scores + bias
        highest = jnp.max(scores, axis=0, keepdims=True)
        exponent = jnp.exp(scores - highest)
        total = jnp.sum(exponent, axis=0, keepdims=True)
        totals.append(highest + jnp.log(total))
        mixed.append(dot_tn(v[:, mine], exponent.astype(BF16)) * (1.0 / total))
    return (jnp.concatenate(mixed, axis=0).T, totals)


def attend_pair_back(q, k, v, g, totals, bias, scale):
    grads = ([], [], [])
    for i in range(2):
        mine = slice(i * HEAD_DIM, (i + 1) * HEAD_DIM)
        scores = dot_nt(k[:, mine], q[:, mine]) * scale
        if bias is not None:
            scores = scores + bias
        p = jnp.exp(scores - totals[i])
        dp = dot_nt(v[:, mine], g[:, mine])
        ds = (p * (dp - jnp.sum(p * dp, axis=0, keepdims=True))).astype(BF16)
        grads[0].append(dot_tn(k[:, mine], ds) * scale)
        grads[1].append(dot_nn(ds, q[:, mine]) * scale)
        grads[2].append(dot_nn(p.astype(BF16), g[:, mine]))
    return (
        jnp.concatenate(grads[0], axis=0).T,
        jnp.concatenate(grads[1], axis=1),
        jnp.concatenate(grads[2], axis=1),
    )


PAIR = 2 * HEAD_DIM


def enter_kernel(
    scale,
    tok, vec, qkv_hbm, out_hbm, time_hbm, time_out_hbm, feed_hbm, first_hbm, masked,
    wq_out, wo_out, wt, wf, wi, joined_out, turned_out, std_out,
    mixed, total_out, inverse, resid_out, next_out, inverse_next, low_out, vec_out,
    rows_in, vec_in, wq, wo, normed, joined, turned, std, base, part, part_out, part_in, resid, std_next, low_next,
    later, head_in, head_out,
    z_send, z_recv, y_send, y_recv, x_send, x_recv, p_send, p_recv, q_send, q_recv,
    t_send, t_recv, v_send, v_recv, u_send, u_recv, w_send, w_recv,
    f_send, f_recv, g_send, g_recv, n_send, n_recv, local, saved,
    i_send, i_recv, j_send, j_recv, k_send, k_recv, l_send, l_recv,
):
    y, x, c, z = (lax.axis_index(name) for name in AXES)
    half = wo.shape[0] // 4
    wide = 3 * half
    span = wt.shape[1] // 4
    size = wf.shape[1] // 4
    own = rows_in.shape[0]
    near_y, near_x, pair = (1 - y, x, c, z), (y, 1 - x, c, z), (y, x, 1 - c, z)
    right_z, left_z = (y, x, c, (z + 1) % 4), (y, x, c, (z + 3) % 4)

    def at(i, length):
        return pl.ds(pl.multiple_of(i * length, length), length)

    def remote(src, dst, send, recv, peer):
        return pltpu.make_async_remote_copy(
            src_ref=src, dst_ref=dst, send_sem=send, recv_sem=recv, device_id=peer, device_id_type=MESH
        )

    def start(all_copies):
        for copy in all_copies:
            copy.start()

    def landed(all_copies):
        for copy in all_copies:
            copy.wait_recv()

    def sent(all_copies):
        for copy in all_copies:
            copy.wait_send()

    core = at(c, half)
    keep = [
        pltpu.make_async_copy(
            qkv_hbm.at[j, :, core], wq.at[:, pl.ds(pl.multiple_of(z * wide + j * half, half), half)], local.at[j]
        )
        for j in range(3)
    ] + [pltpu.make_async_copy(out_hbm.at[core], wo.at[at(z, half)], local.at[3])]
    keep_later = [
        pltpu.make_async_copy(later, wt.at[:, at(z, span)], local.at[4]),
        pltpu.make_async_copy(feed_hbm.at[at(c, 4 * size)], wf.at[z], local.at[5]),
        pltpu.make_async_copy(first_hbm.at[:, at(c, 4 * size)], wi.at[z], local.at[8]),
    ]
    head = [
        pltpu.make_async_copy(time_hbm.at[:, :, at(y, PAIR)], head_in, local.at[9]),
        pltpu.make_async_copy(time_out_hbm.at[at(2 * y + c, HEAD_DIM)], head_out, local.at[10]),
    ]
    start(keep + keep_later[1:] + head)

    barrier = pltpu.get_barrier_semaphore()
    for dc in range(2):
        for dz in range(4):
            if dc or dz:
                peer = (y, x, (c + dc) % 2, (z + dz) % 4)
                pl.semaphore_signal(barrier, inc=1, device_id=peer, device_id_type=MESH)
    for peer in (near_y, near_x):
        pl.semaphore_signal(barrier, inc=1, device_id=peer, device_id_type=MESH)
    pl.semaphore_wait(barrier, 9)

    def spot(dy, dx):
        return 2 * ((y + dy) % 2) + (x + dx) % 2

    def piece(dy, dx, r, split=False):
        s = (z + r) % 4
        rows = at(spot(dy, dx), BLK)
        first = pl.multiple_of(s * wide, half)
        out = wo.at[at(s, half), at(spot(dy, dx), BLK)]
        if split:
            last = pl.multiple_of(s * wide + 2 * half, half)
            return (wq.at[rows, pl.ds(first, 2 * half)], wq.at[rows, pl.ds(last, half)], out)
        return (wq.at[rows, pl.ds(first, wide)], out)

    def time_piece(dx, r):
        return wt.at[at((x + dx) % 2, 2 * BLK), at((z + r) % 4, span)]

    def feed_piece(dy, r):
        return wf.at[(z + r) % 4, at(spot(dy, 0), size)]

    def copies(parts, send, recv, peer):
        return [remote(ref, ref, send.at[i], recv.at[i], peer) for i, ref in enumerate(parts)]

    def leg(right, step):
        if right:
            return (0 if step == 0 else 4 - step), right_z, 3 - step
        return step, left_z, step + 1

    def z_copies(right, step):
        r, peer, lands = leg(right, step)
        return copies(piece(0, 0, r), z_send.at[int(right), step], z_recv.at[lands], peer)

    def time_z(right, step):
        r, peer, lands = leg(right, step)
        source = later.at[at(x, 2 * BLK)] if step == 0 else time_piece(0, r)
        return [remote(source, time_piece(0, r), u_send.at[int(right), step], u_recv.at[lands], peer)]

    def feed_z(right, step):
        r, peer, lands = leg(right, step)
        source = feed_hbm.at[at(4 * c + spot(0, 0), size)] if step == 0 else feed_piece(0, r)
        return [remote(source, feed_piece(0, r), f_send.at[int(right), step], f_recv.at[lands], peer)]

    def first_piece(dy, dx, r):
        return wi.at[(z + r) % 4, at(spot(dy, dx), BLK)]

    def first_z(right, step):
        r, peer, lands = leg(right, step)
        source = first_hbm.at[at(spot(0, 0), BLK), at(c, 4 * size)] if step == 0 else first_piece(0, 0, r)
        return [remote(source, first_piece(0, 0, r), i_send.at[int(right), step], i_recv.at[lands], peer)]

    def first_y(r, dy=0):
        return [remote(first_piece(dy, 0, r), first_piece(dy, 0, r), j_send.at[r], j_recv.at[r], near_y)]

    def first_x(r, dx=0):
        return [remote(first_piece(0, dx, r), first_piece(0, dx, r), k_send.at[r], k_recv.at[r], near_x)]

    def y_copies(r, dy=0):
        return copies(piece(dy, 0, r), y_send.at[r], y_recv.at[r], near_y)

    def x_copies(r, dx=0):
        return copies(piece(0, dx, r), x_send.at[r], x_recv.at[r], near_x)

    def corner_x(r, dx=0):
        return copies(piece(1, dx, r, split=True)[:1], p_send.at[r], p_recv.at[r], near_x)

    def corner_y(r, dy=0):
        return copies(piece(dy, 1, r, split=True)[1:], q_send.at[r], q_recv.at[r], near_y)

    def time_x(r, dx=0):
        return [remote(time_piece(dx, r), time_piece(dx, r), w_send.at[r], w_recv.at[r], near_x)]

    def feed_y(r, dy=0):
        return [remote(feed_piece(dy, r), feed_piece(dy, r), g_send.at[r], g_recv.at[r], near_y)]

    def token_copies(k):
        peer = (y, x, k % 2, 2 * c + k // 2)
        return [
            remote(tok.at[k], rows_in.at[:, at(z, BLK)], t_send.at[k], t_recv.at[z], peer),
            remote(vec, vec_in.at[:, at(z, BLK)], v_send.at[k], v_recv.at[z], peer),
        ]

    def token_local(k):
        return [
            pltpu.make_async_copy(tok.at[k], rows_in.at[:, at(z, BLK)], local.at[6]),
            pltpu.make_async_copy(vec, vec_in.at[:, at(z, BLK)], local.at[7]),
        ]

    def stays(k):
        return jnp.logical_and(2 * c + k // 2 == z, c == k % 2)

    def start_tokens(ks):
        for k in ks:
            pl.when(stays(k))(lambda k=k: start(token_local(k)))
            pl.when(jnp.logical_not(stays(k)))(lambda k=k: start(token_copies(k)))

    def each_side(j, act):
        pl.when(z >= j + 1)(lambda: act(3 - j, True))
        pl.when(z <= 2 - j)(lambda: act(j + 1, False))

    def begin(make):
        pl.when(z < 3)(lambda: start(make(True, 0)))
        pl.when(z > 0)(lambda: start(make(False, 0)))

    def onward(j, make, right):
        if j < 2:
            pl.when(z < 3 if right else z > 0)(lambda: start(make(right, j + 1)))

    def forward(j):
        def act(r, right):
            landed(copies(piece(0, 0, r), z_send.at[0, 0], z_recv.at[r], near_y))
            onward(j, z_copies, right)
            start(y_copies(r))
            start(x_copies(r))

        each_side(j, act)

    def corners(j):
        def act(r, right):
            landed(y_copies(r, 1))
            start(corner_x(r))
            landed(x_copies(r, 1))
            start(corner_y(r))

        each_side(j, act)

    def time_forward_step(j):
        def act(r, right):
            landed([remote(time_piece(0, r), time_piece(0, r), u_send.at[0, 0], u_recv.at[r], near_x)])
            onward(j, time_z, right)
            start(time_x(r))

        each_side(j, act)

    def feed_forward_step(j):
        def act(r, right):
            landed([remote(feed_piece(0, r), feed_piece(0, r), f_send.at[0, 0], f_recv.at[r], near_y)])
            onward(j, feed_z, right)
            start(feed_y(r))

        each_side(j, act)

    def first_corner_copy(r, dx=0):
        return [remote(first_piece(1, dx, r), first_piece(1, dx, r), l_send.at[r], l_recv.at[r], near_x)]

    def first_corner(j):
        def act(r, right):
            landed(first_y(r, 1))
            start(first_corner_copy(r))

        each_side(j, act)

    def first_forward_step(j):
        def act(r, right):
            landed([remote(first_piece(0, 0, r), first_piece(0, 0, r), i_send.at[0, 0], i_recv.at[r], near_y)])
            onward(j, first_z, right)
            start(first_y(r))
            start(first_x(r))

        each_side(j, act)

    for copy in keep:
        copy.wait()
    begin(z_copies)

    def gather_head(i, carry):
        rows = at(i, BLK)
        parts = [head_in[j, rows].astype(F32) for j in range(3)]
        parts = [jnp.where(c == 0, v[:, :HEAD_DIM], v[:, HEAD_DIM:]) for v in parts]
        parts.append(head_out[:, rows].astype(F32).T)
        later[rows] = jnp.concatenate(parts, axis=1).astype(BF16)
        return carry

    for copy in head:
        copy.wait()
    lax.fori_loop(0, later.shape[0] // BLK, gather_head, 0)
    keep_later[0].start()
    forward(0)
    start_tokens((0, 1))
    forward(1)
    start_tokens((2, 3))
    begin(first_z)
    begin(time_z)
    begin(feed_z)
    corners(0)
    forward(2)
    corners(1)
    for k in range(4):
        def finish_local(k=k):
            for copy in token_local(k):
                copy.wait()

        pl.when(stays(k))(finish_local)
    for s in range(4):
        def arrived(s=s):
            landed([
                remote(tok.at[0], rows_in.at[:, at(s, BLK)], t_send.at[0], t_recv.at[s], near_y),
                remote(vec, vec_in.at[:, at(s, BLK)], v_send.at[0], v_recv.at[s], near_y),
            ])

        pl.when(jnp.logical_not(jnp.logical_and(z == s, z // 2 == c)))(arrived)

    step = own // 2
    slab = 128
    vec_out[...] = vec_in[...].astype(F32)

    def first_norm(i, carry):
        rows = at(i, step)
        value = jnp.where(masked[rows] > 0.0, vec_out[0:1], rows_in[rows].astype(F32))
        base[rows] = value
        standard, inv = norm_rows(value)
        std[rows] = standard
        inverse[rows] = inv
        normed[rows] = (standard * vec_out[1:2]).astype(BF16)
        return carry

    lax.fori_loop(0, 2, first_norm, 0)
    give_normed = remote(normed.at[pl.ds(0, own)], normed.at[pl.ds(own, own)], n_send.at[0], n_recv.at[0], pair)
    give_normed.start()
    corners(2)

    def turn(i, carry):
        turned[:, at(i, slab)] = normed[at(i, slab)].T
        return carry

    lax.fori_loop(0, own // slab, turn, 0)
    for r in (1, 2, 3):
        landed(corner_x(r, 1))
        landed(corner_y(r, 1))
    saves = [
        pltpu.make_async_copy(wq, wq_out, saved.at[0]),
        pltpu.make_async_copy(wo, wo_out, saved.at[1]),
        pltpu.make_async_copy(std, std_out, saved.at[2]),
    ]
    start(saves)
    first_forward_step(0)

    def attend(i, carry):
        rows = at(i, slab)
        for h in range(wo.shape[0] // PAIR):
            q, k, v = (joined[rows, (3 * h + j) * PAIR : (3 * h + j + 1) * PAIR] for j in range(3))
            out, totals = attend_pair(q, k, v, None, scale)
            mixed[rows, h * PAIR : (h + 1) * PAIR] = out.astype(BF16)
            for j in range(2):
                total_out[i, 2 * h + j : 2 * h + j + 1, :] = totals[j]
        return carry

    def project(t):
        rows = pl.ds(t * own, own)
        joined[rows] = dot_nn(normed[rows], wq[...]).astype(BF16)

    frames = own // slab
    project(0)
    time_forward_step(0)
    lax.fori_loop(0, frames, attend, 0)
    part[...] = dot_nn(mixed[pl.ds(0, own)], wo[...])
    feed_forward_step(0)
    first_forward_step(1)
    first_corner(0)
    give_normed.wait_recv()
    project(1)
    saves.append(pltpu.make_async_copy(joined, joined_out, saved.at[3]))
    saves[3].start()
    lax.fori_loop(frames, 2 * frames, attend, 0)
    part_out[...] = dot_nn(mixed[pl.ds(own, own)], wo[...]).astype(BF16)
    give_part = remote(part_out, part_in, n_send.at[1], n_recv.at[1], pair)
    give_part.start()
    time_forward_step(1)
    feed_forward_step(1)
    first_corner(1)
    lax.fori_loop(own // slab, 2 * own // slab, turn, 0)
    saves.append(pltpu.make_async_copy(turned, turned_out, saved.at[4]))
    saves[4].start()
    give_part.wait_recv()
    first_forward_step(2)

    def second_norm(i, carry):
        rows = at(i, step)
        value = base[rows] + part[rows] + part_in[rows].astype(F32)
        resid[rows] = value
        standard, inv = norm_rows(value)
        std_next[rows] = standard
        inverse_next[rows] = inv
        low_next[rows] = (standard * vec_out[2:3]).astype(BF16)
        return carry

    lax.fori_loop(0, 2, second_norm, 0)
    for i, (src, dst) in enumerate(((resid, resid_out), (std_next, next_out), (low_next, low_out))):
        saves.append(pltpu.make_async_copy(src, dst, saved.at[5 + i]))
        saves[-1].start()
    time_forward_step(2)
    feed_forward_step(2)

    def first_ends(j):
        def act(r, right):
            if j == 2:
                landed(first_y(r, 1))
            else:
                landed(first_corner_copy(r, 1))
                sent(first_corner_copy(r))

        each_side(j, act)

    for j in range(3):
        first_ends(j)
    for copy in keep_later + saves:
        copy.wait()
    give_normed.wait_send()
    give_part.wait_send()
    for r in (1, 2, 3):
        landed(time_x(r, 1))
        landed(feed_y(r, 1))
        landed(first_x(r, 1))
        for group in (y_copies(r), x_copies(r), corner_x(r), corner_y(r), time_x(r), feed_y(r), first_y(r), first_x(r)):
            sent(group)
    for step_z in range(3):
        for make in (z_copies, time_z, first_z, feed_z):
            pl.when(jnp.logical_and(z >= step_z, z < 3))(lambda step_z=step_z, make=make: sent(make(True, step_z)))
            pl.when(jnp.logical_and(z + step_z <= 3, z > 0))(lambda step_z=step_z, make=make: sent(make(False, step_z)))
    for k in range(4):
        pl.when(jnp.logical_not(stays(k)))(lambda k=k: sent(token_copies(k)))


def enter(tok, vec, qkv, out, time_qkv, time_out, feed_weight, first_weight, masked, scale):
    own, width, half = tok.shape[1], 4 * tok.shape[2], out.shape[0] // 2
    size = feed_weight.shape[0] // 2
    dma = pltpu.SemaphoreType.DMA
    anywhere = pl.BlockSpec(memory_space=pl.ANY)
    whole = pl.BlockSpec(memory_space=pltpu.VMEM)
    heads = 4 * half // HEAD_DIM

    def low(*shape):
        return pltpu.VMEM(shape, BF16)

    def high(*shape):
        return pltpu.VMEM(shape, F32)

    shapes = [
        ((width, 12 * half), BF16), ((4 * half, width), BF16), ((width, 16 * HEAD_DIM), BF16),
        ((4, size, width), BF16), ((4, width, size), BF16), ((2 * own, 12 * half), BF16), ((width, 2 * own), BF16), ((own, width), F32),
        ((2 * own, 4 * half), BF16), ((2 * own // 128, heads, 128), F32), ((own, 1), F32), ((own, width), F32),
        ((own, width), F32), ((own, 1), F32), ((own, width), BF16), ((vec.shape[0], width), F32),
    ]
    return pl.pallas_call(
        functools.partial(enter_kernel, scale),
        in_specs=[anywhere] * 8 + [whole],
        out_specs=[anywhere] * 8 + [whole] * 3 + [anywhere] * 2 + [whole, anywhere, whole],
        out_shape=[jax.ShapeDtypeStruct(shape, kind) for shape, kind in shapes],
        scratch_shapes=[
            low(own, width), low(vec.shape[0], width), low(width, 12 * half), low(4 * half, width),
            low(2 * own, width), low(2 * own, 12 * half), low(width, 2 * own), high(own, width), high(own, width),
            high(own, width), low(own, width), low(own, width), high(own, width), high(own, width), low(own, width),
            low(width, 4 * HEAD_DIM), low(3, width, PAIR), low(HEAD_DIM, width),
            dma((2, 3, 2)), dma((4, 2)), dma((4, 2)), dma((4, 2)), dma((4, 2)), dma((4, 2)),
            dma((4, 1)), dma((4, 1)), dma((4, 2)), dma((4, 2)),
            dma((4,)), dma((4,)), dma((4,)), dma((4,)), dma((2, 3)), dma((4,)), dma((4,)), dma((4,)),
            dma((2, 3)), dma((4,)), dma((4,)), dma((4,)), dma((2,)), dma((2,)), dma((11,)), dma((8,)),
            dma((2, 3)), dma((4,)), dma((4,)), dma((4,)), dma((4,)), dma((4,)), dma((4,)), dma((4,)),
        ],
        compiler_params=pltpu.CompilerParams(
            collective_id=0, has_side_effects=True, vmem_limit_bytes=56 * 1024 * 1024
        ),
        cost_estimate=pl.CostEstimate(flops=10**10, transcendentals=10**6, bytes_accessed=10**8),
        name="enter",
    )(tok, vec, qkv, out, time_qkv, time_out, feed_weight, first_weight, masked)


GROUP = 8
CHUNK = 16


def time_kernel(back, scale, heads, *refs):
    if back:
        (own_ref, rider_ref, joined_hbm, total_ref, wide_ref, turned_ref, mixed_hbm, wt_hbm, bias_ref) = refs[:9]
        (delta_ref, grad_hbm, reduced_ref, rider_out) = refs[9:13]
        (half_in, half_own, line_out, line_in, half_send, half_recv, half_local, line_send, line_recv) = refs[-18:-9]
        (out_ref, turned, grad_qkv, grad_out, wt_ref, joined_ref, mixed_ref, load_sem, grad_ref) = refs[-9:]
        refs = refs[13:-18]
        save_grad = pltpu.make_async_copy(grad_ref, grad_hbm, load_sem.at[0])
    else:
        (own_ref, rider_ref, far_ref, in_ref, wt_hbm, bias_ref) = refs[:6]
        (turned_ref, out_hbm, mixed_hbm, total_ref, delta_ref, rider_out, spread_out, in_out) = refs[6:14]
        (turned, wt_ref, out_ref, mixed_ref, load_sem, keep_sem) = refs[-6:]
        refs = refs[14:-6]
    (
        wq_ref, wo_ref, held, wide, narrow, kept, core_out, core_in, near_out, near_in,
        gy_send, gy_recv, gc_send, gc_recv, gd_send, gd_recv, sc_send, sc_recv, sy_send, sy_recv,
        r_send, r_recv, r_local, out_sem, wx_send, wx_recv,
    ) = refs
    y, x, c, z = (lax.axis_index(name) for name in AXES)
    near, pair, near_x = (1 - y, x, c, z), (y, x, 1 - c, z), (y, 1 - x, c, z)
    frames = held.shape[0] // 4
    chunks = held.shape[1] // CHUNK
    width = heads * HEAD_DIM
    groups = CHUNK // GROUP

    loads = [(wt_hbm, wt_ref), (own_ref, held.at[pl.ds(0, frames)])]
    if back:
        loads += [(joined_hbm, joined_ref), (mixed_hbm, mixed_ref)]
    loads = [pltpu.make_async_copy(src, dst, load_sem.at[i]) for i, (src, dst) in enumerate(loads)]
    for copy in loads:
        copy.start()
    barrier = pltpu.get_barrier_semaphore()
    for dc in range(2):
        for dz in range(4):
            if dc or dz:
                pl.semaphore_signal(barrier, inc=1, device_id=(y, x, (c + dc) % 2, (z + dz) % 4), device_id_type=MESH)
    pl.semaphore_signal(barrier, inc=1, device_id=near, device_id_type=MESH)
    pl.semaphore_signal(barrier, inc=1, device_id=near_x, device_id_type=MESH)
    pl.semaphore_wait(barrier, 9)

    def remote(src, dst, send, recv, peer):
        return pltpu.make_async_remote_copy(
            src_ref=src, dst_ref=dst, send_sem=send, recv_sem=recv, device_id=peer, device_id_type=MESH
        )

    def patches(k):
        return pl.ds(pl.multiple_of(k * CHUNK, CHUNK), CHUNK)

    def block(b, k):
        return held.at[pl.ds(b * frames, frames), patches(k)]

    def gather_y(k):
        return remote(own_ref.at[:, patches(k)], block(1, k), gy_send.at[k], gy_recv.at[k], near)

    def gather_c(k):
        return remote(own_ref.at[:, patches(k)], block(2, k), gc_send.at[k], gc_recv.at[k], pair)

    def gather_d(k):
        return remote(block(1, k), block(3, k), gd_send.at[k], gd_recv.at[k], pair)

    def scatter_c(k):
        return remote(core_out.at[k], core_in.at[k], sc_send.at[k], sc_recv.at[k], pair)

    def scatter_y(k):
        return remote(near_out.at[k], near_in.at[k], sy_send.at[k], sy_recv.at[k], near)

    def save_results(k):
        return [
            pltpu.make_async_copy(src.at[:, patches(k)], dst.at[:, patches(k)], keep_sem.at[i, k])
            for i, (src, dst) in enumerate(((out_ref, out_hbm), (mixed_ref, mixed_hbm)))
        ]

    def save(k):
        there = (turned_ref.at[k], turned.at[k]) if back else (turned.at[k], turned_ref.at[k])
        return pltpu.make_async_copy(*there, out_sem.at[k])

    def columns(s):
        return pl.ds(pl.multiple_of(s * BLK, BLK), BLK)

    def stays(k):
        if back:
            return jnp.logical_and(z == k, z // 2 == c)
        return jnp.logical_and(2 * c + k // 2 == z, c == k % 2)

    def ride(k):
        if back:
            src, dst = rider_ref.at[:, columns(k)], rider_out.at[2 * (z % 2) + c]
            peer, slot = (y, x, z // 2, k), 2 * (z % 2) + c
        else:
            src, dst = rider_ref.at[k], rider_out.at[:, columns(z)]
            peer, slot = (y, x, k % 2, 2 * c + k // 2), z
        return src, dst, peer, slot

    def ride_remote(k):
        src, dst, peer, slot = ride(k)
        return remote(src, dst, r_send.at[k], r_recv.at[slot], peer)

    def ride_local(k):
        src, dst, _, _ = ride(k)
        return pltpu.make_async_copy(src, dst, r_local.at[0])

    def ride_landed(k):
        if back:
            src, dst = rider_ref.at[:, columns(k)], rider_out.at[k]
        else:
            src, dst = rider_ref.at[k], rider_out.at[:, columns(k)]
        return remote(src, dst, r_send.at[k], r_recv.at[k], near)

    def from_self(k):
        if back:
            return jnp.logical_and(2 * c + k // 2 == z, c == k % 2)
        return jnp.logical_and(z == k, z // 2 == c)

    def spread_x(i, dx=0):
        r, yb = i // 2 + 1, i % 2
        size = far_ref.shape[1] // 4
        at = pl.multiple_of(size * (2 * yb + (x + dx) % 2), size)
        src = far_ref.at[(z + r) % 4, pl.ds(at, size)]
        return remote(src, spread_out.at[(z + r) % 4, pl.ds(at, size)], wx_send.at[i], wx_recv.at[i], near_x)

    gather_y(0).start()
    for k in range(chunks):
        if k > 0:
            gather_y(k).start()
        gather_c(k).start()
    def spread_in(dx=0):
        at = pl.multiple_of(BLK * (2 * (1 - y) + (x + dx) % 2), BLK)
        there = in_out.at[3 - z, pl.ds(at, BLK)]
        return remote(in_ref.at[3 - z, pl.ds(at, BLK)], there, wx_send.at[6], wx_recv.at[6], near_x)

    at_end = jnp.logical_or(z == 0, z == 3)

    def half_away(s):
        return remote(wide_ref.at[1 - x, s], half_in.at[s], half_send.at[s], half_recv.at[s], near_x)

    def half_here(s):
        return pltpu.make_async_copy(wide_ref.at[x, s], half_own.at[s], half_local.at[s])

    def line_away(r):
        return remote(line_out.at[r], line_in.at[r], line_send.at[r], line_recv.at[r], (y, x, c, (z + r) % 4))

    def halve():
        for s in range(4):
            half_away(s).wait_recv()
            half_here(s).wait()
        for r in range(4):
            s = (z + r) % 4
            whole = half_own[s].astype(F32) + half_in[s].astype(F32)
            if r == 0:
                reduced_ref[...] = whole
            else:
                line_out[r] = whole.astype(BF16)
                line_away(r).start()

    if back:
        for s in range(4):
            half_away(s).start()
            half_here(s).start()
    else:
        pl.when(at_end)(lambda: spread_in().start())
        for i in range(6):
            spread_x(i).start()
    for k in range(4):
        pl.when(stays(k))(lambda k=k: ride_local(k).start())
        pl.when(jnp.logical_not(stays(k)))(lambda k=k: ride_remote(k).start())
    if back:
        for k in range(chunks):
            save(k).start()

    def assemble(i, carry):
        rows = pl.ds(pl.multiple_of(i * BLK, BLK), BLK)
        for s in range(0, heads, 2):
            for part in range(4):
                both = [
                    wt_ref[rows, (s + j) * 4 * HEAD_DIM + part * HEAD_DIM : (s + j) * 4 * HEAD_DIM + (part + 1) * HEAD_DIM]
                    for j in range(2)
                ]
                both = jnp.concatenate(both, axis=1)
                if part < 3:
                    wq_ref[rows, part * width + s * HEAD_DIM : part * width + s * HEAD_DIM + PAIR] = both
                else:
                    wo_ref[rows, s * HEAD_DIM : s * HEAD_DIM + PAIR] = both
        return carry

    loads[0].wait()
    lax.fori_loop(0, wt_ref.shape[0] // BLK, assemble, 0)
    for copy in loads[1:]:
        copy.wait()

    def finish(k):
        scatter_c(k).wait_recv()
        both = kept[:, patches(k)] + core_in[k].astype(F32)
        near_out[k] = both[frames:].astype(BF16)
        delta_ref[:, patches(k)] = both[:frames]
        scatter_y(k).start()

    def pass_on(k):
        gather_y(k).wait_recv()
        gather_d(k).start()

    def one_group(i, rows):
        at = pl.ds(pl.multiple_of(i * GROUP, GROUP), GROUP)
        count = 4 * frames * GROUP
        bias = bias_ref[...]
        for lo in range(0, width, PAIR):
            q, k, v = (
                wide[:, at, part * width + lo : part * width + lo + PAIR].reshape(count, PAIR).astype(BF16)
                for part in range(3)
            )
            h = lo // HEAD_DIM
            if back:
                g = narrow[:, at, lo : lo + PAIR].reshape(count, PAIR).astype(BF16)
                totals = [total_ref[rows * groups + i, h + j : h + j + 1, :] for j in range(2)]
                grads = attend_pair_back(q, k, v, g, totals, bias, scale)
                for part in range(3):
                    wide[:, at, part * width + lo : part * width + lo + PAIR] = grads[part].reshape(
                        4 * frames, GROUP, PAIR
                    )
            else:
                mixed, totals = attend_pair(q, k, v, bias, scale)
                narrow[:, at, lo : lo + PAIR] = mixed.reshape(4 * frames, GROUP, PAIR)
                for j in range(2):
                    total_ref[rows * groups + i, h + j : h + j + 1, :] = totals[j]

    def one_chunk(k, carry):
        pl.when(k + 1 < chunks)(lambda: pass_on(k + 1))
        gather_c(k).wait_recv()
        gather_d(k).wait_recv()
        count = 4 * frames * CHUNK
        lhs = held[:, patches(k)].reshape(count, held.shape[2])
        if back:
            wide[...] = joined_ref[:, patches(k)].astype(F32)
            narrow[...] = dot_nn(lhs, wo_ref[...]).astype(BF16).astype(F32).reshape(narrow.shape)
        else:
            joined = dot_nn(lhs, wq_ref[...]).astype(BF16)
            out_ref[:, patches(k)] = joined.reshape(wide.shape)
            wide[...] = joined.astype(F32).reshape(wide.shape)
        lax.fori_loop(0, groups, lambda i, carry: (one_group(i, k), carry)[1], 0)
        if back:
            grads = wide[...].astype(BF16)
            out_ref[:, patches(k)] = grads
            partial = dot_nt(grads.reshape(count, 3 * width), wq_ref[...])
        else:
            mixed = narrow[...].astype(BF16)
            mixed_ref[:, patches(k)] = mixed
            partial = dot_nt(mixed.reshape(count, width), wo_ref[...])
        partial = partial.reshape(4 * frames, CHUNK, held.shape[2])
        kept[:, patches(k)] = partial[: 2 * frames]
        core_out[k] = partial[2 * frames :].astype(BF16)
        scatter_c(k).start()
        pl.when(k > 0)(lambda: finish(k - 1))
        if not back:
            for b in range(4):
                slab = held[b * frames : (b + 1) * frames, patches(k)].reshape(frames * CHUNK, held.shape[2])
                turned[k, :, b * frames * CHUNK : (b + 1) * frames * CHUNK] = slab.T
            save(k).start()
            for copy in save_results(k):
                copy.start()
        if back:
            pl.when(k == chunks // 2 - 1)(halve)
        return carry

    pass_on(0)
    lax.fori_loop(0, chunks, one_chunk, 0)
    finish(chunks - 1)

    def weigh(k, carry):
        count = 4 * frames * CHUNK
        save(k).wait()
        grad_qkv[...] = grad_qkv[...] + dot_nn(turned[k], out_ref[:, patches(k)].reshape(count, 3 * width))
        grad_out[...] = grad_out[...] + dot_tn(
            mixed_ref[:, patches(k)].reshape(count, width), held[:, patches(k)].reshape(count, held.shape[2])
        )
        return carry

    def arrange(i, carry):
        rows = pl.ds(pl.multiple_of(i * BLK, BLK), BLK)
        last = grad_out[:, rows].T
        for s in range(heads):
            mine = slice(s * HEAD_DIM, (s + 1) * HEAD_DIM)
            parts = [grad_qkv[rows, j * width : (j + 1) * width][:, mine] for j in range(3)] + [last[:, mine]]
            grad_ref[rows, 2 * s * PAIR : (2 * s + 1) * PAIR] = jnp.concatenate(parts[:2], axis=1).astype(BF16)
            grad_ref[rows, (2 * s + 1) * PAIR : (2 * s + 2) * PAIR] = jnp.concatenate(parts[2:], axis=1).astype(BF16)
        return carry

    if back:
        grad_qkv[...] = jnp.zeros_like(grad_qkv)
        grad_out[...] = jnp.zeros_like(grad_out)
        lax.fori_loop(0, chunks, weigh, 0)
        lax.fori_loop(0, grad_ref.shape[0] // BLK, arrange, 0)
        save_grad.start()
    for k in range(chunks):
        scatter_y(k).wait_recv()
        delta_ref[:, patches(k)] = delta_ref[:, patches(k)] + near_in[k].astype(F32)
    if back:
        for r in (1, 2, 3):
            line_away(r).wait_recv()
            reduced_ref[...] = reduced_ref[...] + line_in[r].astype(F32)
        for r in (1, 2, 3):
            line_away(r).wait_send()
        for s in range(4):
            half_away(s).wait_send()
        save_grad.wait()
    for k in range(chunks):
        for copy in (gather_y(k), gather_c(k), gather_d(k), scatter_c(k), scatter_y(k)):
            copy.wait_send()
        if not back:
            save(k).wait()
            for copy in save_results(k):
                copy.wait()
    if not back:
        for i in range(6):
            spread_x(i, 1).wait_recv()
            spread_x(i).wait_send()

        def spread_in_end():
            spread_in(1).wait_recv()
            spread_in().wait_send()

        pl.when(at_end)(spread_in_end)
    for k in range(4):
        pl.when(stays(k))(lambda k=k: ride_local(k).wait())
        pl.when(jnp.logical_not(stays(k)))(lambda k=k: ride_remote(k).wait_send())
        pl.when(jnp.logical_not(from_self(k)))(lambda k=k: ride_landed(k).wait_recv())


def time_call(back, own, rider, saved, weights, bias, scale):
    frames, patches, features = own.shape
    width = weights.shape[1] // 4
    heads = width // HEAD_DIM
    chunks = patches // CHUNK
    rows = 4 * frames * GROUP
    dma = pltpu.SemaphoreType.DMA
    anywhere = pl.BlockSpec(memory_space=pl.ANY)
    whole = pl.BlockSpec(memory_space=pltpu.VMEM)
    turned = (chunks, features, 4 * frames * CHUNK)
    if back:
        out_shape = []
    else:
        out_shape = [
            jax.ShapeDtypeStruct(turned, BF16),
            jax.ShapeDtypeStruct((4 * frames, patches, 3 * width), BF16),
            jax.ShapeDtypeStruct((4 * frames, patches, width), BF16),
            jax.ShapeDtypeStruct((patches // GROUP, heads, rows), F32),
        ]
    rider_shape = (4, frames * patches, BLK) if back else (frames * patches, features)
    out_shape += [
        jax.ShapeDtypeStruct((frames, patches, features), F32),
        jax.ShapeDtypeStruct(rider_shape, BF16),
    ]
    held = 2
    half = saved[2].shape[1:] if back else None
    if back:
        out_shape.insert(-1, jax.ShapeDtypeStruct((features, features), BF16))
        out_shape.insert(-1, jax.ShapeDtypeStruct(half[1:], F32))
    else:
        out_shape += [jax.ShapeDtypeStruct(w.shape, BF16) for w in saved]
        held = 4
    return pl.pallas_call(
        functools.partial(time_kernel, back, scale, heads),
        in_specs=[anywhere] * 2
        + ([anywhere, whole, anywhere, anywhere, anywhere] if back else [anywhere] * 2)
        + [anywhere, whole],
        out_specs=([] if back else [anywhere] * 3) + ([whole, anywhere, whole] if back else [whole] * 2) + [anywhere] * (held - 1),
        out_shape=out_shape,
        scratch_shapes=[
            pltpu.VMEM((features, 3 * width), BF16),
            pltpu.VMEM((features, width), BF16),
            pltpu.VMEM((4 * frames, patches, features), BF16),
            pltpu.VMEM((4 * frames, CHUNK, 3 * width), F32),
            pltpu.VMEM((4 * frames, CHUNK, width), F32),
            pltpu.VMEM((2 * frames, patches, features), F32),
            pltpu.VMEM((chunks, 2 * frames, CHUNK, features), BF16),
            pltpu.VMEM((chunks, 2 * frames, CHUNK, features), BF16),
            pltpu.VMEM((chunks, frames, CHUNK, features), BF16),
            pltpu.VMEM((chunks, frames, CHUNK, features), BF16),
        ]
        + [dma((chunks,))] * 10
        + [dma((4,)), dma((4,)), dma((1,)), dma((chunks,))]
        + [dma((7,))] * 2
        + ([pltpu.VMEM(half, BF16)] * 4 + [dma((4,))] * 5 if back else [])
        + ([pltpu.VMEM((4 * frames, patches, 3 * width), BF16)] if back else [])
        + [pltpu.VMEM(turned, BF16)]
        + ([pltpu.VMEM((features, 3 * width), F32), pltpu.VMEM((width, features), F32)] if back else [])
        + [pltpu.VMEM(weights.shape, BF16)]
        + ([pltpu.VMEM(saved[0].shape, BF16), pltpu.VMEM(saved[4].shape, BF16)] if back else [])
        + ([] if back else [pltpu.VMEM(out_shape[1].shape, BF16), pltpu.VMEM(out_shape[2].shape, BF16)])
        + [dma((4,))]
        + [pltpu.VMEM((features, features), BF16) if back else dma((2, chunks))],
        compiler_params=pltpu.CompilerParams(
            collective_id=2 if back else 1, has_side_effects=True, vmem_limit_bytes=60 * 1024 * 1024
        ),
        cost_estimate=pl.CostEstimate(flops=10**10, transcendentals=10**6, bytes_accessed=10**8),
        name="time_back" if back else "time_forward",
    )(own, rider, *saved, weights, bias)


def feed_kernel(
    resid_hbm, delta_hbm, upstream_hbm, masked, gain, w_in_hbm, w_in_far_hbm, w_out_hbm, w_far_hbm,
    half_in_hbm, half_out_hbm, grad_hbm, low_hbm, rows_hbm, gain_out,
    resid, delta, upstream, grad_out, low_out, rows_out, move_sem,
    w_in, w_out, standard, inverse, normed, grads, normed_t, grads_t, hidden, pulled, g_in, g_out, back, ahead,
    back_out, back_in, ahead_out, ahead_in, from_x, from_y, slopes,
    w_sem, g_sem, n_send, n_recv, b_send, b_recv, hx_send, hx_recv, hy_send, hy_recv,
):
    y, x, c, z = (lax.axis_index(name) for name in AXES)
    pair, near_y, near_x = (y, x, 1 - c, z), (1 - y, x, c, z), (y, 1 - x, c, z)
    own = resid.shape[0]
    moves = [
        pltpu.make_async_copy(src, dst, move_sem.at[i])
        for i, (src, dst) in enumerate((
            (resid_hbm, resid), (delta_hbm, delta), (upstream_hbm, upstream),
            (grad_out, grad_hbm), (low_out, low_hbm), (rows_out, rows_hbm),
        ))
    ]
    for copy in moves[:3]:
        copy.start()
    step = own // 2
    slab = 128

    def fetch(s, far, last=False):
        size = w_out.shape[1] // 4
        copies = []
        for i in range(4):
            rows = pl.ds(pl.multiple_of(BLK * (2 * ((y + i // 2) % 2) + (x + i % 2) % 2), BLK), BLK)
            source = w_in_far_hbm if last and i == 3 else w_in_hbm
            copies.append(pltpu.make_async_copy(source.at[s, rows], w_in.at[s, rows], w_sem.at[5 + i, s]))
        for i in range(4):
            rows = pl.ds(pl.multiple_of(size * (2 * (i // 2) + (x + i % 2) % 2), size), size)
            source = w_far_hbm if far and i % 2 else w_out_hbm
            copies.append(pltpu.make_async_copy(source.at[s, rows], w_out.at[s, rows], w_sem.at[i, s]))
        return copies

    def fetch_now(s, far, last):
        for copy in fetch(s, far, last):
            copy.start()

    for s in range(4):
        pl.when(z == s)(lambda s=s: fetch_now(s, False, False))
        if s in (0, 3):
            pl.when(z == 3 - s)(lambda s=s: fetch_now(s, True, True))
            pl.when(jnp.logical_and(z != s, z != 3 - s))(lambda s=s: fetch_now(s, True, False))
        else:
            pl.when(z != s)(lambda s=s: fetch_now(s, True, False))
    barrier = pltpu.get_barrier_semaphore()
    for peer in (pair, near_y, near_x):
        pl.semaphore_signal(barrier, inc=1, device_id=peer, device_id_type=MESH)

    def remote(src, dst, send, recv, peer=pair):
        return pltpu.make_async_remote_copy(
            src_ref=src, dst_ref=dst, send_sem=send, recv_sem=recv, device_id=peer, device_id_type=MESH
        )

    def block(yb, xb):
        return pl.ds(pl.multiple_of(BLK * (2 * yb + xb), BLK), BLK)

    def away_x(s, i):
        return remote(g_out.at[s, block(i, 1 - x)], from_x.at[i, s], hx_send.at[i, s], hx_recv.at[i, s], near_x)

    def away_y(s, i):
        return remote(g_in.at[s, block(1 - y, i)], from_y.at[i, s], hy_send.at[i, s], hy_recv.at[i, s], near_y)

    def keep(s, i):
        return (
            pltpu.make_async_copy(g_out.at[s, block(i, x)], half_out_hbm.at[i, s], g_sem.at[0, i, s]),
            pltpu.make_async_copy(g_in.at[s, block(y, i)], half_in_hbm.at[i, s], g_sem.at[1, i, s]),
        )

    def combine(s):
        for i in range(2):
            away_x(s, i).wait_recv()
            g_out[s, block(i, x)] = (g_out[s, block(i, x)].astype(F32) + from_x[i, s].astype(F32)).astype(BF16)
            away_y(s, i).wait_recv()
            g_in[s, block(y, i)] = (g_in[s, block(y, i)].astype(F32) + from_y[i, s].astype(F32)).astype(BF16)
            for copy in keep(s, i):
                copy.start()

    def at(i, size):
        return pl.ds(pl.multiple_of(i * size, size), size)

    def prepare(i, carry):
        rows = at(i, step)
        grads[rows] = jnp.where(masked[rows] > 0.0, upstream[rows].astype(F32), 0.0).astype(BF16)
        std, inv = norm_rows(resid[rows] + delta[rows])
        standard[rows] = std
        inverse[rows] = inv
        normed[rows] = (std * gain[3:4]).astype(BF16)
        return carry

    for copy in moves[:3]:
        copy.wait()
    lax.fori_loop(0, 2, prepare, 0)
    pl.semaphore_wait(barrier, 3)
    mine, theirs = pl.ds(0, own), pl.ds(own, own)
    give_grads = remote(grads.at[mine], grads.at[theirs], n_send.at[0], n_recv.at[0])
    give_normed = remote(normed.at[mine], normed.at[theirs], n_send.at[1], n_recv.at[1])
    give_normed.start()
    give_grads.start()

    def turn(i, carry):
        rows = at(i, slab)
        normed_t[:, rows] = normed[rows].T
        grads_t[:, rows] = grads[rows].T
        return carry

    lax.fori_loop(0, own // slab, turn, 0)
    rate = math.sqrt(2.0 / math.pi)

    def bend_step(s, rows):
        inner = dot_nn(normed[rows], w_in[s])
        square = inner * inner
        bend = jnp.tanh(rate * inner * (1.0 + 0.044715 * square))
        hidden[rows] = (0.5 * inner * (1.0 + bend)).astype(BF16)
        slopes[rows] = 0.5 * (1.0 + bend) + 0.5 * inner * (1.0 - bend * bend) * (rate * (1.0 + 3.0 * 0.044715 * square))

    def pull_step(s, rows):
        pulled[rows] = (dot_nt(grads[rows], w_out[s]) * slopes[rows]).astype(BF16)

    def add_step(s, rows):
        ahead[rows] = ahead[rows] + dot_nn(hidden[rows], w_out[s])
        back[rows] = back[rows] + dot_nt(pulled[rows], w_in[s])

    def clear():
        back[...] = jnp.zeros_like(back)
        ahead[...] = jnp.zeros_like(ahead)

    def meet():
        give_normed.wait_recv()
        give_grads.wait_recv()
        lax.fori_loop(own // slab, 2 * own // slab, turn, 0)

    def one_piece(s, carry):
        for copy in fetch(s, False):
            copy.wait()

        def first_half(t, carry):
            pl.when(jnp.logical_and(s == 0, t == 1))(meet)
            bend_step(s, at(t, own))
            return carry

        lax.fori_loop(0, 2, first_half, 0)
        g_out[s] = dot_nn(grads_t[...], hidden[...]).astype(BF16)
        for i in range(2):
            away_x(s, i).start()
        lax.fori_loop(0, 2, lambda t, carry: (pull_step(s, at(t, own)), carry)[1], 0)
        g_in[s] = dot_nn(normed_t[...], pulled[...]).astype(BF16)
        for i in range(2):
            away_y(s, i).start()
        pl.when(s == 0)(clear)
        lax.fori_loop(0, 2, lambda t, carry: (add_step(s, at(t, own)), carry)[1], 0)
        return carry

    lax.fori_loop(0, 4, one_piece, 0)
    back_out[...] = back[theirs].astype(BF16)
    give_back = remote(back_out, back_in, b_send.at[0], b_recv.at[0])
    give_back.start()
    ahead_out[...] = ahead[theirs].astype(BF16)
    give_ahead = remote(ahead_out, ahead_in, b_send.at[1], b_recv.at[1])
    give_ahead.start()
    give_back.wait_recv()

    def finish(i, total):
        rows = at(i, step)
        grad = back[rows] + back_in[rows].astype(F32)
        std = standard[rows]
        inner = grad * gain[3:4]
        mean = jnp.mean(inner, axis=-1, keepdims=True)
        along = jnp.mean(inner * std, axis=-1, keepdims=True)
        full = grads[rows].astype(F32) + (inner - mean - std * along) * inverse[rows]
        grad_out[rows] = full
        low_out[rows] = full.astype(BF16)
        return total + jnp.sum(grad * std, axis=0, keepdims=True)

    gain_out[...] = lax.fori_loop(0, 2, finish, jnp.zeros((1, resid.shape[1]), F32))
    moves[3].start()
    moves[4].start()
    give_ahead.wait_recv()

    def emit(i, carry):
        rows = at(i, step)
        rows_out[rows] = (resid[rows] + delta[rows] + ahead[rows] + ahead_in[rows].astype(F32)).astype(BF16)
        return carry

    lax.fori_loop(0, 2, emit, 0)
    moves[5].start()
    lax.fori_loop(0, 4, lambda s, carry: (combine(s), carry)[1], 0)
    for copy in (give_normed, give_grads, give_back, give_ahead):
        copy.wait_send()
    for s in range(4):
        for i in range(2):
            away_x(s, i).wait_send()
            away_y(s, i).wait_send()
            for copy in keep(s, i):
                copy.wait()
    for copy in moves[3:]:
        copy.wait()


def feed(resid, delta, upstream, masked, gain, w_in, w_in_far, w_out, w_far):
    own, features = resid.shape
    units = w_in.shape[2]
    dma = pltpu.SemaphoreType.DMA
    anywhere = pl.BlockSpec(memory_space=pl.ANY)
    whole = pl.BlockSpec(memory_space=pltpu.VMEM)

    def low(*shape):
        return pltpu.VMEM(shape, BF16)

    def high(*shape):
        return pltpu.VMEM(shape, F32)

    return pl.pallas_call(
        feed_kernel,
        in_specs=[anywhere] * 3 + [whole] * 2 + [anywhere] * 4,
        out_specs=[anywhere] * 5 + [whole],
        out_shape=[
            jax.ShapeDtypeStruct((2, 4, BLK, units), BF16),
            jax.ShapeDtypeStruct((2, 4, BLK, units), BF16),
            jax.ShapeDtypeStruct((own, features), F32),
            jax.ShapeDtypeStruct((own, features), BF16),
            jax.ShapeDtypeStruct((own, features), BF16),
            jax.ShapeDtypeStruct((1, features), F32),
        ],
        scratch_shapes=[
            high(own, features), high(own, features), low(own, features),
            high(own, features), low(own, features), low(own, features), dma((6,)),
            low(4, features, units), low(4, units, features), high(own, features), high(own, 1),
            low(2 * own, features), low(2 * own, features), low(features, 2 * own), low(features, 2 * own),
            low(2 * own, units), low(2 * own, units), low(4, features, units), low(4, features, units),
            high(2 * own, features), high(2 * own, features),
            low(own, features), low(own, features), low(own, features), low(own, features),
            low(2, 4, BLK, units), low(2, 4, BLK, units), high(2 * own, units),
            dma((9, 4)), dma((2, 2, 4)), dma((2,)), dma((2,)), dma((2,)), dma((2,)),
            dma((2, 4)), dma((2, 4)), dma((2, 4)), dma((2, 4)),
        ],
        compiler_params=pltpu.CompilerParams(
            collective_id=4, has_side_effects=True, vmem_limit_bytes=60 * 1024 * 1024
        ),
        cost_estimate=pl.CostEstimate(flops=26 * 10**9, transcendentals=2 * 10**6, bytes_accessed=10**8),
        name="feed",
    )(resid, delta, upstream, masked, gain, w_in, w_in_far, w_out, w_far)


def leave_kernel(
    scale,
    part_hbm, next_hbm, grad_hbm, out_hbm, joined_hbm, mixed_hbm, lhs_hbm, weight_hbm, std_hbm, time_hbm, feed_hbm, feed_in_hbm,
    totals, inverse_next, inverse, masked, gains, later_grad,
    space_qkv, space_out, feed_in_out, feed_out_out, time_qkv, time_out, rows_out, gains_out, embed_out,
    rows_in,
    part, std, base, w_out, dj, mixed, lhs, weight, low_grads, turned, dmixed, go,
    t_own, t_in, tz_out, tz_in, t_total, ty_out, ty_in, tc_out, tc_in,
    f_own, f_in, fz_out, fz_in, f_total, f_other, fc_out, fc_in,
    grads, a1_out, a1_in, b1_out, b1_in, a2_out, a2_in, b2_out, b2_in, z_out, z_in,
    half_out, half_in, ready, core_out, core_in, sums, sum_out, sum_in, share_in,
    a1_send, a1_recv, b1_send, b1_recv, a2_send, a2_recv, b2_send, b2_recv, z_send, z_recv,
    h_send, h_recv, r_send, r_recv, c_send, c_recv, s_send, s_recv, p_send, p_recv, local,
    g_send, g_recv, tx_send, tx_recv, tz_send, tz_recv, ty_send, ty_recv, fy_send, fy_recv, fz_send, fz_recv, t_local, f_local, fetched,
):
    y, x, c, z = (lax.axis_index(name) for name in AXES)
    near_y, near_x, pair = (1 - y, x, c, z), (y, 1 - x, c, z), (y, x, 1 - c, z)
    own = std.shape[0]
    third = go.shape[1] // 4
    wide = 3 * third
    two = 2 * third
    slab = 128

    fetches = [
        pltpu.make_async_copy(src, dst, fetched.at[i])
        for i, (src, dst) in enumerate((
            (part_hbm, part), (next_hbm, std), (grad_hbm, base), (out_hbm, w_out), (joined_hbm, dj), (mixed_hbm, mixed),
            (lhs_hbm, lhs), (weight_hbm, weight), (feed_in_hbm, f_other),
        ))
    ]
    for copy in fetches:
        copy.start()
    fetch_std = pltpu.make_async_copy(std_hbm, std, fetched.at[9])

    barrier = pltpu.get_barrier_semaphore()
    for dc in range(2):
        for dz in range(4):
            if dc or dz:
                pl.semaphore_signal(barrier, inc=1, device_id=(y, x, (c + dc) % 2, (z + dz) % 4), device_id_type=MESH)
    for peer in (near_y, near_x):
        pl.semaphore_signal(barrier, inc=1, device_id=peer, device_id_type=MESH)
    pl.semaphore_wait(barrier, 9)

    def remote(src, dst, send, recv, peer):
        return pltpu.make_async_remote_copy(
            src_ref=src, dst_ref=dst, send_sem=send, recv_sem=recv, device_id=peer, device_id_type=MESH
        )

    def at(i, length):
        return pl.ds(pl.multiple_of(i * length, length), length)

    def along(r):
        return (y, x, c, (z + r) % 4)

    def time_x(yb):
        return remote(time_hbm.at[at(2 * yb + 1 - x, BLK)], t_in.at[yb], tx_send.at[yb], tx_recv.at[yb], near_x)

    def time_keep(yb):
        return pltpu.make_async_copy(time_hbm.at[at(2 * yb + x, BLK)], t_own.at[yb], t_local.at[yb])

    def time_z(r):
        return remote(tz_out.at[r], tz_in.at[r], tz_send.at[r], tz_recv.at[r], along(1))

    def feed_y(r):
        s = (z + r) % 4
        return remote(feed_hbm.at[1 - y, s], f_in.at[r], fy_send.at[r], fy_recv.at[r], near_y)

    def feed_keep(r):
        return pltpu.make_async_copy(feed_hbm.at[y, (z + r) % 4], f_own.at[r], f_local.at[r])

    def feed_z(r):
        return remote(fz_out.at[r], fz_in.at[r], fz_send.at[r], fz_recv.at[r], along(1))

    for r in (3, 2, 1, 0):
        feed_y(r).start()
        feed_keep(r).start()
    for yb in range(2):
        time_x(yb).start()
        time_keep(yb).start()

    def feed_step(t):
        r = 3 - t
        feed_y(r).wait_recv()
        feed_keep(r).wait()
        total = f_own[r].astype(F32) + f_in[r].astype(F32)
        if t > 0:
            feed_z(t - 1).wait_recv()
            total = total + fz_in[t - 1].astype(F32)
        if t == 3:
            f_total[...] = total
        else:
            fz_out[t] = total.astype(BF16)
            feed_z(t).start()

    def time_step(t):
        if t == 0:
            for yb in range(2):
                time_x(yb).wait_recv()
                time_keep(yb).wait()
        else:
            time_z(t - 1).wait_recv()
        piece_at = at((z + 3 - t) % 4, BLK)
        for yb in range(2):
            total = t_own[yb, :, piece_at].astype(F32) + t_in[yb, :, piece_at].astype(F32)
            if t > 0:
                total = total + tz_in[t - 1, yb].astype(F32)
            if t == 3:
                t_total[yb] = total
            else:
                tz_out[t, yb] = total.astype(BF16)
        if t < 3:
            time_z(t).start()

    step = own // 2
    for copy in fetches[:3]:
        copy.wait()

    def norm_back(grad, standard, weights, inv):
        inner = grad * weights
        mean = jnp.mean(inner, axis=-1, keepdims=True)
        slope = jnp.mean(inner * standard, axis=-1, keepdims=True)
        return (inner - mean - standard * slope) * inv

    def after_time(i, total):
        rows = at(i, step)
        grad, standard = part[rows], std[rows]
        full = base[rows] + norm_back(grad, standard, gains[2:3], inverse_next[rows])
        base[rows] = full
        low_grads[rows] = full.astype(BF16)
        return total + jnp.sum(grad * standard, axis=0, keepdims=True)

    zero = jnp.zeros((1, std.shape[1]), F32)
    next_grad = lax.fori_loop(0, 2, after_time, zero)
    give = remote(low_grads.at[pl.ds(0, own)], low_grads.at[pl.ds(own, own)], g_send.at[0], g_recv.at[0], pair)
    give.start()
    fetch_std.start()
    for copy in fetches[3:6]:
        copy.wait()

    def attend(i, carry):
        rows = at(i, slab)
        for h in range(mixed.shape[1] // PAIR):
            places = [pl.ds((3 * h + j) * PAIR, PAIR) for j in range(3)]
            q, k, v = (dj[rows, place] for place in places)
            lines = [totals[i, 2 * h + j : 2 * h + j + 1, :] for j in range(2)]
            found = attend_pair_back(q, k, v, dmixed[rows, h * PAIR : (h + 1) * PAIR], lines, None, scale)
            for place, value in zip(places, found):
                dj[rows, place] = value.astype(BF16)
        return carry

    def turn(i, carry):
        turned[:, at(i, slab)] = low_grads[at(i, slab)].T
        return carry

    def attend_half(t, *between):
        rows = pl.ds(t * own, own)
        first, count = t * own // slab, own // slab
        dmixed[rows] = dot_nt(low_grads[rows], w_out[...]).astype(BF16)
        between[0]()
        lax.fori_loop(first, first + count // 2, attend, 0)
        between[1]()
        lax.fori_loop(first + count // 2, first + count, attend, 0)
        between[2]()
        lax.fori_loop(first, first + count, turn, 0)

    def nothing():
        pass

    attend_half(0, lambda: feed_step(0), nothing, lambda: feed_step(1))
    give.wait_recv()
    attend_half(1, nothing, lambda: feed_step(2), lambda: time_step(0))
    for copy in fetches[6:]:
        copy.wait()
    def away(i, carry):
        rows = pl.ds(pl.multiple_of(own + i * step, step), step)
        half_out[pl.ds(pl.multiple_of(i * step, step), step)] = dot_nt(dj[rows], weight[...]).astype(BF16)
        return carry

    lax.fori_loop(0, 2, away, 0)
    swap = remote(half_out, half_in, h_send.at[0], h_recv.at[0], pair)
    swap.start()

    def block(yb, xb):
        return pl.ds(pl.multiple_of(BLK * (2 * yb + xb), BLK), BLK)

    def a1(i):
        return remote(a1_out.at[i], a1_in.at[i], a1_send.at[i], a1_recv.at[i], near_x)

    def b1(i):
        return remote(b1_out.at[i], b1_in.at[i], b1_send.at[i], b1_recv.at[i], near_y)

    def a2(i):
        return remote(a2_out.at[i], a2_in.at[i], a2_send.at[i], a2_recv.at[i], near_y)

    def b2(i):
        return remote(b2_out.at[i], b2_in.at[i], b2_send.at[i], b2_recv.at[i], near_x)

    def to_z(r):
        return remote(z_out.at[r], z_in.at[r], z_send.at[r], z_recv.at[r], along(r))

    def send_first(i):
        a1(i).start()
        b1(i).start()

    def piece(i, carry):
        s = (z + i + 1) % 4
        made = dot_nn(lhs[...], dj[:, pl.ds(pl.multiple_of(s * wide, third), wide)])
        grads[i, :, :wide] = made
        grads[i, :, wide:] = go[:, pl.ds(pl.multiple_of(s * third, third), third)].astype(F32)
        for b in range(2):
            a1_out[i, b] = grads[i, block(b, 1 - x), :two].astype(BF16)
            b1_out[i, b] = grads[i, block(1 - y, b), two:].astype(BF16)
        pl.when(i < 2)(lambda: send_first(i))
        return carry


    def second(i):
        a1(i).wait_recv()
        a2_out[i] = (grads[i, block(1 - y, x), :two] + a1_in[i, 1 - y].astype(F32)).astype(BF16)
        a2(i).start()
        b1(i).wait_recv()
        b2_out[i] = (grads[i, block(y, 1 - x), two:] + b1_in[i, 1 - x].astype(F32)).astype(BF16)
        b2(i).start()
        grads[i, block(y, x), :two] = grads[i, block(y, x), :two] + a1_in[i, y].astype(F32)
        grads[i, block(y, x), two:] = grads[i, block(y, x), two:] + b1_in[i, x].astype(F32)

    def third_step(i):
        a2(i).wait_recv()
        b2(i).wait_recv()
        grads[i, block(y, x), :two] = grads[i, block(y, x), :two] + a2_in[i].astype(F32)
        grads[i, block(y, x), two:] = grads[i, block(y, x), two:] + b2_in[i].astype(F32)
        if i < 3:
            z_out[i + 1] = grads[i, block(y, x), :].astype(BF16)
            to_z(i + 1).start()

    fetch_std.wait()
    sums[...] = jnp.zeros_like(sums)
    sums[1:2] = next_grad
    sums[2:3] = later_grad[...]
    swap.wait_recv()

    def home(i, totals):
        rows = pl.ds(pl.multiple_of(i * step, step), step)
        grad = dot_nt(dj[rows], weight[...]) + half_in[rows].astype(F32)
        standard = std[rows]
        full = base[rows] + norm_back(grad, standard, gains[1:2], inverse[rows])
        hide = masked[rows] > 0.0
        ready[rows] = jnp.where(hide, 0.0, full).astype(BF16)
        return (
            totals[0] + jnp.sum(grad * standard, axis=0, keepdims=True),
            totals[1] + jnp.sum(jnp.where(hide, full, 0.0), axis=0, keepdims=True),
        )

    gain_grad, embed_grad = lax.fori_loop(0, 2, home, (zero, zero))
    sums[0:1] = gain_grad
    sums[3:4] = embed_grad

    def columns(s):
        return pl.ds(pl.multiple_of(s * BLK, BLK), BLK)

    def stays(k):
        return jnp.logical_and(z == k, z // 2 == c)

    def ride(k):
        slot = 2 * (z % 2) + c
        return remote(ready.at[:, columns(k)], rows_in.at[slot], r_send.at[k], r_recv.at[slot], (y, x, z // 2, k))

    def ride_local(k):
        return pltpu.make_async_copy(ready.at[:, columns(k)], rows_in.at[2 * (z % 2) + c], local.at[3])

    for k in range(4):
        pl.when(stays(k))(lambda k=k: ride_local(k).start())
        pl.when(jnp.logical_not(stays(k)))(lambda k=k: ride(k).start())
    time_step(1)
    go[...] = dot_nn(turned[...], mixed[...]).astype(BF16)
    lax.fori_loop(0, 4, piece, 0)

    def share(h):
        peer = (pair, near_y, near_x)[h]
        return remote(sum_out.at[h], sum_in.at[h], s_send.at[h], s_recv.at[h], peer)

    def begin_share(h):
        sum_out[h] = sums[...]
        share(h).start()

    def end_share(h):
        share(h).wait_recv()
        sums[...] = sums[...] + sum_in[h]

    begin_share(0)
    second(0)
    send_first(2)
    time_step(2)
    second(1)
    send_first(3)
    third_step(0)
    end_share(0)
    begin_share(1)
    second(2)
    third_step(1)
    end_share(1)
    begin_share(2)
    second(3)
    third_step(2)
    end_share(2)
    sum_out[3] = sums[...]

    def deal(r):
        s = (z + r) % 4
        return remote(sum_out.at[3, :, columns(s)], share_in.at[r], p_send.at[r], p_recv.at[r], (y, x, c, s))

    for r in (1, 2, 3):
        deal(r).start()
    third_step(3)
    parity = BLK // 2

    time_step(3)
    ty_out[...] = t_total[1 - y].astype(BF16)
    swap_y = remote(ty_out, ty_in, ty_send.at[0], ty_recv.at[0], near_y)
    swap_y.start()
    feed_step(3)
    fc_out[0] = f_other[at(1 - c, parity)].astype(BF16)
    fc_out[1] = f_total[at(1 - c, parity)].astype(BF16)
    swap_feed = remote(fc_out, fc_in, c_send.at[1], c_recv.at[1], pair)
    swap_feed.start()
    units = f_total.shape[1]
    feed_in_out[:, at(c, units)] = f_other[at(c, parity)]
    feed_out_out[at(c, units)] = f_total[at(c, parity)].T
    swap_y.wait_recv()
    tc_out[0] = t_total[y, at(1 - c, parity)].astype(BF16)
    tc_out[1] = ty_in[at(1 - c, parity)]
    swap_time = remote(tc_out, tc_in, c_send.at[2], c_recv.at[2], pair)
    swap_time.start()
    for k in range(4):
        pl.when(stays(k))(lambda k=k: ride_local(k).wait())
        from_self = jnp.logical_and(2 * c + k // 2 == z, c == k % 2)

        def landed(k=k):
            remote(ready.at[:, columns(k)], rows_in.at[k], r_send.at[k], r_recv.at[k], near_y).wait_recv()

        pl.when(jnp.logical_not(from_self))(landed)
    rows_out[...] = rows_in[...].astype(F32)
    for r in (1, 2, 3):
        to_z(r).wait_recv()
    total = grads[3, block(y, x), :]
    for r in (1, 2, 3):
        total = total + z_in[r].astype(F32)
    grads[3, block(y, x), :] = total
    rows = BLK // 2

    def core_rows(core):
        return pl.ds(pl.multiple_of(BLK * (2 * y + x) + rows * core, rows), rows)

    core_out[...] = grads[3, core_rows(1 - c), :].astype(BF16)
    last = remote(core_out, core_in, c_send.at[0], c_recv.at[0], pair)
    last.start()
    def place(core, value):
        for j in range(3):
            space_qkv[j, :, at(core, third)] = value[:, j * third : (j + 1) * third]
        space_out[at(core, third)] = value[:, 3 * third :].T

    place(c, grads[3, core_rows(c), :])
    result = sums[:, columns(z)]
    for r in (1, 2, 3):
        deal(r).wait_recv()
        result = result + share_in[r]
    gains_out[...] = result[:3]
    embed_out[...] = result[3:4]
    swap_feed.wait_recv()
    feed_in_out[:, at(1 - c, units)] = fc_in[0].astype(F32)
    feed_out_out[at(1 - c, units)] = fc_in[1].astype(F32).T
    swap_time.wait_recv()
    mine = (t_total[y, at(c, parity)], ty_in[at(c, parity)].astype(F32))
    other = (tc_in[0].astype(F32), tc_in[1].astype(F32))
    by_head = []
    for yb in range(2):
        for cb in range(2):
            by_head.append(
                jnp.where(
                    c == cb,
                    jnp.where(y == yb, mine[0], mine[1]),
                    jnp.where(y == yb, other[0], other[1]),
                )
            )
    for j in range(4):
        made = jnp.concatenate([v[:, j * HEAD_DIM : (j + 1) * HEAD_DIM] for v in by_head], axis=1)
        if j < 3:
            time_qkv[j] = made
        else:
            time_out[...] = made.T
    last.wait_recv()
    place(1 - c, core_in[...].astype(F32))

    for copy in (last, swap, give, swap_y, swap_feed, swap_time):
        copy.wait_send()
    for yb in range(2):
        time_x(yb).wait_send()
    for r in range(4):
        feed_y(r).wait_send()
    for t in range(3):
        time_z(t).wait_send()
        feed_z(t).wait_send()
    for i in range(4):
        for copy in (a1(i), b1(i), a2(i), b2(i)):
            copy.wait_send()
    for r in (1, 2, 3):
        to_z(r).wait_send()
        deal(r).wait_send()
    for h in range(3):
        share(h).wait_send()
    for k in range(4):
        pl.when(jnp.logical_not(stays(k)))(lambda k=k: ride(k).wait_send())


def leave(
    part, std_next, grad, w_out, joined, mixed, lhs, weight, std, g_time, g_out, g_in,
    totals, inverse_next, inverse, masked, gains, later_grad, scale,
):
    own, features = std.shape
    cols4 = mixed.shape[1]
    quarter = cols4 // 4
    units = g_in.shape[1]
    dma = pltpu.SemaphoreType.DMA
    anywhere = pl.BlockSpec(memory_space=pl.ANY)
    whole = pl.BlockSpec(memory_space=pltpu.VMEM)
    parity = BLK // 2

    def low(*shape):
        return pltpu.VMEM(shape, BF16)

    def high(*shape):
        return pltpu.VMEM(shape, F32)

    return pl.pallas_call(
        functools.partial(leave_kernel, scale),
        in_specs=[anywhere] * 12 + [whole] * 6,
        out_specs=[whole] * 9,
        out_shape=[
            jax.ShapeDtypeStruct(shape, F32)
            for shape in (
                (3, parity, 2 * quarter), (2 * quarter, parity), (parity, 2 * units), (2 * units, parity),
                (3, parity, BLK), (BLK, parity), (4, own, BLK), (3, BLK), (1, BLK),
            )
        ],
        scratch_shapes=[
            low(4, own, BLK),
            high(own, features), high(own, features), high(own, features), low(*w_out.shape), low(*joined.shape),
            low(*mixed.shape), low(*lhs.shape), low(*weight.shape), low(2 * own, features), low(features, 2 * own),
            low(*mixed.shape), low(features, cols4),
            low(2, BLK, features), low(2, BLK, features), low(4, 2, BLK, BLK), low(4, 2, BLK, BLK), high(2, BLK, BLK),
            low(BLK, BLK), low(BLK, BLK), low(2, parity, BLK), low(2, parity, BLK),
            low(4, BLK, units), low(4, BLK, units), low(4, BLK, units), low(4, BLK, units),
            high(BLK, units), high(BLK, units), low(2, parity, units), low(2, parity, units),
            high(4, features, cols4),
            low(4, 2, BLK, 2 * quarter), low(4, 2, BLK, 2 * quarter), low(4, 2, BLK, 2 * quarter), low(4, 2, BLK, 2 * quarter),
            low(4, BLK, 2 * quarter), low(4, BLK, 2 * quarter), low(4, BLK, 2 * quarter), low(4, BLK, 2 * quarter),
            low(4, BLK, cols4), low(4, BLK, cols4),
            low(own, features), low(own, features), low(own, features),
            low(parity, cols4), low(parity, cols4),
            high(8, features), high(4, 8, features), high(3, 8, features), high(4, 8, BLK),
        ]
        + [dma((4,))] * 10
        + [dma((1,)), dma((1,)), dma((4,)), dma((4,)), dma((3,)), dma((3,)), dma((3,)), dma((3,)), dma((4,)), dma((4,)), dma((4,))]
        + [dma((1,)), dma((1,)), dma((2,)), dma((2,)), dma((4,)), dma((4,)), dma((1,)), dma((1,))]
        + [dma((4,)), dma((4,)), dma((4,)), dma((4,)), dma((2,)), dma((4,)), dma((10,))],
        compiler_params=pltpu.CompilerParams(
            collective_id=3, has_side_effects=True, vmem_limit_bytes=62 * 1024 * 1024
        ),
        cost_estimate=pl.CostEstimate(flops=2 * 10**10, transcendentals=10**6, bytes_accessed=10**8),
        name="leave",
    )(
        part, std_next, grad, w_out, joined, mixed, lhs, weight, std, g_time, g_out, g_in,
        totals, inverse_next, inverse, masked, gains, later_grad,
    )


def tie(*values):
    return lax.optimization_barrier(values)


def norm_rows(resid):
    mean = jnp.mean(resid, axis=-1, keepdims=True)
    centered = resid - mean
    inverse = lax.rsqrt(jnp.mean(centered * centered, axis=-1, keepdims=True) + eps_norm)
    return (centered * inverse, inverse)


def norm_rows_back(grad, standardized, inverse, gain):
    gain_grad = jnp.sum(grad * standardized, axis=0)
    inner = grad * gain
    mean = jnp.mean(inner, axis=-1, keepdims=True)
    along = jnp.mean(inner * standardized, axis=-1, keepdims=True)
    return ((inner - mean - standardized * along) * inverse, gain_grad)


def cols(parts):
    return jnp.concatenate(parts, axis=1)


def rows_of(parts):
    return jnp.concatenate(parts, axis=0)


def token_parallel(
    tokens,
    cotangent,
    ratio,
    priority,
    frame_order,
    mask_embed,
    gains,
    qkv_space,
    out_space,
    qkv_time,
    out_time,
    w_in,
    w_out,
):
    scale = 1.0 / math.sqrt(HEAD_DIM)
    y, x, c, z = (lax.axis_index(name) for name in AXES)
    patches = tokens.shape[2]
    width = qkv_space.shape[0]
    frames_own = tokens.shape[0] * tokens.shape[1] // 4
    frames_all = frame_order.shape[1]
    own = frames_own * patches
    hidden_own = w_in.shape[1] // 2
    plane = 2 * y + x
    k_own = 2 * (z % 2) + c

    masked_here = (priority < ratio[:, None, None]).astype(jnp.int32).reshape(2, -1)
    info = cols([masked_here, frame_order])
    info = jnp.where(z // 2 == c, info, hop_c(info))
    info = lax.dynamic_index_in_dim(info, z % 2, 0, keepdims=False)
    masked = lax.dynamic_slice_in_dim(info, c * own, own, 0)[:, None] != 0
    order = info[2 * own :].reshape(2, 2, frames_own)
    order = jnp.where(y == 1, order[::-1], order)
    order = jnp.where(c == 1, order[:, ::-1], order).swapaxes(0, 1).reshape(frames_all)
    order = jnp.repeat(order, GROUP)
    patch = jnp.arange(frames_all * GROUP) % GROUP
    visible = (order[:, None] <= order[None, :]) & (patch[:, None] == patch[None, :])
    bias = jnp.where(visible, 0.0, -1e30).astype(F32)

    vectors = rows_of([mask_embed[None], gains, jnp.zeros((4, BLK), BF16)])
    (
        ws_qkv, ws_out, wt_all, wf_out, wf_in, joined0, turned0, std0,
        mixed0, total0, inv0, resid1, std1, inv1, normed1, vectors,
    ) = enter(
        tokens.reshape(4, own, BLK),
        vectors,
        jnp.swapaxes(qkv_space, 0, 1),
        out_space,
        jnp.swapaxes(qkv_time, 0, 1),
        out_time,
        w_out,
        w_in,
        masked.astype(F32),
        scale,
    )

    half = qkv_space.shape[2] // 2
    turned1, joined1, mixed1, total1, delta, upstream, wf_far, wf_in_far = time_call(
        False,
        normed1.reshape(frames_own, patches, width),
        cotangent.reshape(4, own, BLK),
        [wf_out, wf_in],
        wt_all,
        bias,
        scale,
    )
    w_in_half, w_out_half, grad2, grad2_low, block_rows, gain_grad2 = feed(
        resid1, delta.reshape(own, width), upstream, masked.astype(F32), vectors, wf_in, wf_in_far, wf_out, wf_far
    )

    part1, g_time, g_w_in, block_out = time_call(
        True,
        grad2_low.reshape(frames_own, patches, width),
        block_rows,
        [joined1, total1, w_in_half, turned1, mixed1],
        wt_all,
        bias,
        scale,
    )
    block_out = block_out.reshape(tokens.shape)
    grad_qkv_space, grad_out_space, grad_w_in, grad_w_out, grad_qkv_time, grad_out_time, grad_tokens, grad_gains, grad_embed = leave(
        part1.reshape(own, width), std1, grad2, ws_out, joined0, mixed0, turned0, ws_qkv, std0, g_time, w_out_half, g_w_in,
        total0, inv1, inv0, masked.astype(F32), vectors, gain_grad2, scale,
    )
    return (
        block_out,
        grad_tokens.reshape(tokens.shape),
        grad_embed.reshape(BLK),
        grad_gains,
        jnp.swapaxes(grad_qkv_space, 0, 1),
        grad_out_space,
        jnp.swapaxes(grad_qkv_time, 0, 1),
        grad_out_time,
        grad_w_in,
        grad_w_out,
    )


def solution(mesh):
    sizes = (mesh.shape["tm"], mesh.shape["clip"], mesh.shape["mp"])
    if sizes == (2, 4, 4):
        mesh = jax.sharding.Mesh(mesh.devices.reshape(2, 2, 2, 4), AXES)
        step, clip = token_parallel, ("x", "c")
    else:
        step, clip = shards, ("clip",)
    return jax.shard_map(
        step,
        mesh=mesh,
        in_specs=(
            P(clip, "tm", None, "mp"),
            P(clip, "tm", None, "mp"),
            P(clip),
            P(clip, "tm", None),
            P(clip, None),
            P("mp"),
            P(None, "mp"),
            P(None, None, "mp"),
            P("mp", None),
            P(None, None, "mp"),
            P("mp", None),
            P(None, "mp"),
            P("mp", None),
        ),
        out_specs=(
            P(clip, "tm", None, "mp"),
            P(clip, "tm", None, "mp"),
            P("mp"),
            P(None, "mp"),
            P(("tm",) + clip, None, "mp"),
            P("mp", ("tm",) + clip),
            P(("tm",) + clip, None, "mp"),
            P("mp", ("tm",) + clip),
            P(("tm",) + clip, "mp"),
            P("mp", ("tm",) + clip),
        ),
        check_vma=False,
    )
```
